32 devices in a mesh: grp: 4 (over x, core), shard: 8 (over z, y).
Axes of the slice: x: 2, y: 2, z: 4, core: 2. Of those that a mesh axis runs over, the one named last changes fastest.
Arguments:
- tokens: bfloat16 [8, 512, 2048], P('grp', 'shard'), may hold values from -6 to 6
- lengths: int32 [8], P('grp'), may hold values from 128 to 512, as said below
- prenorm_gain: bfloat16 [2048], P('shard'), may hold values from 0.099609375 to 1.8984375
- query_weight: bfloat16 [2048, 2048], P('shard'), may hold values from -0.125 to 0.125
- key_weight: bfloat16 [1024, 2048], P('shard'), may hold values from -0.125 to 0.125
- value_weight: bfloat16 [1024, 2048], P('shard'), may hold values from -0.125 to 0.125
- out_weight: bfloat16 [2048, 2048], P('shard'), may hold values from -2 to 2
- midnorm_gain: bfloat16 [2048], P('shard'), may hold values from 0.099609375 to 1.8984375
- gate_weight: bfloat16 [8192, 2048], P('shard'), may hold values from -0.125 to 0.125
- up_weight: bfloat16 [8192, 2048], P('shard'), may hold values from -0.125 to 0.125
- down_weight: bfloat16 [8192, 2048], P('shard'), may hold values from -0.0625 to 0.0625
- cotangent: bfloat16 [8, 512, 2048], P('grp', 'shard'), may hold values from -6 to 6
Outputs:
- mixed: bfloat16 [8, 512, 2048], P('grp', 'shard')
- input_gradient: bfloat16 [8, 512, 2048], P('grp', 'shard')
- prenorm_gradient: float32 [2048], P('shard')
- query_gradient: float32 [2048, 2048], P('shard')
- key_gradient: float32 [1024, 2048], P('shard')
- value_gradient: float32 [1024, 2048], P('shard')
- out_gradient: float32 [2048, 2048], P('shard')
- midnorm_gradient: float32 [2048], P('shard')
- gate_gradient: float32 [8192, 2048], P('shard')
- up_gradient: float32 [8192, 2048], P('shard')
- down_gradient: float32 [8192, 2048], P('shard')
The draws below stay inside these ranges and needn't reach their ends.
Inputs may be any that keep to these rules, and one draw needn't show every extreme that they name: Each sequence's valid slots are its first lengths[n] slots; in every draw some sequence has all 512 slots valid.
All inputs are finite; a program needn't handle non-finite values.
Results may differ from the reference program's by a relative error of at most 0.02.
Values may be sent and summed in bfloat16 or wider, within the bound.
A program may use at most 448 MiB of HBM per device.

```python
import math
import jax
import jax.numpy as jnp
from jax import lax

D = 2048
NH = 8
KVH = 4
HD = 256
FF = 8192
QD = 2048
KVD = 1024
SLOT = 512
NSEQ = 8


def draw_lengths(key, part):
    base_lengths = jax.random.randint(key, (NSEQ,), SLOT // 4, SLOT + 1)
    full_index = jax.random.randint(jax.random.fold_in(key, 7), (), 0, NSEQ)
    return jnp.where(jnp.arange(NSEQ) == full_index, SLOT, base_lengths).astype(jnp.int32)


def steps_of(stream_key, dims, pieces, low, largest):
    factor_of = 1.0
    for dim, blocks in pieces:
        draws = jax.random.uniform(jax.random.fold_in(jax.random.fold_in(stream_key, 6), dim), (blocks,), jnp.float32, low / len(pieces), largest / len(pieces))
        factor_of = factor_of * jnp.repeat(jnp.exp(draws), dims[dim] // blocks).reshape((-1,) + (1,) * (len(dims) - 1 - dim))
    return factor_of


def gaussian(own_key, extent, deviation, bound, split=(), kind=jnp.bfloat16):
    entries = deviation * jax.random.normal(own_key, extent, jnp.float32)
    if split:
        entries = entries * steps_of(own_key, extent, split, -0.22, 0.18)
    return jnp.clip(entries, -bound, bound).astype(kind)


def setup_inputs(seed: int = 0) -> dict:
    splits = jax.random.split(jax.random.key(seed), 13)
    return {
        "tokens": gaussian(splits[0], (NSEQ, SLOT, D), 1.0, 6.0, ((0, 4), (1, 8))),
        "lengths": draw_lengths(jax.random.fold_in(splits[12], 71), 0),
        "prenorm_gain": jnp.clip(1.0 + 0.18 * jax.random.normal(splits[2], (D,), jnp.float32), 0.099609375, 1.8984375).astype(jnp.bfloat16),
        "query_weight": gaussian(splits[3], (QD, D), D ** -0.5, 0.125, ((0, 8),)),
        "key_weight": gaussian(splits[4], (KVD, D), D ** -0.5, 0.125, ((0, 8),)),
        "value_weight": gaussian(splits[5], (KVD, D), D ** -0.5, 0.125, ((0, 8),)),
        "out_weight": gaussian(splits[6], (QD, D), 8 ** -0.5, 2.0, ((0, 8),)),
        "midnorm_gain": jnp.clip(1.0 + 0.18 * jax.random.normal(splits[7], (D,), jnp.float32), 0.099609375, 1.8984375).astype(jnp.bfloat16),
        "gate_weight": gaussian(splits[8], (FF, D), D ** -0.5, 0.125, ((0, 8),)),
        "up_weight": gaussian(splits[9], (FF, D), D ** -0.5, 0.125, ((0, 8),)),
        "down_weight": gaussian(splits[10], (FF, D), FF ** -0.5, 0.0625, ((0, 8),)),
        "cotangent": gaussian(splits[11], (NSEQ, SLOT, D), 1.0, 6.0, ((0, 4), (1, 8))),
    }


@jax.custom_vjp
def low(v):
    return lax.optimization_barrier(v.astype(jnp.bfloat16)).astype(jnp.float32)

@jax.custom_vjp
def low_back(v):
    return v

def low_keep(v):
    return (low(v), None)

def low_pass(kept, grad):
    return (grad,)

def back_keep(v):
    return (v, None)

def back_low(kept, grad):
    return (low(grad),)
low.defvjp(low_keep, low_pass)
low_back.defvjp(back_keep, back_low)
highest = lax.Precision.HIGHEST
epsilon = 1e-06
theta_base = 1000042.0
masked_value = -1e+30

def turned(source):
    half_width = source.shape[-1] // 2
    return jnp.concatenate([-source[..., half_width:], source[..., :half_width]], -1)

def rotate(source, cosine_table, sine_table):
    return source * cosine_table + turned(source) * sine_table

def rms_scaled(source, norm_gain):
    return source * lax.rsqrt(lax.optimization_barrier(jnp.mean(source * source, -1, keepdims=True)) + epsilon) * norm_gain

def tables(slot_count):
    inverse = theta_base ** (-(jnp.arange(0, HD, 2).astype(jnp.float32) / HD))
    angles = jnp.arange(slot_count).astype(jnp.float32)[:, None] * inverse[None, :]
    cosine_table = jnp.concatenate([jnp.cos(angles), jnp.cos(angles)], -1)[:, None, :]
    sine_table = jnp.concatenate([jnp.sin(angles), jnp.sin(angles)], -1)[:, None, :]
    return (cosine_table, sine_table)

def layer_forward(source, prenorm, query_w, key_w, value_w, out_w, midnorm, gate_w, up_w, down_w, length, cosine_table, sine_table):
    slot_count = source.shape[0]
    normed_first = low(rms_scaled(source, prenorm))
    query_pre = low_back(jnp.dot(normed_first, query_w.T, precision=highest)).reshape(slot_count, NH, HD)
    key_pre = low_back(jnp.dot(normed_first, key_w.T, precision=highest)).reshape(slot_count, KVH, HD)
    values = low(low_back(jnp.dot(normed_first, value_w.T, precision=highest))).reshape(slot_count, KVH, HD)
    queries = low(rotate(query_pre, cosine_table, sine_table))
    keys = low(rotate(key_pre, cosine_table, sine_table))
    keys_rep = jnp.repeat(keys, NH // KVH, axis=1)
    values_rep = jnp.repeat(values, NH // KVH, axis=1)
    block_rows = math.gcd(slot_count, 512)
    key_pos = jnp.arange(slot_count).astype(jnp.int32)

    def attend(first_row):
        query_block = lax.dynamic_slice_in_dim(queries, first_row, block_rows, 0)
        scores = jnp.einsum('qhd,khd->hqk', query_block, keys_rep, precision=highest) * (1.0 / math.sqrt(HD))
        query_pos = first_row + jnp.arange(block_rows).astype(jnp.int32)
        allowed = (key_pos[None, :] <= query_pos[:, None]) & (key_pos[None, :] < length)
        scores = low_back(jnp.where(allowed[None], scores, masked_value))
        row_max = lax.optimization_barrier(jnp.max(scores, -1, keepdims=True))
        exp_scores = jnp.exp(scores - row_max)
        attention_probs = exp_scores / lax.optimization_barrier(jnp.sum(exp_scores, -1, keepdims=True))
        return jnp.einsum('hqk,khd->qhd', low(attention_probs), values_rep, precision=highest)
    starts = (jnp.arange(slot_count // block_rows) * block_rows).astype(jnp.int32)
    attended = lax.map(jax.checkpoint(attend), starts).reshape(slot_count, NH * HD)
    attended = low(low_back(attended))
    branch = low_back(jnp.dot(attended, out_w, precision=highest))
    middle = source + branch
    normed_second = low(rms_scaled(middle, midnorm))
    gate_pre = low_back(jnp.dot(normed_second, gate_w.T, precision=highest))
    up_pre = low_back(jnp.dot(normed_second, up_w.T, precision=highest))
    hidden = low(gate_pre * jax.nn.sigmoid(gate_pre) * up_pre)
    result = middle + jnp.dot(hidden, down_w, precision=highest)
    valid_rows = key_pos < length
    return jnp.where(valid_rows[:, None], result, 0.0)

def reference(tokens, lengths, prenorm_gain, query_weight, key_weight, value_weight, out_weight, midnorm_gain, gate_weight, up_weight, down_weight, cotangent):
    weights = tuple((weight.astype(jnp.float32) for weight in (prenorm_gain, query_weight, key_weight, value_weight, out_weight, midnorm_gain, gate_weight, up_weight, down_weight)))
    cosine_table, sine_table = tables(SLOT)

    def per_sequence(totals, current):
        row_tokens, length, row_cotangent = current

        def forward(row_float, *parameters):
            return layer_forward(row_float, *parameters, length, cosine_table, sine_table)
        result, pullback = jax.vjp(forward, row_tokens.astype(jnp.float32), *weights)
        gradients = pullback(row_cotangent.astype(jnp.float32))
        totals = jax.tree.map(jnp.add, totals, tuple(gradients[1:]))
        return (totals, (result.astype(jnp.bfloat16), gradients[0].astype(jnp.bfloat16)))
    initial = tuple((jnp.zeros(weight.shape, jnp.float32) for weight in weights))
    totals, outputs = lax.scan(per_sequence, initial, (tokens, lengths, cotangent))
    return (outputs[0], outputs[1], totals[0], totals[1], totals[2], totals[3], totals[4], totals[5], totals[6], totals[7], totals[8])
```

```python
import math

import jax
import jax.numpy as jnp
from jax import lax
from jax.sharding import PartitionSpec as P

NH = 8
KVH = 4
HD = 256


epsilon = 1e-06
theta_base = 1000042.0
masked_value = -1e30


def turned(source):
    half_width = source.shape[-1] // 2
    return jnp.concatenate([-source[..., half_width:], source[..., :half_width]], -1)


def rotate(source, cosine_table, sine_table):
    return source * cosine_table + turned(source) * sine_table


def unrotate(source, cosine_table, sine_table):
    return source * cosine_table - turned(source) * sine_table


def norm_forward(source, norm_gain):
    inverse = lax.rsqrt(jnp.mean(source * source, -1, keepdims=True) + epsilon)
    return (source * inverse * norm_gain, inverse)


def norm_backward(source, inverse, norm_gain, grad_out):
    weighted = grad_out * norm_gain
    inner_sum = jnp.sum(weighted * source, -1, keepdims=True)
    grad_in = (
        inverse * weighted - source * inverse * inverse * inverse * inner_sum / source.shape[-1]
    )
    return (grad_in, jnp.sum(grad_out * source * inverse, 0))


def weight_terms(normed, query_grad, key_grad, value_grad, attended, branch_grad, shard_count):
    token_count, model_width = normed.shape
    query_share = query_grad.shape[1] // shard_count
    kv_share = key_grad.shape[1] // shard_count
    shard_rows = 2 * query_share + 2 * kv_share

    def weight_term(first_row, row_count):
        blocks = row_count // shard_rows

        def columns(matrix, share_cols):
            return matrix.reshape(token_count, blocks, share_cols)

        part_query = jnp.einsum(
            "tmr,td->mrd",
            columns(query_grad, query_share),
            normed,
            preferred_element_type=jnp.float32,
        )
        part_key = jnp.einsum(
            "tmr,td->mrd", columns(key_grad, kv_share), normed, preferred_element_type=jnp.float32
        )
        part_value = jnp.einsum(
            "tmr,td->mrd", columns(value_grad, kv_share), normed, preferred_element_type=jnp.float32
        )
        part_out = jnp.einsum(
            "tmr,td->mrd",
            columns(attended, query_share),
            branch_grad,
            preferred_element_type=jnp.float32,
        )
        return jnp.concatenate([part_query, part_key, part_value, part_out], 1).reshape(
            row_count, model_width
        )

    return (weight_term, shard_rows)


def local_rows(
    tokens,
    lengths,
    prenorm_gain,
    query_weight,
    key_weight,
    value_weight,
    out_weight,
    midnorm_gain,
    gate_weight,
    up_weight,
    down_weight,
    cotangent,
):
    shard_count = lax.axis_size("shard")
    shard_rank = lax.axis_index("shard")
    micro_count, seq_dev, model_width = tokens.shape
    slot_count = seq_dev * shard_count
    repeat_heads = NH // KVH
    query_width = NH * HD
    kv_width = KVH * HD
    score_scale = 1.0 / math.sqrt(HD)
    local_pos = shard_rank * seq_dev + jnp.arange(seq_dev, dtype=jnp.int32)
    key_pos = jnp.arange(slot_count, dtype=jnp.int32)
    inverse_freq = theta_base ** (-(jnp.arange(0, HD, 2).astype(jnp.float32) / HD))
    angles = local_pos.astype(jnp.float32)[:, None] * inverse_freq[None, :]
    cosine_table = jnp.concatenate([jnp.cos(angles), jnp.cos(angles)], -1)[:, None, :]
    sine_table = jnp.concatenate([jnp.sin(angles), jnp.sin(angles)], -1)[:, None, :]
    gate_total = jnp.zeros(gate_weight.shape, jnp.float32)
    up_total = jnp.zeros(up_weight.shape, jnp.float32)
    down_total = jnp.zeros(down_weight.shape, jnp.float32)
    prenorm_total = jnp.zeros((model_width,), jnp.float32)
    midnorm_total = jnp.zeros((model_width,), jnp.float32)
    attn_total = None
    mixed_rows = []
    input_rows = []
    for micro_index in range(micro_count):
        gathered = (
            lax.all_gather(query_weight, "shard", axis=0, tiled=True),
            lax.all_gather(key_weight, "shard", axis=0, tiled=True),
            lax.all_gather(value_weight, "shard", axis=0, tiled=True),
            lax.all_gather(prenorm_gain, "shard", axis=0, tiled=True),
            lax.all_gather(midnorm_gain, "shard", axis=0, tiled=True),
        )
        query_full, key_full, value_full, prenorm_full, midnorm_full = gathered
        prenorm_f = prenorm_full.astype(jnp.float32)
        midnorm_f = midnorm_full.astype(jnp.float32)
        source = tokens[micro_index].astype(jnp.float32)
        length_now = lengths[micro_index]
        valid_rows = local_pos < length_now
        scaled_first, inverse_first = norm_forward(source, prenorm_f)
        normed_first = scaled_first.astype(jnp.bfloat16)
        query_pre = jnp.einsum(
            "sd,qd->sq", normed_first, query_full, preferred_element_type=jnp.float32
        ).reshape(seq_dev, NH, HD)
        key_pre = jnp.einsum(
            "sd,qd->sq", normed_first, key_full, preferred_element_type=jnp.float32
        ).reshape(seq_dev, KVH, HD)
        value_pre = jnp.einsum(
            "sd,qd->sq", normed_first, value_full, preferred_element_type=jnp.float32
        )
        query_rot = rotate(query_pre, cosine_table, sine_table).astype(jnp.bfloat16)
        key_rot = rotate(key_pre, cosine_table, sine_table).astype(jnp.bfloat16)
        key_value = jnp.concatenate(
            [key_rot.reshape(seq_dev, kv_width), value_pre.astype(jnp.bfloat16)], 1
        )
        kv_all = lax.all_gather(key_value, "shard", axis=0, tiled=True)
        keys_all = kv_all[:, :kv_width].reshape(slot_count, KVH, HD)
        values_all = kv_all[:, kv_width:].reshape(slot_count, KVH, HD)
        query_group = query_rot.reshape(seq_dev, KVH, repeat_heads, HD)
        scores = (
            jnp.einsum("skrd,tkd->krst", query_group, keys_all, preferred_element_type=jnp.float32)
            * score_scale
        )
        allowed = (key_pos[None, :] <= local_pos[:, None]) & (key_pos[None, :] < length_now)
        scores = jnp.where(allowed, scores, masked_value)
        row_max = jnp.max(scores, -1, keepdims=True)
        exp_scores = jnp.exp(scores - row_max)
        attention_probs = exp_scores / jnp.sum(exp_scores, -1, keepdims=True)
        probs_low = attention_probs.astype(jnp.bfloat16)
        attended = (
            jnp.einsum("krst,tkd->skrd", probs_low, values_all, preferred_element_type=jnp.float32)
            .astype(jnp.bfloat16)
            .reshape(seq_dev, query_width)
        )
        branch = jnp.dot(
            attended,
            lax.all_gather(out_weight, "shard", axis=0, tiled=True),
            preferred_element_type=jnp.float32,
        )
        middle = source + branch
        scaled_second, inverse_second = norm_forward(middle, midnorm_f)
        normed_second = scaled_second.astype(jnp.bfloat16)
        normed_all = lax.all_gather(normed_second, "shard", axis=0, tiled=True)
        gate_pre = jnp.einsum(
            "sd,fd->sf", normed_all, gate_weight, preferred_element_type=jnp.float32
        )
        up_pre = jnp.einsum("sd,fd->sf", normed_all, up_weight, preferred_element_type=jnp.float32)
        sigmoid_gate = jax.nn.sigmoid(gate_pre)
        silu_gate = gate_pre * sigmoid_gate
        hidden = (silu_gate * up_pre).astype(jnp.bfloat16)
        ffn_part = lax.psum_scatter(
            jnp.dot(hidden, down_weight, preferred_element_type=jnp.float32).astype(jnp.bfloat16),
            "shard",
            scatter_dimension=0,
            tiled=True,
        ).astype(jnp.float32)
        mixed_rows.append(
            jnp.where(valid_rows[:, None], middle + ffn_part, 0.0).astype(jnp.bfloat16)
        )
        cot_low = jnp.where(
            valid_rows[:, None], cotangent[micro_index], jnp.zeros_like(cotangent[micro_index])
        )
        cot_all = lax.all_gather(cot_low, "shard", axis=0, tiled=True)
        hidden_grad = jnp.einsum(
            "sd,fd->sf", cot_all, down_weight, preferred_element_type=jnp.float32
        )
        down_total = down_total + jnp.einsum(
            "sf,sd->fd", hidden, cot_all, preferred_element_type=jnp.float32
        )
        gate_grad = (
            hidden_grad * up_pre * sigmoid_gate * (1.0 + gate_pre * (1.0 - sigmoid_gate))
        ).astype(jnp.bfloat16)
        up_grad = (hidden_grad * silu_gate).astype(jnp.bfloat16)
        gate_total = gate_total + jnp.einsum(
            "sf,sd->fd", gate_grad, normed_all, preferred_element_type=jnp.float32
        )
        up_total = up_total + jnp.einsum(
            "sf,sd->fd", up_grad, normed_all, preferred_element_type=jnp.float32
        )
        second_grad = lax.psum_scatter(
            jnp.dot(gate_grad, gate_weight, preferred_element_type=jnp.float32)
            + jnp.dot(up_grad, up_weight, preferred_element_type=jnp.float32),
            "shard",
            scatter_dimension=0,
            tiled=True,
        )
        middle_part, midnorm_part = norm_backward(middle, inverse_second, midnorm_f, second_grad)
        middle_grad = cot_low.astype(jnp.float32) + middle_part
        midnorm_total = midnorm_total + midnorm_part
        branch_grad = middle_grad.astype(jnp.bfloat16)
        attended_grad = jnp.einsum(
            "sd,qd->sq",
            branch_grad,
            lax.all_gather(out_weight, "shard", axis=0, tiled=True),
            preferred_element_type=jnp.float32,
        ).astype(jnp.bfloat16)
        attended_group = attended_grad.reshape(seq_dev, KVH, repeat_heads, HD)
        probs_grad = jnp.einsum(
            "skrd,tkd->krst", attended_group, values_all, preferred_element_type=jnp.float32
        )
        inner_sum = jnp.sum(attention_probs * probs_grad, -1, keepdims=True)
        scores_grad = (attention_probs * (probs_grad - inner_sum)).astype(jnp.bfloat16)
        query_rot_grad = (
            jnp.einsum(
                "krst,tkd->skrd", scores_grad, keys_all, preferred_element_type=jnp.float32
            ).reshape(seq_dev, NH, HD)
            * score_scale
        )
        query_grad = (
            unrotate(query_rot_grad, cosine_table, sine_table)
            .astype(jnp.bfloat16)
            .reshape(seq_dev, query_width)
        )
        row_count = lax.axis_size("shard") * seq_dev
        key_part = (
            jnp.einsum(
                "krst,skrd->tkd", scores_grad, query_group, preferred_element_type=jnp.float32
            )
            * score_scale
        )
        value_part = jnp.einsum(
            "krst,skrd->tkd", probs_low, attended_group, preferred_element_type=jnp.float32
        )
        kv_grad = lax.psum_scatter(
            jnp.concatenate(
                [key_part.reshape(row_count, kv_width), value_part.reshape(row_count, kv_width)], 1
            ).astype(jnp.bfloat16),
            "shard",
            scatter_dimension=0,
            tiled=True,
        ).astype(jnp.float32)
        key_grad = (
            unrotate(kv_grad[:, :kv_width].reshape(seq_dev, KVH, HD), cosine_table, sine_table)
            .astype(jnp.bfloat16)
            .reshape(seq_dev, kv_width)
        )
        value_grad = kv_grad[:, kv_width:].astype(jnp.bfloat16)
        first_grad = jnp.einsum(
            "sq,qd->sd", query_grad, query_full, preferred_element_type=jnp.float32
        )
        first_grad = first_grad + jnp.einsum(
            "sq,qd->sd", key_grad, key_full, preferred_element_type=jnp.float32
        )
        first_grad = first_grad + jnp.einsum(
            "sq,qd->sd", value_grad, value_full, preferred_element_type=jnp.float32
        )
        source_part, prenorm_part = norm_backward(source, inverse_first, prenorm_f, first_grad)
        input_rows.append((middle_grad + source_part).astype(jnp.bfloat16))
        prenorm_total = prenorm_total + prenorm_part
        saved = (normed_first, query_grad, key_grad, value_grad, attended, branch_grad)
        weight_term, shard_rows = weight_terms(*saved, shard_count)
        reduced = lax.psum_scatter(
            weight_term(jnp.int32(0), lax.axis_size("shard") * shard_rows).astype(jnp.bfloat16),
            "shard",
            scatter_dimension=0,
            tiled=True,
        ).astype(jnp.float32)
        attn_total = reduced if attn_total is None else attn_total + reduced
    gain_sums = lax.psum((prenorm_total, midnorm_total), ("grp", "shard"))
    gain_share = model_width // shard_count
    prenorm_gradient = lax.dynamic_slice_in_dim(
        gain_sums[0], shard_rank * gain_share, gain_share, 0
    )
    midnorm_gradient = lax.dynamic_slice_in_dim(
        gain_sums[1], shard_rank * gain_share, gain_share, 0
    )
    summed = (
        lax.psum(attn_total.astype(jnp.bfloat16), "grp").astype(jnp.float32),
        lax.psum(gate_total.astype(jnp.bfloat16), "grp").astype(jnp.float32),
        lax.psum(up_total.astype(jnp.bfloat16), "grp").astype(jnp.float32),
        lax.psum(down_total.astype(jnp.bfloat16), "grp").astype(jnp.float32),
    )
    attn_rows = summed[0]
    query_share = query_width // shard_count
    kv_share = kv_width // shard_count
    query_gradient = attn_rows[:query_share]
    key_gradient = attn_rows[query_share : query_share + kv_share]
    value_gradient = attn_rows[query_share + kv_share : query_share + 2 * kv_share]
    out_gradient = attn_rows[query_share + 2 * kv_share :]
    return (
        jnp.stack(mixed_rows),
        jnp.stack(input_rows),
        prenorm_gradient,
        query_gradient,
        key_gradient,
        value_gradient,
        out_gradient,
        midnorm_gradient,
        summed[1],
        summed[2],
        summed[3],
    )


def local_heads(
    tokens,
    lengths,
    prenorm_gain,
    query_weight,
    key_weight,
    value_weight,
    out_weight,
    midnorm_gain,
    gate_weight,
    up_weight,
    down_weight,
    cotangent,
):
    low = jnp.bfloat16
    shard_count = lax.axis_size("shard")
    shard_rank = lax.axis_index("shard")
    seqs, seq_dev, model_width = tokens.shape
    slot_count = seq_dev * shard_count
    own_rows = seqs * seq_dev
    score_scale = 1.0 / math.sqrt(HD)
    pairs = [[2 * pair, 2 * pair + 1] for pair in range(shard_count // 2)]
    half = HD // 2
    upper = shard_rank % 2

    def gather(rows):
        width = rows.shape[-1]
        return lax.all_gather(rows.reshape(seqs, seq_dev, width), "shard", axis=1, tiled=True)

    def scatter(partial):
        return lax.psum_scatter(
            partial.astype(low), "shard", scatter_dimension=1, tiled=True
        ).reshape(own_rows, partial.shape[-1])

    def times(rows, weight):
        return jnp.einsum("sta,ba->stb", rows, weight, preferred_element_type=jnp.float32)

    def into(rows, weight):
        return jnp.einsum("stb,ba->sta", rows, weight, preferred_element_type=jnp.float32)

    def outer(left, right):
        return jnp.einsum("stb,sta->ba", left, right, preferred_element_type=jnp.float32)

    key_pos = jnp.arange(slot_count, dtype=jnp.int32)
    local_pos = shard_rank * seq_dev + jnp.arange(seq_dev, dtype=jnp.int32)
    inverse_freq = theta_base ** (-(jnp.arange(0, HD, 2).astype(jnp.float32) / HD))
    angles = key_pos.astype(jnp.float32)[:, None] * inverse_freq[None, :]
    cosine_table = jnp.concatenate([jnp.cos(angles), jnp.cos(angles)], -1)
    sine_table = jnp.concatenate([jnp.sin(angles), jnp.sin(angles)], -1)

    prenorm_f = lax.all_gather(prenorm_gain, "shard", axis=0, tiled=True).astype(jnp.float32)
    midnorm_f = lax.all_gather(midnorm_gain, "shard", axis=0, tiled=True).astype(jnp.float32)
    valid_rows = (local_pos[None, :] < lengths[:, None]).reshape(own_rows, 1)
    cot_low = jnp.where(valid_rows, cotangent.reshape(own_rows, model_width), jnp.zeros((), low))

    key_head = lax.all_gather(
        key_weight, "shard", axis=0, tiled=True, axis_index_groups=pairs
    )
    value_head = lax.all_gather(
        value_weight, "shard", axis=0, tiled=True, axis_index_groups=pairs
    )

    source = tokens.reshape(own_rows, model_width).astype(jnp.float32)
    scaled_first, inverse_first = norm_forward(source, prenorm_f)
    normed_first = gather(scaled_first.astype(low))
    cot_all = gather(cot_low)

    queries = rotate(times(normed_first, query_weight), cosine_table, sine_table).astype(low)
    keys = rotate(times(normed_first, key_head), cosine_table, sine_table).astype(low)
    values = times(normed_first, value_head).astype(low)
    scores = (
        jnp.einsum("sqd,skd->sqk", queries, keys, preferred_element_type=jnp.float32) * score_scale
    )
    allowed = (key_pos[None, None, :] <= key_pos[None, :, None]) & (
        key_pos[None, None, :] < lengths[:, None, None]
    )
    scores = jnp.where(allowed, scores, masked_value)
    exp_scores = jnp.exp(scores - jnp.max(scores, -1, keepdims=True))
    probs = exp_scores / jnp.sum(exp_scores, -1, keepdims=True)
    probs_low = probs.astype(low)
    attended = jnp.einsum(
        "sqk,skd->sqd", probs_low, values, preferred_element_type=jnp.float32
    ).astype(low)
    middle = source + scatter(into(attended, out_weight)).astype(jnp.float32)
    scaled_second, inverse_second = norm_forward(middle, midnorm_f)
    normed_second = gather(scaled_second.astype(low))

    gate_pre = times(normed_second, gate_weight)
    up_pre = times(normed_second, up_weight)
    sigmoid_gate = jax.nn.sigmoid(gate_pre)
    silu_gate = gate_pre * sigmoid_gate
    hidden = (silu_gate * up_pre).astype(low)
    hidden_grad = times(cot_all, down_weight)
    gate_grad = (
        hidden_grad * up_pre * sigmoid_gate * (1.0 + gate_pre * (1.0 - sigmoid_gate))
    ).astype(low)
    up_grad = (hidden_grad * silu_gate).astype(low)
    second_grad = scatter(into(gate_grad, gate_weight) + into(up_grad, up_weight)).astype(
        jnp.float32
    )
    ffn_part = scatter(into(hidden, down_weight)).astype(jnp.float32)
    mixed = jnp.where(valid_rows, middle + ffn_part, 0.0).astype(low)
    gate_total = lax.psum(outer(gate_grad, normed_second).astype(low), "grp")
    up_total = lax.psum(outer(up_grad, normed_second).astype(low), "grp")
    down_total = lax.psum(outer(hidden, cot_all).astype(low), "grp")

    middle_part, midnorm_part = norm_backward(middle, inverse_second, midnorm_f, second_grad)
    middle_grad = cot_low.astype(jnp.float32) + middle_part
    branch_grad = gather(middle_grad.astype(low))
    attended_grad = times(branch_grad, out_weight).astype(low)
    out_total = outer(attended, branch_grad)
    probs_grad = jnp.einsum(
        "sqd,skd->sqk", attended_grad, values, preferred_element_type=jnp.float32
    )
    inner_sum = jnp.sum(probs * probs_grad, -1, keepdims=True)
    scores_grad = (probs * (probs_grad - inner_sum)).astype(low)
    query_grad = unrotate(
        jnp.einsum("sqk,skd->sqd", scores_grad, keys, preferred_element_type=jnp.float32)
        * score_scale,
        cosine_table,
        sine_table,
    ).astype(low)
    key_grad = unrotate(
        jnp.einsum("sqk,sqd->skd", scores_grad, queries, preferred_element_type=jnp.float32)
        * score_scale,
        cosine_table,
        sine_table,
    ).astype(low)
    value_grad = jnp.einsum(
        "sqk,sqd->skd", probs_low, attended_grad, preferred_element_type=jnp.float32
    ).astype(low)
    first_grad = scatter(
        into(query_grad, query_weight) + into(key_grad, key_head) + into(value_grad, value_head)
    ).astype(jnp.float32)

    def halves(grad):
        first, second = grad[..., :half], grad[..., half:]
        return (
            jnp.where(upper == 0, first, second),
            jnp.where(upper == 0, second, first),
        )

    key_own, key_other = halves(key_grad)
    value_own, value_other = halves(value_grad)
    swaps = [(rank, rank ^ 1) for rank in range(shard_count)]
    swapped = lax.ppermute(jnp.concatenate([key_other, value_other], -1), "shard", swaps)
    key_own = (key_own.astype(jnp.float32) + swapped[..., :half].astype(jnp.float32)).astype(low)
    value_own = (value_own.astype(jnp.float32) + swapped[..., half:].astype(jnp.float32)).astype(
        low
    )
    attn_total = lax.psum(
        jnp.concatenate(
            [
                outer(query_grad, normed_first),
                outer(key_own, normed_first),
                outer(value_own, normed_first),
                out_total,
            ],
            0,
        ).astype(low),
        "grp",
    )
    source_part, prenorm_part = norm_backward(source, inverse_first, prenorm_f, first_grad)
    input_gradient = (middle_grad + source_part).astype(low)

    gain_sums = lax.psum(jnp.stack([prenorm_part, midnorm_part]), ("grp", "shard"))
    gain_share = model_width // shard_count
    gain_own = lax.dynamic_slice_in_dim(gain_sums, shard_rank * gain_share, gain_share, 1)
    f32 = jnp.float32
    share = query_weight.shape[0]
    kv_share = key_weight.shape[0]
    return (
        mixed.reshape(tokens.shape),
        input_gradient.reshape(tokens.shape),
        gain_own[0],
        attn_total[:share].astype(f32),
        attn_total[share : share + kv_share].astype(f32),
        attn_total[share + kv_share : share + 2 * kv_share].astype(f32),
        attn_total[share + 2 * kv_share :].astype(f32),
        gain_own[1],
        gate_total.astype(f32),
        up_total.astype(f32),
        down_total.astype(f32),
    )


def solution(mesh):
    local = local_heads if mesh.shape["shard"] == NH else local_rows
    in_specs = (
        P("grp", "shard", None),
        P("grp"),
        P("shard"),
        P("shard", None),
        P("shard", None),
        P("shard", None),
        P("shard", None),
        P("shard"),
        P("shard", None),
        P("shard", None),
        P("shard", None),
        P("grp", "shard", None),
    )
    out_specs = (
        P("grp", "shard", None),
        P("grp", "shard", None),
        P("shard"),
        P("shard", None),
        P("shard", None),
        P("shard", None),
        P("shard", None),
        P("shard"),
        P("shard", None),
        P("shard", None),
        P("shard", None),
    )
    return jax.shard_map(local, mesh=mesh, in_specs=in_specs, out_specs=out_specs, check_vma=False)
```

```python
import functools
import math

import jax
import jax.numpy as jnp
from jax import lax
from jax.experimental import pallas as pl
from jax.experimental.pallas import tpu as pltpu
from jax.sharding import PartitionSpec as P

MESH = pl.DeviceIdType.MESH
DEPTH = 2

NH = 8
KVH = 4
HD = 256


def greet(me, line, cross):
    z = me // 2
    barrier = pltpu.get_barrier_semaphore()
    def signal(peer):
        pl.semaphore_signal(barrier, inc=1, device_id={"shard": peer}, device_id_type=MESH)
    signal(cross)
    @pl.when(z > 0)
    def _(): signal(me - 2)
    @pl.when(z < line - 1)
    def _(): signal(me + 2)
    ends = jnp.where(z > 0, 1, 0) + jnp.where(z < line - 1, 1, 0)
    pl.semaphore_wait(barrier, 1 + ends)


def gather_kernel(line, split, own_ref, out_ref, local_sem, send_sem, recv_sem):
    me = lax.axis_index("shard")
    z, y = me // 2, lax.rem(me, 2)
    cross = me + 1 - 2 * y
    rows = own_ref.shape[0]
    parts = [pl.ds(0, split), pl.ds(split, rows - split)] if split < rows else [pl.ds(0, rows)]
    greet(me, line, cross)
    keep = pltpu.make_async_copy(own_ref, out_ref.at[me], local_sem)
    keep.start()
    UP, DOWN, CROSS = 0, 1, 2
    def copy(way, origin, part, own=False):
        peer = {UP: me + 2, DOWN: me - 2, CROSS: cross}[way]
        return pltpu.make_async_remote_copy(
            src_ref=own_ref.at[parts[part]] if own else out_ref.at[origin, parts[part]],
            dst_ref=out_ref.at[origin, parts[part]],
            send_sem=send_sem.at[way, origin, part],
            recv_sem=recv_sem.at[origin, part],
            device_id={"shard": peer}, device_id_type=MESH)
    def arrived(origin, part):
        copy(CROSS, origin, part).wait_recv()
    sent = []
    def send(cond, way, origin, part, own=False):
        c = copy(way, origin, part, own)
        if cond is None:
            c.start()
        else:
            pl.when(cond)(c.start)
        sent.append((cond, way, origin, part, own))
    has_b = len(parts) > 1
    if has_b:
        send(None, CROSS, me, 1, True)
    send(None, CROSS, me, 0, True)
    send(z < line - 1, UP, me, 0, True)
    send(z > 0, DOWN, me, 0, True)
    if has_b:
        send(z < line - 1, UP, me, 1, True)
        send(z > 0, DOWN, me, 1, True)
        arrived(cross, 1)
        send(z < line - 1, UP, cross, 1)
        send(z > 0, DOWN, cross, 1)
    for k in range(1, line):
        for part in range(len(parts)):
            for other in ([False] if part == 0 else [False, True]):
                for sign in (-1, 1):
                    origin = me + 2 * k * sign + (1 - 2 * y if other else 0)
                    there = z >= k if sign < 0 else z + k < line
                    way = UP if sign < 0 else DOWN
                    more = (there & (z < line - 1)) if sign < 0 else (there & (z > 0))
                    pl.when(there)(functools.partial(arrived, origin, part))
                    send(more, way, origin, part)
                    if part == 0:
                        send(there, CROSS, origin, 0)
    for k in range(line):
        arrived(2 * k + 1 - y, 0)
    for cond, way, origin, part, own in sent:
        c = copy(way, origin, part, own)
        if cond is None:
            c.wait_send()
        else:
            pl.when(cond)(c.wait_send)
    keep.wait()

def gather(own, count, ident, space=pltpu.VMEM, split=112):
    rows, width = own.shape
    return pl.pallas_call(
        functools.partial(gather_kernel, count // 2, split),
        out_shape=jax.ShapeDtypeStruct((count, rows, width), own.dtype),
        in_specs=[pl.BlockSpec(memory_space=space)],
        out_specs=pl.BlockSpec(memory_space=space),
        scratch_shapes=[pltpu.SemaphoreType.DMA, pltpu.SemaphoreType.DMA((3, count, 2)), pltpu.SemaphoreType.DMA((count, 2))],
        compiler_params=pltpu.CompilerParams(collective_id=ident, has_side_effects=True),
        name=f"gather{ident}")(own)

def total_into(dst, *srcs):
    rows = dst.shape[0]
    step = 16
    @pl.loop(0, rows // step)
    def _(i):
        at = pl.ds(pl.multiple_of(i * step, step), step)
        v = srcs[0][at].astype(jnp.float32)
        for s in srcs[1:]:
            v = v + s[at].astype(jnp.float32)
        dst[at] = v.astype(dst.dtype)

def reduce_kernel(line, split, in_ref, out_ref, cross_in, up_in, down_in, up_out, down_out, bup_in, bdn_in, bup_out, bdn_out, bx_out, bx_in, send_sem, recv_sem):
    me = lax.axis_index("shard")
    z, y = me // 2, lax.rem(me, 2)
    cross = me + 1 - 2 * y
    rows = in_ref.shape[1]
    A = pl.ds(0, split); B = pl.ds(split, rows - split)
    has_b = rows > split
    greet(me, line, cross)
    UP, DOWN, CROSS, BUP0, BUP1, BDN0, BDN1, BX = range(8)
    def desc(way, slot, src, dst, peer):
        return pltpu.make_async_remote_copy(src_ref=src, dst_ref=dst, send_sem=send_sem.at[way, slot], recv_sem=recv_sem.at[way, slot], device_id={"shard": peer}, device_id_type=MESH)
    def cross_copy(dest):
        return desc(CROSS, dest, in_ref.at[2 * dest + 1 - y, A], cross_in.at[dest], cross)
    def up_copy(dest, src=None):
        return desc(UP, dest, up_out.at[dest] if src is None else src, up_in.at[dest], me + 2)
    def down_copy(dest, src=None):
        return desc(DOWN, dest, down_out.at[dest] if src is None else src, down_in.at[dest], me - 2)
    def b_copy(up, dest, o, src=None):
        buf_o, buf_i = (bup_out, bup_in) if up else (bdn_out, bdn_in)
        return desc((BUP0 if up else BDN0) + o, dest, buf_o.at[dest, o] if src is None else src, buf_i.at[dest, o], me + 2 if up else me - 2)
    def bx_copy():
        return desc(BX, 0, bx_out, bx_in, cross)
    def col(o):
        return y if o == 0 else 1 - y
    tables = []
    for zz in range(line):
        seq = []
        for k in range(line - 1, -1, -1):
            for d in ((zz + k, zz - k) if k else (zz,)):
                if 0 <= d < line:
                    seq.append(d)
        tables.append(seq)
    def nth(i):
        d = jnp.int32(tables[0][i])
        for zz in range(1, line):
            d = jnp.where(z == zz, tables[zz][i], d)
        return d
    order = [nth(i) for i in range(line)]
    for i in range(DEPTH):
        cross_copy(order[i]).start()
    def b_hop(up, dest):
        first = (z == 0) if up else (z == line - 1)
        for o in (1, 0):
            mine = in_ref.at[2 * dest + col(o), B]
            @pl.when(first)
            def _():
                b_copy(up, dest, o, mine).start()
            @pl.when(jnp.logical_not(first))
            def _():
                b_copy(up, dest, o).wait_recv()
                buf_o, buf_i = (bup_out, bup_in) if up else (bdn_out, bdn_in)
                total_into(buf_o.at[dest, o], mine, buf_i.at[dest, o])
                b_copy(up, dest, o).start()
    def a_hop(up, dest):
        first = (z == 0) if up else (z == line - 1)
        buf_o, buf_i = (up_out, up_in) if up else (down_out, down_in)
        c = (up_copy if up else down_copy)(dest)
        mine = in_ref.at[2 * dest + y, A]
        @pl.when(first)
        def _():
            total_into(buf_o.at[dest], mine, cross_in.at[dest])
        @pl.when(jnp.logical_not(first))
        def _():
            c.wait_recv()
            total_into(buf_o.at[dest], mine, cross_in.at[dest], buf_i.at[dest])
        c.start()
    for i in range(line - 1):
        if has_b:
            pl.when(order[i] > z)(lambda: b_hop(True, order[i]))
            pl.when(order[i] < z)(lambda: b_hop(False, order[i]))
    for i in range(line - 1):
        cross_copy(order[i]).wait_recv()
        if i + DEPTH < line:
            cross_copy(order[i + DEPTH]).start()
        pl.when(order[i] > z)(lambda: a_hop(True, order[i]))
        pl.when(order[i] < z)(lambda: a_hop(False, order[i]))
    low_end, high_end = z == 0, z == line - 1
    def finish(dst, mine, ups, downs):
        @pl.when(low_end)
        def _(): total_into(dst, *mine, downs)
        @pl.when(high_end)
        def _(): total_into(dst, *mine, ups)
        @pl.when(jnp.logical_not(low_end | high_end))
        def _(): total_into(dst, *mine, ups, downs)
    if has_b:
        for o in (1, 0):
            pl.when(jnp.logical_not(low_end))(lambda: b_copy(True, z, o).wait_recv())
            pl.when(jnp.logical_not(high_end))(lambda: b_copy(False, z, o).wait_recv())
            if o:
                finish(bx_out, (in_ref.at[2 * z + col(o), B],), bup_in.at[z, o], bdn_in.at[z, o])
                bx_copy().start()
        bx_copy().wait_recv()
        finish(out_ref.at[B], (in_ref.at[me, B], bx_in), bup_in.at[z, 0], bdn_in.at[z, 0])
    cross_copy(z).wait_recv()
    pl.when(jnp.logical_not(low_end))(lambda: up_copy(z).wait_recv())
    pl.when(jnp.logical_not(high_end))(lambda: down_copy(z).wait_recv())
    finish(out_ref.at[A], (in_ref.at[me, A], cross_in.at[z]), up_in.at[z], down_in.at[z])
    if has_b:
        bx_copy().wait_send()
    for dest in range(line):
        cross_copy(dest).wait_send()
        @pl.when(dest > z)
        def _():
            up_copy(dest).wait_send()
            if has_b:
                b_copy(True, dest, 0).wait_send(); b_copy(True, dest, 1).wait_send()
        @pl.when(dest < z)
        def _():
            down_copy(dest).wait_send()
            if has_b:
                b_copy(False, dest, 0).wait_send(); b_copy(False, dest, 1).wait_send()

def reduce(parts, ident, split=112, out_dtype=jnp.float32):
    count, rows, width = parts.shape
    line = count // 2
    V = pltpu.VMEM; d = parts.dtype
    b = max(rows - split, 16)
    return pl.pallas_call(
        functools.partial(reduce_kernel, line, split),
        out_shape=jax.ShapeDtypeStruct((rows, width), out_dtype),
        in_specs=[pl.BlockSpec(memory_space=V)],
        out_specs=pl.BlockSpec(memory_space=V),
        scratch_shapes=[V((line, split, width), d)] * 5 + [V((line, 2, b, width), d)] * 4 + [V((b, width), d)] * 2 + [pltpu.SemaphoreType.DMA((8, line)), pltpu.SemaphoreType.DMA((8, line))],
        compiler_params=pltpu.CompilerParams(collective_id=ident, has_side_effects=True),
        name=f"reduce{ident}")(parts)


def everyone(axis, count, me, barrier):
    for step in range(1, count):
        pl.semaphore_signal(
            barrier, inc=1, device_id={axis: lax.rem(me + step, count)}, device_id_type=MESH
        )
    pl.semaphore_wait(barrier, count - 1)


def small_gather_kernel(count, own_ref, out_ref, send_sem, recv_sem):
    me = lax.axis_index("shard")
    everyone("shard", count, me, pltpu.get_barrier_semaphore())

    def copy(step, peer, origin):
        return pltpu.make_async_remote_copy(
            src_ref=own_ref,
            dst_ref=out_ref.at[origin],
            send_sem=send_sem.at[step],
            recv_sem=recv_sem.at[step],
            device_id={"shard": peer},
            device_id_type=MESH,
        )

    for step in range(1, count):
        copy(step, lax.rem(me + step, count), me).start()
    out_ref[me] = own_ref[...]
    for step in range(1, count):
        c = copy(step, me, lax.rem(me + count - step, count))
        c.wait_send()
        c.wait_recv()


def small_gather(own, count, ident):
    return pl.pallas_call(
        functools.partial(small_gather_kernel, count),
        out_shape=jax.ShapeDtypeStruct((count,) + own.shape, own.dtype),
        in_specs=[pl.BlockSpec(memory_space=pltpu.VMEM)],
        out_specs=pl.BlockSpec(memory_space=pltpu.VMEM),
        scratch_shapes=[pltpu.SemaphoreType.DMA((count,)), pltpu.SemaphoreType.DMA((count,))],
        compiler_params=pltpu.CompilerParams(collective_id=ident, has_side_effects=True),
        name="small_gather",
    )(own)


def gain_sum_kernel(count, groups, parts_ref, out_ref, first, held, second, send_sem, recv_sem, send2, recv2):
    me = lax.axis_index("shard")
    group = lax.axis_index("grp")
    barrier = pltpu.get_barrier_semaphore()
    for step in range(1, count):
        pl.semaphore_signal(
            barrier, inc=1, device_id={"shard": lax.rem(me + step, count)}, device_id_type=MESH
        )
    for step in range(1, groups):
        pl.semaphore_signal(
            barrier, inc=1, device_id={"grp": lax.rem(group + step, groups)}, device_id_type=MESH
        )
    pl.semaphore_wait(barrier, count + groups - 2)

    def copy(step, peer, origin):
        return pltpu.make_async_remote_copy(
            src_ref=parts_ref.at[peer],
            dst_ref=first.at[origin],
            send_sem=send_sem.at[step],
            recv_sem=recv_sem.at[step],
            device_id={"shard": peer},
            device_id_type=MESH,
        )

    def copy2(step, peer, origin):
        return pltpu.make_async_remote_copy(
            src_ref=held,
            dst_ref=second.at[origin],
            send_sem=send2.at[step],
            recv_sem=recv2.at[step],
            device_id={"grp": peer},
            device_id_type=MESH,
        )

    for step in range(1, count):
        copy(step, lax.rem(me + step, count), me).start()
    first[me] = parts_ref[me]
    for step in range(1, count):
        copy(step, me, lax.rem(me + count - step, count)).wait_recv()
    total = first[0]
    for peer in range(1, count):
        total = total + first[peer]
    held[...] = total
    second[group] = total
    for step in range(1, groups):
        copy2(step, lax.rem(group + step, groups), group).start()
    for step in range(1, groups):
        copy2(step, group, lax.rem(group + groups - step, groups)).wait_recv()
    total = second[0]
    for peer in range(1, groups):
        total = total + second[peer]
    out_ref[...] = total
    for step in range(1, count):
        copy(step, lax.rem(me + step, count), me).wait_send()
    for step in range(1, groups):
        copy2(step, lax.rem(group + step, groups), group).wait_send()


def gain_sum(parts, groups, ident):
    count = parts.shape[0]
    shape = parts.shape[1:]
    vmem = pltpu.VMEM
    dma = pltpu.SemaphoreType.DMA
    return pl.pallas_call(
        functools.partial(gain_sum_kernel, count, groups),
        out_shape=jax.ShapeDtypeStruct(shape, parts.dtype),
        in_specs=[pl.BlockSpec(memory_space=vmem)],
        out_specs=pl.BlockSpec(memory_space=vmem),
        scratch_shapes=[
            vmem((count,) + shape, parts.dtype),
            vmem(shape, parts.dtype),
            vmem((groups,) + shape, parts.dtype),
            dma((count,)),
            dma((count,)),
            dma((groups,)),
            dma((groups,)),
        ],
        compiler_params=pltpu.CompilerParams(collective_id=ident, has_side_effects=True),
        name="gain_sum",
    )(parts)


def group_total(part):
    rank = lax.axis_index("grp")
    core = lax.rem(rank, 2)
    rows = part.shape[0] // 2
    cores = [(0, 1), (1, 0), (2, 3), (3, 2)]
    chips = [(0, 2), (2, 0), (1, 3), (3, 1)]
    f32 = jnp.float32
    first, second = part[:rows], part[rows:]
    mine = jnp.where(core == 0, first, second)
    other = lax.ppermute(jnp.where(core == 0, second, first), "grp", cores)
    pair = (mine.astype(f32) + other.astype(f32)).astype(part.dtype)
    whole = (pair.astype(f32) + lax.ppermute(pair, "grp", chips).astype(f32)).astype(part.dtype)
    swapped = lax.ppermute(whole, "grp", cores)
    return jnp.concatenate(
        [jnp.where(core == 0, whole, swapped), jnp.where(core == 0, swapped, whole)], 0
    ).astype(f32)


epsilon = 1e-06
theta_base = 1000042.0
masked_value = -1e30


def turned(source):
    half_width = source.shape[-1] // 2
    return jnp.concatenate([-source[..., half_width:], source[..., :half_width]], -1)


def rotate(source, cosine_table, sine_table):
    return source * cosine_table + turned(source) * sine_table


def unrotate(source, cosine_table, sine_table):
    return source * cosine_table - turned(source) * sine_table


def norm_forward(source, norm_gain):
    inverse = lax.rsqrt(jnp.mean(source * source, -1, keepdims=True) + epsilon)
    return (source * inverse * norm_gain, inverse)


def norm_backward(source, inverse, norm_gain, grad_out):
    weighted = grad_out * norm_gain
    inner_sum = jnp.sum(weighted * source, -1, keepdims=True)
    grad_in = (
        inverse * weighted - source * inverse * inverse * inverse * inner_sum / source.shape[-1]
    )
    return (grad_in, jnp.sum(grad_out * source * inverse, 0))


def weight_terms(normed, query_grad, key_grad, value_grad, attended, branch_grad, shard_count):
    token_count, model_width = normed.shape
    query_share = query_grad.shape[1] // shard_count
    kv_share = key_grad.shape[1] // shard_count
    shard_rows = 2 * query_share + 2 * kv_share

    def weight_term(first_row, row_count):
        blocks = row_count // shard_rows

        def columns(matrix, share_cols):
            return matrix.reshape(token_count, blocks, share_cols)

        part_query = jnp.einsum(
            "tmr,td->mrd",
            columns(query_grad, query_share),
            normed,
            preferred_element_type=jnp.float32,
        )
        part_key = jnp.einsum(
            "tmr,td->mrd", columns(key_grad, kv_share), normed, preferred_element_type=jnp.float32
        )
        part_value = jnp.einsum(
            "tmr,td->mrd", columns(value_grad, kv_share), normed, preferred_element_type=jnp.float32
        )
        part_out = jnp.einsum(
            "tmr,td->mrd",
            columns(attended, query_share),
            branch_grad,
            preferred_element_type=jnp.float32,
        )
        return jnp.concatenate([part_query, part_key, part_value, part_out], 1).reshape(
            row_count, model_width
        )

    return (weight_term, shard_rows)


def local_rows(
    tokens,
    lengths,
    prenorm_gain,
    query_weight,
    key_weight,
    value_weight,
    out_weight,
    midnorm_gain,
    gate_weight,
    up_weight,
    down_weight,
    cotangent,
):
    shard_count = lax.axis_size("shard")
    shard_rank = lax.axis_index("shard")
    micro_count, seq_dev, model_width = tokens.shape
    slot_count = seq_dev * shard_count
    repeat_heads = NH // KVH
    query_width = NH * HD
    kv_width = KVH * HD
    score_scale = 1.0 / math.sqrt(HD)
    local_pos = shard_rank * seq_dev + jnp.arange(seq_dev, dtype=jnp.int32)
    key_pos = jnp.arange(slot_count, dtype=jnp.int32)
    inverse_freq = theta_base ** (-(jnp.arange(0, HD, 2).astype(jnp.float32) / HD))
    angles = local_pos.astype(jnp.float32)[:, None] * inverse_freq[None, :]
    cosine_table = jnp.concatenate([jnp.cos(angles), jnp.cos(angles)], -1)[:, None, :]
    sine_table = jnp.concatenate([jnp.sin(angles), jnp.sin(angles)], -1)[:, None, :]
    gate_total = jnp.zeros(gate_weight.shape, jnp.float32)
    up_total = jnp.zeros(up_weight.shape, jnp.float32)
    down_total = jnp.zeros(down_weight.shape, jnp.float32)
    prenorm_total = jnp.zeros((model_width,), jnp.float32)
    midnorm_total = jnp.zeros((model_width,), jnp.float32)
    attn_total = None
    mixed_rows = []
    input_rows = []
    for micro_index in range(micro_count):
        gathered = (
            lax.all_gather(query_weight, "shard", axis=0, tiled=True),
            lax.all_gather(key_weight, "shard", axis=0, tiled=True),
            lax.all_gather(value_weight, "shard", axis=0, tiled=True),
            lax.all_gather(prenorm_gain, "shard", axis=0, tiled=True),
            lax.all_gather(midnorm_gain, "shard", axis=0, tiled=True),
        )
        query_full, key_full, value_full, prenorm_full, midnorm_full = gathered
        prenorm_f = prenorm_full.astype(jnp.float32)
        midnorm_f = midnorm_full.astype(jnp.float32)
        source = tokens[micro_index].astype(jnp.float32)
        length_now = lengths[micro_index]
        valid_rows = local_pos < length_now
        scaled_first, inverse_first = norm_forward(source, prenorm_f)
        normed_first = scaled_first.astype(jnp.bfloat16)
        query_pre = jnp.einsum(
            "sd,qd->sq", normed_first, query_full, preferred_element_type=jnp.float32
        ).reshape(seq_dev, NH, HD)
        key_pre = jnp.einsum(
            "sd,qd->sq", normed_first, key_full, preferred_element_type=jnp.float32
        ).reshape(seq_dev, KVH, HD)
        value_pre = jnp.einsum(
            "sd,qd->sq", normed_first, value_full, preferred_element_type=jnp.float32
        )
        query_rot = rotate(query_pre, cosine_table, sine_table).astype(jnp.bfloat16)
        key_rot = rotate(key_pre, cosine_table, sine_table).astype(jnp.bfloat16)
        key_value = jnp.concatenate(
            [key_rot.reshape(seq_dev, kv_width), value_pre.astype(jnp.bfloat16)], 1
        )
        kv_all = lax.all_gather(key_value, "shard", axis=0, tiled=True)
        keys_all = kv_all[:, :kv_width].reshape(slot_count, KVH, HD)
        values_all = kv_all[:, kv_width:].reshape(slot_count, KVH, HD)
        query_group = query_rot.reshape(seq_dev, KVH, repeat_heads, HD)
        scores = (
            jnp.einsum("skrd,tkd->krst", query_group, keys_all, preferred_element_type=jnp.float32)
            * score_scale
        )
        allowed = (key_pos[None, :] <= local_pos[:, None]) & (key_pos[None, :] < length_now)
        scores = jnp.where(allowed, scores, masked_value)
        row_max = jnp.max(scores, -1, keepdims=True)
        exp_scores = jnp.exp(scores - row_max)
        attention_probs = exp_scores / jnp.sum(exp_scores, -1, keepdims=True)
        probs_low = attention_probs.astype(jnp.bfloat16)
        attended = (
            jnp.einsum("krst,tkd->skrd", probs_low, values_all, preferred_element_type=jnp.float32)
            .astype(jnp.bfloat16)
            .reshape(seq_dev, query_width)
        )
        branch = jnp.dot(
            attended,
            lax.all_gather(out_weight, "shard", axis=0, tiled=True),
            preferred_element_type=jnp.float32,
        )
        middle = source + branch
        scaled_second, inverse_second = norm_forward(middle, midnorm_f)
        normed_second = scaled_second.astype(jnp.bfloat16)
        normed_all = lax.all_gather(normed_second, "shard", axis=0, tiled=True)
        gate_pre = jnp.einsum(
            "sd,fd->sf", normed_all, gate_weight, preferred_element_type=jnp.float32
        )
        up_pre = jnp.einsum("sd,fd->sf", normed_all, up_weight, preferred_element_type=jnp.float32)
        sigmoid_gate = jax.nn.sigmoid(gate_pre)
        silu_gate = gate_pre * sigmoid_gate
        hidden = (silu_gate * up_pre).astype(jnp.bfloat16)
        ffn_part = lax.psum_scatter(
            jnp.dot(hidden, down_weight, preferred_element_type=jnp.float32).astype(jnp.bfloat16),
            "shard",
            scatter_dimension=0,
            tiled=True,
        ).astype(jnp.float32)
        mixed_rows.append(
            jnp.where(valid_rows[:, None], middle + ffn_part, 0.0).astype(jnp.bfloat16)
        )
        cot_low = jnp.where(
            valid_rows[:, None], cotangent[micro_index], jnp.zeros_like(cotangent[micro_index])
        )
        cot_all = lax.all_gather(cot_low, "shard", axis=0, tiled=True)
        hidden_grad = jnp.einsum(
            "sd,fd->sf", cot_all, down_weight, preferred_element_type=jnp.float32
        )
        down_total = down_total + jnp.einsum(
            "sf,sd->fd", hidden, cot_all, preferred_element_type=jnp.float32
        )
        gate_grad = (
            hidden_grad * up_pre * sigmoid_gate * (1.0 + gate_pre * (1.0 - sigmoid_gate))
        ).astype(jnp.bfloat16)
        up_grad = (hidden_grad * silu_gate).astype(jnp.bfloat16)
        gate_total = gate_total + jnp.einsum(
            "sf,sd->fd", gate_grad, normed_all, preferred_element_type=jnp.float32
        )
        up_total = up_total + jnp.einsum(
            "sf,sd->fd", up_grad, normed_all, preferred_element_type=jnp.float32
        )
        second_grad = lax.psum_scatter(
            jnp.dot(gate_grad, gate_weight, preferred_element_type=jnp.float32)
            + jnp.dot(up_grad, up_weight, preferred_element_type=jnp.float32),
            "shard",
            scatter_dimension=0,
            tiled=True,
        )
        middle_part, midnorm_part = norm_backward(middle, inverse_second, midnorm_f, second_grad)
        middle_grad = cot_low.astype(jnp.float32) + middle_part
        midnorm_total = midnorm_total + midnorm_part
        branch_grad = middle_grad.astype(jnp.bfloat16)
        attended_grad = jnp.einsum(
            "sd,qd->sq",
            branch_grad,
            lax.all_gather(out_weight, "shard", axis=0, tiled=True),
            preferred_element_type=jnp.float32,
        ).astype(jnp.bfloat16)
        attended_group = attended_grad.reshape(seq_dev, KVH, repeat_heads, HD)
        probs_grad = jnp.einsum(
            "skrd,tkd->krst", attended_group, values_all, preferred_element_type=jnp.float32
        )
        inner_sum = jnp.sum(attention_probs * probs_grad, -1, keepdims=True)
        scores_grad = (attention_probs * (probs_grad - inner_sum)).astype(jnp.bfloat16)
        query_rot_grad = (
            jnp.einsum(
                "krst,tkd->skrd", scores_grad, keys_all, preferred_element_type=jnp.float32
            ).reshape(seq_dev, NH, HD)
            * score_scale
        )
        query_grad = (
            unrotate(query_rot_grad, cosine_table, sine_table)
            .astype(jnp.bfloat16)
            .reshape(seq_dev, query_width)
        )
        row_count = lax.axis_size("shard") * seq_dev
        key_part = (
            jnp.einsum(
                "krst,skrd->tkd", scores_grad, query_group, preferred_element_type=jnp.float32
            )
            * score_scale
        )
        value_part = jnp.einsum(
            "krst,skrd->tkd", probs_low, attended_group, preferred_element_type=jnp.float32
        )
        kv_grad = lax.psum_scatter(
            jnp.concatenate(
                [key_part.reshape(row_count, kv_width), value_part.reshape(row_count, kv_width)], 1
            ).astype(jnp.bfloat16),
            "shard",
            scatter_dimension=0,
            tiled=True,
        ).astype(jnp.float32)
        key_grad = (
            unrotate(kv_grad[:, :kv_width].reshape(seq_dev, KVH, HD), cosine_table, sine_table)
            .astype(jnp.bfloat16)
            .reshape(seq_dev, kv_width)
        )
        value_grad = kv_grad[:, kv_width:].astype(jnp.bfloat16)
        first_grad = jnp.einsum(
            "sq,qd->sd", query_grad, query_full, preferred_element_type=jnp.float32
        )
        first_grad = first_grad + jnp.einsum(
            "sq,qd->sd", key_grad, key_full, preferred_element_type=jnp.float32
        )
        first_grad = first_grad + jnp.einsum(
            "sq,qd->sd", value_grad, value_full, preferred_element_type=jnp.float32
        )
        source_part, prenorm_part = norm_backward(source, inverse_first, prenorm_f, first_grad)
        input_rows.append((middle_grad + source_part).astype(jnp.bfloat16))
        prenorm_total = prenorm_total + prenorm_part
        saved = (normed_first, query_grad, key_grad, value_grad, attended, branch_grad)
        weight_term, shard_rows = weight_terms(*saved, shard_count)
        reduced = lax.psum_scatter(
            weight_term(jnp.int32(0), lax.axis_size("shard") * shard_rows).astype(jnp.bfloat16),
            "shard",
            scatter_dimension=0,
            tiled=True,
        ).astype(jnp.float32)
        attn_total = reduced if attn_total is None else attn_total + reduced
    gain_sums = lax.psum((prenorm_total, midnorm_total), ("grp", "shard"))
    gain_share = model_width // shard_count
    prenorm_gradient = lax.dynamic_slice_in_dim(
        gain_sums[0], shard_rank * gain_share, gain_share, 0
    )
    midnorm_gradient = lax.dynamic_slice_in_dim(
        gain_sums[1], shard_rank * gain_share, gain_share, 0
    )
    summed = (
        lax.psum(attn_total.astype(jnp.bfloat16), "grp").astype(jnp.float32),
        lax.psum(gate_total.astype(jnp.bfloat16), "grp").astype(jnp.float32),
        lax.psum(up_total.astype(jnp.bfloat16), "grp").astype(jnp.float32),
        lax.psum(down_total.astype(jnp.bfloat16), "grp").astype(jnp.float32),
    )
    attn_rows = summed[0]
    query_share = query_width // shard_count
    kv_share = kv_width // shard_count
    query_gradient = attn_rows[:query_share]
    key_gradient = attn_rows[query_share : query_share + kv_share]
    value_gradient = attn_rows[query_share + kv_share : query_share + 2 * kv_share]
    out_gradient = attn_rows[query_share + 2 * kv_share :]
    return (
        jnp.stack(mixed_rows),
        jnp.stack(input_rows),
        prenorm_gradient,
        query_gradient,
        key_gradient,
        value_gradient,
        out_gradient,
        midnorm_gradient,
        summed[1],
        summed[2],
        summed[3],
    )


def local_heads(
    tokens,
    lengths,
    prenorm_gain,
    query_weight,
    key_weight,
    value_weight,
    out_weight,
    midnorm_gain,
    gate_weight,
    up_weight,
    down_weight,
    cotangent,
):
    low = jnp.bfloat16
    shard_count = lax.axis_size("shard")
    shard_rank = lax.axis_index("shard")
    seqs, seq_dev, model_width = tokens.shape
    slot_count = seq_dev * shard_count
    own_rows = seqs * seq_dev
    score_scale = 1.0 / math.sqrt(HD)
    half = HD // 2
    upper = shard_rank % 2

    def all_rows(rows, ident):
        return gather(rows, shard_count, ident, pl.ANY).reshape(shard_count * own_rows, -1)

    def scatter(partial, ident):
        return reduce(partial.astype(low).reshape(shard_count, own_rows, -1), ident)

    def by_seq(rows):
        width = rows.shape[-1]
        return (
            rows.reshape(shard_count, seqs, seq_dev, width)
            .transpose(1, 0, 2, 3)
            .reshape(seqs, slot_count, width)
        )

    def by_device(rows):
        width = rows.shape[-1]
        return (
            rows.reshape(seqs, shard_count, seq_dev, width)
            .transpose(1, 0, 2, 3)
            .reshape(shard_count * own_rows, width)
        )

    def times(rows, weight):
        return jnp.einsum("ta,ba->tb", rows, weight, preferred_element_type=jnp.float32)

    def into(rows, weight):
        return jnp.dot(rows, weight, preferred_element_type=jnp.float32)

    def outer(left, right):
        return jnp.einsum("tb,ta->ba", left, right, preferred_element_type=jnp.float32)

    key_pos = jnp.arange(slot_count, dtype=jnp.int32)
    local_pos = shard_rank * seq_dev + jnp.arange(seq_dev, dtype=jnp.int32)
    inverse_freq = theta_base ** (-(jnp.arange(0, HD, 2).astype(jnp.float32) / HD))
    angles = key_pos.astype(jnp.float32)[:, None] * inverse_freq[None, :]
    cosine_table = jnp.concatenate([jnp.cos(angles), jnp.cos(angles)], -1)
    sine_table = jnp.concatenate([jnp.sin(angles), jnp.sin(angles)], -1)

    gains = jnp.broadcast_to(
        jnp.stack([prenorm_gain, midnorm_gain])[:, None, :], (2, 8, prenorm_gain.shape[0])
    ).reshape(16, -1)
    gains = small_gather(gains, shard_count, 1).astype(jnp.float32)
    prenorm_f = gains[:, 0].reshape(-1)
    midnorm_f = gains[:, 8].reshape(-1)
    valid_rows = (local_pos[None, :] < lengths[:, None]).reshape(own_rows, 1)
    cot_low = jnp.where(valid_rows, cotangent.reshape(own_rows, model_width), jnp.zeros((), low))

    swaps = [(rank, rank ^ 1) for rank in range(shard_count)]
    swapped = lax.ppermute(jnp.concatenate([key_weight, value_weight], 0), "shard", swaps)
    key_swap, value_swap = swapped[:half], swapped[half:]

    def whole_head(own, other):
        return jnp.concatenate(
            [jnp.where(upper == 0, own, other), jnp.where(upper == 0, other, own)], 0
        )

    key_head = whole_head(key_weight, key_swap)
    value_head = whole_head(value_weight, value_swap)

    source = tokens.reshape(own_rows, model_width).astype(jnp.float32)
    scaled_first, inverse_first = norm_forward(source, prenorm_f)
    normed_first = all_rows(scaled_first.astype(low), 2)
    cot_all = all_rows(cot_low, 3)

    queries = rotate(by_seq(times(normed_first, query_weight)), cosine_table, sine_table).astype(low)
    keys = rotate(by_seq(times(normed_first, key_head)), cosine_table, sine_table).astype(low)
    values = by_seq(times(normed_first, value_head).astype(low))
    scores = (
        jnp.einsum("sqd,skd->sqk", queries, keys, preferred_element_type=jnp.float32) * score_scale
    )
    allowed = (key_pos[None, None, :] <= key_pos[None, :, None]) & (
        key_pos[None, None, :] < lengths[:, None, None]
    )
    scores = jnp.where(allowed, scores, masked_value)
    exp_scores = jnp.exp(scores - jnp.max(scores, -1, keepdims=True))
    probs = exp_scores / jnp.sum(exp_scores, -1, keepdims=True)
    probs_low = probs.astype(low)
    attended = by_device(
        jnp.einsum(
            "sqk,skd->sqd", probs_low, values, preferred_element_type=jnp.float32
        ).astype(low)
    )
    middle = source + scatter(into(attended, out_weight), 4)
    scaled_second, inverse_second = norm_forward(middle, midnorm_f)
    normed_second = all_rows(scaled_second.astype(low), 5)

    gate_pre = times(normed_second, gate_weight)
    up_pre = times(normed_second, up_weight)
    sigmoid_gate = jax.nn.sigmoid(gate_pre)
    silu_gate = gate_pre * sigmoid_gate
    hidden = (silu_gate * up_pre).astype(low)
    hidden_grad = times(cot_all, down_weight)
    gate_grad = (
        hidden_grad * up_pre * sigmoid_gate * (1.0 + gate_pre * (1.0 - sigmoid_gate))
    ).astype(low)
    up_grad = (hidden_grad * silu_gate).astype(low)
    second_grad = scatter(into(gate_grad, gate_weight) + into(up_grad, up_weight), 6)
    ffn_part = scatter(into(hidden, down_weight), 7)
    mixed = jnp.where(valid_rows, middle + ffn_part, 0.0).astype(low)
    gate_total = group_total(outer(gate_grad, normed_second).astype(low))
    up_total = group_total(outer(up_grad, normed_second).astype(low))
    down_total = group_total(outer(hidden, cot_all).astype(low))

    middle_part, midnorm_part = norm_backward(middle, inverse_second, midnorm_f, second_grad)
    middle_grad = cot_low.astype(jnp.float32) + middle_part
    branch_grad = all_rows(middle_grad.astype(low), 8)
    attended_grad = by_seq(times(branch_grad, out_weight).astype(low))
    out_total = outer(attended, branch_grad)
    probs_grad = jnp.einsum(
        "sqd,skd->sqk", attended_grad, values, preferred_element_type=jnp.float32
    )
    inner_sum = jnp.sum(probs * probs_grad, -1, keepdims=True)
    scores_grad = (probs * (probs_grad - inner_sum)).astype(low)
    query_grad = by_device(unrotate(
        jnp.einsum("sqk,skd->sqd", scores_grad, keys, preferred_element_type=jnp.float32)
        * score_scale,
        cosine_table,
        sine_table,
    ).astype(low))
    key_grad = by_device(unrotate(
        jnp.einsum("sqk,sqd->skd", scores_grad, queries, preferred_element_type=jnp.float32)
        * score_scale,
        cosine_table,
        sine_table,
    ).astype(low))
    value_grad = by_device(jnp.einsum(
        "sqk,sqd->skd", probs_low, attended_grad, preferred_element_type=jnp.float32
    ).astype(low))
    first_grad = scatter(
        into(query_grad, query_weight) + into(key_grad, key_head) + into(value_grad, value_head),
        9,
    )

    def halves(grad):
        first, second = grad[..., :half], grad[..., half:]
        return (
            jnp.where(upper == 0, first, second),
            jnp.where(upper == 0, second, first),
        )

    key_own, key_other = halves(key_grad)
    value_own, value_other = halves(value_grad)
    swapped = lax.ppermute(jnp.concatenate([key_other, value_other], -1), "shard", swaps)
    key_own = (key_own.astype(jnp.float32) + swapped[..., :half].astype(jnp.float32)).astype(low)
    value_own = (value_own.astype(jnp.float32) + swapped[..., half:].astype(jnp.float32)).astype(
        low
    )
    out_total = group_total(out_total.astype(low))
    attn_total = group_total(
        jnp.concatenate(
            [
                outer(query_grad, normed_first),
                outer(key_own, normed_first),
                outer(value_own, normed_first),
            ],
            0,
        ).astype(low)
    )
    source_part, prenorm_part = norm_backward(source, inverse_first, prenorm_f, first_grad)
    input_gradient = (middle_grad + source_part).astype(low)

    gain_parts = jnp.stack([prenorm_part, midnorm_part]).reshape(2, shard_count, 1, -1)
    gain_parts = jnp.broadcast_to(
        gain_parts.transpose(1, 0, 2, 3), (shard_count, 2, 8, gain_parts.shape[-1])
    )
    gain_own = gain_sum(gain_parts, lax.axis_size("grp"), 10)[:, 0]
    share = query_weight.shape[0]
    kv_share = key_weight.shape[0]
    return (
        mixed.reshape(tokens.shape),
        input_gradient.reshape(tokens.shape),
        gain_own[0],
        attn_total[:share],
        attn_total[share : share + kv_share],
        attn_total[share + kv_share :],
        out_total,
        gain_own[1],
        gate_total,
        up_total,
        down_total,
    )


def solution(mesh):
    local = local_heads if mesh.shape["shard"] == NH else local_rows
    in_specs = (
        P("grp", "shard", None),
        P("grp"),
        P("shard"),
        P("shard", None),
        P("shard", None),
        P("shard", None),
        P("shard", None),
        P("shard"),
        P("shard", None),
        P("shard", None),
        P("shard", None),
        P("grp", "shard", None),
    )
    out_specs = (
        P("grp", "shard", None),
        P("grp", "shard", None),
        P("shard"),
        P("shard", None),
        P("shard", None),
        P("shard", None),
        P("shard", None),
        P("shard"),
        P("shard", None),
        P("shard", None),
        P("shard", None),
    )
    return jax.shard_map(local, mesh=mesh, in_specs=in_specs, out_specs=out_specs, check_vma=False)
```

```python
import functools
import math

import jax
import jax.numpy as jnp
from jax import lax
from jax.experimental import pallas as pl
from jax.experimental.pallas import tpu as pltpu
from jax.sharding import PartitionSpec as P

MESH = pl.DeviceIdType.MESH
DEPTH = 2

NH = 8
KVH = 4
HD = 256


F32 = jnp.float32
VMEM_LIMIT = 66_000_000


def either(condition, action):
    pl.when(condition)(action)


def total_into(dst, *srcs):
    step = 16

    @pl.loop(0, dst.shape[0] // step)
    def _(i):
        at = pl.ds(pl.multiple_of(i * step, step), step)
        value = srcs[0][at].astype(F32)
        for src in srcs[1:]:
            value = value + src[at].astype(F32)
        dst[at] = value.astype(dst.dtype)


class Place:
    def __init__(self, line):
        self.line = line
        self.me = lax.axis_index("shard")
        self.z = self.me // 2
        self.y = lax.rem(self.me, 2)
        self.cross = self.me + 1 - 2 * self.y
        self.low_end = self.z == 0
        self.high_end = self.z == line - 1
        near = []
        for z in range(line):
            order = [z]
            for k in range(1, line):
                order += [d for d in (z - k, z + k) if 0 <= d < line]
            near.append(order)
        self.tables = near

    def near(self, i):
        out = jnp.int32(0)
        for z in range(self.line):
            row = jnp.int32(self.tables[z][0])
            for k in range(1, self.line):
                row = jnp.where(i == k, self.tables[z][k], row)
            out = jnp.where(self.z == z, row, out)
        return out

    def far(self, i):
        return self.near(self.line - 1 - i)

    def greet(self, groups=()):
        barrier = pltpu.get_barrier_semaphore()

        def signal(**peer):
            pl.semaphore_signal(barrier, inc=1, device_id=peer, device_id_type=MESH)

        signal(shard=self.cross)
        either(self.z > 0, lambda: signal(shard=self.me - 2))
        either(self.z < self.line - 1, lambda: signal(shard=self.me + 2))
        for group in groups:
            signal(grp=group)
        ends = jnp.where(self.z > 0, 1, 0) + jnp.where(self.z < self.line - 1, 1, 0)
        pl.semaphore_wait(barrier, 1 + ends + len(groups))


class Gather:
    UP, DOWN, CROSS = 0, 1, 2

    def __init__(self, place, split, own, out, local_sem, send_sem, recv_sem):
        self.p, self.own, self.out = place, own, out
        self.local_sem, self.send_sem, self.recv_sem = local_sem, send_sem, recv_sem
        self.parts = (pl.ds(0, split), pl.ds(split, own.shape[0] - split))

    def copy(self, way, origin, part, own=False):
        p = self.p
        peer = (p.me + 2, p.me - 2, p.cross)[way]
        at = self.parts[part]
        return pltpu.make_async_remote_copy(
            src_ref=self.own.at[at] if own else self.out.at[origin, at],
            dst_ref=self.out.at[origin, at],
            send_sem=self.send_sem.at[way, origin, part],
            recv_sem=self.recv_sem.at[origin, part],
            device_id={"shard": peer},
            device_id_type=MESH,
        )

    def arrived(self, origin, part):
        self.copy(self.CROSS, origin, part).wait_recv()

    def start(self):
        p = self.p
        self.keep = pltpu.make_async_copy(self.own, self.out.at[p.me], self.local_sem)
        self.keep.start()
        self.copy(self.CROSS, p.me, 1, True).start()
        self.copy(self.CROSS, p.me, 0, True).start()
        for part in (0, 1):
            either(p.z < p.line - 1, self.copy(self.UP, p.me, part, True).start)
            either(p.z > 0, self.copy(self.DOWN, p.me, part, True).start)
        self.arrived(p.cross, 1)
        either(p.z < p.line - 1, self.copy(self.UP, p.cross, 1).start)
        either(p.z > 0, self.copy(self.DOWN, p.cross, 1).start)
        self.keep.wait()

    def hop(self, k):
        p = self.p

        def take(origin, other, way, more):
            self.arrived(origin, 0)
            self.copy(self.CROSS, origin, 0).start()
            either(more, self.copy(way, origin, 0).start)
            for block in (origin, other):
                self.arrived(block, 1)
                either(more, self.copy(way, block, 1).start)

        below, above = p.me - 2 * k, p.me + 2 * k
        either(p.z - k >= 0, lambda: take(below, p.cross - 2 * k, self.UP, p.z < p.line - 1))
        either(p.z + k < p.line, lambda: take(above, p.cross + 2 * k, self.DOWN, p.z > 0))

    def whole(self, position):
        self.arrived(2 * position + 1 - self.p.y, 0)

    def drain(self):
        p = self.p

        @pl.loop(0, p.line)
        def _(d):
            mine, other = 2 * d + p.y, 2 * d + 1 - p.y
            self.copy(self.CROSS, mine, 0).wait_send()

            @pl.when(d == p.z)
            def _():
                self.copy(self.CROSS, mine, 1).wait_send()

            @pl.when((d <= p.z) & (p.z < p.line - 1))
            def _():
                for block, part in ((mine, 0), (mine, 1), (other, 1)):
                    self.copy(self.UP, block, part).wait_send()

            @pl.when((d >= p.z) & (p.z > 0))
            def _():
                for block, part in ((mine, 0), (mine, 1), (other, 1)):
                    self.copy(self.DOWN, block, part).wait_send()


class Reduce:
    UP, DOWN, CROSS, BUP, BDN, BX = 0, 1, 2, 3, 5, 7

    @staticmethod
    def scratch(line, rows, split, width, dtype):
        v = pltpu.VMEM
        rest = rows - split
        dma = pltpu.SemaphoreType.DMA
        return (
            [v((line, split, width), dtype)] * 5
            + [v((line, 2, rest, width), dtype)] * 4
            + [v((rest, width), dtype)] * 2
            + [dma((8, line)), dma((8, line))]
        )

    def __init__(self, place, split, parts, out, scratch):
        self.p, self.parts, self.out = place, parts, out
        (self.cross_in, self.up_in, self.down_in, self.up_out, self.down_out) = scratch[:5]
        (self.bup_in, self.bdn_in, self.bup_out, self.bdn_out) = scratch[5:9]
        self.bx_out, self.bx_in, self.send_sem, self.recv_sem = scratch[9:]
        self.a = pl.ds(0, split)
        self.b = pl.ds(split, parts.shape[1] - split)

    def desc(self, way, slot, src, dst, peer):
        return pltpu.make_async_remote_copy(
            src_ref=src,
            dst_ref=dst,
            send_sem=self.send_sem.at[way, slot],
            recv_sem=self.recv_sem.at[way, slot],
            device_id={"shard": peer},
            device_id_type=MESH,
        )

    def cross_copy(self, d):
        p = self.p
        return self.desc(
            self.CROSS, d, self.parts.at[2 * d + 1 - p.y, self.a], self.cross_in.at[d], p.cross
        )

    def line_copy(self, up, d):
        p = self.p
        if up:
            return self.desc(self.UP, d, self.up_out.at[d], self.up_in.at[d], p.me + 2)
        return self.desc(self.DOWN, d, self.down_out.at[d], self.down_in.at[d], p.me - 2)

    def b_copy(self, up, d, o, src=None):
        p = self.p
        out, into = (self.bup_out, self.bup_in) if up else (self.bdn_out, self.bdn_in)
        return self.desc(
            (self.BUP if up else self.BDN) + o,
            d,
            out.at[d, o] if src is None else src,
            into.at[d, o],
            p.me + 2 if up else p.me - 2,
        )

    def bx_copy(self):
        return self.desc(self.BX, 0, self.bx_out, self.bx_in, self.p.cross)

    def column(self, o):
        return self.p.y if o == 0 else 1 - self.p.y

    def send_across(self, i):
        self.cross_copy(self.p.far(i)).start()

    def b_hop(self, i):
        p = self.p
        d = p.far(i)

        def go(up):
            first = p.low_end if up else p.high_end
            out, into = (self.bup_out, self.bup_in) if up else (self.bdn_out, self.bdn_in)
            for o in (1, 0):
                mine = self.parts.at[2 * d + self.column(o), self.b]
                either(first, self.b_copy(up, d, o, mine).start)

                @pl.when(jnp.logical_not(first))
                def _():
                    self.b_copy(up, d, o).wait_recv()
                    total_into(out.at[d, o], mine, into.at[d, o])
                    self.b_copy(up, d, o).start()

        either(d > p.z, lambda: go(True))
        either(d < p.z, lambda: go(False))

    def hop(self, i):
        p = self.p
        d = p.far(i)
        self.cross_copy(d).wait_recv()
        mine = self.parts.at[2 * d + p.y, self.a]

        def go(up):
            first = p.low_end if up else p.high_end
            out, into = (self.up_out, self.up_in) if up else (self.down_out, self.down_in)
            either(first, lambda: total_into(out.at[d], mine, self.cross_in.at[d]))

            @pl.when(jnp.logical_not(first))
            def _():
                self.line_copy(up, d).wait_recv()
                total_into(out.at[d], mine, self.cross_in.at[d], into.at[d])

            self.line_copy(up, d).start()

        either(d > p.z, lambda: go(True))
        either(d < p.z, lambda: go(False))

    def close(self, dst, mine, ups, downs):
        p = self.p
        either(p.low_end, lambda: total_into(dst, *mine, downs))
        either(p.high_end, lambda: total_into(dst, *mine, ups))
        either(
            jnp.logical_not(p.low_end | p.high_end), lambda: total_into(dst, *mine, ups, downs)
        )

    def finish(self):
        p = self.p
        for o in (1, 0):
            either(jnp.logical_not(p.low_end), self.b_copy(True, p.z, o).wait_recv)
            either(jnp.logical_not(p.high_end), self.b_copy(False, p.z, o).wait_recv)
            if o:
                mine = self.parts.at[2 * p.z + self.column(o), self.b]
                self.close(self.bx_out, (mine,), self.bup_in.at[p.z, o], self.bdn_in.at[p.z, o])
                self.bx_copy().start()
        self.bx_copy().wait_recv()
        self.close(
            self.out.at[self.b],
            (self.parts.at[p.me, self.b], self.bx_in),
            self.bup_in.at[p.z, 0],
            self.bdn_in.at[p.z, 0],
        )
        self.cross_copy(p.z).wait_recv()
        either(jnp.logical_not(p.low_end), self.line_copy(True, p.z).wait_recv)
        either(jnp.logical_not(p.high_end), self.line_copy(False, p.z).wait_recv)
        self.close(
            self.out.at[self.a],
            (self.parts.at[p.me, self.a], self.cross_in.at[p.z]),
            self.up_in.at[p.z],
            self.down_in.at[p.z],
        )

    def drain(self):
        p = self.p
        self.bx_copy().wait_send()

        @pl.loop(0, p.line)
        def _(d):
            self.cross_copy(d).wait_send()

            @pl.when(d > p.z)
            def _():
                self.line_copy(True, d).wait_send()
                self.b_copy(True, d, 0).wait_send()
                self.b_copy(True, d, 1).wait_send()

            @pl.when(d < p.z)
            def _():
                self.line_copy(False, d).wait_send()
                self.b_copy(False, d, 0).wait_send()
                self.b_copy(False, d, 1).wait_send()


def dot_t(a, b):
    return lax.dot_general(a, b, (((1,), (1,)), ((), ())), preferred_element_type=F32)


def t_dot(a, b):
    return lax.dot_general(a, b, (((0,), (0,)), ((), ())), preferred_element_type=F32)


def ffn_kernel(
    line, split,
    own, cot_hbm, gate_hbm, up_hbm, down_hbm,
    second, ffn_hbm, mine_hbm, theirs_hbm,
    normed, cot, gate_w, up_w, down_w, hidden, gate_g, up_g, parts, stage,
    g_local, g_send, g_recv, load_sem, ffn_sem, stage_send, stage_recv, stage_local, *r_scratch,
):
    p = Place(line)
    rank = lax.axis_index("grp")
    core = lax.rem(rank, 2)
    partner = rank + 1 - 2 * core
    loads = [
        pltpu.make_async_copy(src, dst, load_sem.at[i])
        for i, (src, dst) in enumerate(
            ((gate_hbm, gate_w), (up_hbm, up_w), (cot_hbm, cot), (down_hbm, down_w))
        )
    ]
    for load in loads:
        load.start()
    p.greet((partner,))
    gather = Gather(p, split, own, normed, g_local, g_send, g_recv)
    gather.start()
    for load in loads:
        load.wait()
    rows = own.shape[0]
    pair = 2 * rows
    low = own.dtype

    @pl.loop(0, line)
    def _(i):
        gather.hop(i + 1)
        d = p.near(i)
        gather.whole(d)
        x = normed[pl.ds(2 * d, 2)].reshape(pair, -1)
        g = dot_t(x, gate_w[...])
        u = dot_t(x, up_w[...])
        dh = dot_t(cot[pl.ds(2 * d, 2)].reshape(pair, -1), down_w[...])
        s = 1.0 / (1.0 + jnp.exp(-g))
        silu = g * s
        at = pl.ds(pl.multiple_of(d * pair, pair), pair)
        hidden[at] = (silu * u).astype(low)
        up_g[at] = (dh * silu).astype(low)
        gate_g[at] = (dh * u * s * (1.0 + g * (1.0 - s))).astype(low)
        part = jnp.dot(gate_g[at], gate_w[...], preferred_element_type=F32)
        part = part + jnp.dot(up_g[at], up_w[...], preferred_element_type=F32)
        parts[pl.ds(2 * d, 2)] = part.astype(low).reshape(2, rows, -1)

    reduce = Reduce(p, split, parts, second, r_scratch)
    for i in range(DEPTH):
        reduce.send_across(i)
    for i in range(line - 1):
        reduce.b_hop(i)

    units = hidden.shape[1]
    quarter = units // 4
    half = units // 2

    def put(n, slot):
        which, q = n // 4, lax.rem(n, 4)
        keep = (q // 2) == core
        at = pl.ds(pl.multiple_of(lax.rem(q, 2) * quarter, quarter), quarter)
        local = pltpu.make_async_copy(stage.at[slot], mine_hbm.at[which, at], stage_local.at[slot])
        remote = pltpu.make_async_remote_copy(
            src_ref=stage.at[slot],
            dst_ref=theirs_hbm.at[which, at],
            send_sem=stage_send.at[slot],
            recv_sem=stage_recv.at[which, lax.rem(q, 2)],
            device_id={"grp": partner},
            device_id_type=MESH,
        )
        return keep, local, remote

    def release(n, slot):
        keep, local, remote = put(n, slot)
        either(keep, local.wait)
        either(jnp.logical_not(keep), remote.wait_send)

    def gradient(which, left, right):
        @pl.loop(0, 4)
        def _(q):
            n = which * 4 + q
            slot = lax.rem(n, 2)
            either(n >= 2, lambda: release(n - 2, slot))
            cols = pl.ds(pl.multiple_of(q * quarter, quarter), quarter)
            stage[slot] = t_dot(left[:, cols], right[...].reshape(left.shape[0], -1)).astype(low)
            keep, local, remote = put(n, slot)
            either(keep, local.start)
            either(jnp.logical_not(keep), remote.start)

    sources = ((hidden, cot), (gate_g, normed), (up_g, normed))
    for i in range(line - 1):
        gradient(i, *sources[i])
        reduce.hop(i)
        if i + DEPTH < line:
            reduce.send_across(i + DEPTH)
    release(10, 0)
    release(11, 1)
    reduce.finish()
    reduce.drain()
    gather.drain()

    @pl.loop(0, line)
    def _(d):
        at = pl.ds(pl.multiple_of(d * pair, pair), pair)
        part = jnp.dot(hidden[at], down_w[...], preferred_element_type=F32)
        parts[pl.ds(2 * d, 2)] = part.astype(low).reshape(2, rows, -1)

    ffn = pltpu.make_async_copy(parts, ffn_hbm, ffn_sem)
    ffn.start()
    for which in range(3):
        for q in range(2):
            pltpu.make_async_remote_copy(
                src_ref=stage.at[0],
                dst_ref=theirs_hbm.at[which, pl.ds(q * quarter, quarter)],
                send_sem=stage_send.at[0],
                recv_sem=stage_recv.at[which, q],
                device_id={"grp": partner},
                device_id_type=MESH,
            ).wait_recv()
    ffn.wait()


def ffn(own, cot, gate_w, up_w, down_w, ident, split=112):
    rows, width = own.shape
    count = cot.shape[0]
    units = gate_w.shape[0]
    low = own.dtype
    hbm = pl.BlockSpec(memory_space=pl.ANY)
    vm = pl.BlockSpec(memory_space=pltpu.VMEM)
    v = pltpu.VMEM
    dma = pltpu.SemaphoreType.DMA
    tokens = count * rows
    shape = jax.ShapeDtypeStruct
    return pl.pallas_call(
        functools.partial(ffn_kernel, count // 2, split),
        out_shape=(
            shape((rows, width), F32),
            shape((count, rows, width), low),
            shape((3, units // 2, width), low),
            shape((3, units // 2, width), low),
        ),
        in_specs=[vm] + [hbm] * 4,
        out_specs=(vm, hbm, hbm, hbm),
        scratch_shapes=[
            v((count, rows, width), low),
            v((count, rows, width), low),
            v((units, width), low),
            v((units, width), low),
            v((units, width), low),
            v((tokens, units), low),
            v((tokens, units), low),
            v((tokens, units), low),
            v((count, rows, width), low),
            v((2, units // 4, width), low),
            dma, dma((3, count, 2)), dma((count, 2)), dma((4,)), dma, dma((2,)), dma((3, 2)), dma((2,)),
        ] + Reduce.scratch(count // 2, rows, split, width, low),
        compiler_params=pltpu.CompilerParams(collective_id=ident, has_side_effects=True, vmem_limit_bytes=VMEM_LIMIT),
        name="ffn",
    )(own, cot, gate_w, up_w, down_w)


def gather_kernel(line, split, own, out, local_sem, send_sem, recv_sem):
    p = Place(line)
    p.greet()
    g = Gather(p, split, own, out, local_sem, send_sem, recv_sem)
    g.start()
    for k in range(1, line):
        g.hop(k)
    for d in range(line):
        g.whole(d)
    g.drain()


def gather(own, count, ident, split=112):
    rows, width = own.shape
    hbm = pl.BlockSpec(memory_space=pl.ANY)
    dma = pltpu.SemaphoreType.DMA
    return pl.pallas_call(
        functools.partial(gather_kernel, count // 2, split),
        out_shape=jax.ShapeDtypeStruct((count, rows, width), own.dtype),
        in_specs=[hbm],
        out_specs=hbm,
        scratch_shapes=[dma, dma((3, count, 2)), dma((count, 2))],
        compiler_params=pltpu.CompilerParams(collective_id=ident, has_side_effects=True),
        name="gather",
    )(own)


def reduce_kernel(line, split, parts, out, *scratch):
    p = Place(line)
    p.greet()
    r = Reduce(p, split, parts, out, scratch)
    for i in range(DEPTH):
        r.send_across(i)
    for i in range(line - 1):
        r.b_hop(i)
    for i in range(line - 1):
        r.hop(i)
        if i + DEPTH < line:
            r.send_across(i + DEPTH)
    r.finish()
    r.drain()


def reduce(parts, ident, split=112):
    count, rows, width = parts.shape
    vm = pl.BlockSpec(memory_space=pltpu.VMEM)
    return pl.pallas_call(
        functools.partial(reduce_kernel, count // 2, split),
        out_shape=jax.ShapeDtypeStruct((rows, width), F32),
        in_specs=[vm],
        out_specs=vm,
        scratch_shapes=Reduce.scratch(count // 2, rows, split, width, parts.dtype),
        compiler_params=pltpu.CompilerParams(collective_id=ident, has_side_effects=True),
        name="reduce",
    )(parts)


def everyone(axis, count, me, barrier):
    for step in range(1, count):
        pl.semaphore_signal(
            barrier, inc=1, device_id={axis: lax.rem(me + step, count)}, device_id_type=MESH
        )
    pl.semaphore_wait(barrier, count - 1)


def first_gather_kernel(
    line, split, own, small, out, small_out, local_sem, send_sem, recv_sem, ssem, rsem
):
    count = 2 * line
    p = Place(line)
    me = p.me

    def copy(step, peer, origin):
        return pltpu.make_async_remote_copy(
            src_ref=small,
            dst_ref=small_out.at[origin],
            send_sem=ssem.at[step],
            recv_sem=rsem.at[step],
            device_id={"shard": peer},
            device_id_type=MESH,
        )

    everyone("shard", count, me, pltpu.get_barrier_semaphore())
    for step in range(1, count):
        copy(step, lax.rem(me + step, count), me).start()
    g = Gather(p, split, own, out, local_sem, send_sem, recv_sem)
    g.start()
    small_out[me] = small[...]
    for k in range(1, line):
        g.hop(k)
    for d in range(line):
        g.whole(d)
    g.drain()
    for step in range(1, count):
        c = copy(step, me, lax.rem(me + count - step, count))
        c.wait_send()
        c.wait_recv()


def first_gather(own, small, count, ident, split=112):
    rows, width = own.shape
    any_spec = pl.BlockSpec(memory_space=pl.ANY)
    vmem_spec = pl.BlockSpec(memory_space=pltpu.VMEM)
    dma = pltpu.SemaphoreType.DMA
    return pl.pallas_call(
        functools.partial(first_gather_kernel, count // 2, split),
        out_shape=(
            jax.ShapeDtypeStruct((count, rows, width), own.dtype),
            jax.ShapeDtypeStruct((count,) + small.shape, small.dtype),
        ),
        in_specs=[any_spec, vmem_spec],
        out_specs=(any_spec, vmem_spec),
        scratch_shapes=[dma, dma((3, count, 2)), dma((count, 2)), dma((count,)), dma((count,))],
        compiler_params=pltpu.CompilerParams(collective_id=ident, has_side_effects=True),
        name="first_gather",
    )(own, small)


def gain_sum_kernel(count, groups, parts_ref, out_ref, first, held, second, send_sem, recv_sem, send2, recv2):
    me = lax.axis_index("shard")
    group = lax.axis_index("grp")
    barrier = pltpu.get_barrier_semaphore()
    for step in range(1, count):
        pl.semaphore_signal(
            barrier, inc=1, device_id={"shard": lax.rem(me + step, count)}, device_id_type=MESH
        )
    for step in range(1, groups):
        pl.semaphore_signal(
            barrier, inc=1, device_id={"grp": lax.rem(group + step, groups)}, device_id_type=MESH
        )
    pl.semaphore_wait(barrier, count + groups - 2)

    def copy(step, peer, origin):
        return pltpu.make_async_remote_copy(
            src_ref=parts_ref.at[peer],
            dst_ref=first.at[origin],
            send_sem=send_sem.at[step],
            recv_sem=recv_sem.at[step],
            device_id={"shard": peer},
            device_id_type=MESH,
        )

    def copy2(step, peer, origin):
        return pltpu.make_async_remote_copy(
            src_ref=held,
            dst_ref=second.at[origin],
            send_sem=send2.at[step],
            recv_sem=recv2.at[step],
            device_id={"grp": peer},
            device_id_type=MESH,
        )

    for step in range(1, count):
        copy(step, lax.rem(me + step, count), me).start()
    first[me] = parts_ref[me]
    for step in range(1, count):
        copy(step, me, lax.rem(me + count - step, count)).wait_recv()
    total = first[0]
    for peer in range(1, count):
        total = total + first[peer]
    held[...] = total
    second[group] = total
    for step in range(1, groups):
        copy2(step, lax.rem(group + step, groups), group).start()
    for step in range(1, groups):
        copy2(step, group, lax.rem(group + groups - step, groups)).wait_recv()
    total = second[0]
    for peer in range(1, groups):
        total = total + second[peer]
    out_ref[...] = total
    for step in range(1, count):
        copy(step, lax.rem(me + step, count), me).wait_send()
    for step in range(1, groups):
        copy2(step, lax.rem(group + step, groups), group).wait_send()


def gain_sum(parts, groups, ident):
    count = parts.shape[0]
    shape = parts.shape[1:]
    vmem = pltpu.VMEM
    dma = pltpu.SemaphoreType.DMA
    return pl.pallas_call(
        functools.partial(gain_sum_kernel, count, groups),
        out_shape=jax.ShapeDtypeStruct(shape, parts.dtype),
        in_specs=[pl.BlockSpec(memory_space=vmem)],
        out_specs=pl.BlockSpec(memory_space=vmem),
        scratch_shapes=[
            vmem((count,) + shape, parts.dtype),
            vmem(shape, parts.dtype),
            vmem((groups,) + shape, parts.dtype),
            dma((count,)),
            dma((count,)),
            dma((groups,)),
            dma((groups,)),
        ],
        compiler_params=pltpu.CompilerParams(collective_id=ident, has_side_effects=True),
        name="gain_sum",
    )(parts)


MASKED = -1e30


def probabilities(query, keys, rows_from, bias):
    scores = dot_t(query, keys) * (1.0 / math.sqrt(HD))
    row = lax.broadcasted_iota(jnp.int32, scores.shape, 0) + rows_from
    col = lax.broadcasted_iota(jnp.int32, scores.shape, 1)
    scores = jnp.where((col <= row) & (bias >= 0.0), scores, MASKED)
    weight = jnp.exp(scores - jnp.max(scores, -1, keepdims=True))
    return weight / jnp.sum(weight, -1, keepdims=True)


def attention_grad_kernel(
    line, split, seqs,
    own, bias, cosine, sine, ffn_hbm, normed_hbm, attended_hbm, q_hbm, k_hbm, v_hbm, wq_hbm, wk_hbm, wv_hbm, wo_hbm, sums_hbm,
    first, ffn_own, sums_in_hbm, mine_hbm, theirs_hbm,
    dbranch, normed, attended, q, k, v, wq, wk, wv, wo, da, dk_acc, dv_acc, dq_rows, dk_rows, dv_rows, halves, half_in, ffn_parts, parts, stage,
    g_local, g_send, g_recv, load_sem, sum_send, sum_recv, half_send, half_recv, stage_send, stage_recv, stage_local, *r_scratch,
):
    p = Place(line)
    rank = lax.axis_index("grp")
    core = lax.rem(rank, 2)
    partner = rank + 1 - 2 * core
    opposite = lax.rem(rank + 2, 4)
    pairs_in = ((wo_hbm, wo), (q_hbm, q), (k_hbm, k), (v_hbm, v), (ffn_hbm, ffn_parts), (wq_hbm, wq), (wk_hbm, wk), (wv_hbm, wv), (attended_hbm, attended), (normed_hbm, normed))
    loads = [pltpu.make_async_copy(src, dst, load_sem.at[i]) for i, (src, dst) in enumerate(pairs_in)]
    for load in loads:
        load.start()
    p.greet((partner, opposite))
    gather = Gather(p, split, own, dbranch, g_local, g_send, g_recv)
    n_sums = sums_hbm.shape[0]

    def sum_copy(i):
        return pltpu.make_async_remote_copy(
            src_ref=sums_hbm.at[i],
            dst_ref=sums_in_hbm.at[i],
            send_sem=sum_send.at[i],
            recv_sem=sum_recv.at[i],
            device_id={"grp": opposite},
            device_id_type=MESH,
        )

    for i in range(n_sums):
        sum_copy(i).start()
    gather.start()
    for load in loads:
        load.wait()
    rows = own.shape[0]
    pair = 2 * rows
    slots = rows // seqs
    low = own.dtype
    scale = 1.0 / math.sqrt(HD)

    @pl.loop(0, line)
    def _(i):
        gather.hop(i + 1)
        d = p.near(i)
        gather.whole(d)
        grad = dot_t(dbranch[pl.ds(2 * d, 2)].reshape(pair, -1), wo[...]).astype(low)
        for block in range(2):
            for n in range(seqs):
                at = pl.ds(pl.multiple_of(d * 2 * slots + block * slots, slots), slots)
                da[n, at] = grad[block * rows + n * slots : block * rows + (n + 1) * slots]

    ffn_sum = Reduce(p, split, ffn_parts, ffn_own, r_scratch[: len(r_scratch) // 2])
    for i in range(DEPTH):
        ffn_sum.send_across(i)
    for i in range(line - 1):
        ffn_sum.b_hop(i)

    total_slots = q.shape[1]
    tile = min(256, total_slots)

    def backward(n):
        dk_acc[...] = jnp.zeros_like(dk_acc)
        dv_acc[...] = jnp.zeros_like(dv_acc)

        def to_rows(target, value, start, count):
            for c in range(count // slots):
                b = (start + c * slots) // slots
                target[pl.ds(b * rows + n * slots, slots)] = value[c * slots : (c + 1) * slots]

        for t in range(total_slots // tile):
            span = (t + 1) * tile
            at = pl.ds(t * tile, tile)
            query, keys, values, grad = q[n, at], k[n, pl.ds(0, span)], v[n, pl.ds(0, span)], da[n, at]
            probs = probabilities(query, keys, t * tile, bias[n][:, :span])
            dprobs = dot_t(grad, values)
            dscores = (probs * (dprobs - jnp.sum(probs * dprobs, -1, keepdims=True))).astype(low)
            dq = jnp.dot(dscores, keys, preferred_element_type=F32) * scale
            dq = dq * cosine[at] - turned(dq) * sine[at]
            to_rows(dq_rows, dq.astype(low), t * tile, tile)
            dk_acc[pl.ds(0, span)] += t_dot(dscores, query)
            dv_acc[pl.ds(0, span)] += t_dot(probs.astype(low), grad)
        dk = dk_acc[...] * scale
        dk = (dk * cosine[...] - turned(dk) * sine[...]).astype(low)
        dv = dv_acc[...].astype(low)
        to_rows(dk_rows, dk, 0, total_slots)
        to_rows(dv_rows, dv, 0, total_slots)

    half = HD // 2

    def swap():
        return pltpu.make_async_remote_copy(
            src_ref=halves.at[1 - p.y],
            dst_ref=half_in,
            send_sem=half_send,
            recv_sem=half_recv,
            device_id={"shard": p.cross},
            device_id_type=MESH,
        )

    @pl.loop(0, seqs)
    def _(n):
        backward(n)
        ffn_sum.hop(n)
        ffn_sum.send_across(n + DEPTH)

    for h in range(2):
        at = pl.ds(h * half, half)
        halves[h, 0] = dk_rows[:, at]
        halves[h, 1] = dv_rows[:, at]
    swap().start()
    reduce = Reduce(p, split, parts, first, r_scratch[len(r_scratch) // 2 :])

    @pl.loop(0, line)
    def _(i):
        d = p.far(i)
        at = pl.ds(pl.multiple_of(d * pair, pair), pair)
        part = jnp.dot(dq_rows[at], wq[...], preferred_element_type=F32)
        part = part + jnp.dot(dk_rows[at], wk[...], preferred_element_type=F32)
        part = part + jnp.dot(dv_rows[at], wv[...], preferred_element_type=F32)
        parts[pl.ds(2 * d, 2)] = part.astype(low).reshape(2, rows, -1)
        reduce.send_across(i)

    for i in range(line - 1):
        reduce.b_hop(i)
    for i in range(seqs, line - 1):
        ffn_sum.hop(i)
    ffn_sum.finish()

    chunk = half

    def put(n, slot):
        keep = (n // 3) == core
        at = pl.ds(pl.multiple_of(lax.rem(n, 3) * chunk, chunk), chunk)
        local = pltpu.make_async_copy(stage.at[slot], mine_hbm.at[at], stage_local.at[slot])
        remote = pltpu.make_async_remote_copy(
            src_ref=stage.at[slot],
            dst_ref=theirs_hbm.at[at],
            send_sem=stage_send.at[slot],
            recv_sem=stage_recv.at[lax.rem(n, 3)],
            device_id={"grp": partner},
            device_id_type=MESH,
        )
        return keep, local, remote

    def release(n):
        keep, local, remote = put(n, n % 2)
        either(keep, local.wait)
        either(jnp.logical_not(keep), remote.wait_send)

    def gradient(n, left, right):
        slot = n % 2
        if n >= 2:
            release(n - 2)
        stage[slot] = t_dot(left, right[...].reshape(left.shape[0], -1)).astype(low)
        keep, local, remote = put(n, slot)
        either(keep, local.start)
        either(jnp.logical_not(keep), remote.start)

    def summed(which):
        return (halves[p.y, which].astype(F32) + half_in[which].astype(F32)).astype(low)

    reduce.hop(0)
    gradient(0, attended[:, :chunk], dbranch)
    gradient(1, attended[:, chunk:], dbranch)
    gradient(2, dq_rows[:, :chunk], normed)
    reduce.hop(1)
    gradient(3, dq_rows[:, chunk:], normed)
    swap().wait_recv()
    gradient(4, summed(0), normed)
    gradient(5, summed(1), normed)
    reduce.hop(2)
    release(4)
    release(5)
    reduce.finish()
    reduce.drain()
    ffn_sum.drain()
    gather.drain()
    swap().wait_send()
    for n in range(3):
        put(n, 0)[2].wait_recv()
    for i in range(n_sums):
        sum_copy(i).wait_send()
        sum_copy(i).wait_recv()


def attention_grad(own, bias, cosine, sine, ffn_parts, normed, attended, q, k, v, wq, wk, wv, wo, sums, ident, split=112):
    rows, width = own.shape
    count = normed.shape[0]
    line = count // 2
    seqs, total_slots, hd = q.shape
    low = own.dtype
    hbm = pl.BlockSpec(memory_space=pl.ANY)
    vm = pl.BlockSpec(memory_space=pltpu.VMEM)
    vmem = pltpu.VMEM
    dma = pltpu.SemaphoreType.DMA
    tokens = count * rows
    half = hd // 2
    shape = jax.ShapeDtypeStruct
    big = vmem((count, rows, width), low)
    head = vmem((seqs, total_slots, hd), low)
    weight = vmem((hd, width), low)
    flat = vmem((tokens, hd), low)
    return pl.pallas_call(
        functools.partial(attention_grad_kernel, line, split, seqs),
        out_shape=(
            shape((rows, width), F32),
            shape((rows, width), F32),
            shape(sums.shape, low),
            shape((3 * half, width), low),
            shape((3 * half, width), low),
        ),
        in_specs=[vm] * 4 + [hbm] * 11,
        out_specs=(vm, vm, hbm, hbm, hbm),
        scratch_shapes=[
            big, big, flat, head, head, head, weight, weight, weight, weight, head,
            vmem((total_slots, hd), F32), vmem((total_slots, hd), F32),
            flat, flat, flat,
            vmem((2, 2, tokens, half), low), vmem((2, tokens, half), low),
            big, big, vmem((2, half, width), low),
            dma, dma((3, count, 2)), dma((count, 2)), dma((10,)), dma((sums.shape[0],)), dma((sums.shape[0],)),
            dma, dma, dma((2,)), dma((3,)), dma((2,)),
        ] + Reduce.scratch(line, rows, split, width, low) * 2,
        compiler_params=pltpu.CompilerParams(collective_id=ident, has_side_effects=True, vmem_limit_bytes=VMEM_LIMIT),
        name="attention_grad",
    )(own, bias, cosine, sine, ffn_parts, normed, attended, q, k, v, wq, wk, wv, wo, sums)


def between_chips(pair):
    return lax.ppermute(pair, "grp", [(0, 2), (2, 0), (1, 3), (3, 1)])


def both_halves(pair, other):
    whole = (pair.astype(F32) + other.astype(F32)).astype(pair.dtype)
    swapped = lax.ppermute(whole, "grp", [(0, 1), (1, 0), (2, 3), (3, 2)])
    core = lax.rem(lax.axis_index("grp"), 2)
    return jnp.concatenate(
        [jnp.where(core == 0, whole, swapped), jnp.where(core == 0, swapped, whole)], -2
    ).astype(F32)


epsilon = 1e-06
theta_base = 1000042.0
masked_value = -1e30


def turned(source):
    half_width = source.shape[-1] // 2
    return jnp.concatenate([-source[..., half_width:], source[..., :half_width]], -1)


def rotate(source, cosine_table, sine_table):
    return source * cosine_table + turned(source) * sine_table


def unrotate(source, cosine_table, sine_table):
    return source * cosine_table - turned(source) * sine_table


def norm_forward(source, norm_gain):
    inverse = lax.rsqrt(jnp.mean(source * source, -1, keepdims=True) + epsilon)
    return (source * inverse * norm_gain, inverse)


def norm_backward(source, inverse, norm_gain, grad_out):
    weighted = grad_out * norm_gain
    inner_sum = jnp.sum(weighted * source, -1, keepdims=True)
    grad_in = (
        inverse * weighted - source * inverse * inverse * inverse * inner_sum / source.shape[-1]
    )
    return (grad_in, jnp.sum(grad_out * source * inverse, 0))


def weight_terms(normed, query_grad, key_grad, value_grad, attended, branch_grad, shard_count):
    token_count, model_width = normed.shape
    query_share = query_grad.shape[1] // shard_count
    kv_share = key_grad.shape[1] // shard_count
    shard_rows = 2 * query_share + 2 * kv_share

    def weight_term(first_row, row_count):
        blocks = row_count // shard_rows

        def columns(matrix, share_cols):
            return matrix.reshape(token_count, blocks, share_cols)

        part_query = jnp.einsum(
            "tmr,td->mrd",
            columns(query_grad, query_share),
            normed,
            preferred_element_type=jnp.float32,
        )
        part_key = jnp.einsum(
            "tmr,td->mrd", columns(key_grad, kv_share), normed, preferred_element_type=jnp.float32
        )
        part_value = jnp.einsum(
            "tmr,td->mrd", columns(value_grad, kv_share), normed, preferred_element_type=jnp.float32
        )
        part_out = jnp.einsum(
            "tmr,td->mrd",
            columns(attended, query_share),
            branch_grad,
            preferred_element_type=jnp.float32,
        )
        return jnp.concatenate([part_query, part_key, part_value, part_out], 1).reshape(
            row_count, model_width
        )

    return (weight_term, shard_rows)


def local_rows(
    tokens,
    lengths,
    prenorm_gain,
    query_weight,
    key_weight,
    value_weight,
    out_weight,
    midnorm_gain,
    gate_weight,
    up_weight,
    down_weight,
    cotangent,
):
    shard_count = lax.axis_size("shard")
    shard_rank = lax.axis_index("shard")
    micro_count, seq_dev, model_width = tokens.shape
    slot_count = seq_dev * shard_count
    repeat_heads = NH // KVH
    query_width = NH * HD
    kv_width = KVH * HD
    score_scale = 1.0 / math.sqrt(HD)
    local_pos = shard_rank * seq_dev + jnp.arange(seq_dev, dtype=jnp.int32)
    key_pos = jnp.arange(slot_count, dtype=jnp.int32)
    inverse_freq = theta_base ** (-(jnp.arange(0, HD, 2).astype(jnp.float32) / HD))
    angles = local_pos.astype(jnp.float32)[:, None] * inverse_freq[None, :]
    cosine_table = jnp.concatenate([jnp.cos(angles), jnp.cos(angles)], -1)[:, None, :]
    sine_table = jnp.concatenate([jnp.sin(angles), jnp.sin(angles)], -1)[:, None, :]
    gate_total = jnp.zeros(gate_weight.shape, jnp.float32)
    up_total = jnp.zeros(up_weight.shape, jnp.float32)
    down_total = jnp.zeros(down_weight.shape, jnp.float32)
    prenorm_total = jnp.zeros((model_width,), jnp.float32)
    midnorm_total = jnp.zeros((model_width,), jnp.float32)
    attn_total = None
    mixed_rows = []
    input_rows = []
    for micro_index in range(micro_count):
        gathered = (
            lax.all_gather(query_weight, "shard", axis=0, tiled=True),
            lax.all_gather(key_weight, "shard", axis=0, tiled=True),
            lax.all_gather(value_weight, "shard", axis=0, tiled=True),
            lax.all_gather(prenorm_gain, "shard", axis=0, tiled=True),
            lax.all_gather(midnorm_gain, "shard", axis=0, tiled=True),
        )
        query_full, key_full, value_full, prenorm_full, midnorm_full = gathered
        prenorm_f = prenorm_full.astype(jnp.float32)
        midnorm_f = midnorm_full.astype(jnp.float32)
        source = tokens[micro_index].astype(jnp.float32)
        length_now = lengths[micro_index]
        valid_rows = local_pos < length_now
        scaled_first, inverse_first = norm_forward(source, prenorm_f)
        normed_first = scaled_first.astype(jnp.bfloat16)
        query_pre = jnp.einsum(
            "sd,qd->sq", normed_first, query_full, preferred_element_type=jnp.float32
        ).reshape(seq_dev, NH, HD)
        key_pre = jnp.einsum(
            "sd,qd->sq", normed_first, key_full, preferred_element_type=jnp.float32
        ).reshape(seq_dev, KVH, HD)
        value_pre = jnp.einsum(
            "sd,qd->sq", normed_first, value_full, preferred_element_type=jnp.float32
        )
        query_rot = rotate(query_pre, cosine_table, sine_table).astype(jnp.bfloat16)
        key_rot = rotate(key_pre, cosine_table, sine_table).astype(jnp.bfloat16)
        key_value = jnp.concatenate(
            [key_rot.reshape(seq_dev, kv_width), value_pre.astype(jnp.bfloat16)], 1
        )
        kv_all = lax.all_gather(key_value, "shard", axis=0, tiled=True)
        keys_all = kv_all[:, :kv_width].reshape(slot_count, KVH, HD)
        values_all = kv_all[:, kv_width:].reshape(slot_count, KVH, HD)
        query_group = query_rot.reshape(seq_dev, KVH, repeat_heads, HD)
        scores = (
            jnp.einsum("skrd,tkd->krst", query_group, keys_all, preferred_element_type=jnp.float32)
            * score_scale
        )
        allowed = (key_pos[None, :] <= local_pos[:, None]) & (key_pos[None, :] < length_now)
        scores = jnp.where(allowed, scores, masked_value)
        row_max = jnp.max(scores, -1, keepdims=True)
        exp_scores = jnp.exp(scores - row_max)
        attention_probs = exp_scores / jnp.sum(exp_scores, -1, keepdims=True)
        probs_low = attention_probs.astype(jnp.bfloat16)
        attended = (
            jnp.einsum("krst,tkd->skrd", probs_low, values_all, preferred_element_type=jnp.float32)
            .astype(jnp.bfloat16)
            .reshape(seq_dev, query_width)
        )
        branch = jnp.dot(
            attended,
            lax.all_gather(out_weight, "shard", axis=0, tiled=True),
            preferred_element_type=jnp.float32,
        )
        middle = source + branch
        scaled_second, inverse_second = norm_forward(middle, midnorm_f)
        normed_second = scaled_second.astype(jnp.bfloat16)
        normed_all = lax.all_gather(normed_second, "shard", axis=0, tiled=True)
        gate_pre = jnp.einsum(
            "sd,fd->sf", normed_all, gate_weight, preferred_element_type=jnp.float32
        )
        up_pre = jnp.einsum("sd,fd->sf", normed_all, up_weight, preferred_element_type=jnp.float32)
        sigmoid_gate = jax.nn.sigmoid(gate_pre)
        silu_gate = gate_pre * sigmoid_gate
        hidden = (silu_gate * up_pre).astype(jnp.bfloat16)
        ffn_part = lax.psum_scatter(
            jnp.dot(hidden, down_weight, preferred_element_type=jnp.float32).astype(jnp.bfloat16),
            "shard",
            scatter_dimension=0,
            tiled=True,
        ).astype(jnp.float32)
        mixed_rows.append(
            jnp.where(valid_rows[:, None], middle + ffn_part, 0.0).astype(jnp.bfloat16)
        )
        cot_low = jnp.where(
            valid_rows[:, None], cotangent[micro_index], jnp.zeros_like(cotangent[micro_index])
        )
        cot_all = lax.all_gather(cot_low, "shard", axis=0, tiled=True)
        hidden_grad = jnp.einsum(
            "sd,fd->sf", cot_all, down_weight, preferred_element_type=jnp.float32
        )
        down_total = down_total + jnp.einsum(
            "sf,sd->fd", hidden, cot_all, preferred_element_type=jnp.float32
        )
        gate_grad = (
            hidden_grad * up_pre * sigmoid_gate * (1.0 + gate_pre * (1.0 - sigmoid_gate))
        ).astype(jnp.bfloat16)
        up_grad = (hidden_grad * silu_gate).astype(jnp.bfloat16)
        gate_total = gate_total + jnp.einsum(
            "sf,sd->fd", gate_grad, normed_all, preferred_element_type=jnp.float32
        )
        up_total = up_total + jnp.einsum(
            "sf,sd->fd", up_grad, normed_all, preferred_element_type=jnp.float32
        )
        second_grad = lax.psum_scatter(
            jnp.dot(gate_grad, gate_weight, preferred_element_type=jnp.float32)
            + jnp.dot(up_grad, up_weight, preferred_element_type=jnp.float32),
            "shard",
            scatter_dimension=0,
            tiled=True,
        )
        middle_part, midnorm_part = norm_backward(middle, inverse_second, midnorm_f, second_grad)
        middle_grad = cot_low.astype(jnp.float32) + middle_part
        midnorm_total = midnorm_total + midnorm_part
        branch_grad = middle_grad.astype(jnp.bfloat16)
        attended_grad = jnp.einsum(
            "sd,qd->sq",
            branch_grad,
            lax.all_gather(out_weight, "shard", axis=0, tiled=True),
            preferred_element_type=jnp.float32,
        ).astype(jnp.bfloat16)
        attended_group = attended_grad.reshape(seq_dev, KVH, repeat_heads, HD)
        probs_grad = jnp.einsum(
            "skrd,tkd->krst", attended_group, values_all, preferred_element_type=jnp.float32
        )
        inner_sum = jnp.sum(attention_probs * probs_grad, -1, keepdims=True)
        scores_grad = (attention_probs * (probs_grad - inner_sum)).astype(jnp.bfloat16)
        query_rot_grad = (
            jnp.einsum(
                "krst,tkd->skrd", scores_grad, keys_all, preferred_element_type=jnp.float32
            ).reshape(seq_dev, NH, HD)
            * score_scale
        )
        query_grad = (
            unrotate(query_rot_grad, cosine_table, sine_table)
            .astype(jnp.bfloat16)
            .reshape(seq_dev, query_width)
        )
        row_count = lax.axis_size("shard") * seq_dev
        key_part = (
            jnp.einsum(
                "krst,skrd->tkd", scores_grad, query_group, preferred_element_type=jnp.float32
            )
            * score_scale
        )
        value_part = jnp.einsum(
            "krst,skrd->tkd", probs_low, attended_group, preferred_element_type=jnp.float32
        )
        kv_grad = lax.psum_scatter(
            jnp.concatenate(
                [key_part.reshape(row_count, kv_width), value_part.reshape(row_count, kv_width)], 1
            ).astype(jnp.bfloat16),
            "shard",
            scatter_dimension=0,
            tiled=True,
        ).astype(jnp.float32)
        key_grad = (
            unrotate(kv_grad[:, :kv_width].reshape(seq_dev, KVH, HD), cosine_table, sine_table)
            .astype(jnp.bfloat16)
            .reshape(seq_dev, kv_width)
        )
        value_grad = kv_grad[:, kv_width:].astype(jnp.bfloat16)
        first_grad = jnp.einsum(
            "sq,qd->sd", query_grad, query_full, preferred_element_type=jnp.float32
        )
        first_grad = first_grad + jnp.einsum(
            "sq,qd->sd", key_grad, key_full, preferred_element_type=jnp.float32
        )
        first_grad = first_grad + jnp.einsum(
            "sq,qd->sd", value_grad, value_full, preferred_element_type=jnp.float32
        )
        source_part, prenorm_part = norm_backward(source, inverse_first, prenorm_f, first_grad)
        input_rows.append((middle_grad + source_part).astype(jnp.bfloat16))
        prenorm_total = prenorm_total + prenorm_part
        saved = (normed_first, query_grad, key_grad, value_grad, attended, branch_grad)
        weight_term, shard_rows = weight_terms(*saved, shard_count)
        reduced = lax.psum_scatter(
            weight_term(jnp.int32(0), lax.axis_size("shard") * shard_rows).astype(jnp.bfloat16),
            "shard",
            scatter_dimension=0,
            tiled=True,
        ).astype(jnp.float32)
        attn_total = reduced if attn_total is None else attn_total + reduced
    gain_sums = lax.psum((prenorm_total, midnorm_total), ("grp", "shard"))
    gain_share = model_width // shard_count
    prenorm_gradient = lax.dynamic_slice_in_dim(
        gain_sums[0], shard_rank * gain_share, gain_share, 0
    )
    midnorm_gradient = lax.dynamic_slice_in_dim(
        gain_sums[1], shard_rank * gain_share, gain_share, 0
    )
    summed = (
        lax.psum(attn_total.astype(jnp.bfloat16), "grp").astype(jnp.float32),
        lax.psum(gate_total.astype(jnp.bfloat16), "grp").astype(jnp.float32),
        lax.psum(up_total.astype(jnp.bfloat16), "grp").astype(jnp.float32),
        lax.psum(down_total.astype(jnp.bfloat16), "grp").astype(jnp.float32),
    )
    attn_rows = summed[0]
    query_share = query_width // shard_count
    kv_share = kv_width // shard_count
    query_gradient = attn_rows[:query_share]
    key_gradient = attn_rows[query_share : query_share + kv_share]
    value_gradient = attn_rows[query_share + kv_share : query_share + 2 * kv_share]
    out_gradient = attn_rows[query_share + 2 * kv_share :]
    return (
        jnp.stack(mixed_rows),
        jnp.stack(input_rows),
        prenorm_gradient,
        query_gradient,
        key_gradient,
        value_gradient,
        out_gradient,
        midnorm_gradient,
        summed[1],
        summed[2],
        summed[3],
    )


def local_heads(
    tokens,
    lengths,
    prenorm_gain,
    query_weight,
    key_weight,
    value_weight,
    out_weight,
    midnorm_gain,
    gate_weight,
    up_weight,
    down_weight,
    cotangent,
):
    low = jnp.bfloat16
    shard_count = lax.axis_size("shard")
    shard_rank = lax.axis_index("shard")
    seqs, seq_dev, model_width = tokens.shape
    slot_count = seq_dev * shard_count
    own_rows = seqs * seq_dev
    score_scale = 1.0 / math.sqrt(HD)
    half = HD // 2
    upper = shard_rank % 2

    def all_rows(rows, ident):
        return gather(rows, shard_count, ident).reshape(shard_count * own_rows, -1)

    def scatter(partial, ident):
        return reduce(partial.astype(low).reshape(shard_count, own_rows, -1), ident)

    def by_seq(rows):
        width = rows.shape[-1]
        return (
            rows.reshape(shard_count, seqs, seq_dev, width)
            .transpose(1, 0, 2, 3)
            .reshape(seqs, slot_count, width)
        )

    def by_device(rows):
        width = rows.shape[-1]
        return (
            rows.reshape(seqs, shard_count, seq_dev, width)
            .transpose(1, 0, 2, 3)
            .reshape(shard_count * own_rows, width)
        )

    def times(rows, weight):
        return jnp.einsum("ta,ba->tb", rows, weight, preferred_element_type=jnp.float32)

    def into(rows, weight):
        return jnp.dot(rows, weight, preferred_element_type=jnp.float32)

    def outer(left, right):
        return jnp.einsum("tb,ta->ba", left, right, preferred_element_type=jnp.float32)

    key_pos = jnp.arange(slot_count, dtype=jnp.int32)
    local_pos = shard_rank * seq_dev + jnp.arange(seq_dev, dtype=jnp.int32)
    inverse_freq = theta_base ** (-(jnp.arange(0, HD, 2).astype(jnp.float32) / HD))
    angles = key_pos.astype(jnp.float32)[:, None] * inverse_freq[None, :]
    cosine_table = jnp.concatenate([jnp.cos(angles), jnp.cos(angles)], -1)
    sine_table = jnp.concatenate([jnp.sin(angles), jnp.sin(angles)], -1)

    gains = jnp.broadcast_to(
        jnp.stack([prenorm_gain, midnorm_gain])[:, None, :], (2, 8, prenorm_gain.shape[0])
    ).reshape(16, -1)
    tokens_all, gains = first_gather(
        tokens.reshape(own_rows, model_width), gains, shard_count, 1
    )
    gains = gains.astype(jnp.float32)
    prenorm_f = gains[:, 0].reshape(-1)
    midnorm_f = gains[:, 8].reshape(-1)
    valid_rows = (local_pos[None, :] < lengths[:, None]).reshape(own_rows, 1)
    cot_low = jnp.where(valid_rows, cotangent.reshape(own_rows, model_width), jnp.zeros((), low))

    swaps = [(rank, rank ^ 1) for rank in range(shard_count)]
    swapped = lax.ppermute(jnp.concatenate([key_weight, value_weight], 0), "shard", swaps)
    key_swap, value_swap = swapped[:half], swapped[half:]

    def whole_head(own, other):
        return jnp.concatenate(
            [jnp.where(upper == 0, own, other), jnp.where(upper == 0, other, own)], 0
        )

    key_head = whole_head(key_weight, key_swap)
    value_head = whole_head(value_weight, value_swap)

    source = tokens.reshape(own_rows, model_width).astype(jnp.float32)
    inverse_first = lax.rsqrt(jnp.mean(source * source, -1, keepdims=True) + epsilon)
    normed_first = (
        norm_forward(
            tokens_all.reshape(shard_count * own_rows, model_width).astype(jnp.float32), prenorm_f
        )[0]
    ).astype(low)
    cot_all = all_rows(cot_low, 3)

    queries = rotate(by_seq(times(normed_first, query_weight)), cosine_table, sine_table).astype(low)
    keys = rotate(by_seq(times(normed_first, key_head)), cosine_table, sine_table).astype(low)
    values = by_seq(times(normed_first, value_head).astype(low))
    scores = (
        jnp.einsum("sqd,skd->sqk", queries, keys, preferred_element_type=jnp.float32) * score_scale
    )
    allowed = (key_pos[None, None, :] <= key_pos[None, :, None]) & (
        key_pos[None, None, :] < lengths[:, None, None]
    )
    scores = jnp.where(allowed, scores, masked_value)
    exp_scores = jnp.exp(scores - jnp.max(scores, -1, keepdims=True))
    probs = exp_scores / jnp.sum(exp_scores, -1, keepdims=True)
    probs_low = probs.astype(low)
    attended = by_device(
        jnp.einsum(
            "sqk,skd->sqd", probs_low, values, preferred_element_type=jnp.float32
        ).astype(low)
    )
    middle = source + scatter(into(attended, out_weight), 4)
    scaled_second, inverse_second = norm_forward(middle, midnorm_f)
    second_grad, ffn_parts, mine, theirs = ffn(
        scaled_second.astype(low),
        cot_all.reshape(shard_count, own_rows, model_width),
        gate_weight,
        up_weight,
        down_weight,
        5,
    )
    ffn_pair = (mine.astype(F32) + theirs.astype(F32)).astype(low)

    middle_part, midnorm_part = norm_backward(middle, inverse_second, midnorm_f, second_grad)
    middle_grad = cot_low.astype(jnp.float32) + middle_part
    bias = jnp.where(key_pos[None, None, :] < lengths[:, None, None], 0.0, -1.0)
    first_grad, ffn_part, ffn_other, mine, theirs = attention_grad(
        middle_grad.astype(low),
        bias,
        cosine_table,
        sine_table,
        ffn_parts,
        normed_first.reshape(shard_count, own_rows, model_width),
        attended,
        queries,
        keys,
        values,
        query_weight,
        key_head,
        value_head,
        out_weight,
        ffn_pair,
        6,
    )
    mixed = jnp.where(valid_rows, middle + ffn_part, 0.0).astype(low)
    attn_pair = (mine.astype(F32) + theirs.astype(F32)).astype(low)
    attn_total = both_halves(attn_pair, between_chips(attn_pair))
    down_total, gate_total, up_total = (
        both_halves(ffn_pair[i], ffn_other[i]) for i in range(3)
    )

    source_part, prenorm_part = norm_backward(source, inverse_first, prenorm_f, first_grad)
    input_gradient = (middle_grad + source_part).astype(low)

    gain_parts = jnp.stack([prenorm_part, midnorm_part]).reshape(2, shard_count, 1, -1)
    gain_parts = jnp.broadcast_to(
        gain_parts.transpose(1, 0, 2, 3), (shard_count, 2, 8, gain_parts.shape[-1])
    )
    gain_own = gain_sum(gain_parts, lax.axis_size("grp"), 10)[:, 0]
    share = query_weight.shape[0]
    kv_share = key_weight.shape[0]
    return (
        mixed.reshape(tokens.shape),
        input_gradient.reshape(tokens.shape),
        gain_own[0],
        attn_total[share : 2 * share],
        attn_total[2 * share : 2 * share + kv_share],
        attn_total[2 * share + kv_share :],
        attn_total[:share],
        gain_own[1],
        gate_total,
        up_total,
        down_total,
    )


def solution(mesh):
    local = local_heads if mesh.shape["shard"] == NH else local_rows
    in_specs = (
        P("grp", "shard", None),
        P("grp"),
        P("shard"),
        P("shard", None),
        P("shard", None),
        P("shard", None),
        P("shard", None),
        P("shard"),
        P("shard", None),
        P("shard", None),
        P("shard", None),
        P("grp", "shard", None),
    )
    out_specs = (
        P("grp", "shard", None),
        P("grp", "shard", None),
        P("shard"),
        P("shard", None),
        P("shard", None),
        P("shard", None),
        P("shard", None),
        P("shard"),
        P("shard", None),
        P("shard", None),
        P("shard", None),
    )
    return jax.shard_map(local, mesh=mesh, in_specs=in_specs, out_specs=out_specs, check_vma=False)
```

```python
import functools
import math

import jax
import jax.numpy as jnp
from jax import lax
from jax.experimental import pallas as pl
from jax.experimental.pallas import tpu as pltpu
from jax.sharding import PartitionSpec as P

NH = 8
KVH = 4
HD = 256
MASKED = -1e30
EPSILON = 1e-06
DEPTH = 2
MESH = pl.DeviceIdType.MESH
F32 = jnp.float32
VMEM_LIMIT = 66_000_000


def either(condition, action):
    pl.when(condition)(action)


def total_into(dst, *srcs):
    step = 16

    @pl.loop(0, dst.shape[0] // step)
    def _(i):
        at = pl.ds(pl.multiple_of(i * step, step), step)
        value = srcs[0][at].astype(F32)
        for src in srcs[1:]:
            value = value + src[at].astype(F32)
        dst[at] = value.astype(dst.dtype)


class Place:
    def __init__(self, line):
        self.line = line
        self.me = lax.axis_index("shard")
        self.z = self.me // 2
        self.y = lax.rem(self.me, 2)
        self.cross = self.me + 1 - 2 * self.y
        self.low_end = self.z == 0
        self.high_end = self.z == line - 1
        near = []
        for z in range(line):
            order = [z]
            for k in range(1, line):
                order += [d for d in (z - k, z + k) if 0 <= d < line]
            near.append(order)
        self.tables = near

    def near(self, i):
        out = jnp.int32(0)
        for z in range(self.line):
            row = jnp.int32(self.tables[z][0])
            for k in range(1, self.line):
                row = jnp.where(i == k, self.tables[z][k], row)
            out = jnp.where(self.z == z, row, out)
        return out

    def far(self, i):
        return self.near(self.line - 1 - i)

    def greet(self, groups):
        barrier = pltpu.get_barrier_semaphore()
        count = 2 * self.line
        rank = lax.axis_index("grp")
        for step in range(1, count):
            pl.semaphore_signal(
                barrier,
                inc=1,
                device_id={"shard": lax.rem(self.me + step, count)},
                device_id_type=MESH,
            )
        for step in range(1, groups):
            pl.semaphore_signal(
                barrier,
                inc=1,
                device_id={"grp": lax.rem(rank + step, groups)},
                device_id_type=MESH,
            )
        pl.semaphore_wait(barrier, count + groups - 2)


class Gather:
    UP, DOWN, CROSS = 0, 1, 2

    def __init__(self, place, split, own, out, local_sem, send_sem, recv_sem):
        self.p, self.own, self.out = place, own, out
        self.local_sem, self.send_sem, self.recv_sem = local_sem, send_sem, recv_sem
        self.parts = (pl.ds(0, split), pl.ds(split, own.shape[0] - split))

    def copy(self, way, origin, part, own=False):
        p = self.p
        peer = (p.me + 2, p.me - 2, p.cross)[way]
        at = self.parts[part]
        return pltpu.make_async_remote_copy(
            src_ref=self.own.at[at] if own else self.out.at[origin, at],
            dst_ref=self.out.at[origin, at],
            send_sem=self.send_sem.at[way, origin, part],
            recv_sem=self.recv_sem.at[origin, part],
            device_id={"shard": peer},
            device_id_type=MESH,
        )

    def arrived(self, origin, part):
        self.copy(self.CROSS, origin, part).wait_recv()

    def start(self):
        p = self.p
        self.keep = pltpu.make_async_copy(self.own, self.out.at[p.me], self.local_sem)
        self.keep.start()
        self.copy(self.CROSS, p.me, 1, True).start()
        self.copy(self.CROSS, p.me, 0, True).start()
        for part in (0, 1):
            either(p.z < p.line - 1, lambda: self.copy(self.UP, p.me, part, True).start())
            either(p.z > 0, lambda: self.copy(self.DOWN, p.me, part, True).start())
        self.arrived(p.cross, 1)
        either(p.z < p.line - 1, lambda: self.copy(self.UP, p.cross, 1).start())
        either(p.z > 0, lambda: self.copy(self.DOWN, p.cross, 1).start())
        self.keep.wait()

    def hop(self, k):
        p = self.p

        def take(origin, other, way, more):
            self.arrived(origin, 0)
            self.copy(self.CROSS, origin, 0).start()
            either(more, lambda: self.copy(way, origin, 0).start())
            for block in (origin, other):
                self.arrived(block, 1)
                either(more, lambda: self.copy(way, block, 1).start())

        below, above = p.me - 2 * k, p.me + 2 * k
        either(p.z - k >= 0, lambda: take(below, p.cross - 2 * k, self.UP, p.z < p.line - 1))
        either(p.z + k < p.line, lambda: take(above, p.cross + 2 * k, self.DOWN, p.z > 0))

    def whole(self, position):
        self.arrived(2 * position + 1 - self.p.y, 0)

    def drain(self):
        p = self.p

        @pl.loop(0, p.line)
        def _(d):
            mine, other = 2 * d + p.y, 2 * d + 1 - p.y
            self.copy(self.CROSS, mine, 0).wait_send()

            @pl.when(d == p.z)
            def _():
                self.copy(self.CROSS, mine, 1).wait_send()

            @pl.when((d <= p.z) & (p.z < p.line - 1))
            def _():
                for block, part in ((mine, 0), (mine, 1), (other, 1)):
                    self.copy(self.UP, block, part).wait_send()

            @pl.when((d >= p.z) & (p.z > 0))
            def _():
                for block, part in ((mine, 0), (mine, 1), (other, 1)):
                    self.copy(self.DOWN, block, part).wait_send()


class Reduce:
    UP, DOWN, CROSS, BUP, BDN, BX = 0, 1, 2, 3, 5, 7
    N_SCRATCH = 9

    @staticmethod
    def scratch(line, rows, split, width, dtype):
        v = pltpu.VMEM
        rest = rows - split
        dma = pltpu.SemaphoreType.DMA
        return (
            [v((line, split, width), dtype)] * 3
            + [v((line, 2, rest, width), dtype)] * 2
            + [v((rest, width), dtype)] * 2
            + [dma((8, line)), dma((8, line))]
        )

    def __init__(self, place, split, parts, out, scratch):
        self.p, self.parts, self.out = place, parts, out
        self.cross_in, self.up_in, self.down_in, self.bup_in, self.bdn_in = scratch[:5]
        self.bx_out, self.bx_in, self.send_sem, self.recv_sem = scratch[5:]
        self.a = pl.ds(0, split)
        self.b = pl.ds(split, parts.shape[1] - split)

    def desc(self, way, slot, src, dst, peer):
        return pltpu.make_async_remote_copy(
            src_ref=src,
            dst_ref=dst,
            send_sem=self.send_sem.at[way, slot],
            recv_sem=self.recv_sem.at[way, slot],
            device_id={"shard": peer},
            device_id_type=MESH,
        )

    def cross_copy(self, d):
        p = self.p
        return self.desc(
            self.CROSS, d, self.parts.at[2 * d + 1 - p.y, self.a], self.cross_in.at[d], p.cross
        )

    def line_copy(self, up, d):
        p = self.p
        if up:
            return self.desc(self.UP, d, self.cross_in.at[d], self.up_in.at[d], p.me + 2)
        return self.desc(self.DOWN, d, self.cross_in.at[d], self.down_in.at[d], p.me - 2)

    def b_copy(self, up, d, o, src=None):
        p = self.p
        held = self.bup_in if up else self.bdn_in
        return self.desc(
            (self.BUP if up else self.BDN) + o,
            d,
            held.at[d, o] if src is None else src,
            held.at[d, o],
            p.me + 2 if up else p.me - 2,
        )

    def bx_copy(self):
        return self.desc(self.BX, 0, self.bx_out, self.bx_in, self.p.cross)

    def column(self, o):
        return self.p.y if o == 0 else 1 - self.p.y

    def send_across(self, i):
        self.cross_copy(self.p.far(i)).start()

    def b_hop(self, i):
        p = self.p
        d = p.far(i)

        def go(up):
            first = p.low_end if up else p.high_end
            held = self.bup_in if up else self.bdn_in
            for o in (1, 0):
                mine = self.parts.at[2 * d + self.column(o), self.b]
                either(first, lambda: self.b_copy(up, d, o, mine).start())

                @pl.when(jnp.logical_not(first))
                def _():
                    self.b_copy(up, d, o).wait_recv()
                    total_into(held.at[d, o], mine, held.at[d, o])
                    self.b_copy(up, d, o).start()

        either(d > p.z, lambda: go(True))
        either(d < p.z, lambda: go(False))

    def hop(self, i):
        p = self.p
        d = p.far(i)
        self.cross_copy(d).wait_recv()
        mine = self.parts.at[2 * d + p.y, self.a]
        held = self.cross_in.at[d]

        def go(up):
            first = p.low_end if up else p.high_end
            came = self.up_in if up else self.down_in
            either(first, lambda: total_into(held, mine, held))

            @pl.when(jnp.logical_not(first))
            def _():
                self.line_copy(up, d).wait_recv()
                total_into(held, mine, held, came.at[d])

            self.line_copy(up, d).start()

        either(d > p.z, lambda: go(True))
        either(d < p.z, lambda: go(False))

    def close(self, dst, mine, ups, downs):
        p = self.p
        either(p.low_end, lambda: total_into(dst, *mine, downs))
        either(p.high_end, lambda: total_into(dst, *mine, ups))
        either(
            jnp.logical_not(p.low_end | p.high_end), lambda: total_into(dst, *mine, ups, downs)
        )

    def finish(self):
        p = self.p
        for o in (1, 0):
            either(jnp.logical_not(p.low_end), lambda: self.b_copy(True, p.z, o).wait_recv())
            either(jnp.logical_not(p.high_end), lambda: self.b_copy(False, p.z, o).wait_recv())
            if o:
                mine = self.parts.at[2 * p.z + self.column(o), self.b]
                self.close(self.bx_out, (mine,), self.bup_in.at[p.z, o], self.bdn_in.at[p.z, o])
                self.bx_copy().start()
        self.bx_copy().wait_recv()
        self.close(
            self.out.at[self.b],
            (self.parts.at[p.me, self.b], self.bx_in),
            self.bup_in.at[p.z, 0],
            self.bdn_in.at[p.z, 0],
        )
        self.cross_copy(p.z).wait_recv()
        either(jnp.logical_not(p.low_end), lambda: self.line_copy(True, p.z).wait_recv())
        either(jnp.logical_not(p.high_end), lambda: self.line_copy(False, p.z).wait_recv())
        self.close(
            self.out.at[self.a],
            (self.parts.at[p.me, self.a], self.cross_in.at[p.z]),
            self.up_in.at[p.z],
            self.down_in.at[p.z],
        )

    def drain(self):
        p = self.p
        self.bx_copy().wait_send()

        @pl.loop(0, p.line)
        def _(d):
            self.cross_copy(d).wait_send()

            @pl.when(d > p.z)
            def _():
                self.line_copy(True, d).wait_send()
                self.b_copy(True, d, 0).wait_send()
                self.b_copy(True, d, 1).wait_send()

            @pl.when(d < p.z)
            def _():
                self.line_copy(False, d).wait_send()
                self.b_copy(False, d, 0).wait_send()
                self.b_copy(False, d, 1).wait_send()


def dot(a, b):
    return jnp.dot(a, b, preferred_element_type=F32)


def dot_t(a, b):
    return lax.dot_general(a, b, (((1,), (1,)), ((), ())), preferred_element_type=F32)


def t_dot(a, b):
    return lax.dot_general(a, b, (((0,), (0,)), ((), ())), preferred_element_type=F32)


def to_peer(axis, peer, src, dst, send_sem, recv_sem):
    return pltpu.make_async_remote_copy(
        src_ref=src,
        dst_ref=dst,
        send_sem=send_sem,
        recv_sem=recv_sem,
        device_id={axis: peer},
        device_id_type=MESH,
    )


def turn_by(v, cosine, sine):
    half = v.shape[-1] // 2
    a, b = v[:, :half], v[:, half:]
    return jnp.concatenate([a * cosine - b * sine, b * cosine + a * sine], -1)


def turn_back(v, cosine, sine):
    return turn_by(v, cosine, -sine)


def probabilities(query, keys, rows_from, bias):
    scores = dot_t(query, keys) * (1.0 / math.sqrt(HD))
    row = lax.broadcasted_iota(jnp.int32, scores.shape, 0) + rows_from
    col = lax.broadcasted_iota(jnp.int32, scores.shape, 1)
    scores = jnp.where((col <= row) & (bias >= 0.0), scores, MASKED)
    weight = jnp.exp(scores - jnp.max(scores, -1, keepdims=True))
    return weight / jnp.sum(weight, -1, keepdims=True)


def start_all(copies):
    for c in copies:
        c.start()


def wait_all(copies):
    for c in copies:
        c.wait()


def hbm():
    return pl.BlockSpec(memory_space=pl.ANY)


def vm():
    return pl.BlockSpec(memory_space=pltpu.VMEM)


def params(ident):
    return pltpu.CompilerParams(
        collective_id=ident, has_side_effects=True, vmem_limit_bytes=VMEM_LIMIT
    )


DMA = pltpu.SemaphoreType.DMA


def gather_sems(count):
    return [DMA, DMA((3, count, 2)), DMA((count, 2))]


def attention_kernel(
    line, split, groups, seqs,
    own, cot_own, small, bias, freq, wq_hbm, wk_hbm, wv_hbm, wo_hbm,
    branch, small_out, normed_hbm, cot_hbm, q_hbm, k_hbm, v_hbm, attended_hbm, wkv_hbm, cos_hbm, sin_hbm,
    rows_all, normed, cot_all, q, k, v, attended, wq, wkv, wo, cosine, sine, parts,
    *scratch,
):
    p = Place(line)
    count = 2 * line
    rank = lax.axis_index("grp")
    g1, g2 = scratch[:3], scratch[3:6]
    (load_sem, small_send, small_recv, wy_send, wg_send, w_recv, save_sem) = scratch[6:13]
    r_scratch = scratch[13:]
    half = wk_hbm.shape[0]
    piece = half // 2
    at_own = pl.ds(pl.multiple_of(p.y * half, half), half)
    loads = [
        pltpu.make_async_copy(src, dst, load_sem.at[i])
        for i, (src, dst) in enumerate(
            (
                (wk_hbm, wkv.at[0, at_own]),
                (wv_hbm, wkv.at[1, at_own]),
                (wq_hbm, wq),
                (wo_hbm, wo),
            )
        )
    ]
    start_all(loads)
    p.greet(groups)

    def small_copy(step, peer, origin):
        return to_peer(
            "shard", peer, small, small_out.at[origin], small_send.at[step], small_recv.at[step]
        )

    for step in range(1, count):
        small_copy(step, lax.rem(p.me + step, count), p.me).start()
    gather = Gather(p, split, own, rows_all, *g1)
    gather.start()
    small_out[p.me] = small[...]

    def rows_of(quarter, column):
        return wkv.at[
            quarter // 2,
            pl.ds(pl.multiple_of(column * half + lax.rem(quarter, 2) * piece, piece), piece),
        ]

    def across():
        ref = rows_of(rank, p.y)
        return to_peer("shard", p.cross, ref, ref, wy_send, w_recv.at[rank])

    def share(step):
        ref = rows_of(rank, 1 - p.y)
        return to_peer(
            "grp", lax.rem(rank + step, groups), ref, ref, wg_send.at[step], w_recv.at[rank]
        )

    wait_all(loads)
    across().start()
    pos = lax.broadcasted_iota(jnp.int32, cosine.shape, 0).astype(F32)
    angle = pos * freq[...]
    cosine[...] = jnp.cos(angle)
    sine[...] = jnp.sin(angle)
    for step in range(1, count):
        small_copy(step, p.me, lax.rem(p.me + count - step, count)).wait_recv()
    gain = jnp.concatenate([small_out[s, 0:1] for s in range(count)], 1).astype(F32)
    across().wait_recv()
    for step in range(1, groups):
        share(step).start()
    rows = own.shape[0]
    pair = 2 * rows
    slots = rows // seqs
    low = own.dtype
    for step in range(1, groups):
        quarter = lax.rem(rank + step, groups)
        ref = rows_of(quarter, 1 - p.y)
        to_peer("grp", rank, ref, ref, wg_send.at[step], w_recv.at[quarter]).wait_recv()

    @pl.loop(0, line)
    def _(i):
        gather.hop(i + 1)
        d = p.near(i)
        gather.whole(d)
        x = rows_all[pl.ds(2 * d, 2)].reshape(pair, -1).astype(F32)
        n = (
            x * lax.rsqrt(jnp.mean(x * x, -1, keepdims=True) + EPSILON) * gain
        ).astype(low)
        normed[pl.ds(2 * d, 2)] = n.reshape(2, rows, -1)
        at = pl.ds(pl.multiple_of(d * 2 * slots, 2 * slots), 2 * slots)
        c, s = cosine[at], sine[at]

        def by_rows(t):
            return jnp.concatenate([t[:slots]] * seqs + [t[slots:]] * seqs, 0)

        c, s = by_rows(c), by_rows(s)

        def put(target, value):
            for block in range(2):
                for m in range(seqs):
                    to = pl.ds(
                        pl.multiple_of(d * 2 * slots + block * slots, slots), slots
                    )
                    target[m, to] = value[block * rows + m * slots : block * rows + (m + 1) * slots]

        put(q, turn_by(dot_t(n, wq[...]), c, s).astype(low))
        put(k, turn_by(dot_t(n, wkv[0]), c, s).astype(low))
        put(v, dot_t(n, wkv[1]).astype(low))

    saves = [
        pltpu.make_async_copy(src, dst, save_sem.at[i])
        for i, (src, dst) in enumerate(
            (
                (normed, normed_hbm),
                (q, q_hbm),
                (k, k_hbm),
                (v, v_hbm),
                (wkv, wkv_hbm),
                (cosine, cos_hbm),
                (sine, sin_hbm),
            )
        )
    ]
    start_all(saves)
    cots = Gather(p, split, cot_own, cot_all, *g2)
    cots.start()
    total_slots = q.shape[1]
    tile = min(256, total_slots)

    @pl.loop(0, seqs)
    def _(n):
        for t in range(total_slots // tile):
            span = (t + 1) * tile
            at = pl.ds(t * tile, tile)
            probs = probabilities(q[n, at], k[n, pl.ds(0, span)], t * tile, bias[n][:, :span])
            out = dot(probs.astype(low), v[n, pl.ds(0, span)]).astype(low)
            for c in range(tile // slots):
                b = (t * tile) // slots + c
                attended[pl.ds(pl.multiple_of(b * rows + n * slots, slots), slots)] = out[
                    c * slots : (c + 1) * slots
                ]
        cots.hop(n + 1)

    for h in range(seqs + 1, line):
        cots.hop(h)

    @pl.loop(0, line)
    def _(d):
        at = pl.ds(pl.multiple_of(d * pair, pair), pair)
        parts[pl.ds(2 * d, 2)] = dot(attended[at], wo[...]).astype(low).reshape(2, rows, -1)

    reduce = Reduce(p, split, parts, branch, r_scratch)
    for i in range(DEPTH):
        reduce.send_across(i)
    saves2 = [pltpu.make_async_copy(attended, attended_hbm, save_sem.at[7])]
    start_all(saves2)
    for d in range(line):
        cots.whole(d)
    saves3 = [pltpu.make_async_copy(cot_all, cot_hbm, save_sem.at[8])]
    start_all(saves3)
    for i in range(line - 1):
        reduce.b_hop(i)
    for i in range(line - 1):
        reduce.hop(i)
        if i + DEPTH < line:
            reduce.send_across(i + DEPTH)
    reduce.finish()
    reduce.drain()
    gather.drain()
    cots.drain()
    wait_all(saves + saves2 + saves3)
    across().wait_send()
    for step in range(1, groups):
        share(step).wait_send()
    for step in range(1, count):
        small_copy(step, lax.rem(p.me + step, count), p.me).wait_send()


def attention(own, cot, small, bias, freq, wq, wk, wv, wo, count, groups, ident, split=112):
    rows, width = own.shape
    seqs, _, total_slots = bias.shape
    line = count // 2
    low = own.dtype
    v = pltpu.VMEM
    shape = jax.ShapeDtypeStruct
    hd = wq.shape[0]
    big = (count, rows, width)
    head = (seqs, total_slots, hd)
    table = (total_slots, hd // 2)
    flat = (count * rows, hd)
    return pl.pallas_call(
        functools.partial(attention_kernel, line, split, groups, seqs),
        out_shape=(
            shape((rows, width), F32),
            shape((count,) + small.shape, small.dtype),
            shape(big, low),
            shape(big, low),
            shape(head, low),
            shape(head, low),
            shape(head, low),
            shape(flat, low),
            shape((2, hd, width), low),
            shape(table, F32),
            shape(table, F32),
        ),
        in_specs=[vm()] * 5 + [hbm()] * 4,
        out_specs=(vm(), vm()) + (hbm(),) * 9,
        scratch_shapes=[
            v(big, low), v(big, low), v(big, low), v(head, low), v(head, low), v(head, low), v(flat, low),
            v((hd, width), low), v((2, hd, width), low), v((hd, width), low), v(table, F32), v(table, F32), v(big, low),
        ]
        + gather_sems(count) * 2
        + [DMA((4,)), DMA((count,)), DMA((count,)), DMA, DMA((groups,)), DMA((groups,)), DMA((9,))]
        + Reduce.scratch(line, rows, split, width, low),
        compiler_params=params(ident),
        name="attention",
    )(own, cot, small, bias, freq, wq, wk, wv, wo)


def ffn_kernel(
    line, split, groups,
    own, cot_hbm, gate_hbm, up_hbm, down_hbm,
    second, ffn_hbm, pair_hbm, total_hbm,
    normed, cot, gate_w, up_w, down_w, hidden, gate_g, up_g, parts, stage, theirs, chip_in,
    *scratch,
):
    p = Place(line)
    rank = lax.axis_index("grp")
    core = lax.rem(rank, 2)
    partner = rank + 1 - 2 * core
    opposite = lax.rem(rank + 2, groups)
    (load_sem, out_sem, stage_send, stage_recv, chip_send, chip_recv, back_send, back_recv) = scratch[3:11]
    loads = [
        pltpu.make_async_copy(src, dst, load_sem.at[i])
        for i, (src, dst) in enumerate(
            ((gate_hbm, gate_w), (up_hbm, up_w), (cot_hbm, cot), (down_hbm, down_w))
        )
    ]
    start_all(loads)
    p.greet(groups)
    gather = Gather(p, split, own, normed, *scratch[:3])
    gather.start()
    wait_all(loads)
    rows = own.shape[0]
    pair = 2 * rows
    low = own.dtype

    @pl.loop(0, line)
    def _(i):
        gather.hop(i + 1)
        d = p.near(i)
        gather.whole(d)
        x = normed[pl.ds(2 * d, 2)].reshape(pair, -1)
        g = dot_t(x, gate_w[...])
        u = dot_t(x, up_w[...])
        dh = dot_t(cot[pl.ds(2 * d, 2)].reshape(pair, -1), down_w[...])
        s = 1.0 / (1.0 + jnp.exp(-g))
        silu = g * s
        at = pl.ds(pl.multiple_of(d * pair, pair), pair)
        hidden[at] = (silu * u).astype(low)
        up_g[at] = (dh * silu).astype(low)
        gate_g[at] = (dh * u * s * (1.0 + g * (1.0 - s))).astype(low)
        part = dot(gate_g[at], gate_w[...]) + dot(up_g[at], up_w[...])
        parts[pl.ds(2 * d, 2)] = part.astype(low).reshape(2, rows, -1)

    reduce = Reduce(p, split, parts, second, scratch[11:])
    for i in range(DEPTH):
        reduce.send_across(i)
    for i in range(line - 1):
        reduce.b_hop(i)

    units = hidden.shape[1]
    quarter = units // 4
    half = units // 2
    mine = (up_w.at[pl.ds(0, half)], gate_w.at[pl.ds(0, half)], gate_w.at[pl.ds(half, half)])

    def to_partner(which, j):
        return to_peer(
            "grp",
            partner,
            stage.at[j],
            theirs.at[which, pl.ds(j * quarter, quarter)],
            stage_send.at[j],
            stage_recv.at[which, j],
        )

    def gradient(which, left, right):
        def block(q):
            cols = pl.ds(pl.multiple_of(q * quarter, quarter), quarter)
            return t_dot(left[:, cols], right[...].reshape(left.shape[0], -1)).astype(low)

        @pl.loop(0, 2)
        def _(j):
            if which:
                to_partner(which - 1, j).wait_send()
            stage[j] = block(2 * (1 - core) + j)
            to_partner(which, j).start()

        @pl.loop(0, 2)
        def _(j):
            at = pl.ds(pl.multiple_of(j * quarter, quarter), quarter)
            mine[which][at] = block(2 * core + j)

    def add_theirs(which):
        for j in range(2):
            to_partner(which, j).wait_recv()
        total_into(mine[which], mine[which], theirs.at[which])

    def chip_copy():
        return to_peer("grp", opposite, mine[0], chip_in, chip_send, chip_recv)

    def save_pair(which):
        return pltpu.make_async_copy(mine[which], pair_hbm.at[which - 1], out_sem.at[which])

    gradient(0, hidden, cot)
    reduce.hop(0)
    reduce.send_across(DEPTH)
    add_theirs(0)
    chip_copy().start()
    gradient(1, gate_g, normed)
    reduce.hop(1)
    reduce.send_across(DEPTH + 1)
    add_theirs(1)
    save_pair(1).start()
    gradient(2, up_g, normed)
    reduce.hop(2)
    gather.drain()

    @pl.loop(0, line)
    def _(d):
        at = pl.ds(pl.multiple_of(d * pair, pair), pair)
        normed[pl.ds(2 * d, 2)] = dot(hidden[at], down_w[...]).astype(low).reshape(2, rows, -1)

    ffn_save = pltpu.make_async_copy(normed, ffn_hbm, out_sem.at[0])
    ffn_save.start()
    add_theirs(2)
    save_pair(2).start()
    reduce.finish()
    for j in range(2):
        to_partner(2, j).wait_send()

    at = pl.ds(pl.multiple_of(core * half, half), half)
    keep = pltpu.make_async_copy(chip_in, total_hbm.at[at], out_sem.at[3])
    give = to_peer("grp", partner, chip_in, total_hbm.at[at], back_send, back_recv)
    chip_copy().wait_recv()
    total_into(chip_in, mine[0], chip_in)
    keep.start()
    give.start()
    reduce.drain()
    chip_copy().wait_send()
    ffn_save.wait()
    for which in (1, 2):
        save_pair(which).wait()
    keep.wait()
    give.wait()


def ffn(own, cot, gate_w, up_w, down_w, groups, ident, split=112):
    rows, width = own.shape
    count = cot.shape[0]
    line = count // 2
    units = gate_w.shape[0]
    low = own.dtype
    v = pltpu.VMEM
    tokens = count * rows
    shape = jax.ShapeDtypeStruct
    big = (count, rows, width)
    half = (units // 2, width)
    return pl.pallas_call(
        functools.partial(ffn_kernel, line, split, groups),
        out_shape=(
            shape((rows, width), F32),
            shape(big, low),
            shape((2,) + half, low),
            shape((units, width), low),
        ),
        in_specs=[vm()] + [hbm()] * 4,
        out_specs=(vm(), hbm(), hbm(), hbm()),
        scratch_shapes=[v(big, low)] * 2
        + [v((units, width), low)] * 3
        + [v((tokens, units), low)] * 3
        + [v(big, low), v((2, units // 4, width), low), v((3,) + half, low), v(half, low)]
        + gather_sems(count)
        + [DMA((4,)), DMA((4,)), DMA((2,)), DMA((3, 2)), DMA, DMA, DMA, DMA]
        + Reduce.scratch(line, rows, split, width, low),
        compiler_params=params(ident),
        name="ffn",
    )(own, cot, gate_w, up_w, down_w)


def attention_grad_kernel(
    line, split, groups, seqs,
    own, bias, cosine, sine, gain, gain_parts,
    ffn_hbm, normed_hbm, attended_hbm, q_hbm, k_hbm, v_hbm, wq_hbm, wkv_hbm, wo_hbm, sums_hbm,
    first, ffn_own, gain_out, total_hbm, attn_hbm,
    dbranch, normed, attended, q, k, v, wq, wkv, wo, da, dk_acc, dv_acc, dq_rows, dk_rows, dv_rows,
    halves, half_in, ffn_parts, parts, sums, sums_in, stage, mine, theirs, mine_in, gain_held, gain_in, gain_sum, gain_all,
    *scratch,
):
    p = Place(line)
    count = 2 * line
    rank = lax.axis_index("grp")
    core = lax.rem(rank, 2)
    partner = rank + 1 - 2 * core
    opposite = lax.rem(rank + 2, groups)
    (
        load_sem, chip_send, chip_recv, half_send, half_recv, stage_send, stage_recv,
        back_send, back_recv, keep_sem, ga_send, ga_recv, gb_send, gb_recv,
    ) = scratch[3:17]
    n = Reduce.N_SCRATCH
    loads = [
        pltpu.make_async_copy(src, dst, load_sem.at[i])
        for i, (src, dst) in enumerate(
            (
                (wo_hbm, wo),
                (ffn_hbm, ffn_parts),
                (attended_hbm, attended),
                (q_hbm, q),
                (k_hbm, k),
                (v_hbm, v),
                (wq_hbm, wq),
                (wkv_hbm, wkv),
                (normed_hbm, normed),
                (sums_hbm, sums),
            )
        )
    ]
    start_all(loads)
    p.greet(groups)
    gather = Gather(p, split, own, dbranch, *scratch[:3])
    n_sums = sums_hbm.shape[0]
    part_rows = sums.shape[1]

    def chip_copy(i):
        return to_peer(
            "grp", opposite, sums_hbm.at[i], sums_in.at[i], chip_send.at[i], chip_recv.at[i]
        )

    for i in range(n_sums):
        chip_copy(i).start()
    gather.start()
    wait_all(loads)
    rows = own.shape[0]
    pair = 2 * rows
    slots = rows // seqs
    low = own.dtype
    scale = 1.0 / math.sqrt(HD)

    @pl.loop(0, line)
    def _(i):
        gather.hop(i + 1)
        d = p.near(i)
        gather.whole(d)
        grad = dot_t(dbranch[pl.ds(2 * d, 2)].reshape(pair, -1), wo[...]).astype(low)
        for block in range(2):
            for m in range(seqs):
                at = pl.ds(pl.multiple_of(d * 2 * slots + block * slots, slots), slots)
                da[m, at] = grad[block * rows + m * slots : block * rows + (m + 1) * slots]

    ffn_sum = Reduce(p, split, ffn_parts, ffn_own, scratch[17 : 17 + n])
    for i in range(DEPTH):
        ffn_sum.send_across(i)
    for i in range(line - 1):
        ffn_sum.b_hop(i)

    chunk = stage.shape[1]

    def to_partner(b):
        return to_peer(
            "grp",
            partner,
            stage.at[b % 3],
            theirs.at[pl.ds((b % 3) * chunk, chunk)],
            stage_send.at[b % 3],
            stage_recv.at[b % 3],
        )

    def gradient(b, left, right):
        value = t_dot(left, right[...].reshape(left.shape[0], -1)).astype(low)
        keep = core == b // 3

        @pl.when(keep)
        def _():
            mine[pl.ds((b % 3) * chunk, chunk)] = value

        @pl.when(jnp.logical_not(keep))
        def _():
            stage[b % 3] = value
            to_partner(b).start()

    total_slots = q.shape[1]
    tile = min(256, total_slots)

    def backward(m):
        dk_acc[...] = jnp.zeros_like(dk_acc)
        dv_acc[...] = jnp.zeros_like(dv_acc)

        def to_rows(target, value, start, size):
            for c in range(size // slots):
                b = start // slots + c
                target[pl.ds(pl.multiple_of(b * rows + m * slots, slots), slots)] = value[
                    c * slots : (c + 1) * slots
                ]

        for t in range(total_slots // tile):
            span = (t + 1) * tile
            at = pl.ds(t * tile, tile)
            query, grad = q[m, at], da[m, at]
            keys, values = k[m, pl.ds(0, span)], v[m, pl.ds(0, span)]
            probs = probabilities(query, keys, t * tile, bias[m][:, :span])
            dprobs = dot_t(grad, values)
            inner = jnp.sum(probs * dprobs, -1, keepdims=True)
            dscores = (probs * (dprobs - inner)).astype(low)
            dq = turn_back(dot(dscores, keys) * scale, cosine[at], sine[at])
            to_rows(dq_rows, dq.astype(low), t * tile, tile)
            dk_acc[pl.ds(0, span)] += t_dot(dscores, query)
            dv_acc[pl.ds(0, span)] += t_dot(probs.astype(low), grad)
        dk = turn_back(dk_acc[...] * scale, cosine[...], sine[...])
        to_rows(dk_rows, dk.astype(low), 0, total_slots)
        to_rows(dv_rows, dv_acc[...].astype(low), 0, total_slots)

    half = HD // 2

    def swap():
        return to_peer("shard", p.cross, halves.at[1 - p.y], half_in, half_send, half_recv)

    gradient(0, attended[:, :chunk], dbranch)
    gradient(1, attended[:, chunk:], dbranch)

    @pl.loop(0, seqs)
    def _(m):
        backward(m)
        ffn_sum.hop(m)
        ffn_sum.send_across(m + DEPTH)

    for h in range(2):
        halves[h, 0] = dk_rows[:, h * half : (h + 1) * half]
        halves[h, 1] = dv_rows[:, h * half : (h + 1) * half]
    swap().start()
    gradient(2, dq_rows[:, :chunk], normed)
    gradient(3, dq_rows[:, chunk:], normed)

    @pl.loop(0, line)
    def _(d):
        at = pl.ds(pl.multiple_of(d * pair, pair), pair)
        part = dot(dq_rows[at], wq[...]) + dot(dk_rows[at], wkv[0]) + dot(dv_rows[at], wkv[1])
        parts[pl.ds(2 * d, 2)] = part.astype(low).reshape(2, rows, -1)

    for i in range(seqs, line - 1):
        ffn_sum.hop(i)
    reduce = Reduce(p, split, parts, first, scratch[17 + n :])
    for i in range(DEPTH):
        reduce.send_across(i)
    swap().wait_recv()

    def summed(which):
        return (halves[p.y, which].astype(F32) + half_in[which].astype(F32)).astype(low)

    gradient(4, summed(0), normed)
    gradient(5, summed(1), normed)

    def attn_chip():
        return to_peer(
            "grp", opposite, mine, mine_in, chip_send.at[n_sums], chip_recv.at[n_sums]
        )

    for b in range(3):
        to_partner(b).wait_recv()
    total_into(mine, mine, theirs)
    attn_chip().start()
    ffn_sum.finish()
    for i in range(line - 1):
        reduce.b_hop(i)

    def back(i):
        if i < n_sums:
            whole, size, out = sums.at[i], part_rows, total_hbm.at[i]
        else:
            whole, size, out = mine, 3 * chunk, attn_hbm
        at = pl.ds(pl.multiple_of(core * size, size), size)
        return (
            pltpu.make_async_copy(whole, out.at[at], keep_sem.at[i]),
            to_peer("grp", partner, whole, out.at[at], back_send.at[i], back_recv.at[i]),
        )

    def sum_up(i):
        chip_copy(i).wait()
        total_into(sums.at[i], sums.at[i], sums_in.at[i])
        start_all(back(i))

    def gain_copy(step, peer, origin):
        return to_peer(
            "shard", peer, gain_held.at[peer], gain_in.at[origin], ga_send.at[step], ga_recv.at[step]
        )

    def gain_group(step, peer, origin):
        return to_peer(
            "grp", peer, gain_sum, gain_all.at[origin], gb_send.at[step], gb_recv.at[step]
        )

    def gain_first():
        def body(i, total):
            at = pl.ds(pl.multiple_of(i * 16, 16), 16)
            for b in range(count):
                total = total + parts[b, at].astype(F32) * normed[b, at].astype(F32)
            return total

        total = lax.fori_loop(0, rows // 16, body, jnp.zeros((16, parts.shape[2]), F32))
        total = jnp.sum(total, 0, keepdims=True) / gain[...]
        share = gain_held.shape[2]
        for b in range(count):
            gain_held[b] = gain_parts[b]
            gain_held[b, 0:1] = total[:, b * share : (b + 1) * share]
        for step in range(1, count):
            gain_copy(step, lax.rem(p.me + step, count), p.me).start()

    def gain_second():
        for step in range(1, count):
            gain_copy(step, p.me, lax.rem(p.me + count - step, count)).wait_recv()
        gain_in[p.me] = gain_held[p.me]
        total = gain_in[0]
        for b in range(1, count):
            total = total + gain_in[b]
        gain_sum[...] = total
        gain_all[rank] = total
        for step in range(1, groups):
            gain_group(step, lax.rem(rank + step, groups), rank).start()

    reduce.hop(0)
    reduce.send_across(DEPTH)
    gain_first()
    sum_up(0)
    reduce.hop(1)
    reduce.send_across(DEPTH + 1)
    gain_second()
    reduce.hop(2)
    for i in range(1, n_sums):
        sum_up(i)
    reduce.finish()
    for step in range(1, groups):
        gain_group(step, rank, lax.rem(rank + groups - step, groups)).wait_recv()
    total = gain_all[0]
    for b in range(1, groups):
        total = total + gain_all[b]
    gain_out[...] = total
    attn_chip().wait()
    total_into(mine, mine, mine_in)
    start_all(back(n_sums))
    reduce.drain()
    ffn_sum.drain()
    gather.drain()
    swap().wait_send()
    for b in range(3):
        to_partner(b).wait_send()
    for step in range(1, count):
        gain_copy(step, lax.rem(p.me + step, count), p.me).wait_send()
    for step in range(1, groups):
        gain_group(step, lax.rem(rank + step, groups), rank).wait_send()
    for i in range(n_sums + 1):
        wait_all(back(i))


def attention_grad(
    own, bias, cosine, sine, gain, gain_parts, ffn_parts, normed, attended, q, k, v, wq, wkv, wo, sums,
    groups, ident, split=112,
):
    rows, width = own.shape
    count = normed.shape[0]
    line = count // 2
    seqs, total_slots, hd = q.shape
    low = own.dtype
    vmem = pltpu.VMEM
    tokens = count * rows
    half = hd // 2
    n_sums, part_rows, _ = sums.shape
    shape = jax.ShapeDtypeStruct
    big = vmem((count, rows, width), low)
    head = vmem((seqs, total_slots, hd), low)
    weight = vmem((hd, width), low)
    flat = vmem((tokens, hd), low)
    acc = vmem((total_slots, hd), F32)
    third = vmem((3 * half, width), low)
    g = gain_parts.shape
    return pl.pallas_call(
        functools.partial(attention_grad_kernel, line, split, groups, seqs),
        out_shape=(
            shape((rows, width), F32),
            shape((rows, width), F32),
            shape(g[1:], F32),
            shape((n_sums, 2 * part_rows, width), low),
            shape((6 * half, width), low),
        ),
        in_specs=[vm()] * 6 + [hbm()] * 10,
        out_specs=(vm(), vm(), vm(), hbm(), hbm()),
        scratch_shapes=[
            big, big, flat, head, head, head, weight, vmem((2, hd, width), low), weight, head, acc, acc,
            flat, flat, flat,
            vmem((2, 2, tokens, half), low), vmem((2, tokens, half), low), big, big,
            vmem(sums.shape, low), vmem(sums.shape, low), vmem((3, half, width), low), third, third, third,
            vmem(g, F32), vmem(g, F32), vmem(g[1:], F32), vmem((groups,) + g[1:], F32),
        ]
        + gather_sems(count)
        + [
            DMA((10,)), DMA((n_sums + 1,)), DMA((n_sums + 1,)), DMA, DMA, DMA((3,)), DMA((3,)),
            DMA((n_sums + 1,)), DMA((n_sums + 1,)), DMA((n_sums + 1,)),
            DMA((count,)), DMA((count,)), DMA((groups,)), DMA((groups,)),
        ]
        + Reduce.scratch(line, rows, split, width, low) * 2,
        compiler_params=params(ident),
        name="attention_grad",
    )(own, bias, cosine, sine, gain, gain_parts, ffn_parts, normed, attended, q, k, v, wq, wkv, wo, sums)


epsilon = 1e-06
theta_base = 1000042.0
masked_value = -1e30


def turned(source):
    half_width = source.shape[-1] // 2
    return jnp.concatenate([-source[..., half_width:], source[..., :half_width]], -1)


def rotate(source, cosine_table, sine_table):
    return source * cosine_table + turned(source) * sine_table


def unrotate(source, cosine_table, sine_table):
    return source * cosine_table - turned(source) * sine_table


def norm_forward(source, norm_gain):
    inverse = lax.rsqrt(jnp.mean(source * source, -1, keepdims=True) + epsilon)
    return (source * inverse * norm_gain, inverse)


def norm_backward(source, inverse, norm_gain, grad_out):
    weighted = grad_out * norm_gain
    inner_sum = jnp.sum(weighted * source, -1, keepdims=True)
    grad_in = (
        inverse * weighted - source * inverse * inverse * inverse * inner_sum / source.shape[-1]
    )
    return (grad_in, jnp.sum(grad_out * source * inverse, 0))


def weight_terms(normed, query_grad, key_grad, value_grad, attended, branch_grad, shard_count):
    token_count, model_width = normed.shape
    query_share = query_grad.shape[1] // shard_count
    kv_share = key_grad.shape[1] // shard_count
    shard_rows = 2 * query_share + 2 * kv_share

    def weight_term(first_row, row_count):
        blocks = row_count // shard_rows

        def columns(matrix, share_cols):
            return matrix.reshape(token_count, blocks, share_cols)

        part_query = jnp.einsum(
            "tmr,td->mrd",
            columns(query_grad, query_share),
            normed,
            preferred_element_type=jnp.float32,
        )
        part_key = jnp.einsum(
            "tmr,td->mrd", columns(key_grad, kv_share), normed, preferred_element_type=jnp.float32
        )
        part_value = jnp.einsum(
            "tmr,td->mrd", columns(value_grad, kv_share), normed, preferred_element_type=jnp.float32
        )
        part_out = jnp.einsum(
            "tmr,td->mrd",
            columns(attended, query_share),
            branch_grad,
            preferred_element_type=jnp.float32,
        )
        return jnp.concatenate([part_query, part_key, part_value, part_out], 1).reshape(
            row_count, model_width
        )

    return (weight_term, shard_rows)


def local_rows(
    tokens,
    lengths,
    prenorm_gain,
    query_weight,
    key_weight,
    value_weight,
    out_weight,
    midnorm_gain,
    gate_weight,
    up_weight,
    down_weight,
    cotangent,
):
    shard_count = lax.axis_size("shard")
    shard_rank = lax.axis_index("shard")
    micro_count, seq_dev, model_width = tokens.shape
    slot_count = seq_dev * shard_count
    repeat_heads = NH // KVH
    query_width = NH * HD
    kv_width = KVH * HD
    score_scale = 1.0 / math.sqrt(HD)
    local_pos = shard_rank * seq_dev + jnp.arange(seq_dev, dtype=jnp.int32)
    key_pos = jnp.arange(slot_count, dtype=jnp.int32)
    inverse_freq = theta_base ** (-(jnp.arange(0, HD, 2).astype(jnp.float32) / HD))
    angles = local_pos.astype(jnp.float32)[:, None] * inverse_freq[None, :]
    cosine_table = jnp.concatenate([jnp.cos(angles), jnp.cos(angles)], -1)[:, None, :]
    sine_table = jnp.concatenate([jnp.sin(angles), jnp.sin(angles)], -1)[:, None, :]
    gate_total = jnp.zeros(gate_weight.shape, jnp.float32)
    up_total = jnp.zeros(up_weight.shape, jnp.float32)
    down_total = jnp.zeros(down_weight.shape, jnp.float32)
    prenorm_total = jnp.zeros((model_width,), jnp.float32)
    midnorm_total = jnp.zeros((model_width,), jnp.float32)
    attn_total = None
    mixed_rows = []
    input_rows = []
    for micro_index in range(micro_count):
        gathered = (
            lax.all_gather(query_weight, "shard", axis=0, tiled=True),
            lax.all_gather(key_weight, "shard", axis=0, tiled=True),
            lax.all_gather(value_weight, "shard", axis=0, tiled=True),
            lax.all_gather(prenorm_gain, "shard", axis=0, tiled=True),
            lax.all_gather(midnorm_gain, "shard", axis=0, tiled=True),
        )
        query_full, key_full, value_full, prenorm_full, midnorm_full = gathered
        prenorm_f = prenorm_full.astype(jnp.float32)
        midnorm_f = midnorm_full.astype(jnp.float32)
        source = tokens[micro_index].astype(jnp.float32)
        length_now = lengths[micro_index]
        valid_rows = local_pos < length_now
        scaled_first, inverse_first = norm_forward(source, prenorm_f)
        normed_first = scaled_first.astype(jnp.bfloat16)
        query_pre = jnp.einsum(
            "sd,qd->sq", normed_first, query_full, preferred_element_type=jnp.float32
        ).reshape(seq_dev, NH, HD)
        key_pre = jnp.einsum(
            "sd,qd->sq", normed_first, key_full, preferred_element_type=jnp.float32
        ).reshape(seq_dev, KVH, HD)
        value_pre = jnp.einsum(
            "sd,qd->sq", normed_first, value_full, preferred_element_type=jnp.float32
        )
        query_rot = rotate(query_pre, cosine_table, sine_table).astype(jnp.bfloat16)
        key_rot = rotate(key_pre, cosine_table, sine_table).astype(jnp.bfloat16)
        key_value = jnp.concatenate(
            [key_rot.reshape(seq_dev, kv_width), value_pre.astype(jnp.bfloat16)], 1
        )
        kv_all = lax.all_gather(key_value, "shard", axis=0, tiled=True)
        keys_all = kv_all[:, :kv_width].reshape(slot_count, KVH, HD)
        values_all = kv_all[:, kv_width:].reshape(slot_count, KVH, HD)
        query_group = query_rot.reshape(seq_dev, KVH, repeat_heads, HD)
        scores = (
            jnp.einsum("skrd,tkd->krst", query_group, keys_all, preferred_element_type=jnp.float32)
            * score_scale
        )
        allowed = (key_pos[None, :] <= local_pos[:, None]) & (key_pos[None, :] < length_now)
        scores = jnp.where(allowed, scores, masked_value)
        row_max = jnp.max(scores, -1, keepdims=True)
        exp_scores = jnp.exp(scores - row_max)
        attention_probs = exp_scores / jnp.sum(exp_scores, -1, keepdims=True)
        probs_low = attention_probs.astype(jnp.bfloat16)
        attended = (
            jnp.einsum("krst,tkd->skrd", probs_low, values_all, preferred_element_type=jnp.float32)
            .astype(jnp.bfloat16)
            .reshape(seq_dev, query_width)
        )
        branch = jnp.dot(
            attended,
            lax.all_gather(out_weight, "shard", axis=0, tiled=True),
            preferred_element_type=jnp.float32,
        )
        middle = source + branch
        scaled_second, inverse_second = norm_forward(middle, midnorm_f)
        normed_second = scaled_second.astype(jnp.bfloat16)
        normed_all = lax.all_gather(normed_second, "shard", axis=0, tiled=True)
        gate_pre = jnp.einsum(
            "sd,fd->sf", normed_all, gate_weight, preferred_element_type=jnp.float32
        )
        up_pre = jnp.einsum("sd,fd->sf", normed_all, up_weight, preferred_element_type=jnp.float32)
        sigmoid_gate = jax.nn.sigmoid(gate_pre)
        silu_gate = gate_pre * sigmoid_gate
        hidden = (silu_gate * up_pre).astype(jnp.bfloat16)
        ffn_part = lax.psum_scatter(
            jnp.dot(hidden, down_weight, preferred_element_type=jnp.float32).astype(jnp.bfloat16),
            "shard",
            scatter_dimension=0,
            tiled=True,
        ).astype(jnp.float32)
        mixed_rows.append(
            jnp.where(valid_rows[:, None], middle + ffn_part, 0.0).astype(jnp.bfloat16)
        )
        cot_low = jnp.where(
            valid_rows[:, None], cotangent[micro_index], jnp.zeros_like(cotangent[micro_index])
        )
        cot_all = lax.all_gather(cot_low, "shard", axis=0, tiled=True)
        hidden_grad = jnp.einsum(
            "sd,fd->sf", cot_all, down_weight, preferred_element_type=jnp.float32
        )
        down_total = down_total + jnp.einsum(
            "sf,sd->fd", hidden, cot_all, preferred_element_type=jnp.float32
        )
        gate_grad = (
            hidden_grad * up_pre * sigmoid_gate * (1.0 + gate_pre * (1.0 - sigmoid_gate))
        ).astype(jnp.bfloat16)
        up_grad = (hidden_grad * silu_gate).astype(jnp.bfloat16)
        gate_total = gate_total + jnp.einsum(
            "sf,sd->fd", gate_grad, normed_all, preferred_element_type=jnp.float32
        )
        up_total = up_total + jnp.einsum(
            "sf,sd->fd", up_grad, normed_all, preferred_element_type=jnp.float32
        )
        second_grad = lax.psum_scatter(
            jnp.dot(gate_grad, gate_weight, preferred_element_type=jnp.float32)
            + jnp.dot(up_grad, up_weight, preferred_element_type=jnp.float32),
            "shard",
            scatter_dimension=0,
            tiled=True,
        )
        middle_part, midnorm_part = norm_backward(middle, inverse_second, midnorm_f, second_grad)
        middle_grad = cot_low.astype(jnp.float32) + middle_part
        midnorm_total = midnorm_total + midnorm_part
        branch_grad = middle_grad.astype(jnp.bfloat16)
        attended_grad = jnp.einsum(
            "sd,qd->sq",
            branch_grad,
            lax.all_gather(out_weight, "shard", axis=0, tiled=True),
            preferred_element_type=jnp.float32,
        ).astype(jnp.bfloat16)
        attended_group = attended_grad.reshape(seq_dev, KVH, repeat_heads, HD)
        probs_grad = jnp.einsum(
            "skrd,tkd->krst", attended_group, values_all, preferred_element_type=jnp.float32
        )
        inner_sum = jnp.sum(attention_probs * probs_grad, -1, keepdims=True)
        scores_grad = (attention_probs * (probs_grad - inner_sum)).astype(jnp.bfloat16)
        query_rot_grad = (
            jnp.einsum(
                "krst,tkd->skrd", scores_grad, keys_all, preferred_element_type=jnp.float32
            ).reshape(seq_dev, NH, HD)
            * score_scale
        )
        query_grad = (
            unrotate(query_rot_grad, cosine_table, sine_table)
            .astype(jnp.bfloat16)
            .reshape(seq_dev, query_width)
        )
        row_count = lax.axis_size("shard") * seq_dev
        key_part = (
            jnp.einsum(
                "krst,skrd->tkd", scores_grad, query_group, preferred_element_type=jnp.float32
            )
            * score_scale
        )
        value_part = jnp.einsum(
            "krst,skrd->tkd", probs_low, attended_group, preferred_element_type=jnp.float32
        )
        kv_grad = lax.psum_scatter(
            jnp.concatenate(
                [key_part.reshape(row_count, kv_width), value_part.reshape(row_count, kv_width)], 1
            ).astype(jnp.bfloat16),
            "shard",
            scatter_dimension=0,
            tiled=True,
        ).astype(jnp.float32)
        key_grad = (
            unrotate(kv_grad[:, :kv_width].reshape(seq_dev, KVH, HD), cosine_table, sine_table)
            .astype(jnp.bfloat16)
            .reshape(seq_dev, kv_width)
        )
        value_grad = kv_grad[:, kv_width:].astype(jnp.bfloat16)
        first_grad = jnp.einsum(
            "sq,qd->sd", query_grad, query_full, preferred_element_type=jnp.float32
        )
        first_grad = first_grad + jnp.einsum(
            "sq,qd->sd", key_grad, key_full, preferred_element_type=jnp.float32
        )
        first_grad = first_grad + jnp.einsum(
            "sq,qd->sd", value_grad, value_full, preferred_element_type=jnp.float32
        )
        source_part, prenorm_part = norm_backward(source, inverse_first, prenorm_f, first_grad)
        input_rows.append((middle_grad + source_part).astype(jnp.bfloat16))
        prenorm_total = prenorm_total + prenorm_part
        saved = (normed_first, query_grad, key_grad, value_grad, attended, branch_grad)
        weight_term, shard_rows = weight_terms(*saved, shard_count)
        reduced = lax.psum_scatter(
            weight_term(jnp.int32(0), lax.axis_size("shard") * shard_rows).astype(jnp.bfloat16),
            "shard",
            scatter_dimension=0,
            tiled=True,
        ).astype(jnp.float32)
        attn_total = reduced if attn_total is None else attn_total + reduced
    gain_sums = lax.psum((prenorm_total, midnorm_total), ("grp", "shard"))
    gain_share = model_width // shard_count
    prenorm_gradient = lax.dynamic_slice_in_dim(
        gain_sums[0], shard_rank * gain_share, gain_share, 0
    )
    midnorm_gradient = lax.dynamic_slice_in_dim(
        gain_sums[1], shard_rank * gain_share, gain_share, 0
    )
    summed = (
        lax.psum(attn_total.astype(jnp.bfloat16), "grp").astype(jnp.float32),
        lax.psum(gate_total.astype(jnp.bfloat16), "grp").astype(jnp.float32),
        lax.psum(up_total.astype(jnp.bfloat16), "grp").astype(jnp.float32),
        lax.psum(down_total.astype(jnp.bfloat16), "grp").astype(jnp.float32),
    )
    attn_rows = summed[0]
    query_share = query_width // shard_count
    kv_share = kv_width // shard_count
    query_gradient = attn_rows[:query_share]
    key_gradient = attn_rows[query_share : query_share + kv_share]
    value_gradient = attn_rows[query_share + kv_share : query_share + 2 * kv_share]
    out_gradient = attn_rows[query_share + 2 * kv_share :]
    return (
        jnp.stack(mixed_rows),
        jnp.stack(input_rows),
        prenorm_gradient,
        query_gradient,
        key_gradient,
        value_gradient,
        out_gradient,
        midnorm_gradient,
        summed[1],
        summed[2],
        summed[3],
    )


def local_heads(
    tokens,
    lengths,
    prenorm_gain,
    query_weight,
    key_weight,
    value_weight,
    out_weight,
    midnorm_gain,
    gate_weight,
    up_weight,
    down_weight,
    cotangent,
):
    low = jnp.bfloat16
    count = lax.axis_size("shard")
    groups = lax.axis_size("grp")
    shard_rank = lax.axis_index("shard")
    seqs, seq_dev, model_width = tokens.shape
    rows = seqs * seq_dev
    key_pos = jnp.arange(seq_dev * count, dtype=jnp.int32)
    local_pos = shard_rank * seq_dev + jnp.arange(seq_dev, dtype=jnp.int32)
    valid_rows = (local_pos[None, :] < lengths[:, None]).reshape(rows, 1)
    bias = jnp.where(key_pos[None, None, :] < lengths[:, None, None], 0.0, -1.0)
    inverse_freq = theta_base ** (-(jnp.arange(0, HD, 2).astype(jnp.float32) / HD))
    cot_low = jnp.where(valid_rows, cotangent.reshape(rows, model_width), jnp.zeros((), low))
    share = prenorm_gain.shape[0]
    own_gains = jnp.broadcast_to(
        jnp.stack([prenorm_gain, midnorm_gain])[:, None, :], (2, 8, share)
    ).reshape(16, share)
    tokens_low = tokens.reshape(rows, model_width)
    branch, gains, normed_first, cot_all, queries, keys, values, attended, kv_head, cosine, sine = (
        attention(
            tokens_low,
            cot_low,
            own_gains,
            bias,
            inverse_freq[None, :],
            query_weight,
            key_weight,
            value_weight,
            out_weight,
            count,
            groups,
            1,
        )
    )
    gains = gains.astype(jnp.float32)
    prenorm_f = gains[:, 0].reshape(-1)
    midnorm_f = gains[:, 8].reshape(-1)
    source = tokens_low.astype(jnp.float32)
    middle = source + branch
    scaled_second, inverse_second = norm_forward(middle, midnorm_f)
    second_grad, ffn_parts, pair_sums, down_total = ffn(
        scaled_second.astype(low), cot_all, gate_weight, up_weight, down_weight, groups, 2
    )
    middle_part, midnorm_part = norm_backward(middle, inverse_second, midnorm_f, second_grad)
    middle_grad = cot_low.astype(jnp.float32) + middle_part
    gain_parts = jnp.concatenate(
        [
            jnp.zeros((count, 1, share), jnp.float32),
            midnorm_part.reshape(count, 1, share),
            jnp.zeros((count, 6, share), jnp.float32),
        ],
        1,
    )
    first_grad, ffn_part, gain_own, totals, attn_total = attention_grad(
        middle_grad.astype(low),
        bias,
        cosine,
        sine,
        prenorm_f[None, :],
        gain_parts,
        ffn_parts,
        normed_first,
        attended,
        queries,
        keys,
        values,
        query_weight,
        kv_head,
        out_weight,
        pair_sums,
        groups,
        3,
    )
    mixed = jnp.where(valid_rows, middle + ffn_part, 0.0).astype(low)
    inverse_first = lax.rsqrt(jnp.mean(source * source, -1, keepdims=True) + epsilon)
    weighted = first_grad * prenorm_f
    inner_sum = jnp.sum(weighted * source, -1, keepdims=True)
    input_gradient = (
        middle_grad
        + inverse_first * weighted
        - source * inverse_first * inverse_first * inverse_first * inner_sum / model_width
    ).astype(low)
    head = query_weight.shape[0]
    kv_share = key_weight.shape[0]
    f32 = jnp.float32
    return (
        mixed.reshape(tokens.shape),
        input_gradient.reshape(tokens.shape),
        gain_own[0],
        attn_total[head : 2 * head].astype(f32),
        attn_total[2 * head : 2 * head + kv_share].astype(f32),
        attn_total[2 * head + kv_share :].astype(f32),
        attn_total[:head].astype(f32),
        gain_own[1],
        totals[0].astype(f32),
        totals[1].astype(f32),
        down_total.astype(f32),
    )


def solution(mesh):
    planes = mesh.shape["shard"] == NH and mesh.shape["grp"] == 4
    local = local_heads if planes else local_rows
    in_specs = (
        P("grp", "shard", None),
        P("grp"),
        P("shard"),
        P("shard", None),
        P("shard", None),
        P("shard", None),
        P("shard", None),
        P("shard"),
        P("shard", None),
        P("shard", None),
        P("shard", None),
        P("grp", "shard", None),
    )
    out_specs = (
        P("grp", "shard", None),
        P("grp", "shard", None),
        P("shard"),
        P("shard", None),
        P("shard", None),
        P("shard", None),
        P("shard", None),
        P("shard"),
        P("shard", None),
        P("shard", None),
        P("shard", None),
    )
    return jax.shard_map(local, mesh=mesh, in_specs=in_specs, out_specs=out_specs, check_vma=False)
```

```python
import functools
import math

import jax
import jax.numpy as jnp
from jax import lax
from jax.experimental import pallas as pl
from jax.experimental.pallas import tpu as pltpu
from jax.sharding import PartitionSpec as P

NH = 8
KVH = 4
HD = 256
MASKED = -1e30
EPSILON = 1e-06
DEPTH = 2
MESH = pl.DeviceIdType.MESH
F32 = jnp.float32
DMA = pltpu.SemaphoreType.DMA
REST = 16
CHUNKS = 2


def pieces(rows):
    size = -(-(rows - REST) // (16 * CHUNKS)) * 16
    cuts = [min(i * size, rows - REST) for i in range(CHUNKS + 1)] + [rows]
    return [pl.ds(a, b - a) for a, b in zip(cuts, cuts[1:])]


VMEM_LIMIT = 66_000_000


def either(condition, action):
    pl.when(condition)(action)


def total_into(dst, *srcs):
    step = 16

    @pl.loop(0, dst.shape[0] // step)
    def _(i):
        at = pl.ds(pl.multiple_of(i * step, step), step)
        value = srcs[0][at].astype(F32)
        for src in srcs[1:]:
            value = value + src[at].astype(F32)
        dst[at] = value.astype(dst.dtype)


class Place:
    def __init__(self, line):
        self.line = line
        self.me = lax.axis_index("shard")
        self.z = self.me // 2
        self.y = lax.rem(self.me, 2)
        self.cross = self.me + 1 - 2 * self.y
        self.low_end = self.z == 0
        self.high_end = self.z == line - 1
        near = []
        for z in range(line):
            order = [z]
            for k in range(1, line):
                order += [d for d in (z - k, z + k) if 0 <= d < line]
            near.append(order)
        self.tables = near

    def near(self, i):
        out = jnp.int32(0)
        for z in range(self.line):
            row = jnp.int32(self.tables[z][0])
            for k in range(1, self.line):
                row = jnp.where(i == k, self.tables[z][k], row)
            out = jnp.where(self.z == z, row, out)
        return out

    def far(self, i):
        return self.near(self.line - 1 - i)

    def greet(self, groups):
        barrier = pltpu.get_barrier_semaphore()
        count = 2 * self.line
        rank = lax.axis_index("grp")
        for step in range(1, count):
            pl.semaphore_signal(
                barrier,
                inc=1,
                device_id={"shard": lax.rem(self.me + step, count)},
                device_id_type=MESH,
            )
        for step in range(1, groups):
            pl.semaphore_signal(
                barrier,
                inc=1,
                device_id={"grp": lax.rem(rank + step, groups)},
                device_id_type=MESH,
            )
        pl.semaphore_wait(barrier, count + groups - 2)


class Gather:
    UP, DOWN, CROSS = 0, 1, 2

    def __init__(self, place, own, out, local_sem, send_sem, recv_sem):
        self.p, self.own, self.out = place, own, out
        self.local_sem, self.send_sem, self.recv_sem = local_sem, send_sem, recv_sem
        self.pieces = pieces(own.shape[0])
        self.last = len(self.pieces) - 1

    def copy(self, way, origin, part, own=False):
        p = self.p
        peer = (p.me + 2, p.me - 2, p.cross)[way]
        at = self.pieces[part]
        return pltpu.make_async_remote_copy(
            src_ref=self.own.at[at] if own else self.out.at[origin, at],
            dst_ref=self.out.at[origin, at],
            send_sem=self.send_sem.at[way, origin, part],
            recv_sem=self.recv_sem.at[origin, part],
            device_id={"shard": peer},
            device_id_type=MESH,
        )

    def arrived(self, origin, part):
        self.copy(self.CROSS, origin, part).wait_recv()

    def start(self):
        p = self.p
        self.keep = pltpu.make_async_copy(self.own, self.out.at[p.me], self.local_sem)
        self.keep.start()
        for part in (self.last,) + tuple(range(self.last)):
            self.copy(self.CROSS, p.me, part, True).start()
        for part in range(self.last + 1):
            either(p.z < p.line - 1, lambda: self.copy(self.UP, p.me, part, True).start())
            either(p.z > 0, lambda: self.copy(self.DOWN, p.me, part, True).start())
        self.arrived(p.cross, self.last)
        either(p.z < p.line - 1, lambda: self.copy(self.UP, p.cross, self.last).start())
        either(p.z > 0, lambda: self.copy(self.DOWN, p.cross, self.last).start())
        self.keep.wait()

    def hop(self, k):
        p = self.p
        below, above = p.me - 2 * k, p.me + 2 * k
        has_below, has_above = p.z - k >= 0, p.z + k < p.line

        def first(origin, part, way, more):
            self.arrived(origin, part)
            self.copy(self.CROSS, origin, part).start()
            either(more, lambda: self.copy(way, origin, part).start())

        def last(origin, other, way, more):
            for block in (origin, other):
                self.arrived(block, self.last)
                either(more, lambda: self.copy(way, block, self.last).start())

        for part in range(self.last):
            either(has_below, lambda: first(below, part, self.UP, p.z < p.line - 1))
            either(has_above, lambda: first(above, part, self.DOWN, p.z > 0))
        either(has_below, lambda: last(below, p.cross - 2 * k, self.UP, p.z < p.line - 1))
        either(has_above, lambda: last(above, p.cross + 2 * k, self.DOWN, p.z > 0))

    def whole(self, position):
        for part in range(self.last):
            self.arrived(2 * position + 1 - self.p.y, part)

    def drain(self):
        p = self.p

        @pl.loop(0, p.line)
        def _(d):
            mine, other = 2 * d + p.y, 2 * d + 1 - p.y
            for part in range(self.last):
                self.copy(self.CROSS, mine, part).wait_send()

            @pl.when(d == p.z)
            def _():
                self.copy(self.CROSS, mine, self.last).wait_send()

            def line_sent(way):
                for part in range(self.last + 1):
                    self.copy(way, mine, part).wait_send()
                self.copy(way, other, self.last).wait_send()

            either((d <= p.z) & (p.z < p.line - 1), lambda: line_sent(self.UP))
            either((d >= p.z) & (p.z > 0), lambda: line_sent(self.DOWN))


class Reduce:
    BUP, BDN, BX = 0, 2, 4
    UP, DOWN, CROSS = 5, 5 + CHUNKS, 5 + 2 * CHUNKS
    WAYS = 5 + 3 * CHUNKS
    N_SCRATCH = 9

    @staticmethod
    def scratch(line, rows, width, dtype):
        v = pltpu.VMEM
        return (
            [v((line, rows - REST, width), dtype)] * 3
            + [v((line, 2, REST, width), dtype)] * 2
            + [v((REST, width), dtype)] * 2
            + [DMA((Reduce.WAYS, line)), DMA((Reduce.WAYS, line))]
        )

    def __init__(self, place, parts, out, scratch):
        self.p, self.parts, self.out = place, parts, out
        self.cross_in, self.up_in, self.down_in, self.bup_in, self.bdn_in = scratch[:5]
        self.bx_out, self.bx_in, self.send_sem, self.recv_sem = scratch[5:]
        self.pieces = pieces(parts.shape[1])
        self.b = self.pieces[-1]

    def desc(self, way, slot, src, dst, peer):
        return pltpu.make_async_remote_copy(
            src_ref=src,
            dst_ref=dst,
            send_sem=self.send_sem.at[way, slot],
            recv_sem=self.recv_sem.at[way, slot],
            device_id={"shard": peer},
            device_id_type=MESH,
        )

    def cross_copy(self, d, c):
        p, at = self.p, self.pieces[c]
        return self.desc(
            self.CROSS + c,
            d,
            self.parts.at[2 * d + 1 - p.y, at],
            self.cross_in.at[d, at],
            p.cross,
        )

    def line_copy(self, up, d, c):
        p, at = self.p, self.pieces[c]
        came = self.up_in if up else self.down_in
        return self.desc(
            (self.UP if up else self.DOWN) + c,
            d,
            self.cross_in.at[d, at],
            came.at[d, at],
            p.me + 2 if up else p.me - 2,
        )

    def b_copy(self, up, d, o, src=None):
        p = self.p
        held = self.bup_in if up else self.bdn_in
        return self.desc(
            (self.BUP if up else self.BDN) + o,
            d,
            held.at[d, o] if src is None else src,
            held.at[d, o],
            p.me + 2 if up else p.me - 2,
        )

    def bx_copy(self):
        return self.desc(self.BX, 0, self.bx_out, self.bx_in, self.p.cross)

    def column(self, o):
        return self.p.y if o == 0 else 1 - self.p.y

    def send_across(self, i):
        for c in range(CHUNKS):
            self.cross_copy(self.p.far(i), c).start()

    def b_hop(self, i):
        p = self.p
        d = p.far(i)

        def go(up):
            first = p.low_end if up else p.high_end
            held = self.bup_in if up else self.bdn_in
            for o in (1, 0):
                mine = self.parts.at[2 * d + self.column(o), self.b]
                either(first, lambda: self.b_copy(up, d, o, mine).start())

                @pl.when(jnp.logical_not(first))
                def _():
                    self.b_copy(up, d, o).wait_recv()
                    total_into(held.at[d, o], mine, held.at[d, o])
                    self.b_copy(up, d, o).start()

        either(d > p.z, lambda: go(True))
        either(d < p.z, lambda: go(False))

    def hop(self, i):
        p = self.p
        d = p.far(i)
        for c in range(CHUNKS):
            self.cross_copy(d, c).wait_recv()
            at = self.pieces[c]
            mine = self.parts.at[2 * d + p.y, at]
            held = self.cross_in.at[d, at]

            def go(up):
                first = p.low_end if up else p.high_end
                came = self.up_in if up else self.down_in
                either(first, lambda: total_into(held, mine, held))

                @pl.when(jnp.logical_not(first))
                def _():
                    self.line_copy(up, d, c).wait_recv()
                    total_into(held, mine, held, came.at[d, at])

                self.line_copy(up, d, c).start()

            either(d > p.z, lambda: go(True))
            either(d < p.z, lambda: go(False))

    def close(self, dst, mine, ups, downs):
        p = self.p
        either(p.low_end, lambda: total_into(dst, *mine, downs))
        either(p.high_end, lambda: total_into(dst, *mine, ups))
        either(
            jnp.logical_not(p.low_end | p.high_end), lambda: total_into(dst, *mine, ups, downs)
        )

    def finish(self):
        p = self.p
        for o in (1, 0):
            either(jnp.logical_not(p.low_end), lambda: self.b_copy(True, p.z, o).wait_recv())
            either(jnp.logical_not(p.high_end), lambda: self.b_copy(False, p.z, o).wait_recv())
            if o:
                mine = self.parts.at[2 * p.z + self.column(o), self.b]
                self.close(self.bx_out, (mine,), self.bup_in.at[p.z, o], self.bdn_in.at[p.z, o])
                self.bx_copy().start()
        self.bx_copy().wait_recv()
        self.close(
            self.out.at[self.b],
            (self.parts.at[p.me, self.b], self.bx_in),
            self.bup_in.at[p.z, 0],
            self.bdn_in.at[p.z, 0],
        )
        for c in range(CHUNKS):
            self.cross_copy(p.z, c).wait_recv()
            either(jnp.logical_not(p.low_end), lambda: self.line_copy(True, p.z, c).wait_recv())
            either(jnp.logical_not(p.high_end), lambda: self.line_copy(False, p.z, c).wait_recv())
            at = self.pieces[c]
            self.close(
                self.out.at[at],
                (self.parts.at[p.me, at], self.cross_in.at[p.z, at]),
                self.up_in.at[p.z, at],
                self.down_in.at[p.z, at],
            )

    def drain(self):
        p = self.p
        self.bx_copy().wait_send()

        @pl.loop(0, p.line)
        def _(d):
            def line_sent(up):
                for c in range(CHUNKS):
                    self.line_copy(up, d, c).wait_send()
                self.b_copy(up, d, 0).wait_send()
                self.b_copy(up, d, 1).wait_send()

            for c in range(CHUNKS):
                self.cross_copy(d, c).wait_send()
            either(d > p.z, lambda: line_sent(True))
            either(d < p.z, lambda: line_sent(False))


def dot(a, b):
    return jnp.dot(a, b, preferred_element_type=F32)


def dot_t(a, b):
    return lax.dot_general(a, b, (((1,), (1,)), ((), ())), preferred_element_type=F32)


def t_dot(a, b):
    return lax.dot_general(a, b, (((0,), (0,)), ((), ())), preferred_element_type=F32)


def to_peer(axis, peer, src, dst, send_sem, recv_sem):
    return pltpu.make_async_remote_copy(
        src_ref=src,
        dst_ref=dst,
        send_sem=send_sem,
        recv_sem=recv_sem,
        device_id={axis: peer},
        device_id_type=MESH,
    )


def turn_by(v, cosine, sine):
    half = v.shape[-1] // 2
    a, b = v[:, :half], v[:, half:]
    return jnp.concatenate([a * cosine - b * sine, b * cosine + a * sine], -1)


def turn_back(v, cosine, sine):
    return turn_by(v, cosine, -sine)


def probabilities(query, keys, rows_from, limit):
    scores = dot_t(query, keys) * (1.0 / math.sqrt(HD))
    row = lax.broadcasted_iota(jnp.int32, scores.shape, 0) + rows_from
    col = lax.broadcasted_iota(jnp.int32, scores.shape, 1)
    scores = jnp.where((col <= row) & (col < limit), scores, MASKED)
    weight = jnp.exp(scores - jnp.max(scores, -1, keepdims=True))
    return weight / jnp.sum(weight, -1, keepdims=True)


def row_valid(place, lengths, rows):
    slots = rows // lengths.shape[0]
    row = lax.broadcasted_iota(jnp.int32, (rows, 1), 0)
    limit = jnp.full((rows, 1), lengths[0], jnp.int32)
    for n in range(1, lengths.shape[0]):
        limit = jnp.where(row >= n * slots, lengths[n], limit)
    return place.me * slots + lax.rem(row, slots) < limit


def gain_row(shares, which):
    return jnp.concatenate([shares[b, which : which + 1] for b in range(shares.shape[0])], 1)


def inverse_rms(x):
    return lax.rsqrt(jnp.mean(x * x, -1, keepdims=True) + EPSILON)


def norm_grad(x, inverse, gain, grad):
    weighted = grad * gain
    inner = jnp.sum(weighted * x, -1, keepdims=True)
    return inverse * weighted - x * inverse * inverse * inverse * inner / x.shape[-1]


def start_all(copies):
    for c in copies:
        c.start()


def wait_all(copies):
    for c in copies:
        c.wait()


def scalars():
    return pl.BlockSpec(memory_space=pltpu.SMEM)


def hbm():
    return pl.BlockSpec(memory_space=pl.ANY)


def vm():
    return pl.BlockSpec(memory_space=pltpu.VMEM)


def params(ident):
    return pltpu.CompilerParams(
        collective_id=ident, has_side_effects=True, vmem_limit_bytes=VMEM_LIMIT
    )


def gather_sems(count):
    return [DMA, DMA((3, count, CHUNKS + 1)), DMA((count, CHUNKS + 1))]


def attention_kernel(
    line, groups, seqs,
    lengths, own, cot_raw, pre_gain, mid_gain, freq, wq_hbm, wk_hbm, wv_hbm, wo_hbm,
    branch, small_out, normed_hbm, cot_hbm, q_hbm, k_hbm, v_hbm, attended_hbm, wkv_hbm, cos_hbm, sin_hbm,
    small, cot_own, rows_all, normed, cot_all, q, k, v, attended, wq, wkv, wo, cosine, sine, parts,
    *scratch,
):
    p = Place(line)
    count = 2 * line
    rank = lax.axis_index("grp")
    g1, g2 = scratch[:3], scratch[3:6]
    (load_sem, small_send, small_recv, wy_send, wg_send, w_recv, save_sem) = scratch[6:13]
    r_scratch = scratch[13:]
    half = wk_hbm.shape[0]
    piece = half // 2
    at_own = pl.ds(pl.multiple_of(p.y * half, half), half)
    loads = [
        pltpu.make_async_copy(src, dst, load_sem.at[i])
        for i, (src, dst) in enumerate(
            (
                (wk_hbm, wkv.at[0, at_own]),
                (wv_hbm, wkv.at[1, at_own]),
                (wq_hbm, wq),
                (wo_hbm, wo),
            )
        )
    ]
    start_all(loads)
    p.greet(groups)

    small[...] = jnp.zeros_like(small)
    small[0:1] = pre_gain[...].astype(F32)
    small[1:2] = mid_gain[...].astype(F32)

    def small_copy(step, peer, origin):
        return to_peer(
            "shard", peer, small, small_out.at[origin], small_send.at[step], small_recv.at[step]
        )

    for step in range(1, count):
        small_copy(step, lax.rem(p.me + step, count), p.me).start()
    gather = Gather(p, own, rows_all, *g1)
    gather.start()
    small_out[p.me] = small[...]

    def rows_of(quarter, column):
        return wkv.at[
            quarter // 2,
            pl.ds(pl.multiple_of(column * half + lax.rem(quarter, 2) * piece, piece), piece),
        ]

    def across():
        ref = rows_of(rank, p.y)
        return to_peer("shard", p.cross, ref, ref, wy_send, w_recv.at[rank])

    def share(step):
        ref = rows_of(rank, 1 - p.y)
        return to_peer(
            "grp", lax.rem(rank + step, groups), ref, ref, wg_send.at[step], w_recv.at[rank]
        )

    wait_all(loads)
    across().start()
    pos = lax.broadcasted_iota(jnp.int32, cosine.shape, 0).astype(F32)
    angle = pos * freq[...]
    cosine[...] = jnp.cos(angle)
    sine[...] = jnp.sin(angle)
    cot = cot_raw[...]
    cot_own[...] = jnp.where(row_valid(p, lengths, cot.shape[0]), cot, jnp.zeros_like(cot))
    for step in range(1, count):
        small_copy(step, p.me, lax.rem(p.me + count - step, count)).wait_recv()
    gain = gain_row(small_out, 0)
    across().wait_recv()
    for step in range(1, groups):
        share(step).start()
    rows = own.shape[0]
    pair = 2 * rows
    slots = rows // seqs
    low = own.dtype
    for step in range(1, groups):
        quarter = lax.rem(rank + step, groups)
        ref = rows_of(quarter, 1 - p.y)
        to_peer("grp", rank, ref, ref, wg_send.at[step], w_recv.at[quarter]).wait_recv()

    @pl.loop(0, line)
    def _(i):
        gather.hop(i + 1)
        d = p.near(i)
        gather.whole(d)
        x = rows_all[pl.ds(2 * d, 2)].reshape(pair, -1).astype(F32)
        n = (x * inverse_rms(x) * gain).astype(low)
        normed[pl.ds(2 * d, 2)] = n.reshape(2, rows, -1)
        at = pl.ds(pl.multiple_of(d * 2 * slots, 2 * slots), 2 * slots)
        c, s = cosine[at], sine[at]

        def by_rows(t):
            return jnp.concatenate([t[:slots]] * seqs + [t[slots:]] * seqs, 0)

        c, s = by_rows(c), by_rows(s)

        def put(target, value):
            for block in range(2):
                for m in range(seqs):
                    to = pl.ds(
                        pl.multiple_of(d * 2 * slots + block * slots, slots), slots
                    )
                    target[m, to] = value[block * rows + m * slots : block * rows + (m + 1) * slots]

        put(q, turn_by(dot_t(n, wq[...]), c, s).astype(low))
        put(k, turn_by(dot_t(n, wkv[0]), c, s).astype(low))
        put(v, dot_t(n, wkv[1]).astype(low))

    saves = [
        pltpu.make_async_copy(src, dst, save_sem.at[i])
        for i, (src, dst) in enumerate(
            (
                (normed, normed_hbm),
                (q, q_hbm),
                (k, k_hbm),
                (v, v_hbm),
                (wkv, wkv_hbm),
                (cosine, cos_hbm),
                (sine, sin_hbm),
            )
        )
    ]
    start_all(saves)
    cots = Gather(p, cot_own, cot_all, *g2)
    cots.start()
    total_slots = q.shape[1]
    tile = min(256, total_slots)

    @pl.loop(0, seqs)
    def _(n):
        for t in range(total_slots // tile):
            span = (t + 1) * tile
            at = pl.ds(t * tile, tile)
            probs = probabilities(q[n, at], k[n, pl.ds(0, span)], t * tile, lengths[n])
            out = dot(probs.astype(low), v[n, pl.ds(0, span)]).astype(low)
            for c in range(tile // slots):
                b = (t * tile) // slots + c
                attended[pl.ds(pl.multiple_of(b * rows + n * slots, slots), slots)] = out[
                    c * slots : (c + 1) * slots
                ]
        cots.hop(n + 1)

    for h in range(seqs + 1, line):
        cots.hop(h)

    @pl.loop(0, line)
    def _(d):
        at = pl.ds(pl.multiple_of(d * pair, pair), pair)
        parts[pl.ds(2 * d, 2)] = dot(attended[at], wo[...]).astype(low).reshape(2, rows, -1)

    reduce = Reduce(p, parts, branch, r_scratch)
    saves2 = [pltpu.make_async_copy(attended, attended_hbm, save_sem.at[7])]
    start_all(saves2)
    for d in range(line):
        cots.whole(d)
    for i in range(DEPTH):
        reduce.send_across(i)
    saves3 = [pltpu.make_async_copy(cot_all, cot_hbm, save_sem.at[8])]
    start_all(saves3)
    for i in range(line - 1):
        reduce.b_hop(i)
    for i in range(line - 1):
        reduce.hop(i)
        if i + DEPTH < line:
            reduce.send_across(i + DEPTH)
    reduce.finish()
    reduce.drain()
    gather.drain()
    cots.drain()
    wait_all(saves + saves2 + saves3)
    across().wait_send()
    for step in range(1, groups):
        share(step).wait_send()
    for step in range(1, count):
        small_copy(step, lax.rem(p.me + step, count), p.me).wait_send()


def attention(lengths, own, cot, pre_gain, mid_gain, freq, wq, wk, wv, wo, count, groups, ident):
    rows, width = own.shape
    seqs = lengths.shape[0]
    total_slots = count * rows // seqs
    small = (8, pre_gain.shape[1])
    line = count // 2
    low = own.dtype
    v = pltpu.VMEM
    shape = jax.ShapeDtypeStruct
    hd = wq.shape[0]
    big = (count, rows, width)
    head = (seqs, total_slots, hd)
    table = (total_slots, hd // 2)
    flat = (count * rows, hd)
    return pl.pallas_call(
        functools.partial(attention_kernel, line, groups, seqs),
        out_shape=(
            shape((rows, width), F32),
            shape((count,) + small, F32),
            shape(big, low),
            shape(big, low),
            shape(head, low),
            shape(head, low),
            shape(head, low),
            shape(flat, low),
            shape((2, hd, width), low),
            shape(table, F32),
            shape(table, F32),
        ),
        in_specs=[scalars()] + [vm()] * 5 + [hbm()] * 4,
        out_specs=(vm(), vm()) + (hbm(),) * 9,
        scratch_shapes=[
            v(small, F32), v((rows, width), low), v(big, low), v(big, low), v(big, low), v(head, low), v(head, low), v(head, low), v(flat, low),
            v((hd, width), low), v((2, hd, width), low), v((hd, width), low), v(table, F32), v(table, F32), v(big, low),
        ]
        + gather_sems(count) * 2
        + [DMA((4,)), DMA((count,)), DMA((count,)), DMA, DMA((groups,)), DMA((groups,)), DMA((9,))]
        + Reduce.scratch(line, rows, width, low),
        compiler_params=params(ident),
        name="attention",
    )(lengths, own, cot, pre_gain, mid_gain, freq, wq, wk, wv, wo)


def ffn_kernel(
    line, groups,
    tokens, branch, gains, cot_hbm, gate_hbm, up_hbm, down_hbm,
    second, ffn_hbm, pair_hbm, chip_in,
    own, normed, cot, gate_w, up_w, down_w, hidden, gate_g, up_g, parts, stage, theirs,
    *scratch,
):
    p = Place(line)
    rank = lax.axis_index("grp")
    core = lax.rem(rank, 2)
    partner = rank + 1 - 2 * core
    opposite = lax.rem(rank + 2, groups)
    (load_sem, out_sem, stage_send, stage_recv, chip_send, chip_recv) = scratch[3:9]
    loads = [
        pltpu.make_async_copy(src, dst, load_sem.at[i])
        for i, (src, dst) in enumerate(
            ((gate_hbm, gate_w), (up_hbm, up_w), (cot_hbm, cot), (down_hbm, down_w))
        )
    ]
    start_all(loads)
    middle = tokens[...].astype(F32) + branch[...]
    own[...] = (middle * inverse_rms(middle) * gain_row(gains, 1)).astype(own.dtype)
    p.greet(groups)
    gather = Gather(p, own, normed, *scratch[:3])
    gather.start()
    wait_all(loads)
    rows = own.shape[0]
    pair = 2 * rows
    low = own.dtype

    @pl.loop(0, line)
    def _(i):
        gather.hop(i + 1)
        d = p.near(i)
        gather.whole(d)
        x = normed[pl.ds(2 * d, 2)].reshape(pair, -1)
        g = dot_t(x, gate_w[...])
        u = dot_t(x, up_w[...])
        dh = dot_t(cot[pl.ds(2 * d, 2)].reshape(pair, -1), down_w[...])
        s = 1.0 / (1.0 + jnp.exp(-g))
        silu = g * s
        at = pl.ds(pl.multiple_of(d * pair, pair), pair)
        hidden[at] = (silu * u).astype(low)
        up_g[at] = (dh * silu).astype(low)
        gate_g[at] = (dh * u * s * (1.0 + g * (1.0 - s))).astype(low)
        part = dot(gate_g[at], gate_w[...]) + dot(up_g[at], up_w[...])
        parts[pl.ds(2 * d, 2)] = part.astype(low).reshape(2, rows, -1)

    reduce = Reduce(p, parts, second, scratch[9:])
    for i in range(DEPTH):
        reduce.send_across(i)
    for i in range(line - 1):
        reduce.b_hop(i)

    units = hidden.shape[1]
    quarter = units // 4
    half = units // 2
    mine = (up_w.at[pl.ds(0, half)], gate_w.at[pl.ds(0, half)], gate_w.at[pl.ds(half, half)])

    def to_partner(which, j):
        return to_peer(
            "grp",
            partner,
            stage.at[j],
            theirs.at[which, pl.ds(j * quarter, quarter)],
            stage_send.at[j],
            stage_recv.at[which, j],
        )

    def gradient(which, left, right):
        def block(q):
            cols = pl.ds(pl.multiple_of(q * quarter, quarter), quarter)
            return t_dot(left[:, cols], right[...].reshape(left.shape[0], -1)).astype(low)

        @pl.loop(0, 2)
        def _(j):
            if which:
                to_partner(which - 1, j).wait_send()
            stage[j] = block(2 * (1 - core) + j)
            to_partner(which, j).start()

        @pl.loop(0, 2)
        def _(j):
            at = pl.ds(pl.multiple_of(j * quarter, quarter), quarter)
            mine[which][at] = block(2 * core + j)

    def add_theirs(which):
        for j in range(2):
            to_partner(which, j).wait_recv()
        total_into(mine[which], mine[which], theirs.at[which])

    def chip_copy():
        return to_peer(
            "grp", opposite, mine[0].at[pl.ds(0, quarter)], chip_in, chip_send, chip_recv
        )

    def save_pair(which):
        return pltpu.make_async_copy(mine[which], pair_hbm.at[which], out_sem.at[which])

    gradient(0, hidden, cot)
    reduce.hop(0)
    reduce.send_across(DEPTH)
    add_theirs(0)
    chip_copy().start()
    save_pair(0).start()
    gradient(1, gate_g, normed)
    reduce.hop(1)
    reduce.send_across(DEPTH + 1)
    add_theirs(1)
    save_pair(1).start()
    gradient(2, up_g, normed)
    reduce.hop(2)
    gather.drain()

    @pl.loop(0, line)
    def _(d):
        at = pl.ds(pl.multiple_of(d * pair, pair), pair)
        normed[pl.ds(2 * d, 2)] = dot(hidden[at], down_w[...]).astype(low).reshape(2, rows, -1)

    ffn_save = pltpu.make_async_copy(normed, ffn_hbm, out_sem.at[3])
    ffn_save.start()
    add_theirs(2)
    save_pair(2).start()
    reduce.finish()
    for j in range(2):
        to_partner(2, j).wait_send()

    reduce.drain()
    chip_copy().wait()
    ffn_save.wait()
    for which in range(3):
        save_pair(which).wait()


def ffn(tokens, branch, gains, cot, gate_w, up_w, down_w, groups, ident):
    rows, width = tokens.shape
    count = cot.shape[0]
    line = count // 2
    units = gate_w.shape[0]
    low = tokens.dtype
    v = pltpu.VMEM
    tall = count * rows
    shape = jax.ShapeDtypeStruct
    big = (count, rows, width)
    half = (units // 2, width)
    return pl.pallas_call(
        functools.partial(ffn_kernel, line, groups),
        out_shape=(
            shape((rows, width), F32),
            shape(big, low),
            shape((3,) + half, low),
            shape((units // 4, width), low),
        ),
        in_specs=[vm()] * 3 + [hbm()] * 4,
        out_specs=(vm(), hbm(), hbm(), hbm()),
        scratch_shapes=[v((rows, width), low)]
        + [v(big, low)] * 2
        + [v((units, width), low)] * 3
        + [v((tall, units), low)] * 3
        + [v(big, low), v((2, units // 4, width), low), v((3,) + half, low)]
        + gather_sems(count)
        + [DMA((4,)), DMA((4,)), DMA((2,)), DMA((3, 2)), DMA, DMA]
        + Reduce.scratch(line, rows, width, low),
        compiler_params=params(ident),
        name="ffn",
    )(tokens, branch, gains, cot, gate_w, up_w, down_w)


def attention_grad_kernel(
    line, groups, seqs,
    lengths, tokens, branch, cot, second, gains, cosine, sine,
    ffn_hbm, normed_hbm, attended_hbm, q_hbm, k_hbm, v_hbm, wq_hbm, wkv_hbm, wo_hbm, sums_hbm, early_hbm,
    mixed, input_grad, gain_out, total_hbm, attn_hbm,
    own, middle_grad, first, ffn_own, dbranch, normed, attended, q, k, v, wq, wkv, wo, da, dk_acc, dv_acc, dq_rows, dk_rows, dv_rows,
    halves, half_in, ffn_parts, sums, sums_in, stage, mine, theirs, mine_in, gain_held, gain_in, gain_sum, gain_all,
    *scratch,
):
    p = Place(line)
    count = 2 * line
    rank = lax.axis_index("grp")
    core = lax.rem(rank, 2)
    partner = rank + 1 - 2 * core
    opposite = lax.rem(rank + 2, groups)
    (
        load_sem, chip_send, chip_recv, half_send, half_recv, stage_send, stage_recv,
        back_send, back_recv, keep_sem, ga_send, ga_recv, gb_send, gb_recv,
    ) = scratch[3:17]
    n = Reduce.N_SCRATCH
    loads = [
        pltpu.make_async_copy(src, dst, load_sem.at[i])
        for i, (src, dst) in enumerate(
            (
                (wo_hbm, wo),
                (ffn_hbm, ffn_parts),
                (attended_hbm, attended),
                (q_hbm, q),
                (k_hbm, k),
                (v_hbm, v),
                (wq_hbm, wq),
                (wkv_hbm, wkv),
                (normed_hbm, normed),
                (early_hbm, sums_in.at[0]),
            )
        )
    ]
    start_all(loads)

    def load_sum(i):
        return pltpu.make_async_copy(sums_hbm.at[i], sums.at[i % 2], load_sem.at[10 + i % 2])

    load_sum(0).start()
    load_sum(1).start()
    middle = tokens[...].astype(F32) + branch[...]
    inverse = inverse_rms(middle)
    grad = cot[...].astype(F32)
    grad = jnp.where(row_valid(p, lengths, grad.shape[0]), grad, jnp.zeros_like(grad))
    grad = grad + norm_grad(middle, inverse, gain_row(gains, 1), second[...])
    middle_grad[...] = grad
    own[...] = grad.astype(own.dtype)
    mid_total = jnp.sum(second[...] * middle * inverse, 0, keepdims=True)
    share = gain_held.shape[2]
    for b in range(count):
        gain_held[b] = jnp.zeros(gain_held.shape[1:], F32)
        gain_held[b, 1:2] = mid_total[:, b * share : (b + 1) * share]
    p.greet(groups)
    gather = Gather(p, own, dbranch, *scratch[:3])
    n_sums = sums_hbm.shape[0]
    part_rows = sums.shape[1]

    def chip_copy(i):
        return to_peer(
            "grp", opposite, sums_hbm.at[i], sums_in.at[i], chip_send.at[i], chip_recv.at[i]
        )

    for i in range(1, n_sums):
        chip_copy(i).start()
    gather.start()
    wait_all(loads)
    rows = own.shape[0]
    pair = 2 * rows
    slots = rows // seqs
    low = own.dtype
    scale = 1.0 / math.sqrt(HD)

    @pl.loop(0, line)
    def _(i):
        gather.hop(i + 1)
        d = p.near(i)
        gather.whole(d)
        grad = dot_t(dbranch[pl.ds(2 * d, 2)].reshape(pair, -1), wo[...]).astype(low)
        for block in range(2):
            for m in range(seqs):
                at = pl.ds(pl.multiple_of(d * 2 * slots + block * slots, slots), slots)
                da[m, at] = grad[block * rows + m * slots : block * rows + (m + 1) * slots]

    ffn_sum = Reduce(p, ffn_parts, ffn_own, scratch[17 : 17 + n])
    for i in range(DEPTH):
        ffn_sum.send_across(i)
    for i in range(line - 1):
        ffn_sum.b_hop(i)

    chunk = stage.shape[1]

    def to_partner(b):
        return to_peer(
            "grp",
            partner,
            stage.at[b % 3],
            theirs.at[pl.ds((b % 3) * chunk, chunk)],
            stage_send.at[b % 3],
            stage_recv.at[b % 3],
        )

    def gradient(b, left, right):
        value = t_dot(left, right[...].reshape(left.shape[0], -1)).astype(low)
        keep = core == b // 3

        @pl.when(keep)
        def _():
            mine[pl.ds((b % 3) * chunk, chunk)] = value

        @pl.when(jnp.logical_not(keep))
        def _():
            stage[b % 3] = value
            to_partner(b).start()

    total_slots = q.shape[1]
    tile = min(256, total_slots)

    def backward(m):
        dk_acc[...] = jnp.zeros_like(dk_acc)
        dv_acc[...] = jnp.zeros_like(dv_acc)

        def to_rows(target, value, start, size):
            for c in range(size // slots):
                b = start // slots + c
                target[pl.ds(pl.multiple_of(b * rows + m * slots, slots), slots)] = value[
                    c * slots : (c + 1) * slots
                ]

        for t in range(total_slots // tile):
            span = (t + 1) * tile
            at = pl.ds(t * tile, tile)
            query, grad = q[m, at], da[m, at]
            keys, values = k[m, pl.ds(0, span)], v[m, pl.ds(0, span)]
            probs = probabilities(query, keys, t * tile, lengths[m])
            dprobs = dot_t(grad, values)
            inner = jnp.sum(probs * dprobs, -1, keepdims=True)
            dscores = (probs * (dprobs - inner)).astype(low)
            dq = turn_back(dot(dscores, keys) * scale, cosine[at], sine[at])
            to_rows(dq_rows, dq.astype(low), t * tile, tile)
            dk_acc[pl.ds(0, span)] += t_dot(dscores, query)
            dv_acc[pl.ds(0, span)] += t_dot(probs.astype(low), grad)
        dk = turn_back(dk_acc[...] * scale, cosine[...], sine[...])
        to_rows(dk_rows, dk.astype(low), 0, total_slots)
        to_rows(dv_rows, dv_acc[...].astype(low), 0, total_slots)

    half = HD // 2

    def swap():
        return to_peer("shard", p.cross, halves.at[1 - p.y], half_in, half_send, half_recv)

    gradient(0, attended[:, :chunk], dbranch)
    gradient(1, attended[:, chunk:], dbranch)

    @pl.loop(0, seqs)
    def _(m):
        backward(m)
        ffn_sum.hop(m)
        ffn_sum.send_across(m + DEPTH)

    for h in range(2):
        halves[h, 0] = dk_rows[:, h * half : (h + 1) * half]
        halves[h, 1] = dv_rows[:, h * half : (h + 1) * half]
    swap().start()
    gather.drain()
    parts = dbranch
    gradient(2, dq_rows[:, :chunk], normed)
    gradient(3, dq_rows[:, chunk:], normed)

    @pl.loop(0, line)
    def _(d):
        at = pl.ds(pl.multiple_of(d * pair, pair), pair)
        part = dot(dq_rows[at], wq[...]) + dot(dk_rows[at], wkv[0]) + dot(dv_rows[at], wkv[1])
        parts[pl.ds(2 * d, 2)] = part.astype(low).reshape(2, rows, -1)

    for i in range(seqs, line - 1):
        ffn_sum.hop(i)
    reduce = Reduce(p, parts, first, scratch[17 + n :])
    swap().wait_recv()

    def summed(which):
        return (halves[p.y, which].astype(F32) + half_in[which].astype(F32)).astype(low)

    gradient(4, summed(0), normed)
    gradient(5, summed(1), normed)

    def attn_chip():
        return to_peer(
            "grp", opposite, mine, mine_in, chip_send.at[n_sums], chip_recv.at[n_sums]
        )

    for b in range(3):
        to_partner(b).wait_recv()
    total_into(mine, mine, theirs)
    attn_chip().start()
    ffn_sum.finish()
    for i in range(DEPTH):
        reduce.send_across(i)
    for i in range(line - 1):
        reduce.b_hop(i)
    valid = row_valid(p, lengths, rows)
    result = tokens[...].astype(F32) + branch[...] + ffn_own[...]
    mixed[...] = jnp.where(valid, result, jnp.zeros_like(result)).astype(low)

    def back(i):
        if i < n_sums:
            whole, size, out = sums_in.at[i], part_rows, total_hbm.at[i // 2]
            start = core * 2 * size + (i % 2) * size
        else:
            whole, size, out = mine, 3 * chunk, attn_hbm
            start = core * size
        at = pl.ds(pl.multiple_of(start, size), size)
        return (
            pltpu.make_async_copy(whole, out.at[at], keep_sem.at[i]),
            to_peer("grp", partner, whole, out.at[at], back_send.at[i], back_recv.at[i]),
        )

    def sum_up(i):
        if i:
            chip_copy(i).wait()
        load_sum(i).wait()
        total_into(sums_in.at[i], sums.at[i % 2], sums_in.at[i])
        if i + 2 < n_sums:
            load_sum(i + 2).start()
        start_all(back(i))

    def gain_copy(step, peer, origin):
        return to_peer(
            "shard", peer, gain_held.at[peer], gain_in.at[origin], ga_send.at[step], ga_recv.at[step]
        )

    def gain_group(step, peer, origin):
        return to_peer(
            "grp", peer, gain_sum, gain_all.at[origin], gb_send.at[step], gb_recv.at[step]
        )

    def gain_first():
        def body(i, total):
            at = pl.ds(pl.multiple_of(i * 16, 16), 16)
            for b in range(count):
                total = total + parts[b, at].astype(F32) * normed[b, at].astype(F32)
            return total

        total = lax.fori_loop(0, rows // 16, body, jnp.zeros((16, parts.shape[2]), F32))
        total = jnp.sum(total, 0, keepdims=True) / gain_row(gains, 0)
        for b in range(count):
            gain_held[b, 0:1] = total[:, b * share : (b + 1) * share]
        for step in range(1, count):
            gain_copy(step, lax.rem(p.me + step, count), p.me).start()

    def gain_second():
        for step in range(1, count):
            gain_copy(step, p.me, lax.rem(p.me + count - step, count)).wait_recv()
        gain_in[p.me] = gain_held[p.me]
        total = gain_in[0]
        for b in range(1, count):
            total = total + gain_in[b]
        gain_sum[...] = total
        gain_all[rank] = total
        for step in range(1, groups):
            gain_group(step, lax.rem(rank + step, groups), rank).start()

    reduce.hop(0)
    reduce.send_across(DEPTH)
    gain_first()
    sum_up(0)
    sum_up(1)
    reduce.hop(1)
    reduce.send_across(DEPTH + 1)
    gain_second()
    sum_up(2)
    sum_up(3)
    reduce.hop(2)
    sum_up(4)
    reduce.finish()
    for step in range(1, groups):
        gain_group(step, rank, lax.rem(rank + groups - step, groups)).wait_recv()
    total = gain_all[0]
    for b in range(1, groups):
        total = total + gain_all[b]
    gain_out[...] = total
    source = tokens[...].astype(F32)
    inner = norm_grad(source, inverse_rms(source), gain_row(gains, 0), first[...])
    input_grad[...] = (middle_grad[...] + inner).astype(low)
    sum_up(5)
    attn_chip().wait()
    total_into(mine, mine, mine_in)
    start_all(back(n_sums))
    reduce.drain()
    ffn_sum.drain()
    swap().wait_send()
    for b in range(3):
        to_partner(b).wait_send()
    for step in range(1, count):
        gain_copy(step, lax.rem(p.me + step, count), p.me).wait_send()
    for step in range(1, groups):
        gain_group(step, lax.rem(rank + step, groups), rank).wait_send()
    for i in range(n_sums + 1):
        wait_all(back(i))


def attention_grad(
    lengths, tokens, branch, cot, second, gains, cosine, sine, ffn_parts, normed, attended, q, k, v, wq, wkv, wo, sums, early,
    groups, ident,
):
    rows, width = tokens.shape
    count = normed.shape[0]
    line = count // 2
    seqs, total_slots, hd = q.shape
    low = tokens.dtype
    vmem = pltpu.VMEM
    tall = count * rows
    half = hd // 2
    sums = sums.reshape((-1,) + early.shape)
    n_sums, part_rows, _ = sums.shape
    shape = jax.ShapeDtypeStruct
    big = vmem((count, rows, width), low)
    head = vmem((seqs, total_slots, hd), low)
    weight = vmem((hd, width), low)
    flat = vmem((tall, hd), low)
    acc = vmem((total_slots, hd), F32)
    third = vmem((3 * half, width), low)
    g = gains.shape
    block = vmem((rows, width), F32)
    return pl.pallas_call(
        functools.partial(attention_grad_kernel, line, groups, seqs),
        out_shape=(
            shape((rows, width), low),
            shape((rows, width), low),
            shape(g[1:], F32),
            shape((n_sums // 2, 4 * part_rows, width), low),
            shape((6 * half, width), low),
        ),
        in_specs=[scalars()] + [vm()] * 7 + [hbm()] * 11,
        out_specs=(vm(), vm(), vm(), hbm(), hbm()),
        scratch_shapes=[
            vmem((rows, width), low), block, block, block,
            big, big, flat, head, head, head, weight, vmem((2, hd, width), low), weight, head, acc, acc,
            flat, flat, flat,
            vmem((2, 2, tall, half), low), vmem((2, tall, half), low), big,
            vmem((2,) + early.shape, low), vmem(sums.shape, low), vmem((3, half, width), low), third, third, third,
            vmem(g, F32), vmem(g, F32), vmem(g[1:], F32), vmem((groups,) + g[1:], F32),
        ]
        + gather_sems(count)
        + [
            DMA((12,)), DMA((n_sums + 1,)), DMA((n_sums + 1,)), DMA, DMA, DMA((3,)), DMA((3,)),
            DMA((n_sums + 1,)), DMA((n_sums + 1,)), DMA((n_sums + 1,)),
            DMA((count,)), DMA((count,)), DMA((groups,)), DMA((groups,)),
        ]
        + Reduce.scratch(line, rows, width, low) * 2,
        compiler_params=params(ident),
        name="attention_grad",
    )(
        lengths, tokens, branch, cot, second, gains, cosine, sine, ffn_parts, normed, attended, q, k, v, wq, wkv, wo, sums, early
    )


epsilon = 1e-06
theta_base = 1000042.0
masked_value = -1e30


def turned(source):
    half_width = source.shape[-1] // 2
    return jnp.concatenate([-source[..., half_width:], source[..., :half_width]], -1)


def rotate(source, cosine_table, sine_table):
    return source * cosine_table + turned(source) * sine_table


def unrotate(source, cosine_table, sine_table):
    return source * cosine_table - turned(source) * sine_table


def norm_forward(source, norm_gain):
    inverse = lax.rsqrt(jnp.mean(source * source, -1, keepdims=True) + epsilon)
    return (source * inverse * norm_gain, inverse)


def norm_backward(source, inverse, norm_gain, grad_out):
    weighted = grad_out * norm_gain
    inner_sum = jnp.sum(weighted * source, -1, keepdims=True)
    grad_in = (
        inverse * weighted - source * inverse * inverse * inverse * inner_sum / source.shape[-1]
    )
    return (grad_in, jnp.sum(grad_out * source * inverse, 0))


def weight_terms(normed, query_grad, key_grad, value_grad, attended, branch_grad, shard_count):
    token_count, model_width = normed.shape
    query_share = query_grad.shape[1] // shard_count
    kv_share = key_grad.shape[1] // shard_count
    shard_rows = 2 * query_share + 2 * kv_share

    def weight_term(first_row, row_count):
        blocks = row_count // shard_rows

        def columns(matrix, share_cols):
            return matrix.reshape(token_count, blocks, share_cols)

        part_query = jnp.einsum(
            "tmr,td->mrd",
            columns(query_grad, query_share),
            normed,
            preferred_element_type=jnp.float32,
        )
        part_key = jnp.einsum(
            "tmr,td->mrd", columns(key_grad, kv_share), normed, preferred_element_type=jnp.float32
        )
        part_value = jnp.einsum(
            "tmr,td->mrd", columns(value_grad, kv_share), normed, preferred_element_type=jnp.float32
        )
        part_out = jnp.einsum(
            "tmr,td->mrd",
            columns(attended, query_share),
            branch_grad,
            preferred_element_type=jnp.float32,
        )
        return jnp.concatenate([part_query, part_key, part_value, part_out], 1).reshape(
            row_count, model_width
        )

    return (weight_term, shard_rows)


def local_rows(
    tokens,
    lengths,
    prenorm_gain,
    query_weight,
    key_weight,
    value_weight,
    out_weight,
    midnorm_gain,
    gate_weight,
    up_weight,
    down_weight,
    cotangent,
):
    shard_count = lax.axis_size("shard")
    shard_rank = lax.axis_index("shard")
    micro_count, seq_dev, model_width = tokens.shape
    slot_count = seq_dev * shard_count
    repeat_heads = NH // KVH
    query_width = NH * HD
    kv_width = KVH * HD
    score_scale = 1.0 / math.sqrt(HD)
    local_pos = shard_rank * seq_dev + jnp.arange(seq_dev, dtype=jnp.int32)
    key_pos = jnp.arange(slot_count, dtype=jnp.int32)
    inverse_freq = theta_base ** (-(jnp.arange(0, HD, 2).astype(jnp.float32) / HD))
    angles = local_pos.astype(jnp.float32)[:, None] * inverse_freq[None, :]
    cosine_table = jnp.concatenate([jnp.cos(angles), jnp.cos(angles)], -1)[:, None, :]
    sine_table = jnp.concatenate([jnp.sin(angles), jnp.sin(angles)], -1)[:, None, :]
    gate_total = jnp.zeros(gate_weight.shape, jnp.float32)
    up_total = jnp.zeros(up_weight.shape, jnp.float32)
    down_total = jnp.zeros(down_weight.shape, jnp.float32)
    prenorm_total = jnp.zeros((model_width,), jnp.float32)
    midnorm_total = jnp.zeros((model_width,), jnp.float32)
    attn_total = None
    mixed_rows = []
    input_rows = []
    for micro_index in range(micro_count):
        gathered = (
            lax.all_gather(query_weight, "shard", axis=0, tiled=True),
            lax.all_gather(key_weight, "shard", axis=0, tiled=True),
            lax.all_gather(value_weight, "shard", axis=0, tiled=True),
            lax.all_gather(prenorm_gain, "shard", axis=0, tiled=True),
            lax.all_gather(midnorm_gain, "shard", axis=0, tiled=True),
        )
        query_full, key_full, value_full, prenorm_full, midnorm_full = gathered
        prenorm_f = prenorm_full.astype(jnp.float32)
        midnorm_f = midnorm_full.astype(jnp.float32)
        source = tokens[micro_index].astype(jnp.float32)
        length_now = lengths[micro_index]
        valid_rows = local_pos < length_now
        scaled_first, inverse_first = norm_forward(source, prenorm_f)
        normed_first = scaled_first.astype(jnp.bfloat16)
        query_pre = jnp.einsum(
            "sd,qd->sq", normed_first, query_full, preferred_element_type=jnp.float32
        ).reshape(seq_dev, NH, HD)
        key_pre = jnp.einsum(
            "sd,qd->sq", normed_first, key_full, preferred_element_type=jnp.float32
        ).reshape(seq_dev, KVH, HD)
        value_pre = jnp.einsum(
            "sd,qd->sq", normed_first, value_full, preferred_element_type=jnp.float32
        )
        query_rot = rotate(query_pre, cosine_table, sine_table).astype(jnp.bfloat16)
        key_rot = rotate(key_pre, cosine_table, sine_table).astype(jnp.bfloat16)
        key_value = jnp.concatenate(
            [key_rot.reshape(seq_dev, kv_width), value_pre.astype(jnp.bfloat16)], 1
        )
        kv_all = lax.all_gather(key_value, "shard", axis=0, tiled=True)
        keys_all = kv_all[:, :kv_width].reshape(slot_count, KVH, HD)
        values_all = kv_all[:, kv_width:].reshape(slot_count, KVH, HD)
        query_group = query_rot.reshape(seq_dev, KVH, repeat_heads, HD)
        scores = (
            jnp.einsum("skrd,tkd->krst", query_group, keys_all, preferred_element_type=jnp.float32)
            * score_scale
        )
        allowed = (key_pos[None, :] <= local_pos[:, None]) & (key_pos[None, :] < length_now)
        scores = jnp.where(allowed, scores, masked_value)
        row_max = jnp.max(scores, -1, keepdims=True)
        exp_scores = jnp.exp(scores - row_max)
        attention_probs = exp_scores / jnp.sum(exp_scores, -1, keepdims=True)
        probs_low = attention_probs.astype(jnp.bfloat16)
        attended = (
            jnp.einsum("krst,tkd->skrd", probs_low, values_all, preferred_element_type=jnp.float32)
            .astype(jnp.bfloat16)
            .reshape(seq_dev, query_width)
        )
        branch = jnp.dot(
            attended,
            lax.all_gather(out_weight, "shard", axis=0, tiled=True),
            preferred_element_type=jnp.float32,
        )
        middle = source + branch
        scaled_second, inverse_second = norm_forward(middle, midnorm_f)
        normed_second = scaled_second.astype(jnp.bfloat16)
        normed_all = lax.all_gather(normed_second, "shard", axis=0, tiled=True)
        gate_pre = jnp.einsum(
            "sd,fd->sf", normed_all, gate_weight, preferred_element_type=jnp.float32
        )
        up_pre = jnp.einsum("sd,fd->sf", normed_all, up_weight, preferred_element_type=jnp.float32)
        sigmoid_gate = jax.nn.sigmoid(gate_pre)
        silu_gate = gate_pre * sigmoid_gate
        hidden = (silu_gate * up_pre).astype(jnp.bfloat16)
        ffn_part = lax.psum_scatter(
            jnp.dot(hidden, down_weight, preferred_element_type=jnp.float32).astype(jnp.bfloat16),
            "shard",
            scatter_dimension=0,
            tiled=True,
        ).astype(jnp.float32)
        mixed_rows.append(
            jnp.where(valid_rows[:, None], middle + ffn_part, 0.0).astype(jnp.bfloat16)
        )
        cot_low = jnp.where(
            valid_rows[:, None], cotangent[micro_index], jnp.zeros_like(cotangent[micro_index])
        )
        cot_all = lax.all_gather(cot_low, "shard", axis=0, tiled=True)
        hidden_grad = jnp.einsum(
            "sd,fd->sf", cot_all, down_weight, preferred_element_type=jnp.float32
        )
        down_total = down_total + jnp.einsum(
            "sf,sd->fd", hidden, cot_all, preferred_element_type=jnp.float32
        )
        gate_grad = (
            hidden_grad * up_pre * sigmoid_gate * (1.0 + gate_pre * (1.0 - sigmoid_gate))
        ).astype(jnp.bfloat16)
        up_grad = (hidden_grad * silu_gate).astype(jnp.bfloat16)
        gate_total = gate_total + jnp.einsum(
            "sf,sd->fd", gate_grad, normed_all, preferred_element_type=jnp.float32
        )
        up_total = up_total + jnp.einsum(
            "sf,sd->fd", up_grad, normed_all, preferred_element_type=jnp.float32
        )
        second_grad = lax.psum_scatter(
            jnp.dot(gate_grad, gate_weight, preferred_element_type=jnp.float32)
            + jnp.dot(up_grad, up_weight, preferred_element_type=jnp.float32),
            "shard",
            scatter_dimension=0,
            tiled=True,
        )
        middle_part, midnorm_part = norm_backward(middle, inverse_second, midnorm_f, second_grad)
        middle_grad = cot_low.astype(jnp.float32) + middle_part
        midnorm_total = midnorm_total + midnorm_part
        branch_grad = middle_grad.astype(jnp.bfloat16)
        attended_grad = jnp.einsum(
            "sd,qd->sq",
            branch_grad,
            lax.all_gather(out_weight, "shard", axis=0, tiled=True),
            preferred_element_type=jnp.float32,
        ).astype(jnp.bfloat16)
        attended_group = attended_grad.reshape(seq_dev, KVH, repeat_heads, HD)
        probs_grad = jnp.einsum(
            "skrd,tkd->krst", attended_group, values_all, preferred_element_type=jnp.float32
        )
        inner_sum = jnp.sum(attention_probs * probs_grad, -1, keepdims=True)
        scores_grad = (attention_probs * (probs_grad - inner_sum)).astype(jnp.bfloat16)
        query_rot_grad = (
            jnp.einsum(
                "krst,tkd->skrd", scores_grad, keys_all, preferred_element_type=jnp.float32
            ).reshape(seq_dev, NH, HD)
            * score_scale
        )
        query_grad = (
            unrotate(query_rot_grad, cosine_table, sine_table)
            .astype(jnp.bfloat16)
            .reshape(seq_dev, query_width)
        )
        row_count = lax.axis_size("shard") * seq_dev
        key_part = (
            jnp.einsum(
                "krst,skrd->tkd", scores_grad, query_group, preferred_element_type=jnp.float32
            )
            * score_scale
        )
        value_part = jnp.einsum(
            "krst,skrd->tkd", probs_low, attended_group, preferred_element_type=jnp.float32
        )
        kv_grad = lax.psum_scatter(
            jnp.concatenate(
                [key_part.reshape(row_count, kv_width), value_part.reshape(row_count, kv_width)], 1
            ).astype(jnp.bfloat16),
            "shard",
            scatter_dimension=0,
            tiled=True,
        ).astype(jnp.float32)
        key_grad = (
            unrotate(kv_grad[:, :kv_width].reshape(seq_dev, KVH, HD), cosine_table, sine_table)
            .astype(jnp.bfloat16)
            .reshape(seq_dev, kv_width)
        )
        value_grad = kv_grad[:, kv_width:].astype(jnp.bfloat16)
        first_grad = jnp.einsum(
            "sq,qd->sd", query_grad, query_full, preferred_element_type=jnp.float32
        )
        first_grad = first_grad + jnp.einsum(
            "sq,qd->sd", key_grad, key_full, preferred_element_type=jnp.float32
        )
        first_grad = first_grad + jnp.einsum(
            "sq,qd->sd", value_grad, value_full, preferred_element_type=jnp.float32
        )
        source_part, prenorm_part = norm_backward(source, inverse_first, prenorm_f, first_grad)
        input_rows.append((middle_grad + source_part).astype(jnp.bfloat16))
        prenorm_total = prenorm_total + prenorm_part
        saved = (normed_first, query_grad, key_grad, value_grad, attended, branch_grad)
        weight_term, shard_rows = weight_terms(*saved, shard_count)
        reduced = lax.psum_scatter(
            weight_term(jnp.int32(0), lax.axis_size("shard") * shard_rows).astype(jnp.bfloat16),
            "shard",
            scatter_dimension=0,
            tiled=True,
        ).astype(jnp.float32)
        attn_total = reduced if attn_total is None else attn_total + reduced
    gain_sums = lax.psum((prenorm_total, midnorm_total), ("grp", "shard"))
    gain_share = model_width // shard_count
    prenorm_gradient = lax.dynamic_slice_in_dim(
        gain_sums[0], shard_rank * gain_share, gain_share, 0
    )
    midnorm_gradient = lax.dynamic_slice_in_dim(
        gain_sums[1], shard_rank * gain_share, gain_share, 0
    )
    summed = (
        lax.psum(attn_total.astype(jnp.bfloat16), "grp").astype(jnp.float32),
        lax.psum(gate_total.astype(jnp.bfloat16), "grp").astype(jnp.float32),
        lax.psum(up_total.astype(jnp.bfloat16), "grp").astype(jnp.float32),
        lax.psum(down_total.astype(jnp.bfloat16), "grp").astype(jnp.float32),
    )
    attn_rows = summed[0]
    query_share = query_width // shard_count
    kv_share = kv_width // shard_count
    query_gradient = attn_rows[:query_share]
    key_gradient = attn_rows[query_share : query_share + kv_share]
    value_gradient = attn_rows[query_share + kv_share : query_share + 2 * kv_share]
    out_gradient = attn_rows[query_share + 2 * kv_share :]
    return (
        jnp.stack(mixed_rows),
        jnp.stack(input_rows),
        prenorm_gradient,
        query_gradient,
        key_gradient,
        value_gradient,
        out_gradient,
        midnorm_gradient,
        summed[1],
        summed[2],
        summed[3],
    )


def local_heads(
    tokens,
    lengths,
    prenorm_gain,
    query_weight,
    key_weight,
    value_weight,
    out_weight,
    midnorm_gain,
    gate_weight,
    up_weight,
    down_weight,
    cotangent,
):
    low = jnp.bfloat16
    count = lax.axis_size("shard")
    groups = lax.axis_size("grp")
    seqs, seq_dev, model_width = tokens.shape
    rows = seqs * seq_dev
    inverse_freq = theta_base ** (-(jnp.arange(0, HD, 2).astype(jnp.float32) / HD))
    tokens_low = tokens.reshape(rows, model_width)
    cot_low = cotangent.reshape(rows, model_width)
    branch, gains, normed_first, cot_all, queries, keys, values, attended, kv_head, cosine, sine = (
        attention(
            lengths,
            tokens_low,
            cot_low,
            prenorm_gain[None, :],
            midnorm_gain[None, :],
            inverse_freq[None, :],
            query_weight,
            key_weight,
            value_weight,
            out_weight,
            count,
            groups,
            1,
        )
    )
    second_grad, ffn_parts, pair_sums, early = ffn(
        tokens_low, branch, gains, cot_all, gate_weight, up_weight, down_weight, groups, 2
    )
    mixed, input_gradient, gain_own, totals, attn_total = attention_grad(
        lengths,
        tokens_low,
        branch,
        cot_low,
        second_grad,
        gains,
        cosine,
        sine,
        ffn_parts,
        normed_first,
        attended,
        queries,
        keys,
        values,
        query_weight,
        kv_head,
        out_weight,
        pair_sums,
        early,
        groups,
        3,
    )
    head = query_weight.shape[0]
    kv_share = key_weight.shape[0]
    f32 = jnp.float32
    return (
        mixed.reshape(tokens.shape),
        input_gradient.reshape(tokens.shape),
        gain_own[0],
        attn_total[head : 2 * head].astype(f32),
        attn_total[2 * head : 2 * head + kv_share].astype(f32),
        attn_total[2 * head + kv_share :].astype(f32),
        attn_total[:head].astype(f32),
        gain_own[1],
        totals[1].astype(f32),
        totals[2].astype(f32),
        totals[0].astype(f32),
    )


def solution(mesh):
    planes = mesh.shape["shard"] == NH and mesh.shape["grp"] == 4
    local = local_heads if planes else local_rows
    in_specs = (
        P("grp", "shard", None),
        P("grp"),
        P("shard"),
        P("shard", None),
        P("shard", None),
        P("shard", None),
        P("shard", None),
        P("shard"),
        P("shard", None),
        P("shard", None),
        P("shard", None),
        P("grp", "shard", None),
    )
    out_specs = (
        P("grp", "shard", None),
        P("grp", "shard", None),
        P("shard"),
        P("shard", None),
        P("shard", None),
        P("shard", None),
        P("shard", None),
        P("shard"),
        P("shard", None),
        P("shard", None),
        P("shard", None),
    )
    return jax.shard_map(local, mesh=mesh, in_specs=in_specs, out_specs=out_specs, check_vma=False)
```

```python
import functools
import math

import jax
import jax.numpy as jnp
from jax import lax
from jax.experimental import pallas as pl
from jax.experimental.pallas import tpu as pltpu
from jax.sharding import PartitionSpec as P

NH = 8
KVH = 4
HD = 256
MASKED = -1e30
EPSILON = 1e-06
DEPTH = 2
MESH = pl.DeviceIdType.MESH
F32 = jnp.float32
DMA = pltpu.SemaphoreType.DMA
REST = 16
PIECE = 128
EARLY = 3
CHUNKS = 2


def pieces(rows):
    size = -(-(rows - REST) // (16 * CHUNKS)) * 16
    cuts = [min(i * size, rows - REST) for i in range(CHUNKS + 1)] + [rows]
    return [pl.ds(a, b - a) for a, b in zip(cuts, cuts[1:])]


VMEM_LIMIT = 66_000_000


def either(condition, action):
    pl.when(condition)(action)


def total_into(dst, *srcs):
    step = 16

    @pl.loop(0, dst.shape[0] // step)
    def _(i):
        at = pl.ds(pl.multiple_of(i * step, step), step)
        value = srcs[0][at].astype(F32)
        for src in srcs[1:]:
            value = value + src[at].astype(F32)
        dst[at] = value.astype(dst.dtype)


class Place:
    def __init__(self, line):
        self.line = line
        self.me = lax.axis_index("shard")
        self.z = self.me // 2
        self.y = lax.rem(self.me, 2)
        self.cross = self.me + 1 - 2 * self.y
        self.low_end = self.z == 0
        self.high_end = self.z == line - 1
        near = []
        for z in range(line):
            order = [z]
            for k in range(1, line):
                order += [d for d in (z - k, z + k) if 0 <= d < line]
            near.append(order)
        self.tables = near

    def near(self, i):
        out = jnp.int32(0)
        for z in range(self.line):
            row = jnp.int32(self.tables[z][0])
            for k in range(1, self.line):
                row = jnp.where(i == k, self.tables[z][k], row)
            out = jnp.where(self.z == z, row, out)
        return out

    def far(self, i):
        return self.near(self.line - 1 - i)

    def greet(self, groups):
        barrier = pltpu.get_barrier_semaphore()
        count = 2 * self.line
        rank = lax.axis_index("grp")
        for step in range(1, count):
            pl.semaphore_signal(
                barrier,
                inc=1,
                device_id={"shard": lax.rem(self.me + step, count)},
                device_id_type=MESH,
            )
        for step in range(1, groups):
            pl.semaphore_signal(
                barrier,
                inc=1,
                device_id={"grp": lax.rem(rank + step, groups)},
                device_id_type=MESH,
            )
        pl.semaphore_wait(barrier, count + groups - 2)


class Gather:
    UP, DOWN, CROSS = 0, 1, 2

    def __init__(self, place, own, out, local_sem, send_sem, recv_sem):
        self.p, self.own, self.out = place, own, out
        self.local_sem, self.send_sem, self.recv_sem = local_sem, send_sem, recv_sem
        self.pieces = pieces(own.shape[0])
        self.last = len(self.pieces) - 1

    def copy(self, way, origin, part, own=False):
        p = self.p
        peer = (p.me + 2, p.me - 2, p.cross)[way]
        at = self.pieces[part]
        return pltpu.make_async_remote_copy(
            src_ref=self.own.at[at] if own else self.out.at[origin, at],
            dst_ref=self.out.at[origin, at],
            send_sem=self.send_sem.at[way, origin, part],
            recv_sem=self.recv_sem.at[origin, part],
            device_id={"shard": peer},
            device_id_type=MESH,
        )

    def arrived(self, origin, part):
        self.copy(self.CROSS, origin, part).wait_recv()

    def start(self):
        self.send_own()
        self.pass_rest()

    def send_own(self):
        p = self.p
        pltpu.make_async_copy(self.own, self.out.at[p.me], self.local_sem).start()
        for part in (self.last,) + tuple(range(self.last)):
            self.copy(self.CROSS, p.me, part, True).start()
        for part in range(self.last + 1):
            either(p.z < p.line - 1, lambda: self.copy(self.UP, p.me, part, True).start())
            either(p.z > 0, lambda: self.copy(self.DOWN, p.me, part, True).start())

    def pass_rest(self):
        p = self.p
        self.arrived(p.cross, self.last)
        either(p.z < p.line - 1, lambda: self.copy(self.UP, p.cross, self.last).start())
        either(p.z > 0, lambda: self.copy(self.DOWN, p.cross, self.last).start())
        pltpu.make_async_copy(self.own, self.out.at[p.me], self.local_sem).wait()

    def hop(self, k):
        p = self.p
        below, above = p.me - 2 * k, p.me + 2 * k
        has_below, has_above = p.z - k >= 0, p.z + k < p.line

        def first(origin, part, way, more):
            self.arrived(origin, part)
            self.copy(self.CROSS, origin, part).start()
            either(more, lambda: self.copy(way, origin, part).start())

        def last(origin, other, way, more):
            for block in (origin, other):
                self.arrived(block, self.last)
                either(more, lambda: self.copy(way, block, self.last).start())

        for part in range(self.last):
            either(has_below, lambda: first(below, part, self.UP, p.z < p.line - 1))
            either(has_above, lambda: first(above, part, self.DOWN, p.z > 0))
        either(has_below, lambda: last(below, p.cross - 2 * k, self.UP, p.z < p.line - 1))
        either(has_above, lambda: last(above, p.cross + 2 * k, self.DOWN, p.z > 0))

    def whole(self, position):
        for part in range(self.last):
            self.arrived(2 * position + 1 - self.p.y, part)

    def drain(self):
        p = self.p

        @pl.loop(0, p.line)
        def _(d):
            mine, other = 2 * d + p.y, 2 * d + 1 - p.y
            for part in range(self.last):
                self.copy(self.CROSS, mine, part).wait_send()

            @pl.when(d == p.z)
            def _():
                self.copy(self.CROSS, mine, self.last).wait_send()

            def line_sent(way):
                for part in range(self.last + 1):
                    self.copy(way, mine, part).wait_send()
                self.copy(way, other, self.last).wait_send()

            either((d <= p.z) & (p.z < p.line - 1), lambda: line_sent(self.UP))
            either((d >= p.z) & (p.z > 0), lambda: line_sent(self.DOWN))


class Reduce:
    BUP, BDN, BX = 0, 2, 4
    UP, DOWN, CROSS = 5, 5 + CHUNKS, 5 + 2 * CHUNKS
    WAYS = 5 + 3 * CHUNKS
    N_SCRATCH = 9

    @staticmethod
    def scratch(line, rows, width, dtype):
        v = pltpu.VMEM
        return (
            [v((line, rows - REST, width), dtype)] * 3
            + [v((line, 2, REST, width), dtype)] * 2
            + [v((REST, width), dtype)] * 2
            + [DMA((Reduce.WAYS, line)), DMA((Reduce.WAYS, line))]
        )

    def __init__(self, place, parts, out, scratch):
        self.p, self.parts, self.out = place, parts, out
        self.cross_in, self.up_in, self.down_in, self.bup_in, self.bdn_in = scratch[:5]
        self.bx_out, self.bx_in, self.send_sem, self.recv_sem = scratch[5:]
        self.pieces = pieces(parts.shape[1])
        self.b = self.pieces[-1]

    def desc(self, way, slot, src, dst, peer):
        return pltpu.make_async_remote_copy(
            src_ref=src,
            dst_ref=dst,
            send_sem=self.send_sem.at[way, slot],
            recv_sem=self.recv_sem.at[way, slot],
            device_id={"shard": peer},
            device_id_type=MESH,
        )

    def cross_copy(self, d, c):
        p, at = self.p, self.pieces[c]
        return self.desc(
            self.CROSS + c,
            d,
            self.parts.at[2 * d + 1 - p.y, at],
            self.cross_in.at[d, at],
            p.cross,
        )

    def line_copy(self, up, d, c):
        p, at = self.p, self.pieces[c]
        came = self.up_in if up else self.down_in
        return self.desc(
            (self.UP if up else self.DOWN) + c,
            d,
            self.cross_in.at[d, at],
            came.at[d, at],
            p.me + 2 if up else p.me - 2,
        )

    def b_copy(self, up, d, o, src=None):
        p = self.p
        held = self.bup_in if up else self.bdn_in
        return self.desc(
            (self.BUP if up else self.BDN) + o,
            d,
            held.at[d, o] if src is None else src,
            held.at[d, o],
            p.me + 2 if up else p.me - 2,
        )

    def bx_copy(self):
        return self.desc(self.BX, 0, self.bx_out, self.bx_in, self.p.cross)

    def column(self, o):
        return self.p.y if o == 0 else 1 - self.p.y

    def send_across(self, i):
        for c in range(CHUNKS):
            self.cross_copy(self.p.far(i), c).start()

    def b_hop(self, i):
        p = self.p
        d = p.far(i)

        def go(up):
            first = p.low_end if up else p.high_end
            held = self.bup_in if up else self.bdn_in
            for o in (1, 0):
                mine = self.parts.at[2 * d + self.column(o), self.b]
                either(first, lambda: self.b_copy(up, d, o, mine).start())

                @pl.when(jnp.logical_not(first))
                def _():
                    self.b_copy(up, d, o).wait_recv()
                    total_into(held.at[d, o], mine, held.at[d, o])
                    self.b_copy(up, d, o).start()

        either(d > p.z, lambda: go(True))
        either(d < p.z, lambda: go(False))

    def hop(self, i):
        p = self.p
        d = p.far(i)
        for c in range(CHUNKS):
            self.cross_copy(d, c).wait_recv()
            at = self.pieces[c]
            mine = self.parts.at[2 * d + p.y, at]
            held = self.cross_in.at[d, at]

            def go(up):
                first = p.low_end if up else p.high_end
                came = self.up_in if up else self.down_in
                either(first, lambda: total_into(held, mine, held))

                @pl.when(jnp.logical_not(first))
                def _():
                    self.line_copy(up, d, c).wait_recv()
                    total_into(held, mine, held, came.at[d, at])

                self.line_copy(up, d, c).start()

            either(d > p.z, lambda: go(True))
            either(d < p.z, lambda: go(False))

    def close(self, dst, mine, ups, downs):
        p = self.p
        either(p.low_end, lambda: total_into(dst, *mine, downs))
        either(p.high_end, lambda: total_into(dst, *mine, ups))
        either(
            jnp.logical_not(p.low_end | p.high_end), lambda: total_into(dst, *mine, ups, downs)
        )

    def finish(self):
        p = self.p
        for o in (1, 0):
            either(jnp.logical_not(p.low_end), lambda: self.b_copy(True, p.z, o).wait_recv())
            either(jnp.logical_not(p.high_end), lambda: self.b_copy(False, p.z, o).wait_recv())
            if o:
                mine = self.parts.at[2 * p.z + self.column(o), self.b]
                self.close(self.bx_out, (mine,), self.bup_in.at[p.z, o], self.bdn_in.at[p.z, o])
                self.bx_copy().start()
        self.bx_copy().wait_recv()
        self.close(
            self.out.at[self.b],
            (self.parts.at[p.me, self.b], self.bx_in),
            self.bup_in.at[p.z, 0],
            self.bdn_in.at[p.z, 0],
        )
        for c in range(CHUNKS):
            self.cross_copy(p.z, c).wait_recv()
            either(jnp.logical_not(p.low_end), lambda: self.line_copy(True, p.z, c).wait_recv())
            either(jnp.logical_not(p.high_end), lambda: self.line_copy(False, p.z, c).wait_recv())
            at = self.pieces[c]
            self.close(
                self.out.at[at],
                (self.parts.at[p.me, at], self.cross_in.at[p.z, at]),
                self.up_in.at[p.z, at],
                self.down_in.at[p.z, at],
            )

    def drain(self):
        p = self.p
        self.bx_copy().wait_send()

        @pl.loop(0, p.line)
        def _(d):
            def line_sent(up):
                for c in range(CHUNKS):
                    self.line_copy(up, d, c).wait_send()
                self.b_copy(up, d, 0).wait_send()
                self.b_copy(up, d, 1).wait_send()

            for c in range(CHUNKS):
                self.cross_copy(d, c).wait_send()
            either(d > p.z, lambda: line_sent(True))
            either(d < p.z, lambda: line_sent(False))


def dot(a, b):
    return jnp.dot(a, b, preferred_element_type=F32)


def dot_t(a, b):
    return lax.dot_general(a, b, (((1,), (1,)), ((), ())), preferred_element_type=F32)


def t_dot(a, b):
    return lax.dot_general(a, b, (((0,), (0,)), ((), ())), preferred_element_type=F32)


def to_peer(axis, peer, src, dst, send_sem, recv_sem):
    return pltpu.make_async_remote_copy(
        src_ref=src,
        dst_ref=dst,
        send_sem=send_sem,
        recv_sem=recv_sem,
        device_id={axis: peer},
        device_id_type=MESH,
    )


def turn_by(v, cosine, sine):
    half = v.shape[-1] // 2
    a, b = v[:, :half], v[:, half:]
    return jnp.concatenate([a * cosine - b * sine, b * cosine + a * sine], -1)


def turn_back(v, cosine, sine):
    return turn_by(v, cosine, -sine)


def probabilities(query, keys, rows_from, limit):
    scores = dot_t(query, keys) * (1.0 / math.sqrt(HD))
    row = lax.broadcasted_iota(jnp.int32, scores.shape, 0) + rows_from
    col = lax.broadcasted_iota(jnp.int32, scores.shape, 1)
    scores = jnp.where((col <= row) & (col < limit), scores, MASKED)
    weight = jnp.exp(scores - jnp.max(scores, -1, keepdims=True))
    return weight / jnp.sum(weight, -1, keepdims=True)


def row_valid(place, lengths, rows):
    slots = rows // lengths.shape[0]
    row = lax.broadcasted_iota(jnp.int32, (rows, 1), 0)
    limit = jnp.full((rows, 1), lengths[0], jnp.int32)
    for n in range(1, lengths.shape[0]):
        limit = jnp.where(row >= n * slots, lengths[n], limit)
    return place.me * slots + lax.rem(row, slots) < limit


def gain_row(shares, which):
    return jnp.concatenate([shares[b, which : which + 1] for b in range(shares.shape[0])], 1)


def inverse_rms(x):
    return lax.rsqrt(jnp.mean(x * x, -1, keepdims=True) + EPSILON)


def norm_grad(x, inverse, gain, grad):
    weighted = grad * gain
    inner = jnp.sum(weighted * x, -1, keepdims=True)
    return inverse * weighted - x * inverse * inverse * inverse * inner / x.shape[-1]


def start_all(copies):
    for c in copies:
        c.start()


def wait_all(copies):
    for c in copies:
        c.wait()


def scalars():
    return pl.BlockSpec(memory_space=pltpu.SMEM)


def hbm():
    return pl.BlockSpec(memory_space=pl.ANY)


def vm():
    return pl.BlockSpec(memory_space=pltpu.VMEM)


def params(ident):
    return pltpu.CompilerParams(
        collective_id=ident, has_side_effects=True, vmem_limit_bytes=VMEM_LIMIT
    )


def gather_sems(count):
    return [DMA, DMA((3, count, CHUNKS + 1)), DMA((count, CHUNKS + 1))]


def attention_kernel(
    line, groups, seqs,
    lengths, own, cot_raw, pre_gain, mid_gain, freq, wq_hbm, wk_hbm, wv_hbm, wo_hbm,
    branch, small_out, normed_hbm, cot_hbm, q_hbm, k_hbm, v_hbm, attended_hbm, wkv_hbm, cos_hbm, sin_hbm,
    small, cot_own, rows_all, normed, cot_all, q, k, v, attended, wq, wkv, wo, cosine, sine, parts,
    *scratch,
):
    p = Place(line)
    count = 2 * line
    rank = lax.axis_index("grp")
    g1, g2 = scratch[:3], scratch[3:6]
    (load_sem, small_send, small_recv, wy_send, wg_send, w_recv, save_sem) = scratch[6:13]
    r_scratch = scratch[13:]
    half = wk_hbm.shape[0]
    piece = half // 2
    at_own = pl.ds(pl.multiple_of(p.y * half, half), half)
    loads = [
        pltpu.make_async_copy(src, dst, load_sem.at[i])
        for i, (src, dst) in enumerate(
            (
                (wk_hbm, wkv.at[0, at_own]),
                (wv_hbm, wkv.at[1, at_own]),
                (wq_hbm, wq),
                (wo_hbm, wo),
            )
        )
    ]
    start_all(loads)
    p.greet(groups)

    small[...] = jnp.zeros_like(small)
    small[0:1] = pre_gain[...].astype(F32)
    small[1:2] = mid_gain[...].astype(F32)

    def small_copy(step, peer, origin):
        return to_peer(
            "shard", peer, small, small_out.at[origin], small_send.at[step], small_recv.at[step]
        )

    for step in range(1, count):
        small_copy(step, lax.rem(p.me + step, count), p.me).start()
    gather = Gather(p, own, rows_all, *g1)
    gather.start()
    cots = Gather(p, cot_own, cot_all, *g2)
    small_out[p.me] = small[...]

    def rows_of(quarter, column):
        return wkv.at[
            quarter // 2,
            pl.ds(pl.multiple_of(column * half + lax.rem(quarter, 2) * piece, piece), piece),
        ]

    def across():
        ref = rows_of(rank, p.y)
        return to_peer("shard", p.cross, ref, ref, wy_send, w_recv.at[rank])

    def share(step):
        ref = rows_of(rank, 1 - p.y)
        return to_peer(
            "grp", lax.rem(rank + step, groups), ref, ref, wg_send.at[step], w_recv.at[rank]
        )

    wait_all(loads)
    across().start()
    pos = lax.broadcasted_iota(jnp.int32, cosine.shape, 0).astype(F32)
    angle = pos * freq[...]
    cosine[...] = jnp.cos(angle)
    sine[...] = jnp.sin(angle)
    cot = cot_raw[...]
    cot_own[...] = jnp.where(row_valid(p, lengths, cot.shape[0]), cot, jnp.zeros_like(cot))
    gather.hop(1)
    for step in range(1, count):
        small_copy(step, p.me, lax.rem(p.me + count - step, count)).wait_recv()
    gain = gain_row(small_out, 0)
    across().wait_recv()
    for step in range(1, groups):
        share(step).start()
    rows = own.shape[0]
    pair = 2 * rows
    slots = rows // seqs
    low = own.dtype
    for step in range(1, groups):
        quarter = lax.rem(rank + step, groups)
        ref = rows_of(quarter, 1 - p.y)
        to_peer("grp", rank, ref, ref, wg_send.at[step], w_recv.at[quarter]).wait_recv()

    @pl.loop(0, line)
    def _(i):
        d = p.near(i)
        gather.whole(d)
        x = rows_all[pl.ds(2 * d, 2)].reshape(pair, -1).astype(F32)
        n = (x * inverse_rms(x) * gain).astype(low)
        normed[pl.ds(2 * d, 2)] = n.reshape(2, rows, -1)
        at = pl.ds(pl.multiple_of(d * 2 * slots, 2 * slots), 2 * slots)
        c, s = cosine[at], sine[at]

        def by_rows(t):
            return jnp.concatenate([t[:slots]] * seqs + [t[slots:]] * seqs, 0)

        c, s = by_rows(c), by_rows(s)

        def put(target, value):
            for block in range(2):
                for m in range(seqs):
                    to = pl.ds(
                        pl.multiple_of(d * 2 * slots + block * slots, slots), slots
                    )
                    target[m, to] = value[block * rows + m * slots : block * rows + (m + 1) * slots]

        put(q, turn_by(dot_t(n, wq[...]), c, s).astype(low))
        put(k, turn_by(dot_t(n, wkv[0]), c, s).astype(low))
        put(v, dot_t(n, wkv[1]).astype(low))
        gather.hop(i + 2)
        either(i == line - 3, cots.send_own)

    saves = [
        pltpu.make_async_copy(src, dst, save_sem.at[i])
        for i, (src, dst) in enumerate(
            (
                (normed, normed_hbm),
                (q, q_hbm),
                (k, k_hbm),
                (v, v_hbm),
                (wkv, wkv_hbm),
                (cosine, cos_hbm),
                (sine, sin_hbm),
            )
        )
    ]
    start_all(saves)
    cots.pass_rest()
    total_slots = q.shape[1]
    tile = min(256, total_slots)

    @pl.loop(0, seqs)
    def _(n):
        for t in range(total_slots // tile):
            span = (t + 1) * tile
            at = pl.ds(t * tile, tile)
            probs = probabilities(q[n, at], k[n, pl.ds(0, span)], t * tile, lengths[n])
            out = dot(probs.astype(low), v[n, pl.ds(0, span)]).astype(low)
            for c in range(tile // slots):
                b = (t * tile) // slots + c
                attended[pl.ds(pl.multiple_of(b * rows + n * slots, slots), slots)] = out[
                    c * slots : (c + 1) * slots
                ]
        cots.hop(n + 1)

    for h in range(seqs + 1, line):
        cots.hop(h)

    @pl.loop(0, line)
    def _(d):
        at = pl.ds(pl.multiple_of(d * pair, pair), pair)
        parts[pl.ds(2 * d, 2)] = dot(attended[at], wo[...]).astype(low).reshape(2, rows, -1)

    reduce = Reduce(p, parts, branch, r_scratch)
    saves2 = [pltpu.make_async_copy(attended, attended_hbm, save_sem.at[7])]
    start_all(saves2)
    for d in range(line):
        cots.whole(d)
    for i in range(DEPTH):
        reduce.send_across(i)
    saves3 = [pltpu.make_async_copy(cot_all, cot_hbm, save_sem.at[8])]
    start_all(saves3)
    for i in range(line - 1):
        reduce.b_hop(i)
    for i in range(line - 1):
        reduce.hop(i)
        if i + DEPTH < line:
            reduce.send_across(i + DEPTH)
    reduce.finish()
    reduce.drain()
    gather.drain()
    cots.drain()
    wait_all(saves + saves2 + saves3)
    across().wait_send()
    for step in range(1, groups):
        share(step).wait_send()
    for step in range(1, count):
        small_copy(step, lax.rem(p.me + step, count), p.me).wait_send()


def attention(lengths, own, cot, pre_gain, mid_gain, freq, wq, wk, wv, wo, count, groups, ident):
    rows, width = own.shape
    seqs = lengths.shape[0]
    total_slots = count * rows // seqs
    small = (8, pre_gain.shape[1])
    line = count // 2
    low = own.dtype
    v = pltpu.VMEM
    shape = jax.ShapeDtypeStruct
    hd = wq.shape[0]
    big = (count, rows, width)
    head = (seqs, total_slots, hd)
    table = (total_slots, hd // 2)
    flat = (count * rows, hd)
    return pl.pallas_call(
        functools.partial(attention_kernel, line, groups, seqs),
        out_shape=(
            shape((rows, width), F32),
            shape((count,) + small, F32),
            shape(big, low),
            shape(big, low),
            shape(head, low),
            shape(head, low),
            shape(head, low),
            shape(flat, low),
            shape((2, hd, width), low),
            shape(table, F32),
            shape(table, F32),
        ),
        in_specs=[scalars()] + [vm()] * 5 + [hbm()] * 4,
        out_specs=(vm(), vm()) + (hbm(),) * 9,
        scratch_shapes=[
            v(small, F32), v((rows, width), low), v(big, low), v(big, low), v(big, low), v(head, low), v(head, low), v(head, low), v(flat, low),
            v((hd, width), low), v((2, hd, width), low), v((hd, width), low), v(table, F32), v(table, F32), v(big, low),
        ]
        + gather_sems(count) * 2
        + [DMA((4,)), DMA((count,)), DMA((count,)), DMA, DMA((groups,)), DMA((groups,)), DMA((9,))]
        + Reduce.scratch(line, rows, width, low),
        compiler_params=params(ident),
        name="attention",
    )(lengths, own, cot, pre_gain, mid_gain, freq, wq, wk, wv, wo)


def ffn_kernel(
    line, groups,
    tokens, branch, gains, cot_hbm, gate_hbm, up_hbm, down_hbm,
    second, ffn_hbm, pair_hbm, chip_in,
    own, normed, cot, gate_w, up_w, down_w, hidden, gate_g, up_g, parts, stage, theirs,
    *scratch,
):
    p = Place(line)
    rank = lax.axis_index("grp")
    core = lax.rem(rank, 2)
    partner = rank + 1 - 2 * core
    opposite = lax.rem(rank + 2, groups)
    (load_sem, out_sem, stage_send, stage_recv, chip_send, chip_recv) = scratch[3:9]
    loads = [
        pltpu.make_async_copy(src, dst, load_sem.at[i])
        for i, (src, dst) in enumerate(
            ((gate_hbm, gate_w), (up_hbm, up_w), (cot_hbm, cot), (down_hbm, down_w))
        )
    ]
    start_all(loads)
    middle = tokens[...].astype(F32) + branch[...]
    own[...] = (middle * inverse_rms(middle) * gain_row(gains, 1)).astype(own.dtype)
    p.greet(groups)
    gather = Gather(p, own, normed, *scratch[:3])
    gather.start()
    wait_all(loads)
    rows = own.shape[0]
    pair = 2 * rows
    low = own.dtype

    @pl.loop(0, line)
    def _(i):
        gather.hop(i + 1)
        d = p.near(i)
        gather.whole(d)
        x = normed[pl.ds(2 * d, 2)].reshape(pair, -1)
        g = dot_t(x, gate_w[...])
        u = dot_t(x, up_w[...])
        dh = dot_t(cot[pl.ds(2 * d, 2)].reshape(pair, -1), down_w[...])
        s = 1.0 / (1.0 + jnp.exp(-g))
        silu = g * s
        at = pl.ds(pl.multiple_of(d * pair, pair), pair)
        hidden[at] = (silu * u).astype(low)
        up_g[at] = (dh * silu).astype(low)
        gate_g[at] = (dh * u * s * (1.0 + g * (1.0 - s))).astype(low)
        part = dot(gate_g[at], gate_w[...]) + dot(up_g[at], up_w[...])
        parts[pl.ds(2 * d, 2)] = part.astype(low).reshape(2, rows, -1)

    reduce = Reduce(p, parts, second, scratch[9:])
    for i in range(DEPTH):
        reduce.send_across(i)
    for i in range(line - 1):
        reduce.b_hop(i)

    units = hidden.shape[1]
    quarter = units // 4
    half = units // 2
    mine = (up_w.at[pl.ds(0, half)], gate_w.at[pl.ds(0, half)], gate_w.at[pl.ds(half, half)])

    def to_partner(which, j):
        return to_peer(
            "grp",
            partner,
            stage.at[j],
            theirs.at[which, pl.ds(j * quarter, quarter)],
            stage_send.at[j],
            stage_recv.at[which, j],
        )

    def gradient(which, left, right):
        def block(q):
            cols = pl.ds(pl.multiple_of(q * quarter, quarter), quarter)
            return t_dot(left[:, cols], right[...].reshape(left.shape[0], -1)).astype(low)

        @pl.loop(0, 2)
        def _(j):
            if which:
                to_partner(which - 1, j).wait_send()
            stage[j] = block(2 * (1 - core) + j)
            to_partner(which, j).start()

        @pl.loop(0, 2)
        def _(j):
            at = pl.ds(pl.multiple_of(j * quarter, quarter), quarter)
            mine[which][at] = block(2 * core + j)

    def add_theirs(which):
        for j in range(2):
            to_partner(which, j).wait_recv()
        total_into(mine[which], mine[which], theirs.at[which])

    def chip_copy():
        return to_peer(
            "grp", opposite, mine[0].at[pl.ds(0, chip_in.shape[0])], chip_in, chip_send, chip_recv
        )

    def save_pair(which):
        return pltpu.make_async_copy(mine[which], pair_hbm.at[which], out_sem.at[which])

    gradient(0, hidden, cot)
    reduce.hop(0)
    reduce.send_across(DEPTH)
    add_theirs(0)
    chip_copy().start()
    save_pair(0).start()
    gradient(1, gate_g, normed)
    reduce.hop(1)
    reduce.send_across(DEPTH + 1)
    add_theirs(1)
    save_pair(1).start()
    gradient(2, up_g, normed)
    reduce.hop(2)
    gather.drain()

    @pl.loop(0, line)
    def _(d):
        at = pl.ds(pl.multiple_of(d * pair, pair), pair)
        normed[pl.ds(2 * d, 2)] = dot(hidden[at], down_w[...]).astype(low).reshape(2, rows, -1)

    ffn_save = pltpu.make_async_copy(normed, ffn_hbm, out_sem.at[3])
    ffn_save.start()
    add_theirs(2)
    save_pair(2).start()
    reduce.finish()
    for j in range(2):
        to_partner(2, j).wait_send()

    reduce.drain()
    chip_copy().wait()
    ffn_save.wait()
    for which in range(3):
        save_pair(which).wait()


def ffn(tokens, branch, gains, cot, gate_w, up_w, down_w, groups, ident):
    rows, width = tokens.shape
    count = cot.shape[0]
    line = count // 2
    units = gate_w.shape[0]
    low = tokens.dtype
    v = pltpu.VMEM
    tall = count * rows
    shape = jax.ShapeDtypeStruct
    big = (count, rows, width)
    half = (units // 2, width)
    return pl.pallas_call(
        functools.partial(ffn_kernel, line, groups),
        out_shape=(
            shape((rows, width), F32),
            shape(big, low),
            shape((3,) + half, low),
            shape((EARLY * PIECE, width), low),
        ),
        in_specs=[vm()] * 3 + [hbm()] * 4,
        out_specs=(vm(), hbm(), hbm(), hbm()),
        scratch_shapes=[v((rows, width), low)]
        + [v(big, low)] * 2
        + [v((units, width), low)] * 3
        + [v((tall, units), low)] * 3
        + [v(big, low), v((2, units // 4, width), low), v((3,) + half, low)]
        + gather_sems(count)
        + [DMA((4,)), DMA((4,)), DMA((2,)), DMA((3, 2)), DMA, DMA]
        + Reduce.scratch(line, rows, width, low),
        compiler_params=params(ident),
        name="ffn",
    )(tokens, branch, gains, cot, gate_w, up_w, down_w)


def attention_grad_kernel(
    line, groups, seqs,
    lengths, tokens, branch, cot, second, gains, cosine, sine,
    ffn_hbm, normed_hbm, attended_hbm, q_hbm, k_hbm, v_hbm, wq_hbm, wkv_hbm, wo_hbm, sums_hbm, early_hbm,
    mixed, input_grad, gain_out, total_hbm, attn_hbm,
    own, middle_grad, first, ffn_own, dbranch, normed, attended, q, k, v, wq, wkv, wo, da, dk_acc, dv_acc, dq_rows, dk_rows, dv_rows,
    halves, half_in, ffn_parts, sums, sums_in, stage, mine, theirs, mine_in, gain_held, gain_in, gain_sum, gain_all,
    *scratch,
):
    p = Place(line)
    count = 2 * line
    rank = lax.axis_index("grp")
    core = lax.rem(rank, 2)
    partner = rank + 1 - 2 * core
    opposite = lax.rem(rank + 2, groups)
    (
        load_sem, chip_send, chip_recv, half_send, half_recv, stage_send, stage_recv,
        back_send, back_recv, keep_sem, ga_send, ga_recv, gb_send, gb_recv,
    ) = scratch[3:17]
    n = Reduce.N_SCRATCH
    loads = [
        pltpu.make_async_copy(src, dst, load_sem.at[i])
        for i, (src, dst) in enumerate(
            (
                (wo_hbm, wo),
                (ffn_hbm, ffn_parts),
                (attended_hbm, attended),
                (q_hbm, q),
                (k_hbm, k),
                (v_hbm, v),
                (wq_hbm, wq),
                (wkv_hbm, wkv),
                (normed_hbm, normed),
                (early_hbm, sums_in.at[pl.ds(0, EARLY)]),
            )
        )
    ]
    start_all(loads)

    def load_sum(i):
        return pltpu.make_async_copy(sums_hbm.at[i], sums.at[lax.rem(i, 2)], load_sem.at[10 + lax.rem(i, 2)])

    load_sum(0).start()
    load_sum(1).start()
    middle = tokens[...].astype(F32) + branch[...]
    inverse = inverse_rms(middle)
    grad = cot[...].astype(F32)
    grad = jnp.where(row_valid(p, lengths, grad.shape[0]), grad, jnp.zeros_like(grad))
    grad = grad + norm_grad(middle, inverse, gain_row(gains, 1), second[...])
    middle_grad[...] = grad
    own[...] = grad.astype(own.dtype)
    mid_total = jnp.sum(second[...] * middle * inverse, 0, keepdims=True)
    share = gain_held.shape[2]
    for b in range(count):
        gain_held[b] = jnp.zeros(gain_held.shape[1:], F32)
        gain_held[b, 1:2] = mid_total[:, b * share : (b + 1) * share]
    p.greet(groups)
    gather = Gather(p, own, dbranch, *scratch[:3])
    n_sums = sums_hbm.shape[0]
    part_rows = sums.shape[1]

    def chip_copy(i):
        return to_peer(
            "grp", opposite, sums_hbm.at[i], sums_in.at[i], chip_send.at[i], chip_recv.at[i]
        )

    gather.start()

    @pl.loop(EARLY, n_sums)
    def _(i):
        chip_copy(i).start()

    wait_all(loads)
    ffn_sum = Reduce(p, ffn_parts, ffn_own, scratch[17 : 17 + n])
    rows = own.shape[0]
    pair = 2 * rows
    slots = rows // seqs
    low = own.dtype
    scale = 1.0 / math.sqrt(HD)

    @pl.loop(0, line)
    def _(i):
        gather.hop(i + 1)

        @pl.when(i == line - 2)
        def _():
            for first_sends in range(DEPTH):
                ffn_sum.send_across(first_sends)

        d = p.near(i)
        gather.whole(d)
        grad = dot_t(dbranch[pl.ds(2 * d, 2)].reshape(pair, -1), wo[...]).astype(low)
        for block in range(2):
            for m in range(seqs):
                at = pl.ds(pl.multiple_of(d * 2 * slots + block * slots, slots), slots)
                da[m, at] = grad[block * rows + m * slots : block * rows + (m + 1) * slots]

    for i in range(line - 1):
        ffn_sum.b_hop(i)

    chunk = stage.shape[1]

    def to_partner(b):
        return to_peer(
            "grp",
            partner,
            stage.at[b % 3],
            theirs.at[pl.ds((b % 3) * chunk, chunk)],
            stage_send.at[b % 3],
            stage_recv.at[b % 3],
        )

    def gradient(b, left, right):
        value = t_dot(left, right[...].reshape(left.shape[0], -1)).astype(low)
        keep = core == b // 3

        @pl.when(keep)
        def _():
            mine[pl.ds((b % 3) * chunk, chunk)] = value

        @pl.when(jnp.logical_not(keep))
        def _():
            stage[b % 3] = value
            to_partner(b).start()

    total_slots = q.shape[1]
    tile = min(256, total_slots)

    def backward(m):
        dk_acc[...] = jnp.zeros_like(dk_acc)
        dv_acc[...] = jnp.zeros_like(dv_acc)

        def to_rows(target, value, start, size):
            for c in range(size // slots):
                b = start // slots + c
                target[pl.ds(pl.multiple_of(b * rows + m * slots, slots), slots)] = value[
                    c * slots : (c + 1) * slots
                ]

        for t in range(total_slots // tile):
            span = (t + 1) * tile
            at = pl.ds(t * tile, tile)
            query, grad = q[m, at], da[m, at]
            keys, values = k[m, pl.ds(0, span)], v[m, pl.ds(0, span)]
            probs = probabilities(query, keys, t * tile, lengths[m])
            dprobs = dot_t(grad, values)
            inner = jnp.sum(probs * dprobs, -1, keepdims=True)
            dscores = (probs * (dprobs - inner)).astype(low)
            dq = turn_back(dot(dscores, keys) * scale, cosine[at], sine[at])
            to_rows(dq_rows, dq.astype(low), t * tile, tile)
            dk_acc[pl.ds(0, span)] += t_dot(dscores, query)
            dv_acc[pl.ds(0, span)] += t_dot(probs.astype(low), grad)
        dk = turn_back(dk_acc[...] * scale, cosine[...], sine[...])
        to_rows(dk_rows, dk.astype(low), 0, total_slots)
        to_rows(dv_rows, dv_acc[...].astype(low), 0, total_slots)

    half = HD // 2

    def swap():
        return to_peer("shard", p.cross, halves.at[1 - p.y], half_in, half_send, half_recv)

    gradient(0, attended[:, :chunk], dbranch)
    gradient(1, attended[:, chunk:], dbranch)

    @pl.loop(0, seqs)
    def _(m):
        backward(m)
        ffn_sum.hop(m)
        ffn_sum.send_across(m + DEPTH)

    for h in range(2):
        halves[h, 0] = dk_rows[:, h * half : (h + 1) * half]
        halves[h, 1] = dv_rows[:, h * half : (h + 1) * half]
    swap().start()
    gather.drain()
    parts = dbranch
    gradient(2, dq_rows[:, :chunk], normed)
    gradient(3, dq_rows[:, chunk:], normed)

    @pl.loop(0, line)
    def _(d):
        at = pl.ds(pl.multiple_of(d * pair, pair), pair)
        part = dot(dq_rows[at], wq[...]) + dot(dk_rows[at], wkv[0]) + dot(dv_rows[at], wkv[1])
        parts[pl.ds(2 * d, 2)] = part.astype(low).reshape(2, rows, -1)

    for i in range(seqs, line - 1):
        ffn_sum.hop(i)
    reduce = Reduce(p, parts, first, scratch[17 + n :])
    swap().wait_recv()

    def summed(which):
        return (halves[p.y, which].astype(F32) + half_in[which].astype(F32)).astype(low)

    gradient(4, summed(0), normed)
    gradient(5, summed(1), normed)

    def attn_chip():
        return to_peer(
            "grp", opposite, mine, mine_in, chip_send.at[n_sums], chip_recv.at[n_sums]
        )

    for b in range(3):
        to_partner(b).wait_recv()
    total_into(mine, mine, theirs)
    attn_chip().start()
    ffn_sum.finish()
    for i in range(DEPTH):
        reduce.send_across(i)
    for i in range(line - 1):
        reduce.b_hop(i)
    valid = row_valid(p, lengths, rows)
    result = tokens[...].astype(F32) + branch[...] + ffn_own[...]
    mixed[...] = jnp.where(valid, result, jnp.zeros_like(result)).astype(low)

    def back(i):
        per_half = n_sums // 3
        start = core * per_half * part_rows + lax.rem(i, per_half) * part_rows
        at = pl.ds(pl.multiple_of(start, part_rows), part_rows)
        out = total_hbm.at[lax.div(i, per_half), at]
        return (
            pltpu.make_async_copy(sums_in.at[i], out, keep_sem.at[i]),
            to_peer("grp", partner, sums_in.at[i], out, back_send.at[i], back_recv.at[i]),
        )

    def back_attn():
        out = attn_hbm.at[pl.ds(pl.multiple_of(core * 3 * chunk, chunk), 3 * chunk)]
        return (
            pltpu.make_async_copy(mine, out, keep_sem.at[n_sums]),
            to_peer("grp", partner, mine, out, back_send.at[n_sums], back_recv.at[n_sums]),
        )

    def sum_up(first_piece, end):
        @pl.loop(first_piece, end)
        def _(i):
            either(i >= EARLY, lambda: chip_copy(i).wait())
            load_sum(i).wait()
            total_into(sums_in.at[i], sums.at[lax.rem(i, 2)], sums_in.at[i])
            either(i + 2 < n_sums, lambda: load_sum(i + 2).start())
            start_all(back(i))

    def gain_copy(step, peer, origin):
        return to_peer(
            "shard", peer, gain_held.at[peer], gain_in.at[origin], ga_send.at[step], ga_recv.at[step]
        )

    def gain_group(step, peer, origin):
        return to_peer(
            "grp", peer, gain_sum, gain_all.at[origin], gb_send.at[step], gb_recv.at[step]
        )

    def gain_first():
        def body(i, total):
            at = pl.ds(pl.multiple_of(i * 16, 16), 16)
            for b in range(count):
                total = total + parts[b, at].astype(F32) * normed[b, at].astype(F32)
            return total

        total = lax.fori_loop(0, rows // 16, body, jnp.zeros((16, parts.shape[2]), F32))
        total = jnp.sum(total, 0, keepdims=True) / gain_row(gains, 0)
        for b in range(count):
            gain_held[b, 0:1] = total[:, b * share : (b + 1) * share]
        for step in range(1, count):
            gain_copy(step, lax.rem(p.me + step, count), p.me).start()

    def gain_second():
        for step in range(1, count):
            gain_copy(step, p.me, lax.rem(p.me + count - step, count)).wait_recv()
        gain_in[p.me] = gain_held[p.me]
        total = gain_in[0]
        for b in range(1, count):
            total = total + gain_in[b]
        gain_sum[...] = total
        gain_all[rank] = total
        for step in range(1, groups):
            gain_group(step, lax.rem(rank + step, groups), rank).start()

    reduce.hop(0)
    reduce.send_across(DEPTH)
    gain_first()
    sum_up(0, n_sums // 2)
    reduce.hop(1)
    reduce.send_across(DEPTH + 1)
    gain_second()
    sum_up(n_sums // 2, n_sums - 3)
    reduce.hop(2)
    sum_up(n_sums - 3, n_sums)
    reduce.finish()
    for step in range(1, groups):
        gain_group(step, rank, lax.rem(rank + groups - step, groups)).wait_recv()
    total = gain_all[0]
    for b in range(1, groups):
        total = total + gain_all[b]
    gain_out[...] = total
    source = tokens[...].astype(F32)
    inner = norm_grad(source, inverse_rms(source), gain_row(gains, 0), first[...])
    input_grad[...] = (middle_grad[...] + inner).astype(low)
    attn_chip().wait()
    total_into(mine, mine, mine_in)
    start_all(back_attn())
    reduce.drain()
    ffn_sum.drain()
    swap().wait_send()
    for b in range(3):
        to_partner(b).wait_send()
    for step in range(1, count):
        gain_copy(step, lax.rem(p.me + step, count), p.me).wait_send()
    for step in range(1, groups):
        gain_group(step, lax.rem(rank + step, groups), rank).wait_send()

    @pl.loop(0, n_sums)
    def _(i):
        wait_all(back(i))

    wait_all(back_attn())


def attention_grad(
    lengths, tokens, branch, cot, second, gains, cosine, sine, ffn_parts, normed, attended, q, k, v, wq, wkv, wo, sums, early,
    groups, ident,
):
    rows, width = tokens.shape
    count = normed.shape[0]
    line = count // 2
    seqs, total_slots, hd = q.shape
    low = tokens.dtype
    vmem = pltpu.VMEM
    tall = count * rows
    half = hd // 2
    sums = sums.reshape(-1, PIECE, width)
    early = early.reshape(-1, PIECE, width)
    n_sums, part_rows, _ = sums.shape
    shape = jax.ShapeDtypeStruct
    big = vmem((count, rows, width), low)
    head = vmem((seqs, total_slots, hd), low)
    weight = vmem((hd, width), low)
    flat = vmem((tall, hd), low)
    acc = vmem((total_slots, hd), F32)
    third = vmem((3 * half, width), low)
    g = gains.shape
    block = vmem((rows, width), F32)
    return pl.pallas_call(
        functools.partial(attention_grad_kernel, line, groups, seqs),
        out_shape=(
            shape((rows, width), low),
            shape((rows, width), low),
            shape(g[1:], F32),
            shape((3, n_sums // 3 * 2 * part_rows, width), low),
            shape((6 * half, width), low),
        ),
        in_specs=[scalars()] + [vm()] * 7 + [hbm()] * 11,
        out_specs=(vm(), vm(), vm(), hbm(), hbm()),
        scratch_shapes=[
            vmem((rows, width), low), block, block, block,
            big, big, flat, head, head, head, weight, vmem((2, hd, width), low), weight, head, acc, acc,
            flat, flat, flat,
            vmem((2, 2, tall, half), low), vmem((2, tall, half), low), big,
            vmem((2,) + sums.shape[1:], low), vmem(sums.shape, low), vmem((3, half, width), low), third, third, third,
            vmem(g, F32), vmem(g, F32), vmem(g[1:], F32), vmem((groups,) + g[1:], F32),
        ]
        + gather_sems(count)
        + [
            DMA((12,)), DMA((n_sums + 1,)), DMA((n_sums + 1,)), DMA, DMA, DMA((3,)), DMA((3,)),
            DMA((n_sums + 1,)), DMA((n_sums + 1,)), DMA((n_sums + 1,)),
            DMA((count,)), DMA((count,)), DMA((groups,)), DMA((groups,)),
        ]
        + Reduce.scratch(line, rows, width, low) * 2,
        compiler_params=params(ident),
        name="attention_grad",
    )(
        lengths, tokens, branch, cot, second, gains, cosine, sine, ffn_parts, normed, attended, q, k, v, wq, wkv, wo, sums, early
    )


epsilon = 1e-06
theta_base = 1000042.0
masked_value = -1e30


def turned(source):
    half_width = source.shape[-1] // 2
    return jnp.concatenate([-source[..., half_width:], source[..., :half_width]], -1)


def rotate(source, cosine_table, sine_table):
    return source * cosine_table + turned(source) * sine_table


def unrotate(source, cosine_table, sine_table):
    return source * cosine_table - turned(source) * sine_table


def norm_forward(source, norm_gain):
    inverse = lax.rsqrt(jnp.mean(source * source, -1, keepdims=True) + epsilon)
    return (source * inverse * norm_gain, inverse)


def norm_backward(source, inverse, norm_gain, grad_out):
    weighted = grad_out * norm_gain
    inner_sum = jnp.sum(weighted * source, -1, keepdims=True)
    grad_in = (
        inverse * weighted - source * inverse * inverse * inverse * inner_sum / source.shape[-1]
    )
    return (grad_in, jnp.sum(grad_out * source * inverse, 0))


def weight_terms(normed, query_grad, key_grad, value_grad, attended, branch_grad, shard_count):
    token_count, model_width = normed.shape
    query_share = query_grad.shape[1] // shard_count
    kv_share = key_grad.shape[1] // shard_count
    shard_rows = 2 * query_share + 2 * kv_share

    def weight_term(first_row, row_count):
        blocks = row_count // shard_rows

        def columns(matrix, share_cols):
            return matrix.reshape(token_count, blocks, share_cols)

        part_query = jnp.einsum(
            "tmr,td->mrd",
            columns(query_grad, query_share),
            normed,
            preferred_element_type=jnp.float32,
        )
        part_key = jnp.einsum(
            "tmr,td->mrd", columns(key_grad, kv_share), normed, preferred_element_type=jnp.float32
        )
        part_value = jnp.einsum(
            "tmr,td->mrd", columns(value_grad, kv_share), normed, preferred_element_type=jnp.float32
        )
        part_out = jnp.einsum(
            "tmr,td->mrd",
            columns(attended, query_share),
            branch_grad,
            preferred_element_type=jnp.float32,
        )
        return jnp.concatenate([part_query, part_key, part_value, part_out], 1).reshape(
            row_count, model_width
        )

    return (weight_term, shard_rows)


def local_rows(
    tokens,
    lengths,
    prenorm_gain,
    query_weight,
    key_weight,
    value_weight,
    out_weight,
    midnorm_gain,
    gate_weight,
    up_weight,
    down_weight,
    cotangent,
):
    shard_count = lax.axis_size("shard")
    shard_rank = lax.axis_index("shard")
    micro_count, seq_dev, model_width = tokens.shape
    slot_count = seq_dev * shard_count
    repeat_heads = NH // KVH
    query_width = NH * HD
    kv_width = KVH * HD
    score_scale = 1.0 / math.sqrt(HD)
    local_pos = shard_rank * seq_dev + jnp.arange(seq_dev, dtype=jnp.int32)
    key_pos = jnp.arange(slot_count, dtype=jnp.int32)
    inverse_freq = theta_base ** (-(jnp.arange(0, HD, 2).astype(jnp.float32) / HD))
    angles = local_pos.astype(jnp.float32)[:, None] * inverse_freq[None, :]
    cosine_table = jnp.concatenate([jnp.cos(angles), jnp.cos(angles)], -1)[:, None, :]
    sine_table = jnp.concatenate([jnp.sin(angles), jnp.sin(angles)], -1)[:, None, :]
    gate_total = jnp.zeros(gate_weight.shape, jnp.float32)
    up_total = jnp.zeros(up_weight.shape, jnp.float32)
    down_total = jnp.zeros(down_weight.shape, jnp.float32)
    prenorm_total = jnp.zeros((model_width,), jnp.float32)
    midnorm_total = jnp.zeros((model_width,), jnp.float32)
    attn_total = None
    mixed_rows = []
    input_rows = []
    for micro_index in range(micro_count):
        gathered = (
            lax.all_gather(query_weight, "shard", axis=0, tiled=True),
            lax.all_gather(key_weight, "shard", axis=0, tiled=True),
            lax.all_gather(value_weight, "shard", axis=0, tiled=True),
            lax.all_gather(prenorm_gain, "shard", axis=0, tiled=True),
            lax.all_gather(midnorm_gain, "shard", axis=0, tiled=True),
        )
        query_full, key_full, value_full, prenorm_full, midnorm_full = gathered
        prenorm_f = prenorm_full.astype(jnp.float32)
        midnorm_f = midnorm_full.astype(jnp.float32)
        source = tokens[micro_index].astype(jnp.float32)
        length_now = lengths[micro_index]
        valid_rows = local_pos < length_now
        scaled_first, inverse_first = norm_forward(source, prenorm_f)
        normed_first = scaled_first.astype(jnp.bfloat16)
        query_pre = jnp.einsum(
            "sd,qd->sq", normed_first, query_full, preferred_element_type=jnp.float32
        ).reshape(seq_dev, NH, HD)
        key_pre = jnp.einsum(
            "sd,qd->sq", normed_first, key_full, preferred_element_type=jnp.float32
        ).reshape(seq_dev, KVH, HD)
        value_pre = jnp.einsum(
            "sd,qd->sq", normed_first, value_full, preferred_element_type=jnp.float32
        )
        query_rot = rotate(query_pre, cosine_table, sine_table).astype(jnp.bfloat16)
        key_rot = rotate(key_pre, cosine_table, sine_table).astype(jnp.bfloat16)
        key_value = jnp.concatenate(
            [key_rot.reshape(seq_dev, kv_width), value_pre.astype(jnp.bfloat16)], 1
        )
        kv_all = lax.all_gather(key_value, "shard", axis=0, tiled=True)
        keys_all = kv_all[:, :kv_width].reshape(slot_count, KVH, HD)
        values_all = kv_all[:, kv_width:].reshape(slot_count, KVH, HD)
        query_group = query_rot.reshape(seq_dev, KVH, repeat_heads, HD)
        scores = (
            jnp.einsum("skrd,tkd->krst", query_group, keys_all, preferred_element_type=jnp.float32)
            * score_scale
        )
        allowed = (key_pos[None, :] <= local_pos[:, None]) & (key_pos[None, :] < length_now)
        scores = jnp.where(allowed, scores, masked_value)
        row_max = jnp.max(scores, -1, keepdims=True)
        exp_scores = jnp.exp(scores - row_max)
        attention_probs = exp_scores / jnp.sum(exp_scores, -1, keepdims=True)
        probs_low = attention_probs.astype(jnp.bfloat16)
        attended = (
            jnp.einsum("krst,tkd->skrd", probs_low, values_all, preferred_element_type=jnp.float32)
            .astype(jnp.bfloat16)
            .reshape(seq_dev, query_width)
        )
        branch = jnp.dot(
            attended,
            lax.all_gather(out_weight, "shard", axis=0, tiled=True),
            preferred_element_type=jnp.float32,
        )
        middle = source + branch
        scaled_second, inverse_second = norm_forward(middle, midnorm_f)
        normed_second = scaled_second.astype(jnp.bfloat16)
        normed_all = lax.all_gather(normed_second, "shard", axis=0, tiled=True)
        gate_pre = jnp.einsum(
            "sd,fd->sf", normed_all, gate_weight, preferred_element_type=jnp.float32
        )
        up_pre = jnp.einsum("sd,fd->sf", normed_all, up_weight, preferred_element_type=jnp.float32)
        sigmoid_gate = jax.nn.sigmoid(gate_pre)
        silu_gate = gate_pre * sigmoid_gate
        hidden = (silu_gate * up_pre).astype(jnp.bfloat16)
        ffn_part = lax.psum_scatter(
            jnp.dot(hidden, down_weight, preferred_element_type=jnp.float32).astype(jnp.bfloat16),
            "shard",
            scatter_dimension=0,
            tiled=True,
        ).astype(jnp.float32)
        mixed_rows.append(
            jnp.where(valid_rows[:, None], middle + ffn_part, 0.0).astype(jnp.bfloat16)
        )
        cot_low = jnp.where(
            valid_rows[:, None], cotangent[micro_index], jnp.zeros_like(cotangent[micro_index])
        )
        cot_all = lax.all_gather(cot_low, "shard", axis=0, tiled=True)
        hidden_grad = jnp.einsum(
            "sd,fd->sf", cot_all, down_weight, preferred_element_type=jnp.float32
        )
        down_total = down_total + jnp.einsum(
            "sf,sd->fd", hidden, cot_all, preferred_element_type=jnp.float32
        )
        gate_grad = (
            hidden_grad * up_pre * sigmoid_gate * (1.0 + gate_pre * (1.0 - sigmoid_gate))
        ).astype(jnp.bfloat16)
        up_grad = (hidden_grad * silu_gate).astype(jnp.bfloat16)
        gate_total = gate_total + jnp.einsum(
            "sf,sd->fd", gate_grad, normed_all, preferred_element_type=jnp.float32
        )
        up_total = up_total + jnp.einsum(
            "sf,sd->fd", up_grad, normed_all, preferred_element_type=jnp.float32
        )
        second_grad = lax.psum_scatter(
            jnp.dot(gate_grad, gate_weight, preferred_element_type=jnp.float32)
            + jnp.dot(up_grad, up_weight, preferred_element_type=jnp.float32),
            "shard",
            scatter_dimension=0,
            tiled=True,
        )
        middle_part, midnorm_part = norm_backward(middle, inverse_second, midnorm_f, second_grad)
        middle_grad = cot_low.astype(jnp.float32) + middle_part
        midnorm_total = midnorm_total + midnorm_part
        branch_grad = middle_grad.astype(jnp.bfloat16)
        attended_grad = jnp.einsum(
            "sd,qd->sq",
            branch_grad,
            lax.all_gather(out_weight, "shard", axis=0, tiled=True),
            preferred_element_type=jnp.float32,
        ).astype(jnp.bfloat16)
        attended_group = attended_grad.reshape(seq_dev, KVH, repeat_heads, HD)
        probs_grad = jnp.einsum(
            "skrd,tkd->krst", attended_group, values_all, preferred_element_type=jnp.float32
        )
        inner_sum = jnp.sum(attention_probs * probs_grad, -1, keepdims=True)
        scores_grad = (attention_probs * (probs_grad - inner_sum)).astype(jnp.bfloat16)
        query_rot_grad = (
            jnp.einsum(
                "krst,tkd->skrd", scores_grad, keys_all, preferred_element_type=jnp.float32
            ).reshape(seq_dev, NH, HD)
            * score_scale
        )
        query_grad = (
            unrotate(query_rot_grad, cosine_table, sine_table)
            .astype(jnp.bfloat16)
            .reshape(seq_dev, query_width)
        )
        row_count = lax.axis_size("shard") * seq_dev
        key_part = (
            jnp.einsum(
                "krst,skrd->tkd", scores_grad, query_group, preferred_element_type=jnp.float32
            )
            * score_scale
        )
        value_part = jnp.einsum(
            "krst,skrd->tkd", probs_low, attended_group, preferred_element_type=jnp.float32
        )
        kv_grad = lax.psum_scatter(
            jnp.concatenate(
                [key_part.reshape(row_count, kv_width), value_part.reshape(row_count, kv_width)], 1
            ).astype(jnp.bfloat16),
            "shard",
            scatter_dimension=0,
            tiled=True,
        ).astype(jnp.float32)
        key_grad = (
            unrotate(kv_grad[:, :kv_width].reshape(seq_dev, KVH, HD), cosine_table, sine_table)
            .astype(jnp.bfloat16)
            .reshape(seq_dev, kv_width)
        )
        value_grad = kv_grad[:, kv_width:].astype(jnp.bfloat16)
        first_grad = jnp.einsum(
            "sq,qd->sd", query_grad, query_full, preferred_element_type=jnp.float32
        )
        first_grad = first_grad + jnp.einsum(
            "sq,qd->sd", key_grad, key_full, preferred_element_type=jnp.float32
        )
        first_grad = first_grad + jnp.einsum(
            "sq,qd->sd", value_grad, value_full, preferred_element_type=jnp.float32
        )
        source_part, prenorm_part = norm_backward(source, inverse_first, prenorm_f, first_grad)
        input_rows.append((middle_grad + source_part).astype(jnp.bfloat16))
        prenorm_total = prenorm_total + prenorm_part
        saved = (normed_first, query_grad, key_grad, value_grad, attended, branch_grad)
        weight_term, shard_rows = weight_terms(*saved, shard_count)
        reduced = lax.psum_scatter(
            weight_term(jnp.int32(0), lax.axis_size("shard") * shard_rows).astype(jnp.bfloat16),
            "shard",
            scatter_dimension=0,
            tiled=True,
        ).astype(jnp.float32)
        attn_total = reduced if attn_total is None else attn_total + reduced
    gain_sums = lax.psum((prenorm_total, midnorm_total), ("grp", "shard"))
    gain_share = model_width // shard_count
    prenorm_gradient = lax.dynamic_slice_in_dim(
        gain_sums[0], shard_rank * gain_share, gain_share, 0
    )
    midnorm_gradient = lax.dynamic_slice_in_dim(
        gain_sums[1], shard_rank * gain_share, gain_share, 0
    )
    summed = (
        lax.psum(attn_total.astype(jnp.bfloat16), "grp").astype(jnp.float32),
        lax.psum(gate_total.astype(jnp.bfloat16), "grp").astype(jnp.float32),
        lax.psum(up_total.astype(jnp.bfloat16), "grp").astype(jnp.float32),
        lax.psum(down_total.astype(jnp.bfloat16), "grp").astype(jnp.float32),
    )
    attn_rows = summed[0]
    query_share = query_width // shard_count
    kv_share = kv_width // shard_count
    query_gradient = attn_rows[:query_share]
    key_gradient = attn_rows[query_share : query_share + kv_share]
    value_gradient = attn_rows[query_share + kv_share : query_share + 2 * kv_share]
    out_gradient = attn_rows[query_share + 2 * kv_share :]
    return (
        jnp.stack(mixed_rows),
        jnp.stack(input_rows),
        prenorm_gradient,
        query_gradient,
        key_gradient,
        value_gradient,
        out_gradient,
        midnorm_gradient,
        summed[1],
        summed[2],
        summed[3],
    )


def local_heads(
    tokens,
    lengths,
    prenorm_gain,
    query_weight,
    key_weight,
    value_weight,
    out_weight,
    midnorm_gain,
    gate_weight,
    up_weight,
    down_weight,
    cotangent,
):
    low = jnp.bfloat16
    count = lax.axis_size("shard")
    groups = lax.axis_size("grp")
    seqs, seq_dev, model_width = tokens.shape
    rows = seqs * seq_dev
    inverse_freq = theta_base ** (-(jnp.arange(0, HD, 2).astype(jnp.float32) / HD))
    tokens_low = tokens.reshape(rows, model_width)
    cot_low = cotangent.reshape(rows, model_width)
    branch, gains, normed_first, cot_all, queries, keys, values, attended, kv_head, cosine, sine = (
        attention(
            lengths,
            tokens_low,
            cot_low,
            prenorm_gain[None, :],
            midnorm_gain[None, :],
            inverse_freq[None, :],
            query_weight,
            key_weight,
            value_weight,
            out_weight,
            count,
            groups,
            1,
        )
    )
    second_grad, ffn_parts, pair_sums, early = ffn(
        tokens_low, branch, gains, cot_all, gate_weight, up_weight, down_weight, groups, 2
    )
    mixed, input_gradient, gain_own, totals, attn_total = attention_grad(
        lengths,
        tokens_low,
        branch,
        cot_low,
        second_grad,
        gains,
        cosine,
        sine,
        ffn_parts,
        normed_first,
        attended,
        queries,
        keys,
        values,
        query_weight,
        kv_head,
        out_weight,
        pair_sums,
        early,
        groups,
        3,
    )
    head = query_weight.shape[0]
    kv_share = key_weight.shape[0]
    f32 = jnp.float32
    return (
        mixed.reshape(tokens.shape),
        input_gradient.reshape(tokens.shape),
        gain_own[0],
        attn_total[head : 2 * head].astype(f32),
        attn_total[2 * head : 2 * head + kv_share].astype(f32),
        attn_total[2 * head + kv_share :].astype(f32),
        attn_total[:head].astype(f32),
        gain_own[1],
        totals[1].astype(f32),
        totals[2].astype(f32),
        totals[0].astype(f32),
    )


def solution(mesh):
    planes = mesh.shape["shard"] == NH and mesh.shape["grp"] == 4
    local = local_heads if planes else local_rows
    in_specs = (
        P("grp", "shard", None),
        P("grp"),
        P("shard"),
        P("shard", None),
        P("shard", None),
        P("shard", None),
        P("shard", None),
        P("shard"),
        P("shard", None),
        P("shard", None),
        P("shard", None),
        P("grp", "shard", None),
    )
    out_specs = (
        P("grp", "shard", None),
        P("grp", "shard", None),
        P("shard"),
        P("shard", None),
        P("shard", None),
        P("shard", None),
        P("shard", None),
        P("shard"),
        P("shard", None),
        P("shard", None),
        P("shard", None),
    )
    return jax.shard_map(local, mesh=mesh, in_specs=in_specs, out_specs=out_specs, check_vma=False)
```

```python
import functools
import math

import jax
import jax.numpy as jnp
from jax import lax
from jax.experimental import pallas as pl
from jax.experimental.pallas import tpu as pltpu
from jax.sharding import PartitionSpec as P

NH = 8
KVH = 4
HD = 256
MASKED = -1e30
EPSILON = 1e-06
DEPTH = 2
MESH = pl.DeviceIdType.MESH
F32 = jnp.float32
DMA = pltpu.SemaphoreType.DMA
REST = 16
PIECE = 128
EARLY = 3
CHUNKS = 2


def pieces(rows):
    size = -(-(rows - REST) // (16 * CHUNKS)) * 16
    cuts = [min(i * size, rows - REST) for i in range(CHUNKS + 1)] + [rows]
    return [pl.ds(a, b - a) for a, b in zip(cuts, cuts[1:])]


VMEM_LIMIT = 66_000_000


def either(condition, action):
    pl.when(condition)(action)


def total_into(dst, *srcs):
    step = 16

    @pl.loop(0, dst.shape[0] // step)
    def _(i):
        at = pl.ds(pl.multiple_of(i * step, step), step)
        value = srcs[0][at].astype(F32)
        for src in srcs[1:]:
            value = value + src[at].astype(F32)
        dst[at] = value.astype(dst.dtype)


class Place:
    def __init__(self, line):
        self.line = line
        self.me = lax.axis_index("shard")
        self.z = self.me // 2
        self.y = lax.rem(self.me, 2)
        self.cross = self.me + 1 - 2 * self.y
        self.low_end = self.z == 0
        self.high_end = self.z == line - 1
        near = []
        for z in range(line):
            order = [z]
            for k in range(1, line):
                order += [d for d in (z - k, z + k) if 0 <= d < line]
            near.append(order)
        self.tables = near

    def near(self, i):
        out = jnp.int32(0)
        for z in range(self.line):
            row = jnp.int32(self.tables[z][0])
            for k in range(1, self.line):
                row = jnp.where(i == k, self.tables[z][k], row)
            out = jnp.where(self.z == z, row, out)
        return out

    def far(self, i):
        return self.near(self.line - 1 - i)

    def greet(self, groups):
        barrier = pltpu.get_barrier_semaphore()
        count = 2 * self.line
        rank = lax.axis_index("grp")
        for step in range(1, count):
            pl.semaphore_signal(
                barrier,
                inc=1,
                device_id={"shard": lax.rem(self.me + step, count)},
                device_id_type=MESH,
            )
        for step in range(1, groups):
            pl.semaphore_signal(
                barrier,
                inc=1,
                device_id={"grp": lax.rem(rank + step, groups)},
                device_id_type=MESH,
            )
        pl.semaphore_wait(barrier, count + groups - 2)


class Gather:
    UP, DOWN, CROSS = 0, 1, 2

    def __init__(self, place, own, out, local_sem, send_sem, recv_sem):
        self.p, self.own, self.out = place, own, out
        self.local_sem, self.send_sem, self.recv_sem = local_sem, send_sem, recv_sem
        self.pieces = pieces(own.shape[0])
        self.last = len(self.pieces) - 1

    def copy(self, way, origin, part, own=False):
        p = self.p
        peer = (p.me + 2, p.me - 2, p.cross)[way]
        at = self.pieces[part]
        return pltpu.make_async_remote_copy(
            src_ref=self.own.at[at] if own else self.out.at[origin, at],
            dst_ref=self.out.at[origin, at],
            send_sem=self.send_sem.at[way, origin, part],
            recv_sem=self.recv_sem.at[origin, part],
            device_id={"shard": peer},
            device_id_type=MESH,
        )

    def arrived(self, origin, part):
        self.copy(self.CROSS, origin, part).wait_recv()

    def start(self):
        self.send_own()
        self.pass_rest()

    def send_own(self):
        p = self.p
        pltpu.make_async_copy(self.own, self.out.at[p.me], self.local_sem).start()
        for part in (self.last,) + tuple(range(self.last)):
            self.copy(self.CROSS, p.me, part, True).start()
        for part in range(self.last + 1):
            either(p.z < p.line - 1, lambda: self.copy(self.UP, p.me, part, True).start())
            either(p.z > 0, lambda: self.copy(self.DOWN, p.me, part, True).start())

    def pass_rest(self):
        p = self.p
        self.arrived(p.cross, self.last)
        either(p.z < p.line - 1, lambda: self.copy(self.UP, p.cross, self.last).start())
        either(p.z > 0, lambda: self.copy(self.DOWN, p.cross, self.last).start())
        pltpu.make_async_copy(self.own, self.out.at[p.me], self.local_sem).wait()

    def hop(self, k):
        p = self.p
        below, above = p.me - 2 * k, p.me + 2 * k
        has_below, has_above = p.z - k >= 0, p.z + k < p.line

        def first(origin, part, way, more):
            self.arrived(origin, part)
            self.copy(self.CROSS, origin, part).start()
            either(more, lambda: self.copy(way, origin, part).start())

        def last(origin, other, way, more):
            for block in (origin, other):
                self.arrived(block, self.last)
                either(more, lambda: self.copy(way, block, self.last).start())

        for part in range(self.last):
            either(has_below, lambda: first(below, part, self.UP, p.z < p.line - 1))
            either(has_above, lambda: first(above, part, self.DOWN, p.z > 0))
        either(has_below, lambda: last(below, p.cross - 2 * k, self.UP, p.z < p.line - 1))
        either(has_above, lambda: last(above, p.cross + 2 * k, self.DOWN, p.z > 0))

    def whole(self, position):
        for part in range(self.last):
            self.arrived(2 * position + 1 - self.p.y, part)

    def drain(self):
        p = self.p

        @pl.loop(0, p.line)
        def _(d):
            mine, other = 2 * d + p.y, 2 * d + 1 - p.y
            for part in range(self.last):
                self.copy(self.CROSS, mine, part).wait_send()

            @pl.when(d == p.z)
            def _():
                self.copy(self.CROSS, mine, self.last).wait_send()

            def line_sent(way):
                for part in range(self.last + 1):
                    self.copy(way, mine, part).wait_send()
                self.copy(way, other, self.last).wait_send()

            either((d <= p.z) & (p.z < p.line - 1), lambda: line_sent(self.UP))
            either((d >= p.z) & (p.z > 0), lambda: line_sent(self.DOWN))


class Reduce:
    BUP, BDN, BX = 0, 2, 4
    UP, DOWN, CROSS = 5, 5 + CHUNKS, 5 + 2 * CHUNKS
    WAYS = 5 + 3 * CHUNKS
    N_SCRATCH = 9

    @staticmethod
    def scratch(line, rows, width, dtype):
        v = pltpu.VMEM
        return (
            [v((line, rows - REST, width), dtype)] * 3
            + [v((line, 2, REST, width), dtype)] * 2
            + [v((REST, width), dtype)] * 2
            + [DMA((Reduce.WAYS, line)), DMA((Reduce.WAYS, line))]
        )

    def __init__(self, place, parts, out, scratch):
        self.p, self.parts, self.out = place, parts, out
        self.cross_in, self.up_in, self.down_in, self.bup_in, self.bdn_in = scratch[:5]
        self.bx_out, self.bx_in, self.send_sem, self.recv_sem = scratch[5:]
        self.pieces = pieces(parts.shape[1])
        self.b = self.pieces[-1]

    def desc(self, way, slot, src, dst, peer):
        return pltpu.make_async_remote_copy(
            src_ref=src,
            dst_ref=dst,
            send_sem=self.send_sem.at[way, slot],
            recv_sem=self.recv_sem.at[way, slot],
            device_id={"shard": peer},
            device_id_type=MESH,
        )

    def cross_copy(self, d, c):
        p, at = self.p, self.pieces[c]
        return self.desc(
            self.CROSS + c,
            d,
            self.parts.at[2 * d + 1 - p.y, at],
            self.cross_in.at[d, at],
            p.cross,
        )

    def line_copy(self, up, d, c):
        p, at = self.p, self.pieces[c]
        came = self.up_in if up else self.down_in
        return self.desc(
            (self.UP if up else self.DOWN) + c,
            d,
            self.cross_in.at[d, at],
            came.at[d, at],
            p.me + 2 if up else p.me - 2,
        )

    def b_copy(self, up, d, o, src=None):
        p = self.p
        held = self.bup_in if up else self.bdn_in
        return self.desc(
            (self.BUP if up else self.BDN) + o,
            d,
            held.at[d, o] if src is None else src,
            held.at[d, o],
            p.me + 2 if up else p.me - 2,
        )

    def bx_copy(self):
        return self.desc(self.BX, 0, self.bx_out, self.bx_in, self.p.cross)

    def column(self, o):
        return self.p.y if o == 0 else 1 - self.p.y

    def send_across(self, i):
        for c in range(CHUNKS):
            self.cross_copy(self.p.far(i), c).start()

    def b_hop(self, i):
        p = self.p
        d = p.far(i)

        def go(up):
            first = p.low_end if up else p.high_end
            held = self.bup_in if up else self.bdn_in
            for o in (1, 0):
                mine = self.parts.at[2 * d + self.column(o), self.b]
                either(first, lambda: self.b_copy(up, d, o, mine).start())

                @pl.when(jnp.logical_not(first))
                def _():
                    self.b_copy(up, d, o).wait_recv()
                    total_into(held.at[d, o], mine, held.at[d, o])
                    self.b_copy(up, d, o).start()

        either(d > p.z, lambda: go(True))
        either(d < p.z, lambda: go(False))

    def hop(self, i):
        p = self.p
        d = p.far(i)
        for c in range(CHUNKS):
            self.cross_copy(d, c).wait_recv()
            at = self.pieces[c]
            mine = self.parts.at[2 * d + p.y, at]
            held = self.cross_in.at[d, at]

            def go(up):
                first = p.low_end if up else p.high_end
                came = self.up_in if up else self.down_in
                either(first, lambda: total_into(held, mine, held))

                @pl.when(jnp.logical_not(first))
                def _():
                    self.line_copy(up, d, c).wait_recv()
                    total_into(held, mine, held, came.at[d, at])

                self.line_copy(up, d, c).start()

            either(d > p.z, lambda: go(True))
            either(d < p.z, lambda: go(False))

    def close(self, dst, mine, ups, downs):
        p = self.p
        either(p.low_end, lambda: total_into(dst, *mine, downs))
        either(p.high_end, lambda: total_into(dst, *mine, ups))
        either(
            jnp.logical_not(p.low_end | p.high_end), lambda: total_into(dst, *mine, ups, downs)
        )

    def finish(self):
        p = self.p
        for o in (1, 0):
            either(jnp.logical_not(p.low_end), lambda: self.b_copy(True, p.z, o).wait_recv())
            either(jnp.logical_not(p.high_end), lambda: self.b_copy(False, p.z, o).wait_recv())
            if o:
                mine = self.parts.at[2 * p.z + self.column(o), self.b]
                self.close(self.bx_out, (mine,), self.bup_in.at[p.z, o], self.bdn_in.at[p.z, o])
                self.bx_copy().start()
        self.bx_copy().wait_recv()
        self.close(
            self.out.at[self.b],
            (self.parts.at[p.me, self.b], self.bx_in),
            self.bup_in.at[p.z, 0],
            self.bdn_in.at[p.z, 0],
        )
        for c in range(CHUNKS):
            self.cross_copy(p.z, c).wait_recv()
            either(jnp.logical_not(p.low_end), lambda: self.line_copy(True, p.z, c).wait_recv())
            either(jnp.logical_not(p.high_end), lambda: self.line_copy(False, p.z, c).wait_recv())
            at = self.pieces[c]
            self.close(
                self.out.at[at],
                (self.parts.at[p.me, at], self.cross_in.at[p.z, at]),
                self.up_in.at[p.z, at],
                self.down_in.at[p.z, at],
            )

    def drain(self):
        p = self.p
        self.bx_copy().wait_send()

        @pl.loop(0, p.line)
        def _(d):
            def line_sent(up):
                for c in range(CHUNKS):
                    self.line_copy(up, d, c).wait_send()
                self.b_copy(up, d, 0).wait_send()
                self.b_copy(up, d, 1).wait_send()

            for c in range(CHUNKS):
                self.cross_copy(d, c).wait_send()
            either(d > p.z, lambda: line_sent(True))
            either(d < p.z, lambda: line_sent(False))


def dot(a, b):
    return jnp.dot(a, b, preferred_element_type=F32)


def dot_t(a, b):
    return lax.dot_general(a, b, (((1,), (1,)), ((), ())), preferred_element_type=F32)


def t_dot(a, b):
    return lax.dot_general(a, b, (((0,), (0,)), ((), ())), preferred_element_type=F32)


def to_peer(axis, peer, src, dst, send_sem, recv_sem):
    return pltpu.make_async_remote_copy(
        src_ref=src,
        dst_ref=dst,
        send_sem=send_sem,
        recv_sem=recv_sem,
        device_id={axis: peer},
        device_id_type=MESH,
    )


def turn_by(v, cosine, sine):
    half = v.shape[-1] // 2
    a, b = v[:, :half], v[:, half:]
    return jnp.concatenate([a * cosine - b * sine, b * cosine + a * sine], -1)


def turn_back(v, cosine, sine):
    return turn_by(v, cosine, -sine)


def probabilities(query, keys, rows_from, limit):
    scores = dot_t(query, keys) * (1.0 / math.sqrt(HD))
    row = lax.broadcasted_iota(jnp.int32, scores.shape, 0) + rows_from
    col = lax.broadcasted_iota(jnp.int32, scores.shape, 1)
    scores = jnp.where((col <= row) & (col < limit), scores, MASKED)
    weight = jnp.exp(scores - jnp.max(scores, -1, keepdims=True))
    return weight / jnp.sum(weight, -1, keepdims=True)


def row_valid(place, lengths, rows):
    slots = rows // lengths.shape[0]
    row = lax.broadcasted_iota(jnp.int32, (rows, 1), 0)
    limit = jnp.full((rows, 1), lengths[0], jnp.int32)
    for n in range(1, lengths.shape[0]):
        limit = jnp.where(row >= n * slots, lengths[n], limit)
    return place.me * slots + lax.rem(row, slots) < limit


def gain_row(shares, which):
    return jnp.concatenate([shares[b, which : which + 1] for b in range(shares.shape[0])], 1)


def inverse_rms(x):
    return lax.rsqrt(jnp.mean(x * x, -1, keepdims=True) + EPSILON)


def norm_grad(x, inverse, gain, grad):
    weighted = grad * gain
    inner = jnp.sum(weighted * x, -1, keepdims=True)
    return inverse * weighted - x * inverse * inverse * inverse * inner / x.shape[-1]


def start_all(copies):
    for c in copies:
        c.start()


def wait_all(copies):
    for c in copies:
        c.wait()


def scalars():
    return pl.BlockSpec(memory_space=pltpu.SMEM)


def hbm():
    return pl.BlockSpec(memory_space=pl.ANY)


def vm():
    return pl.BlockSpec(memory_space=pltpu.VMEM)


def params(ident):
    return pltpu.CompilerParams(
        collective_id=ident, has_side_effects=True, vmem_limit_bytes=VMEM_LIMIT
    )


def gather_sems(count):
    return [DMA, DMA((3, count, CHUNKS + 1)), DMA((count, CHUNKS + 1))]


def attention_kernel(
    line, groups, seqs,
    lengths, own, cot_raw, pre_gain, mid_gain, freq, wq_hbm, wk_hbm, wv_hbm, wo_hbm,
    branch, small_out, normed_hbm, cot_hbm, q_hbm, k_hbm, v_hbm, attended_hbm, wkv_hbm, cos_hbm, sin_hbm,
    small, cot_own, rows_all, normed, cot_all, q, k, v, attended, wq, wkv, wo, cosine, sine, parts,
    *scratch,
):
    p = Place(line)
    count = 2 * line
    rank = lax.axis_index("grp")
    g1, g2 = scratch[:3], scratch[3:6]
    (load_sem, small_send, small_recv, wy_send, wg_send, w_recv, save_sem) = scratch[6:13]
    r_scratch = scratch[13:]
    half = wk_hbm.shape[0]
    piece = half // 2
    at_own = pl.ds(pl.multiple_of(p.y * half, half), half)
    loads = [
        pltpu.make_async_copy(src, dst, load_sem.at[i])
        for i, (src, dst) in enumerate(
            (
                (wk_hbm, wkv.at[0, at_own]),
                (wv_hbm, wkv.at[1, at_own]),
                (wq_hbm, wq),
                (wo_hbm, wo),
            )
        )
    ]
    start_all(loads)
    p.greet(groups)

    small[...] = jnp.zeros_like(small)
    small[0:1] = pre_gain[...].astype(F32)
    small[1:2] = mid_gain[...].astype(F32)

    def small_copy(step, peer, origin):
        return to_peer(
            "shard", peer, small, small_out.at[origin], small_send.at[step], small_recv.at[step]
        )

    for step in range(1, count):
        small_copy(step, lax.rem(p.me + step, count), p.me).start()
    gather = Gather(p, own, rows_all, *g1)
    gather.start()
    cots = Gather(p, cot_own, cot_all, *g2)
    small_out[p.me] = small[...]

    def rows_of(quarter, column):
        return wkv.at[
            quarter // 2,
            pl.ds(pl.multiple_of(column * half + lax.rem(quarter, 2) * piece, piece), piece),
        ]

    def across():
        ref = rows_of(rank, p.y)
        return to_peer("shard", p.cross, ref, ref, wy_send, w_recv.at[rank])

    def share(step):
        ref = rows_of(rank, 1 - p.y)
        return to_peer(
            "grp", lax.rem(rank + step, groups), ref, ref, wg_send.at[step], w_recv.at[rank]
        )

    wait_all(loads)
    across().start()
    pos = lax.broadcasted_iota(jnp.int32, cosine.shape, 0).astype(F32)
    angle = pos * freq[...]
    cosine[...] = jnp.cos(angle)
    sine[...] = jnp.sin(angle)
    cot = cot_raw[...]
    cot_own[...] = jnp.where(row_valid(p, lengths, cot.shape[0]), cot, jnp.zeros_like(cot))
    gather.hop(1)
    for step in range(1, count):
        small_copy(step, p.me, lax.rem(p.me + count - step, count)).wait_recv()
    gain = gain_row(small_out, 0)
    across().wait_recv()
    for step in range(1, groups):
        share(step).start()
    rows = own.shape[0]
    pair = 2 * rows
    slots = rows // seqs
    low = own.dtype
    for step in range(1, groups):
        quarter = lax.rem(rank + step, groups)
        ref = rows_of(quarter, 1 - p.y)
        to_peer("grp", rank, ref, ref, wg_send.at[step], w_recv.at[quarter]).wait_recv()

    @pl.loop(0, line)
    def _(i):
        d = p.near(i)
        gather.whole(d)
        x = rows_all[pl.ds(2 * d, 2)].reshape(pair, -1).astype(F32)
        n = (x * inverse_rms(x) * gain).astype(low)
        normed[pl.ds(2 * d, 2)] = n.reshape(2, rows, -1)
        at = pl.ds(pl.multiple_of(d * 2 * slots, 2 * slots), 2 * slots)
        c, s = cosine[at], sine[at]

        def by_rows(t):
            return jnp.concatenate([t[:slots]] * seqs + [t[slots:]] * seqs, 0)

        c, s = by_rows(c), by_rows(s)

        def put(target, value):
            for block in range(2):
                for m in range(seqs):
                    to = pl.ds(
                        pl.multiple_of(d * 2 * slots + block * slots, slots), slots
                    )
                    target[m, to] = value[block * rows + m * slots : block * rows + (m + 1) * slots]

        put(q, turn_by(dot_t(n, wq[...]), c, s).astype(low))
        put(k, turn_by(dot_t(n, wkv[0]), c, s).astype(low))
        put(v, dot_t(n, wkv[1]).astype(low))
        gather.hop(i + 2)
        either(i == line - 3, cots.send_own)

    saves = [
        pltpu.make_async_copy(src, dst, save_sem.at[i])
        for i, (src, dst) in enumerate(
            (
                (normed, normed_hbm),
                (q, q_hbm),
                (k, k_hbm),
                (v, v_hbm),
                (wkv, wkv_hbm),
                (cosine, cos_hbm),
                (sine, sin_hbm),
            )
        )
    ]
    start_all(saves)
    cots.pass_rest()
    total_slots = q.shape[1]
    tile = min(256, total_slots)

    @pl.loop(0, seqs)
    def _(n):
        for t in range(total_slots // tile):
            span = (t + 1) * tile
            at = pl.ds(t * tile, tile)
            probs = probabilities(q[n, at], k[n, pl.ds(0, span)], t * tile, lengths[n])
            out = dot(probs.astype(low), v[n, pl.ds(0, span)]).astype(low)
            for c in range(tile // slots):
                b = (t * tile) // slots + c
                attended[pl.ds(pl.multiple_of(b * rows + n * slots, slots), slots)] = out[
                    c * slots : (c + 1) * slots
                ]
        cots.hop(n + 1)

    for h in range(seqs + 1, line):
        cots.hop(h)

    @pl.loop(0, line)
    def _(d):
        at = pl.ds(pl.multiple_of(d * pair, pair), pair)
        parts[pl.ds(2 * d, 2)] = dot(attended[at], wo[...]).astype(low).reshape(2, rows, -1)

    reduce = Reduce(p, parts, branch, r_scratch)
    saves2 = [pltpu.make_async_copy(attended, attended_hbm, save_sem.at[7])]
    start_all(saves2)
    for d in range(line):
        cots.whole(d)
    for i in range(DEPTH):
        reduce.send_across(i)
    saves3 = [pltpu.make_async_copy(cot_all, cot_hbm, save_sem.at[8])]
    start_all(saves3)
    for i in range(line - 1):
        reduce.b_hop(i)
    for i in range(line - 1):
        reduce.hop(i)
        if i + DEPTH < line:
            reduce.send_across(i + DEPTH)
    reduce.finish()
    reduce.drain()
    gather.drain()
    cots.drain()
    wait_all(saves + saves2 + saves3)
    across().wait_send()
    for step in range(1, groups):
        share(step).wait_send()
    for step in range(1, count):
        small_copy(step, lax.rem(p.me + step, count), p.me).wait_send()


def attention(lengths, own, cot, pre_gain, mid_gain, freq, wq, wk, wv, wo, count, groups, ident):
    rows, width = own.shape
    seqs = lengths.shape[0]
    total_slots = count * rows // seqs
    small = (8, pre_gain.shape[1])
    line = count // 2
    low = own.dtype
    v = pltpu.VMEM
    shape = jax.ShapeDtypeStruct
    hd = wq.shape[0]
    big = (count, rows, width)
    head = (seqs, total_slots, hd)
    table = (total_slots, hd // 2)
    flat = (count * rows, hd)
    return pl.pallas_call(
        functools.partial(attention_kernel, line, groups, seqs),
        out_shape=(
            shape((rows, width), F32),
            shape((count,) + small, F32),
            shape(big, low),
            shape(big, low),
            shape(head, low),
            shape(head, low),
            shape(head, low),
            shape(flat, low),
            shape((2, hd, width), low),
            shape(table, F32),
            shape(table, F32),
        ),
        in_specs=[scalars()] + [vm()] * 5 + [hbm()] * 4,
        out_specs=(vm(), vm()) + (hbm(),) * 9,
        scratch_shapes=[
            v(small, F32), v((rows, width), low), v(big, low), v(big, low), v(big, low), v(head, low), v(head, low), v(head, low), v(flat, low),
            v((hd, width), low), v((2, hd, width), low), v((hd, width), low), v(table, F32), v(table, F32), v(big, low),
        ]
        + gather_sems(count) * 2
        + [DMA((4,)), DMA((count,)), DMA((count,)), DMA, DMA((groups,)), DMA((groups,)), DMA((9,))]
        + Reduce.scratch(line, rows, width, low),
        compiler_params=params(ident),
        name="attention",
    )(lengths, own, cot, pre_gain, mid_gain, freq, wq, wk, wv, wo)


def ffn_kernel(
    line, groups,
    tokens, branch, gains, cot_hbm, gate_hbm, up_hbm, down_hbm,
    second, ffn_hbm, pair_hbm, chip_in,
    own, normed, cot, gate_w, up_w, down_w, hidden, gate_g, up_g, parts, stage, theirs,
    *scratch,
):
    p = Place(line)
    rank = lax.axis_index("grp")
    core = lax.rem(rank, 2)
    partner = rank + 1 - 2 * core
    opposite = lax.rem(rank + 2, groups)
    (load_sem, out_sem, stage_send, stage_recv, chip_send, chip_recv) = scratch[3:9]
    loads = [
        pltpu.make_async_copy(src, dst, load_sem.at[i])
        for i, (src, dst) in enumerate(
            ((gate_hbm, gate_w), (up_hbm, up_w), (cot_hbm, cot), (down_hbm, down_w))
        )
    ]
    start_all(loads)
    middle = tokens[...].astype(F32) + branch[...]
    own[...] = (middle * inverse_rms(middle) * gain_row(gains, 1)).astype(own.dtype)
    p.greet(groups)
    gather = Gather(p, own, normed, *scratch[:3])
    gather.start()
    wait_all(loads)
    rows = own.shape[0]
    pair = 2 * rows
    low = own.dtype

    @pl.loop(0, line)
    def _(i):
        gather.hop(i + 1)
        d = p.near(i)
        gather.whole(d)
        x = normed[pl.ds(2 * d, 2)].reshape(pair, -1)
        g = dot_t(x, gate_w[...])
        u = dot_t(x, up_w[...])
        dh = dot_t(cot[pl.ds(2 * d, 2)].reshape(pair, -1), down_w[...])
        s = 1.0 / (1.0 + jnp.exp(-g))
        silu = g * s
        at = pl.ds(pl.multiple_of(d * pair, pair), pair)
        hidden[at] = (silu * u).astype(low)
        up_g[at] = (dh * silu).astype(low)
        gate_g[at] = (dh * u * s * (1.0 + g * (1.0 - s))).astype(low)
        part = dot(gate_g[at], gate_w[...]) + dot(up_g[at], up_w[...])
        parts[pl.ds(2 * d, 2)] = part.astype(low).reshape(2, rows, -1)

    reduce = Reduce(p, parts, second, scratch[9:])
    for i in range(DEPTH):
        reduce.send_across(i)

    units = hidden.shape[1]
    quarter = units // 4
    half = units // 2
    mine = (up_w.at[pl.ds(0, half)], gate_w.at[pl.ds(0, half)], gate_w.at[pl.ds(half, half)])

    def to_partner(which, j):
        return to_peer(
            "grp",
            partner,
            stage.at[j],
            theirs.at[which, pl.ds(j * quarter, quarter)],
            stage_send.at[j],
            stage_recv.at[which, j],
        )

    def gradient(which, left, right, between=None):
        def block(q):
            cols = pl.ds(pl.multiple_of(q * quarter, quarter), quarter)
            return t_dot(left[:, cols], right[...].reshape(left.shape[0], -1)).astype(low)

        @pl.loop(0, 2)
        def _(j):
            if which:
                to_partner(which - 1, j).wait_send()
            stage[j] = block(2 * (1 - core) + j)
            to_partner(which, j).start()

        if between is not None:
            between()

        @pl.loop(0, 2)
        def _(j):
            at = pl.ds(pl.multiple_of(j * quarter, quarter), quarter)
            mine[which][at] = block(2 * core + j)

    def add_theirs(which):
        for j in range(2):
            to_partner(which, j).wait_recv()
        total_into(mine[which], mine[which], theirs.at[which])

    def chip_copy():
        return to_peer(
            "grp", opposite, mine[0].at[pl.ds(0, chip_in.shape[0])], chip_in, chip_send, chip_recv
        )

    def save_pair(which):
        return pltpu.make_async_copy(mine[which], pair_hbm.at[which], out_sem.at[which])

    def rest_hops():
        for i in range(line - 1):
            reduce.b_hop(i)

    gradient(0, hidden, cot, rest_hops)
    reduce.hop(0)
    reduce.send_across(DEPTH)
    add_theirs(0)
    chip_copy().start()
    save_pair(0).start()
    gradient(1, gate_g, normed)
    reduce.hop(1)
    reduce.send_across(DEPTH + 1)
    add_theirs(1)
    save_pair(1).start()
    gradient(2, up_g, normed)
    reduce.hop(2)
    gather.drain()

    @pl.loop(0, line)
    def _(d):
        at = pl.ds(pl.multiple_of(d * pair, pair), pair)
        normed[pl.ds(2 * d, 2)] = dot(hidden[at], down_w[...]).astype(low).reshape(2, rows, -1)

    ffn_save = pltpu.make_async_copy(normed, ffn_hbm, out_sem.at[3])
    ffn_save.start()
    add_theirs(2)
    save_pair(2).start()
    reduce.finish()
    for j in range(2):
        to_partner(2, j).wait_send()

    reduce.drain()
    chip_copy().wait()
    ffn_save.wait()
    for which in range(3):
        save_pair(which).wait()


def ffn(tokens, branch, gains, cot, gate_w, up_w, down_w, groups, ident):
    rows, width = tokens.shape
    count = cot.shape[0]
    line = count // 2
    units = gate_w.shape[0]
    low = tokens.dtype
    v = pltpu.VMEM
    tall = count * rows
    shape = jax.ShapeDtypeStruct
    big = (count, rows, width)
    half = (units // 2, width)
    return pl.pallas_call(
        functools.partial(ffn_kernel, line, groups),
        out_shape=(
            shape((rows, width), F32),
            shape(big, low),
            shape((3,) + half, low),
            shape((EARLY * PIECE, width), low),
        ),
        in_specs=[vm()] * 3 + [hbm()] * 4,
        out_specs=(vm(), hbm(), hbm(), hbm()),
        scratch_shapes=[v((rows, width), low)]
        + [v(big, low)] * 2
        + [v((units, width), low)] * 3
        + [v((tall, units), low)] * 3
        + [v(big, low), v((2, units // 4, width), low), v((3,) + half, low)]
        + gather_sems(count)
        + [DMA((4,)), DMA((4,)), DMA((2,)), DMA((3, 2)), DMA, DMA]
        + Reduce.scratch(line, rows, width, low),
        compiler_params=params(ident),
        name="ffn",
    )(tokens, branch, gains, cot, gate_w, up_w, down_w)


def attention_grad_kernel(
    line, groups, seqs,
    lengths, tokens, branch, cot, second, gains, cosine, sine,
    ffn_hbm, normed_hbm, attended_hbm, q_hbm, k_hbm, v_hbm, wq_hbm, wkv_hbm, wo_hbm, sums_hbm, early_hbm,
    mixed, input_grad, gain_out, total_hbm, attn_hbm,
    own, middle_grad, first, ffn_own, dbranch, normed, attended, q, k, v, wq, wkv, wo, da, dk_acc, dv_acc, dq_rows, dk_rows, dv_rows,
    halves, half_in, ffn_parts, sums, sums_in, stage, mine, theirs, mine_in, gain_held, gain_in, gain_sum, gain_all,
    *scratch,
):
    p = Place(line)
    count = 2 * line
    rank = lax.axis_index("grp")
    core = lax.rem(rank, 2)
    partner = rank + 1 - 2 * core
    opposite = lax.rem(rank + 2, groups)
    (
        load_sem, chip_send, chip_recv, half_send, half_recv, stage_send, stage_recv,
        back_send, back_recv, keep_sem, ga_send, ga_recv, gb_send, gb_recv,
    ) = scratch[3:17]
    n = Reduce.N_SCRATCH
    loads = [
        pltpu.make_async_copy(src, dst, load_sem.at[i])
        for i, (src, dst) in enumerate(
            (
                (wo_hbm, wo),
                (ffn_hbm, ffn_parts),
                (attended_hbm, attended),
                (q_hbm, q),
                (k_hbm, k),
                (v_hbm, v),
                (wq_hbm, wq),
                (wkv_hbm, wkv),
                (normed_hbm, normed),
                (early_hbm, sums_in.at[pl.ds(0, EARLY)]),
            )
        )
    ]
    start_all(loads)

    def load_sum(i):
        return pltpu.make_async_copy(sums_hbm.at[i], sums.at[lax.rem(i, 2)], load_sem.at[10 + lax.rem(i, 2)])

    load_sum(0).start()
    load_sum(1).start()
    middle = tokens[...].astype(F32) + branch[...]
    inverse = inverse_rms(middle)
    grad = cot[...].astype(F32)
    grad = jnp.where(row_valid(p, lengths, grad.shape[0]), grad, jnp.zeros_like(grad))
    grad = grad + norm_grad(middle, inverse, gain_row(gains, 1), second[...])
    middle_grad[...] = grad
    own[...] = grad.astype(own.dtype)
    mid_total = jnp.sum(second[...] * middle * inverse, 0, keepdims=True)
    share = gain_held.shape[2]
    for b in range(count):
        gain_held[b] = jnp.zeros(gain_held.shape[1:], F32)
        gain_held[b, 1:2] = mid_total[:, b * share : (b + 1) * share]
    p.greet(groups)
    gather = Gather(p, own, dbranch, *scratch[:3])
    n_sums = sums_hbm.shape[0]
    part_rows = sums.shape[1]

    def chip_copy(i):
        return to_peer(
            "grp", opposite, sums_hbm.at[i], sums_in.at[i], chip_send.at[i], chip_recv.at[i]
        )

    gather.start()

    @pl.loop(EARLY, n_sums)
    def _(i):
        chip_copy(i).start()

    wait_all(loads)
    ffn_sum = Reduce(p, ffn_parts, ffn_own, scratch[17 : 17 + n])
    rows = own.shape[0]
    pair = 2 * rows
    slots = rows // seqs
    low = own.dtype
    scale = 1.0 / math.sqrt(HD)

    @pl.loop(0, line)
    def _(i):
        gather.hop(i + 1)

        @pl.when(i == line - 2)
        def _():
            for first_sends in range(DEPTH):
                ffn_sum.send_across(first_sends)

        d = p.near(i)
        gather.whole(d)
        grad = dot_t(dbranch[pl.ds(2 * d, 2)].reshape(pair, -1), wo[...]).astype(low)
        for block in range(2):
            for m in range(seqs):
                at = pl.ds(pl.multiple_of(d * 2 * slots + block * slots, slots), slots)
                da[m, at] = grad[block * rows + m * slots : block * rows + (m + 1) * slots]

    for i in range(line - 1):
        ffn_sum.b_hop(i)

    chunk = stage.shape[1]

    def to_partner(b):
        return to_peer(
            "grp",
            partner,
            stage.at[b // 2],
            theirs.at[pl.ds(b // 2 * chunk, chunk)],
            stage_send.at[b // 2],
            stage_recv.at[b // 2],
        )

    def gradient(b, left, right):
        value = t_dot(left, right[...].reshape(left.shape[0], -1)).astype(low)
        keep = core == b % 2

        @pl.when(keep)
        def _():
            mine[pl.ds(b // 2 * chunk, chunk)] = value

        @pl.when(jnp.logical_not(keep))
        def _():
            stage[b // 2] = value
            to_partner(b).start()

    total_slots = q.shape[1]
    tile = min(256, total_slots)

    def backward(m):
        dk_acc[...] = jnp.zeros_like(dk_acc)
        dv_acc[...] = jnp.zeros_like(dv_acc)

        def to_rows(target, value, start, size):
            for c in range(size // slots):
                b = start // slots + c
                target[pl.ds(pl.multiple_of(b * rows + m * slots, slots), slots)] = value[
                    c * slots : (c + 1) * slots
                ]

        for t in range(total_slots // tile):
            span = (t + 1) * tile
            at = pl.ds(t * tile, tile)
            query, grad = q[m, at], da[m, at]
            keys, values = k[m, pl.ds(0, span)], v[m, pl.ds(0, span)]
            probs = probabilities(query, keys, t * tile, lengths[m])
            dprobs = dot_t(grad, values)
            inner = jnp.sum(probs * dprobs, -1, keepdims=True)
            dscores = (probs * (dprobs - inner)).astype(low)
            dq = turn_back(dot(dscores, keys) * scale, cosine[at], sine[at])
            to_rows(dq_rows, dq.astype(low), t * tile, tile)
            dk_acc[pl.ds(0, span)] += t_dot(dscores, query)
            dv_acc[pl.ds(0, span)] += t_dot(probs.astype(low), grad)
        dk = turn_back(dk_acc[...] * scale, cosine[...], sine[...])
        to_rows(dk_rows, dk.astype(low), 0, total_slots)
        to_rows(dv_rows, dv_acc[...].astype(low), 0, total_slots)

    half = HD // 2

    def swap():
        return to_peer("shard", p.cross, halves.at[1 - p.y], half_in, half_send, half_recv)

    gradient(0, attended[:, :chunk], dbranch)
    gradient(1, attended[:, chunk:], dbranch)

    @pl.loop(0, seqs)
    def _(m):
        backward(m)
        ffn_sum.hop(m)
        ffn_sum.send_across(m + DEPTH)

    for h in range(2):
        halves[h, 0] = dk_rows[:, h * half : (h + 1) * half]
        halves[h, 1] = dv_rows[:, h * half : (h + 1) * half]
    swap().start()
    gather.drain()
    parts = dbranch
    gradient(2, dq_rows[:, :chunk], normed)
    gradient(3, dq_rows[:, chunk:], normed)

    spans = (pl.ds(0, 2 * chunk), pl.ds(2 * chunk, chunk))

    def attn_chip(part):
        return to_peer(
            "grp",
            opposite,
            mine.at[spans[part]],
            mine_in.at[spans[part]],
            chip_send.at[n_sums + part],
            chip_recv.at[n_sums + part],
        )

    def attn_pair(part, blocks):
        for b in blocks:
            to_partner(2 * b).wait_recv()
        at = mine.at[spans[part]]
        total_into(at, at, theirs.at[spans[part]])
        attn_chip(part).start()

    def back_attn(part):
        size = 2 * chunk if part == 0 else chunk
        start = core * 3 * chunk + part * 2 * chunk
        out = attn_hbm.at[pl.ds(pl.multiple_of(start, chunk), size)]
        at = mine.at[spans[part]]
        sems = keep_sem.at[n_sums + part], back_send.at[n_sums + part], back_recv.at[n_sums + part]
        return pltpu.make_async_copy(at, out, sems[0]), to_peer("grp", partner, at, out, *sems[1:])

    def attn_total(part):
        attn_chip(part).wait()
        at = mine.at[spans[part]]
        total_into(at, at, mine_in.at[spans[part]])
        start_all(back_attn(part))


    @pl.loop(0, line)
    def _(d):
        at = pl.ds(pl.multiple_of(d * pair, pair), pair)
        part = dot(dq_rows[at], wq[...]) + dot(dk_rows[at], wkv[0]) + dot(dv_rows[at], wkv[1])
        parts[pl.ds(2 * d, 2)] = part.astype(low).reshape(2, rows, -1)

    for i in range(seqs, line - 1):
        ffn_sum.hop(i)
    attn_pair(0, (0, 1))
    ffn_sum.finish()
    reduce = Reduce(p, parts, first, scratch[17 + n :])
    for i in range(DEPTH):
        reduce.send_across(i)
    for i in range(line - 1):
        reduce.b_hop(i)

    def summed(which):
        return (halves[p.y, which].astype(F32) + half_in[which].astype(F32)).astype(low)

    valid = row_valid(p, lengths, rows)
    result = tokens[...].astype(F32) + branch[...] + ffn_own[...]
    mixed[...] = jnp.where(valid, result, jnp.zeros_like(result)).astype(low)

    def back(i):
        per_half = n_sums // 3
        start = core * per_half * part_rows + lax.rem(i, per_half) * part_rows
        at = pl.ds(pl.multiple_of(start, part_rows), part_rows)
        out = total_hbm.at[lax.div(i, per_half), at]
        return (
            pltpu.make_async_copy(sums_in.at[i], out, keep_sem.at[i]),
            to_peer("grp", partner, sums_in.at[i], out, back_send.at[i], back_recv.at[i]),
        )

    def sum_up(first_piece, end):
        @pl.loop(first_piece, end)
        def _(i):
            either(i >= EARLY, lambda: chip_copy(i).wait())
            load_sum(i).wait()
            total_into(sums_in.at[i], sums.at[lax.rem(i, 2)], sums_in.at[i])
            either(i + 2 < n_sums, lambda: load_sum(i + 2).start())
            start_all(back(i))

    def gain_copy(step, peer, origin):
        return to_peer(
            "shard", peer, gain_held.at[peer], gain_in.at[origin], ga_send.at[step], ga_recv.at[step]
        )

    def gain_group(step, peer, origin):
        return to_peer(
            "grp", peer, gain_sum, gain_all.at[origin], gb_send.at[step], gb_recv.at[step]
        )

    def gain_first():
        def body(i, total):
            at = pl.ds(pl.multiple_of(i * 16, 16), 16)
            for b in range(count):
                total = total + parts[b, at].astype(F32) * normed[b, at].astype(F32)
            return total

        total = lax.fori_loop(0, rows // 16, body, jnp.zeros((16, parts.shape[2]), F32))
        total = jnp.sum(total, 0, keepdims=True) / gain_row(gains, 0)
        for b in range(count):
            gain_held[b, 0:1] = total[:, b * share : (b + 1) * share]
        for step in range(1, count):
            gain_copy(step, lax.rem(p.me + step, count), p.me).start()

    def gain_second():
        for step in range(1, count):
            gain_copy(step, p.me, lax.rem(p.me + count - step, count)).wait_recv()
        gain_in[p.me] = gain_held[p.me]
        total = gain_in[0]
        for b in range(1, count):
            total = total + gain_in[b]
        gain_sum[...] = total
        gain_all[rank] = total
        for step in range(1, groups):
            gain_group(step, lax.rem(rank + step, groups), rank).start()

    swap().wait_recv()
    gradient(4, summed(0), normed)
    gradient(5, summed(1), normed)
    reduce.hop(0)
    reduce.send_across(DEPTH)
    attn_pair(1, (2,))
    gain_first()
    sum_up(0, n_sums // 2)
    reduce.hop(1)
    reduce.send_across(DEPTH + 1)
    gain_second()
    sum_up(n_sums // 2, n_sums - 3)
    reduce.hop(2)
    sum_up(n_sums - 3, n_sums)
    attn_total(0)
    reduce.finish()
    for step in range(1, groups):
        gain_group(step, rank, lax.rem(rank + groups - step, groups)).wait_recv()
    total = gain_all[0]
    for b in range(1, groups):
        total = total + gain_all[b]
    gain_out[...] = total
    source = tokens[...].astype(F32)
    inner = norm_grad(source, inverse_rms(source), gain_row(gains, 0), first[...])
    input_grad[...] = (middle_grad[...] + inner).astype(low)
    attn_total(1)
    reduce.drain()
    ffn_sum.drain()
    swap().wait_send()
    for b in range(3):
        to_partner(2 * b).wait_send()
    for step in range(1, count):
        gain_copy(step, lax.rem(p.me + step, count), p.me).wait_send()
    for step in range(1, groups):
        gain_group(step, lax.rem(rank + step, groups), rank).wait_send()

    @pl.loop(0, n_sums)
    def _(i):
        wait_all(back(i))

    for part in range(2):
        wait_all(back_attn(part))


def attention_grad(
    lengths, tokens, branch, cot, second, gains, cosine, sine, ffn_parts, normed, attended, q, k, v, wq, wkv, wo, sums, early,
    groups, ident,
):
    rows, width = tokens.shape
    count = normed.shape[0]
    line = count // 2
    seqs, total_slots, hd = q.shape
    low = tokens.dtype
    vmem = pltpu.VMEM
    tall = count * rows
    half = hd // 2
    sums = sums.reshape(-1, PIECE, width)
    early = early.reshape(-1, PIECE, width)
    n_sums, part_rows, _ = sums.shape
    shape = jax.ShapeDtypeStruct
    big = vmem((count, rows, width), low)
    head = vmem((seqs, total_slots, hd), low)
    weight = vmem((hd, width), low)
    flat = vmem((tall, hd), low)
    acc = vmem((total_slots, hd), F32)
    third = vmem((3 * half, width), low)
    g = gains.shape
    block = vmem((rows, width), F32)
    return pl.pallas_call(
        functools.partial(attention_grad_kernel, line, groups, seqs),
        out_shape=(
            shape((rows, width), low),
            shape((rows, width), low),
            shape(g[1:], F32),
            shape((3, n_sums // 3 * 2 * part_rows, width), low),
            shape((6 * half, width), low),
        ),
        in_specs=[scalars()] + [vm()] * 7 + [hbm()] * 11,
        out_specs=(vm(), vm(), vm(), hbm(), hbm()),
        scratch_shapes=[
            vmem((rows, width), low), block, block, block,
            big, big, flat, head, head, head, weight, vmem((2, hd, width), low), weight, head, acc, acc,
            flat, flat, flat,
            vmem((2, 2, tall, half), low), vmem((2, tall, half), low), big,
            vmem((2,) + sums.shape[1:], low), vmem(sums.shape, low), vmem((3, half, width), low), third, third, third,
            vmem(g, F32), vmem(g, F32), vmem(g[1:], F32), vmem((groups,) + g[1:], F32),
        ]
        + gather_sems(count)
        + [
            DMA((12,)), DMA((n_sums + 2,)), DMA((n_sums + 2,)), DMA, DMA, DMA((3,)), DMA((3,)),
            DMA((n_sums + 2,)), DMA((n_sums + 2,)), DMA((n_sums + 2,)),
            DMA((count,)), DMA((count,)), DMA((groups,)), DMA((groups,)),
        ]
        + Reduce.scratch(line, rows, width, low) * 2,
        compiler_params=params(ident),
        name="attention_grad",
    )(
        lengths, tokens, branch, cot, second, gains, cosine, sine, ffn_parts, normed, attended, q, k, v, wq, wkv, wo, sums, early
    )


epsilon = 1e-06
theta_base = 1000042.0
masked_value = -1e30


def turned(source):
    half_width = source.shape[-1] // 2
    return jnp.concatenate([-source[..., half_width:], source[..., :half_width]], -1)


def rotate(source, cosine_table, sine_table):
    return source * cosine_table + turned(source) * sine_table


def unrotate(source, cosine_table, sine_table):
    return source * cosine_table - turned(source) * sine_table


def norm_forward(source, norm_gain):
    inverse = lax.rsqrt(jnp.mean(source * source, -1, keepdims=True) + epsilon)
    return (source * inverse * norm_gain, inverse)


def norm_backward(source, inverse, norm_gain, grad_out):
    weighted = grad_out * norm_gain
    inner_sum = jnp.sum(weighted * source, -1, keepdims=True)
    grad_in = (
        inverse * weighted - source * inverse * inverse * inverse * inner_sum / source.shape[-1]
    )
    return (grad_in, jnp.sum(grad_out * source * inverse, 0))


def weight_terms(normed, query_grad, key_grad, value_grad, attended, branch_grad, shard_count):
    token_count, model_width = normed.shape
    query_share = query_grad.shape[1] // shard_count
    kv_share = key_grad.shape[1] // shard_count
    shard_rows = 2 * query_share + 2 * kv_share

    def weight_term(first_row, row_count):
        blocks = row_count // shard_rows

        def columns(matrix, share_cols):
            return matrix.reshape(token_count, blocks, share_cols)

        part_query = jnp.einsum(
            "tmr,td->mrd",
            columns(query_grad, query_share),
            normed,
            preferred_element_type=jnp.float32,
        )
        part_key = jnp.einsum(
            "tmr,td->mrd", columns(key_grad, kv_share), normed, preferred_element_type=jnp.float32
        )
        part_value = jnp.einsum(
            "tmr,td->mrd", columns(value_grad, kv_share), normed, preferred_element_type=jnp.float32
        )
        part_out = jnp.einsum(
            "tmr,td->mrd",
            columns(attended, query_share),
            branch_grad,
            preferred_element_type=jnp.float32,
        )
        return jnp.concatenate([part_query, part_key, part_value, part_out], 1).reshape(
            row_count, model_width
        )

    return (weight_term, shard_rows)


def local_rows(
    tokens,
    lengths,
    prenorm_gain,
    query_weight,
    key_weight,
    value_weight,
    out_weight,
    midnorm_gain,
    gate_weight,
    up_weight,
    down_weight,
    cotangent,
):
    shard_count = lax.axis_size("shard")
    shard_rank = lax.axis_index("shard")
    micro_count, seq_dev, model_width = tokens.shape
    slot_count = seq_dev * shard_count
    repeat_heads = NH // KVH
    query_width = NH * HD
    kv_width = KVH * HD
    score_scale = 1.0 / math.sqrt(HD)
    local_pos = shard_rank * seq_dev + jnp.arange(seq_dev, dtype=jnp.int32)
    key_pos = jnp.arange(slot_count, dtype=jnp.int32)
    inverse_freq = theta_base ** (-(jnp.arange(0, HD, 2).astype(jnp.float32) / HD))
    angles = local_pos.astype(jnp.float32)[:, None] * inverse_freq[None, :]
    cosine_table = jnp.concatenate([jnp.cos(angles), jnp.cos(angles)], -1)[:, None, :]
    sine_table = jnp.concatenate([jnp.sin(angles), jnp.sin(angles)], -1)[:, None, :]
    gate_total = jnp.zeros(gate_weight.shape, jnp.float32)
    up_total = jnp.zeros(up_weight.shape, jnp.float32)
    down_total = jnp.zeros(down_weight.shape, jnp.float32)
    prenorm_total = jnp.zeros((model_width,), jnp.float32)
    midnorm_total = jnp.zeros((model_width,), jnp.float32)
    attn_total = None
    mixed_rows = []
    input_rows = []
    for micro_index in range(micro_count):
        gathered = (
            lax.all_gather(query_weight, "shard", axis=0, tiled=True),
            lax.all_gather(key_weight, "shard", axis=0, tiled=True),
            lax.all_gather(value_weight, "shard", axis=0, tiled=True),
            lax.all_gather(prenorm_gain, "shard", axis=0, tiled=True),
            lax.all_gather(midnorm_gain, "shard", axis=0, tiled=True),
        )
        query_full, key_full, value_full, prenorm_full, midnorm_full = gathered
        prenorm_f = prenorm_full.astype(jnp.float32)
        midnorm_f = midnorm_full.astype(jnp.float32)
        source = tokens[micro_index].astype(jnp.float32)
        length_now = lengths[micro_index]
        valid_rows = local_pos < length_now
        scaled_first, inverse_first = norm_forward(source, prenorm_f)
        normed_first = scaled_first.astype(jnp.bfloat16)
        query_pre = jnp.einsum(
            "sd,qd->sq", normed_first, query_full, preferred_element_type=jnp.float32
        ).reshape(seq_dev, NH, HD)
        key_pre = jnp.einsum(
            "sd,qd->sq", normed_first, key_full, preferred_element_type=jnp.float32
        ).reshape(seq_dev, KVH, HD)
        value_pre = jnp.einsum(
            "sd,qd->sq", normed_first, value_full, preferred_element_type=jnp.float32
        )
        query_rot = rotate(query_pre, cosine_table, sine_table).astype(jnp.bfloat16)
        key_rot = rotate(key_pre, cosine_table, sine_table).astype(jnp.bfloat16)
        key_value = jnp.concatenate(
            [key_rot.reshape(seq_dev, kv_width), value_pre.astype(jnp.bfloat16)], 1
        )
        kv_all = lax.all_gather(key_value, "shard", axis=0, tiled=True)
        keys_all = kv_all[:, :kv_width].reshape(slot_count, KVH, HD)
        values_all = kv_all[:, kv_width:].reshape(slot_count, KVH, HD)
        query_group = query_rot.reshape(seq_dev, KVH, repeat_heads, HD)
        scores = (
            jnp.einsum("skrd,tkd->krst", query_group, keys_all, preferred_element_type=jnp.float32)
            * score_scale
        )
        allowed = (key_pos[None, :] <= local_pos[:, None]) & (key_pos[None, :] < length_now)
        scores = jnp.where(allowed, scores, masked_value)
        row_max = jnp.max(scores, -1, keepdims=True)
        exp_scores = jnp.exp(scores - row_max)
        attention_probs = exp_scores / jnp.sum(exp_scores, -1, keepdims=True)
        probs_low = attention_probs.astype(jnp.bfloat16)
        attended = (
            jnp.einsum("krst,tkd->skrd", probs_low, values_all, preferred_element_type=jnp.float32)
            .astype(jnp.bfloat16)
            .reshape(seq_dev, query_width)
        )
        branch = jnp.dot(
            attended,
            lax.all_gather(out_weight, "shard", axis=0, tiled=True),
            preferred_element_type=jnp.float32,
        )
        middle = source + branch
        scaled_second, inverse_second = norm_forward(middle, midnorm_f)
        normed_second = scaled_second.astype(jnp.bfloat16)
        normed_all = lax.all_gather(normed_second, "shard", axis=0, tiled=True)
        gate_pre = jnp.einsum(
            "sd,fd->sf", normed_all, gate_weight, preferred_element_type=jnp.float32
        )
        up_pre = jnp.einsum("sd,fd->sf", normed_all, up_weight, preferred_element_type=jnp.float32)
        sigmoid_gate = jax.nn.sigmoid(gate_pre)
        silu_gate = gate_pre * sigmoid_gate
        hidden = (silu_gate * up_pre).astype(jnp.bfloat16)
        ffn_part = lax.psum_scatter(
            jnp.dot(hidden, down_weight, preferred_element_type=jnp.float32).astype(jnp.bfloat16),
            "shard",
            scatter_dimension=0,
            tiled=True,
        ).astype(jnp.float32)
        mixed_rows.append(
            jnp.where(valid_rows[:, None], middle + ffn_part, 0.0).astype(jnp.bfloat16)
        )
        cot_low = jnp.where(
            valid_rows[:, None], cotangent[micro_index], jnp.zeros_like(cotangent[micro_index])
        )
        cot_all = lax.all_gather(cot_low, "shard", axis=0, tiled=True)
        hidden_grad = jnp.einsum(
            "sd,fd->sf", cot_all, down_weight, preferred_element_type=jnp.float32
        )
        down_total = down_total + jnp.einsum(
            "sf,sd->fd", hidden, cot_all, preferred_element_type=jnp.float32
        )
        gate_grad = (
            hidden_grad * up_pre * sigmoid_gate * (1.0 + gate_pre * (1.0 - sigmoid_gate))
        ).astype(jnp.bfloat16)
        up_grad = (hidden_grad * silu_gate).astype(jnp.bfloat16)
        gate_total = gate_total + jnp.einsum(
            "sf,sd->fd", gate_grad, normed_all, preferred_element_type=jnp.float32
        )
        up_total = up_total + jnp.einsum(
            "sf,sd->fd", up_grad, normed_all, preferred_element_type=jnp.float32
        )
        second_grad = lax.psum_scatter(
            jnp.dot(gate_grad, gate_weight, preferred_element_type=jnp.float32)
            + jnp.dot(up_grad, up_weight, preferred_element_type=jnp.float32),
            "shard",
            scatter_dimension=0,
            tiled=True,
        )
        middle_part, midnorm_part = norm_backward(middle, inverse_second, midnorm_f, second_grad)
        middle_grad = cot_low.astype(jnp.float32) + middle_part
        midnorm_total = midnorm_total + midnorm_part
        branch_grad = middle_grad.astype(jnp.bfloat16)
        attended_grad = jnp.einsum(
            "sd,qd->sq",
            branch_grad,
            lax.all_gather(out_weight, "shard", axis=0, tiled=True),
            preferred_element_type=jnp.float32,
        ).astype(jnp.bfloat16)
        attended_group = attended_grad.reshape(seq_dev, KVH, repeat_heads, HD)
        probs_grad = jnp.einsum(
            "skrd,tkd->krst", attended_group, values_all, preferred_element_type=jnp.float32
        )
        inner_sum = jnp.sum(attention_probs * probs_grad, -1, keepdims=True)
        scores_grad = (attention_probs * (probs_grad - inner_sum)).astype(jnp.bfloat16)
        query_rot_grad = (
            jnp.einsum(
                "krst,tkd->skrd", scores_grad, keys_all, preferred_element_type=jnp.float32
            ).reshape(seq_dev, NH, HD)
            * score_scale
        )
        query_grad = (
            unrotate(query_rot_grad, cosine_table, sine_table)
            .astype(jnp.bfloat16)
            .reshape(seq_dev, query_width)
        )
        row_count = lax.axis_size("shard") * seq_dev
        key_part = (
            jnp.einsum(
                "krst,skrd->tkd", scores_grad, query_group, preferred_element_type=jnp.float32
            )
            * score_scale
        )
        value_part = jnp.einsum(
            "krst,skrd->tkd", probs_low, attended_group, preferred_element_type=jnp.float32
        )
        kv_grad = lax.psum_scatter(
            jnp.concatenate(
                [key_part.reshape(row_count, kv_width), value_part.reshape(row_count, kv_width)], 1
            ).astype(jnp.bfloat16),
            "shard",
            scatter_dimension=0,
            tiled=True,
        ).astype(jnp.float32)
        key_grad = (
            unrotate(kv_grad[:, :kv_width].reshape(seq_dev, KVH, HD), cosine_table, sine_table)
            .astype(jnp.bfloat16)
            .reshape(seq_dev, kv_width)
        )
        value_grad = kv_grad[:, kv_width:].astype(jnp.bfloat16)
        first_grad = jnp.einsum(
            "sq,qd->sd", query_grad, query_full, preferred_element_type=jnp.float32
        )
        first_grad = first_grad + jnp.einsum(
            "sq,qd->sd", key_grad, key_full, preferred_element_type=jnp.float32
        )
        first_grad = first_grad + jnp.einsum(
            "sq,qd->sd", value_grad, value_full, preferred_element_type=jnp.float32
        )
        source_part, prenorm_part = norm_backward(source, inverse_first, prenorm_f, first_grad)
        input_rows.append((middle_grad + source_part).astype(jnp.bfloat16))
        prenorm_total = prenorm_total + prenorm_part
        saved = (normed_first, query_grad, key_grad, value_grad, attended, branch_grad)
        weight_term, shard_rows = weight_terms(*saved, shard_count)
        reduced = lax.psum_scatter(
            weight_term(jnp.int32(0), lax.axis_size("shard") * shard_rows).astype(jnp.bfloat16),
            "shard",
            scatter_dimension=0,
            tiled=True,
        ).astype(jnp.float32)
        attn_total = reduced if attn_total is None else attn_total + reduced
    gain_sums = lax.psum((prenorm_total, midnorm_total), ("grp", "shard"))
    gain_share = model_width // shard_count
    prenorm_gradient = lax.dynamic_slice_in_dim(
        gain_sums[0], shard_rank * gain_share, gain_share, 0
    )
    midnorm_gradient = lax.dynamic_slice_in_dim(
        gain_sums[1], shard_rank * gain_share, gain_share, 0
    )
    summed = (
        lax.psum(attn_total.astype(jnp.bfloat16), "grp").astype(jnp.float32),
        lax.psum(gate_total.astype(jnp.bfloat16), "grp").astype(jnp.float32),
        lax.psum(up_total.astype(jnp.bfloat16), "grp").astype(jnp.float32),
        lax.psum(down_total.astype(jnp.bfloat16), "grp").astype(jnp.float32),
    )
    attn_rows = summed[0]
    query_share = query_width // shard_count
    kv_share = kv_width // shard_count
    query_gradient = attn_rows[:query_share]
    key_gradient = attn_rows[query_share : query_share + kv_share]
    value_gradient = attn_rows[query_share + kv_share : query_share + 2 * kv_share]
    out_gradient = attn_rows[query_share + 2 * kv_share :]
    return (
        jnp.stack(mixed_rows),
        jnp.stack(input_rows),
        prenorm_gradient,
        query_gradient,
        key_gradient,
        value_gradient,
        out_gradient,
        midnorm_gradient,
        summed[1],
        summed[2],
        summed[3],
    )


def local_heads(
    tokens,
    lengths,
    prenorm_gain,
    query_weight,
    key_weight,
    value_weight,
    out_weight,
    midnorm_gain,
    gate_weight,
    up_weight,
    down_weight,
    cotangent,
):
    low = jnp.bfloat16
    count = lax.axis_size("shard")
    groups = lax.axis_size("grp")
    seqs, seq_dev, model_width = tokens.shape
    rows = seqs * seq_dev
    inverse_freq = theta_base ** (-(jnp.arange(0, HD, 2).astype(jnp.float32) / HD))
    tokens_low = tokens.reshape(rows, model_width)
    cot_low = cotangent.reshape(rows, model_width)
    branch, gains, normed_first, cot_all, queries, keys, values, attended, kv_head, cosine, sine = (
        attention(
            lengths,
            tokens_low,
            cot_low,
            prenorm_gain[None, :],
            midnorm_gain[None, :],
            inverse_freq[None, :],
            query_weight,
            key_weight,
            value_weight,
            out_weight,
            count,
            groups,
            1,
        )
    )
    second_grad, ffn_parts, pair_sums, early = ffn(
        tokens_low, branch, gains, cot_all, gate_weight, up_weight, down_weight, groups, 2
    )
    mixed, input_gradient, gain_own, totals, attn_total = attention_grad(
        lengths,
        tokens_low,
        branch,
        cot_low,
        second_grad,
        gains,
        cosine,
        sine,
        ffn_parts,
        normed_first,
        attended,
        queries,
        keys,
        values,
        query_weight,
        kv_head,
        out_weight,
        pair_sums,
        early,
        groups,
        3,
    )
    f32 = jnp.float32
    blocks = attn_total.reshape(2, 3, key_weight.shape[0], model_width).astype(f32)
    return (
        mixed.reshape(tokens.shape),
        input_gradient.reshape(tokens.shape),
        gain_own[0],
        blocks[:, 1].reshape(query_weight.shape),
        blocks[0, 2],
        blocks[1, 2],
        blocks[:, 0].reshape(out_weight.shape),
        gain_own[1],
        totals[1].astype(f32),
        totals[2].astype(f32),
        totals[0].astype(f32),
    )


def solution(mesh):
    planes = mesh.shape["shard"] == NH and mesh.shape["grp"] == 4
    local = local_heads if planes else local_rows
    in_specs = (
        P("grp", "shard", None),
        P("grp"),
        P("shard"),
        P("shard", None),
        P("shard", None),
        P("shard", None),
        P("shard", None),
        P("shard"),
        P("shard", None),
        P("shard", None),
        P("shard", None),
        P("grp", "shard", None),
    )
    out_specs = (
        P("grp", "shard", None),
        P("grp", "shard", None),
        P("shard"),
        P("shard", None),
        P("shard", None),
        P("shard", None),
        P("shard", None),
        P("shard"),
        P("shard", None),
        P("shard", None),
        P("shard", None),
    )
    return jax.shard_map(local, mesh=mesh, in_specs=in_specs, out_specs=out_specs, check_vma=False)
```

```python
import functools
import math

import jax
import jax.numpy as jnp
from jax import lax
from jax.experimental import pallas as pl
from jax.experimental.pallas import tpu as pltpu
from jax.sharding import PartitionSpec as P
import numpy as np

NH = 8
KVH = 4
HD = 256
MASKED = -1e30
EPSILON = 1e-06
DEPTH = 2
MESH = pl.DeviceIdType.MESH
F32 = jnp.float32
DMA = pltpu.SemaphoreType.DMA
REST = 16
PIECE = 128
EARLY = 3
CHUNKS = 2


def pieces(rows):
    size = -(-(rows - REST) // (16 * CHUNKS)) * 16
    cuts = [min(i * size, rows - REST) for i in range(CHUNKS + 1)] + [rows]
    return [pl.ds(a, b - a) for a, b in zip(cuts, cuts[1:])]


VMEM_LIMIT = 66_000_000


def either(condition, action):
    pl.when(condition)(action)


def total_into(dst, *srcs):
    step = 16

    @pl.loop(0, dst.shape[0] // step)
    def _(i):
        at = pl.ds(pl.multiple_of(i * step, step), step)
        value = srcs[0][at].astype(F32)
        for src in srcs[1:]:
            value = value + src[at].astype(F32)
        dst[at] = value.astype(dst.dtype)


class Place:
    def __init__(self, line):
        self.line = line
        self.me = lax.axis_index("shard")
        self.z = self.me // 2
        self.y = lax.rem(self.me, 2)
        self.cross = self.me + 1 - 2 * self.y
        self.low_end = self.z == 0
        self.high_end = self.z == line - 1
        near = []
        for z in range(line):
            order = [z]
            for k in range(1, line):
                order += [d for d in (z - k, z + k) if 0 <= d < line]
            near.append(order)
        self.tables = near

    def near(self, i):
        out = jnp.int32(0)
        for z in range(self.line):
            row = jnp.int32(self.tables[z][0])
            for k in range(1, self.line):
                row = jnp.where(i == k, self.tables[z][k], row)
            out = jnp.where(self.z == z, row, out)
        return out

    def far(self, i):
        return self.near(self.line - 1 - i)

    def greet(self, groups):
        barrier = pltpu.get_barrier_semaphore()
        count = 2 * self.line
        rank = lax.axis_index("grp")
        for step in range(1, count):
            pl.semaphore_signal(
                barrier,
                inc=1,
                device_id={"shard": lax.rem(self.me + step, count)},
                device_id_type=MESH,
            )
        for step in range(1, groups):
            pl.semaphore_signal(
                barrier,
                inc=1,
                device_id={"grp": lax.rem(rank + step, groups)},
                device_id_type=MESH,
            )
        pl.semaphore_wait(barrier, count + groups - 2)


class Gather:
    UP, DOWN, CROSS = 0, 1, 2

    def __init__(self, place, own, out, local_sem, send_sem, recv_sem):
        self.p, self.own, self.out = place, own, out
        self.local_sem, self.send_sem, self.recv_sem = local_sem, send_sem, recv_sem
        self.pieces = pieces(own.shape[0])
        self.last = len(self.pieces) - 1

    def copy(self, way, origin, part, own=False):
        p = self.p
        peer = (p.me + 2, p.me - 2, p.cross)[way]
        at = self.pieces[part]
        return pltpu.make_async_remote_copy(
            src_ref=self.own.at[at] if own else self.out.at[origin, at],
            dst_ref=self.out.at[origin, at],
            send_sem=self.send_sem.at[way, origin, part],
            recv_sem=self.recv_sem.at[origin, part],
            device_id={"shard": peer},
            device_id_type=MESH,
        )

    def arrived(self, origin, part):
        self.copy(self.CROSS, origin, part).wait_recv()

    def start(self):
        self.send_own()
        self.pass_rest()

    def send_own(self):
        p = self.p
        pltpu.make_async_copy(self.own, self.out.at[p.me], self.local_sem).start()
        for part in (self.last,) + tuple(range(self.last)):
            self.copy(self.CROSS, p.me, part, True).start()
        for part in range(self.last + 1):
            either(p.z < p.line - 1, lambda: self.copy(self.UP, p.me, part, True).start())
            either(p.z > 0, lambda: self.copy(self.DOWN, p.me, part, True).start())

    def pass_rest(self):
        p = self.p
        self.arrived(p.cross, self.last)
        either(p.z < p.line - 1, lambda: self.copy(self.UP, p.cross, self.last).start())
        either(p.z > 0, lambda: self.copy(self.DOWN, p.cross, self.last).start())
        pltpu.make_async_copy(self.own, self.out.at[p.me], self.local_sem).wait()

    def hop(self, k):
        p = self.p
        below, above = p.me - 2 * k, p.me + 2 * k
        has_below, has_above = p.z - k >= 0, p.z + k < p.line

        def first(origin, part, way, more):
            self.arrived(origin, part)
            self.copy(self.CROSS, origin, part).start()
            either(more, lambda: self.copy(way, origin, part).start())

        def last(origin, other, way, more):
            for block in (origin, other):
                self.arrived(block, self.last)
                either(more, lambda: self.copy(way, block, self.last).start())

        for part in range(self.last):
            either(has_below, lambda: first(below, part, self.UP, p.z < p.line - 1))
            either(has_above, lambda: first(above, part, self.DOWN, p.z > 0))
        either(has_below, lambda: last(below, p.cross - 2 * k, self.UP, p.z < p.line - 1))
        either(has_above, lambda: last(above, p.cross + 2 * k, self.DOWN, p.z > 0))

    def whole(self, position):
        for part in range(self.last):
            self.arrived(2 * position + 1 - self.p.y, part)

    def drain(self):
        p = self.p

        @pl.loop(0, p.line)
        def _(d):
            mine, other = 2 * d + p.y, 2 * d + 1 - p.y
            for part in range(self.last):
                self.copy(self.CROSS, mine, part).wait_send()

            @pl.when(d == p.z)
            def _():
                self.copy(self.CROSS, mine, self.last).wait_send()

            def line_sent(way):
                for part in range(self.last + 1):
                    self.copy(way, mine, part).wait_send()
                self.copy(way, other, self.last).wait_send()

            either((d <= p.z) & (p.z < p.line - 1), lambda: line_sent(self.UP))
            either((d >= p.z) & (p.z > 0), lambda: line_sent(self.DOWN))


class Reduce:
    BUP, BDN, BX = 0, 2, 4
    UP, DOWN, CROSS = 5, 5 + CHUNKS, 5 + 2 * CHUNKS
    WAYS = 5 + 3 * CHUNKS
    N_SCRATCH = 9

    @staticmethod
    def scratch(line, rows, width, dtype):
        v = pltpu.VMEM
        return (
            [v((line, rows - REST, width), dtype)] * 3
            + [v((line, 2, REST, width), dtype)] * 2
            + [v((REST, width), dtype)] * 2
            + [DMA((Reduce.WAYS, line)), DMA((Reduce.WAYS, line))]
        )

    def __init__(self, place, parts, out, scratch):
        self.p, self.parts, self.out = place, parts, out
        self.cross_in, self.up_in, self.down_in, self.bup_in, self.bdn_in = scratch[:5]
        self.bx_out, self.bx_in, self.send_sem, self.recv_sem = scratch[5:]
        self.pieces = pieces(parts.shape[1])
        self.b = self.pieces[-1]

    def desc(self, way, slot, src, dst, peer):
        return pltpu.make_async_remote_copy(
            src_ref=src,
            dst_ref=dst,
            send_sem=self.send_sem.at[way, slot],
            recv_sem=self.recv_sem.at[way, slot],
            device_id={"shard": peer},
            device_id_type=MESH,
        )

    def cross_copy(self, d, c):
        p, at = self.p, self.pieces[c]
        return self.desc(
            self.CROSS + c,
            d,
            self.parts.at[2 * d + 1 - p.y, at],
            self.cross_in.at[d, at],
            p.cross,
        )

    def line_copy(self, up, d, c):
        p, at = self.p, self.pieces[c]
        came = self.up_in if up else self.down_in
        return self.desc(
            (self.UP if up else self.DOWN) + c,
            d,
            self.cross_in.at[d, at],
            came.at[d, at],
            p.me + 2 if up else p.me - 2,
        )

    def b_copy(self, up, d, o, src=None):
        p = self.p
        held = self.bup_in if up else self.bdn_in
        return self.desc(
            (self.BUP if up else self.BDN) + o,
            d,
            held.at[d, o] if src is None else src,
            held.at[d, o],
            p.me + 2 if up else p.me - 2,
        )

    def bx_copy(self):
        return self.desc(self.BX, 0, self.bx_out, self.bx_in, self.p.cross)

    def column(self, o):
        return self.p.y if o == 0 else 1 - self.p.y

    def send_across(self, i):
        for c in range(CHUNKS):
            self.cross_copy(self.p.far(i), c).start()

    def b_hop(self, i):
        p = self.p
        d = p.far(i)

        def go(up):
            first = p.low_end if up else p.high_end
            held = self.bup_in if up else self.bdn_in
            for o in (1, 0):
                mine = self.parts.at[2 * d + self.column(o), self.b]
                either(first, lambda: self.b_copy(up, d, o, mine).start())

                @pl.when(jnp.logical_not(first))
                def _():
                    self.b_copy(up, d, o).wait_recv()
                    total_into(held.at[d, o], mine, held.at[d, o])
                    self.b_copy(up, d, o).start()

        either(d > p.z, lambda: go(True))
        either(d < p.z, lambda: go(False))

    def hop(self, i):
        for c in range(CHUNKS):
            self.step(i, c)

    def step(self, i, c):
        p = self.p
        d = p.far(i)
        self.cross_copy(d, c).wait_recv()
        at = self.pieces[c]
        mine = self.parts.at[2 * d + p.y, at]
        held = self.cross_in.at[d, at]

        def go(up):
            first = p.low_end if up else p.high_end
            came = self.up_in if up else self.down_in
            either(first, lambda: total_into(held, mine, held))

            @pl.when(jnp.logical_not(first))
            def _():
                self.line_copy(up, d, c).wait_recv()
                total_into(held, mine, held, came.at[d, at])

            self.line_copy(up, d, c).start()

        either(d > p.z, lambda: go(True))
        either(d < p.z, lambda: go(False))

    def close(self, dst, mine, ups, downs):
        p = self.p
        either(p.low_end, lambda: total_into(dst, *mine, downs))
        either(p.high_end, lambda: total_into(dst, *mine, ups))
        either(
            jnp.logical_not(p.low_end | p.high_end), lambda: total_into(dst, *mine, ups, downs)
        )

    def finish(self):
        p = self.p
        for o in (1, 0):
            either(jnp.logical_not(p.low_end), lambda: self.b_copy(True, p.z, o).wait_recv())
            either(jnp.logical_not(p.high_end), lambda: self.b_copy(False, p.z, o).wait_recv())
            if o:
                mine = self.parts.at[2 * p.z + self.column(o), self.b]
                self.close(self.bx_out, (mine,), self.bup_in.at[p.z, o], self.bdn_in.at[p.z, o])
                self.bx_copy().start()
        self.bx_copy().wait_recv()
        self.close(
            self.out.at[self.b],
            (self.parts.at[p.me, self.b], self.bx_in),
            self.bup_in.at[p.z, 0],
            self.bdn_in.at[p.z, 0],
        )
        for c in range(CHUNKS):
            self.cross_copy(p.z, c).wait_recv()
            either(jnp.logical_not(p.low_end), lambda: self.line_copy(True, p.z, c).wait_recv())
            either(jnp.logical_not(p.high_end), lambda: self.line_copy(False, p.z, c).wait_recv())
            at = self.pieces[c]
            self.close(
                self.out.at[at],
                (self.parts.at[p.me, at], self.cross_in.at[p.z, at]),
                self.up_in.at[p.z, at],
                self.down_in.at[p.z, at],
            )

    def drain(self):
        p = self.p
        self.bx_copy().wait_send()

        @pl.loop(0, p.line)
        def _(d):
            def line_sent(up):
                for c in range(CHUNKS):
                    self.line_copy(up, d, c).wait_send()
                self.b_copy(up, d, 0).wait_send()
                self.b_copy(up, d, 1).wait_send()

            for c in range(CHUNKS):
                self.cross_copy(d, c).wait_send()
            either(d > p.z, lambda: line_sent(True))
            either(d < p.z, lambda: line_sent(False))


def dot(a, b):
    return jnp.dot(a, b, preferred_element_type=F32)


def dot_t(a, b):
    return lax.dot_general(a, b, (((1,), (1,)), ((), ())), preferred_element_type=F32)


def t_dot(a, b):
    return lax.dot_general(a, b, (((0,), (0,)), ((), ())), preferred_element_type=F32)


def to_peer(axis, peer, src, dst, send_sem, recv_sem):
    return pltpu.make_async_remote_copy(
        src_ref=src,
        dst_ref=dst,
        send_sem=send_sem,
        recv_sem=recv_sem,
        device_id={axis: peer},
        device_id_type=MESH,
    )


def turn_by(v, cosine, sine):
    half = v.shape[-1] // 2
    a, b = v[:, :half], v[:, half:]
    return jnp.concatenate([a * cosine - b * sine, b * cosine + a * sine], -1)


def turn_back(v, cosine, sine):
    return turn_by(v, cosine, -sine)


def probabilities(query, keys, rows_from, limit):
    scores = dot_t(query, keys) * (1.0 / math.sqrt(HD))
    row = lax.broadcasted_iota(jnp.int32, scores.shape, 0) + rows_from
    col = lax.broadcasted_iota(jnp.int32, scores.shape, 1)
    scores = jnp.where((col <= row) & (col < limit), scores, MASKED)
    weight = jnp.exp(scores - jnp.max(scores, -1, keepdims=True))
    return weight / jnp.sum(weight, -1, keepdims=True)


def row_valid(place, lengths, rows):
    slots = rows // lengths.shape[0]
    row = lax.broadcasted_iota(jnp.int32, (rows, 1), 0)
    limit = jnp.full((rows, 1), lengths[0], jnp.int32)
    for n in range(1, lengths.shape[0]):
        limit = jnp.where(row >= n * slots, lengths[n], limit)
    return place.me * slots + lax.rem(row, slots) < limit


def gain_row(shares, which):
    return jnp.concatenate([shares[b, which : which + 1] for b in range(shares.shape[0])], 1)


def inverse_rms(x):
    return lax.rsqrt(jnp.mean(x * x, -1, keepdims=True) + EPSILON)


def norm_grad(x, inverse, gain, grad):
    weighted = grad * gain
    inner = jnp.sum(weighted * x, -1, keepdims=True)
    return inverse * weighted - x * inverse * inverse * inverse * inner / x.shape[-1]


def start_all(copies):
    for c in copies:
        c.start()


def wait_all(copies):
    for c in copies:
        c.wait()


def scalars():
    return pl.BlockSpec(memory_space=pltpu.SMEM)


def hbm():
    return pl.BlockSpec(memory_space=pl.ANY)


def vm():
    return pl.BlockSpec(memory_space=pltpu.VMEM)


def params(ident):
    return pltpu.CompilerParams(
        collective_id=ident, has_side_effects=True, vmem_limit_bytes=VMEM_LIMIT
    )


def gather_sems(count):
    return [DMA, DMA((3, count, CHUNKS + 1)), DMA((count, CHUNKS + 1))]


def attention_kernel(
    line, groups, seqs,
    lengths, own, cot_raw, pre_gain, mid_gain, freq, wq_hbm, wk_hbm, wv_hbm, wo_hbm,
    branch, small_out, normed_hbm, cot_hbm, q_hbm, k_hbm, v_hbm, attended_hbm, wkv_hbm, cos_hbm, sin_hbm,
    small, cot_own, rows_all, normed, cot_all, q, k, v, attended, wq, wkv, wo, cosine, sine, parts,
    *scratch,
):
    p = Place(line)
    count = 2 * line
    rank = lax.axis_index("grp")
    g1, g2 = scratch[:3], scratch[3:6]
    (load_sem, small_send, small_recv, wy_send, wg_send, w_recv, save_sem) = scratch[6:13]
    r_scratch = scratch[13:]
    half = wk_hbm.shape[0]
    piece = half // 2
    at_own = pl.ds(pl.multiple_of(p.y * half, half), half)
    loads = [
        pltpu.make_async_copy(src, dst, load_sem.at[i])
        for i, (src, dst) in enumerate(
            (
                (wk_hbm, wkv.at[0, at_own]),
                (wv_hbm, wkv.at[1, at_own]),
                (wq_hbm, wq),
                (wo_hbm, wo),
            )
        )
    ]
    start_all(loads)
    p.greet(groups)

    small[...] = jnp.zeros_like(small)
    small[0:1] = pre_gain[...].astype(F32)[None, :]
    small[1:2] = mid_gain[...].astype(F32)[None, :]

    def small_copy(step, peer, origin):
        return to_peer(
            "shard", peer, small, small_out.at[origin], small_send.at[step], small_recv.at[step]
        )

    for step in range(1, count):
        small_copy(step, lax.rem(p.me + step, count), p.me).start()
    gather = Gather(p, own, rows_all, *g1)
    gather.start()
    cots = Gather(p, cot_own, cot_all, *g2)
    small_out[p.me] = small[...]

    def rows_of(quarter, column):
        return wkv.at[
            quarter // 2,
            pl.ds(pl.multiple_of(column * half + lax.rem(quarter, 2) * piece, piece), piece),
        ]

    def across():
        ref = rows_of(rank, p.y)
        return to_peer("shard", p.cross, ref, ref, wy_send, w_recv.at[rank])

    def share(step):
        ref = rows_of(rank, 1 - p.y)
        return to_peer(
            "grp", lax.rem(rank + step, groups), ref, ref, wg_send.at[step], w_recv.at[rank]
        )

    wait_all(loads)
    across().start()
    pos = lax.broadcasted_iota(jnp.int32, cosine.shape, 0).astype(F32)
    angle = pos * freq[...]
    cosine[...] = jnp.cos(angle)
    sine[...] = jnp.sin(angle)
    cot = cot_raw[...]
    cot_own[...] = jnp.where(row_valid(p, lengths, cot.shape[0]), cot, jnp.zeros_like(cot))
    gather.hop(1)
    for step in range(1, count):
        small_copy(step, p.me, lax.rem(p.me + count - step, count)).wait_recv()
    gain = gain_row(small_out, 0)
    across().wait_recv()
    for step in range(1, groups):
        share(step).start()
    rows = own.shape[0]
    pair = 2 * rows
    slots = rows // seqs
    low = own.dtype
    for step in range(1, groups):
        quarter = lax.rem(rank + step, groups)
        ref = rows_of(quarter, 1 - p.y)
        to_peer("grp", rank, ref, ref, wg_send.at[step], w_recv.at[quarter]).wait_recv()

    @pl.loop(0, line)
    def _(i):
        d = p.near(i)
        gather.whole(d)
        x = rows_all[pl.ds(2 * d, 2)].reshape(pair, -1).astype(F32)
        n = (x * inverse_rms(x) * gain).astype(low)
        normed[pl.ds(2 * d, 2)] = n.reshape(2, rows, -1)
        at = pl.ds(pl.multiple_of(d * 2 * slots, 2 * slots), 2 * slots)
        c, s = cosine[at], sine[at]

        def by_rows(t):
            return jnp.concatenate([t[:slots]] * seqs + [t[slots:]] * seqs, 0)

        c, s = by_rows(c), by_rows(s)

        def put(target, value):
            for block in range(2):
                for m in range(seqs):
                    to = pl.ds(
                        pl.multiple_of(d * 2 * slots + block * slots, slots), slots
                    )
                    target[m, to] = value[block * rows + m * slots : block * rows + (m + 1) * slots]

        put(q, turn_by(dot_t(n, wq[...]), c, s).astype(low))
        put(k, turn_by(dot_t(n, wkv[0]), c, s).astype(low))
        put(v, dot_t(n, wkv[1]).astype(low))
        gather.hop(i + 2)
        either(i == line - 3, cots.send_own)

    saves = [
        pltpu.make_async_copy(src, dst, save_sem.at[i])
        for i, (src, dst) in enumerate(
            (
                (normed, normed_hbm),
                (q, q_hbm),
                (k, k_hbm),
                (v, v_hbm),
                (wkv, wkv_hbm),
                (cosine, cos_hbm),
                (sine, sin_hbm),
            )
        )
    ]
    start_all(saves)
    cots.pass_rest()
    total_slots = q.shape[1]
    tile = min(256, total_slots)

    @pl.loop(0, seqs)
    def _(n):
        for t in range(total_slots // tile):
            span = (t + 1) * tile
            at = pl.ds(t * tile, tile)
            probs = probabilities(q[n, at], k[n, pl.ds(0, span)], t * tile, lengths[n])
            out = dot(probs.astype(low), v[n, pl.ds(0, span)]).astype(low)
            for c in range(tile // slots):
                b = (t * tile) // slots + c
                attended[pl.ds(pl.multiple_of(b * rows + n * slots, slots), slots)] = out[
                    c * slots : (c + 1) * slots
                ]
        cots.hop(n + 1)

    for h in range(seqs + 1, line):
        cots.hop(h)

    @pl.loop(0, line)
    def _(d):
        at = pl.ds(pl.multiple_of(d * pair, pair), pair)
        parts[pl.ds(2 * d, 2)] = dot(attended[at], wo[...]).astype(low).reshape(2, rows, -1)

    reduce = Reduce(p, parts, branch, r_scratch)
    saves2 = [pltpu.make_async_copy(attended, attended_hbm, save_sem.at[7])]
    start_all(saves2)
    for d in range(line):
        cots.whole(d)
    for i in range(DEPTH):
        reduce.send_across(i)
    saves3 = [pltpu.make_async_copy(cot_all, cot_hbm, save_sem.at[8])]
    start_all(saves3)
    for i in range(line - 1):
        reduce.b_hop(i)
    for i in range(line - 1):
        reduce.hop(i)
        if i + DEPTH < line:
            reduce.send_across(i + DEPTH)
    reduce.finish()
    reduce.drain()
    gather.drain()
    cots.drain()
    wait_all(saves + saves2 + saves3)
    across().wait_send()
    for step in range(1, groups):
        share(step).wait_send()
    for step in range(1, count):
        small_copy(step, lax.rem(p.me + step, count), p.me).wait_send()


def attention(lengths, own, cot, pre_gain, mid_gain, freq, wq, wk, wv, wo, count, groups, ident):
    rows, width = own.shape
    seqs = lengths.shape[0]
    total_slots = count * rows // seqs
    small = (8, pre_gain.shape[0])
    line = count // 2
    low = own.dtype
    v = pltpu.VMEM
    shape = jax.ShapeDtypeStruct
    hd = wq.shape[0]
    big = (count, rows, width)
    head = (seqs, total_slots, hd)
    table = (total_slots, hd // 2)
    flat = (count * rows, hd)
    return pl.pallas_call(
        functools.partial(attention_kernel, line, groups, seqs),
        out_shape=(
            shape((rows, width), F32),
            shape((count,) + small, F32),
            shape(big, low),
            shape(big, low),
            shape(head, low),
            shape(head, low),
            shape(head, low),
            shape(flat, low),
            shape((2, hd, width), low),
            shape(table, F32),
            shape(table, F32),
        ),
        in_specs=[scalars()] + [vm()] * 5 + [hbm()] * 4,
        out_specs=(vm(), vm()) + (hbm(),) * 9,
        scratch_shapes=[
            v(small, F32), v((rows, width), low), v(big, low), v(big, low), v(big, low), v(head, low), v(head, low), v(head, low), v(flat, low),
            v((hd, width), low), v((2, hd, width), low), v((hd, width), low), v(table, F32), v(table, F32), v(big, low),
        ]
        + gather_sems(count) * 2
        + [DMA((4,)), DMA((count,)), DMA((count,)), DMA, DMA((groups,)), DMA((groups,)), DMA((9,))]
        + Reduce.scratch(line, rows, width, low),
        compiler_params=params(ident),
        name="attention",
    )(lengths, own, cot, pre_gain, mid_gain, freq, wq, wk, wv, wo)


def ffn_kernel(
    line, groups,
    tokens, branch, gains, cot_hbm, gate_hbm, up_hbm, down_hbm,
    second, ffn_hbm, pair_hbm, chip_in,
    own, rights, gate_up, down_w, lefts, parts, stage, theirs,
    *scratch,
):
    p = Place(line)
    rank = lax.axis_index("grp")
    core = lax.rem(rank, 2)
    partner = rank + 1 - 2 * core
    opposite = lax.rem(rank + 2, groups)
    (load_sem, out_sem, stage_send, stage_recv, chip_send, chip_recv) = scratch[3:9]
    units = down_w.shape[0]
    gate_w, up_w = gate_up.at[pl.ds(0, units)], gate_up.at[pl.ds(units, units)]
    cot, normed = rights.at[0], rights.at[1]
    hidden, gate_g, up_g = lefts.at[0], lefts.at[1], lefts.at[2]
    loads = [
        pltpu.make_async_copy(src, dst, load_sem.at[i])
        for i, (src, dst) in enumerate(
            ((gate_hbm, gate_w), (up_hbm, up_w), (cot_hbm, cot), (down_hbm, down_w))
        )
    ]
    start_all(loads)
    middle = tokens[...].astype(F32) + branch[...]
    own[...] = (middle * inverse_rms(middle) * gain_row(gains, 1)).astype(own.dtype)
    p.greet(groups)
    gather = Gather(p, own, normed, *scratch[:3])
    gather.start()
    wait_all(loads)
    rows = own.shape[0]
    pair = 2 * rows
    low = own.dtype

    @pl.loop(0, line)
    def _(i):
        gather.hop(i + 1)
        d = p.near(i)
        gather.whole(d)
        x = normed[pl.ds(2 * d, 2)].reshape(pair, -1)
        g = dot_t(x, gate_w[...])
        u = dot_t(x, up_w[...])
        dh = dot_t(cot[pl.ds(2 * d, 2)].reshape(pair, -1), down_w[...])
        s = 1.0 / (1.0 + jnp.exp(-g))
        silu = g * s
        at = pl.ds(pl.multiple_of(d * pair, pair), pair)
        hidden[at] = (silu * u).astype(low)
        up_g[at] = (dh * silu).astype(low)
        gate_g[at] = (dh * u * s * (1.0 + g * (1.0 - s))).astype(low)
        part = dot(gate_g[at], gate_w[...]) + dot(up_g[at], up_w[...])
        parts[pl.ds(2 * d, 2)] = part.astype(low).reshape(2, rows, -1)

    reduce = Reduce(p, parts, second, scratch[9:])
    for i in range(DEPTH):
        reduce.send_across(i)

    for i in range(line - 1):
        reduce.b_hop(i)

    quarter = units // 4
    half = units // 2

    def mine(which):
        start = lax.rem(which + 2, 3) * half
        return gate_up.at[pl.ds(pl.multiple_of(start, half), half)]

    def to_partner(which, j):
        return to_peer(
            "grp",
            partner,
            stage.at[j],
            theirs.at[which, pl.ds(pl.multiple_of(j * quarter, quarter), quarter)],
            stage_send.at[j],
            stage_recv.at[which, j],
        )

    def chip_copy():
        return to_peer(
            "grp",
            opposite,
            gate_up.at[pl.ds(2 * half, chip_in.shape[0])],
            chip_in,
            chip_send,
            chip_recv,
        )

    def save_pair(which):
        return pltpu.make_async_copy(mine(which), pair_hbm.at[which], out_sem.at[which])

    @pl.loop(0, 3)
    def _(which):
        right = rights.at[jnp.minimum(which, 1)]

        def block(q):
            cols = pl.ds(pl.multiple_of(q * quarter, quarter), quarter)
            left = lefts[which, :, cols]
            return t_dot(left, right[...].reshape(left.shape[0], -1)).astype(low)

        @pl.loop(0, 2)
        def _(j):
            either(which > 0, lambda: to_partner(which - 1, j).wait_send())
            stage[j] = block(2 * (1 - core) + j)
            to_partner(which, j).start()

        reduce.step(which, 0)

        @pl.loop(0, 2)
        def _(j):
            at = pl.ds(pl.multiple_of(j * quarter, quarter), quarter)
            mine(which)[at] = block(2 * core + j)

        for c in range(1, CHUNKS):
            reduce.step(which, c)
        either(which + DEPTH < line, lambda: reduce.send_across(which + DEPTH))
        for j in range(2):
            to_partner(which, j).wait_recv()
        total_into(mine(which), mine(which), theirs.at[which])
        either(which == 0, lambda: chip_copy().start())
        save_pair(which).start()

    gather.drain()

    @pl.loop(0, line)
    def _(d):
        at = pl.ds(pl.multiple_of(d * pair, pair), pair)
        normed[pl.ds(2 * d, 2)] = dot(hidden[at], down_w[...]).astype(low).reshape(2, rows, -1)

    ffn_save = pltpu.make_async_copy(normed, ffn_hbm, out_sem.at[3])
    ffn_save.start()
    reduce.finish()
    for j in range(2):
        to_partner(2, j).wait_send()

    reduce.drain()
    chip_copy().wait()
    ffn_save.wait()
    for which in range(3):
        save_pair(which).wait()


def ffn(tokens, branch, gains, cot, gate_w, up_w, down_w, groups, ident):
    rows, width = tokens.shape
    count = cot.shape[0]
    line = count // 2
    units = gate_w.shape[0]
    low = tokens.dtype
    v = pltpu.VMEM
    tall = count * rows
    shape = jax.ShapeDtypeStruct
    big = (count, rows, width)
    half = (units // 2, width)
    return pl.pallas_call(
        functools.partial(ffn_kernel, line, groups),
        out_shape=(
            shape((rows, width), F32),
            shape(big, low),
            shape((3,) + half, low),
            shape((EARLY * PIECE, width), low),
        ),
        in_specs=[vm()] * 3 + [hbm()] * 4,
        out_specs=(vm(), hbm(), hbm(), hbm()),
        scratch_shapes=[v((rows, width), low)]
        + [v((2,) + big, low), v((2 * units, width), low), v((units, width), low)]
        + [v((3, tall, units), low), v(big, low), v((2, units // 4, width), low), v((3,) + half, low)]
        + gather_sems(count)
        + [DMA((4,)), DMA((4,)), DMA((2,)), DMA((3, 2)), DMA, DMA]
        + Reduce.scratch(line, rows, width, low),
        compiler_params=params(ident),
        name="ffn",
    )(tokens, branch, gains, cot, gate_w, up_w, down_w)


def attention_grad_kernel(
    line, groups, seqs,
    lengths, tokens, branch, cot, second, gains, cosine, sine,
    ffn_hbm, normed_hbm, attended_hbm, q_hbm, k_hbm, v_hbm, wq_hbm, wkv_hbm, wo_hbm, sums_hbm, early_hbm,
    mixed, input_grad, gain_out, total_hbm, attn_hbm,
    own, middle_grad, first, ffn_own, dbranch, normed, attended, q, k, v, wq, wkv, wo, da, dk_acc, dv_acc, dq_rows, dk_rows, dv_rows,
    halves, half_in, ffn_parts, sums, sums_in, stage, mine, theirs, mine_in, gain_held, gain_in, gain_sum, gain_all,
    *scratch,
):
    p = Place(line)
    count = 2 * line
    rank = lax.axis_index("grp")
    core = lax.rem(rank, 2)
    partner = rank + 1 - 2 * core
    opposite = lax.rem(rank + 2, groups)
    (
        load_sem, chip_send, chip_recv, half_send, half_recv, stage_send, stage_recv,
        back_send, back_recv, keep_sem, ga_send, ga_recv, gb_send, gb_recv,
    ) = scratch[3:17]
    n = Reduce.N_SCRATCH
    loads = [
        pltpu.make_async_copy(src, dst, load_sem.at[i])
        for i, (src, dst) in enumerate(
            (
                (wo_hbm, wo),
                (ffn_hbm, ffn_parts),
                (attended_hbm, attended),
                (q_hbm, q),
                (k_hbm, k),
                (v_hbm, v),
                (wq_hbm, wq),
                (wkv_hbm, wkv),
                (normed_hbm, normed),
                (early_hbm, sums_in.at[pl.ds(0, EARLY)]),
            )
        )
    ]
    start_all(loads)

    def load_sum(i):
        return pltpu.make_async_copy(sums_hbm.at[i], sums.at[lax.rem(i, 2)], load_sem.at[10 + lax.rem(i, 2)])

    load_sum(0).start()
    load_sum(1).start()
    middle = tokens[...].astype(F32) + branch[...]
    inverse = inverse_rms(middle)
    grad = cot[...].astype(F32)
    grad = jnp.where(row_valid(p, lengths, grad.shape[0]), grad, jnp.zeros_like(grad))
    grad = grad + norm_grad(middle, inverse, gain_row(gains, 1), second[...])
    middle_grad[...] = grad
    own[...] = grad.astype(own.dtype)
    mid_total = jnp.sum(second[...] * middle * inverse, 0, keepdims=True)
    share = gain_held.shape[2]
    for b in range(count):
        gain_held[b] = jnp.zeros(gain_held.shape[1:], F32)
        gain_held[b, 1:2] = mid_total[:, b * share : (b + 1) * share]
    p.greet(groups)
    gather = Gather(p, own, dbranch, *scratch[:3])
    n_sums = sums_hbm.shape[0]
    part_rows = sums.shape[1]

    def chip_copy(i):
        return to_peer(
            "grp", opposite, sums_hbm.at[i], sums_in.at[i], chip_send.at[i], chip_recv.at[i]
        )

    gather.start()

    @pl.loop(EARLY, n_sums)
    def _(i):
        chip_copy(i).start()

    wait_all(loads)
    ffn_sum = Reduce(p, ffn_parts, ffn_own, scratch[17 : 17 + n])
    rows = own.shape[0]
    pair = 2 * rows
    slots = rows // seqs
    low = own.dtype
    scale = 1.0 / math.sqrt(HD)

    @pl.loop(0, line)
    def _(i):
        gather.hop(i + 1)

        @pl.when(i == line - 2)
        def _():
            for first_sends in range(DEPTH):
                ffn_sum.send_across(first_sends)

        d = p.near(i)
        gather.whole(d)
        grad = dot_t(dbranch[pl.ds(2 * d, 2)].reshape(pair, -1), wo[...]).astype(low)
        for block in range(2):
            for m in range(seqs):
                at = pl.ds(pl.multiple_of(d * 2 * slots + block * slots, slots), slots)
                da[m, at] = grad[block * rows + m * slots : block * rows + (m + 1) * slots]

    for i in range(line - 1):
        ffn_sum.b_hop(i)

    chunk = stage.shape[1]

    def to_partner(b):
        return to_peer(
            "grp",
            partner,
            stage.at[b // 2],
            theirs.at[pl.ds(b // 2 * chunk, chunk)],
            stage_send.at[b // 2],
            stage_recv.at[b // 2],
        )

    def gradient(b, left, right):
        value = t_dot(left, right[...].reshape(left.shape[0], -1)).astype(low)
        keep = core == b % 2

        @pl.when(keep)
        def _():
            mine[pl.ds(b // 2 * chunk, chunk)] = value

        @pl.when(jnp.logical_not(keep))
        def _():
            stage[b // 2] = value
            to_partner(b).start()

    total_slots = q.shape[1]
    tile = min(256, total_slots)

    def backward(m):
        dk_acc[...] = jnp.zeros_like(dk_acc)
        dv_acc[...] = jnp.zeros_like(dv_acc)

        def to_rows(target, value, start, size):
            for c in range(size // slots):
                b = start // slots + c
                target[pl.ds(pl.multiple_of(b * rows + m * slots, slots), slots)] = value[
                    c * slots : (c + 1) * slots
                ]

        for t in range(total_slots // tile):
            span = (t + 1) * tile
            at = pl.ds(t * tile, tile)
            query, grad = q[m, at], da[m, at]
            keys, values = k[m, pl.ds(0, span)], v[m, pl.ds(0, span)]
            probs = probabilities(query, keys, t * tile, lengths[m])
            dprobs = dot_t(grad, values)
            inner = jnp.sum(probs * dprobs, -1, keepdims=True)
            dscores = (probs * (dprobs - inner)).astype(low)
            dq = turn_back(dot(dscores, keys) * scale, cosine[at], sine[at])
            to_rows(dq_rows, dq.astype(low), t * tile, tile)
            dk_acc[pl.ds(0, span)] += t_dot(dscores, query)
            dv_acc[pl.ds(0, span)] += t_dot(probs.astype(low), grad)
        dk = turn_back(dk_acc[...] * scale, cosine[...], sine[...])
        to_rows(dk_rows, dk.astype(low), 0, total_slots)
        to_rows(dv_rows, dv_acc[...].astype(low), 0, total_slots)

    half = HD // 2

    def swap():
        return to_peer("shard", p.cross, halves.at[1 - p.y], half_in, half_send, half_recv)

    gradient(0, attended[:, :chunk], dbranch)
    gradient(1, attended[:, chunk:], dbranch)

    @pl.loop(0, seqs)
    def _(m):
        backward(m)
        ffn_sum.hop(m)
        ffn_sum.send_across(m + DEPTH)

    for h in range(2):
        halves[h, 0] = dk_rows[:, h * half : (h + 1) * half]
        halves[h, 1] = dv_rows[:, h * half : (h + 1) * half]
    swap().start()
    gather.drain()
    parts = dbranch
    gradient(2, dq_rows[:, :chunk], normed)
    gradient(3, dq_rows[:, chunk:], normed)

    spans = (pl.ds(0, 2 * chunk), pl.ds(2 * chunk, chunk))

    def attn_chip(part):
        return to_peer(
            "grp",
            opposite,
            mine.at[spans[part]],
            mine_in.at[spans[part]],
            chip_send.at[n_sums + part],
            chip_recv.at[n_sums + part],
        )

    def attn_pair(part, blocks):
        for b in blocks:
            to_partner(2 * b).wait_recv()
        at = mine.at[spans[part]]
        total_into(at, at, theirs.at[spans[part]])
        attn_chip(part).start()

    def back_attn(part):
        size = 2 * chunk if part == 0 else chunk
        start = core * 3 * chunk + part * 2 * chunk
        out = attn_hbm.at[pl.ds(pl.multiple_of(start, chunk), size)]
        at = mine.at[spans[part]]
        sems = keep_sem.at[n_sums + part], back_send.at[n_sums + part], back_recv.at[n_sums + part]
        return pltpu.make_async_copy(at, out, sems[0]), to_peer("grp", partner, at, out, *sems[1:])

    def attn_total(part):
        attn_chip(part).wait()
        at = mine.at[spans[part]]
        total_into(at, at, mine_in.at[spans[part]])
        start_all(back_attn(part))


    @pl.loop(0, line)
    def _(d):
        at = pl.ds(pl.multiple_of(d * pair, pair), pair)
        part = dot(dq_rows[at], wq[...]) + dot(dk_rows[at], wkv[0]) + dot(dv_rows[at], wkv[1])
        parts[pl.ds(2 * d, 2)] = part.astype(low).reshape(2, rows, -1)

    for i in range(seqs, line - 1):
        ffn_sum.hop(i)
    attn_pair(0, (0, 1))
    ffn_sum.finish()
    reduce = Reduce(p, parts, first, scratch[17 + n :])
    for i in range(DEPTH):
        reduce.send_across(i)
    for i in range(line - 1):
        reduce.b_hop(i)

    def summed(which):
        return (halves[p.y, which].astype(F32) + half_in[which].astype(F32)).astype(low)

    valid = row_valid(p, lengths, rows)
    result = tokens[...].astype(F32) + branch[...] + ffn_own[...]
    mixed[...] = jnp.where(valid, result, jnp.zeros_like(result)).astype(low)

    def back(i):
        per_half = n_sums // 3
        start = core * per_half * part_rows + lax.rem(i, per_half) * part_rows
        at = pl.ds(pl.multiple_of(start, part_rows), part_rows)
        out = total_hbm.at[lax.div(i, per_half), at]
        return (
            pltpu.make_async_copy(sums_in.at[i], out, keep_sem.at[i]),
            to_peer("grp", partner, sums_in.at[i], out, back_send.at[i], back_recv.at[i]),
        )

    def sum_up(first_piece, end):
        @pl.loop(first_piece, end)
        def _(i):
            either(i >= EARLY, lambda: chip_copy(i).wait())
            load_sum(i).wait()
            total_into(sums_in.at[i], sums.at[lax.rem(i, 2)], sums_in.at[i])
            either(i + 2 < n_sums, lambda: load_sum(i + 2).start())
            start_all(back(i))

    def gain_copy(step, peer, origin):
        return to_peer(
            "shard", peer, gain_held.at[peer], gain_in.at[origin], ga_send.at[step], ga_recv.at[step]
        )

    def gain_group(step, peer, origin):
        return to_peer(
            "grp", peer, gain_sum, gain_all.at[origin], gb_send.at[step], gb_recv.at[step]
        )

    def gain_first():
        def body(i, total):
            at = pl.ds(pl.multiple_of(i * 16, 16), 16)
            for b in range(count):
                total = total + parts[b, at].astype(F32) * normed[b, at].astype(F32)
            return total

        total = lax.fori_loop(0, rows // 16, body, jnp.zeros((16, parts.shape[2]), F32))
        total = jnp.sum(total, 0, keepdims=True) / gain_row(gains, 0)
        for b in range(count):
            gain_held[b, 0:1] = total[:, b * share : (b + 1) * share]
        for step in range(1, count):
            gain_copy(step, lax.rem(p.me + step, count), p.me).start()

    def gain_second():
        for step in range(1, count):
            gain_copy(step, p.me, lax.rem(p.me + count - step, count)).wait_recv()
        gain_in[p.me] = gain_held[p.me]
        total = gain_in[0]
        for b in range(1, count):
            total = total + gain_in[b]
        gain_sum[...] = total
        gain_all[rank] = total
        for step in range(1, groups):
            gain_group(step, lax.rem(rank + step, groups), rank).start()

    swap().wait_recv()
    gradient(4, summed(0), normed)
    gradient(5, summed(1), normed)
    reduce.hop(0)
    reduce.send_across(DEPTH)
    attn_pair(1, (2,))
    gain_first()
    sum_up(0, n_sums // 2)
    reduce.hop(1)
    reduce.send_across(DEPTH + 1)
    gain_second()
    sum_up(n_sums // 2, n_sums - 3)
    reduce.hop(2)
    sum_up(n_sums - 3, n_sums)
    attn_total(0)
    reduce.finish()
    for step in range(1, groups):
        gain_group(step, rank, lax.rem(rank + groups - step, groups)).wait_recv()
    total = gain_all[0]
    for b in range(1, groups):
        total = total + gain_all[b]
    gain_out[...] = total
    source = tokens[...].astype(F32)
    inner = norm_grad(source, inverse_rms(source), gain_row(gains, 0), first[...])
    input_grad[...] = (middle_grad[...] + inner).astype(low)
    attn_total(1)
    reduce.drain()
    ffn_sum.drain()
    swap().wait_send()
    for b in range(3):
        to_partner(2 * b).wait_send()
    for step in range(1, count):
        gain_copy(step, lax.rem(p.me + step, count), p.me).wait_send()
    for step in range(1, groups):
        gain_group(step, lax.rem(rank + step, groups), rank).wait_send()

    @pl.loop(0, n_sums)
    def _(i):
        wait_all(back(i))

    for part in range(2):
        wait_all(back_attn(part))


def attention_grad(
    lengths, tokens, branch, cot, second, gains, cosine, sine, ffn_parts, normed, attended, q, k, v, wq, wkv, wo, sums, early,
    groups, ident,
):
    rows, width = tokens.shape
    count = normed.shape[0]
    line = count // 2
    seqs, total_slots, hd = q.shape
    low = tokens.dtype
    vmem = pltpu.VMEM
    tall = count * rows
    half = hd // 2
    sums = sums.reshape(-1, PIECE, width)
    early = early.reshape(-1, PIECE, width)
    n_sums, part_rows, _ = sums.shape
    shape = jax.ShapeDtypeStruct
    big = vmem((count, rows, width), low)
    head = vmem((seqs, total_slots, hd), low)
    weight = vmem((hd, width), low)
    flat = vmem((tall, hd), low)
    acc = vmem((total_slots, hd), F32)
    third = vmem((3 * half, width), low)
    g = gains.shape
    block = vmem((rows, width), F32)
    return pl.pallas_call(
        functools.partial(attention_grad_kernel, line, groups, seqs),
        out_shape=(
            shape((rows, width), low),
            shape((rows, width), low),
            shape(g[1:], F32),
            shape((3, n_sums // 3 * 2 * part_rows, width), low),
            shape((6 * half, width), low),
        ),
        in_specs=[scalars()] + [vm()] * 7 + [hbm()] * 11,
        out_specs=(vm(), vm(), vm(), hbm(), hbm()),
        scratch_shapes=[
            vmem((rows, width), low), block, block, block,
            big, big, flat, head, head, head, weight, vmem((2, hd, width), low), weight, head, acc, acc,
            flat, flat, flat,
            vmem((2, 2, tall, half), low), vmem((2, tall, half), low), big,
            vmem((2,) + sums.shape[1:], low), vmem(sums.shape, low), vmem((3, half, width), low), third, third, third,
            vmem(g, F32), vmem(g, F32), vmem(g[1:], F32), vmem((groups,) + g[1:], F32),
        ]
        + gather_sems(count)
        + [
            DMA((12,)), DMA((n_sums + 2,)), DMA((n_sums + 2,)), DMA, DMA, DMA((3,)), DMA((3,)),
            DMA((n_sums + 2,)), DMA((n_sums + 2,)), DMA((n_sums + 2,)),
            DMA((count,)), DMA((count,)), DMA((groups,)), DMA((groups,)),
        ]
        + Reduce.scratch(line, rows, width, low) * 2,
        compiler_params=params(ident),
        name="attention_grad",
    )(
        lengths, tokens, branch, cot, second, gains, cosine, sine, ffn_parts, normed, attended, q, k, v, wq, wkv, wo, sums, early
    )


epsilon = 1e-06
theta_base = 1000042.0
masked_value = -1e30


def turned(source):
    half_width = source.shape[-1] // 2
    return jnp.concatenate([-source[..., half_width:], source[..., :half_width]], -1)


def rotate(source, cosine_table, sine_table):
    return source * cosine_table + turned(source) * sine_table


def unrotate(source, cosine_table, sine_table):
    return source * cosine_table - turned(source) * sine_table


def norm_forward(source, norm_gain):
    inverse = lax.rsqrt(jnp.mean(source * source, -1, keepdims=True) + epsilon)
    return (source * inverse * norm_gain, inverse)


def norm_backward(source, inverse, norm_gain, grad_out):
    weighted = grad_out * norm_gain
    inner_sum = jnp.sum(weighted * source, -1, keepdims=True)
    grad_in = (
        inverse * weighted - source * inverse * inverse * inverse * inner_sum / source.shape[-1]
    )
    return (grad_in, jnp.sum(grad_out * source * inverse, 0))


def weight_terms(normed, query_grad, key_grad, value_grad, attended, branch_grad, shard_count):
    token_count, model_width = normed.shape
    query_share = query_grad.shape[1] // shard_count
    kv_share = key_grad.shape[1] // shard_count
    shard_rows = 2 * query_share + 2 * kv_share

    def weight_term(first_row, row_count):
        blocks = row_count // shard_rows

        def columns(matrix, share_cols):
            return matrix.reshape(token_count, blocks, share_cols)

        part_query = jnp.einsum(
            "tmr,td->mrd",
            columns(query_grad, query_share),
            normed,
            preferred_element_type=jnp.float32,
        )
        part_key = jnp.einsum(
            "tmr,td->mrd", columns(key_grad, kv_share), normed, preferred_element_type=jnp.float32
        )
        part_value = jnp.einsum(
            "tmr,td->mrd", columns(value_grad, kv_share), normed, preferred_element_type=jnp.float32
        )
        part_out = jnp.einsum(
            "tmr,td->mrd",
            columns(attended, query_share),
            branch_grad,
            preferred_element_type=jnp.float32,
        )
        return jnp.concatenate([part_query, part_key, part_value, part_out], 1).reshape(
            row_count, model_width
        )

    return (weight_term, shard_rows)


def local_rows(
    tokens,
    lengths,
    prenorm_gain,
    query_weight,
    key_weight,
    value_weight,
    out_weight,
    midnorm_gain,
    gate_weight,
    up_weight,
    down_weight,
    cotangent,
):
    shard_count = lax.axis_size("shard")
    shard_rank = lax.axis_index("shard")
    micro_count, seq_dev, model_width = tokens.shape
    slot_count = seq_dev * shard_count
    repeat_heads = NH // KVH
    query_width = NH * HD
    kv_width = KVH * HD
    score_scale = 1.0 / math.sqrt(HD)
    local_pos = shard_rank * seq_dev + jnp.arange(seq_dev, dtype=jnp.int32)
    key_pos = jnp.arange(slot_count, dtype=jnp.int32)
    inverse_freq = theta_base ** (-(jnp.arange(0, HD, 2).astype(jnp.float32) / HD))
    angles = local_pos.astype(jnp.float32)[:, None] * inverse_freq[None, :]
    cosine_table = jnp.concatenate([jnp.cos(angles), jnp.cos(angles)], -1)[:, None, :]
    sine_table = jnp.concatenate([jnp.sin(angles), jnp.sin(angles)], -1)[:, None, :]
    gate_total = jnp.zeros(gate_weight.shape, jnp.float32)
    up_total = jnp.zeros(up_weight.shape, jnp.float32)
    down_total = jnp.zeros(down_weight.shape, jnp.float32)
    prenorm_total = jnp.zeros((model_width,), jnp.float32)
    midnorm_total = jnp.zeros((model_width,), jnp.float32)
    attn_total = None
    mixed_rows = []
    input_rows = []
    for micro_index in range(micro_count):
        gathered = (
            lax.all_gather(query_weight, "shard", axis=0, tiled=True),
            lax.all_gather(key_weight, "shard", axis=0, tiled=True),
            lax.all_gather(value_weight, "shard", axis=0, tiled=True),
            lax.all_gather(prenorm_gain, "shard", axis=0, tiled=True),
            lax.all_gather(midnorm_gain, "shard", axis=0, tiled=True),
        )
        query_full, key_full, value_full, prenorm_full, midnorm_full = gathered
        prenorm_f = prenorm_full.astype(jnp.float32)
        midnorm_f = midnorm_full.astype(jnp.float32)
        source = tokens[micro_index].astype(jnp.float32)
        length_now = lengths[micro_index]
        valid_rows = local_pos < length_now
        scaled_first, inverse_first = norm_forward(source, prenorm_f)
        normed_first = scaled_first.astype(jnp.bfloat16)
        query_pre = jnp.einsum(
            "sd,qd->sq", normed_first, query_full, preferred_element_type=jnp.float32
        ).reshape(seq_dev, NH, HD)
        key_pre = jnp.einsum(
            "sd,qd->sq", normed_first, key_full, preferred_element_type=jnp.float32
        ).reshape(seq_dev, KVH, HD)
        value_pre = jnp.einsum(
            "sd,qd->sq", normed_first, value_full, preferred_element_type=jnp.float32
        )
        query_rot = rotate(query_pre, cosine_table, sine_table).astype(jnp.bfloat16)
        key_rot = rotate(key_pre, cosine_table, sine_table).astype(jnp.bfloat16)
        key_value = jnp.concatenate(
            [key_rot.reshape(seq_dev, kv_width), value_pre.astype(jnp.bfloat16)], 1
        )
        kv_all = lax.all_gather(key_value, "shard", axis=0, tiled=True)
        keys_all = kv_all[:, :kv_width].reshape(slot_count, KVH, HD)
        values_all = kv_all[:, kv_width:].reshape(slot_count, KVH, HD)
        query_group = query_rot.reshape(seq_dev, KVH, repeat_heads, HD)
        scores = (
            jnp.einsum("skrd,tkd->krst", query_group, keys_all, preferred_element_type=jnp.float32)
            * score_scale
        )
        allowed = (key_pos[None, :] <= local_pos[:, None]) & (key_pos[None, :] < length_now)
        scores = jnp.where(allowed, scores, masked_value)
        row_max = jnp.max(scores, -1, keepdims=True)
        exp_scores = jnp.exp(scores - row_max)
        attention_probs = exp_scores / jnp.sum(exp_scores, -1, keepdims=True)
        probs_low = attention_probs.astype(jnp.bfloat16)
        attended = (
            jnp.einsum("krst,tkd->skrd", probs_low, values_all, preferred_element_type=jnp.float32)
            .astype(jnp.bfloat16)
            .reshape(seq_dev, query_width)
        )
        branch = jnp.dot(
            attended,
            lax.all_gather(out_weight, "shard", axis=0, tiled=True),
            preferred_element_type=jnp.float32,
        )
        middle = source + branch
        scaled_second, inverse_second = norm_forward(middle, midnorm_f)
        normed_second = scaled_second.astype(jnp.bfloat16)
        normed_all = lax.all_gather(normed_second, "shard", axis=0, tiled=True)
        gate_pre = jnp.einsum(
            "sd,fd->sf", normed_all, gate_weight, preferred_element_type=jnp.float32
        )
        up_pre = jnp.einsum("sd,fd->sf", normed_all, up_weight, preferred_element_type=jnp.float32)
        sigmoid_gate = jax.nn.sigmoid(gate_pre)
        silu_gate = gate_pre * sigmoid_gate
        hidden = (silu_gate * up_pre).astype(jnp.bfloat16)
        ffn_part = lax.psum_scatter(
            jnp.dot(hidden, down_weight, preferred_element_type=jnp.float32).astype(jnp.bfloat16),
            "shard",
            scatter_dimension=0,
            tiled=True,
        ).astype(jnp.float32)
        mixed_rows.append(
            jnp.where(valid_rows[:, None], middle + ffn_part, 0.0).astype(jnp.bfloat16)
        )
        cot_low = jnp.where(
            valid_rows[:, None], cotangent[micro_index], jnp.zeros_like(cotangent[micro_index])
        )
        cot_all = lax.all_gather(cot_low, "shard", axis=0, tiled=True)
        hidden_grad = jnp.einsum(
            "sd,fd->sf", cot_all, down_weight, preferred_element_type=jnp.float32
        )
        down_total = down_total + jnp.einsum(
            "sf,sd->fd", hidden, cot_all, preferred_element_type=jnp.float32
        )
        gate_grad = (
            hidden_grad * up_pre * sigmoid_gate * (1.0 + gate_pre * (1.0 - sigmoid_gate))
        ).astype(jnp.bfloat16)
        up_grad = (hidden_grad * silu_gate).astype(jnp.bfloat16)
        gate_total = gate_total + jnp.einsum(
            "sf,sd->fd", gate_grad, normed_all, preferred_element_type=jnp.float32
        )
        up_total = up_total + jnp.einsum(
            "sf,sd->fd", up_grad, normed_all, preferred_element_type=jnp.float32
        )
        second_grad = lax.psum_scatter(
            jnp.dot(gate_grad, gate_weight, preferred_element_type=jnp.float32)
            + jnp.dot(up_grad, up_weight, preferred_element_type=jnp.float32),
            "shard",
            scatter_dimension=0,
            tiled=True,
        )
        middle_part, midnorm_part = norm_backward(middle, inverse_second, midnorm_f, second_grad)
        middle_grad = cot_low.astype(jnp.float32) + middle_part
        midnorm_total = midnorm_total + midnorm_part
        branch_grad = middle_grad.astype(jnp.bfloat16)
        attended_grad = jnp.einsum(
            "sd,qd->sq",
            branch_grad,
            lax.all_gather(out_weight, "shard", axis=0, tiled=True),
            preferred_element_type=jnp.float32,
        ).astype(jnp.bfloat16)
        attended_group = attended_grad.reshape(seq_dev, KVH, repeat_heads, HD)
        probs_grad = jnp.einsum(
            "skrd,tkd->krst", attended_group, values_all, preferred_element_type=jnp.float32
        )
        inner_sum = jnp.sum(attention_probs * probs_grad, -1, keepdims=True)
        scores_grad = (attention_probs * (probs_grad - inner_sum)).astype(jnp.bfloat16)
        query_rot_grad = (
            jnp.einsum(
                "krst,tkd->skrd", scores_grad, keys_all, preferred_element_type=jnp.float32
            ).reshape(seq_dev, NH, HD)
            * score_scale
        )
        query_grad = (
            unrotate(query_rot_grad, cosine_table, sine_table)
            .astype(jnp.bfloat16)
            .reshape(seq_dev, query_width)
        )
        row_count = lax.axis_size("shard") * seq_dev
        key_part = (
            jnp.einsum(
                "krst,skrd->tkd", scores_grad, query_group, preferred_element_type=jnp.float32
            )
            * score_scale
        )
        value_part = jnp.einsum(
            "krst,skrd->tkd", probs_low, attended_group, preferred_element_type=jnp.float32
        )
        kv_grad = lax.psum_scatter(
            jnp.concatenate(
                [key_part.reshape(row_count, kv_width), value_part.reshape(row_count, kv_width)], 1
            ).astype(jnp.bfloat16),
            "shard",
            scatter_dimension=0,
            tiled=True,
        ).astype(jnp.float32)
        key_grad = (
            unrotate(kv_grad[:, :kv_width].reshape(seq_dev, KVH, HD), cosine_table, sine_table)
            .astype(jnp.bfloat16)
            .reshape(seq_dev, kv_width)
        )
        value_grad = kv_grad[:, kv_width:].astype(jnp.bfloat16)
        first_grad = jnp.einsum(
            "sq,qd->sd", query_grad, query_full, preferred_element_type=jnp.float32
        )
        first_grad = first_grad + jnp.einsum(
            "sq,qd->sd", key_grad, key_full, preferred_element_type=jnp.float32
        )
        first_grad = first_grad + jnp.einsum(
            "sq,qd->sd", value_grad, value_full, preferred_element_type=jnp.float32
        )
        source_part, prenorm_part = norm_backward(source, inverse_first, prenorm_f, first_grad)
        input_rows.append((middle_grad + source_part).astype(jnp.bfloat16))
        prenorm_total = prenorm_total + prenorm_part
        saved = (normed_first, query_grad, key_grad, value_grad, attended, branch_grad)
        weight_term, shard_rows = weight_terms(*saved, shard_count)
        reduced = lax.psum_scatter(
            weight_term(jnp.int32(0), lax.axis_size("shard") * shard_rows).astype(jnp.bfloat16),
            "shard",
            scatter_dimension=0,
            tiled=True,
        ).astype(jnp.float32)
        attn_total = reduced if attn_total is None else attn_total + reduced
    gain_sums = lax.psum((prenorm_total, midnorm_total), ("grp", "shard"))
    gain_share = model_width // shard_count
    prenorm_gradient = lax.dynamic_slice_in_dim(
        gain_sums[0], shard_rank * gain_share, gain_share, 0
    )
    midnorm_gradient = lax.dynamic_slice_in_dim(
        gain_sums[1], shard_rank * gain_share, gain_share, 0
    )
    summed = (
        lax.psum(attn_total.astype(jnp.bfloat16), "grp").astype(jnp.float32),
        lax.psum(gate_total.astype(jnp.bfloat16), "grp").astype(jnp.float32),
        lax.psum(up_total.astype(jnp.bfloat16), "grp").astype(jnp.float32),
        lax.psum(down_total.astype(jnp.bfloat16), "grp").astype(jnp.float32),
    )
    attn_rows = summed[0]
    query_share = query_width // shard_count
    kv_share = kv_width // shard_count
    query_gradient = attn_rows[:query_share]
    key_gradient = attn_rows[query_share : query_share + kv_share]
    value_gradient = attn_rows[query_share + kv_share : query_share + 2 * kv_share]
    out_gradient = attn_rows[query_share + 2 * kv_share :]
    return (
        jnp.stack(mixed_rows),
        jnp.stack(input_rows),
        prenorm_gradient,
        query_gradient,
        key_gradient,
        value_gradient,
        out_gradient,
        midnorm_gradient,
        summed[1],
        summed[2],
        summed[3],
    )


def local_heads(
    tokens,
    lengths,
    prenorm_gain,
    query_weight,
    key_weight,
    value_weight,
    out_weight,
    midnorm_gain,
    gate_weight,
    up_weight,
    down_weight,
    cotangent,
):
    low = jnp.bfloat16
    count = lax.axis_size("shard")
    groups = lax.axis_size("grp")
    seqs, seq_dev, model_width = tokens.shape
    rows = seqs * seq_dev
    inverse_freq = jnp.asarray(theta_base ** (-np.arange(0, HD, 2) / HD), jnp.float32)
    tokens_low = tokens.reshape(rows, model_width)
    cot_low = cotangent.reshape(rows, model_width)
    branch, gains, normed_first, cot_all, queries, keys, values, attended, kv_head, cosine, sine = (
        attention(
            lengths,
            tokens_low,
            cot_low,
            prenorm_gain,
            midnorm_gain,
            inverse_freq[None, :],
            query_weight,
            key_weight,
            value_weight,
            out_weight,
            count,
            groups,
            1,
        )
    )
    second_grad, ffn_parts, pair_sums, early = ffn(
        tokens_low, branch, gains, cot_all, gate_weight, up_weight, down_weight, groups, 2
    )
    mixed, input_gradient, gain_own, totals, attn_total = attention_grad(
        lengths,
        tokens_low,
        branch,
        cot_low,
        second_grad,
        gains,
        cosine,
        sine,
        ffn_parts,
        normed_first,
        attended,
        queries,
        keys,
        values,
        query_weight,
        kv_head,
        out_weight,
        pair_sums,
        early,
        groups,
        3,
    )
    f32 = jnp.float32
    blocks = attn_total.reshape(2, 3, key_weight.shape[0], model_width).astype(f32)
    return (
        mixed.reshape(tokens.shape),
        input_gradient.reshape(tokens.shape),
        gain_own[0],
        blocks[:, 1].reshape(query_weight.shape),
        blocks[0, 2],
        blocks[1, 2],
        blocks[:, 0].reshape(out_weight.shape),
        gain_own[1],
        totals[1].astype(f32),
        totals[2].astype(f32),
        totals[0].astype(f32),
    )


def solution(mesh):
    planes = mesh.shape["shard"] == NH and mesh.shape["grp"] == 4
    local = local_heads if planes else local_rows
    in_specs = (
        P("grp", "shard", None),
        P("grp"),
        P("shard"),
        P("shard", None),
        P("shard", None),
        P("shard", None),
        P("shard", None),
        P("shard"),
        P("shard", None),
        P("shard", None),
        P("shard", None),
        P("grp", "shard", None),
    )
    out_specs = (
        P("grp", "shard", None),
        P("grp", "shard", None),
        P("shard"),
        P("shard", None),
        P("shard", None),
        P("shard", None),
        P("shard", None),
        P("shard"),
        P("shard", None),
        P("shard", None),
        P("shard", None),
    )
    return jax.shard_map(local, mesh=mesh, in_specs=in_specs, out_specs=out_specs, check_vma=False)
```

```python
import functools
import math

import jax
import jax.numpy as jnp
from jax import lax
from jax.experimental import pallas as pl
from jax.experimental.pallas import tpu as pltpu
from jax.sharding import PartitionSpec as P
import numpy as np

NH = 8
KVH = 4
HD = 256
MASKED = -1e30
EPSILON = 1e-06
DEPTH = 2
MESH = pl.DeviceIdType.MESH
F32 = jnp.float32
DMA = pltpu.SemaphoreType.DMA
REST = 16
PIECE = 128
EARLY = 3
CHUNKS = 2


def pieces(rows):
    size = -(-(rows - REST) // (16 * CHUNKS)) * 16
    cuts = [min(i * size, rows - REST) for i in range(CHUNKS + 1)] + [rows]
    return [pl.ds(a, b - a) for a, b in zip(cuts, cuts[1:])]


VMEM_LIMIT = 66_000_000


def either(condition, action):
    pl.when(condition)(action)


def total_into(dst, *srcs):
    step = 16

    @pl.loop(0, dst.shape[0] // step)
    def _(i):
        at = pl.ds(pl.multiple_of(i * step, step), step)
        value = srcs[0][at].astype(F32)
        for src in srcs[1:]:
            value = value + src[at].astype(F32)
        dst[at] = value.astype(dst.dtype)


class Place:
    def __init__(self, line):
        self.line = line
        self.me = lax.axis_index("shard")
        self.z = self.me // 2
        self.y = lax.rem(self.me, 2)
        self.cross = self.me + 1 - 2 * self.y
        self.low_end = self.z == 0
        self.high_end = self.z == line - 1
        near = []
        for z in range(line):
            order = [z]
            for k in range(1, line):
                order += [d for d in (z - k, z + k) if 0 <= d < line]
            near.append(order)
        self.tables = near

    def near(self, i):
        out = jnp.int32(0)
        for z in range(self.line):
            row = jnp.int32(self.tables[z][0])
            for k in range(1, self.line):
                row = jnp.where(i == k, self.tables[z][k], row)
            out = jnp.where(self.z == z, row, out)
        return out

    def far(self, i):
        return self.near(self.line - 1 - i)

    def greet(self, groups):
        barrier = pltpu.get_barrier_semaphore()
        count = 2 * self.line
        rank = lax.axis_index("grp")
        for step in range(1, count):
            pl.semaphore_signal(
                barrier,
                inc=1,
                device_id={"shard": lax.rem(self.me + step, count)},
                device_id_type=MESH,
            )
        for step in range(1, groups):
            pl.semaphore_signal(
                barrier,
                inc=1,
                device_id={"grp": lax.rem(rank + step, groups)},
                device_id_type=MESH,
            )
        pl.semaphore_wait(barrier, count + groups - 2)


class Gather:
    UP, DOWN, CROSS = 0, 1, 2

    def __init__(self, place, own, out, local_sem, send_sem, recv_sem):
        self.p, self.own, self.out = place, own, out
        self.local_sem, self.send_sem, self.recv_sem = local_sem, send_sem, recv_sem
        self.pieces = pieces(own.shape[0])
        self.last = len(self.pieces) - 1

    def copy(self, way, origin, part, own=False):
        p = self.p
        peer = (p.me + 2, p.me - 2, p.cross)[way]
        at = self.pieces[part]
        return pltpu.make_async_remote_copy(
            src_ref=self.own.at[at] if own else self.out.at[origin, at],
            dst_ref=self.out.at[origin, at],
            send_sem=self.send_sem.at[way, origin, part],
            recv_sem=self.recv_sem.at[origin, part],
            device_id={"shard": peer},
            device_id_type=MESH,
        )

    def arrived(self, origin, part):
        self.copy(self.CROSS, origin, part).wait_recv()

    def start(self):
        self.send_own()
        self.pass_rest()

    def send_own(self):
        p = self.p
        pltpu.make_async_copy(self.own, self.out.at[p.me], self.local_sem).start()
        for part in (self.last,) + tuple(range(self.last)):
            self.copy(self.CROSS, p.me, part, True).start()
        for part in range(self.last + 1):
            either(p.z < p.line - 1, lambda: self.copy(self.UP, p.me, part, True).start())
            either(p.z > 0, lambda: self.copy(self.DOWN, p.me, part, True).start())

    def pass_rest(self):
        p = self.p
        self.arrived(p.cross, self.last)
        either(p.z < p.line - 1, lambda: self.copy(self.UP, p.cross, self.last).start())
        either(p.z > 0, lambda: self.copy(self.DOWN, p.cross, self.last).start())
        pltpu.make_async_copy(self.own, self.out.at[p.me], self.local_sem).wait()

    def hop(self, k):
        p = self.p
        below, above = p.me - 2 * k, p.me + 2 * k
        has_below, has_above = p.z - k >= 0, p.z + k < p.line

        def first(origin, part, way, more):
            self.arrived(origin, part)
            self.copy(self.CROSS, origin, part).start()
            either(more, lambda: self.copy(way, origin, part).start())

        def last(origin, other, way, more):
            for block in (origin, other):
                self.arrived(block, self.last)
                either(more, lambda: self.copy(way, block, self.last).start())

        for part in range(self.last):
            either(has_below, lambda: first(below, part, self.UP, p.z < p.line - 1))
            either(has_above, lambda: first(above, part, self.DOWN, p.z > 0))
        either(has_below, lambda: last(below, p.cross - 2 * k, self.UP, p.z < p.line - 1))
        either(has_above, lambda: last(above, p.cross + 2 * k, self.DOWN, p.z > 0))

    def whole(self, position):
        for part in range(self.last):
            self.arrived(2 * position + 1 - self.p.y, part)

    def drain(self):
        p = self.p

        @pl.loop(0, p.line)
        def _(d):
            mine, other = 2 * d + p.y, 2 * d + 1 - p.y
            for part in range(self.last):
                self.copy(self.CROSS, mine, part).wait_send()

            @pl.when(d == p.z)
            def _():
                self.copy(self.CROSS, mine, self.last).wait_send()

            def line_sent(way):
                for part in range(self.last + 1):
                    self.copy(way, mine, part).wait_send()
                self.copy(way, other, self.last).wait_send()

            either((d <= p.z) & (p.z < p.line - 1), lambda: line_sent(self.UP))
            either((d >= p.z) & (p.z > 0), lambda: line_sent(self.DOWN))


class Reduce:
    BUP, BDN, BX = 0, 2, 4
    UP, DOWN, CROSS = 5, 5 + CHUNKS, 5 + 2 * CHUNKS
    WAYS = 5 + 3 * CHUNKS
    N_SCRATCH = 9

    @staticmethod
    def scratch(line, rows, width, dtype):
        v = pltpu.VMEM
        return (
            [v((line, rows - REST, width), dtype)] * 3
            + [v((line, 2, REST, width), dtype)] * 2
            + [v((REST, width), dtype)] * 2
            + [DMA((Reduce.WAYS, line)), DMA((Reduce.WAYS, line))]
        )

    def __init__(self, place, parts, out, scratch):
        self.p, self.parts, self.out = place, parts, out
        self.cross_in, self.up_in, self.down_in, self.bup_in, self.bdn_in = scratch[:5]
        self.bx_out, self.bx_in, self.send_sem, self.recv_sem = scratch[5:]
        self.pieces = pieces(parts.shape[1])
        self.b = self.pieces[-1]

    def desc(self, way, slot, src, dst, peer):
        return pltpu.make_async_remote_copy(
            src_ref=src,
            dst_ref=dst,
            send_sem=self.send_sem.at[way, slot],
            recv_sem=self.recv_sem.at[way, slot],
            device_id={"shard": peer},
            device_id_type=MESH,
        )

    def cross_copy(self, d, c):
        p, at = self.p, self.pieces[c]
        return self.desc(
            self.CROSS + c,
            d,
            self.parts.at[2 * d + 1 - p.y, at],
            self.cross_in.at[d, at],
            p.cross,
        )

    def line_copy(self, up, d, c):
        p, at = self.p, self.pieces[c]
        came = self.up_in if up else self.down_in
        return self.desc(
            (self.UP if up else self.DOWN) + c,
            d,
            self.cross_in.at[d, at],
            came.at[d, at],
            p.me + 2 if up else p.me - 2,
        )

    def b_copy(self, up, d, o, src=None):
        p = self.p
        held = self.bup_in if up else self.bdn_in
        return self.desc(
            (self.BUP if up else self.BDN) + o,
            d,
            held.at[d, o] if src is None else src,
            held.at[d, o],
            p.me + 2 if up else p.me - 2,
        )

    def bx_copy(self):
        return self.desc(self.BX, 0, self.bx_out, self.bx_in, self.p.cross)

    def column(self, o):
        return self.p.y if o == 0 else 1 - self.p.y

    def send_across(self, i):
        for c in range(CHUNKS):
            self.cross_copy(self.p.far(i), c).start()

    def b_hop(self, i):
        p = self.p
        d = p.far(i)

        def go(up):
            first = p.low_end if up else p.high_end
            held = self.bup_in if up else self.bdn_in
            for o in (1, 0):
                mine = self.parts.at[2 * d + self.column(o), self.b]
                either(first, lambda: self.b_copy(up, d, o, mine).start())

                @pl.when(jnp.logical_not(first))
                def _():
                    self.b_copy(up, d, o).wait_recv()
                    total_into(held.at[d, o], mine, held.at[d, o])
                    self.b_copy(up, d, o).start()

        either(d > p.z, lambda: go(True))
        either(d < p.z, lambda: go(False))

    def hop(self, i):
        for c in range(CHUNKS):
            self.step(i, c)

    def step(self, i, c):
        p = self.p
        d = p.far(i)
        self.cross_copy(d, c).wait_recv()
        at = self.pieces[c]
        mine = self.parts.at[2 * d + p.y, at]
        held = self.cross_in.at[d, at]

        def go(up):
            first = p.low_end if up else p.high_end
            came = self.up_in if up else self.down_in
            either(first, lambda: total_into(held, mine, held))

            @pl.when(jnp.logical_not(first))
            def _():
                self.line_copy(up, d, c).wait_recv()
                total_into(held, mine, held, came.at[d, at])

            self.line_copy(up, d, c).start()

        either(d > p.z, lambda: go(True))
        either(d < p.z, lambda: go(False))

    def close(self, dst, mine, ups, downs):
        p = self.p
        either(p.low_end, lambda: total_into(dst, *mine, downs))
        either(p.high_end, lambda: total_into(dst, *mine, ups))
        either(
            jnp.logical_not(p.low_end | p.high_end), lambda: total_into(dst, *mine, ups, downs)
        )

    def finish(self):
        p = self.p
        for o in (1, 0):
            either(jnp.logical_not(p.low_end), lambda: self.b_copy(True, p.z, o).wait_recv())
            either(jnp.logical_not(p.high_end), lambda: self.b_copy(False, p.z, o).wait_recv())
            if o:
                mine = self.parts.at[2 * p.z + self.column(o), self.b]
                self.close(self.bx_out, (mine,), self.bup_in.at[p.z, o], self.bdn_in.at[p.z, o])
                self.bx_copy().start()
        self.bx_copy().wait_recv()
        self.close(
            self.out.at[self.b],
            (self.parts.at[p.me, self.b], self.bx_in),
            self.bup_in.at[p.z, 0],
            self.bdn_in.at[p.z, 0],
        )
        for c in range(CHUNKS):
            self.cross_copy(p.z, c).wait_recv()
            either(jnp.logical_not(p.low_end), lambda: self.line_copy(True, p.z, c).wait_recv())
            either(jnp.logical_not(p.high_end), lambda: self.line_copy(False, p.z, c).wait_recv())
            at = self.pieces[c]
            self.close(
                self.out.at[at],
                (self.parts.at[p.me, at], self.cross_in.at[p.z, at]),
                self.up_in.at[p.z, at],
                self.down_in.at[p.z, at],
            )

    def drain(self):
        p = self.p
        self.bx_copy().wait_send()

        @pl.loop(0, p.line)
        def _(d):
            def line_sent(up):
                for c in range(CHUNKS):
                    self.line_copy(up, d, c).wait_send()
                self.b_copy(up, d, 0).wait_send()
                self.b_copy(up, d, 1).wait_send()

            for c in range(CHUNKS):
                self.cross_copy(d, c).wait_send()
            either(d > p.z, lambda: line_sent(True))
            either(d < p.z, lambda: line_sent(False))


def dot(a, b):
    return jnp.dot(a, b, preferred_element_type=F32)


def dot_t(a, b):
    return lax.dot_general(a, b, (((1,), (1,)), ((), ())), preferred_element_type=F32)


def t_dot(a, b):
    return lax.dot_general(a, b, (((0,), (0,)), ((), ())), preferred_element_type=F32)


def to_peer(axis, peer, src, dst, send_sem, recv_sem):
    return pltpu.make_async_remote_copy(
        src_ref=src,
        dst_ref=dst,
        send_sem=send_sem,
        recv_sem=recv_sem,
        device_id={axis: peer},
        device_id_type=MESH,
    )


def turn_by(v, cosine, sine):
    half = v.shape[-1] // 2
    a, b = v[:, :half], v[:, half:]
    return jnp.concatenate([a * cosine - b * sine, b * cosine + a * sine], -1)


def turn_back(v, cosine, sine):
    return turn_by(v, cosine, -sine)


def probabilities(query, keys, rows_from, limit):
    scores = dot_t(query, keys) * (1.0 / math.sqrt(HD))
    row = lax.broadcasted_iota(jnp.int32, scores.shape, 0) + rows_from
    col = lax.broadcasted_iota(jnp.int32, scores.shape, 1)
    scores = jnp.where((col <= row) & (col < limit), scores, MASKED)
    weight = jnp.exp(scores - jnp.max(scores, -1, keepdims=True))
    return weight / jnp.sum(weight, -1, keepdims=True)


def row_valid(place, lengths, rows):
    slots = rows // lengths.shape[0]
    row = lax.broadcasted_iota(jnp.int32, (rows, 1), 0)
    limit = jnp.full((rows, 1), lengths[0], jnp.int32)
    for n in range(1, lengths.shape[0]):
        limit = jnp.where(row >= n * slots, lengths[n], limit)
    return place.me * slots + lax.rem(row, slots) < limit


def gain_row(shares, which):
    return jnp.concatenate([shares[b, which : which + 1] for b in range(shares.shape[0])], 1)


def inverse_rms(x):
    return lax.rsqrt(jnp.mean(x * x, -1, keepdims=True) + EPSILON)


def norm_grad(x, inverse, gain, grad):
    weighted = grad * gain
    inner = jnp.sum(weighted * x, -1, keepdims=True)
    return inverse * weighted - x * inverse * inverse * inverse * inner / x.shape[-1]


def start_all(copies):
    for c in copies:
        c.start()


def wait_all(copies):
    for c in copies:
        c.wait()


def scalars():
    return pl.BlockSpec(memory_space=pltpu.SMEM)


def hbm():
    return pl.BlockSpec(memory_space=pl.ANY)


def vm():
    return pl.BlockSpec(memory_space=pltpu.VMEM)


def params(ident):
    return pltpu.CompilerParams(
        collective_id=ident, has_side_effects=True, vmem_limit_bytes=VMEM_LIMIT
    )


def gather_sems(count):
    return [DMA, DMA((3, count, CHUNKS + 1)), DMA((count, CHUNKS + 1))]


def attention_kernel(
    line, groups, seqs,
    lengths, own, cot_raw, pre_gain, mid_gain, freq, wq_hbm, wk_hbm, wv_hbm, wo_hbm,
    branch, small_out, normed_hbm, cot_hbm, q_hbm, k_hbm, v_hbm, attended_hbm, wkv_hbm, cos_hbm, sin_hbm,
    small, cot_own, rows_all, normed, cot_all, q, k, v, attended, wq, wkv, wo, cosine, sine, parts,
    *scratch,
):
    p = Place(line)
    count = 2 * line
    rank = lax.axis_index("grp")
    g1, g2 = scratch[:3], scratch[3:6]
    (load_sem, small_send, small_recv, wy_send, wg_send, w_recv, save_sem) = scratch[6:13]
    r_scratch = scratch[13:]
    half = wk_hbm.shape[0]
    piece = half // 2
    at_own = pl.ds(pl.multiple_of(p.y * half, half), half)
    loads = [
        pltpu.make_async_copy(src, dst, load_sem.at[i])
        for i, (src, dst) in enumerate(
            (
                (wk_hbm, wkv.at[0, at_own]),
                (wv_hbm, wkv.at[1, at_own]),
                (wq_hbm, wq),
                (wo_hbm, wo),
            )
        )
    ]
    start_all(loads)
    p.greet(groups)

    small[...] = jnp.zeros_like(small)
    small[0:1] = pre_gain[...].astype(F32)[None, :]
    small[1:2] = mid_gain[...].astype(F32)[None, :]

    def small_copy(step, peer, origin):
        return to_peer(
            "shard", peer, small, small_out.at[origin], small_send.at[step], small_recv.at[step]
        )

    for step in range(1, count):
        small_copy(step, lax.rem(p.me + step, count), p.me).start()
    gather = Gather(p, own, rows_all, *g1)
    gather.start()
    cots = Gather(p, cot_own, cot_all, *g2)
    small_out[p.me] = small[...]

    def rows_of(quarter, column):
        return wkv.at[
            quarter // 2,
            pl.ds(pl.multiple_of(column * half + lax.rem(quarter, 2) * piece, piece), piece),
        ]

    def across():
        ref = rows_of(rank, p.y)
        return to_peer("shard", p.cross, ref, ref, wy_send, w_recv.at[rank])

    def share(step):
        ref = rows_of(rank, 1 - p.y)
        return to_peer(
            "grp", lax.rem(rank + step, groups), ref, ref, wg_send.at[step], w_recv.at[rank]
        )

    wait_all(loads)
    across().start()
    pos = lax.broadcasted_iota(jnp.int32, cosine.shape, 0).astype(F32)
    angle = pos * freq[...]
    cosine[...] = jnp.cos(angle)
    sine[...] = jnp.sin(angle)
    cot = cot_raw[...]
    cot_own[...] = jnp.where(row_valid(p, lengths, cot.shape[0]), cot, jnp.zeros_like(cot))
    gather.hop(1)
    for step in range(1, count):
        small_copy(step, p.me, lax.rem(p.me + count - step, count)).wait_recv()
    gain = gain_row(small_out, 0)
    across().wait_recv()
    for step in range(1, groups):
        share(step).start()
    rows = own.shape[0]
    pair = 2 * rows
    slots = rows // seqs
    low = own.dtype
    for step in range(1, groups):
        quarter = lax.rem(rank + step, groups)
        ref = rows_of(quarter, 1 - p.y)
        to_peer("grp", rank, ref, ref, wg_send.at[step], w_recv.at[quarter]).wait_recv()

    @pl.loop(0, line)
    def _(i):
        d = p.near(i)
        gather.whole(d)
        x = rows_all[pl.ds(2 * d, 2)].reshape(pair, -1).astype(F32)
        n = (x * inverse_rms(x) * gain).astype(low)
        normed[pl.ds(2 * d, 2)] = n.reshape(2, rows, -1)
        at = pl.ds(pl.multiple_of(d * 2 * slots, 2 * slots), 2 * slots)
        c, s = cosine[at], sine[at]

        def by_rows(t):
            return jnp.concatenate([t[:slots]] * seqs + [t[slots:]] * seqs, 0)

        c, s = by_rows(c), by_rows(s)

        def put(target, value):
            for block in range(2):
                for m in range(seqs):
                    to = pl.ds(
                        pl.multiple_of(d * 2 * slots + block * slots, slots), slots
                    )
                    target[m, to] = value[block * rows + m * slots : block * rows + (m + 1) * slots]

        put(q, turn_by(dot_t(n, wq[...]), c, s).astype(low))
        put(k, turn_by(dot_t(n, wkv[0]), c, s).astype(low))
        put(v, dot_t(n, wkv[1]).astype(low))
        gather.hop(i + 2)
        either(i == line - 3, cots.send_own)

    saves = [
        pltpu.make_async_copy(src, dst, save_sem.at[i])
        for i, (src, dst) in enumerate(
            (
                (normed, normed_hbm),
                (q, q_hbm),
                (k, k_hbm),
                (v, v_hbm),
                (wkv, wkv_hbm),
                (cosine, cos_hbm),
                (sine, sin_hbm),
            )
        )
    ]
    start_all(saves)
    cots.pass_rest()
    total_slots = q.shape[1]
    tile = min(256, total_slots)

    @pl.loop(0, seqs)
    def _(n):
        for t in range(total_slots // tile):
            span = (t + 1) * tile
            at = pl.ds(t * tile, tile)
            probs = probabilities(q[n, at], k[n, pl.ds(0, span)], t * tile, lengths[n])
            out = dot(probs.astype(low), v[n, pl.ds(0, span)]).astype(low)
            for c in range(tile // slots):
                b = (t * tile) // slots + c
                attended[pl.ds(pl.multiple_of(b * rows + n * slots, slots), slots)] = out[
                    c * slots : (c + 1) * slots
                ]
        cots.hop(n + 1)

    for h in range(seqs + 1, line):
        cots.hop(h)

    @pl.loop(0, line)
    def _(d):
        at = pl.ds(pl.multiple_of(d * pair, pair), pair)
        parts[pl.ds(2 * d, 2)] = dot(attended[at], wo[...]).astype(low).reshape(2, rows, -1)

    reduce = Reduce(p, parts, branch, r_scratch)
    saves2 = [pltpu.make_async_copy(attended, attended_hbm, save_sem.at[7])]
    start_all(saves2)
    for d in range(line):
        cots.whole(d)
    for i in range(DEPTH):
        reduce.send_across(i)
    saves3 = [pltpu.make_async_copy(cot_all, cot_hbm, save_sem.at[8])]
    start_all(saves3)
    for i in range(line - 1):
        reduce.b_hop(i)
    for i in range(line - 1):
        reduce.hop(i)
        if i + DEPTH < line:
            reduce.send_across(i + DEPTH)
    reduce.finish()
    reduce.drain()
    gather.drain()
    cots.drain()
    wait_all(saves + saves2 + saves3)
    across().wait_send()
    for step in range(1, groups):
        share(step).wait_send()
    for step in range(1, count):
        small_copy(step, lax.rem(p.me + step, count), p.me).wait_send()


def attention(lengths, own, cot, pre_gain, mid_gain, freq, wq, wk, wv, wo, count, groups, ident):
    rows, width = own.shape
    seqs = lengths.shape[0]
    total_slots = count * rows // seqs
    small = (8, pre_gain.shape[0])
    line = count // 2
    low = own.dtype
    v = pltpu.VMEM
    shape = jax.ShapeDtypeStruct
    hd = wq.shape[0]
    big = (count, rows, width)
    head = (seqs, total_slots, hd)
    table = (total_slots, hd // 2)
    flat = (count * rows, hd)
    return pl.pallas_call(
        functools.partial(attention_kernel, line, groups, seqs),
        out_shape=(
            shape((rows, width), F32),
            shape((count,) + small, F32),
            shape(big, low),
            shape(big, low),
            shape(head, low),
            shape(head, low),
            shape(head, low),
            shape(flat, low),
            shape((2, hd, width), low),
            shape(table, F32),
            shape(table, F32),
        ),
        in_specs=[scalars()] + [vm()] * 5 + [hbm()] * 4,
        out_specs=(vm(), vm()) + (hbm(),) * 9,
        scratch_shapes=[
            v(small, F32), v((rows, width), low), v(big, low), v(big, low), v(big, low), v(head, low), v(head, low), v(head, low), v(flat, low),
            v((hd, width), low), v((2, hd, width), low), v((hd, width), low), v(table, F32), v(table, F32), v(big, low),
        ]
        + gather_sems(count) * 2
        + [DMA((4,)), DMA((count,)), DMA((count,)), DMA, DMA((groups,)), DMA((groups,)), DMA((9,))]
        + Reduce.scratch(line, rows, width, low),
        compiler_params=params(ident),
        name="attention",
    )(lengths, own, cot, pre_gain, mid_gain, freq, wq, wk, wv, wo)


def ffn_kernel(
    line, groups,
    tokens, branch, gains, cot_hbm, gate_hbm, up_hbm, down_hbm,
    second, ffn_hbm, pair_hbm, chip_in,
    own, rights, gate_up, down_w, lefts, parts, stage, theirs,
    *scratch,
):
    p = Place(line)
    rank = lax.axis_index("grp")
    core = lax.rem(rank, 2)
    partner = rank + 1 - 2 * core
    opposite = lax.rem(rank + 2, groups)
    (load_sem, out_sem, stage_send, stage_recv, chip_send, chip_recv) = scratch[3:9]
    units = down_w.shape[0]
    gate_w, up_w = gate_up.at[pl.ds(0, units)], gate_up.at[pl.ds(units, units)]
    cot, normed = rights.at[0], rights.at[1]
    hidden, gate_g, up_g = lefts.at[0], lefts.at[1], lefts.at[2]
    loads = [
        pltpu.make_async_copy(src, dst, load_sem.at[i])
        for i, (src, dst) in enumerate(
            ((gate_hbm, gate_w), (up_hbm, up_w), (cot_hbm, cot), (down_hbm, down_w))
        )
    ]
    start_all(loads)
    middle = tokens[...].astype(F32) + branch[...]
    own[...] = (middle * inverse_rms(middle) * gain_row(gains, 1)).astype(own.dtype)
    p.greet(groups)
    gather = Gather(p, own, normed, *scratch[:3])
    gather.start()
    wait_all(loads)
    rows = own.shape[0]
    pair = 2 * rows
    low = own.dtype

    @pl.loop(0, line)
    def _(i):
        gather.hop(i + 1)
        d = p.near(i)
        gather.whole(d)
        x = normed[pl.ds(2 * d, 2)].reshape(pair, -1)
        g = dot_t(x, gate_w[...])
        u = dot_t(x, up_w[...])
        dh = dot_t(cot[pl.ds(2 * d, 2)].reshape(pair, -1), down_w[...])
        s = 1.0 / (1.0 + jnp.exp(-g))
        silu = g * s
        at = pl.ds(pl.multiple_of(d * pair, pair), pair)
        hidden[at] = (silu * u).astype(low)
        up_g[at] = (dh * silu).astype(low)
        gate_g[at] = (dh * u * s * (1.0 + g * (1.0 - s))).astype(low)
        part = dot(gate_g[at], gate_w[...]) + dot(up_g[at], up_w[...])
        parts[pl.ds(2 * d, 2)] = part.astype(low).reshape(2, rows, -1)

    reduce = Reduce(p, parts, second, scratch[9:])
    for i in range(line):
        reduce.send_across(i)

    quarter = units // 4
    half = units // 2

    def mine(which):
        start = lax.rem(which + 2, 3) * half
        return gate_up.at[pl.ds(pl.multiple_of(start, half), half)]

    def to_partner(which, j):
        return to_peer(
            "grp",
            partner,
            stage.at[j],
            theirs.at[which, pl.ds(pl.multiple_of(j * quarter, quarter), quarter)],
            stage_send.at[j],
            stage_recv.at[which, j],
        )

    def chip_copy():
        return to_peer(
            "grp",
            opposite,
            gate_up.at[pl.ds(2 * half, chip_in.shape[0])],
            chip_in,
            chip_send,
            chip_recv,
        )

    def save_pair(which):
        return pltpu.make_async_copy(mine(which), pair_hbm.at[which], out_sem.at[which])

    @pl.loop(0, 3)
    def _(which):
        right = rights.at[jnp.minimum(which, 1)]

        def block(q):
            cols = pl.ds(pl.multiple_of(q * quarter, quarter), quarter)
            left = lefts[which, :, cols]
            return t_dot(left, right[...].reshape(left.shape[0], -1)).astype(low)

        @pl.loop(0, 2)
        def _(j):
            either(which > 0, lambda: to_partner(which - 1, j).wait_send())
            stage[j] = block(2 * (1 - core) + j)
            to_partner(which, j).start()

        @pl.when(which == 0)
        def _():
            for i in range(line - 1):
                reduce.b_hop(i)

        at_end = p.low_end | p.high_end
        either(at_end, lambda: reduce.step(which, 0))

        @pl.loop(0, 2)
        def _(j):
            at = pl.ds(pl.multiple_of(j * quarter, quarter), quarter)
            mine(which)[at] = block(2 * core + j)

        @pl.when(at_end)
        def _():
            for c in range(1, CHUNKS):
                reduce.step(which, c)

        for j in range(2):
            to_partner(which, j).wait_recv()
        total_into(mine(which), mine(which), theirs.at[which])
        either(which == 0, lambda: chip_copy().start())
        save_pair(which).start()

        @pl.when(jnp.logical_not(at_end))
        def _():
            for c in range(CHUNKS):
                reduce.step(which, c)

    gather.drain()

    @pl.loop(0, line)
    def _(d):
        at = pl.ds(pl.multiple_of(d * pair, pair), pair)
        normed[pl.ds(2 * d, 2)] = dot(hidden[at], down_w[...]).astype(low).reshape(2, rows, -1)

    ffn_save = pltpu.make_async_copy(normed, ffn_hbm, out_sem.at[3])
    ffn_save.start()
    reduce.finish()
    for j in range(2):
        to_partner(2, j).wait_send()

    reduce.drain()
    chip_copy().wait()
    ffn_save.wait()
    for which in range(3):
        save_pair(which).wait()


def ffn(tokens, branch, gains, cot, gate_w, up_w, down_w, groups, ident):
    rows, width = tokens.shape
    count = cot.shape[0]
    line = count // 2
    units = gate_w.shape[0]
    low = tokens.dtype
    v = pltpu.VMEM
    tall = count * rows
    shape = jax.ShapeDtypeStruct
    big = (count, rows, width)
    half = (units // 2, width)
    return pl.pallas_call(
        functools.partial(ffn_kernel, line, groups),
        out_shape=(
            shape((rows, width), F32),
            shape(big, low),
            shape((3,) + half, low),
            shape((EARLY * PIECE, width), low),
        ),
        in_specs=[vm()] * 3 + [hbm()] * 4,
        out_specs=(vm(), hbm(), hbm(), hbm()),
        scratch_shapes=[v((rows, width), low)]
        + [v((2,) + big, low), v((2 * units, width), low), v((units, width), low)]
        + [v((3, tall, units), low), v(big, low), v((2, units // 4, width), low), v((3,) + half, low)]
        + gather_sems(count)
        + [DMA((4,)), DMA((4,)), DMA((2,)), DMA((3, 2)), DMA, DMA]
        + Reduce.scratch(line, rows, width, low),
        compiler_params=params(ident),
        name="ffn",
    )(tokens, branch, gains, cot, gate_w, up_w, down_w)


def attention_grad_kernel(
    line, groups, seqs,
    lengths, tokens, branch, cot, second, gains, cosine, sine,
    ffn_hbm, normed_hbm, attended_hbm, q_hbm, k_hbm, v_hbm, wq_hbm, wkv_hbm, wo_hbm, sums_hbm, early_hbm,
    mixed, input_grad, gain_out, total_hbm, attn_hbm,
    own, middle_grad, first, ffn_own, dbranch, normed, attended, q, k, v, wq, wkv, wo, da, dk_acc, dv_acc, dq_rows, dk_rows, dv_rows,
    halves, half_in, ffn_parts, sums, sums_in, stage, mine, theirs, mine_in, gain_held, gain_in, gain_sum, gain_all,
    *scratch,
):
    p = Place(line)
    count = 2 * line
    rank = lax.axis_index("grp")
    core = lax.rem(rank, 2)
    partner = rank + 1 - 2 * core
    opposite = lax.rem(rank + 2, groups)
    (
        load_sem, chip_send, chip_recv, half_send, half_recv, stage_send, stage_recv,
        back_send, back_recv, keep_sem, ga_send, ga_recv, gb_send, gb_recv,
    ) = scratch[3:17]
    n = Reduce.N_SCRATCH
    loads = [
        pltpu.make_async_copy(src, dst, load_sem.at[i])
        for i, (src, dst) in enumerate(
            (
                (wo_hbm, wo),
                (ffn_hbm, ffn_parts),
                (attended_hbm, attended),
                (q_hbm, q),
                (k_hbm, k),
                (v_hbm, v),
                (wq_hbm, wq),
                (wkv_hbm, wkv),
                (normed_hbm, normed),
                (early_hbm, sums_in.at[pl.ds(0, EARLY)]),
            )
        )
    ]
    start_all(loads)

    def load_sum(i):
        return pltpu.make_async_copy(sums_hbm.at[i], sums.at[lax.rem(i, 2)], load_sem.at[10 + lax.rem(i, 2)])

    load_sum(0).start()
    load_sum(1).start()
    middle = tokens[...].astype(F32) + branch[...]
    inverse = inverse_rms(middle)
    grad = cot[...].astype(F32)
    grad = jnp.where(row_valid(p, lengths, grad.shape[0]), grad, jnp.zeros_like(grad))
    grad = grad + norm_grad(middle, inverse, gain_row(gains, 1), second[...])
    middle_grad[...] = grad
    own[...] = grad.astype(own.dtype)
    mid_total = jnp.sum(second[...] * middle * inverse, 0, keepdims=True)
    share = gain_held.shape[2]
    for b in range(count):
        gain_held[b] = jnp.zeros(gain_held.shape[1:], F32)
        gain_held[b, 1:2] = mid_total[:, b * share : (b + 1) * share]
    p.greet(groups)
    gather = Gather(p, own, dbranch, *scratch[:3])
    n_sums = sums_hbm.shape[0]
    part_rows = sums.shape[1]

    def chip_copy(i):
        return to_peer(
            "grp", opposite, sums_hbm.at[i], sums_in.at[i], chip_send.at[i], chip_recv.at[i]
        )

    gather.start()

    @pl.loop(EARLY, n_sums)
    def _(i):
        chip_copy(i).start()

    wait_all(loads)
    ffn_sum = Reduce(p, ffn_parts, ffn_own, scratch[17 : 17 + n])
    rows = own.shape[0]
    pair = 2 * rows
    slots = rows // seqs
    low = own.dtype
    scale = 1.0 / math.sqrt(HD)

    @pl.loop(0, line)
    def _(i):
        gather.hop(i + 1)

        @pl.when(i == line - 2)
        def _():
            for first_sends in range(DEPTH):
                ffn_sum.send_across(first_sends)

        d = p.near(i)
        gather.whole(d)
        grad = dot_t(dbranch[pl.ds(2 * d, 2)].reshape(pair, -1), wo[...]).astype(low)
        for block in range(2):
            for m in range(seqs):
                at = pl.ds(pl.multiple_of(d * 2 * slots + block * slots, slots), slots)
                da[m, at] = grad[block * rows + m * slots : block * rows + (m + 1) * slots]

    for i in range(line - 1):
        ffn_sum.b_hop(i)

    chunk = stage.shape[1]

    def to_partner(b):
        return to_peer(
            "grp",
            partner,
            stage.at[b // 2],
            theirs.at[pl.ds(b // 2 * chunk, chunk)],
            stage_send.at[b // 2],
            stage_recv.at[b // 2],
        )

    def gradient(b, left, right):
        value = t_dot(left, right[...].reshape(left.shape[0], -1)).astype(low)
        keep = core == b % 2

        @pl.when(keep)
        def _():
            mine[pl.ds(b // 2 * chunk, chunk)] = value

        @pl.when(jnp.logical_not(keep))
        def _():
            stage[b // 2] = value
            to_partner(b).start()

    total_slots = q.shape[1]
    tile = min(256, total_slots)

    def backward(m):
        dk_acc[...] = jnp.zeros_like(dk_acc)
        dv_acc[...] = jnp.zeros_like(dv_acc)

        def to_rows(target, value, start, size):
            for c in range(size // slots):
                b = start // slots + c
                target[pl.ds(pl.multiple_of(b * rows + m * slots, slots), slots)] = value[
                    c * slots : (c + 1) * slots
                ]

        for t in range(total_slots // tile):
            span = (t + 1) * tile
            at = pl.ds(t * tile, tile)
            query, grad = q[m, at], da[m, at]
            keys, values = k[m, pl.ds(0, span)], v[m, pl.ds(0, span)]
            probs = probabilities(query, keys, t * tile, lengths[m])
            dprobs = dot_t(grad, values)
            inner = jnp.sum(probs * dprobs, -1, keepdims=True)
            dscores = (probs * (dprobs - inner)).astype(low)
            dq = turn_back(dot(dscores, keys) * scale, cosine[at], sine[at])
            to_rows(dq_rows, dq.astype(low), t * tile, tile)
            dk_acc[pl.ds(0, span)] += t_dot(dscores, query)
            dv_acc[pl.ds(0, span)] += t_dot(probs.astype(low), grad)
        dk = turn_back(dk_acc[...] * scale, cosine[...], sine[...])
        to_rows(dk_rows, dk.astype(low), 0, total_slots)
        to_rows(dv_rows, dv_acc[...].astype(low), 0, total_slots)

    half = HD // 2

    def swap():
        return to_peer("shard", p.cross, halves.at[1 - p.y], half_in, half_send, half_recv)

    gradient(0, attended[:, :chunk], dbranch)
    gradient(1, attended[:, chunk:], dbranch)

    @pl.loop(0, seqs)
    def _(m):
        backward(m)
        ffn_sum.hop(m)
        ffn_sum.send_across(m + DEPTH)

    for h in range(2):
        halves[h, 0] = dk_rows[:, h * half : (h + 1) * half]
        halves[h, 1] = dv_rows[:, h * half : (h + 1) * half]
    swap().start()
    gather.drain()
    parts = dbranch
    gradient(2, dq_rows[:, :chunk], normed)
    gradient(3, dq_rows[:, chunk:], normed)

    spans = (pl.ds(0, 2 * chunk), pl.ds(2 * chunk, chunk))

    def attn_chip(part):
        return to_peer(
            "grp",
            opposite,
            mine.at[spans[part]],
            mine_in.at[spans[part]],
            chip_send.at[n_sums + part],
            chip_recv.at[n_sums + part],
        )

    def attn_pair(part, blocks):
        for b in blocks:
            to_partner(2 * b).wait_recv()
        at = mine.at[spans[part]]
        total_into(at, at, theirs.at[spans[part]])
        attn_chip(part).start()

    def back_attn(part):
        size = 2 * chunk if part == 0 else chunk
        start = core * 3 * chunk + part * 2 * chunk
        out = attn_hbm.at[pl.ds(pl.multiple_of(start, chunk), size)]
        at = mine.at[spans[part]]
        sems = keep_sem.at[n_sums + part], back_send.at[n_sums + part], back_recv.at[n_sums + part]
        return pltpu.make_async_copy(at, out, sems[0]), to_peer("grp", partner, at, out, *sems[1:])

    def attn_total(part):
        attn_chip(part).wait()
        at = mine.at[spans[part]]
        total_into(at, at, mine_in.at[spans[part]])
        start_all(back_attn(part))


    @pl.loop(0, line)
    def _(d):
        at = pl.ds(pl.multiple_of(d * pair, pair), pair)
        part = dot(dq_rows[at], wq[...]) + dot(dk_rows[at], wkv[0]) + dot(dv_rows[at], wkv[1])
        parts[pl.ds(2 * d, 2)] = part.astype(low).reshape(2, rows, -1)

    for i in range(seqs, line - 1):
        ffn_sum.hop(i)
    attn_pair(0, (0, 1))
    ffn_sum.finish()
    reduce = Reduce(p, parts, first, scratch[17 + n :])
    for i in range(DEPTH):
        reduce.send_across(i)
    for i in range(line - 1):
        reduce.b_hop(i)

    def summed(which):
        return (halves[p.y, which].astype(F32) + half_in[which].astype(F32)).astype(low)

    valid = row_valid(p, lengths, rows)
    result = tokens[...].astype(F32) + branch[...] + ffn_own[...]
    mixed[...] = jnp.where(valid, result, jnp.zeros_like(result)).astype(low)

    def back(i):
        per_half = n_sums // 3
        start = core * per_half * part_rows + lax.rem(i, per_half) * part_rows
        at = pl.ds(pl.multiple_of(start, part_rows), part_rows)
        out = total_hbm.at[lax.div(i, per_half), at]
        return (
            pltpu.make_async_copy(sums_in.at[i], out, keep_sem.at[i]),
            to_peer("grp", partner, sums_in.at[i], out, back_send.at[i], back_recv.at[i]),
        )

    def sum_up(first_piece, end):
        @pl.loop(first_piece, end)
        def _(i):
            either(i >= EARLY, lambda: chip_copy(i).wait())
            load_sum(i).wait()
            total_into(sums_in.at[i], sums.at[lax.rem(i, 2)], sums_in.at[i])
            either(i + 2 < n_sums, lambda: load_sum(i + 2).start())
            start_all(back(i))

    def gain_copy(step, peer, origin):
        return to_peer(
            "shard", peer, gain_held.at[peer], gain_in.at[origin], ga_send.at[step], ga_recv.at[step]
        )

    def gain_group(step, peer, origin):
        return to_peer(
            "grp", peer, gain_sum, gain_all.at[origin], gb_send.at[step], gb_recv.at[step]
        )

    def gain_first():
        def body(i, total):
            at = pl.ds(pl.multiple_of(i * 16, 16), 16)
            for b in range(count):
                total = total + parts[b, at].astype(F32) * normed[b, at].astype(F32)
            return total

        total = lax.fori_loop(0, rows // 16, body, jnp.zeros((16, parts.shape[2]), F32))
        total = jnp.sum(total, 0, keepdims=True) / gain_row(gains, 0)
        for b in range(count):
            gain_held[b, 0:1] = total[:, b * share : (b + 1) * share]
        for step in range(1, count):
            gain_copy(step, lax.rem(p.me + step, count), p.me).start()

    def gain_second():
        for step in range(1, count):
            gain_copy(step, p.me, lax.rem(p.me + count - step, count)).wait_recv()
        gain_in[p.me] = gain_held[p.me]
        total = gain_in[0]
        for b in range(1, count):
            total = total + gain_in[b]
        gain_sum[...] = total
        gain_all[rank] = total
        for step in range(1, groups):
            gain_group(step, lax.rem(rank + step, groups), rank).start()

    swap().wait_recv()
    gradient(4, summed(0), normed)
    gradient(5, summed(1), normed)
    reduce.hop(0)
    reduce.send_across(DEPTH)
    attn_pair(1, (2,))
    gain_first()
    sum_up(0, n_sums // 2)
    reduce.hop(1)
    reduce.send_across(DEPTH + 1)
    gain_second()
    sum_up(n_sums // 2, n_sums - 3)
    reduce.hop(2)
    sum_up(n_sums - 3, n_sums)
    attn_total(0)
    reduce.finish()
    for step in range(1, groups):
        gain_group(step, rank, lax.rem(rank + groups - step, groups)).wait_recv()
    total = gain_all[0]
    for b in range(1, groups):
        total = total + gain_all[b]
    gain_out[...] = total
    source = tokens[...].astype(F32)
    inner = norm_grad(source, inverse_rms(source), gain_row(gains, 0), first[...])
    input_grad[...] = (middle_grad[...] + inner).astype(low)
    attn_total(1)
    reduce.drain()
    ffn_sum.drain()
    swap().wait_send()
    for b in range(3):
        to_partner(2 * b).wait_send()
    for step in range(1, count):
        gain_copy(step, lax.rem(p.me + step, count), p.me).wait_send()
    for step in range(1, groups):
        gain_group(step, lax.rem(rank + step, groups), rank).wait_send()

    @pl.loop(0, n_sums)
    def _(i):
        wait_all(back(i))

    for part in range(2):
        wait_all(back_attn(part))


def attention_grad(
    lengths, tokens, branch, cot, second, gains, cosine, sine, ffn_parts, normed, attended, q, k, v, wq, wkv, wo, sums, early,
    groups, ident,
):
    rows, width = tokens.shape
    count = normed.shape[0]
    line = count // 2
    seqs, total_slots, hd = q.shape
    low = tokens.dtype
    vmem = pltpu.VMEM
    tall = count * rows
    half = hd // 2
    sums = sums.reshape(-1, PIECE, width)
    early = early.reshape(-1, PIECE, width)
    n_sums, part_rows, _ = sums.shape
    shape = jax.ShapeDtypeStruct
    big = vmem((count, rows, width), low)
    head = vmem((seqs, total_slots, hd), low)
    weight = vmem((hd, width), low)
    flat = vmem((tall, hd), low)
    acc = vmem((total_slots, hd), F32)
    third = vmem((3 * half, width), low)
    g = gains.shape
    block = vmem((rows, width), F32)
    return pl.pallas_call(
        functools.partial(attention_grad_kernel, line, groups, seqs),
        out_shape=(
            shape((rows, width), low),
            shape((rows, width), low),
            shape(g[1:], F32),
            shape((3, n_sums // 3 * 2 * part_rows, width), low),
            shape((6 * half, width), low),
        ),
        in_specs=[scalars()] + [vm()] * 7 + [hbm()] * 11,
        out_specs=(vm(), vm(), vm(), hbm(), hbm()),
        scratch_shapes=[
            vmem((rows, width), low), block, block, block,
            big, big, flat, head, head, head, weight, vmem((2, hd, width), low), weight, head, acc, acc,
            flat, flat, flat,
            vmem((2, 2, tall, half), low), vmem((2, tall, half), low), big,
            vmem((2,) + sums.shape[1:], low), vmem(sums.shape, low), vmem((3, half, width), low), third, third, third,
            vmem(g, F32), vmem(g, F32), vmem(g[1:], F32), vmem((groups,) + g[1:], F32),
        ]
        + gather_sems(count)
        + [
            DMA((12,)), DMA((n_sums + 2,)), DMA((n_sums + 2,)), DMA, DMA, DMA((3,)), DMA((3,)),
            DMA((n_sums + 2,)), DMA((n_sums + 2,)), DMA((n_sums + 2,)),
            DMA((count,)), DMA((count,)), DMA((groups,)), DMA((groups,)),
        ]
        + Reduce.scratch(line, rows, width, low) * 2,
        compiler_params=params(ident),
        name="attention_grad",
    )(
        lengths, tokens, branch, cot, second, gains, cosine, sine, ffn_parts, normed, attended, q, k, v, wq, wkv, wo, sums, early
    )


epsilon = 1e-06
theta_base = 1000042.0
masked_value = -1e30


def turned(source):
    half_width = source.shape[-1] // 2
    return jnp.concatenate([-source[..., half_width:], source[..., :half_width]], -1)


def rotate(source, cosine_table, sine_table):
    return source * cosine_table + turned(source) * sine_table


def unrotate(source, cosine_table, sine_table):
    return source * cosine_table - turned(source) * sine_table


def norm_forward(source, norm_gain):
    inverse = lax.rsqrt(jnp.mean(source * source, -1, keepdims=True) + epsilon)
    return (source * inverse * norm_gain, inverse)


def norm_backward(source, inverse, norm_gain, grad_out):
    weighted = grad_out * norm_gain
    inner_sum = jnp.sum(weighted * source, -1, keepdims=True)
    grad_in = (
        inverse * weighted - source * inverse * inverse * inverse * inner_sum / source.shape[-1]
    )
    return (grad_in, jnp.sum(grad_out * source * inverse, 0))


def weight_terms(normed, query_grad, key_grad, value_grad, attended, branch_grad, shard_count):
    token_count, model_width = normed.shape
    query_share = query_grad.shape[1] // shard_count
    kv_share = key_grad.shape[1] // shard_count
    shard_rows = 2 * query_share + 2 * kv_share

    def weight_term(first_row, row_count):
        blocks = row_count // shard_rows

        def columns(matrix, share_cols):
            return matrix.reshape(token_count, blocks, share_cols)

        part_query = jnp.einsum(
            "tmr,td->mrd",
            columns(query_grad, query_share),
            normed,
            preferred_element_type=jnp.float32,
        )
        part_key = jnp.einsum(
            "tmr,td->mrd", columns(key_grad, kv_share), normed, preferred_element_type=jnp.float32
        )
        part_value = jnp.einsum(
            "tmr,td->mrd", columns(value_grad, kv_share), normed, preferred_element_type=jnp.float32
        )
        part_out = jnp.einsum(
            "tmr,td->mrd",
            columns(attended, query_share),
            branch_grad,
            preferred_element_type=jnp.float32,
        )
        return jnp.concatenate([part_query, part_key, part_value, part_out], 1).reshape(
            row_count, model_width
        )

    return (weight_term, shard_rows)


def local_rows(
    tokens,
    lengths,
    prenorm_gain,
    query_weight,
    key_weight,
    value_weight,
    out_weight,
    midnorm_gain,
    gate_weight,
    up_weight,
    down_weight,
    cotangent,
):
    shard_count = lax.axis_size("shard")
    shard_rank = lax.axis_index("shard")
    micro_count, seq_dev, model_width = tokens.shape
    slot_count = seq_dev * shard_count
    repeat_heads = NH // KVH
    query_width = NH * HD
    kv_width = KVH * HD
    score_scale = 1.0 / math.sqrt(HD)
    local_pos = shard_rank * seq_dev + jnp.arange(seq_dev, dtype=jnp.int32)
    key_pos = jnp.arange(slot_count, dtype=jnp.int32)
    inverse_freq = theta_base ** (-(jnp.arange(0, HD, 2).astype(jnp.float32) / HD))
    angles = local_pos.astype(jnp.float32)[:, None] * inverse_freq[None, :]
    cosine_table = jnp.concatenate([jnp.cos(angles), jnp.cos(angles)], -1)[:, None, :]
    sine_table = jnp.concatenate([jnp.sin(angles), jnp.sin(angles)], -1)[:, None, :]
    gate_total = jnp.zeros(gate_weight.shape, jnp.float32)
    up_total = jnp.zeros(up_weight.shape, jnp.float32)
    down_total = jnp.zeros(down_weight.shape, jnp.float32)
    prenorm_total = jnp.zeros((model_width,), jnp.float32)
    midnorm_total = jnp.zeros((model_width,), jnp.float32)
    attn_total = None
    mixed_rows = []
    input_rows = []
    for micro_index in range(micro_count):
        gathered = (
            lax.all_gather(query_weight, "shard", axis=0, tiled=True),
            lax.all_gather(key_weight, "shard", axis=0, tiled=True),
            lax.all_gather(value_weight, "shard", axis=0, tiled=True),
            lax.all_gather(prenorm_gain, "shard", axis=0, tiled=True),
            lax.all_gather(midnorm_gain, "shard", axis=0, tiled=True),
        )
        query_full, key_full, value_full, prenorm_full, midnorm_full = gathered
        prenorm_f = prenorm_full.astype(jnp.float32)
        midnorm_f = midnorm_full.astype(jnp.float32)
        source = tokens[micro_index].astype(jnp.float32)
        length_now = lengths[micro_index]
        valid_rows = local_pos < length_now
        scaled_first, inverse_first = norm_forward(source, prenorm_f)
        normed_first = scaled_first.astype(jnp.bfloat16)
        query_pre = jnp.einsum(
            "sd,qd->sq", normed_first, query_full, preferred_element_type=jnp.float32
        ).reshape(seq_dev, NH, HD)
        key_pre = jnp.einsum(
            "sd,qd->sq", normed_first, key_full, preferred_element_type=jnp.float32
        ).reshape(seq_dev, KVH, HD)
        value_pre = jnp.einsum(
            "sd,qd->sq", normed_first, value_full, preferred_element_type=jnp.float32
        )
        query_rot = rotate(query_pre, cosine_table, sine_table).astype(jnp.bfloat16)
        key_rot = rotate(key_pre, cosine_table, sine_table).astype(jnp.bfloat16)
        key_value = jnp.concatenate(
            [key_rot.reshape(seq_dev, kv_width), value_pre.astype(jnp.bfloat16)], 1
        )
        kv_all = lax.all_gather(key_value, "shard", axis=0, tiled=True)
        keys_all = kv_all[:, :kv_width].reshape(slot_count, KVH, HD)
        values_all = kv_all[:, kv_width:].reshape(slot_count, KVH, HD)
        query_group = query_rot.reshape(seq_dev, KVH, repeat_heads, HD)
        scores = (
            jnp.einsum("skrd,tkd->krst", query_group, keys_all, preferred_element_type=jnp.float32)
            * score_scale
        )
        allowed = (key_pos[None, :] <= local_pos[:, None]) & (key_pos[None, :] < length_now)
        scores = jnp.where(allowed, scores, masked_value)
        row_max = jnp.max(scores, -1, keepdims=True)
        exp_scores = jnp.exp(scores - row_max)
        attention_probs = exp_scores / jnp.sum(exp_scores, -1, keepdims=True)
        probs_low = attention_probs.astype(jnp.bfloat16)
        attended = (
            jnp.einsum("krst,tkd->skrd", probs_low, values_all, preferred_element_type=jnp.float32)
            .astype(jnp.bfloat16)
            .reshape(seq_dev, query_width)
        )
        branch = jnp.dot(
            attended,
            lax.all_gather(out_weight, "shard", axis=0, tiled=True),
            preferred_element_type=jnp.float32,
        )
        middle = source + branch
        scaled_second, inverse_second = norm_forward(middle, midnorm_f)
        normed_second = scaled_second.astype(jnp.bfloat16)
        normed_all = lax.all_gather(normed_second, "shard", axis=0, tiled=True)
        gate_pre = jnp.einsum(
            "sd,fd->sf", normed_all, gate_weight, preferred_element_type=jnp.float32
        )
        up_pre = jnp.einsum("sd,fd->sf", normed_all, up_weight, preferred_element_type=jnp.float32)
        sigmoid_gate = jax.nn.sigmoid(gate_pre)
        silu_gate = gate_pre * sigmoid_gate
        hidden = (silu_gate * up_pre).astype(jnp.bfloat16)
        ffn_part = lax.psum_scatter(
            jnp.dot(hidden, down_weight, preferred_element_type=jnp.float32).astype(jnp.bfloat16),
            "shard",
            scatter_dimension=0,
            tiled=True,
        ).astype(jnp.float32)
        mixed_rows.append(
            jnp.where(valid_rows[:, None], middle + ffn_part, 0.0).astype(jnp.bfloat16)
        )
        cot_low = jnp.where(
            valid_rows[:, None], cotangent[micro_index], jnp.zeros_like(cotangent[micro_index])
        )
        cot_all = lax.all_gather(cot_low, "shard", axis=0, tiled=True)
        hidden_grad = jnp.einsum(
            "sd,fd->sf", cot_all, down_weight, preferred_element_type=jnp.float32
        )
        down_total = down_total + jnp.einsum(
            "sf,sd->fd", hidden, cot_all, preferred_element_type=jnp.float32
        )
        gate_grad = (
            hidden_grad * up_pre * sigmoid_gate * (1.0 + gate_pre * (1.0 - sigmoid_gate))
        ).astype(jnp.bfloat16)
        up_grad = (hidden_grad * silu_gate).astype(jnp.bfloat16)
        gate_total = gate_total + jnp.einsum(
            "sf,sd->fd", gate_grad, normed_all, preferred_element_type=jnp.float32
        )
        up_total = up_total + jnp.einsum(
            "sf,sd->fd", up_grad, normed_all, preferred_element_type=jnp.float32
        )
        second_grad = lax.psum_scatter(
            jnp.dot(gate_grad, gate_weight, preferred_element_type=jnp.float32)
            + jnp.dot(up_grad, up_weight, preferred_element_type=jnp.float32),
            "shard",
            scatter_dimension=0,
            tiled=True,
        )
        middle_part, midnorm_part = norm_backward(middle, inverse_second, midnorm_f, second_grad)
        middle_grad = cot_low.astype(jnp.float32) + middle_part
        midnorm_total = midnorm_total + midnorm_part
        branch_grad = middle_grad.astype(jnp.bfloat16)
        attended_grad = jnp.einsum(
            "sd,qd->sq",
            branch_grad,
            lax.all_gather(out_weight, "shard", axis=0, tiled=True),
            preferred_element_type=jnp.float32,
        ).astype(jnp.bfloat16)
        attended_group = attended_grad.reshape(seq_dev, KVH, repeat_heads, HD)
        probs_grad = jnp.einsum(
            "skrd,tkd->krst", attended_group, values_all, preferred_element_type=jnp.float32
        )
        inner_sum = jnp.sum(attention_probs * probs_grad, -1, keepdims=True)
        scores_grad = (attention_probs * (probs_grad - inner_sum)).astype(jnp.bfloat16)
        query_rot_grad = (
            jnp.einsum(
                "krst,tkd->skrd", scores_grad, keys_all, preferred_element_type=jnp.float32
            ).reshape(seq_dev, NH, HD)
            * score_scale
        )
        query_grad = (
            unrotate(query_rot_grad, cosine_table, sine_table)
            .astype(jnp.bfloat16)
            .reshape(seq_dev, query_width)
        )
        row_count = lax.axis_size("shard") * seq_dev
        key_part = (
            jnp.einsum(
                "krst,skrd->tkd", scores_grad, query_group, preferred_element_type=jnp.float32
            )
            * score_scale
        )
        value_part = jnp.einsum(
            "krst,skrd->tkd", probs_low, attended_group, preferred_element_type=jnp.float32
        )
        kv_grad = lax.psum_scatter(
            jnp.concatenate(
                [key_part.reshape(row_count, kv_width), value_part.reshape(row_count, kv_width)], 1
            ).astype(jnp.bfloat16),
            "shard",
            scatter_dimension=0,
            tiled=True,
        ).astype(jnp.float32)
        key_grad = (
            unrotate(kv_grad[:, :kv_width].reshape(seq_dev, KVH, HD), cosine_table, sine_table)
            .astype(jnp.bfloat16)
            .reshape(seq_dev, kv_width)
        )
        value_grad = kv_grad[:, kv_width:].astype(jnp.bfloat16)
        first_grad = jnp.einsum(
            "sq,qd->sd", query_grad, query_full, preferred_element_type=jnp.float32
        )
        first_grad = first_grad + jnp.einsum(
            "sq,qd->sd", key_grad, key_full, preferred_element_type=jnp.float32
        )
        first_grad = first_grad + jnp.einsum(
            "sq,qd->sd", value_grad, value_full, preferred_element_type=jnp.float32
        )
        source_part, prenorm_part = norm_backward(source, inverse_first, prenorm_f, first_grad)
        input_rows.append((middle_grad + source_part).astype(jnp.bfloat16))
        prenorm_total = prenorm_total + prenorm_part
        saved = (normed_first, query_grad, key_grad, value_grad, attended, branch_grad)
        weight_term, shard_rows = weight_terms(*saved, shard_count)
        reduced = lax.psum_scatter(
            weight_term(jnp.int32(0), lax.axis_size("shard") * shard_rows).astype(jnp.bfloat16),
            "shard",
            scatter_dimension=0,
            tiled=True,
        ).astype(jnp.float32)
        attn_total = reduced if attn_total is None else attn_total + reduced
    gain_sums = lax.psum((prenorm_total, midnorm_total), ("grp", "shard"))
    gain_share = model_width // shard_count
    prenorm_gradient = lax.dynamic_slice_in_dim(
        gain_sums[0], shard_rank * gain_share, gain_share, 0
    )
    midnorm_gradient = lax.dynamic_slice_in_dim(
        gain_sums[1], shard_rank * gain_share, gain_share, 0
    )
    summed = (
        lax.psum(attn_total.astype(jnp.bfloat16), "grp").astype(jnp.float32),
        lax.psum(gate_total.astype(jnp.bfloat16), "grp").astype(jnp.float32),
        lax.psum(up_total.astype(jnp.bfloat16), "grp").astype(jnp.float32),
        lax.psum(down_total.astype(jnp.bfloat16), "grp").astype(jnp.float32),
    )
    attn_rows = summed[0]
    query_share = query_width // shard_count
    kv_share = kv_width // shard_count
    query_gradient = attn_rows[:query_share]
    key_gradient = attn_rows[query_share : query_share + kv_share]
    value_gradient = attn_rows[query_share + kv_share : query_share + 2 * kv_share]
    out_gradient = attn_rows[query_share + 2 * kv_share :]
    return (
        jnp.stack(mixed_rows),
        jnp.stack(input_rows),
        prenorm_gradient,
        query_gradient,
        key_gradient,
        value_gradient,
        out_gradient,
        midnorm_gradient,
        summed[1],
        summed[2],
        summed[3],
    )


def local_heads(
    tokens,
    lengths,
    prenorm_gain,
    query_weight,
    key_weight,
    value_weight,
    out_weight,
    midnorm_gain,
    gate_weight,
    up_weight,
    down_weight,
    cotangent,
):
    low = jnp.bfloat16
    count = lax.axis_size("shard")
    groups = lax.axis_size("grp")
    seqs, seq_dev, model_width = tokens.shape
    rows = seqs * seq_dev
    inverse_freq = jnp.asarray(theta_base ** (-np.arange(0, HD, 2) / HD), jnp.float32)
    tokens_low = tokens.reshape(rows, model_width)
    cot_low = cotangent.reshape(rows, model_width)
    branch, gains, normed_first, cot_all, queries, keys, values, attended, kv_head, cosine, sine = (
        attention(
            lengths,
            tokens_low,
            cot_low,
            prenorm_gain,
            midnorm_gain,
            inverse_freq[None, :],
            query_weight,
            key_weight,
            value_weight,
            out_weight,
            count,
            groups,
            1,
        )
    )
    second_grad, ffn_parts, pair_sums, early = ffn(
        tokens_low, branch, gains, cot_all, gate_weight, up_weight, down_weight, groups, 2
    )
    mixed, input_gradient, gain_own, totals, attn_total = attention_grad(
        lengths,
        tokens_low,
        branch,
        cot_low,
        second_grad,
        gains,
        cosine,
        sine,
        ffn_parts,
        normed_first,
        attended,
        queries,
        keys,
        values,
        query_weight,
        kv_head,
        out_weight,
        pair_sums,
        early,
        groups,
        3,
    )
    f32 = jnp.float32
    blocks = attn_total.reshape(2, 3, key_weight.shape[0], model_width).astype(f32)
    return (
        mixed.reshape(tokens.shape),
        input_gradient.reshape(tokens.shape),
        gain_own[0],
        blocks[:, 1].reshape(query_weight.shape),
        blocks[0, 2],
        blocks[1, 2],
        blocks[:, 0].reshape(out_weight.shape),
        gain_own[1],
        totals[1].astype(f32),
        totals[2].astype(f32),
        totals[0].astype(f32),
    )


def solution(mesh):
    planes = mesh.shape["shard"] == NH and mesh.shape["grp"] == 4
    local = local_heads if planes else local_rows
    in_specs = (
        P("grp", "shard", None),
        P("grp"),
        P("shard"),
        P("shard", None),
        P("shard", None),
        P("shard", None),
        P("shard", None),
        P("shard"),
        P("shard", None),
        P("shard", None),
        P("shard", None),
        P("grp", "shard", None),
    )
    out_specs = (
        P("grp", "shard", None),
        P("grp", "shard", None),
        P("shard"),
        P("shard", None),
        P("shard", None),
        P("shard", None),
        P("shard", None),
        P("shard"),
        P("shard", None),
        P("shard", None),
        P("shard", None),
    )
    return jax.shard_map(local, mesh=mesh, in_specs=in_specs, out_specs=out_specs, check_vma=False)
```

```python
import functools
import math

import jax
import jax.numpy as jnp
from jax import lax
from jax.experimental import pallas as pl
from jax.experimental.pallas import tpu as pltpu
from jax.sharding import PartitionSpec as P
import numpy as np

NH = 8
KVH = 4
HD = 256
MASKED = -1e30
EPSILON = 1e-06
DEPTH = 2
MESH = pl.DeviceIdType.MESH
F32 = jnp.float32
DMA = pltpu.SemaphoreType.DMA
REST = 16
PIECE = 128
EARLY = 3
CHUNKS = 2


def pieces(rows, rest=REST):
    size = -(-(rows - rest) // (16 * CHUNKS)) * 16
    cuts = [min(i * size, rows - rest) for i in range(CHUNKS + 1)] + [rows]
    return [pl.ds(a, b - a) for a, b in zip(cuts, cuts[1:])]


VMEM_LIMIT = 66_000_000


def either(condition, action):
    pl.when(condition)(action)


def total_into(dst, *srcs):
    step = 16

    @pl.loop(0, dst.shape[0] // step)
    def _(i):
        at = pl.ds(pl.multiple_of(i * step, step), step)
        value = srcs[0][at].astype(F32)
        for src in srcs[1:]:
            value = value + src[at].astype(F32)
        dst[at] = value.astype(dst.dtype)


class Place:
    def __init__(self, line):
        self.line = line
        self.me = lax.axis_index("shard")
        self.z = self.me // 2
        self.y = lax.rem(self.me, 2)
        self.cross = self.me + 1 - 2 * self.y
        self.low_end = self.z == 0
        self.high_end = self.z == line - 1
        near = []
        for z in range(line):
            order = [z]
            for k in range(1, line):
                order += [d for d in (z - k, z + k) if 0 <= d < line]
            near.append(order)
        self.tables = near

    def near(self, i):
        out = jnp.int32(0)
        for z in range(self.line):
            row = jnp.int32(self.tables[z][0])
            for k in range(1, self.line):
                row = jnp.where(i == k, self.tables[z][k], row)
            out = jnp.where(self.z == z, row, out)
        return out

    def far(self, i):
        return self.near(self.line - 1 - i)

    def greet(self, groups):
        barrier = pltpu.get_barrier_semaphore()
        count = 2 * self.line
        rank = lax.axis_index("grp")
        for step in range(1, count):
            pl.semaphore_signal(
                barrier,
                inc=1,
                device_id={"shard": lax.rem(self.me + step, count)},
                device_id_type=MESH,
            )
        for step in range(1, groups):
            pl.semaphore_signal(
                barrier,
                inc=1,
                device_id={"grp": lax.rem(rank + step, groups)},
                device_id_type=MESH,
            )
        pl.semaphore_wait(barrier, count + groups - 2)


class Gather:
    UP, DOWN, CROSS = 0, 1, 2

    def __init__(self, place, own, out, local_sem, send_sem, recv_sem, rest=REST):
        self.p, self.own, self.out = place, own, out
        self.local_sem, self.send_sem, self.recv_sem = local_sem, send_sem, recv_sem
        self.pieces = pieces(own.shape[0], rest)
        self.last = len(self.pieces) - 1

    def copy(self, way, origin, part, own=False):
        p = self.p
        peer = (p.me + 2, p.me - 2, p.cross)[way]
        at = self.pieces[part]
        return pltpu.make_async_remote_copy(
            src_ref=self.own.at[at] if own else self.out.at[origin, at],
            dst_ref=self.out.at[origin, at],
            send_sem=self.send_sem.at[way, origin, part],
            recv_sem=self.recv_sem.at[origin, part],
            device_id={"shard": peer},
            device_id_type=MESH,
        )

    def arrived(self, origin, part):
        self.copy(self.CROSS, origin, part).wait_recv()

    def start(self):
        self.send_own()
        self.pass_rest()

    def send_own(self):
        p = self.p
        pltpu.make_async_copy(self.own, self.out.at[p.me], self.local_sem).start()
        for part in (self.last,) + tuple(range(self.last)):
            self.copy(self.CROSS, p.me, part, True).start()
        for part in range(self.last + 1):
            either(p.z < p.line - 1, lambda: self.copy(self.UP, p.me, part, True).start())
            either(p.z > 0, lambda: self.copy(self.DOWN, p.me, part, True).start())

    def pass_rest(self):
        p = self.p
        self.arrived(p.cross, self.last)
        either(p.z < p.line - 1, lambda: self.copy(self.UP, p.cross, self.last).start())
        either(p.z > 0, lambda: self.copy(self.DOWN, p.cross, self.last).start())
        pltpu.make_async_copy(self.own, self.out.at[p.me], self.local_sem).wait()

    def hop(self, k):
        p = self.p
        below, above = p.me - 2 * k, p.me + 2 * k
        has_below, has_above = p.z - k >= 0, p.z + k < p.line

        def first(origin, part, way, more):
            self.arrived(origin, part)
            self.copy(self.CROSS, origin, part).start()
            either(more, lambda: self.copy(way, origin, part).start())

        def last(origin, other, way, more):
            for block in (origin, other):
                self.arrived(block, self.last)
                either(more, lambda: self.copy(way, block, self.last).start())

        for part in range(self.last):
            either(has_below, lambda: first(below, part, self.UP, p.z < p.line - 1))
            either(has_above, lambda: first(above, part, self.DOWN, p.z > 0))
        either(has_below, lambda: last(below, p.cross - 2 * k, self.UP, p.z < p.line - 1))
        either(has_above, lambda: last(above, p.cross + 2 * k, self.DOWN, p.z > 0))

    def whole(self, position):
        for part in range(self.last):
            self.arrived(2 * position + 1 - self.p.y, part)

    def drain(self):
        p = self.p

        @pl.loop(0, p.line)
        def _(d):
            mine, other = 2 * d + p.y, 2 * d + 1 - p.y
            for part in range(self.last):
                self.copy(self.CROSS, mine, part).wait_send()

            @pl.when(d == p.z)
            def _():
                self.copy(self.CROSS, mine, self.last).wait_send()

            def line_sent(way):
                for part in range(self.last + 1):
                    self.copy(way, mine, part).wait_send()
                self.copy(way, other, self.last).wait_send()

            either((d <= p.z) & (p.z < p.line - 1), lambda: line_sent(self.UP))
            either((d >= p.z) & (p.z > 0), lambda: line_sent(self.DOWN))


class Reduce:
    BUP, BDN, BX = 0, 2, 4
    UP, DOWN, CROSS = 5, 5 + CHUNKS, 5 + 2 * CHUNKS
    WAYS = 5 + 3 * CHUNKS
    N_SCRATCH = 9

    @staticmethod
    def scratch(line, rows, width, dtype):
        v = pltpu.VMEM
        return (
            [v((line, rows - REST, width), dtype)] * 3
            + [v((line, 2, REST, width), dtype)] * 2
            + [v((REST, width), dtype)] * 2
            + [DMA((Reduce.WAYS, line)), DMA((Reduce.WAYS, line))]
        )

    def __init__(self, place, parts, out, scratch):
        self.p, self.parts, self.out = place, parts, out
        self.cross_in, self.up_in, self.down_in, self.bup_in, self.bdn_in = scratch[:5]
        self.bx_out, self.bx_in, self.send_sem, self.recv_sem = scratch[5:]
        self.pieces = pieces(parts.shape[1])
        self.b = self.pieces[-1]

    def desc(self, way, slot, src, dst, peer):
        return pltpu.make_async_remote_copy(
            src_ref=src,
            dst_ref=dst,
            send_sem=self.send_sem.at[way, slot],
            recv_sem=self.recv_sem.at[way, slot],
            device_id={"shard": peer},
            device_id_type=MESH,
        )

    def cross_copy(self, d, c):
        p, at = self.p, self.pieces[c]
        return self.desc(
            self.CROSS + c,
            d,
            self.parts.at[2 * d + 1 - p.y, at],
            self.cross_in.at[d, at],
            p.cross,
        )

    def line_copy(self, up, d, c):
        p, at = self.p, self.pieces[c]
        came = self.up_in if up else self.down_in
        return self.desc(
            (self.UP if up else self.DOWN) + c,
            d,
            self.cross_in.at[d, at],
            came.at[d, at],
            p.me + 2 if up else p.me - 2,
        )

    def b_copy(self, up, d, o, src=None):
        p = self.p
        held = self.bup_in if up else self.bdn_in
        return self.desc(
            (self.BUP if up else self.BDN) + o,
            d,
            held.at[d, o] if src is None else src,
            held.at[d, o],
            p.me + 2 if up else p.me - 2,
        )

    def bx_copy(self):
        return self.desc(self.BX, 0, self.bx_out, self.bx_in, self.p.cross)

    def column(self, o):
        return self.p.y if o == 0 else 1 - self.p.y

    def send_across(self, i):
        for c in range(CHUNKS):
            self.cross_copy(self.p.far(i), c).start()

    def b_hop(self, i):
        p = self.p
        d = p.far(i)

        def go(up):
            first = p.low_end if up else p.high_end
            held = self.bup_in if up else self.bdn_in
            for o in (1, 0):
                mine = self.parts.at[2 * d + self.column(o), self.b]
                either(first, lambda: self.b_copy(up, d, o, mine).start())

                @pl.when(jnp.logical_not(first))
                def _():
                    self.b_copy(up, d, o).wait_recv()
                    total_into(held.at[d, o], mine, held.at[d, o])
                    self.b_copy(up, d, o).start()

        either(d > p.z, lambda: go(True))
        either(d < p.z, lambda: go(False))

    def hop(self, i):
        for c in range(CHUNKS):
            self.step(i, c)

    def step(self, i, c):
        p = self.p
        d = p.far(i)
        self.cross_copy(d, c).wait_recv()
        at = self.pieces[c]
        mine = self.parts.at[2 * d + p.y, at]
        held = self.cross_in.at[d, at]

        def go(up):
            first = p.low_end if up else p.high_end
            came = self.up_in if up else self.down_in
            either(first, lambda: total_into(held, mine, held))

            @pl.when(jnp.logical_not(first))
            def _():
                self.line_copy(up, d, c).wait_recv()
                total_into(held, mine, held, came.at[d, at])

            self.line_copy(up, d, c).start()

        either(d > p.z, lambda: go(True))
        either(d < p.z, lambda: go(False))

    def close(self, dst, mine, ups, downs):
        p = self.p
        either(p.low_end, lambda: total_into(dst, *mine, downs))
        either(p.high_end, lambda: total_into(dst, *mine, ups))
        either(
            jnp.logical_not(p.low_end | p.high_end), lambda: total_into(dst, *mine, ups, downs)
        )

    def finish(self):
        p = self.p
        for o in (1, 0):
            either(jnp.logical_not(p.low_end), lambda: self.b_copy(True, p.z, o).wait_recv())
            either(jnp.logical_not(p.high_end), lambda: self.b_copy(False, p.z, o).wait_recv())
            if o:
                mine = self.parts.at[2 * p.z + self.column(o), self.b]
                self.close(self.bx_out, (mine,), self.bup_in.at[p.z, o], self.bdn_in.at[p.z, o])
                self.bx_copy().start()
        self.bx_copy().wait_recv()
        self.close(
            self.out.at[self.b],
            (self.parts.at[p.me, self.b], self.bx_in),
            self.bup_in.at[p.z, 0],
            self.bdn_in.at[p.z, 0],
        )
        for c in range(CHUNKS):
            self.cross_copy(p.z, c).wait_recv()
            either(jnp.logical_not(p.low_end), lambda: self.line_copy(True, p.z, c).wait_recv())
            either(jnp.logical_not(p.high_end), lambda: self.line_copy(False, p.z, c).wait_recv())
            at = self.pieces[c]
            self.close(
                self.out.at[at],
                (self.parts.at[p.me, at], self.cross_in.at[p.z, at]),
                self.up_in.at[p.z, at],
                self.down_in.at[p.z, at],
            )

    def drain(self):
        p = self.p
        self.bx_copy().wait_send()

        @pl.loop(0, p.line)
        def _(d):
            def line_sent(up):
                for c in range(CHUNKS):
                    self.line_copy(up, d, c).wait_send()
                self.b_copy(up, d, 0).wait_send()
                self.b_copy(up, d, 1).wait_send()

            for c in range(CHUNKS):
                self.cross_copy(d, c).wait_send()
            either(d > p.z, lambda: line_sent(True))
            either(d < p.z, lambda: line_sent(False))


def dot(a, b):
    return jnp.dot(a, b, preferred_element_type=F32)


def dot_t(a, b):
    return lax.dot_general(a, b, (((1,), (1,)), ((), ())), preferred_element_type=F32)


def t_dot(a, b):
    return lax.dot_general(a, b, (((0,), (0,)), ((), ())), preferred_element_type=F32)


def to_peer(axis, peer, src, dst, send_sem, recv_sem):
    return pltpu.make_async_remote_copy(
        src_ref=src,
        dst_ref=dst,
        send_sem=send_sem,
        recv_sem=recv_sem,
        device_id={axis: peer},
        device_id_type=MESH,
    )


def turn_by(v, cosine, sine):
    half = v.shape[-1] // 2
    a, b = v[:, :half], v[:, half:]
    return jnp.concatenate([a * cosine - b * sine, b * cosine + a * sine], -1)


def turn_back(v, cosine, sine):
    return turn_by(v, cosine, -sine)


def probabilities(query, keys, rows_from, limit):
    scores = dot_t(query, keys) * (1.0 / math.sqrt(HD))
    row = lax.broadcasted_iota(jnp.int32, scores.shape, 0) + rows_from
    col = lax.broadcasted_iota(jnp.int32, scores.shape, 1)
    scores = jnp.where((col <= row) & (col < limit), scores, MASKED)
    weight = jnp.exp(scores - jnp.max(scores, -1, keepdims=True))
    return weight / jnp.sum(weight, -1, keepdims=True)


def row_valid(place, lengths, rows):
    slots = rows // lengths.shape[0]
    row = lax.broadcasted_iota(jnp.int32, (rows, 1), 0)
    limit = jnp.full((rows, 1), lengths[0], jnp.int32)
    for n in range(1, lengths.shape[0]):
        limit = jnp.where(row >= n * slots, lengths[n], limit)
    return place.me * slots + lax.rem(row, slots) < limit


def gain_row(shares, which):
    return jnp.concatenate([shares[b, which : which + 1] for b in range(shares.shape[0])], 1)


def inverse_rms(x):
    return lax.rsqrt(jnp.mean(x * x, -1, keepdims=True) + EPSILON)


def norm_grad(x, inverse, gain, grad):
    weighted = grad * gain
    inner = jnp.sum(weighted * x, -1, keepdims=True)
    return inverse * weighted - x * inverse * inverse * inverse * inner / x.shape[-1]


def start_all(copies):
    for c in copies:
        c.start()


def wait_all(copies):
    for c in copies:
        c.wait()


def scalars():
    return pl.BlockSpec(memory_space=pltpu.SMEM)


def hbm():
    return pl.BlockSpec(memory_space=pl.ANY)


def vm():
    return pl.BlockSpec(memory_space=pltpu.VMEM)


def params(ident):
    return pltpu.CompilerParams(
        collective_id=ident, has_side_effects=True, vmem_limit_bytes=VMEM_LIMIT
    )


def gather_sems(count):
    return [DMA, DMA((3, count, CHUNKS + 1)), DMA((count, CHUNKS + 1))]


def attention_kernel(
    line, groups, seqs,
    lengths, own, cot_raw, pre_gain, mid_gain, freq, wq_hbm, wk_hbm, wv_hbm, wo_hbm,
    branch, small_out, normed_hbm, cot_hbm, q_hbm, k_hbm, v_hbm, attended_hbm, wkv_hbm, cos_hbm, sin_hbm,
    small, cot_own, rows_all, normed, cot_all, q, k, v, attended, wq, wkv, wo, cosine, sine, parts,
    *scratch,
):
    p = Place(line)
    count = 2 * line
    rank = lax.axis_index("grp")
    g1, g2 = scratch[:3], scratch[3:6]
    (load_sem, small_send, small_recv, wy_send, wg_send, w_recv, save_sem) = scratch[6:13]
    r_scratch = scratch[13:]
    half = wk_hbm.shape[0]
    piece = half // 2
    at_own = pl.ds(pl.multiple_of(p.y * half, half), half)
    loads = [
        pltpu.make_async_copy(src, dst, load_sem.at[i])
        for i, (src, dst) in enumerate(
            (
                (wk_hbm, wkv.at[0, at_own]),
                (wv_hbm, wkv.at[1, at_own]),
                (wq_hbm, wq),
                (wo_hbm, wo),
            )
        )
    ]
    start_all(loads)
    p.greet(groups)

    small[...] = jnp.zeros_like(small)
    small[0:1] = pre_gain[...].astype(F32)[None, :]
    small[1:2] = mid_gain[...].astype(F32)[None, :]

    def small_copy(step, peer, origin):
        return to_peer(
            "shard", peer, small, small_out.at[origin], small_send.at[step], small_recv.at[step]
        )

    for step in range(1, count):
        small_copy(step, lax.rem(p.me + step, count), p.me).start()
    gather = Gather(p, own, rows_all, *g1, rest=2 * REST)
    gather.start()
    cots = Gather(p, cot_own, cot_all, *g2)
    small_out[p.me] = small[...]

    def rows_of(quarter, column):
        return wkv.at[
            quarter // 2,
            pl.ds(pl.multiple_of(column * half + lax.rem(quarter, 2) * piece, piece), piece),
        ]

    def across():
        ref = rows_of(rank, p.y)
        return to_peer("shard", p.cross, ref, ref, wy_send, w_recv.at[rank])

    def share(step):
        ref = rows_of(rank, 1 - p.y)
        return to_peer(
            "grp", lax.rem(rank + step, groups), ref, ref, wg_send.at[step], w_recv.at[rank]
        )

    wait_all(loads)
    across().start()
    pos = lax.broadcasted_iota(jnp.int32, cosine.shape, 0).astype(F32)
    angle = pos * freq[...]
    cosine[...] = jnp.cos(angle)
    sine[...] = jnp.sin(angle)
    cot = cot_raw[...]
    cot_own[...] = jnp.where(row_valid(p, lengths, cot.shape[0]), cot, jnp.zeros_like(cot))
    gather.hop(1)
    for step in range(1, count):
        small_copy(step, p.me, lax.rem(p.me + count - step, count)).wait_recv()
    gain = gain_row(small_out, 0)
    across().wait_recv()
    for step in range(1, groups):
        share(step).start()
    rows = own.shape[0]
    pair = 2 * rows
    slots = rows // seqs
    low = own.dtype
    for step in range(1, groups):
        quarter = lax.rem(rank + step, groups)
        ref = rows_of(quarter, 1 - p.y)
        to_peer("grp", rank, ref, ref, wg_send.at[step], w_recv.at[quarter]).wait_recv()

    @pl.loop(0, line)
    def _(i):
        d = p.near(i)
        gather.whole(d)
        x = rows_all[pl.ds(2 * d, 2)].reshape(pair, -1).astype(F32)
        n = (x * inverse_rms(x) * gain).astype(low)
        normed[pl.ds(2 * d, 2)] = n.reshape(2, rows, -1)
        at = pl.ds(pl.multiple_of(d * 2 * slots, 2 * slots), 2 * slots)
        c, s = cosine[at], sine[at]

        def by_rows(t):
            return jnp.concatenate([t[:slots]] * seqs + [t[slots:]] * seqs, 0)

        c, s = by_rows(c), by_rows(s)

        def put(target, value):
            for block in range(2):
                for m in range(seqs):
                    to = pl.ds(
                        pl.multiple_of(d * 2 * slots + block * slots, slots), slots
                    )
                    target[m, to] = value[block * rows + m * slots : block * rows + (m + 1) * slots]

        put(q, turn_by(dot_t(n, wq[...]), c, s).astype(low))
        put(k, turn_by(dot_t(n, wkv[0]), c, s).astype(low))
        put(v, dot_t(n, wkv[1]).astype(low))
        gather.hop(i + 2)
        either(i == line - 3, cots.send_own)

    saves = [
        pltpu.make_async_copy(src, dst, save_sem.at[i])
        for i, (src, dst) in enumerate(
            (
                (normed, normed_hbm),
                (q, q_hbm),
                (k, k_hbm),
                (v, v_hbm),
                (wkv, wkv_hbm),
                (cosine, cos_hbm),
                (sine, sin_hbm),
            )
        )
    ]
    start_all(saves)
    cots.pass_rest()
    total_slots = q.shape[1]
    tile = min(256, total_slots)

    @pl.loop(0, seqs)
    def _(n):
        for t in range(total_slots // tile):
            span = (t + 1) * tile
            at = pl.ds(t * tile, tile)
            probs = probabilities(q[n, at], k[n, pl.ds(0, span)], t * tile, lengths[n])
            out = dot(probs.astype(low), v[n, pl.ds(0, span)]).astype(low)
            for c in range(tile // slots):
                b = (t * tile) // slots + c
                attended[pl.ds(pl.multiple_of(b * rows + n * slots, slots), slots)] = out[
                    c * slots : (c + 1) * slots
                ]
        cots.hop(n + 1)

    for h in range(seqs + 1, line):
        cots.hop(h)

    @pl.loop(0, line)
    def _(d):
        at = pl.ds(pl.multiple_of(d * pair, pair), pair)
        parts[pl.ds(2 * d, 2)] = dot(attended[at], wo[...]).astype(low).reshape(2, rows, -1)

    reduce = Reduce(p, parts, branch, r_scratch)
    saves2 = [pltpu.make_async_copy(attended, attended_hbm, save_sem.at[7])]
    start_all(saves2)
    for d in range(line):
        cots.whole(d)
    for i in range(DEPTH):
        reduce.send_across(i)
    saves3 = [pltpu.make_async_copy(cot_all, cot_hbm, save_sem.at[8])]
    start_all(saves3)
    for i in range(line - 1):
        reduce.b_hop(i)
    for i in range(line - 1):
        reduce.hop(i)
        if i + DEPTH < line:
            reduce.send_across(i + DEPTH)
    reduce.finish()
    reduce.drain()
    gather.drain()
    cots.drain()
    wait_all(saves + saves2 + saves3)
    across().wait_send()
    for step in range(1, groups):
        share(step).wait_send()
    for step in range(1, count):
        small_copy(step, lax.rem(p.me + step, count), p.me).wait_send()


def attention(lengths, own, cot, pre_gain, mid_gain, freq, wq, wk, wv, wo, count, groups, ident):
    rows, width = own.shape
    seqs = lengths.shape[0]
    total_slots = count * rows // seqs
    small = (8, pre_gain.shape[0])
    line = count // 2
    low = own.dtype
    v = pltpu.VMEM
    shape = jax.ShapeDtypeStruct
    hd = wq.shape[0]
    big = (count, rows, width)
    head = (seqs, total_slots, hd)
    table = (total_slots, hd // 2)
    flat = (count * rows, hd)
    return pl.pallas_call(
        functools.partial(attention_kernel, line, groups, seqs),
        out_shape=(
            shape((rows, width), F32),
            shape((count,) + small, F32),
            shape(big, low),
            shape(big, low),
            shape(head, low),
            shape(head, low),
            shape(head, low),
            shape(flat, low),
            shape((2, hd, width), low),
            shape(table, F32),
            shape(table, F32),
        ),
        in_specs=[scalars()] + [vm()] * 5 + [hbm()] * 4,
        out_specs=(vm(), vm()) + (hbm(),) * 9,
        scratch_shapes=[
            v(small, F32), v((rows, width), low), v(big, low), v(big, low), v(big, low), v(head, low), v(head, low), v(head, low), v(flat, low),
            v((hd, width), low), v((2, hd, width), low), v((hd, width), low), v(table, F32), v(table, F32), v(big, low),
        ]
        + gather_sems(count) * 2
        + [DMA((4,)), DMA((count,)), DMA((count,)), DMA, DMA((groups,)), DMA((groups,)), DMA((9,))]
        + Reduce.scratch(line, rows, width, low),
        compiler_params=params(ident),
        name="attention",
    )(lengths, own, cot, pre_gain, mid_gain, freq, wq, wk, wv, wo)


def ffn_kernel(
    line, groups,
    tokens, branch, gains, cot_hbm, gate_hbm, up_hbm, down_hbm,
    second, ffn_hbm, pair_hbm, chip_in,
    own, rights, gate_up, down_w, lefts, parts, stage, theirs,
    *scratch,
):
    p = Place(line)
    rank = lax.axis_index("grp")
    core = lax.rem(rank, 2)
    partner = rank + 1 - 2 * core
    opposite = lax.rem(rank + 2, groups)
    (load_sem, out_sem, stage_send, stage_recv, chip_send, chip_recv) = scratch[3:9]
    units = down_w.shape[0]
    gate_w, up_w = gate_up.at[pl.ds(0, units)], gate_up.at[pl.ds(units, units)]
    cot, normed = rights.at[0], rights.at[1]
    hidden, gate_g, up_g = lefts.at[0], lefts.at[1], lefts.at[2]
    loads = [
        pltpu.make_async_copy(src, dst, load_sem.at[i])
        for i, (src, dst) in enumerate(
            ((gate_hbm, gate_w), (up_hbm, up_w), (cot_hbm, cot), (down_hbm, down_w))
        )
    ]
    start_all(loads)
    middle = tokens[...].astype(F32) + branch[...]
    own[...] = (middle * inverse_rms(middle) * gain_row(gains, 1)).astype(own.dtype)
    p.greet(groups)
    gather = Gather(p, own, normed, *scratch[:3])
    gather.start()
    wait_all(loads)
    rows = own.shape[0]
    pair = 2 * rows
    low = own.dtype

    def branch_rows(block, count):
        size = count * rows
        x = normed[pl.ds(block, count)].reshape(size, -1)
        g = dot_t(x, gate_w[...])
        u = dot_t(x, up_w[...])
        dh = dot_t(cot[pl.ds(block, count)].reshape(size, -1), down_w[...])
        s = 1.0 / (1.0 + jnp.exp(-g))
        silu = g * s
        at = pl.ds(pl.multiple_of(block * rows, rows), size)
        hidden[at] = (silu * u).astype(low)
        up_g[at] = (dh * silu).astype(low)
        gate_g[at] = (dh * u * s * (1.0 + g * (1.0 - s))).astype(low)
        part = dot(gate_g[at], gate_w[...]) + dot(up_g[at], up_w[...])
        parts[pl.ds(block, count)] = part.astype(low).reshape(count, rows, -1)

    @pl.loop(0, line - 1)
    def _(i):
        gather.hop(i + 1)
        d = p.near(i)
        gather.whole(d)
        branch_rows(2 * d, 2)

    last = p.far(0)

    @pl.loop(0, 2)
    def _(i):
        either(i == 1, lambda: gather.whole(last))
        branch_rows(2 * last + lax.rem(p.y + i, 2), 1)

    reduce = Reduce(p, parts, second, scratch[9:])
    for i in range(line):
        reduce.send_across(i)

    quarter = units // 4
    half = units // 2

    def mine(which):
        start = lax.rem(which + 2, 3) * half
        return gate_up.at[pl.ds(pl.multiple_of(start, half), half)]

    def to_partner(which, j):
        return to_peer(
            "grp",
            partner,
            stage.at[j],
            theirs.at[which, pl.ds(pl.multiple_of(j * quarter, quarter), quarter)],
            stage_send.at[j],
            stage_recv.at[which, j],
        )

    def chip_copy():
        return to_peer(
            "grp",
            opposite,
            gate_up.at[pl.ds(2 * half, chip_in.shape[0])],
            chip_in,
            chip_send,
            chip_recv,
        )

    def save_pair(which):
        return pltpu.make_async_copy(mine(which), pair_hbm.at[which], out_sem.at[which])

    @pl.loop(0, 3)
    def _(which):
        right = rights.at[jnp.minimum(which, 1)]

        def block(q):
            cols = pl.ds(pl.multiple_of(q * quarter, quarter), quarter)
            left = lefts[which, :, cols]
            return t_dot(left, right[...].reshape(left.shape[0], -1)).astype(low)

        @pl.loop(0, 2)
        def _(j):
            either(which > 0, lambda: to_partner(which - 1, j).wait_send())
            stage[j] = block(2 * (1 - core) + j)
            to_partner(which, j).start()

        @pl.when(which == 0)
        def _():
            for i in range(line - 1):
                reduce.b_hop(i)

        at_end = p.low_end | p.high_end
        either(at_end, lambda: reduce.step(which, 0))

        @pl.loop(0, 2)
        def _(j):
            at = pl.ds(pl.multiple_of(j * quarter, quarter), quarter)
            mine(which)[at] = block(2 * core + j)

        @pl.when(at_end)
        def _():
            for c in range(1, CHUNKS):
                reduce.step(which, c)

        for j in range(2):
            to_partner(which, j).wait_recv()
        total_into(mine(which), mine(which), theirs.at[which])
        either(which == 0, lambda: chip_copy().start())
        save_pair(which).start()

        @pl.when(jnp.logical_not(at_end))
        def _():
            for c in range(CHUNKS):
                reduce.step(which, c)

    gather.drain()

    @pl.loop(0, line)
    def _(d):
        at = pl.ds(pl.multiple_of(d * pair, pair), pair)
        normed[pl.ds(2 * d, 2)] = dot(hidden[at], down_w[...]).astype(low).reshape(2, rows, -1)

    ffn_save = pltpu.make_async_copy(normed, ffn_hbm, out_sem.at[3])
    ffn_save.start()
    reduce.finish()
    for j in range(2):
        to_partner(2, j).wait_send()

    reduce.drain()
    chip_copy().wait()
    ffn_save.wait()
    for which in range(3):
        save_pair(which).wait()


def ffn(tokens, branch, gains, cot, gate_w, up_w, down_w, groups, ident):
    rows, width = tokens.shape
    count = cot.shape[0]
    line = count // 2
    units = gate_w.shape[0]
    low = tokens.dtype
    v = pltpu.VMEM
    tall = count * rows
    shape = jax.ShapeDtypeStruct
    big = (count, rows, width)
    half = (units // 2, width)
    return pl.pallas_call(
        functools.partial(ffn_kernel, line, groups),
        out_shape=(
            shape((rows, width), F32),
            shape(big, low),
            shape((3,) + half, low),
            shape((EARLY * PIECE, width), low),
        ),
        in_specs=[vm()] * 3 + [hbm()] * 4,
        out_specs=(vm(), hbm(), hbm(), hbm()),
        scratch_shapes=[v((rows, width), low)]
        + [v((2,) + big, low), v((2 * units, width), low), v((units, width), low)]
        + [v((3, tall, units), low), v(big, low), v((2, units // 4, width), low), v((3,) + half, low)]
        + gather_sems(count)
        + [DMA((4,)), DMA((4,)), DMA((2,)), DMA((3, 2)), DMA, DMA]
        + Reduce.scratch(line, rows, width, low),
        compiler_params=params(ident),
        name="ffn",
    )(tokens, branch, gains, cot, gate_w, up_w, down_w)


def attention_grad_kernel(
    line, groups, seqs,
    lengths, tokens, branch, cot, second, gains, cosine, sine,
    ffn_hbm, normed_hbm, attended_hbm, q_hbm, k_hbm, v_hbm, wq_hbm, wkv_hbm, wo_hbm, sums_hbm, early_hbm,
    mixed, input_grad, gain_out, total_hbm, wide_hbm, narrow_hbm,
    own, middle_grad, first, ffn_own, dbranch, normed, attended, q, k, v, wq, wkv, wo, da, dk_acc, dv_acc, dq_rows, dk_rows, dv_rows,
    halves, half_in, ffn_parts, sums, sums_in, stage, mine, theirs, mine_in, gain_held, gain_in, gain_sum, gain_all,
    *scratch,
):
    p = Place(line)
    count = 2 * line
    rank = lax.axis_index("grp")
    core = lax.rem(rank, 2)
    partner = rank + 1 - 2 * core
    opposite = lax.rem(rank + 2, groups)
    (
        load_sem, chip_send, chip_recv, half_send, half_recv, stage_send, stage_recv,
        back_send, back_recv, keep_sem, ga_send, ga_recv, gb_send, gb_recv,
    ) = scratch[3:17]
    n = Reduce.N_SCRATCH
    loads = [
        pltpu.make_async_copy(src, dst, load_sem.at[i])
        for i, (src, dst) in enumerate(
            (
                (wo_hbm, wo),
                (ffn_hbm, ffn_parts),
                (attended_hbm, attended),
                (q_hbm, q),
                (k_hbm, k),
                (v_hbm, v),
                (wq_hbm, wq),
                (wkv_hbm, wkv),
                (normed_hbm, normed),
                (early_hbm, sums_in.at[pl.ds(0, EARLY)]),
            )
        )
    ]
    start_all(loads)

    def load_sum(i):
        return pltpu.make_async_copy(sums_hbm.at[i], sums.at[lax.rem(i, 2)], load_sem.at[10 + lax.rem(i, 2)])

    load_sum(0).start()
    load_sum(1).start()
    middle = tokens[...].astype(F32) + branch[...]
    inverse = inverse_rms(middle)
    grad = cot[...].astype(F32)
    grad = jnp.where(row_valid(p, lengths, grad.shape[0]), grad, jnp.zeros_like(grad))
    grad = grad + norm_grad(middle, inverse, gain_row(gains, 1), second[...])
    middle_grad[...] = grad
    own[...] = grad.astype(own.dtype)
    mid_total = jnp.sum(second[...] * middle * inverse, 0, keepdims=True)
    share = gain_held.shape[2]
    for b in range(count):
        gain_held[b] = jnp.zeros(gain_held.shape[1:], F32)
        gain_held[b, 1:2] = mid_total[:, b * share : (b + 1) * share]
    p.greet(groups)
    gather = Gather(p, own, dbranch, *scratch[:3])
    n_sums = sums_hbm.shape[0]
    part_rows = sums.shape[1]

    def chip_copy(i):
        return to_peer(
            "grp", opposite, sums_hbm.at[i], sums_in.at[i], chip_send.at[i], chip_recv.at[i]
        )

    gather.start()

    @pl.loop(EARLY, n_sums)
    def _(i):
        chip_copy(i).start()

    wait_all(loads)
    ffn_sum = Reduce(p, ffn_parts, ffn_own, scratch[17 : 17 + n])
    rows = own.shape[0]
    pair = 2 * rows
    slots = rows // seqs
    low = own.dtype
    scale = 1.0 / math.sqrt(HD)

    @pl.loop(0, line)
    def _(i):
        gather.hop(i + 1)

        @pl.when(i == line - 2)
        def _():
            for first_sends in range(DEPTH):
                ffn_sum.send_across(first_sends)

        d = p.near(i)
        gather.whole(d)
        grad = dot_t(dbranch[pl.ds(2 * d, 2)].reshape(pair, -1), wo[...]).astype(low)
        for block in range(2):
            for m in range(seqs):
                at = pl.ds(pl.multiple_of(d * 2 * slots + block * slots, slots), slots)
                da[m, at] = grad[block * rows + m * slots : block * rows + (m + 1) * slots]

    for i in range(line - 1):
        ffn_sum.b_hop(i)

    chunk = stage.shape[1]

    def to_partner(b):
        return to_peer(
            "grp",
            partner,
            stage.at[b // 2],
            theirs.at[pl.ds(b // 2 * chunk, chunk)],
            stage_send.at[b // 2],
            stage_recv.at[b // 2],
        )

    def gradient(b, left, right):
        value = t_dot(left, right[...].reshape(left.shape[0], -1)).astype(low)
        keep = core == b % 2

        @pl.when(keep)
        def _():
            mine[pl.ds(b // 2 * chunk, chunk)] = value

        @pl.when(jnp.logical_not(keep))
        def _():
            stage[b // 2] = value
            to_partner(b).start()

    total_slots = q.shape[1]
    tile = min(256, total_slots)

    def backward(m):
        dk_acc[...] = jnp.zeros_like(dk_acc)
        dv_acc[...] = jnp.zeros_like(dv_acc)

        def to_rows(target, value, start, size):
            for c in range(size // slots):
                b = start // slots + c
                target[pl.ds(pl.multiple_of(b * rows + m * slots, slots), slots)] = value[
                    c * slots : (c + 1) * slots
                ]

        for t in range(total_slots // tile):
            span = (t + 1) * tile
            at = pl.ds(t * tile, tile)
            query, grad = q[m, at], da[m, at]
            keys, values = k[m, pl.ds(0, span)], v[m, pl.ds(0, span)]
            probs = probabilities(query, keys, t * tile, lengths[m])
            dprobs = dot_t(grad, values)
            inner = jnp.sum(probs * dprobs, -1, keepdims=True)
            dscores = (probs * (dprobs - inner)).astype(low)
            dq = turn_back(dot(dscores, keys) * scale, cosine[at], sine[at])
            to_rows(dq_rows, dq.astype(low), t * tile, tile)
            dk_acc[pl.ds(0, span)] += t_dot(dscores, query)
            dv_acc[pl.ds(0, span)] += t_dot(probs.astype(low), grad)
        dk = turn_back(dk_acc[...] * scale, cosine[...], sine[...])
        to_rows(dk_rows, dk.astype(low), 0, total_slots)
        to_rows(dv_rows, dv_acc[...].astype(low), 0, total_slots)

    half = HD // 2

    def swap():
        return to_peer("shard", p.cross, halves.at[1 - p.y], half_in, half_send, half_recv)

    gradient(0, attended[:, :chunk], dbranch)
    gradient(1, attended[:, chunk:], dbranch)

    @pl.loop(0, seqs)
    def _(m):
        backward(m)
        ffn_sum.hop(m)
        ffn_sum.send_across(m + DEPTH)

    for h in range(2):
        halves[h, 0] = dk_rows[:, h * half : (h + 1) * half]
        halves[h, 1] = dv_rows[:, h * half : (h + 1) * half]
    swap().start()
    gather.drain()
    parts = dbranch
    gradient(2, dq_rows[:, :chunk], normed)
    gradient(3, dq_rows[:, chunk:], normed)

    spans = (pl.ds(0, 2 * chunk), pl.ds(2 * chunk, chunk))

    def attn_chip(part):
        return to_peer(
            "grp",
            opposite,
            mine.at[spans[part]],
            mine_in.at[spans[part]],
            chip_send.at[n_sums + part],
            chip_recv.at[n_sums + part],
        )

    def attn_pair(part, blocks):
        for b in blocks:
            to_partner(2 * b).wait_recv()
        at = mine.at[spans[part]]
        total_into(at, at, theirs.at[spans[part]])
        attn_chip(part).start()

    def back_attn(slot):
        if slot < 2:
            out = wide_hbm.at[slot, pl.ds(pl.multiple_of(core * chunk, chunk), chunk)]
        else:
            out = narrow_hbm.at[core]
        at = mine.at[pl.ds(slot * chunk, chunk)]
        n_slot = n_sums + slot
        sems = keep_sem.at[n_slot], back_send.at[n_slot], back_recv.at[n_slot]
        return pltpu.make_async_copy(at, out, sems[0]), to_peer("grp", partner, at, out, *sems[1:])

    def attn_total(part):
        attn_chip(part).wait()
        at = mine.at[spans[part]]
        total_into(at, at, mine_in.at[spans[part]])
        for slot in (0, 1) if part == 0 else (2,):
            start_all(back_attn(slot))


    @pl.loop(0, line)
    def _(d):
        at = pl.ds(pl.multiple_of(d * pair, pair), pair)
        part = dot(dq_rows[at], wq[...]) + dot(dk_rows[at], wkv[0]) + dot(dv_rows[at], wkv[1])
        parts[pl.ds(2 * d, 2)] = part.astype(low).reshape(2, rows, -1)

    for i in range(seqs, line - 1):
        ffn_sum.hop(i)
    attn_pair(0, (0, 1))
    ffn_sum.finish()
    reduce = Reduce(p, parts, first, scratch[17 + n :])
    for i in range(DEPTH):
        reduce.send_across(i)
    for i in range(line - 1):
        reduce.b_hop(i)

    def summed(which):
        return (halves[p.y, which].astype(F32) + half_in[which].astype(F32)).astype(low)

    valid = row_valid(p, lengths, rows)
    result = tokens[...].astype(F32) + branch[...] + ffn_own[...]
    mixed[...] = jnp.where(valid, result, jnp.zeros_like(result)).astype(low)

    def back(i):
        per_half = n_sums // 3
        start = core * per_half * part_rows + lax.rem(i, per_half) * part_rows
        at = pl.ds(pl.multiple_of(start, part_rows), part_rows)
        out = total_hbm.at[lax.div(i, per_half), at]
        return (
            pltpu.make_async_copy(sums_in.at[i], out, keep_sem.at[i]),
            to_peer("grp", partner, sums_in.at[i], out, back_send.at[i], back_recv.at[i]),
        )

    def sum_up(first_piece, end):
        @pl.loop(first_piece, end)
        def _(i):
            either(i >= EARLY, lambda: chip_copy(i).wait())
            load_sum(i).wait()
            total_into(sums_in.at[i], sums.at[lax.rem(i, 2)], sums_in.at[i])
            either(i + 2 < n_sums, lambda: load_sum(i + 2).start())
            start_all(back(i))

    def gain_copy(step, peer, origin):
        return to_peer(
            "shard", peer, gain_held.at[peer], gain_in.at[origin], ga_send.at[step], ga_recv.at[step]
        )

    def gain_group(step, peer, origin):
        return to_peer(
            "grp", peer, gain_sum, gain_all.at[origin], gb_send.at[step], gb_recv.at[step]
        )

    def gain_first():
        def body(i, total):
            at = pl.ds(pl.multiple_of(i * 16, 16), 16)
            for b in range(count):
                total = total + parts[b, at].astype(F32) * normed[b, at].astype(F32)
            return total

        total = lax.fori_loop(0, rows // 16, body, jnp.zeros((16, parts.shape[2]), F32))
        total = jnp.sum(total, 0, keepdims=True) / gain_row(gains, 0)
        for b in range(count):
            gain_held[b, 0:1] = total[:, b * share : (b + 1) * share]
        for step in range(1, count):
            gain_copy(step, lax.rem(p.me + step, count), p.me).start()

    def gain_second():
        for step in range(1, count):
            gain_copy(step, p.me, lax.rem(p.me + count - step, count)).wait_recv()
        gain_in[p.me] = gain_held[p.me]
        total = gain_in[0]
        for b in range(1, count):
            total = total + gain_in[b]
        gain_sum[...] = total
        gain_all[rank] = total
        for step in range(1, groups):
            gain_group(step, lax.rem(rank + step, groups), rank).start()

    swap().wait_recv()
    gradient(4, summed(0), normed)
    gradient(5, summed(1), normed)
    reduce.hop(0)
    reduce.send_across(DEPTH)
    attn_pair(1, (2,))
    gain_first()
    sum_up(0, n_sums // 2)
    reduce.hop(1)
    reduce.send_across(DEPTH + 1)
    gain_second()
    sum_up(n_sums // 2, n_sums - 3)
    reduce.hop(2)
    sum_up(n_sums - 3, n_sums)
    attn_total(0)
    reduce.finish()
    for step in range(1, groups):
        gain_group(step, rank, lax.rem(rank + groups - step, groups)).wait_recv()
    total = gain_all[0]
    for b in range(1, groups):
        total = total + gain_all[b]
    gain_out[...] = total
    source = tokens[...].astype(F32)
    inner = norm_grad(source, inverse_rms(source), gain_row(gains, 0), first[...])
    input_grad[...] = (middle_grad[...] + inner).astype(low)
    attn_total(1)
    reduce.drain()
    ffn_sum.drain()
    swap().wait_send()
    for b in range(3):
        to_partner(2 * b).wait_send()
    for step in range(1, count):
        gain_copy(step, lax.rem(p.me + step, count), p.me).wait_send()
    for step in range(1, groups):
        gain_group(step, lax.rem(rank + step, groups), rank).wait_send()

    @pl.loop(0, n_sums)
    def _(i):
        wait_all(back(i))

    for slot in range(3):
        wait_all(back_attn(slot))


def attention_grad(
    lengths, tokens, branch, cot, second, gains, cosine, sine, ffn_parts, normed, attended, q, k, v, wq, wkv, wo, sums, early,
    groups, ident,
):
    rows, width = tokens.shape
    count = normed.shape[0]
    line = count // 2
    seqs, total_slots, hd = q.shape
    low = tokens.dtype
    vmem = pltpu.VMEM
    tall = count * rows
    half = hd // 2
    sums = sums.reshape(-1, PIECE, width)
    early = early.reshape(-1, PIECE, width)
    n_sums, part_rows, _ = sums.shape
    shape = jax.ShapeDtypeStruct
    big = vmem((count, rows, width), low)
    head = vmem((seqs, total_slots, hd), low)
    weight = vmem((hd, width), low)
    flat = vmem((tall, hd), low)
    acc = vmem((total_slots, hd), F32)
    third = vmem((3 * half, width), low)
    g = gains.shape
    block = vmem((rows, width), F32)
    return pl.pallas_call(
        functools.partial(attention_grad_kernel, line, groups, seqs),
        out_shape=(
            shape((rows, width), low),
            shape((rows, width), low),
            shape(g[1:], F32),
            shape((3, n_sums // 3 * 2 * part_rows, width), low),
            shape((2, 2 * half, width), low),
            shape((2, half, width), low),
        ),
        in_specs=[scalars()] + [vm()] * 7 + [hbm()] * 11,
        out_specs=(vm(), vm(), vm(), hbm(), hbm(), hbm()),
        scratch_shapes=[
            vmem((rows, width), low), block, block, block,
            big, big, flat, head, head, head, weight, vmem((2, hd, width), low), weight, head, acc, acc,
            flat, flat, flat,
            vmem((2, 2, tall, half), low), vmem((2, tall, half), low), big,
            vmem((2,) + sums.shape[1:], low), vmem(sums.shape, low), vmem((3, half, width), low), third, third, third,
            vmem(g, F32), vmem(g, F32), vmem(g[1:], F32), vmem((groups,) + g[1:], F32),
        ]
        + gather_sems(count)
        + [
            DMA((12,)), DMA((n_sums + 2,)), DMA((n_sums + 2,)), DMA, DMA, DMA((3,)), DMA((3,)),
            DMA((n_sums + 3,)), DMA((n_sums + 3,)), DMA((n_sums + 3,)),
            DMA((count,)), DMA((count,)), DMA((groups,)), DMA((groups,)),
        ]
        + Reduce.scratch(line, rows, width, low) * 2,
        compiler_params=params(ident),
        name="attention_grad",
    )(
        lengths, tokens, branch, cot, second, gains, cosine, sine, ffn_parts, normed, attended, q, k, v, wq, wkv, wo, sums, early
    )


epsilon = 1e-06
theta_base = 1000042.0
masked_value = -1e30


def turned(source):
    half_width = source.shape[-1] // 2
    return jnp.concatenate([-source[..., half_width:], source[..., :half_width]], -1)


def rotate(source, cosine_table, sine_table):
    return source * cosine_table + turned(source) * sine_table


def unrotate(source, cosine_table, sine_table):
    return source * cosine_table - turned(source) * sine_table


def norm_forward(source, norm_gain):
    inverse = lax.rsqrt(jnp.mean(source * source, -1, keepdims=True) + epsilon)
    return (source * inverse * norm_gain, inverse)


def norm_backward(source, inverse, norm_gain, grad_out):
    weighted = grad_out * norm_gain
    inner_sum = jnp.sum(weighted * source, -1, keepdims=True)
    grad_in = (
        inverse * weighted - source * inverse * inverse * inverse * inner_sum / source.shape[-1]
    )
    return (grad_in, jnp.sum(grad_out * source * inverse, 0))


def weight_terms(normed, query_grad, key_grad, value_grad, attended, branch_grad, shard_count):
    token_count, model_width = normed.shape
    query_share = query_grad.shape[1] // shard_count
    kv_share = key_grad.shape[1] // shard_count
    shard_rows = 2 * query_share + 2 * kv_share

    def weight_term(first_row, row_count):
        blocks = row_count // shard_rows

        def columns(matrix, share_cols):
            return matrix.reshape(token_count, blocks, share_cols)

        part_query = jnp.einsum(
            "tmr,td->mrd",
            columns(query_grad, query_share),
            normed,
            preferred_element_type=jnp.float32,
        )
        part_key = jnp.einsum(
            "tmr,td->mrd", columns(key_grad, kv_share), normed, preferred_element_type=jnp.float32
        )
        part_value = jnp.einsum(
            "tmr,td->mrd", columns(value_grad, kv_share), normed, preferred_element_type=jnp.float32
        )
        part_out = jnp.einsum(
            "tmr,td->mrd",
            columns(attended, query_share),
            branch_grad,
            preferred_element_type=jnp.float32,
        )
        return jnp.concatenate([part_query, part_key, part_value, part_out], 1).reshape(
            row_count, model_width
        )

    return (weight_term, shard_rows)


def local_rows(
    tokens,
    lengths,
    prenorm_gain,
    query_weight,
    key_weight,
    value_weight,
    out_weight,
    midnorm_gain,
    gate_weight,
    up_weight,
    down_weight,
    cotangent,
):
    shard_count = lax.axis_size("shard")
    shard_rank = lax.axis_index("shard")
    micro_count, seq_dev, model_width = tokens.shape
    slot_count = seq_dev * shard_count
    repeat_heads = NH // KVH
    query_width = NH * HD
    kv_width = KVH * HD
    score_scale = 1.0 / math.sqrt(HD)
    local_pos = shard_rank * seq_dev + jnp.arange(seq_dev, dtype=jnp.int32)
    key_pos = jnp.arange(slot_count, dtype=jnp.int32)
    inverse_freq = theta_base ** (-(jnp.arange(0, HD, 2).astype(jnp.float32) / HD))
    angles = local_pos.astype(jnp.float32)[:, None] * inverse_freq[None, :]
    cosine_table = jnp.concatenate([jnp.cos(angles), jnp.cos(angles)], -1)[:, None, :]
    sine_table = jnp.concatenate([jnp.sin(angles), jnp.sin(angles)], -1)[:, None, :]
    gate_total = jnp.zeros(gate_weight.shape, jnp.float32)
    up_total = jnp.zeros(up_weight.shape, jnp.float32)
    down_total = jnp.zeros(down_weight.shape, jnp.float32)
    prenorm_total = jnp.zeros((model_width,), jnp.float32)
    midnorm_total = jnp.zeros((model_width,), jnp.float32)
    attn_total = None
    mixed_rows = []
    input_rows = []
    for micro_index in range(micro_count):
        gathered = (
            lax.all_gather(query_weight, "shard", axis=0, tiled=True),
            lax.all_gather(key_weight, "shard", axis=0, tiled=True),
            lax.all_gather(value_weight, "shard", axis=0, tiled=True),
            lax.all_gather(prenorm_gain, "shard", axis=0, tiled=True),
            lax.all_gather(midnorm_gain, "shard", axis=0, tiled=True),
        )
        query_full, key_full, value_full, prenorm_full, midnorm_full = gathered
        prenorm_f = prenorm_full.astype(jnp.float32)
        midnorm_f = midnorm_full.astype(jnp.float32)
        source = tokens[micro_index].astype(jnp.float32)
        length_now = lengths[micro_index]
        valid_rows = local_pos < length_now
        scaled_first, inverse_first = norm_forward(source, prenorm_f)
        normed_first = scaled_first.astype(jnp.bfloat16)
        query_pre = jnp.einsum(
            "sd,qd->sq", normed_first, query_full, preferred_element_type=jnp.float32
        ).reshape(seq_dev, NH, HD)
        key_pre = jnp.einsum(
            "sd,qd->sq", normed_first, key_full, preferred_element_type=jnp.float32
        ).reshape(seq_dev, KVH, HD)
        value_pre = jnp.einsum(
            "sd,qd->sq", normed_first, value_full, preferred_element_type=jnp.float32
        )
        query_rot = rotate(query_pre, cosine_table, sine_table).astype(jnp.bfloat16)
        key_rot = rotate(key_pre, cosine_table, sine_table).astype(jnp.bfloat16)
        key_value = jnp.concatenate(
            [key_rot.reshape(seq_dev, kv_width), value_pre.astype(jnp.bfloat16)], 1
        )
        kv_all = lax.all_gather(key_value, "shard", axis=0, tiled=True)
        keys_all = kv_all[:, :kv_width].reshape(slot_count, KVH, HD)
        values_all = kv_all[:, kv_width:].reshape(slot_count, KVH, HD)
        query_group = query_rot.reshape(seq_dev, KVH, repeat_heads, HD)
        scores = (
            jnp.einsum("skrd,tkd->krst", query_group, keys_all, preferred_element_type=jnp.float32)
            * score_scale
        )
        allowed = (key_pos[None, :] <= local_pos[:, None]) & (key_pos[None, :] < length_now)
        scores = jnp.where(allowed, scores, masked_value)
        row_max = jnp.max(scores, -1, keepdims=True)
        exp_scores = jnp.exp(scores - row_max)
        attention_probs = exp_scores / jnp.sum(exp_scores, -1, keepdims=True)
        probs_low = attention_probs.astype(jnp.bfloat16)
        attended = (
            jnp.einsum("krst,tkd->skrd", probs_low, values_all, preferred_element_type=jnp.float32)
            .astype(jnp.bfloat16)
            .reshape(seq_dev, query_width)
        )
        branch = jnp.dot(
            attended,
            lax.all_gather(out_weight, "shard", axis=0, tiled=True),
            preferred_element_type=jnp.float32,
        )
        middle = source + branch
        scaled_second, inverse_second = norm_forward(middle, midnorm_f)
        normed_second = scaled_second.astype(jnp.bfloat16)
        normed_all = lax.all_gather(normed_second, "shard", axis=0, tiled=True)
        gate_pre = jnp.einsum(
            "sd,fd->sf", normed_all, gate_weight, preferred_element_type=jnp.float32
        )
        up_pre = jnp.einsum("sd,fd->sf", normed_all, up_weight, preferred_element_type=jnp.float32)
        sigmoid_gate = jax.nn.sigmoid(gate_pre)
        silu_gate = gate_pre * sigmoid_gate
        hidden = (silu_gate * up_pre).astype(jnp.bfloat16)
        ffn_part = lax.psum_scatter(
            jnp.dot(hidden, down_weight, preferred_element_type=jnp.float32).astype(jnp.bfloat16),
            "shard",
            scatter_dimension=0,
            tiled=True,
        ).astype(jnp.float32)
        mixed_rows.append(
            jnp.where(valid_rows[:, None], middle + ffn_part, 0.0).astype(jnp.bfloat16)
        )
        cot_low = jnp.where(
            valid_rows[:, None], cotangent[micro_index], jnp.zeros_like(cotangent[micro_index])
        )
        cot_all = lax.all_gather(cot_low, "shard", axis=0, tiled=True)
        hidden_grad = jnp.einsum(
            "sd,fd->sf", cot_all, down_weight, preferred_element_type=jnp.float32
        )
        down_total = down_total + jnp.einsum(
            "sf,sd->fd", hidden, cot_all, preferred_element_type=jnp.float32
        )
        gate_grad = (
            hidden_grad * up_pre * sigmoid_gate * (1.0 + gate_pre * (1.0 - sigmoid_gate))
        ).astype(jnp.bfloat16)
        up_grad = (hidden_grad * silu_gate).astype(jnp.bfloat16)
        gate_total = gate_total + jnp.einsum(
            "sf,sd->fd", gate_grad, normed_all, preferred_element_type=jnp.float32
        )
        up_total = up_total + jnp.einsum(
            "sf,sd->fd", up_grad, normed_all, preferred_element_type=jnp.float32
        )
        second_grad = lax.psum_scatter(
            jnp.dot(gate_grad, gate_weight, preferred_element_type=jnp.float32)
            + jnp.dot(up_grad, up_weight, preferred_element_type=jnp.float32),
            "shard",
            scatter_dimension=0,
            tiled=True,
        )
        middle_part, midnorm_part = norm_backward(middle, inverse_second, midnorm_f, second_grad)
        middle_grad = cot_low.astype(jnp.float32) + middle_part
        midnorm_total = midnorm_total + midnorm_part
        branch_grad = middle_grad.astype(jnp.bfloat16)
        attended_grad = jnp.einsum(
            "sd,qd->sq",
            branch_grad,
            lax.all_gather(out_weight, "shard", axis=0, tiled=True),
            preferred_element_type=jnp.float32,
        ).astype(jnp.bfloat16)
        attended_group = attended_grad.reshape(seq_dev, KVH, repeat_heads, HD)
        probs_grad = jnp.einsum(
            "skrd,tkd->krst", attended_group, values_all, preferred_element_type=jnp.float32
        )
        inner_sum = jnp.sum(attention_probs * probs_grad, -1, keepdims=True)
        scores_grad = (attention_probs * (probs_grad - inner_sum)).astype(jnp.bfloat16)
        query_rot_grad = (
            jnp.einsum(
                "krst,tkd->skrd", scores_grad, keys_all, preferred_element_type=jnp.float32
            ).reshape(seq_dev, NH, HD)
            * score_scale
        )
        query_grad = (
            unrotate(query_rot_grad, cosine_table, sine_table)
            .astype(jnp.bfloat16)
            .reshape(seq_dev, query_width)
        )
        row_count = lax.axis_size("shard") * seq_dev
        key_part = (
            jnp.einsum(
                "krst,skrd->tkd", scores_grad, query_group, preferred_element_type=jnp.float32
            )
            * score_scale
        )
        value_part = jnp.einsum(
            "krst,skrd->tkd", probs_low, attended_group, preferred_element_type=jnp.float32
        )
        kv_grad = lax.psum_scatter(
            jnp.concatenate(
                [key_part.reshape(row_count, kv_width), value_part.reshape(row_count, kv_width)], 1
            ).astype(jnp.bfloat16),
            "shard",
            scatter_dimension=0,
            tiled=True,
        ).astype(jnp.float32)
        key_grad = (
            unrotate(kv_grad[:, :kv_width].reshape(seq_dev, KVH, HD), cosine_table, sine_table)
            .astype(jnp.bfloat16)
            .reshape(seq_dev, kv_width)
        )
        value_grad = kv_grad[:, kv_width:].astype(jnp.bfloat16)
        first_grad = jnp.einsum(
            "sq,qd->sd", query_grad, query_full, preferred_element_type=jnp.float32
        )
        first_grad = first_grad + jnp.einsum(
            "sq,qd->sd", key_grad, key_full, preferred_element_type=jnp.float32
        )
        first_grad = first_grad + jnp.einsum(
            "sq,qd->sd", value_grad, value_full, preferred_element_type=jnp.float32
        )
        source_part, prenorm_part = norm_backward(source, inverse_first, prenorm_f, first_grad)
        input_rows.append((middle_grad + source_part).astype(jnp.bfloat16))
        prenorm_total = prenorm_total + prenorm_part
        saved = (normed_first, query_grad, key_grad, value_grad, attended, branch_grad)
        weight_term, shard_rows = weight_terms(*saved, shard_count)
        reduced = lax.psum_scatter(
            weight_term(jnp.int32(0), lax.axis_size("shard") * shard_rows).astype(jnp.bfloat16),
            "shard",
            scatter_dimension=0,
            tiled=True,
        ).astype(jnp.float32)
        attn_total = reduced if attn_total is None else attn_total + reduced
    gain_sums = lax.psum((prenorm_total, midnorm_total), ("grp", "shard"))
    gain_share = model_width // shard_count
    prenorm_gradient = lax.dynamic_slice_in_dim(
        gain_sums[0], shard_rank * gain_share, gain_share, 0
    )
    midnorm_gradient = lax.dynamic_slice_in_dim(
        gain_sums[1], shard_rank * gain_share, gain_share, 0
    )
    summed = (
        lax.psum(attn_total.astype(jnp.bfloat16), "grp").astype(jnp.float32),
        lax.psum(gate_total.astype(jnp.bfloat16), "grp").astype(jnp.float32),
        lax.psum(up_total.astype(jnp.bfloat16), "grp").astype(jnp.float32),
        lax.psum(down_total.astype(jnp.bfloat16), "grp").astype(jnp.float32),
    )
    attn_rows = summed[0]
    query_share = query_width // shard_count
    kv_share = kv_width // shard_count
    query_gradient = attn_rows[:query_share]
    key_gradient = attn_rows[query_share : query_share + kv_share]
    value_gradient = attn_rows[query_share + kv_share : query_share + 2 * kv_share]
    out_gradient = attn_rows[query_share + 2 * kv_share :]
    return (
        jnp.stack(mixed_rows),
        jnp.stack(input_rows),
        prenorm_gradient,
        query_gradient,
        key_gradient,
        value_gradient,
        out_gradient,
        midnorm_gradient,
        summed[1],
        summed[2],
        summed[3],
    )


def local_heads(
    tokens,
    lengths,
    prenorm_gain,
    query_weight,
    key_weight,
    value_weight,
    out_weight,
    midnorm_gain,
    gate_weight,
    up_weight,
    down_weight,
    cotangent,
):
    low = jnp.bfloat16
    count = lax.axis_size("shard")
    groups = lax.axis_size("grp")
    seqs, seq_dev, model_width = tokens.shape
    rows = seqs * seq_dev
    inverse_freq = jnp.asarray(theta_base ** (-np.arange(0, HD, 2) / HD), jnp.float32)
    tokens_low = tokens.reshape(rows, model_width)
    cot_low = cotangent.reshape(rows, model_width)
    branch, gains, normed_first, cot_all, queries, keys, values, attended, kv_head, cosine, sine = (
        attention(
            lengths,
            tokens_low,
            cot_low,
            prenorm_gain,
            midnorm_gain,
            inverse_freq[None, :],
            query_weight,
            key_weight,
            value_weight,
            out_weight,
            count,
            groups,
            1,
        )
    )
    second_grad, ffn_parts, pair_sums, early = ffn(
        tokens_low, branch, gains, cot_all, gate_weight, up_weight, down_weight, groups, 2
    )
    mixed, input_gradient, gain_own, totals, wide, narrow = attention_grad(
        lengths,
        tokens_low,
        branch,
        cot_low,
        second_grad,
        gains,
        cosine,
        sine,
        ffn_parts,
        normed_first,
        attended,
        queries,
        keys,
        values,
        query_weight,
        kv_head,
        out_weight,
        pair_sums,
        early,
        groups,
        3,
    )
    f32 = jnp.float32
    return (
        mixed.reshape(tokens.shape),
        input_gradient.reshape(tokens.shape),
        gain_own[0],
        wide[1].astype(f32),
        narrow[0].astype(f32),
        narrow[1].astype(f32),
        wide[0].astype(f32),
        gain_own[1],
        totals[1].astype(f32),
        totals[2].astype(f32),
        totals[0].astype(f32),
    )


def solution(mesh):
    planes = mesh.shape["shard"] == NH and mesh.shape["grp"] == 4
    local = local_heads if planes else local_rows
    in_specs = (
        P("grp", "shard", None),
        P("grp"),
        P("shard"),
        P("shard", None),
        P("shard", None),
        P("shard", None),
        P("shard", None),
        P("shard"),
        P("shard", None),
        P("shard", None),
        P("shard", None),
        P("grp", "shard", None),
    )
    out_specs = (
        P("grp", "shard", None),
        P("grp", "shard", None),
        P("shard"),
        P("shard", None),
        P("shard", None),
        P("shard", None),
        P("shard", None),
        P("shard"),
        P("shard", None),
        P("shard", None),
        P("shard", None),
    )
    return jax.shard_map(local, mesh=mesh, in_specs=in_specs, out_specs=out_specs, check_vma=False)
```

```python
import functools
import math

import jax
import jax.numpy as jnp
from jax import lax
from jax.experimental import pallas as pl
from jax.experimental.pallas import tpu as pltpu
from jax.sharding import PartitionSpec as P
import numpy as np

NH = 8
KVH = 4
HD = 256
MASKED = -1e30
EPSILON = 1e-06
DEPTH = 2
MESH = pl.DeviceIdType.MESH
F32 = jnp.float32
DMA = pltpu.SemaphoreType.DMA
REST = 16
PIECE = 128
EARLY = 3
CHUNKS = 2


def pieces(rows, rest=REST):
    size = -(-(rows - rest) // (16 * CHUNKS)) * 16
    cuts = [min(i * size, rows - rest) for i in range(CHUNKS + 1)] + [rows]
    return [pl.ds(a, b - a) for a, b in zip(cuts, cuts[1:])]


VMEM_LIMIT = 66_000_000


def either(condition, action):
    pl.when(condition)(action)


def total_into(dst, *srcs):
    step = 16

    @pl.loop(0, dst.shape[0] // step)
    def _(i):
        at = pl.ds(pl.multiple_of(i * step, step), step)
        value = srcs[0][at].astype(F32)
        for src in srcs[1:]:
            value = value + src[at].astype(F32)
        dst[at] = value.astype(dst.dtype)


class Place:
    def __init__(self, line):
        self.line = line
        self.me = lax.axis_index("shard")
        self.z = self.me // 2
        self.y = lax.rem(self.me, 2)
        self.cross = self.me + 1 - 2 * self.y
        self.low_end = self.z == 0
        self.high_end = self.z == line - 1
        near = []
        for z in range(line):
            order = [z]
            for k in range(1, line):
                order += [d for d in (z - k, z + k) if 0 <= d < line]
            near.append(order)
        self.tables = near

    def near(self, i):
        out = jnp.int32(0)
        for z in range(self.line):
            row = jnp.int32(self.tables[z][0])
            for k in range(1, self.line):
                row = jnp.where(i == k, self.tables[z][k], row)
            out = jnp.where(self.z == z, row, out)
        return out

    def far(self, i):
        return self.near(self.line - 1 - i)

    def greet(self, groups):
        self.arrive(groups)
        self.meet(groups)

    def meet(self, groups):
        pl.semaphore_wait(pltpu.get_barrier_semaphore(), 2 * self.line + groups - 2)

    def arrive(self, groups):
        barrier = pltpu.get_barrier_semaphore()
        count = 2 * self.line
        rank = lax.axis_index("grp")
        for step in range(1, count):
            pl.semaphore_signal(
                barrier,
                inc=1,
                device_id={"shard": lax.rem(self.me + step, count)},
                device_id_type=MESH,
            )
        for step in range(1, groups):
            pl.semaphore_signal(
                barrier,
                inc=1,
                device_id={"grp": lax.rem(rank + step, groups)},
                device_id_type=MESH,
            )


class Gather:
    UP, DOWN, CROSS = 0, 1, 2

    def __init__(self, place, own, out, local_sem, send_sem, recv_sem, rest=REST):
        self.p, self.own, self.out = place, own, out
        self.local_sem, self.send_sem, self.recv_sem = local_sem, send_sem, recv_sem
        self.pieces = pieces(own.shape[0], rest)
        self.last = len(self.pieces) - 1

    def copy(self, way, origin, part, own=False):
        p = self.p
        peer = (p.me + 2, p.me - 2, p.cross)[way]
        at = self.pieces[part]
        return pltpu.make_async_remote_copy(
            src_ref=self.own.at[at] if own else self.out.at[origin, at],
            dst_ref=self.out.at[origin, at],
            send_sem=self.send_sem.at[way, origin, part],
            recv_sem=self.recv_sem.at[origin, part],
            device_id={"shard": peer},
            device_id_type=MESH,
        )

    def arrived(self, origin, part):
        self.copy(self.CROSS, origin, part).wait_recv()

    def start(self):
        self.send_own()
        self.pass_rest()

    def send_own(self):
        p = self.p
        pltpu.make_async_copy(self.own, self.out.at[p.me], self.local_sem).start()
        for part in (self.last,) + tuple(range(self.last)):
            self.copy(self.CROSS, p.me, part, True).start()
        for part in range(self.last + 1):
            either(p.z < p.line - 1, lambda: self.copy(self.UP, p.me, part, True).start())
            either(p.z > 0, lambda: self.copy(self.DOWN, p.me, part, True).start())

    def pass_rest(self):
        p = self.p
        self.arrived(p.cross, self.last)
        either(p.z < p.line - 1, lambda: self.copy(self.UP, p.cross, self.last).start())
        either(p.z > 0, lambda: self.copy(self.DOWN, p.cross, self.last).start())
        pltpu.make_async_copy(self.own, self.out.at[p.me], self.local_sem).wait()

    def hop(self, k):
        p = self.p
        below, above = p.me - 2 * k, p.me + 2 * k
        has_below, has_above = p.z - k >= 0, p.z + k < p.line

        def first(origin, part, way, more):
            self.arrived(origin, part)
            self.copy(self.CROSS, origin, part).start()
            either(more, lambda: self.copy(way, origin, part).start())

        def last(origin, other, way, more):
            for block in (origin, other):
                self.arrived(block, self.last)
                either(more, lambda: self.copy(way, block, self.last).start())

        for part in range(self.last):
            either(has_below, lambda: first(below, part, self.UP, p.z < p.line - 1))
            either(has_above, lambda: first(above, part, self.DOWN, p.z > 0))
        either(has_below, lambda: last(below, p.cross - 2 * k, self.UP, p.z < p.line - 1))
        either(has_above, lambda: last(above, p.cross + 2 * k, self.DOWN, p.z > 0))

    def whole(self, position):
        for part in range(self.last):
            self.arrived(2 * position + 1 - self.p.y, part)

    def drain(self):
        p = self.p

        @pl.loop(0, p.line)
        def _(d):
            mine, other = 2 * d + p.y, 2 * d + 1 - p.y
            for part in range(self.last):
                self.copy(self.CROSS, mine, part).wait_send()

            @pl.when(d == p.z)
            def _():
                self.copy(self.CROSS, mine, self.last).wait_send()

            def line_sent(way):
                for part in range(self.last + 1):
                    self.copy(way, mine, part).wait_send()
                self.copy(way, other, self.last).wait_send()

            either((d <= p.z) & (p.z < p.line - 1), lambda: line_sent(self.UP))
            either((d >= p.z) & (p.z > 0), lambda: line_sent(self.DOWN))


class Reduce:
    BUP, BDN, BX = 0, 2, 4
    UP, DOWN, CROSS = 5, 5 + CHUNKS, 5 + 2 * CHUNKS
    WAYS = 5 + 3 * CHUNKS
    N_SCRATCH = 9

    @staticmethod
    def scratch(line, rows, width, dtype):
        v = pltpu.VMEM
        return (
            [v((line, rows - REST, width), dtype)] * 3
            + [v((line, 2, REST, width), dtype)] * 2
            + [v((REST, width), dtype)] * 2
            + [DMA((Reduce.WAYS, line)), DMA((Reduce.WAYS, line))]
        )

    def __init__(self, place, parts, out, scratch):
        self.p, self.parts, self.out = place, parts, out
        self.cross_in, self.up_in, self.down_in, self.bup_in, self.bdn_in = scratch[:5]
        self.bx_out, self.bx_in, self.send_sem, self.recv_sem = scratch[5:]
        self.pieces = pieces(parts.shape[1])
        self.b = self.pieces[-1]

    def desc(self, way, slot, src, dst, peer):
        return pltpu.make_async_remote_copy(
            src_ref=src,
            dst_ref=dst,
            send_sem=self.send_sem.at[way, slot],
            recv_sem=self.recv_sem.at[way, slot],
            device_id={"shard": peer},
            device_id_type=MESH,
        )

    def cross_copy(self, d, c):
        p, at = self.p, self.pieces[c]
        return self.desc(
            self.CROSS + c,
            d,
            self.parts.at[2 * d + 1 - p.y, at],
            self.cross_in.at[d, at],
            p.cross,
        )

    def line_copy(self, up, d, c):
        p, at = self.p, self.pieces[c]
        came = self.up_in if up else self.down_in
        return self.desc(
            (self.UP if up else self.DOWN) + c,
            d,
            self.cross_in.at[d, at],
            came.at[d, at],
            p.me + 2 if up else p.me - 2,
        )

    def b_copy(self, up, d, o, src=None):
        p = self.p
        held = self.bup_in if up else self.bdn_in
        return self.desc(
            (self.BUP if up else self.BDN) + o,
            d,
            held.at[d, o] if src is None else src,
            held.at[d, o],
            p.me + 2 if up else p.me - 2,
        )

    def bx_copy(self):
        return self.desc(self.BX, 0, self.bx_out, self.bx_in, self.p.cross)

    def column(self, o):
        return self.p.y if o == 0 else 1 - self.p.y

    def send_across(self, i):
        for c in range(CHUNKS):
            self.cross_copy(self.p.far(i), c).start()

    def b_hop(self, i):
        p = self.p
        d = p.far(i)

        def go(up):
            first = p.low_end if up else p.high_end
            held = self.bup_in if up else self.bdn_in
            for o in (1, 0):
                mine = self.parts.at[2 * d + self.column(o), self.b]
                either(first, lambda: self.b_copy(up, d, o, mine).start())

                @pl.when(jnp.logical_not(first))
                def _():
                    self.b_copy(up, d, o).wait_recv()
                    total_into(held.at[d, o], mine, held.at[d, o])
                    self.b_copy(up, d, o).start()

        either(d > p.z, lambda: go(True))
        either(d < p.z, lambda: go(False))

    def hop(self, i):
        for c in range(CHUNKS):
            self.step(i, c)

    def step(self, i, c):
        p = self.p
        d = p.far(i)
        self.cross_copy(d, c).wait_recv()
        at = self.pieces[c]
        mine = self.parts.at[2 * d + p.y, at]
        held = self.cross_in.at[d, at]

        def go(up):
            first = p.low_end if up else p.high_end
            came = self.up_in if up else self.down_in
            either(first, lambda: total_into(held, mine, held))

            @pl.when(jnp.logical_not(first))
            def _():
                self.line_copy(up, d, c).wait_recv()
                total_into(held, mine, held, came.at[d, at])

            self.line_copy(up, d, c).start()

        either(d > p.z, lambda: go(True))
        either(d < p.z, lambda: go(False))

    def close(self, dst, mine, ups, downs):
        p = self.p
        either(p.low_end, lambda: total_into(dst, *mine, downs))
        either(p.high_end, lambda: total_into(dst, *mine, ups))
        either(
            jnp.logical_not(p.low_end | p.high_end), lambda: total_into(dst, *mine, ups, downs)
        )

    def finish(self):
        p = self.p
        for o in (1, 0):
            either(jnp.logical_not(p.low_end), lambda: self.b_copy(True, p.z, o).wait_recv())
            either(jnp.logical_not(p.high_end), lambda: self.b_copy(False, p.z, o).wait_recv())
            if o:
                mine = self.parts.at[2 * p.z + self.column(o), self.b]
                self.close(self.bx_out, (mine,), self.bup_in.at[p.z, o], self.bdn_in.at[p.z, o])
                self.bx_copy().start()
        self.bx_copy().wait_recv()
        self.close(
            self.out.at[self.b],
            (self.parts.at[p.me, self.b], self.bx_in),
            self.bup_in.at[p.z, 0],
            self.bdn_in.at[p.z, 0],
        )
        for c in range(CHUNKS):
            self.cross_copy(p.z, c).wait_recv()
            either(jnp.logical_not(p.low_end), lambda: self.line_copy(True, p.z, c).wait_recv())
            either(jnp.logical_not(p.high_end), lambda: self.line_copy(False, p.z, c).wait_recv())
            at = self.pieces[c]
            self.close(
                self.out.at[at],
                (self.parts.at[p.me, at], self.cross_in.at[p.z, at]),
                self.up_in.at[p.z, at],
                self.down_in.at[p.z, at],
            )

    def drain(self):
        p = self.p
        self.bx_copy().wait_send()

        @pl.loop(0, p.line)
        def _(d):
            def line_sent(up):
                for c in range(CHUNKS):
                    self.line_copy(up, d, c).wait_send()
                self.b_copy(up, d, 0).wait_send()
                self.b_copy(up, d, 1).wait_send()

            for c in range(CHUNKS):
                self.cross_copy(d, c).wait_send()
            either(d > p.z, lambda: line_sent(True))
            either(d < p.z, lambda: line_sent(False))


def dot(a, b):
    return jnp.dot(a, b, preferred_element_type=F32)


def dot_t(a, b):
    return lax.dot_general(a, b, (((1,), (1,)), ((), ())), preferred_element_type=F32)


def t_dot(a, b):
    return lax.dot_general(a, b, (((0,), (0,)), ((), ())), preferred_element_type=F32)


def to_peer(axis, peer, src, dst, send_sem, recv_sem):
    return pltpu.make_async_remote_copy(
        src_ref=src,
        dst_ref=dst,
        send_sem=send_sem,
        recv_sem=recv_sem,
        device_id={axis: peer},
        device_id_type=MESH,
    )


def turn_by(v, cosine, sine):
    half = v.shape[-1] // 2
    a, b = v[:, :half], v[:, half:]
    return jnp.concatenate([a * cosine - b * sine, b * cosine + a * sine], -1)


def turn_back(v, cosine, sine):
    return turn_by(v, cosine, -sine)


def probabilities(query, keys, rows_from, limit):
    scores = dot_t(query, keys) * (1.0 / math.sqrt(HD))
    row = lax.broadcasted_iota(jnp.int32, scores.shape, 0) + rows_from
    col = lax.broadcasted_iota(jnp.int32, scores.shape, 1)
    scores = jnp.where((col <= row) & (col < limit), scores, MASKED)
    weight = jnp.exp(scores - jnp.max(scores, -1, keepdims=True))
    return weight / jnp.sum(weight, -1, keepdims=True)


def row_valid(place, lengths, rows):
    slots = rows // lengths.shape[0]
    row = lax.broadcasted_iota(jnp.int32, (rows, 1), 0)
    limit = jnp.full((rows, 1), lengths[0], jnp.int32)
    for n in range(1, lengths.shape[0]):
        limit = jnp.where(row >= n * slots, lengths[n], limit)
    return place.me * slots + lax.rem(row, slots) < limit


def gain_row(shares, which):
    return jnp.concatenate([shares[b, which : which + 1] for b in range(shares.shape[0])], 1)


def inverse_rms(x):
    return lax.rsqrt(jnp.mean(x * x, -1, keepdims=True) + EPSILON)


def norm_grad(x, inverse, gain, grad):
    weighted = grad * gain
    inner = jnp.sum(weighted * x, -1, keepdims=True)
    return inverse * weighted - x * inverse * inverse * inverse * inner / x.shape[-1]


def start_all(copies):
    for c in copies:
        c.start()


def wait_all(copies):
    for c in copies:
        c.wait()


def scalars():
    return pl.BlockSpec(memory_space=pltpu.SMEM)


def hbm():
    return pl.BlockSpec(memory_space=pl.ANY)


def vm():
    return pl.BlockSpec(memory_space=pltpu.VMEM)


def params(ident):
    return pltpu.CompilerParams(
        collective_id=ident, has_side_effects=True, vmem_limit_bytes=VMEM_LIMIT
    )


def gather_sems(count):
    return [DMA, DMA((3, count, CHUNKS + 1)), DMA((count, CHUNKS + 1))]


def attention_kernel(
    line, groups, seqs,
    lengths, own, cot_raw, pre_gain, mid_gain, freq, wq_hbm, wk_hbm, wv_hbm, wo_hbm,
    branch, small_out, normed_hbm, cot_hbm, q_hbm, k_hbm, v_hbm, attended_hbm, wkv_hbm, cos_hbm, sin_hbm,
    small, cot_own, rows_all, normed, cot_all, q, k, v, attended, wq, wkv, wo, cosine, sine, parts,
    *scratch,
):
    p = Place(line)
    count = 2 * line
    rank = lax.axis_index("grp")
    g1, g2 = scratch[:3], scratch[3:6]
    (load_sem, small_send, small_recv, wy_send, wg_send, w_recv, save_sem) = scratch[6:13]
    r_scratch = scratch[13:]
    half = wk_hbm.shape[0]
    piece = half // 2
    at_own = pl.ds(pl.multiple_of(p.y * half, half), half)
    loads = [
        pltpu.make_async_copy(src, dst, load_sem.at[i])
        for i, (src, dst) in enumerate(
            (
                (wk_hbm, wkv.at[0, at_own]),
                (wv_hbm, wkv.at[1, at_own]),
                (wq_hbm, wq),
                (wo_hbm, wo),
            )
        )
    ]
    p.arrive(groups)
    start_all(loads)

    small[...] = jnp.zeros_like(small)
    small[0:1] = pre_gain[...].astype(F32)[None, :]
    small[1:2] = mid_gain[...].astype(F32)[None, :]
    p.meet(groups)

    def small_copy(step, peer, origin):
        return to_peer(
            "shard", peer, small, small_out.at[origin], small_send.at[step], small_recv.at[step]
        )

    for step in range(1, count):
        small_copy(step, lax.rem(p.me + step, count), p.me).start()
    gather = Gather(p, own, rows_all, *g1, rest=2 * REST)
    gather.start()
    cots = Gather(p, cot_own, cot_all, *g2)
    small_out[p.me] = small[...]

    def rows_of(quarter, column):
        return wkv.at[
            quarter // 2,
            pl.ds(pl.multiple_of(column * half + lax.rem(quarter, 2) * piece, piece), piece),
        ]

    def across():
        ref = rows_of(rank, p.y)
        return to_peer("shard", p.cross, ref, ref, wy_send, w_recv.at[rank])

    def share(step):
        ref = rows_of(rank, 1 - p.y)
        return to_peer(
            "grp", lax.rem(rank + step, groups), ref, ref, wg_send.at[step], w_recv.at[rank]
        )

    wait_all(loads)
    across().start()
    pos = lax.broadcasted_iota(jnp.int32, cosine.shape, 0).astype(F32)
    angle = pos * freq[...]
    cosine[...] = jnp.cos(angle)
    sine[...] = jnp.sin(angle)
    cot = cot_raw[...]
    cot_own[...] = jnp.where(row_valid(p, lengths, cot.shape[0]), cot, jnp.zeros_like(cot))
    gather.hop(1)
    for step in range(1, count):
        small_copy(step, p.me, lax.rem(p.me + count - step, count)).wait_recv()
    gain = gain_row(small_out, 0)
    across().wait_recv()
    for step in range(1, groups):
        share(step).start()
    rows = own.shape[0]
    pair = 2 * rows
    slots = rows // seqs
    low = own.dtype
    for step in range(1, groups):
        quarter = lax.rem(rank + step, groups)
        ref = rows_of(quarter, 1 - p.y)
        to_peer("grp", rank, ref, ref, wg_send.at[step], w_recv.at[quarter]).wait_recv()

    @pl.loop(0, line)
    def _(i):
        d = p.near(i)
        gather.whole(d)
        x = rows_all[pl.ds(2 * d, 2)].reshape(pair, -1).astype(F32)
        n = (x * inverse_rms(x) * gain).astype(low)
        normed[pl.ds(2 * d, 2)] = n.reshape(2, rows, -1)
        at = pl.ds(pl.multiple_of(d * 2 * slots, 2 * slots), 2 * slots)
        c, s = cosine[at], sine[at]

        def by_rows(t):
            return jnp.concatenate([t[:slots]] * seqs + [t[slots:]] * seqs, 0)

        c, s = by_rows(c), by_rows(s)

        def put(target, value):
            for block in range(2):
                for m in range(seqs):
                    to = pl.ds(
                        pl.multiple_of(d * 2 * slots + block * slots, slots), slots
                    )
                    target[m, to] = value[block * rows + m * slots : block * rows + (m + 1) * slots]

        put(q, turn_by(dot_t(n, wq[...]), c, s).astype(low))
        put(k, turn_by(dot_t(n, wkv[0]), c, s).astype(low))
        put(v, dot_t(n, wkv[1]).astype(low))
        gather.hop(i + 2)
        either(i == line - 3, cots.send_own)

    saves = [
        pltpu.make_async_copy(src, dst, save_sem.at[i])
        for i, (src, dst) in enumerate(
            (
                (normed, normed_hbm),
                (q, q_hbm),
                (k, k_hbm),
                (v, v_hbm),
                (wkv, wkv_hbm),
                (cosine, cos_hbm),
                (sine, sin_hbm),
            )
        )
    ]
    start_all(saves)
    cots.pass_rest()
    total_slots = q.shape[1]
    tile = min(256, total_slots)

    @pl.loop(0, seqs)
    def _(n):
        for t in range(total_slots // tile):
            span = (t + 1) * tile
            at = pl.ds(t * tile, tile)
            probs = probabilities(q[n, at], k[n, pl.ds(0, span)], t * tile, lengths[n])
            out = dot(probs.astype(low), v[n, pl.ds(0, span)]).astype(low)
            for c in range(tile // slots):
                b = (t * tile) // slots + c
                attended[pl.ds(pl.multiple_of(b * rows + n * slots, slots), slots)] = out[
                    c * slots : (c + 1) * slots
                ]
        cots.hop(n + 1)

    for h in range(seqs + 1, line):
        cots.hop(h)

    @pl.loop(0, line)
    def _(d):
        at = pl.ds(pl.multiple_of(d * pair, pair), pair)
        parts[pl.ds(2 * d, 2)] = dot(attended[at], wo[...]).astype(low).reshape(2, rows, -1)

    reduce = Reduce(p, parts, branch, r_scratch)
    saves2 = [pltpu.make_async_copy(attended, attended_hbm, save_sem.at[7])]
    start_all(saves2)
    for d in range(line):
        cots.whole(d)
    for i in range(DEPTH):
        reduce.send_across(i)
    saves3 = [pltpu.make_async_copy(cot_all, cot_hbm, save_sem.at[8])]
    start_all(saves3)
    for i in range(line - 1):
        reduce.b_hop(i)
    for i in range(line - 1):
        reduce.hop(i)
        if i + DEPTH < line:
            reduce.send_across(i + DEPTH)
    reduce.finish()
    reduce.drain()
    gather.drain()
    cots.drain()
    wait_all(saves + saves2 + saves3)
    across().wait_send()
    for step in range(1, groups):
        share(step).wait_send()
    for step in range(1, count):
        small_copy(step, lax.rem(p.me + step, count), p.me).wait_send()


def attention(lengths, own, cot, pre_gain, mid_gain, freq, wq, wk, wv, wo, count, groups, ident):
    rows, width = own.shape
    seqs = lengths.shape[0]
    total_slots = count * rows // seqs
    small = (8, pre_gain.shape[0])
    line = count // 2
    low = own.dtype
    v = pltpu.VMEM
    shape = jax.ShapeDtypeStruct
    hd = wq.shape[0]
    big = (count, rows, width)
    head = (seqs, total_slots, hd)
    table = (total_slots, hd // 2)
    flat = (count * rows, hd)
    return pl.pallas_call(
        functools.partial(attention_kernel, line, groups, seqs),
        out_shape=(
            shape((rows, width), F32),
            shape((count,) + small, F32),
            shape(big, low),
            shape(big, low),
            shape(head, low),
            shape(head, low),
            shape(head, low),
            shape(flat, low),
            shape((2, hd, width), low),
            shape(table, F32),
            shape(table, F32),
        ),
        in_specs=[scalars()] + [vm()] * 5 + [hbm()] * 4,
        out_specs=(vm(), vm()) + (hbm(),) * 9,
        scratch_shapes=[
            v(small, F32), v((rows, width), low), v(big, low), v(big, low), v(big, low), v(head, low), v(head, low), v(head, low), v(flat, low),
            v((hd, width), low), v((2, hd, width), low), v((hd, width), low), v(table, F32), v(table, F32), v(big, low),
        ]
        + gather_sems(count) * 2
        + [DMA((4,)), DMA((count,)), DMA((count,)), DMA, DMA((groups,)), DMA((groups,)), DMA((9,))]
        + Reduce.scratch(line, rows, width, low),
        compiler_params=params(ident),
        name="attention",
    )(lengths, own, cot, pre_gain, mid_gain, freq, wq, wk, wv, wo)


def ffn_kernel(
    line, groups,
    tokens, branch, gains, cot_hbm, gate_hbm, up_hbm, down_hbm,
    second, ffn_hbm, pair_hbm, chip_in,
    own, rights, gate_up, down_w, lefts, parts, stage, theirs,
    *scratch,
):
    p = Place(line)
    rank = lax.axis_index("grp")
    core = lax.rem(rank, 2)
    partner = rank + 1 - 2 * core
    opposite = lax.rem(rank + 2, groups)
    (load_sem, out_sem, stage_send, stage_recv, chip_send, chip_recv) = scratch[3:9]
    units = down_w.shape[0]
    gate_w, up_w = gate_up.at[pl.ds(0, units)], gate_up.at[pl.ds(units, units)]
    cot, normed = rights.at[0], rights.at[1]
    hidden, gate_g, up_g = lefts.at[0], lefts.at[1], lefts.at[2]
    loads = [
        pltpu.make_async_copy(src, dst, load_sem.at[i])
        for i, (src, dst) in enumerate(
            ((cot_hbm, cot), (down_hbm, down_w), (gate_hbm, gate_w), (up_hbm, up_w))
        )
    ]
    p.arrive(groups)
    start_all(loads)
    middle = tokens[...].astype(F32) + branch[...]
    own[...] = (middle * inverse_rms(middle) * gain_row(gains, 1)).astype(own.dtype)
    p.meet(groups)
    gather = Gather(p, own, normed, *scratch[:3])
    gather.send_own()
    wait_all(loads[:2])
    rows = own.shape[0]
    pair = 2 * rows
    low = own.dtype

    @pl.loop(0, line)
    def _(d):
        at = pl.ds(pl.multiple_of(d * pair, pair), pair)
        gate_g[at] = dot_t(cot[pl.ds(2 * d, 2)].reshape(pair, -1), down_w[...]).astype(low)

    gather.pass_rest()
    wait_all(loads[2:])

    @pl.loop(0, line)
    def _(i):
        gather.hop(i + 1)
        d = p.near(i)
        gather.whole(d)
        x = normed[pl.ds(2 * d, 2)].reshape(pair, -1)
        g = dot_t(x, gate_w[...])
        u = dot_t(x, up_w[...])
        s = 1.0 / (1.0 + jnp.exp(-g))
        silu = g * s
        at = pl.ds(pl.multiple_of(d * pair, pair), pair)
        dh = gate_g[at].astype(F32)
        hidden[at] = (silu * u).astype(low)
        up_g[at] = (dh * silu).astype(low)
        gate_g[at] = (dh * u * s * (1.0 + g * (1.0 - s))).astype(low)
        part = dot(gate_g[at], gate_w[...]) + dot(up_g[at], up_w[...])
        parts[pl.ds(2 * d, 2)] = part.astype(low).reshape(2, rows, -1)

    reduce = Reduce(p, parts, second, scratch[9:])
    for i in range(line):
        reduce.send_across(i)

    quarter = units // 4
    half = units // 2

    def mine(which):
        start = lax.rem(which + 2, 3) * half
        return gate_up.at[pl.ds(pl.multiple_of(start, half), half)]

    def to_partner(which, j):
        return to_peer(
            "grp",
            partner,
            stage.at[j],
            theirs.at[which, pl.ds(pl.multiple_of(j * quarter, quarter), quarter)],
            stage_send.at[j],
            stage_recv.at[which, j],
        )

    def chip_copy():
        return to_peer(
            "grp",
            opposite,
            gate_up.at[pl.ds(2 * half, chip_in.shape[0])],
            chip_in,
            chip_send,
            chip_recv,
        )

    def save_pair(which):
        return pltpu.make_async_copy(mine(which), pair_hbm.at[which], out_sem.at[which])

    @pl.loop(0, 3)
    def _(which):
        right = rights.at[jnp.minimum(which, 1)]

        def block(q):
            cols = pl.ds(pl.multiple_of(q * quarter, quarter), quarter)
            left = lefts[which, :, cols]
            return t_dot(left, right[...].reshape(left.shape[0], -1)).astype(low)

        @pl.loop(0, 2)
        def _(j):
            either(which > 0, lambda: to_partner(which - 1, j).wait_send())
            stage[j] = block(2 * (1 - core) + j)
            to_partner(which, j).start()

        @pl.when(which == 0)
        def _():
            for i in range(line - 1):
                reduce.b_hop(i)

        at_end = p.low_end | p.high_end
        either(at_end, lambda: reduce.step(which, 0))

        @pl.loop(0, 2)
        def _(j):
            at = pl.ds(pl.multiple_of(j * quarter, quarter), quarter)
            mine(which)[at] = block(2 * core + j)

        @pl.when(at_end)
        def _():
            for c in range(1, CHUNKS):
                reduce.step(which, c)

        for j in range(2):
            to_partner(which, j).wait_recv()
        total_into(mine(which), mine(which), theirs.at[which])
        either(which == 0, lambda: chip_copy().start())
        save_pair(which).start()

        @pl.when(jnp.logical_not(at_end))
        def _():
            for c in range(CHUNKS):
                reduce.step(which, c)

    gather.drain()

    @pl.loop(0, line)
    def _(d):
        at = pl.ds(pl.multiple_of(d * pair, pair), pair)
        normed[pl.ds(2 * d, 2)] = dot(hidden[at], down_w[...]).astype(low).reshape(2, rows, -1)

    ffn_save = pltpu.make_async_copy(normed, ffn_hbm, out_sem.at[3])
    ffn_save.start()
    reduce.finish()
    for j in range(2):
        to_partner(2, j).wait_send()

    reduce.drain()
    chip_copy().wait()
    ffn_save.wait()
    for which in range(3):
        save_pair(which).wait()


def ffn(tokens, branch, gains, cot, gate_w, up_w, down_w, groups, ident):
    rows, width = tokens.shape
    count = cot.shape[0]
    line = count // 2
    units = gate_w.shape[0]
    low = tokens.dtype
    v = pltpu.VMEM
    tall = count * rows
    shape = jax.ShapeDtypeStruct
    big = (count, rows, width)
    half = (units // 2, width)
    return pl.pallas_call(
        functools.partial(ffn_kernel, line, groups),
        out_shape=(
            shape((rows, width), F32),
            shape(big, low),
            shape((3,) + half, low),
            shape((EARLY * PIECE, width), low),
        ),
        in_specs=[vm()] * 3 + [hbm()] * 4,
        out_specs=(vm(), hbm(), hbm(), hbm()),
        scratch_shapes=[v((rows, width), low)]
        + [v((2,) + big, low), v((2 * units, width), low), v((units, width), low)]
        + [v((3, tall, units), low), v(big, low), v((2, units // 4, width), low), v((3,) + half, low)]
        + gather_sems(count)
        + [DMA((4,)), DMA((4,)), DMA((2,)), DMA((3, 2)), DMA, DMA]
        + Reduce.scratch(line, rows, width, low),
        compiler_params=params(ident),
        name="ffn",
    )(tokens, branch, gains, cot, gate_w, up_w, down_w)


def attention_grad_kernel(
    line, groups, seqs,
    lengths, tokens, branch, cot, second, gains, cosine, sine,
    ffn_hbm, normed_hbm, attended_hbm, q_hbm, k_hbm, v_hbm, wq_hbm, wkv_hbm, wo_hbm, sums_hbm, early_hbm,
    mixed, input_grad, gain_out, total_hbm, wide_hbm, narrow_hbm,
    own, middle_grad, first, ffn_own, dbranch, normed, attended, q, k, v, wq, wkv, wo, da, dk_acc, dv_acc, dq_rows, dk_rows, dv_rows,
    halves, half_in, ffn_parts, sums, sums_in, stage, mine, theirs, mine_in, gain_held, gain_in, gain_sum, gain_all,
    *scratch,
):
    p = Place(line)
    count = 2 * line
    rank = lax.axis_index("grp")
    core = lax.rem(rank, 2)
    partner = rank + 1 - 2 * core
    opposite = lax.rem(rank + 2, groups)
    (
        load_sem, chip_send, chip_recv, half_send, half_recv, stage_send, stage_recv,
        back_send, back_recv, keep_sem, ga_send, ga_recv, gb_send, gb_recv,
    ) = scratch[3:17]
    n = Reduce.N_SCRATCH
    loads = [
        pltpu.make_async_copy(src, dst, load_sem.at[i])
        for i, (src, dst) in enumerate(
            (
                (wo_hbm, wo),
                (ffn_hbm, ffn_parts),
                (attended_hbm, attended),
                (q_hbm, q),
                (k_hbm, k),
                (v_hbm, v),
                (wq_hbm, wq),
                (wkv_hbm, wkv),
                (normed_hbm, normed),
                (early_hbm, sums_in.at[pl.ds(0, EARLY)]),
            )
        )
    ]
    p.arrive(groups)
    start_all(loads)

    def load_sum(i):
        return pltpu.make_async_copy(sums_hbm.at[i], sums.at[lax.rem(i, 2)], load_sem.at[10 + lax.rem(i, 2)])

    load_sum(0).start()
    load_sum(1).start()
    middle = tokens[...].astype(F32) + branch[...]
    inverse = inverse_rms(middle)
    grad = cot[...].astype(F32)
    grad = jnp.where(row_valid(p, lengths, grad.shape[0]), grad, jnp.zeros_like(grad))
    grad = grad + norm_grad(middle, inverse, gain_row(gains, 1), second[...])
    middle_grad[...] = grad
    own[...] = grad.astype(own.dtype)
    mid_total = jnp.sum(second[...] * middle * inverse, 0, keepdims=True)
    share = gain_held.shape[2]
    for b in range(count):
        gain_held[b] = jnp.zeros(gain_held.shape[1:], F32)
        gain_held[b, 1:2] = mid_total[:, b * share : (b + 1) * share]
    p.meet(groups)
    gather = Gather(p, own, dbranch, *scratch[:3])
    n_sums = sums_hbm.shape[0]
    part_rows = sums.shape[1]

    def chip_copy(i):
        return to_peer(
            "grp", opposite, sums_hbm.at[i], sums_in.at[i], chip_send.at[i], chip_recv.at[i]
        )

    gather.start()

    @pl.loop(EARLY, n_sums)
    def _(i):
        chip_copy(i).start()

    wait_all(loads)
    ffn_sum = Reduce(p, ffn_parts, ffn_own, scratch[17 : 17 + n])
    rows = own.shape[0]
    pair = 2 * rows
    slots = rows // seqs
    low = own.dtype
    scale = 1.0 / math.sqrt(HD)

    @pl.loop(0, line)
    def _(i):
        gather.hop(i + 1)

        @pl.when(i == line - 2)
        def _():
            for first_sends in range(DEPTH):
                ffn_sum.send_across(first_sends)

        d = p.near(i)
        gather.whole(d)
        grad = dot_t(dbranch[pl.ds(2 * d, 2)].reshape(pair, -1), wo[...]).astype(low)
        for block in range(2):
            for m in range(seqs):
                at = pl.ds(pl.multiple_of(d * 2 * slots + block * slots, slots), slots)
                da[m, at] = grad[block * rows + m * slots : block * rows + (m + 1) * slots]

    for i in range(line - 1):
        ffn_sum.b_hop(i)

    chunk = stage.shape[1]

    def to_partner(b):
        return to_peer(
            "grp",
            partner,
            stage.at[b // 2],
            theirs.at[pl.ds(b // 2 * chunk, chunk)],
            stage_send.at[b // 2],
            stage_recv.at[b // 2],
        )

    def gradient(b, left, right):
        value = t_dot(left, right[...].reshape(left.shape[0], -1)).astype(low)
        keep = core == b % 2

        @pl.when(keep)
        def _():
            mine[pl.ds(b // 2 * chunk, chunk)] = value

        @pl.when(jnp.logical_not(keep))
        def _():
            stage[b // 2] = value
            to_partner(b).start()

    total_slots = q.shape[1]
    tile = min(256, total_slots)

    def backward(m):
        dk_acc[...] = jnp.zeros_like(dk_acc)
        dv_acc[...] = jnp.zeros_like(dv_acc)

        def to_rows(target, value, start, size):
            for c in range(size // slots):
                b = start // slots + c
                target[pl.ds(pl.multiple_of(b * rows + m * slots, slots), slots)] = value[
                    c * slots : (c + 1) * slots
                ]

        for t in range(total_slots // tile):
            span = (t + 1) * tile
            at = pl.ds(t * tile, tile)
            query, grad = q[m, at], da[m, at]
            keys, values = k[m, pl.ds(0, span)], v[m, pl.ds(0, span)]
            probs = probabilities(query, keys, t * tile, lengths[m])
            dprobs = dot_t(grad, values)
            inner = jnp.sum(probs * dprobs, -1, keepdims=True)
            dscores = (probs * (dprobs - inner)).astype(low)
            dq = turn_back(dot(dscores, keys) * scale, cosine[at], sine[at])
            to_rows(dq_rows, dq.astype(low), t * tile, tile)
            dk_acc[pl.ds(0, span)] += t_dot(dscores, query)
            dv_acc[pl.ds(0, span)] += t_dot(probs.astype(low), grad)
        dk = turn_back(dk_acc[...] * scale, cosine[...], sine[...])
        to_rows(dk_rows, dk.astype(low), 0, total_slots)
        to_rows(dv_rows, dv_acc[...].astype(low), 0, total_slots)

    half = HD // 2

    def swap():
        return to_peer("shard", p.cross, halves.at[1 - p.y], half_in, half_send, half_recv)

    gradient(0, attended[:, :chunk], dbranch)
    gradient(1, attended[:, chunk:], dbranch)

    @pl.loop(0, seqs)
    def _(m):
        backward(m)
        ffn_sum.hop(m)
        ffn_sum.send_across(m + DEPTH)

    for h in range(2):
        halves[h, 0] = dk_rows[:, h * half : (h + 1) * half]
        halves[h, 1] = dv_rows[:, h * half : (h + 1) * half]
    swap().start()
    gather.drain()
    parts = dbranch
    gradient(2, dq_rows[:, :chunk], normed)
    gradient(3, dq_rows[:, chunk:], normed)

    spans = (pl.ds(0, 2 * chunk), pl.ds(2 * chunk, chunk))

    def attn_chip(part):
        return to_peer(
            "grp",
            opposite,
            mine.at[spans[part]],
            mine_in.at[spans[part]],
            chip_send.at[n_sums + part],
            chip_recv.at[n_sums + part],
        )

    def attn_pair(part, blocks):
        for b in blocks:
            to_partner(2 * b).wait_recv()
        at = mine.at[spans[part]]
        total_into(at, at, theirs.at[spans[part]])
        attn_chip(part).start()

    def back_attn(slot):
        if slot < 2:
            out = wide_hbm.at[slot, pl.ds(pl.multiple_of(core * chunk, chunk), chunk)]
        else:
            out = narrow_hbm.at[core]
        at = mine.at[pl.ds(slot * chunk, chunk)]
        n_slot = n_sums + slot
        sems = keep_sem.at[n_slot], back_send.at[n_slot], back_recv.at[n_slot]
        return pltpu.make_async_copy(at, out, sems[0]), to_peer("grp", partner, at, out, *sems[1:])

    def attn_total(part):
        attn_chip(part).wait()
        at = mine.at[spans[part]]
        total_into(at, at, mine_in.at[spans[part]])
        for slot in (0, 1) if part == 0 else (2,):
            start_all(back_attn(slot))


    @pl.loop(0, line)
    def _(d):
        at = pl.ds(pl.multiple_of(d * pair, pair), pair)
        part = dot(dq_rows[at], wq[...]) + dot(dk_rows[at], wkv[0]) + dot(dv_rows[at], wkv[1])
        parts[pl.ds(2 * d, 2)] = part.astype(low).reshape(2, rows, -1)

    for i in range(seqs, line - 1):
        ffn_sum.hop(i)
    def back(i):
        per_half = n_sums // 3
        start = core * per_half * part_rows + lax.rem(i, per_half) * part_rows
        at = pl.ds(pl.multiple_of(start, part_rows), part_rows)
        out = total_hbm.at[lax.div(i, per_half), at]
        return (
            pltpu.make_async_copy(sums_in.at[i], out, keep_sem.at[i]),
            to_peer("grp", partner, sums_in.at[i], out, back_send.at[i], back_recv.at[i]),
        )

    def sum_up(first_piece, end):
        @pl.loop(first_piece, end)
        def _(i):
            either(i >= EARLY, lambda: chip_copy(i).wait())
            load_sum(i).wait()
            total_into(sums_in.at[i], sums.at[lax.rem(i, 2)], sums_in.at[i])
            either(i + 2 < n_sums, lambda: load_sum(i + 2).start())
            start_all(back(i))

    def gain_copy(step, peer, origin):
        return to_peer(
            "shard", peer, gain_held.at[peer], gain_in.at[origin], ga_send.at[step], ga_recv.at[step]
        )

    def gain_group(step, peer, origin):
        return to_peer(
            "grp", peer, gain_sum, gain_all.at[origin], gb_send.at[step], gb_recv.at[step]
        )

    def gain_first():
        def body(i, total):
            at = pl.ds(pl.multiple_of(i * 16, 16), 16)
            for b in range(count):
                total = total + parts[b, at].astype(F32) * normed[b, at].astype(F32)
            return total

        total = lax.fori_loop(0, rows // 16, body, jnp.zeros((16, parts.shape[2]), F32))
        total = jnp.sum(total, 0, keepdims=True) / gain_row(gains, 0)
        for b in range(count):
            gain_held[b, 0:1] = total[:, b * share : (b + 1) * share]
        for step in range(1, count):
            gain_copy(step, lax.rem(p.me + step, count), p.me).start()

    def gain_second():
        for step in range(1, count):
            gain_copy(step, p.me, lax.rem(p.me + count - step, count)).wait_recv()
        gain_in[p.me] = gain_held[p.me]
        total = gain_in[0]
        for b in range(1, count):
            total = total + gain_in[b]
        gain_sum[...] = total
        gain_all[rank] = total
        for step in range(1, groups):
            gain_group(step, lax.rem(rank + step, groups), rank).start()

    sum_up(0, n_sums // 3)
    attn_pair(0, (0, 1))
    gain_first()
    ffn_sum.finish()
    reduce = Reduce(p, parts, first, scratch[17 + n :])
    for i in range(DEPTH):
        reduce.send_across(i)
    for i in range(line - 1):
        reduce.b_hop(i)

    def summed(which):
        return (halves[p.y, which].astype(F32) + half_in[which].astype(F32)).astype(low)

    valid = row_valid(p, lengths, rows)
    result = tokens[...].astype(F32) + branch[...] + ffn_own[...]
    mixed[...] = jnp.where(valid, result, jnp.zeros_like(result)).astype(low)

    swap().wait_recv()
    gradient(4, summed(0), normed)
    gradient(5, summed(1), normed)
    reduce.hop(0)
    reduce.send_across(DEPTH)
    attn_pair(1, (2,))
    sum_up(n_sums // 3, n_sums // 2)
    reduce.hop(1)
    reduce.send_across(DEPTH + 1)
    gain_second()
    sum_up(n_sums // 2, n_sums - 3)
    reduce.hop(2)
    sum_up(n_sums - 3, n_sums)
    attn_total(0)
    reduce.finish()
    attn_total(1)
    for step in range(1, groups):
        gain_group(step, rank, lax.rem(rank + groups - step, groups)).wait_recv()
    total = gain_all[0]
    for b in range(1, groups):
        total = total + gain_all[b]
    gain_out[...] = total
    source = tokens[...].astype(F32)
    inner = norm_grad(source, inverse_rms(source), gain_row(gains, 0), first[...])
    input_grad[...] = (middle_grad[...] + inner).astype(low)
    reduce.drain()
    ffn_sum.drain()
    swap().wait_send()
    for b in range(3):
        to_partner(2 * b).wait_send()
    for step in range(1, count):
        gain_copy(step, lax.rem(p.me + step, count), p.me).wait_send()
    for step in range(1, groups):
        gain_group(step, lax.rem(rank + step, groups), rank).wait_send()

    @pl.loop(0, n_sums)
    def _(i):
        wait_all(back(i))

    for slot in range(3):
        wait_all(back_attn(slot))


def attention_grad(
    lengths, tokens, branch, cot, second, gains, cosine, sine, ffn_parts, normed, attended, q, k, v, wq, wkv, wo, sums, early,
    groups, ident,
):
    rows, width = tokens.shape
    count = normed.shape[0]
    line = count // 2
    seqs, total_slots, hd = q.shape
    low = tokens.dtype
    vmem = pltpu.VMEM
    tall = count * rows
    half = hd // 2
    sums = sums.reshape(-1, PIECE, width)
    early = early.reshape(-1, PIECE, width)
    n_sums, part_rows, _ = sums.shape
    shape = jax.ShapeDtypeStruct
    big = vmem((count, rows, width), low)
    head = vmem((seqs, total_slots, hd), low)
    weight = vmem((hd, width), low)
    flat = vmem((tall, hd), low)
    acc = vmem((total_slots, hd), F32)
    third = vmem((3 * half, width), low)
    g = gains.shape
    block = vmem((rows, width), F32)
    return pl.pallas_call(
        functools.partial(attention_grad_kernel, line, groups, seqs),
        out_shape=(
            shape((rows, width), low),
            shape((rows, width), low),
            shape(g[1:], F32),
            shape((3, n_sums // 3 * 2 * part_rows, width), low),
            shape((2, 2 * half, width), low),
            shape((2, half, width), low),
        ),
        in_specs=[scalars()] + [vm()] * 7 + [hbm()] * 11,
        out_specs=(vm(), vm(), vm(), hbm(), hbm(), hbm()),
        scratch_shapes=[
            vmem((rows, width), low), block, block, block,
            big, big, flat, head, head, head, weight, vmem((2, hd, width), low), weight, head, acc, acc,
            flat, flat, flat,
            vmem((2, 2, tall, half), low), vmem((2, tall, half), low), big,
            vmem((2,) + sums.shape[1:], low), vmem(sums.shape, low), vmem((3, half, width), low), third, third, third,
            vmem(g, F32), vmem(g, F32), vmem(g[1:], F32), vmem((groups,) + g[1:], F32),
        ]
        + gather_sems(count)
        + [
            DMA((12,)), DMA((n_sums + 2,)), DMA((n_sums + 2,)), DMA, DMA, DMA((3,)), DMA((3,)),
            DMA((n_sums + 3,)), DMA((n_sums + 3,)), DMA((n_sums + 3,)),
            DMA((count,)), DMA((count,)), DMA((groups,)), DMA((groups,)),
        ]
        + Reduce.scratch(line, rows, width, low) * 2,
        compiler_params=params(ident),
        name="attention_grad",
    )(
        lengths, tokens, branch, cot, second, gains, cosine, sine, ffn_parts, normed, attended, q, k, v, wq, wkv, wo, sums, early
    )


epsilon = 1e-06
theta_base = 1000042.0
masked_value = -1e30


def turned(source):
    half_width = source.shape[-1] // 2
    return jnp.concatenate([-source[..., half_width:], source[..., :half_width]], -1)


def rotate(source, cosine_table, sine_table):
    return source * cosine_table + turned(source) * sine_table


def unrotate(source, cosine_table, sine_table):
    return source * cosine_table - turned(source) * sine_table


def norm_forward(source, norm_gain):
    inverse = lax.rsqrt(jnp.mean(source * source, -1, keepdims=True) + epsilon)
    return (source * inverse * norm_gain, inverse)


def norm_backward(source, inverse, norm_gain, grad_out):
    weighted = grad_out * norm_gain
    inner_sum = jnp.sum(weighted * source, -1, keepdims=True)
    grad_in = (
        inverse * weighted - source * inverse * inverse * inverse * inner_sum / source.shape[-1]
    )
    return (grad_in, jnp.sum(grad_out * source * inverse, 0))


def weight_terms(normed, query_grad, key_grad, value_grad, attended, branch_grad, shard_count):
    token_count, model_width = normed.shape
    query_share = query_grad.shape[1] // shard_count
    kv_share = key_grad.shape[1] // shard_count
    shard_rows = 2 * query_share + 2 * kv_share

    def weight_term(first_row, row_count):
        blocks = row_count // shard_rows

        def columns(matrix, share_cols):
            return matrix.reshape(token_count, blocks, share_cols)

        part_query = jnp.einsum(
            "tmr,td->mrd",
            columns(query_grad, query_share),
            normed,
            preferred_element_type=jnp.float32,
        )
        part_key = jnp.einsum(
            "tmr,td->mrd", columns(key_grad, kv_share), normed, preferred_element_type=jnp.float32
        )
        part_value = jnp.einsum(
            "tmr,td->mrd", columns(value_grad, kv_share), normed, preferred_element_type=jnp.float32
        )
        part_out = jnp.einsum(
            "tmr,td->mrd",
            columns(attended, query_share),
            branch_grad,
            preferred_element_type=jnp.float32,
        )
        return jnp.concatenate([part_query, part_key, part_value, part_out], 1).reshape(
            row_count, model_width
        )

    return (weight_term, shard_rows)


def local_rows(
    tokens,
    lengths,
    prenorm_gain,
    query_weight,
    key_weight,
    value_weight,
    out_weight,
    midnorm_gain,
    gate_weight,
    up_weight,
    down_weight,
    cotangent,
):
    shard_count = lax.axis_size("shard")
    shard_rank = lax.axis_index("shard")
    micro_count, seq_dev, model_width = tokens.shape
    slot_count = seq_dev * shard_count
    repeat_heads = NH // KVH
    query_width = NH * HD
    kv_width = KVH * HD
    score_scale = 1.0 / math.sqrt(HD)
    local_pos = shard_rank * seq_dev + jnp.arange(seq_dev, dtype=jnp.int32)
    key_pos = jnp.arange(slot_count, dtype=jnp.int32)
    inverse_freq = theta_base ** (-(jnp.arange(0, HD, 2).astype(jnp.float32) / HD))
    angles = local_pos.astype(jnp.float32)[:, None] * inverse_freq[None, :]
    cosine_table = jnp.concatenate([jnp.cos(angles), jnp.cos(angles)], -1)[:, None, :]
    sine_table = jnp.concatenate([jnp.sin(angles), jnp.sin(angles)], -1)[:, None, :]
    gate_total = jnp.zeros(gate_weight.shape, jnp.float32)
    up_total = jnp.zeros(up_weight.shape, jnp.float32)
    down_total = jnp.zeros(down_weight.shape, jnp.float32)
    prenorm_total = jnp.zeros((model_width,), jnp.float32)
    midnorm_total = jnp.zeros((model_width,), jnp.float32)
    attn_total = None
    mixed_rows = []
    input_rows = []
    for micro_index in range(micro_count):
        gathered = (
            lax.all_gather(query_weight, "shard", axis=0, tiled=True),
            lax.all_gather(key_weight, "shard", axis=0, tiled=True),
            lax.all_gather(value_weight, "shard", axis=0, tiled=True),
            lax.all_gather(prenorm_gain, "shard", axis=0, tiled=True),
            lax.all_gather(midnorm_gain, "shard", axis=0, tiled=True),
        )
        query_full, key_full, value_full, prenorm_full, midnorm_full = gathered
        prenorm_f = prenorm_full.astype(jnp.float32)
        midnorm_f = midnorm_full.astype(jnp.float32)
        source = tokens[micro_index].astype(jnp.float32)
        length_now = lengths[micro_index]
        valid_rows = local_pos < length_now
        scaled_first, inverse_first = norm_forward(source, prenorm_f)
        normed_first = scaled_first.astype(jnp.bfloat16)
        query_pre = jnp.einsum(
            "sd,qd->sq", normed_first, query_full, preferred_element_type=jnp.float32
        ).reshape(seq_dev, NH, HD)
        key_pre = jnp.einsum(
            "sd,qd->sq", normed_first, key_full, preferred_element_type=jnp.float32
        ).reshape(seq_dev, KVH, HD)
        value_pre = jnp.einsum(
            "sd,qd->sq", normed_first, value_full, preferred_element_type=jnp.float32
        )
        query_rot = rotate(query_pre, cosine_table, sine_table).astype(jnp.bfloat16)
        key_rot = rotate(key_pre, cosine_table, sine_table).astype(jnp.bfloat16)
        key_value = jnp.concatenate(
            [key_rot.reshape(seq_dev, kv_width), value_pre.astype(jnp.bfloat16)], 1
        )
        kv_all = lax.all_gather(key_value, "shard", axis=0, tiled=True)
        keys_all = kv_all[:, :kv_width].reshape(slot_count, KVH, HD)
        values_all = kv_all[:, kv_width:].reshape(slot_count, KVH, HD)
        query_group = query_rot.reshape(seq_dev, KVH, repeat_heads, HD)
        scores = (
            jnp.einsum("skrd,tkd->krst", query_group, keys_all, preferred_element_type=jnp.float32)
            * score_scale
        )
        allowed = (key_pos[None, :] <= local_pos[:, None]) & (key_pos[None, :] < length_now)
        scores = jnp.where(allowed, scores, masked_value)
        row_max = jnp.max(scores, -1, keepdims=True)
        exp_scores = jnp.exp(scores - row_max)
        attention_probs = exp_scores / jnp.sum(exp_scores, -1, keepdims=True)
        probs_low = attention_probs.astype(jnp.bfloat16)
        attended = (
            jnp.einsum("krst,tkd->skrd", probs_low, values_all, preferred_element_type=jnp.float32)
            .astype(jnp.bfloat16)
            .reshape(seq_dev, query_width)
        )
        branch = jnp.dot(
            attended,
            lax.all_gather(out_weight, "shard", axis=0, tiled=True),
            preferred_element_type=jnp.float32,
        )
        middle = source + branch
        scaled_second, inverse_second = norm_forward(middle, midnorm_f)
        normed_second = scaled_second.astype(jnp.bfloat16)
        normed_all = lax.all_gather(normed_second, "shard", axis=0, tiled=True)
        gate_pre = jnp.einsum(
            "sd,fd->sf", normed_all, gate_weight, preferred_element_type=jnp.float32
        )
        up_pre = jnp.einsum("sd,fd->sf", normed_all, up_weight, preferred_element_type=jnp.float32)
        sigmoid_gate = jax.nn.sigmoid(gate_pre)
        silu_gate = gate_pre * sigmoid_gate
        hidden = (silu_gate * up_pre).astype(jnp.bfloat16)
        ffn_part = lax.psum_scatter(
            jnp.dot(hidden, down_weight, preferred_element_type=jnp.float32).astype(jnp.bfloat16),
            "shard",
            scatter_dimension=0,
            tiled=True,
        ).astype(jnp.float32)
        mixed_rows.append(
            jnp.where(valid_rows[:, None], middle + ffn_part, 0.0).astype(jnp.bfloat16)
        )
        cot_low = jnp.where(
            valid_rows[:, None], cotangent[micro_index], jnp.zeros_like(cotangent[micro_index])
        )
        cot_all = lax.all_gather(cot_low, "shard", axis=0, tiled=True)
        hidden_grad = jnp.einsum(
            "sd,fd->sf", cot_all, down_weight, preferred_element_type=jnp.float32
        )
        down_total = down_total + jnp.einsum(
            "sf,sd->fd", hidden, cot_all, preferred_element_type=jnp.float32
        )
        gate_grad = (
            hidden_grad * up_pre * sigmoid_gate * (1.0 + gate_pre * (1.0 - sigmoid_gate))
        ).astype(jnp.bfloat16)
        up_grad = (hidden_grad * silu_gate).astype(jnp.bfloat16)
        gate_total = gate_total + jnp.einsum(
            "sf,sd->fd", gate_grad, normed_all, preferred_element_type=jnp.float32
        )
        up_total = up_total + jnp.einsum(
            "sf,sd->fd", up_grad, normed_all, preferred_element_type=jnp.float32
        )
        second_grad = lax.psum_scatter(
            jnp.dot(gate_grad, gate_weight, preferred_element_type=jnp.float32)
            + jnp.dot(up_grad, up_weight, preferred_element_type=jnp.float32),
            "shard",
            scatter_dimension=0,
            tiled=True,
        )
        middle_part, midnorm_part = norm_backward(middle, inverse_second, midnorm_f, second_grad)
        middle_grad = cot_low.astype(jnp.float32) + middle_part
        midnorm_total = midnorm_total + midnorm_part
        branch_grad = middle_grad.astype(jnp.bfloat16)
        attended_grad = jnp.einsum(
            "sd,qd->sq",
            branch_grad,
            lax.all_gather(out_weight, "shard", axis=0, tiled=True),
            preferred_element_type=jnp.float32,
        ).astype(jnp.bfloat16)
        attended_group = attended_grad.reshape(seq_dev, KVH, repeat_heads, HD)
        probs_grad = jnp.einsum(
            "skrd,tkd->krst", attended_group, values_all, preferred_element_type=jnp.float32
        )
        inner_sum = jnp.sum(attention_probs * probs_grad, -1, keepdims=True)
        scores_grad = (attention_probs * (probs_grad - inner_sum)).astype(jnp.bfloat16)
        query_rot_grad = (
            jnp.einsum(
                "krst,tkd->skrd", scores_grad, keys_all, preferred_element_type=jnp.float32
            ).reshape(seq_dev, NH, HD)
            * score_scale
        )
        query_grad = (
            unrotate(query_rot_grad, cosine_table, sine_table)
            .astype(jnp.bfloat16)
            .reshape(seq_dev, query_width)
        )
        row_count = lax.axis_size("shard") * seq_dev
        key_part = (
            jnp.einsum(
                "krst,skrd->tkd", scores_grad, query_group, preferred_element_type=jnp.float32
            )
            * score_scale
        )
        value_part = jnp.einsum(
            "krst,skrd->tkd", probs_low, attended_group, preferred_element_type=jnp.float32
        )
        kv_grad = lax.psum_scatter(
            jnp.concatenate(
                [key_part.reshape(row_count, kv_width), value_part.reshape(row_count, kv_width)], 1
            ).astype(jnp.bfloat16),
            "shard",
            scatter_dimension=0,
            tiled=True,
        ).astype(jnp.float32)
        key_grad = (
            unrotate(kv_grad[:, :kv_width].reshape(seq_dev, KVH, HD), cosine_table, sine_table)
            .astype(jnp.bfloat16)
            .reshape(seq_dev, kv_width)
        )
        value_grad = kv_grad[:, kv_width:].astype(jnp.bfloat16)
        first_grad = jnp.einsum(
            "sq,qd->sd", query_grad, query_full, preferred_element_type=jnp.float32
        )
        first_grad = first_grad + jnp.einsum(
            "sq,qd->sd", key_grad, key_full, preferred_element_type=jnp.float32
        )
        first_grad = first_grad + jnp.einsum(
            "sq,qd->sd", value_grad, value_full, preferred_element_type=jnp.float32
        )
        source_part, prenorm_part = norm_backward(source, inverse_first, prenorm_f, first_grad)
        input_rows.append((middle_grad + source_part).astype(jnp.bfloat16))
        prenorm_total = prenorm_total + prenorm_part
        saved = (normed_first, query_grad, key_grad, value_grad, attended, branch_grad)
        weight_term, shard_rows = weight_terms(*saved, shard_count)
        reduced = lax.psum_scatter(
            weight_term(jnp.int32(0), lax.axis_size("shard") * shard_rows).astype(jnp.bfloat16),
            "shard",
            scatter_dimension=0,
            tiled=True,
        ).astype(jnp.float32)
        attn_total = reduced if attn_total is None else attn_total + reduced
    gain_sums = lax.psum((prenorm_total, midnorm_total), ("grp", "shard"))
    gain_share = model_width // shard_count
    prenorm_gradient = lax.dynamic_slice_in_dim(
        gain_sums[0], shard_rank * gain_share, gain_share, 0
    )
    midnorm_gradient = lax.dynamic_slice_in_dim(
        gain_sums[1], shard_rank * gain_share, gain_share, 0
    )
    summed = (
        lax.psum(attn_total.astype(jnp.bfloat16), "grp").astype(jnp.float32),
        lax.psum(gate_total.astype(jnp.bfloat16), "grp").astype(jnp.float32),
        lax.psum(up_total.astype(jnp.bfloat16), "grp").astype(jnp.float32),
        lax.psum(down_total.astype(jnp.bfloat16), "grp").astype(jnp.float32),
    )
    attn_rows = summed[0]
    query_share = query_width // shard_count
    kv_share = kv_width // shard_count
    query_gradient = attn_rows[:query_share]
    key_gradient = attn_rows[query_share : query_share + kv_share]
    value_gradient = attn_rows[query_share + kv_share : query_share + 2 * kv_share]
    out_gradient = attn_rows[query_share + 2 * kv_share :]
    return (
        jnp.stack(mixed_rows),
        jnp.stack(input_rows),
        prenorm_gradient,
        query_gradient,
        key_gradient,
        value_gradient,
        out_gradient,
        midnorm_gradient,
        summed[1],
        summed[2],
        summed[3],
    )


def local_heads(
    tokens,
    lengths,
    prenorm_gain,
    query_weight,
    key_weight,
    value_weight,
    out_weight,
    midnorm_gain,
    gate_weight,
    up_weight,
    down_weight,
    cotangent,
):
    low = jnp.bfloat16
    count = lax.axis_size("shard")
    groups = lax.axis_size("grp")
    seqs, seq_dev, model_width = tokens.shape
    rows = seqs * seq_dev
    inverse_freq = jnp.asarray(theta_base ** (-np.arange(0, HD, 2) / HD), jnp.float32)
    tokens_low = tokens.reshape(rows, model_width)
    cot_low = cotangent.reshape(rows, model_width)
    branch, gains, normed_first, cot_all, queries, keys, values, attended, kv_head, cosine, sine = (
        attention(
            lengths,
            tokens_low,
            cot_low,
            prenorm_gain,
            midnorm_gain,
            inverse_freq[None, :],
            query_weight,
            key_weight,
            value_weight,
            out_weight,
            count,
            groups,
            1,
        )
    )
    second_grad, ffn_parts, pair_sums, early = ffn(
        tokens_low, branch, gains, cot_all, gate_weight, up_weight, down_weight, groups, 2
    )
    mixed, input_gradient, gain_own, totals, wide, narrow = attention_grad(
        lengths,
        tokens_low,
        branch,
        cot_low,
        second_grad,
        gains,
        cosine,
        sine,
        ffn_parts,
        normed_first,
        attended,
        queries,
        keys,
        values,
        query_weight,
        kv_head,
        out_weight,
        pair_sums,
        early,
        groups,
        3,
    )
    f32 = jnp.float32
    return (
        mixed.reshape(tokens.shape),
        input_gradient.reshape(tokens.shape),
        gain_own[0],
        wide[1].astype(f32),
        narrow[0].astype(f32),
        narrow[1].astype(f32),
        wide[0].astype(f32),
        gain_own[1],
        totals[1].astype(f32),
        totals[2].astype(f32),
        totals[0].astype(f32),
    )


def solution(mesh):
    planes = mesh.shape["shard"] == NH and mesh.shape["grp"] == 4
    local = local_heads if planes else local_rows
    in_specs = (
        P("grp", "shard", None),
        P("grp"),
        P("shard"),
        P("shard", None),
        P("shard", None),
        P("shard", None),
        P("shard", None),
        P("shard"),
        P("shard", None),
        P("shard", None),
        P("shard", None),
        P("grp", "shard", None),
    )
    out_specs = (
        P("grp", "shard", None),
        P("grp", "shard", None),
        P("shard"),
        P("shard", None),
        P("shard", None),
        P("shard", None),
        P("shard", None),
        P("shard"),
        P("shard", None),
        P("shard", None),
        P("shard", None),
    )
    return jax.shard_map(local, mesh=mesh, in_specs=in_specs, out_specs=out_specs, check_vma=False)
```

```python
import functools
import math

import jax
import jax.numpy as jnp
from jax import lax
from jax.experimental import pallas as pl
from jax.experimental.pallas import tpu as pltpu
from jax.sharding import PartitionSpec as P
import numpy as np

NH = 8
KVH = 4
HD = 256
MASKED = -1e30
EPSILON = 1e-06
DEPTH = 2
MESH = pl.DeviceIdType.MESH
F32 = jnp.float32
DMA = pltpu.SemaphoreType.DMA
REST = 16
PIECE = 128
EARLY = 3
CHUNKS = 2


def pieces(rows, rest=REST):
    size = -(-(rows - rest) // (16 * CHUNKS)) * 16
    cuts = [min(i * size, rows - rest) for i in range(CHUNKS + 1)] + [rows]
    return [pl.ds(a, b - a) for a, b in zip(cuts, cuts[1:])]


VMEM_LIMIT = 66_000_000


def either(condition, action):
    pl.when(condition)(action)


def total_into(dst, *srcs):
    step = 16

    @pl.loop(0, dst.shape[0] // step)
    def _(i):
        at = pl.ds(pl.multiple_of(i * step, step), step)
        value = srcs[0][at].astype(F32)
        for src in srcs[1:]:
            value = value + src[at].astype(F32)
        dst[at] = value.astype(dst.dtype)


class Place:
    def __init__(self, line):
        self.line = line
        self.me = lax.axis_index("shard")
        self.z = self.me // 2
        self.y = lax.rem(self.me, 2)
        self.cross = self.me + 1 - 2 * self.y
        self.low_end = self.z == 0
        self.high_end = self.z == line - 1
        near = []
        for z in range(line):
            order = [z]
            for k in range(1, line):
                order += [d for d in (z - k, z + k) if 0 <= d < line]
            near.append(order)
        self.tables = near

    def near(self, i):
        out = jnp.int32(0)
        for z in range(self.line):
            row = jnp.int32(self.tables[z][0])
            for k in range(1, self.line):
                row = jnp.where(i == k, self.tables[z][k], row)
            out = jnp.where(self.z == z, row, out)
        return out

    def far(self, i):
        return self.near(self.line - 1 - i)

    def greet(self, groups):
        self.arrive(groups)
        self.meet(groups)

    def meet(self, groups):
        pl.semaphore_wait(pltpu.get_barrier_semaphore(), 2 * self.line + groups - 2)

    def arrive(self, groups):
        barrier = pltpu.get_barrier_semaphore()
        count = 2 * self.line
        rank = lax.axis_index("grp")
        for step in range(1, count):
            pl.semaphore_signal(
                barrier,
                inc=1,
                device_id={"shard": lax.rem(self.me + step, count)},
                device_id_type=MESH,
            )
        for step in range(1, groups):
            pl.semaphore_signal(
                barrier,
                inc=1,
                device_id={"grp": lax.rem(rank + step, groups)},
                device_id_type=MESH,
            )


    def arrive_near(self, ranks):
        barrier = pltpu.get_barrier_semaphore()

        def signal(**peer):
            pl.semaphore_signal(barrier, inc=1, device_id=peer, device_id_type=MESH)

        signal(shard=self.cross)
        either(self.z > 0, lambda: signal(shard=self.me - 2))
        either(self.z < self.line - 1, lambda: signal(shard=self.me + 2))
        for rank in ranks:
            signal(grp=rank)

    def meet_near(self, ranks):
        ends = jnp.where(self.z > 0, 1, 0) + jnp.where(self.z < self.line - 1, 1, 0)
        pl.semaphore_wait(pltpu.get_barrier_semaphore(), 1 + len(ranks) + ends)


class Gather:
    UP, DOWN, CROSS = 0, 1, 2

    def __init__(self, place, own, out, local_sem, send_sem, recv_sem, rest=REST):
        self.p, self.own, self.out = place, own, out
        self.local_sem, self.send_sem, self.recv_sem = local_sem, send_sem, recv_sem
        self.pieces = pieces(own.shape[0], rest)
        self.last = len(self.pieces) - 1

    def copy(self, way, origin, part, own=False):
        p = self.p
        peer = (p.me + 2, p.me - 2, p.cross)[way]
        at = self.pieces[part]
        return pltpu.make_async_remote_copy(
            src_ref=self.own.at[at] if own else self.out.at[origin, at],
            dst_ref=self.out.at[origin, at],
            send_sem=self.send_sem.at[way, origin, part],
            recv_sem=self.recv_sem.at[origin, part],
            device_id={"shard": peer},
            device_id_type=MESH,
        )

    def arrived(self, origin, part):
        self.copy(self.CROSS, origin, part).wait_recv()

    def start(self):
        self.send_own()
        self.pass_rest()

    def send_own(self):
        p = self.p
        pltpu.make_async_copy(self.own, self.out.at[p.me], self.local_sem).start()
        for part in (self.last,) + tuple(range(self.last)):
            self.copy(self.CROSS, p.me, part, True).start()
        for part in range(self.last + 1):
            either(p.z < p.line - 1, lambda: self.copy(self.UP, p.me, part, True).start())
            either(p.z > 0, lambda: self.copy(self.DOWN, p.me, part, True).start())

    def pass_rest(self):
        p = self.p
        self.arrived(p.cross, self.last)
        either(p.z < p.line - 1, lambda: self.copy(self.UP, p.cross, self.last).start())
        either(p.z > 0, lambda: self.copy(self.DOWN, p.cross, self.last).start())
        pltpu.make_async_copy(self.own, self.out.at[p.me], self.local_sem).wait()

    def hop(self, k):
        p = self.p
        below, above = p.me - 2 * k, p.me + 2 * k
        has_below, has_above = p.z - k >= 0, p.z + k < p.line

        def first(origin, part, way, more):
            self.arrived(origin, part)
            self.copy(self.CROSS, origin, part).start()
            either(more, lambda: self.copy(way, origin, part).start())

        def last(origin, other, way, more):
            for block in (origin, other):
                self.arrived(block, self.last)
                either(more, lambda: self.copy(way, block, self.last).start())

        for part in range(self.last):
            either(has_below, lambda: first(below, part, self.UP, p.z < p.line - 1))
            either(has_above, lambda: first(above, part, self.DOWN, p.z > 0))
        either(has_below, lambda: last(below, p.cross - 2 * k, self.UP, p.z < p.line - 1))
        either(has_above, lambda: last(above, p.cross + 2 * k, self.DOWN, p.z > 0))

    def whole(self, position):
        for part in range(self.last):
            self.arrived(2 * position + 1 - self.p.y, part)

    def drain(self):
        p = self.p

        @pl.loop(0, p.line)
        def _(d):
            mine, other = 2 * d + p.y, 2 * d + 1 - p.y
            for part in range(self.last):
                self.copy(self.CROSS, mine, part).wait_send()

            @pl.when(d == p.z)
            def _():
                self.copy(self.CROSS, mine, self.last).wait_send()

            def line_sent(way):
                for part in range(self.last + 1):
                    self.copy(way, mine, part).wait_send()
                self.copy(way, other, self.last).wait_send()

            either((d <= p.z) & (p.z < p.line - 1), lambda: line_sent(self.UP))
            either((d >= p.z) & (p.z > 0), lambda: line_sent(self.DOWN))


class Reduce:
    BUP, BDN, BX = 0, 2, 4
    UP, DOWN, CROSS = 5, 5 + CHUNKS, 5 + 2 * CHUNKS
    WAYS = 5 + 3 * CHUNKS
    N_SCRATCH = 9

    @staticmethod
    def scratch(line, rows, width, dtype):
        v = pltpu.VMEM
        return (
            [v((line, rows - REST, width), dtype)] * 3
            + [v((line, 2, REST, width), dtype)] * 2
            + [v((REST, width), dtype)] * 2
            + [DMA((Reduce.WAYS, line)), DMA((Reduce.WAYS, line))]
        )

    def __init__(self, place, parts, out, scratch):
        self.p, self.parts, self.out = place, parts, out
        self.cross_in, self.up_in, self.down_in, self.bup_in, self.bdn_in = scratch[:5]
        self.bx_out, self.bx_in, self.send_sem, self.recv_sem = scratch[5:]
        self.pieces = pieces(parts.shape[1])
        self.b = self.pieces[-1]

    def desc(self, way, slot, src, dst, peer):
        return pltpu.make_async_remote_copy(
            src_ref=src,
            dst_ref=dst,
            send_sem=self.send_sem.at[way, slot],
            recv_sem=self.recv_sem.at[way, slot],
            device_id={"shard": peer},
            device_id_type=MESH,
        )

    def cross_copy(self, d, c):
        p, at = self.p, self.pieces[c]
        return self.desc(
            self.CROSS + c,
            d,
            self.parts.at[2 * d + 1 - p.y, at],
            self.cross_in.at[d, at],
            p.cross,
        )

    def line_copy(self, up, d, c):
        p, at = self.p, self.pieces[c]
        came = self.up_in if up else self.down_in
        return self.desc(
            (self.UP if up else self.DOWN) + c,
            d,
            self.cross_in.at[d, at],
            came.at[d, at],
            p.me + 2 if up else p.me - 2,
        )

    def b_copy(self, up, d, o, src=None):
        p = self.p
        held = self.bup_in if up else self.bdn_in
        return self.desc(
            (self.BUP if up else self.BDN) + o,
            d,
            held.at[d, o] if src is None else src,
            held.at[d, o],
            p.me + 2 if up else p.me - 2,
        )

    def bx_copy(self):
        return self.desc(self.BX, 0, self.bx_out, self.bx_in, self.p.cross)

    def column(self, o):
        return self.p.y if o == 0 else 1 - self.p.y

    def send_across(self, i):
        for c in range(CHUNKS):
            self.cross_copy(self.p.far(i), c).start()

    def b_hop(self, i):
        p = self.p
        d = p.far(i)

        def go(up):
            first = p.low_end if up else p.high_end
            held = self.bup_in if up else self.bdn_in
            for o in (1, 0):
                mine = self.parts.at[2 * d + self.column(o), self.b]
                either(first, lambda: self.b_copy(up, d, o, mine).start())

                @pl.when(jnp.logical_not(first))
                def _():
                    self.b_copy(up, d, o).wait_recv()
                    total_into(held.at[d, o], mine, held.at[d, o])
                    self.b_copy(up, d, o).start()

        either(d > p.z, lambda: go(True))
        either(d < p.z, lambda: go(False))

    def hop(self, i):
        for c in range(CHUNKS):
            self.step(i, c)

    def step(self, i, c):
        p = self.p
        d = p.far(i)
        self.cross_copy(d, c).wait_recv()
        at = self.pieces[c]
        mine = self.parts.at[2 * d + p.y, at]
        held = self.cross_in.at[d, at]

        def go(up):
            first = p.low_end if up else p.high_end
            came = self.up_in if up else self.down_in
            either(first, lambda: total_into(held, mine, held))

            @pl.when(jnp.logical_not(first))
            def _():
                self.line_copy(up, d, c).wait_recv()
                total_into(held, mine, held, came.at[d, at])

            self.line_copy(up, d, c).start()

        either(d > p.z, lambda: go(True))
        either(d < p.z, lambda: go(False))

    def close(self, dst, mine, ups, downs):
        p = self.p
        either(p.low_end, lambda: total_into(dst, *mine, downs))
        either(p.high_end, lambda: total_into(dst, *mine, ups))
        either(
            jnp.logical_not(p.low_end | p.high_end), lambda: total_into(dst, *mine, ups, downs)
        )

    def finish(self):
        p = self.p
        for o in (1, 0):
            either(jnp.logical_not(p.low_end), lambda: self.b_copy(True, p.z, o).wait_recv())
            either(jnp.logical_not(p.high_end), lambda: self.b_copy(False, p.z, o).wait_recv())
            if o:
                mine = self.parts.at[2 * p.z + self.column(o), self.b]
                self.close(self.bx_out, (mine,), self.bup_in.at[p.z, o], self.bdn_in.at[p.z, o])
                self.bx_copy().start()
        self.bx_copy().wait_recv()
        self.close(
            self.out.at[self.b],
            (self.parts.at[p.me, self.b], self.bx_in),
            self.bup_in.at[p.z, 0],
            self.bdn_in.at[p.z, 0],
        )
        for c in range(CHUNKS):
            self.cross_copy(p.z, c).wait_recv()
            either(jnp.logical_not(p.low_end), lambda: self.line_copy(True, p.z, c).wait_recv())
            either(jnp.logical_not(p.high_end), lambda: self.line_copy(False, p.z, c).wait_recv())
            at = self.pieces[c]
            self.close(
                self.out.at[at],
                (self.parts.at[p.me, at], self.cross_in.at[p.z, at]),
                self.up_in.at[p.z, at],
                self.down_in.at[p.z, at],
            )

    def drain(self):
        p = self.p
        self.bx_copy().wait_send()

        @pl.loop(0, p.line)
        def _(d):
            def line_sent(up):
                for c in range(CHUNKS):
                    self.line_copy(up, d, c).wait_send()
                self.b_copy(up, d, 0).wait_send()
                self.b_copy(up, d, 1).wait_send()

            for c in range(CHUNKS):
                self.cross_copy(d, c).wait_send()
            either(d > p.z, lambda: line_sent(True))
            either(d < p.z, lambda: line_sent(False))


def dot(a, b):
    return jnp.dot(a, b, preferred_element_type=F32)


def dot_t(a, b):
    return lax.dot_general(a, b, (((1,), (1,)), ((), ())), preferred_element_type=F32)


def t_dot(a, b):
    return lax.dot_general(a, b, (((0,), (0,)), ((), ())), preferred_element_type=F32)


def to_peer(axis, peer, src, dst, send_sem, recv_sem):
    return pltpu.make_async_remote_copy(
        src_ref=src,
        dst_ref=dst,
        send_sem=send_sem,
        recv_sem=recv_sem,
        device_id={axis: peer},
        device_id_type=MESH,
    )


def turn_by(v, cosine, sine):
    half = v.shape[-1] // 2
    a, b = v[:, :half], v[:, half:]
    return jnp.concatenate([a * cosine - b * sine, b * cosine + a * sine], -1)


def turn_back(v, cosine, sine):
    return turn_by(v, cosine, -sine)


def probabilities(query, keys, rows_from, limit):
    scores = dot_t(query, keys) * (1.0 / math.sqrt(HD))
    row = lax.broadcasted_iota(jnp.int32, scores.shape, 0) + rows_from
    col = lax.broadcasted_iota(jnp.int32, scores.shape, 1)
    scores = jnp.where((col <= row) & (col < limit), scores, MASKED)
    weight = jnp.exp(scores - jnp.max(scores, -1, keepdims=True))
    return weight / jnp.sum(weight, -1, keepdims=True)


def row_valid(place, lengths, rows):
    slots = rows // lengths.shape[0]
    row = lax.broadcasted_iota(jnp.int32, (rows, 1), 0)
    limit = jnp.full((rows, 1), lengths[0], jnp.int32)
    for n in range(1, lengths.shape[0]):
        limit = jnp.where(row >= n * slots, lengths[n], limit)
    return place.me * slots + lax.rem(row, slots) < limit


def gain_row(shares, which):
    return jnp.concatenate([shares[b, which : which + 1] for b in range(shares.shape[0])], 1)


def inverse_rms(x):
    return lax.rsqrt(jnp.mean(x * x, -1, keepdims=True) + EPSILON)


def norm_grad(x, inverse, gain, grad):
    weighted = grad * gain
    inner = jnp.sum(weighted * x, -1, keepdims=True)
    return inverse * weighted - x * inverse * inverse * inverse * inner / x.shape[-1]


def start_all(copies):
    for c in copies:
        c.start()


def wait_all(copies):
    for c in copies:
        c.wait()


def scalars():
    return pl.BlockSpec(memory_space=pltpu.SMEM)


def hbm():
    return pl.BlockSpec(memory_space=pl.ANY)


def vm():
    return pl.BlockSpec(memory_space=pltpu.VMEM)


def params(ident):
    return pltpu.CompilerParams(
        collective_id=ident, has_side_effects=True, vmem_limit_bytes=VMEM_LIMIT
    )


def gather_sems(count):
    return [DMA, DMA((3, count, CHUNKS + 1)), DMA((count, CHUNKS + 1))]


def attention_kernel(
    line, groups, seqs,
    lengths, own, cot_raw, pre_gain, mid_gain, freq, wq_hbm, wk_hbm, wv_hbm, wo_hbm,
    branch, small_out, normed_hbm, cot_hbm, q_hbm, k_hbm, v_hbm, attended_hbm, wkv_hbm, cos_hbm, sin_hbm,
    small, cot_own, rows_all, normed, cot_all, q, k, v, attended, wq, wkv, wo, cosine, sine, parts,
    *scratch,
):
    p = Place(line)
    count = 2 * line
    rank = lax.axis_index("grp")
    g1, g2 = scratch[:3], scratch[3:6]
    (load_sem, small_send, small_recv, wy_send, wg_send, w_recv, save_sem) = scratch[6:13]
    r_scratch = scratch[13:]
    half = wk_hbm.shape[0]
    piece = half // 2
    at_own = pl.ds(pl.multiple_of(p.y * half, half), half)
    loads = [
        pltpu.make_async_copy(src, dst, load_sem.at[i])
        for i, (src, dst) in enumerate(
            (
                (wk_hbm, wkv.at[0, at_own]),
                (wv_hbm, wkv.at[1, at_own]),
                (wq_hbm, wq),
                (wo_hbm, wo),
            )
        )
    ]
    p.arrive(groups)
    start_all(loads)

    small[...] = jnp.zeros_like(small)
    small[0:1] = pre_gain[...].astype(F32)[None, :]
    small[1:2] = mid_gain[...].astype(F32)[None, :]
    p.meet(groups)

    def small_copy(step, peer, origin):
        return to_peer(
            "shard", peer, small, small_out.at[origin], small_send.at[step], small_recv.at[step]
        )

    for step in range(1, count):
        small_copy(step, lax.rem(p.me + step, count), p.me).start()
    gather = Gather(p, own, rows_all, *g1, rest=2 * REST)
    gather.start()
    cots = Gather(p, cot_own, cot_all, *g2)
    small_out[p.me] = small[...]

    def rows_of(quarter, column):
        return wkv.at[
            quarter // 2,
            pl.ds(pl.multiple_of(column * half + lax.rem(quarter, 2) * piece, piece), piece),
        ]

    def across():
        ref = rows_of(rank, p.y)
        return to_peer("shard", p.cross, ref, ref, wy_send, w_recv.at[rank])

    def share(step):
        ref = rows_of(rank, 1 - p.y)
        return to_peer(
            "grp", lax.rem(rank + step, groups), ref, ref, wg_send.at[step], w_recv.at[rank]
        )

    wait_all(loads)
    across().start()
    pos = lax.broadcasted_iota(jnp.int32, cosine.shape, 0).astype(F32)
    angle = pos * freq[...]
    cosine[...] = jnp.cos(angle)
    sine[...] = jnp.sin(angle)
    cot = cot_raw[...]
    cot_own[...] = jnp.where(row_valid(p, lengths, cot.shape[0]), cot, jnp.zeros_like(cot))
    gather.hop(1)
    for step in range(1, count):
        small_copy(step, p.me, lax.rem(p.me + count - step, count)).wait_recv()
    gain = gain_row(small_out, 0)
    across().wait_recv()
    for step in range(1, groups):
        share(step).start()
    rows = own.shape[0]
    pair = 2 * rows
    slots = rows // seqs
    low = own.dtype
    for step in range(1, groups):
        quarter = lax.rem(rank + step, groups)
        ref = rows_of(quarter, 1 - p.y)
        to_peer("grp", rank, ref, ref, wg_send.at[step], w_recv.at[quarter]).wait_recv()

    @pl.loop(0, line)
    def _(i):
        d = p.near(i)
        gather.whole(d)
        x = rows_all[pl.ds(2 * d, 2)].reshape(pair, -1).astype(F32)
        n = (x * inverse_rms(x) * gain).astype(low)
        normed[pl.ds(2 * d, 2)] = n.reshape(2, rows, -1)
        at = pl.ds(pl.multiple_of(d * 2 * slots, 2 * slots), 2 * slots)
        c, s = cosine[at], sine[at]

        def by_rows(t):
            return jnp.concatenate([t[:slots]] * seqs + [t[slots:]] * seqs, 0)

        c, s = by_rows(c), by_rows(s)

        def put(target, value):
            for block in range(2):
                for m in range(seqs):
                    to = pl.ds(
                        pl.multiple_of(d * 2 * slots + block * slots, slots), slots
                    )
                    target[m, to] = value[block * rows + m * slots : block * rows + (m + 1) * slots]

        put(q, turn_by(dot_t(n, wq[...]), c, s).astype(low))
        put(k, turn_by(dot_t(n, wkv[0]), c, s).astype(low))
        put(v, dot_t(n, wkv[1]).astype(low))
        gather.hop(i + 2)
        either(i == line - 3, cots.send_own)

    saves = [
        pltpu.make_async_copy(src, dst, save_sem.at[i])
        for i, (src, dst) in enumerate(
            (
                (normed, normed_hbm),
                (q, q_hbm),
                (k, k_hbm),
                (v, v_hbm),
                (wkv, wkv_hbm),
                (cosine, cos_hbm),
                (sine, sin_hbm),
            )
        )
    ]
    start_all(saves)
    cots.pass_rest()
    total_slots = q.shape[1]
    tile = min(256, total_slots)

    @pl.loop(0, seqs)
    def _(n):
        for t in range(total_slots // tile):
            span = (t + 1) * tile
            at = pl.ds(t * tile, tile)
            probs = probabilities(q[n, at], k[n, pl.ds(0, span)], t * tile, lengths[n])
            out = dot(probs.astype(low), v[n, pl.ds(0, span)]).astype(low)
            for c in range(tile // slots):
                b = (t * tile) // slots + c
                attended[pl.ds(pl.multiple_of(b * rows + n * slots, slots), slots)] = out[
                    c * slots : (c + 1) * slots
                ]
        cots.hop(n + 1)

    for h in range(seqs + 1, line):
        cots.hop(h)

    @pl.loop(0, line)
    def _(d):
        at = pl.ds(pl.multiple_of(d * pair, pair), pair)
        parts[pl.ds(2 * d, 2)] = dot(attended[at], wo[...]).astype(low).reshape(2, rows, -1)

    reduce = Reduce(p, parts, branch, r_scratch)
    saves2 = [pltpu.make_async_copy(attended, attended_hbm, save_sem.at[7])]
    start_all(saves2)
    for d in range(line):
        cots.whole(d)
    for i in range(DEPTH):
        reduce.send_across(i)
    saves3 = [pltpu.make_async_copy(cot_all, cot_hbm, save_sem.at[8])]
    start_all(saves3)
    for i in range(line - 1):
        reduce.b_hop(i)
    for i in range(line - 1):
        reduce.hop(i)
        if i + DEPTH < line:
            reduce.send_across(i + DEPTH)
    reduce.finish()
    reduce.drain()
    gather.drain()
    cots.drain()
    wait_all(saves + saves2 + saves3)
    across().wait_send()
    for step in range(1, groups):
        share(step).wait_send()
    for step in range(1, count):
        small_copy(step, lax.rem(p.me + step, count), p.me).wait_send()


def attention(lengths, own, cot, pre_gain, mid_gain, freq, wq, wk, wv, wo, count, groups, ident):
    rows, width = own.shape
    seqs = lengths.shape[0]
    total_slots = count * rows // seqs
    small = (8, pre_gain.shape[0])
    line = count // 2
    low = own.dtype
    v = pltpu.VMEM
    shape = jax.ShapeDtypeStruct
    hd = wq.shape[0]
    big = (count, rows, width)
    head = (seqs, total_slots, hd)
    table = (total_slots, hd // 2)
    flat = (count * rows, hd)
    return pl.pallas_call(
        functools.partial(attention_kernel, line, groups, seqs),
        out_shape=(
            shape((rows, width), F32),
            shape((count,) + small, F32),
            shape(big, low),
            shape(big, low),
            shape(head, low),
            shape(head, low),
            shape(head, low),
            shape(flat, low),
            shape((2, hd, width), low),
            shape(table, F32),
            shape(table, F32),
        ),
        in_specs=[scalars()] + [vm()] * 5 + [hbm()] * 4,
        out_specs=(vm(), vm()) + (hbm(),) * 9,
        scratch_shapes=[
            v(small, F32), v((rows, width), low), v(big, low), v(big, low), v(big, low), v(head, low), v(head, low), v(head, low), v(flat, low),
            v((hd, width), low), v((2, hd, width), low), v((hd, width), low), v(table, F32), v(table, F32), v(big, low),
        ]
        + gather_sems(count) * 2
        + [DMA((4,)), DMA((count,)), DMA((count,)), DMA, DMA((groups,)), DMA((groups,)), DMA((9,))]
        + Reduce.scratch(line, rows, width, low),
        compiler_params=params(ident),
        name="attention",
    )(lengths, own, cot, pre_gain, mid_gain, freq, wq, wk, wv, wo)


def ffn_kernel(
    line, groups,
    tokens, branch, gains, cot_hbm, gate_hbm, up_hbm, down_hbm,
    second, ffn_hbm, pair_hbm, chip_in,
    own, rights, gate_up, down_w, lefts, parts, stage, theirs,
    *scratch,
):
    p = Place(line)
    rank = lax.axis_index("grp")
    core = lax.rem(rank, 2)
    partner = rank + 1 - 2 * core
    opposite = lax.rem(rank + 2, groups)
    (load_sem, out_sem, stage_send, stage_recv, chip_send, chip_recv) = scratch[3:9]
    units = down_w.shape[0]
    gate_w, up_w = gate_up.at[pl.ds(0, units)], gate_up.at[pl.ds(units, units)]
    cot, normed = rights.at[0], rights.at[1]
    hidden, gate_g, up_g = lefts.at[0], lefts.at[1], lefts.at[2]
    loads = [
        pltpu.make_async_copy(src, dst, load_sem.at[i])
        for i, (src, dst) in enumerate(
            ((cot_hbm, cot), (down_hbm, down_w), (gate_hbm, gate_w), (up_hbm, up_w))
        )
    ]
    p.arrive_near((partner, opposite))
    start_all(loads)
    middle = tokens[...].astype(F32) + branch[...]
    own[...] = (middle * inverse_rms(middle) * gain_row(gains, 1)).astype(own.dtype)
    p.meet_near((partner, opposite))
    gather = Gather(p, own, normed, *scratch[:3])
    gather.send_own()
    wait_all(loads[:2])
    rows = own.shape[0]
    pair = 2 * rows
    low = own.dtype

    @pl.loop(0, line)
    def _(d):
        at = pl.ds(pl.multiple_of(d * pair, pair), pair)
        gate_g[at] = dot_t(cot[pl.ds(2 * d, 2)].reshape(pair, -1), down_w[...]).astype(low)

    gather.pass_rest()
    wait_all(loads[2:])

    @pl.loop(0, line)
    def _(i):
        gather.hop(i + 1)
        d = p.near(i)
        gather.whole(d)
        x = normed[pl.ds(2 * d, 2)].reshape(pair, -1)
        g = dot_t(x, gate_w[...])
        u = dot_t(x, up_w[...])
        s = 1.0 / (1.0 + jnp.exp(-g))
        silu = g * s
        at = pl.ds(pl.multiple_of(d * pair, pair), pair)
        dh = gate_g[at].astype(F32)
        hidden[at] = (silu * u).astype(low)
        up_g[at] = (dh * silu).astype(low)
        gate_g[at] = (dh * u * s * (1.0 + g * (1.0 - s))).astype(low)
        part = dot(gate_g[at], gate_w[...]) + dot(up_g[at], up_w[...])
        parts[pl.ds(2 * d, 2)] = part.astype(low).reshape(2, rows, -1)

    reduce = Reduce(p, parts, second, scratch[9:])
    for i in range(line):
        reduce.send_across(i)

    quarter = units // 4
    half = units // 2

    def mine(which):
        start = lax.rem(which + 2, 3) * half
        return gate_up.at[pl.ds(pl.multiple_of(start, half), half)]

    def to_partner(which, j):
        return to_peer(
            "grp",
            partner,
            stage.at[j],
            theirs.at[which, pl.ds(pl.multiple_of(j * quarter, quarter), quarter)],
            stage_send.at[j],
            stage_recv.at[which, j],
        )

    def chip_copy():
        return to_peer(
            "grp",
            opposite,
            gate_up.at[pl.ds(2 * half, chip_in.shape[0])],
            chip_in,
            chip_send,
            chip_recv,
        )

    def save_pair(which):
        return pltpu.make_async_copy(mine(which), pair_hbm.at[which], out_sem.at[which])

    @pl.loop(0, 3)
    def _(which):
        right = rights.at[jnp.minimum(which, 1)]

        def block(q):
            cols = pl.ds(pl.multiple_of(q * quarter, quarter), quarter)
            left = lefts[which, :, cols]
            return t_dot(left, right[...].reshape(left.shape[0], -1)).astype(low)

        @pl.loop(0, 2)
        def _(j):
            either(which > 0, lambda: to_partner(which - 1, j).wait_send())
            stage[j] = block(2 * (1 - core) + j)
            to_partner(which, j).start()

        @pl.when(which == 0)
        def _():
            for i in range(line - 1):
                reduce.b_hop(i)

        at_end = p.low_end | p.high_end
        either(at_end, lambda: reduce.step(which, 0))

        @pl.loop(0, 2)
        def _(j):
            at = pl.ds(pl.multiple_of(j * quarter, quarter), quarter)
            mine(which)[at] = block(2 * core + j)

        @pl.when(at_end)
        def _():
            for c in range(1, CHUNKS):
                reduce.step(which, c)

        for j in range(2):
            to_partner(which, j).wait_recv()
        total_into(mine(which), mine(which), theirs.at[which])
        either(which == 0, lambda: chip_copy().start())
        save_pair(which).start()

        @pl.when(jnp.logical_not(at_end))
        def _():
            for c in range(CHUNKS):
                reduce.step(which, c)

    gather.drain()

    @pl.loop(0, line)
    def _(d):
        at = pl.ds(pl.multiple_of(d * pair, pair), pair)
        normed[pl.ds(2 * d, 2)] = dot(hidden[at], down_w[...]).astype(low).reshape(2, rows, -1)

    ffn_save = pltpu.make_async_copy(normed, ffn_hbm, out_sem.at[3])
    ffn_save.start()
    reduce.finish()
    for j in range(2):
        to_partner(2, j).wait_send()

    reduce.drain()
    chip_copy().wait()
    ffn_save.wait()
    for which in range(3):
        save_pair(which).wait()


def ffn(tokens, branch, gains, cot, gate_w, up_w, down_w, groups, ident):
    rows, width = tokens.shape
    count = cot.shape[0]
    line = count // 2
    units = gate_w.shape[0]
    low = tokens.dtype
    v = pltpu.VMEM
    tall = count * rows
    shape = jax.ShapeDtypeStruct
    big = (count, rows, width)
    half = (units // 2, width)
    return pl.pallas_call(
        functools.partial(ffn_kernel, line, groups),
        out_shape=(
            shape((rows, width), F32),
            shape(big, low),
            shape((3,) + half, low),
            shape((EARLY * PIECE, width), low),
        ),
        in_specs=[vm()] * 3 + [hbm()] * 4,
        out_specs=(vm(), hbm(), hbm(), hbm()),
        scratch_shapes=[v((rows, width), low)]
        + [v((2,) + big, low), v((2 * units, width), low), v((units, width), low)]
        + [v((3, tall, units), low), v(big, low), v((2, units // 4, width), low), v((3,) + half, low)]
        + gather_sems(count)
        + [DMA((4,)), DMA((4,)), DMA((2,)), DMA((3, 2)), DMA, DMA]
        + Reduce.scratch(line, rows, width, low),
        compiler_params=params(ident),
        name="ffn",
    )(tokens, branch, gains, cot, gate_w, up_w, down_w)


def attention_grad_kernel(
    line, groups, seqs,
    lengths, tokens, branch, cot, second, gains, cosine, sine,
    ffn_hbm, normed_hbm, attended_hbm, q_hbm, k_hbm, v_hbm, wq_hbm, wkv_hbm, wo_hbm, sums_hbm, early_hbm,
    mixed, input_grad, gain_out, total_hbm, wide_hbm, narrow_hbm,
    own, middle_grad, first, ffn_own, dbranch, normed, attended, q, k, v, wq, wkv, wo, da, dk_acc, dv_acc, dq_rows, dk_rows, dv_rows,
    halves, half_in, ffn_parts, sums, sums_in, stage, mine, theirs, mine_in, gain_held, gain_in, gain_sum, gain_all,
    *scratch,
):
    p = Place(line)
    count = 2 * line
    rank = lax.axis_index("grp")
    core = lax.rem(rank, 2)
    partner = rank + 1 - 2 * core
    opposite = lax.rem(rank + 2, groups)
    (
        load_sem, chip_send, chip_recv, half_send, half_recv, stage_send, stage_recv,
        back_send, back_recv, keep_sem, ga_send, ga_recv, gb_send, gb_recv,
    ) = scratch[3:17]
    n = Reduce.N_SCRATCH
    loads = [
        pltpu.make_async_copy(src, dst, load_sem.at[i])
        for i, (src, dst) in enumerate(
            (
                (wo_hbm, wo),
                (ffn_hbm, ffn_parts),
                (attended_hbm, attended),
                (q_hbm, q),
                (k_hbm, k),
                (v_hbm, v),
                (wq_hbm, wq),
                (wkv_hbm, wkv),
                (normed_hbm, normed),
                (early_hbm, sums_in.at[pl.ds(0, EARLY)]),
            )
        )
    ]
    p.arrive(groups)
    start_all(loads)

    def load_sum(i):
        return pltpu.make_async_copy(sums_hbm.at[i], sums.at[lax.rem(i, 2)], load_sem.at[10 + lax.rem(i, 2)])

    load_sum(0).start()
    load_sum(1).start()
    middle = tokens[...].astype(F32) + branch[...]
    inverse = inverse_rms(middle)
    grad = cot[...].astype(F32)
    grad = jnp.where(row_valid(p, lengths, grad.shape[0]), grad, jnp.zeros_like(grad))
    grad = grad + norm_grad(middle, inverse, gain_row(gains, 1), second[...])
    middle_grad[...] = grad
    own[...] = grad.astype(own.dtype)
    mid_total = jnp.sum(second[...] * middle * inverse, 0, keepdims=True)
    share = gain_held.shape[2]
    for b in range(count):
        gain_held[b] = jnp.zeros(gain_held.shape[1:], F32)
        gain_held[b, 1:2] = mid_total[:, b * share : (b + 1) * share]
    p.meet(groups)
    gather = Gather(p, own, dbranch, *scratch[:3])
    n_sums = sums_hbm.shape[0]
    part_rows = sums.shape[1]

    def chip_copy(i):
        return to_peer(
            "grp", opposite, sums_hbm.at[i], sums_in.at[i], chip_send.at[i], chip_recv.at[i]
        )

    gather.start()

    @pl.loop(EARLY, n_sums)
    def _(i):
        chip_copy(i).start()

    wait_all(loads)
    ffn_sum = Reduce(p, ffn_parts, ffn_own, scratch[17 : 17 + n])
    rows = own.shape[0]
    pair = 2 * rows
    slots = rows // seqs
    low = own.dtype
    scale = 1.0 / math.sqrt(HD)

    @pl.loop(0, line)
    def _(i):
        gather.hop(i + 1)

        @pl.when(i == line - 2)
        def _():
            for first_sends in range(DEPTH):
                ffn_sum.send_across(first_sends)

        d = p.near(i)
        gather.whole(d)
        grad = dot_t(dbranch[pl.ds(2 * d, 2)].reshape(pair, -1), wo[...]).astype(low)
        for block in range(2):
            for m in range(seqs):
                at = pl.ds(pl.multiple_of(d * 2 * slots + block * slots, slots), slots)
                da[m, at] = grad[block * rows + m * slots : block * rows + (m + 1) * slots]

    for i in range(line - 1):
        ffn_sum.b_hop(i)

    chunk = stage.shape[1]

    def to_partner(b):
        return to_peer(
            "grp",
            partner,
            stage.at[b // 2],
            theirs.at[pl.ds(b // 2 * chunk, chunk)],
            stage_send.at[b // 2],
            stage_recv.at[b // 2],
        )

    def gradient(b, left, right):
        value = t_dot(left, right[...].reshape(left.shape[0], -1)).astype(low)
        keep = core == b % 2

        @pl.when(keep)
        def _():
            mine[pl.ds(b // 2 * chunk, chunk)] = value

        @pl.when(jnp.logical_not(keep))
        def _():
            stage[b // 2] = value
            to_partner(b).start()

    total_slots = q.shape[1]
    tile = min(256, total_slots)

    def backward(m):
        dk_acc[...] = jnp.zeros_like(dk_acc)
        dv_acc[...] = jnp.zeros_like(dv_acc)

        def to_rows(target, value, start, size):
            for c in range(size // slots):
                b = start // slots + c
                target[pl.ds(pl.multiple_of(b * rows + m * slots, slots), slots)] = value[
                    c * slots : (c + 1) * slots
                ]

        for t in range(total_slots // tile):
            span = (t + 1) * tile
            at = pl.ds(t * tile, tile)
            query, grad = q[m, at], da[m, at]
            keys, values = k[m, pl.ds(0, span)], v[m, pl.ds(0, span)]
            probs = probabilities(query, keys, t * tile, lengths[m])
            dprobs = dot_t(grad, values)
            inner = jnp.sum(probs * dprobs, -1, keepdims=True)
            dscores = (probs * (dprobs - inner)).astype(low)
            dq = turn_back(dot(dscores, keys) * scale, cosine[at], sine[at])
            to_rows(dq_rows, dq.astype(low), t * tile, tile)
            dk_acc[pl.ds(0, span)] += t_dot(dscores, query)
            dv_acc[pl.ds(0, span)] += t_dot(probs.astype(low), grad)
        dk = turn_back(dk_acc[...] * scale, cosine[...], sine[...])
        to_rows(dk_rows, dk.astype(low), 0, total_slots)
        to_rows(dv_rows, dv_acc[...].astype(low), 0, total_slots)

    half = HD // 2

    def swap():
        return to_peer("shard", p.cross, halves.at[1 - p.y], half_in, half_send, half_recv)

    gradient(0, attended[:, :chunk], dbranch)
    gradient(1, attended[:, chunk:], dbranch)

    @pl.loop(0, seqs)
    def _(m):
        backward(m)
        ffn_sum.hop(m)
        ffn_sum.send_across(m + DEPTH)

    for h in range(2):
        halves[h, 0] = dk_rows[:, h * half : (h + 1) * half]
        halves[h, 1] = dv_rows[:, h * half : (h + 1) * half]
    swap().start()
    gather.drain()
    parts = dbranch
    gradient(2, dq_rows[:, :chunk], normed)
    gradient(3, dq_rows[:, chunk:], normed)

    spans = (pl.ds(0, 2 * chunk), pl.ds(2 * chunk, chunk))

    def attn_chip(part):
        return to_peer(
            "grp",
            opposite,
            mine.at[spans[part]],
            mine_in.at[spans[part]],
            chip_send.at[n_sums + part],
            chip_recv.at[n_sums + part],
        )

    def attn_pair(part, blocks):
        for b in blocks:
            to_partner(2 * b).wait_recv()
        at = mine.at[spans[part]]
        total_into(at, at, theirs.at[spans[part]])
        attn_chip(part).start()

    def back_attn(slot):
        if slot < 2:
            out = wide_hbm.at[slot, pl.ds(pl.multiple_of(core * chunk, chunk), chunk)]
        else:
            out = narrow_hbm.at[core]
        at = mine.at[pl.ds(slot * chunk, chunk)]
        n_slot = n_sums + slot
        sems = keep_sem.at[n_slot], back_send.at[n_slot], back_recv.at[n_slot]
        return pltpu.make_async_copy(at, out, sems[0]), to_peer("grp", partner, at, out, *sems[1:])

    def attn_total(part):
        attn_chip(part).wait()
        at = mine.at[spans[part]]
        total_into(at, at, mine_in.at[spans[part]])
        for slot in (0, 1) if part == 0 else (2,):
            start_all(back_attn(slot))


    @pl.loop(0, line)
    def _(d):
        at = pl.ds(pl.multiple_of(d * pair, pair), pair)
        part = dot(dq_rows[at], wq[...]) + dot(dk_rows[at], wkv[0]) + dot(dv_rows[at], wkv[1])
        parts[pl.ds(2 * d, 2)] = part.astype(low).reshape(2, rows, -1)

    for i in range(seqs, line - 1):
        ffn_sum.hop(i)
    def back(i):
        per_half = n_sums // 3
        start = core * per_half * part_rows + lax.rem(i, per_half) * part_rows
        at = pl.ds(pl.multiple_of(start, part_rows), part_rows)
        out = total_hbm.at[lax.div(i, per_half), at]
        return (
            pltpu.make_async_copy(sums_in.at[i], out, keep_sem.at[i]),
            to_peer("grp", partner, sums_in.at[i], out, back_send.at[i], back_recv.at[i]),
        )

    def sum_up(first_piece, end):
        @pl.loop(first_piece, end)
        def _(i):
            either(i >= EARLY, lambda: chip_copy(i).wait())
            load_sum(i).wait()
            total_into(sums_in.at[i], sums.at[lax.rem(i, 2)], sums_in.at[i])
            either(i + 2 < n_sums, lambda: load_sum(i + 2).start())
            start_all(back(i))

    def gain_copy(step, peer, origin):
        return to_peer(
            "shard", peer, gain_held.at[peer], gain_in.at[origin], ga_send.at[step], ga_recv.at[step]
        )

    def gain_group(step, peer, origin):
        return to_peer(
            "grp", peer, gain_sum, gain_all.at[origin], gb_send.at[step], gb_recv.at[step]
        )

    def gain_first():
        def body(i, total):
            at = pl.ds(pl.multiple_of(i * 16, 16), 16)
            for b in range(count):
                total = total + parts[b, at].astype(F32) * normed[b, at].astype(F32)
            return total

        total = lax.fori_loop(0, rows // 16, body, jnp.zeros((16, parts.shape[2]), F32))
        total = jnp.sum(total, 0, keepdims=True) / gain_row(gains, 0)
        for b in range(count):
            gain_held[b, 0:1] = total[:, b * share : (b + 1) * share]
        for step in range(1, count):
            gain_copy(step, lax.rem(p.me + step, count), p.me).start()

    def gain_second():
        for step in range(1, count):
            gain_copy(step, p.me, lax.rem(p.me + count - step, count)).wait_recv()
        gain_in[p.me] = gain_held[p.me]
        total = gain_in[0]
        for b in range(1, count):
            total = total + gain_in[b]
        gain_sum[...] = total
        gain_all[rank] = total
        for step in range(1, groups):
            gain_group(step, lax.rem(rank + step, groups), rank).start()

    sum_up(0, n_sums // 3)
    attn_pair(0, (0, 1))
    gain_first()
    ffn_sum.finish()
    reduce = Reduce(p, parts, first, scratch[17 + n :])
    for i in range(DEPTH):
        reduce.send_across(i)
    for i in range(line - 1):
        reduce.b_hop(i)

    def summed(which):
        return (halves[p.y, which].astype(F32) + half_in[which].astype(F32)).astype(low)

    valid = row_valid(p, lengths, rows)
    result = tokens[...].astype(F32) + branch[...] + ffn_own[...]
    mixed[...] = jnp.where(valid, result, jnp.zeros_like(result)).astype(low)

    swap().wait_recv()
    gradient(4, summed(0), normed)
    gradient(5, summed(1), normed)
    reduce.hop(0)
    reduce.send_across(DEPTH)
    attn_pair(1, (2,))
    sum_up(n_sums // 3, n_sums // 2)
    reduce.hop(1)
    reduce.send_across(DEPTH + 1)
    gain_second()
    sum_up(n_sums // 2, n_sums - 3)
    reduce.hop(2)
    sum_up(n_sums - 3, n_sums)
    attn_total(0)
    reduce.finish()
    attn_total(1)
    for step in range(1, groups):
        gain_group(step, rank, lax.rem(rank + groups - step, groups)).wait_recv()
    total = gain_all[0]
    for b in range(1, groups):
        total = total + gain_all[b]
    gain_out[...] = total
    source = tokens[...].astype(F32)
    inner = norm_grad(source, inverse_rms(source), gain_row(gains, 0), first[...])
    input_grad[...] = (middle_grad[...] + inner).astype(low)
    reduce.drain()
    ffn_sum.drain()
    swap().wait_send()
    for b in range(3):
        to_partner(2 * b).wait_send()
    for step in range(1, count):
        gain_copy(step, lax.rem(p.me + step, count), p.me).wait_send()
    for step in range(1, groups):
        gain_group(step, lax.rem(rank + step, groups), rank).wait_send()

    @pl.loop(0, n_sums)
    def _(i):
        wait_all(back(i))

    for slot in range(3):
        wait_all(back_attn(slot))


def attention_grad(
    lengths, tokens, branch, cot, second, gains, cosine, sine, ffn_parts, normed, attended, q, k, v, wq, wkv, wo, sums, early,
    groups, ident,
):
    rows, width = tokens.shape
    count = normed.shape[0]
    line = count // 2
    seqs, total_slots, hd = q.shape
    low = tokens.dtype
    vmem = pltpu.VMEM
    tall = count * rows
    half = hd // 2
    sums = sums.reshape(-1, PIECE, width)
    early = early.reshape(-1, PIECE, width)
    n_sums, part_rows, _ = sums.shape
    shape = jax.ShapeDtypeStruct
    big = vmem((count, rows, width), low)
    head = vmem((seqs, total_slots, hd), low)
    weight = vmem((hd, width), low)
    flat = vmem((tall, hd), low)
    acc = vmem((total_slots, hd), F32)
    third = vmem((3 * half, width), low)
    g = gains.shape
    block = vmem((rows, width), F32)
    return pl.pallas_call(
        functools.partial(attention_grad_kernel, line, groups, seqs),
        out_shape=(
            shape((rows, width), low),
            shape((rows, width), low),
            shape(g[1:], F32),
            shape((3, n_sums // 3 * 2 * part_rows, width), low),
            shape((2, 2 * half, width), low),
            shape((2, half, width), low),
        ),
        in_specs=[scalars()] + [vm()] * 7 + [hbm()] * 11,
        out_specs=(vm(), vm(), vm(), hbm(), hbm(), hbm()),
        scratch_shapes=[
            vmem((rows, width), low), block, block, block,
            big, big, flat, head, head, head, weight, vmem((2, hd, width), low), weight, head, acc, acc,
            flat, flat, flat,
            vmem((2, 2, tall, half), low), vmem((2, tall, half), low), big,
            vmem((2,) + sums.shape[1:], low), vmem(sums.shape, low), vmem((3, half, width), low), third, third, third,
            vmem(g, F32), vmem(g, F32), vmem(g[1:], F32), vmem((groups,) + g[1:], F32),
        ]
        + gather_sems(count)
        + [
            DMA((12,)), DMA((n_sums + 2,)), DMA((n_sums + 2,)), DMA, DMA, DMA((3,)), DMA((3,)),
            DMA((n_sums + 3,)), DMA((n_sums + 3,)), DMA((n_sums + 3,)),
            DMA((count,)), DMA((count,)), DMA((groups,)), DMA((groups,)),
        ]
        + Reduce.scratch(line, rows, width, low) * 2,
        compiler_params=params(ident),
        name="attention_grad",
    )(
        lengths, tokens, branch, cot, second, gains, cosine, sine, ffn_parts, normed, attended, q, k, v, wq, wkv, wo, sums, early
    )


epsilon = 1e-06
theta_base = 1000042.0
masked_value = -1e30


def turned(source):
    half_width = source.shape[-1] // 2
    return jnp.concatenate([-source[..., half_width:], source[..., :half_width]], -1)


def rotate(source, cosine_table, sine_table):
    return source * cosine_table + turned(source) * sine_table


def unrotate(source, cosine_table, sine_table):
    return source * cosine_table - turned(source) * sine_table


def norm_forward(source, norm_gain):
    inverse = lax.rsqrt(jnp.mean(source * source, -1, keepdims=True) + epsilon)
    return (source * inverse * norm_gain, inverse)


def norm_backward(source, inverse, norm_gain, grad_out):
    weighted = grad_out * norm_gain
    inner_sum = jnp.sum(weighted * source, -1, keepdims=True)
    grad_in = (
        inverse * weighted - source * inverse * inverse * inverse * inner_sum / source.shape[-1]
    )
    return (grad_in, jnp.sum(grad_out * source * inverse, 0))


def weight_terms(normed, query_grad, key_grad, value_grad, attended, branch_grad, shard_count):
    token_count, model_width = normed.shape
    query_share = query_grad.shape[1] // shard_count
    kv_share = key_grad.shape[1] // shard_count
    shard_rows = 2 * query_share + 2 * kv_share

    def weight_term(first_row, row_count):
        blocks = row_count // shard_rows

        def columns(matrix, share_cols):
            return matrix.reshape(token_count, blocks, share_cols)

        part_query = jnp.einsum(
            "tmr,td->mrd",
            columns(query_grad, query_share),
            normed,
            preferred_element_type=jnp.float32,
        )
        part_key = jnp.einsum(
            "tmr,td->mrd", columns(key_grad, kv_share), normed, preferred_element_type=jnp.float32
        )
        part_value = jnp.einsum(
            "tmr,td->mrd", columns(value_grad, kv_share), normed, preferred_element_type=jnp.float32
        )
        part_out = jnp.einsum(
            "tmr,td->mrd",
            columns(attended, query_share),
            branch_grad,
            preferred_element_type=jnp.float32,
        )
        return jnp.concatenate([part_query, part_key, part_value, part_out], 1).reshape(
            row_count, model_width
        )

    return (weight_term, shard_rows)


def local_rows(
    tokens,
    lengths,
    prenorm_gain,
    query_weight,
    key_weight,
    value_weight,
    out_weight,
    midnorm_gain,
    gate_weight,
    up_weight,
    down_weight,
    cotangent,
):
    shard_count = lax.axis_size("shard")
    shard_rank = lax.axis_index("shard")
    micro_count, seq_dev, model_width = tokens.shape
    slot_count = seq_dev * shard_count
    repeat_heads = NH // KVH
    query_width = NH * HD
    kv_width = KVH * HD
    score_scale = 1.0 / math.sqrt(HD)
    local_pos = shard_rank * seq_dev + jnp.arange(seq_dev, dtype=jnp.int32)
    key_pos = jnp.arange(slot_count, dtype=jnp.int32)
    inverse_freq = theta_base ** (-(jnp.arange(0, HD, 2).astype(jnp.float32) / HD))
    angles = local_pos.astype(jnp.float32)[:, None] * inverse_freq[None, :]
    cosine_table = jnp.concatenate([jnp.cos(angles), jnp.cos(angles)], -1)[:, None, :]
    sine_table = jnp.concatenate([jnp.sin(angles), jnp.sin(angles)], -1)[:, None, :]
    gate_total = jnp.zeros(gate_weight.shape, jnp.float32)
    up_total = jnp.zeros(up_weight.shape, jnp.float32)
    down_total = jnp.zeros(down_weight.shape, jnp.float32)
    prenorm_total = jnp.zeros((model_width,), jnp.float32)
    midnorm_total = jnp.zeros((model_width,), jnp.float32)
    attn_total = None
    mixed_rows = []
    input_rows = []
    for micro_index in range(micro_count):
        gathered = (
            lax.all_gather(query_weight, "shard", axis=0, tiled=True),
            lax.all_gather(key_weight, "shard", axis=0, tiled=True),
            lax.all_gather(value_weight, "shard", axis=0, tiled=True),
            lax.all_gather(prenorm_gain, "shard", axis=0, tiled=True),
            lax.all_gather(midnorm_gain, "shard", axis=0, tiled=True),
        )
        query_full, key_full, value_full, prenorm_full, midnorm_full = gathered
        prenorm_f = prenorm_full.astype(jnp.float32)
        midnorm_f = midnorm_full.astype(jnp.float32)
        source = tokens[micro_index].astype(jnp.float32)
        length_now = lengths[micro_index]
        valid_rows = local_pos < length_now
        scaled_first, inverse_first = norm_forward(source, prenorm_f)
        normed_first = scaled_first.astype(jnp.bfloat16)
        query_pre = jnp.einsum(
            "sd,qd->sq", normed_first, query_full, preferred_element_type=jnp.float32
        ).reshape(seq_dev, NH, HD)
        key_pre = jnp.einsum(
            "sd,qd->sq", normed_first, key_full, preferred_element_type=jnp.float32
        ).reshape(seq_dev, KVH, HD)
        value_pre = jnp.einsum(
            "sd,qd->sq", normed_first, value_full, preferred_element_type=jnp.float32
        )
        query_rot = rotate(query_pre, cosine_table, sine_table).astype(jnp.bfloat16)
        key_rot = rotate(key_pre, cosine_table, sine_table).astype(jnp.bfloat16)
        key_value = jnp.concatenate(
            [key_rot.reshape(seq_dev, kv_width), value_pre.astype(jnp.bfloat16)], 1
        )
        kv_all = lax.all_gather(key_value, "shard", axis=0, tiled=True)
        keys_all = kv_all[:, :kv_width].reshape(slot_count, KVH, HD)
        values_all = kv_all[:, kv_width:].reshape(slot_count, KVH, HD)
        query_group = query_rot.reshape(seq_dev, KVH, repeat_heads, HD)
        scores = (
            jnp.einsum("skrd,tkd->krst", query_group, keys_all, preferred_element_type=jnp.float32)
            * score_scale
        )
        allowed = (key_pos[None, :] <= local_pos[:, None]) & (key_pos[None, :] < length_now)
        scores = jnp.where(allowed, scores, masked_value)
        row_max = jnp.max(scores, -1, keepdims=True)
        exp_scores = jnp.exp(scores - row_max)
        attention_probs = exp_scores / jnp.sum(exp_scores, -1, keepdims=True)
        probs_low = attention_probs.astype(jnp.bfloat16)
        attended = (
            jnp.einsum("krst,tkd->skrd", probs_low, values_all, preferred_element_type=jnp.float32)
            .astype(jnp.bfloat16)
            .reshape(seq_dev, query_width)
        )
        branch = jnp.dot(
            attended,
            lax.all_gather(out_weight, "shard", axis=0, tiled=True),
            preferred_element_type=jnp.float32,
        )
        middle = source + branch
        scaled_second, inverse_second = norm_forward(middle, midnorm_f)
        normed_second = scaled_second.astype(jnp.bfloat16)
        normed_all = lax.all_gather(normed_second, "shard", axis=0, tiled=True)
        gate_pre = jnp.einsum(
            "sd,fd->sf", normed_all, gate_weight, preferred_element_type=jnp.float32
        )
        up_pre = jnp.einsum("sd,fd->sf", normed_all, up_weight, preferred_element_type=jnp.float32)
        sigmoid_gate = jax.nn.sigmoid(gate_pre)
        silu_gate = gate_pre * sigmoid_gate
        hidden = (silu_gate * up_pre).astype(jnp.bfloat16)
        ffn_part = lax.psum_scatter(
            jnp.dot(hidden, down_weight, preferred_element_type=jnp.float32).astype(jnp.bfloat16),
            "shard",
            scatter_dimension=0,
            tiled=True,
        ).astype(jnp.float32)
        mixed_rows.append(
            jnp.where(valid_rows[:, None], middle + ffn_part, 0.0).astype(jnp.bfloat16)
        )
        cot_low = jnp.where(
            valid_rows[:, None], cotangent[micro_index], jnp.zeros_like(cotangent[micro_index])
        )
        cot_all = lax.all_gather(cot_low, "shard", axis=0, tiled=True)
        hidden_grad = jnp.einsum(
            "sd,fd->sf", cot_all, down_weight, preferred_element_type=jnp.float32
        )
        down_total = down_total + jnp.einsum(
            "sf,sd->fd", hidden, cot_all, preferred_element_type=jnp.float32
        )
        gate_grad = (
            hidden_grad * up_pre * sigmoid_gate * (1.0 + gate_pre * (1.0 - sigmoid_gate))
        ).astype(jnp.bfloat16)
        up_grad = (hidden_grad * silu_gate).astype(jnp.bfloat16)
        gate_total = gate_total + jnp.einsum(
            "sf,sd->fd", gate_grad, normed_all, preferred_element_type=jnp.float32
        )
        up_total = up_total + jnp.einsum(
            "sf,sd->fd", up_grad, normed_all, preferred_element_type=jnp.float32
        )
        second_grad = lax.psum_scatter(
            jnp.dot(gate_grad, gate_weight, preferred_element_type=jnp.float32)
            + jnp.dot(up_grad, up_weight, preferred_element_type=jnp.float32),
            "shard",
            scatter_dimension=0,
            tiled=True,
        )
        middle_part, midnorm_part = norm_backward(middle, inverse_second, midnorm_f, second_grad)
        middle_grad = cot_low.astype(jnp.float32) + middle_part
        midnorm_total = midnorm_total + midnorm_part
        branch_grad = middle_grad.astype(jnp.bfloat16)
        attended_grad = jnp.einsum(
            "sd,qd->sq",
            branch_grad,
            lax.all_gather(out_weight, "shard", axis=0, tiled=True),
            preferred_element_type=jnp.float32,
        ).astype(jnp.bfloat16)
        attended_group = attended_grad.reshape(seq_dev, KVH, repeat_heads, HD)
        probs_grad = jnp.einsum(
            "skrd,tkd->krst", attended_group, values_all, preferred_element_type=jnp.float32
        )
        inner_sum = jnp.sum(attention_probs * probs_grad, -1, keepdims=True)
        scores_grad = (attention_probs * (probs_grad - inner_sum)).astype(jnp.bfloat16)
        query_rot_grad = (
            jnp.einsum(
                "krst,tkd->skrd", scores_grad, keys_all, preferred_element_type=jnp.float32
            ).reshape(seq_dev, NH, HD)
            * score_scale
        )
        query_grad = (
            unrotate(query_rot_grad, cosine_table, sine_table)
            .astype(jnp.bfloat16)
            .reshape(seq_dev, query_width)
        )
        row_count = lax.axis_size("shard") * seq_dev
        key_part = (
            jnp.einsum(
                "krst,skrd->tkd", scores_grad, query_group, preferred_element_type=jnp.float32
            )
            * score_scale
        )
        value_part = jnp.einsum(
            "krst,skrd->tkd", probs_low, attended_group, preferred_element_type=jnp.float32
        )
        kv_grad = lax.psum_scatter(
            jnp.concatenate(
                [key_part.reshape(row_count, kv_width), value_part.reshape(row_count, kv_width)], 1
            ).astype(jnp.bfloat16),
            "shard",
            scatter_dimension=0,
            tiled=True,
        ).astype(jnp.float32)
        key_grad = (
            unrotate(kv_grad[:, :kv_width].reshape(seq_dev, KVH, HD), cosine_table, sine_table)
            .astype(jnp.bfloat16)
            .reshape(seq_dev, kv_width)
        )
        value_grad = kv_grad[:, kv_width:].astype(jnp.bfloat16)
        first_grad = jnp.einsum(
            "sq,qd->sd", query_grad, query_full, preferred_element_type=jnp.float32
        )
        first_grad = first_grad + jnp.einsum(
            "sq,qd->sd", key_grad, key_full, preferred_element_type=jnp.float32
        )
        first_grad = first_grad + jnp.einsum(
            "sq,qd->sd", value_grad, value_full, preferred_element_type=jnp.float32
        )
        source_part, prenorm_part = norm_backward(source, inverse_first, prenorm_f, first_grad)
        input_rows.append((middle_grad + source_part).astype(jnp.bfloat16))
        prenorm_total = prenorm_total + prenorm_part
        saved = (normed_first, query_grad, key_grad, value_grad, attended, branch_grad)
        weight_term, shard_rows = weight_terms(*saved, shard_count)
        reduced = lax.psum_scatter(
            weight_term(jnp.int32(0), lax.axis_size("shard") * shard_rows).astype(jnp.bfloat16),
            "shard",
            scatter_dimension=0,
            tiled=True,
        ).astype(jnp.float32)
        attn_total = reduced if attn_total is None else attn_total + reduced
    gain_sums = lax.psum((prenorm_total, midnorm_total), ("grp", "shard"))
    gain_share = model_width // shard_count
    prenorm_gradient = lax.dynamic_slice_in_dim(
        gain_sums[0], shard_rank * gain_share, gain_share, 0
    )
    midnorm_gradient = lax.dynamic_slice_in_dim(
        gain_sums[1], shard_rank * gain_share, gain_share, 0
    )
    summed = (
        lax.psum(attn_total.astype(jnp.bfloat16), "grp").astype(jnp.float32),
        lax.psum(gate_total.astype(jnp.bfloat16), "grp").astype(jnp.float32),
        lax.psum(up_total.astype(jnp.bfloat16), "grp").astype(jnp.float32),
        lax.psum(down_total.astype(jnp.bfloat16), "grp").astype(jnp.float32),
    )
    attn_rows = summed[0]
    query_share = query_width // shard_count
    kv_share = kv_width // shard_count
    query_gradient = attn_rows[:query_share]
    key_gradient = attn_rows[query_share : query_share + kv_share]
    value_gradient = attn_rows[query_share + kv_share : query_share + 2 * kv_share]
    out_gradient = attn_rows[query_share + 2 * kv_share :]
    return (
        jnp.stack(mixed_rows),
        jnp.stack(input_rows),
        prenorm_gradient,
        query_gradient,
        key_gradient,
        value_gradient,
        out_gradient,
        midnorm_gradient,
        summed[1],
        summed[2],
        summed[3],
    )


def local_heads(
    tokens,
    lengths,
    prenorm_gain,
    query_weight,
    key_weight,
    value_weight,
    out_weight,
    midnorm_gain,
    gate_weight,
    up_weight,
    down_weight,
    cotangent,
):
    low = jnp.bfloat16
    count = lax.axis_size("shard")
    groups = lax.axis_size("grp")
    seqs, seq_dev, model_width = tokens.shape
    rows = seqs * seq_dev
    inverse_freq = jnp.asarray(theta_base ** (-np.arange(0, HD, 2) / HD), jnp.float32)
    tokens_low = tokens.reshape(rows, model_width)
    cot_low = cotangent.reshape(rows, model_width)
    branch, gains, normed_first, cot_all, queries, keys, values, attended, kv_head, cosine, sine = (
        attention(
            lengths,
            tokens_low,
            cot_low,
            prenorm_gain,
            midnorm_gain,
            inverse_freq[None, :],
            query_weight,
            key_weight,
            value_weight,
            out_weight,
            count,
            groups,
            1,
        )
    )
    second_grad, ffn_parts, pair_sums, early = ffn(
        tokens_low, branch, gains, cot_all, gate_weight, up_weight, down_weight, groups, 2
    )
    mixed, input_gradient, gain_own, totals, wide, narrow = attention_grad(
        lengths,
        tokens_low,
        branch,
        cot_low,
        second_grad,
        gains,
        cosine,
        sine,
        ffn_parts,
        normed_first,
        attended,
        queries,
        keys,
        values,
        query_weight,
        kv_head,
        out_weight,
        pair_sums,
        early,
        groups,
        3,
    )
    f32 = jnp.float32
    return (
        mixed.reshape(tokens.shape),
        input_gradient.reshape(tokens.shape),
        gain_own[0],
        wide[1].astype(f32),
        narrow[0].astype(f32),
        narrow[1].astype(f32),
        wide[0].astype(f32),
        gain_own[1],
        totals[1].astype(f32),
        totals[2].astype(f32),
        totals[0].astype(f32),
    )


def solution(mesh):
    planes = mesh.shape["shard"] == NH and mesh.shape["grp"] == 4
    local = local_heads if planes else local_rows
    in_specs = (
        P("grp", "shard", None),
        P("grp"),
        P("shard"),
        P("shard", None),
        P("shard", None),
        P("shard", None),
        P("shard", None),
        P("shard"),
        P("shard", None),
        P("shard", None),
        P("shard", None),
        P("grp", "shard", None),
    )
    out_specs = (
        P("grp", "shard", None),
        P("grp", "shard", None),
        P("shard"),
        P("shard", None),
        P("shard", None),
        P("shard", None),
        P("shard", None),
        P("shard"),
        P("shard", None),
        P("shard", None),
        P("shard", None),
    )
    return jax.shard_map(local, mesh=mesh, in_specs=in_specs, out_specs=out_specs, check_vma=False)
```

```python
import functools
import math

import jax
import jax.numpy as jnp
from jax import lax
from jax.experimental import pallas as pl
from jax.experimental.pallas import tpu as pltpu
from jax.sharding import PartitionSpec as P
import numpy as np

NH = 8
KVH = 4
HD = 256
MASKED = -1e30
EPSILON = 1e-06
DEPTH = 2
MESH = pl.DeviceIdType.MESH
F32 = jnp.float32
DMA = pltpu.SemaphoreType.DMA
REST = 16
PIECE = 128
EARLY = 3
CHUNKS = 2


def pieces(rows, rest=REST):
    size = -(-(rows - rest) // (16 * CHUNKS)) * 16
    cuts = [min(i * size, rows - rest) for i in range(CHUNKS + 1)] + [rows]
    return [pl.ds(a, b - a) for a, b in zip(cuts, cuts[1:])]


VMEM_LIMIT = 66_000_000


def either(condition, action):
    pl.when(condition)(action)


def total_into(dst, *srcs):
    step = 16

    @pl.loop(0, dst.shape[0] // step)
    def _(i):
        at = pl.ds(pl.multiple_of(i * step, step), step)
        value = srcs[0][at].astype(F32)
        for src in srcs[1:]:
            value = value + src[at].astype(F32)
        dst[at] = value.astype(dst.dtype)


class Place:
    def __init__(self, line):
        self.line = line
        self.me = lax.axis_index("shard")
        self.z = self.me // 2
        self.y = lax.rem(self.me, 2)
        self.cross = self.me + 1 - 2 * self.y
        self.low_end = self.z == 0
        self.high_end = self.z == line - 1
        near = []
        for z in range(line):
            order = [z]
            for k in range(1, line):
                order += [d for d in (z - k, z + k) if 0 <= d < line]
            near.append(order)
        self.tables = near

    def near(self, i):
        out = jnp.int32(0)
        for z in range(self.line):
            row = jnp.int32(self.tables[z][0])
            for k in range(1, self.line):
                row = jnp.where(i == k, self.tables[z][k], row)
            out = jnp.where(self.z == z, row, out)
        return out

    def far(self, i):
        return self.near(self.line - 1 - i)

    def greet(self, groups):
        self.arrive(groups)
        self.meet(groups)

    def meet(self, groups):
        pl.semaphore_wait(pltpu.get_barrier_semaphore(), 2 * self.line + groups - 2)

    def arrive(self, groups):
        barrier = pltpu.get_barrier_semaphore()
        count = 2 * self.line
        rank = lax.axis_index("grp")
        for step in range(1, count):
            pl.semaphore_signal(
                barrier,
                inc=1,
                device_id={"shard": lax.rem(self.me + step, count)},
                device_id_type=MESH,
            )
        for step in range(1, groups):
            pl.semaphore_signal(
                barrier,
                inc=1,
                device_id={"grp": lax.rem(rank + step, groups)},
                device_id_type=MESH,
            )


    def arrive_near(self, ranks):
        barrier = pltpu.get_barrier_semaphore()

        def signal(**peer):
            pl.semaphore_signal(barrier, inc=1, device_id=peer, device_id_type=MESH)

        signal(shard=self.cross)
        either(self.z > 0, lambda: signal(shard=self.me - 2))
        either(self.z < self.line - 1, lambda: signal(shard=self.me + 2))
        for rank in ranks:
            signal(grp=rank)

    def meet_near(self, ranks):
        ends = jnp.where(self.z > 0, 1, 0) + jnp.where(self.z < self.line - 1, 1, 0)
        pl.semaphore_wait(pltpu.get_barrier_semaphore(), 1 + len(ranks) + ends)


class Gather:
    UP, DOWN, CROSS = 0, 1, 2

    def __init__(self, place, own, out, local_sem, send_sem, recv_sem, rest=REST):
        self.p, self.own, self.out = place, own, out
        self.local_sem, self.send_sem, self.recv_sem = local_sem, send_sem, recv_sem
        self.pieces = pieces(own.shape[0], rest)
        self.last = len(self.pieces) - 1

    def copy(self, way, origin, part, own=False):
        p = self.p
        peer = (p.me + 2, p.me - 2, p.cross)[way]
        at = self.pieces[part]
        return pltpu.make_async_remote_copy(
            src_ref=self.own.at[at] if own else self.out.at[origin, at],
            dst_ref=self.out.at[origin, at],
            send_sem=self.send_sem.at[way, origin, part],
            recv_sem=self.recv_sem.at[origin, part],
            device_id={"shard": peer},
            device_id_type=MESH,
        )

    def arrived(self, origin, part):
        self.copy(self.CROSS, origin, part).wait_recv()

    def start(self):
        self.send_own()
        self.pass_rest()

    def send_own(self):
        p = self.p
        pltpu.make_async_copy(self.own, self.out.at[p.me], self.local_sem).start()
        for part in (self.last,) + tuple(range(self.last)):
            self.copy(self.CROSS, p.me, part, True).start()
        for part in range(self.last + 1):
            either(p.z < p.line - 1, lambda: self.copy(self.UP, p.me, part, True).start())
            either(p.z > 0, lambda: self.copy(self.DOWN, p.me, part, True).start())

    def pass_rest(self):
        p = self.p
        self.arrived(p.cross, self.last)
        either(p.z < p.line - 1, lambda: self.copy(self.UP, p.cross, self.last).start())
        either(p.z > 0, lambda: self.copy(self.DOWN, p.cross, self.last).start())
        pltpu.make_async_copy(self.own, self.out.at[p.me], self.local_sem).wait()

    def hop(self, k):
        p = self.p
        below, above = p.me - 2 * k, p.me + 2 * k
        has_below, has_above = p.z - k >= 0, p.z + k < p.line

        def first(origin, part, way, more):
            self.arrived(origin, part)
            self.copy(self.CROSS, origin, part).start()
            either(more, lambda: self.copy(way, origin, part).start())

        def last(origin, other, way, more):
            for block in (origin, other):
                self.arrived(block, self.last)
                either(more, lambda: self.copy(way, block, self.last).start())

        for part in range(self.last):
            either(has_below, lambda: first(below, part, self.UP, p.z < p.line - 1))
            either(has_above, lambda: first(above, part, self.DOWN, p.z > 0))
        either(has_below, lambda: last(below, p.cross - 2 * k, self.UP, p.z < p.line - 1))
        either(has_above, lambda: last(above, p.cross + 2 * k, self.DOWN, p.z > 0))

    def whole(self, position):
        for part in range(self.last):
            self.arrived(2 * position + 1 - self.p.y, part)

    def drain(self):
        p = self.p

        @pl.loop(0, p.line)
        def _(d):
            mine, other = 2 * d + p.y, 2 * d + 1 - p.y
            for part in range(self.last):
                self.copy(self.CROSS, mine, part).wait_send()

            @pl.when(d == p.z)
            def _():
                self.copy(self.CROSS, mine, self.last).wait_send()

            def line_sent(way):
                for part in range(self.last + 1):
                    self.copy(way, mine, part).wait_send()
                self.copy(way, other, self.last).wait_send()

            either((d <= p.z) & (p.z < p.line - 1), lambda: line_sent(self.UP))
            either((d >= p.z) & (p.z > 0), lambda: line_sent(self.DOWN))


class Reduce:
    BUP, BDN, BX = 0, 2, 4
    UP, DOWN, CROSS = 5, 5 + CHUNKS, 5 + 2 * CHUNKS
    WAYS = 5 + 3 * CHUNKS
    N_SCRATCH = 9

    @staticmethod
    def scratch(line, rows, width, dtype):
        v = pltpu.VMEM
        return (
            [v((line, rows - REST, width), dtype)] * 3
            + [v((line, 2, REST, width), dtype)] * 2
            + [v((REST, width), dtype)] * 2
            + [DMA((Reduce.WAYS, line)), DMA((Reduce.WAYS, line))]
        )

    def __init__(self, place, parts, out, scratch):
        self.p, self.parts, self.out = place, parts, out
        self.cross_in, self.up_in, self.down_in, self.bup_in, self.bdn_in = scratch[:5]
        self.bx_out, self.bx_in, self.send_sem, self.recv_sem = scratch[5:]
        self.pieces = pieces(parts.shape[1])
        self.b = self.pieces[-1]

    def desc(self, way, slot, src, dst, peer):
        return pltpu.make_async_remote_copy(
            src_ref=src,
            dst_ref=dst,
            send_sem=self.send_sem.at[way, slot],
            recv_sem=self.recv_sem.at[way, slot],
            device_id={"shard": peer},
            device_id_type=MESH,
        )

    def cross_copy(self, d, c):
        p, at = self.p, self.pieces[c]
        return self.desc(
            self.CROSS + c,
            d,
            self.parts.at[2 * d + 1 - p.y, at],
            self.cross_in.at[d, at],
            p.cross,
        )

    def line_copy(self, up, d, c):
        p, at = self.p, self.pieces[c]
        came = self.up_in if up else self.down_in
        return self.desc(
            (self.UP if up else self.DOWN) + c,
            d,
            self.cross_in.at[d, at],
            came.at[d, at],
            p.me + 2 if up else p.me - 2,
        )

    def b_copy(self, up, d, o, src=None):
        p = self.p
        held = self.bup_in if up else self.bdn_in
        return self.desc(
            (self.BUP if up else self.BDN) + o,
            d,
            held.at[d, o] if src is None else src,
            held.at[d, o],
            p.me + 2 if up else p.me - 2,
        )

    def bx_copy(self):
        return self.desc(self.BX, 0, self.bx_out, self.bx_in, self.p.cross)

    def column(self, o):
        return self.p.y if o == 0 else 1 - self.p.y

    def send_across(self, i):
        for c in range(CHUNKS):
            self.cross_copy(self.p.far(i), c).start()

    def b_hop(self, i):
        p = self.p
        d = p.far(i)

        def go(up):
            first = p.low_end if up else p.high_end
            held = self.bup_in if up else self.bdn_in
            for o in (1, 0):
                mine = self.parts.at[2 * d + self.column(o), self.b]
                either(first, lambda: self.b_copy(up, d, o, mine).start())

                @pl.when(jnp.logical_not(first))
                def _():
                    self.b_copy(up, d, o).wait_recv()
                    total_into(held.at[d, o], mine, held.at[d, o])
                    self.b_copy(up, d, o).start()

        either(d > p.z, lambda: go(True))
        either(d < p.z, lambda: go(False))

    def hop(self, i):
        for c in range(CHUNKS):
            self.step(i, c)

    def step(self, i, c):
        p = self.p
        d = p.far(i)
        self.cross_copy(d, c).wait_recv()
        at = self.pieces[c]
        mine = self.parts.at[2 * d + p.y, at]
        held = self.cross_in.at[d, at]

        def go(up):
            first = p.low_end if up else p.high_end
            came = self.up_in if up else self.down_in
            either(first, lambda: total_into(held, mine, held))

            @pl.when(jnp.logical_not(first))
            def _():
                self.line_copy(up, d, c).wait_recv()
                total_into(held, mine, held, came.at[d, at])

            self.line_copy(up, d, c).start()

        either(d > p.z, lambda: go(True))
        either(d < p.z, lambda: go(False))

    def close(self, dst, mine, ups, downs):
        p = self.p
        either(p.low_end, lambda: total_into(dst, *mine, downs))
        either(p.high_end, lambda: total_into(dst, *mine, ups))
        either(
            jnp.logical_not(p.low_end | p.high_end), lambda: total_into(dst, *mine, ups, downs)
        )

    def finish(self):
        p = self.p
        for o in (1, 0):
            either(jnp.logical_not(p.low_end), lambda: self.b_copy(True, p.z, o).wait_recv())
            either(jnp.logical_not(p.high_end), lambda: self.b_copy(False, p.z, o).wait_recv())
            if o:
                mine = self.parts.at[2 * p.z + self.column(o), self.b]
                self.close(self.bx_out, (mine,), self.bup_in.at[p.z, o], self.bdn_in.at[p.z, o])
                self.bx_copy().start()
        self.bx_copy().wait_recv()
        self.close(
            self.out.at[self.b],
            (self.parts.at[p.me, self.b], self.bx_in),
            self.bup_in.at[p.z, 0],
            self.bdn_in.at[p.z, 0],
        )
        for c in range(CHUNKS):
            self.cross_copy(p.z, c).wait_recv()
            either(jnp.logical_not(p.low_end), lambda: self.line_copy(True, p.z, c).wait_recv())
            either(jnp.logical_not(p.high_end), lambda: self.line_copy(False, p.z, c).wait_recv())
            at = self.pieces[c]
            self.close(
                self.out.at[at],
                (self.parts.at[p.me, at], self.cross_in.at[p.z, at]),
                self.up_in.at[p.z, at],
                self.down_in.at[p.z, at],
            )

    def drain(self):
        p = self.p
        self.bx_copy().wait_send()

        @pl.loop(0, p.line)
        def _(d):
            def line_sent(up):
                for c in range(CHUNKS):
                    self.line_copy(up, d, c).wait_send()
                self.b_copy(up, d, 0).wait_send()
                self.b_copy(up, d, 1).wait_send()

            for c in range(CHUNKS):
                self.cross_copy(d, c).wait_send()
            either(d > p.z, lambda: line_sent(True))
            either(d < p.z, lambda: line_sent(False))


def dot(a, b):
    return jnp.dot(a, b, preferred_element_type=F32)


def dot_t(a, b):
    return lax.dot_general(a, b, (((1,), (1,)), ((), ())), preferred_element_type=F32)


def t_dot(a, b):
    return lax.dot_general(a, b, (((0,), (0,)), ((), ())), preferred_element_type=F32)


def to_peer(axis, peer, src, dst, send_sem, recv_sem):
    return pltpu.make_async_remote_copy(
        src_ref=src,
        dst_ref=dst,
        send_sem=send_sem,
        recv_sem=recv_sem,
        device_id={axis: peer},
        device_id_type=MESH,
    )


def turn_by(v, cosine, sine):
    half = v.shape[-1] // 2
    a, b = v[:, :half], v[:, half:]
    return jnp.concatenate([a * cosine - b * sine, b * cosine + a * sine], -1)


def turn_back(v, cosine, sine):
    return turn_by(v, cosine, -sine)


def probabilities(query, keys, rows_from, limit):
    scores = dot_t(query, keys) * (1.0 / math.sqrt(HD))
    row = lax.broadcasted_iota(jnp.int32, scores.shape, 0) + rows_from
    col = lax.broadcasted_iota(jnp.int32, scores.shape, 1)
    scores = jnp.where((col <= row) & (col < limit), scores, MASKED)
    weight = jnp.exp(scores - jnp.max(scores, -1, keepdims=True))
    return weight / jnp.sum(weight, -1, keepdims=True)


def row_valid(place, lengths, rows):
    slots = rows // lengths.shape[0]
    row = lax.broadcasted_iota(jnp.int32, (rows, 1), 0)
    limit = jnp.full((rows, 1), lengths[0], jnp.int32)
    for n in range(1, lengths.shape[0]):
        limit = jnp.where(row >= n * slots, lengths[n], limit)
    return place.me * slots + lax.rem(row, slots) < limit


def gain_row(shares, which):
    return jnp.concatenate([shares[b, which : which + 1] for b in range(shares.shape[0])], 1)


def inverse_rms(x):
    return lax.rsqrt(jnp.mean(x * x, -1, keepdims=True) + EPSILON)


def norm_grad(x, inverse, gain, grad):
    weighted = grad * gain
    inner = jnp.sum(weighted * x, -1, keepdims=True)
    return inverse * weighted - x * inverse * inverse * inverse * inner / x.shape[-1]


def start_all(copies):
    for c in copies:
        c.start()


def wait_all(copies):
    for c in copies:
        c.wait()


def scalars():
    return pl.BlockSpec(memory_space=pltpu.SMEM)


def hbm():
    return pl.BlockSpec(memory_space=pl.ANY)


def vm():
    return pl.BlockSpec(memory_space=pltpu.VMEM)


def params(ident):
    return pltpu.CompilerParams(
        collective_id=ident, has_side_effects=True, vmem_limit_bytes=VMEM_LIMIT
    )


def gather_sems(count):
    return [DMA, DMA((3, count, CHUNKS + 1)), DMA((count, CHUNKS + 1))]


def attention_kernel(
    line, groups, seqs,
    lengths, own, cot_raw, pre_gain, mid_gain, freq, wq_hbm, wk_hbm, wv_hbm, wo_hbm,
    branch, small_out, normed_hbm, cot_hbm, q_hbm, k_hbm, v_hbm, attended_hbm, wkv_hbm, cos_hbm, sin_hbm,
    small, cot_own, rows_all, normed, cot_all, q, k, v, attended, wq, wkv, wo, cosine, sine, parts,
    *scratch,
):
    p = Place(line)
    count = 2 * line
    rank = lax.axis_index("grp")
    g1, g2 = scratch[:3], scratch[3:6]
    (load_sem, small_send, small_recv, wy_send, wg_send, w_recv, save_sem) = scratch[6:13]
    r_scratch = scratch[13:]
    half = wk_hbm.shape[0]
    piece = half // 2
    at_own = pl.ds(pl.multiple_of(p.y * half, half), half)
    loads = [
        pltpu.make_async_copy(src, dst, load_sem.at[i])
        for i, (src, dst) in enumerate(
            (
                (wk_hbm, wkv.at[0, at_own]),
                (wv_hbm, wkv.at[1, at_own]),
                (wq_hbm, wq),
                (wo_hbm, wo),
            )
        )
    ]
    p.arrive(groups)
    start_all(loads)

    small[...] = jnp.zeros_like(small)
    small[0:1] = pre_gain[...].astype(F32)[None, :]
    small[1:2] = mid_gain[...].astype(F32)[None, :]
    p.meet(groups)

    def small_copy(step, peer, origin):
        return to_peer(
            "shard", peer, small, small_out.at[origin], small_send.at[step], small_recv.at[step]
        )

    for step in range(1, count):
        small_copy(step, lax.rem(p.me + step, count), p.me).start()
    gather = Gather(p, own, rows_all, *g1, rest=2 * REST)
    gather.start()
    cots = Gather(p, cot_own, cot_all, *g2)
    small_out[p.me] = small[...]

    def rows_of(quarter, column):
        return wkv.at[
            quarter // 2,
            pl.ds(pl.multiple_of(column * half + lax.rem(quarter, 2) * piece, piece), piece),
        ]

    def across():
        ref = rows_of(rank, p.y)
        return to_peer("shard", p.cross, ref, ref, wy_send, w_recv.at[rank])

    def share(step):
        ref = rows_of(rank, 1 - p.y)
        return to_peer(
            "grp", lax.rem(rank + step, groups), ref, ref, wg_send.at[step], w_recv.at[rank]
        )

    wait_all(loads)
    across().start()
    pos = lax.broadcasted_iota(jnp.int32, cosine.shape, 0).astype(F32)
    angle = pos * freq[...]
    cosine[...] = jnp.cos(angle)
    sine[...] = jnp.sin(angle)
    cot = cot_raw[...]
    cot_own[...] = jnp.where(row_valid(p, lengths, cot.shape[0]), cot, jnp.zeros_like(cot))
    gather.hop(1)
    for step in range(1, count):
        small_copy(step, p.me, lax.rem(p.me + count - step, count)).wait_recv()
    gain = gain_row(small_out, 0)
    across().wait_recv()
    for step in range(1, groups):
        share(step).start()
    rows = own.shape[0]
    pair = 2 * rows
    slots = rows // seqs
    low = own.dtype
    for step in range(1, groups):
        quarter = lax.rem(rank + step, groups)
        ref = rows_of(quarter, 1 - p.y)
        to_peer("grp", rank, ref, ref, wg_send.at[step], w_recv.at[quarter]).wait_recv()

    @pl.loop(0, line)
    def _(i):
        d = p.near(i)
        gather.whole(d)
        x = rows_all[pl.ds(2 * d, 2)].reshape(pair, -1).astype(F32)
        n = (x * inverse_rms(x) * gain).astype(low)
        normed[pl.ds(2 * d, 2)] = n.reshape(2, rows, -1)
        at = pl.ds(pl.multiple_of(d * 2 * slots, 2 * slots), 2 * slots)
        c, s = cosine[at], sine[at]

        def by_rows(t):
            return jnp.concatenate([t[:slots]] * seqs + [t[slots:]] * seqs, 0)

        c, s = by_rows(c), by_rows(s)

        def put(target, value):
            for block in range(2):
                for m in range(seqs):
                    to = pl.ds(
                        pl.multiple_of(d * 2 * slots + block * slots, slots), slots
                    )
                    target[m, to] = value[block * rows + m * slots : block * rows + (m + 1) * slots]

        put(q, turn_by(dot_t(n, wq[...]), c, s).astype(low))
        put(k, turn_by(dot_t(n, wkv[0]), c, s).astype(low))
        put(v, dot_t(n, wkv[1]).astype(low))
        gather.hop(i + 2)
        either(i == line - 3, cots.send_own)

    saves = [
        pltpu.make_async_copy(src, dst, save_sem.at[i])
        for i, (src, dst) in enumerate(
            (
                (normed, normed_hbm),
                (q, q_hbm),
                (k, k_hbm),
                (v, v_hbm),
                (wkv, wkv_hbm),
                (cosine, cos_hbm),
                (sine, sin_hbm),
            )
        )
    ]
    start_all(saves)
    cots.pass_rest()
    total_slots = q.shape[1]
    tile = min(256, total_slots)

    @pl.loop(0, seqs)
    def _(n):
        for t in range(total_slots // tile):
            span = (t + 1) * tile
            at = pl.ds(t * tile, tile)
            probs = probabilities(q[n, at], k[n, pl.ds(0, span)], t * tile, lengths[n])
            out = dot(probs.astype(low), v[n, pl.ds(0, span)]).astype(low)
            for c in range(tile // slots):
                b = (t * tile) // slots + c
                attended[pl.ds(pl.multiple_of(b * rows + n * slots, slots), slots)] = out[
                    c * slots : (c + 1) * slots
                ]
        cots.hop(n + 1)

    for h in range(seqs + 1, line):
        cots.hop(h)

    @pl.loop(0, line)
    def _(d):
        at = pl.ds(pl.multiple_of(d * pair, pair), pair)
        parts[pl.ds(2 * d, 2)] = dot(attended[at], wo[...]).astype(low).reshape(2, rows, -1)

    reduce = Reduce(p, parts, branch, r_scratch)
    saves2 = [pltpu.make_async_copy(attended, attended_hbm, save_sem.at[7])]
    start_all(saves2)
    for d in range(line):
        cots.whole(d)
    for i in range(DEPTH):
        reduce.send_across(i)
    saves3 = [pltpu.make_async_copy(cot_all, cot_hbm, save_sem.at[8])]
    start_all(saves3)
    for i in range(line - 1):
        reduce.b_hop(i)
    for i in range(line - 1):
        reduce.hop(i)
        if i + DEPTH < line:
            reduce.send_across(i + DEPTH)
    reduce.finish()
    reduce.drain()
    gather.drain()
    cots.drain()
    wait_all(saves + saves2 + saves3)
    across().wait_send()
    for step in range(1, groups):
        share(step).wait_send()
    for step in range(1, count):
        small_copy(step, lax.rem(p.me + step, count), p.me).wait_send()


def attention(lengths, own, cot, pre_gain, mid_gain, freq, wq, wk, wv, wo, count, groups, ident):
    rows, width = own.shape
    seqs = lengths.shape[0]
    total_slots = count * rows // seqs
    small = (8, pre_gain.shape[0])
    line = count // 2
    low = own.dtype
    v = pltpu.VMEM
    shape = jax.ShapeDtypeStruct
    hd = wq.shape[0]
    big = (count, rows, width)
    head = (seqs, total_slots, hd)
    table = (total_slots, hd // 2)
    flat = (count * rows, hd)
    return pl.pallas_call(
        functools.partial(attention_kernel, line, groups, seqs),
        out_shape=(
            shape((rows, width), F32),
            shape((count,) + small, F32),
            shape(big, low),
            shape(big, low),
            shape(head, low),
            shape(head, low),
            shape(head, low),
            shape(flat, low),
            shape((2, hd, width), low),
            shape(table, F32),
            shape(table, F32),
        ),
        in_specs=[scalars()] + [vm()] * 5 + [hbm()] * 4,
        out_specs=(vm(), vm()) + (hbm(),) * 9,
        scratch_shapes=[
            v(small, F32), v((rows, width), low), v(big, low), v(big, low), v(big, low), v(head, low), v(head, low), v(head, low), v(flat, low),
            v((hd, width), low), v((2, hd, width), low), v((hd, width), low), v(table, F32), v(table, F32), v(big, low),
        ]
        + gather_sems(count) * 2
        + [DMA((4,)), DMA((count,)), DMA((count,)), DMA, DMA((groups,)), DMA((groups,)), DMA((9,))]
        + Reduce.scratch(line, rows, width, low),
        compiler_params=params(ident),
        name="attention",
    )(lengths, own, cot, pre_gain, mid_gain, freq, wq, wk, wv, wo)


def ffn_kernel(
    line, groups,
    tokens, branch, gains, cot_hbm, gate_hbm, up_hbm, down_hbm,
    second, ffn_hbm, pair_hbm, chip_in,
    own, rights, gate_up, down_w, lefts, parts, stage, theirs,
    *scratch,
):
    p = Place(line)
    rank = lax.axis_index("grp")
    core = lax.rem(rank, 2)
    partner = rank + 1 - 2 * core
    opposite = lax.rem(rank + 2, groups)
    (load_sem, out_sem, stage_send, stage_recv, chip_send, chip_recv) = scratch[3:9]
    units = down_w.shape[0]
    gate_w, up_w = gate_up.at[pl.ds(0, units)], gate_up.at[pl.ds(units, units)]
    cot, normed = rights.at[0], rights.at[1]
    hidden, gate_g, up_g = lefts.at[0], lefts.at[1], lefts.at[2]
    loads = [
        pltpu.make_async_copy(src, dst, load_sem.at[i])
        for i, (src, dst) in enumerate(
            ((cot_hbm, cot), (down_hbm, down_w), (gate_hbm, gate_w), (up_hbm, up_w))
        )
    ]
    p.arrive_near((partner, opposite))
    start_all(loads)
    middle = tokens[...].astype(F32) + branch[...]
    own[...] = (middle * inverse_rms(middle) * gain_row(gains, 1)).astype(own.dtype)
    p.meet_near((partner, opposite))
    gather = Gather(p, own, normed, *scratch[:3])
    gather.send_own()
    wait_all(loads[:2])
    rows = own.shape[0]
    pair = 2 * rows
    low = own.dtype

    @pl.loop(0, line)
    def _(d):
        at = pl.ds(pl.multiple_of(d * pair, pair), pair)
        gate_g[at] = dot_t(cot[pl.ds(2 * d, 2)].reshape(pair, -1), down_w[...]).astype(low)

    gather.pass_rest()
    wait_all(loads[2:])

    @pl.loop(0, line)
    def _(i):
        gather.hop(i + 1)
        d = p.near(i)
        gather.whole(d)
        x = normed[pl.ds(2 * d, 2)].reshape(pair, -1)
        g = dot_t(x, gate_w[...])
        u = dot_t(x, up_w[...])
        s = 1.0 / (1.0 + jnp.exp(-g))
        silu = g * s
        at = pl.ds(pl.multiple_of(d * pair, pair), pair)
        dh = gate_g[at].astype(F32)
        hidden[at] = (silu * u).astype(low)
        up_g[at] = (dh * silu).astype(low)
        gate_g[at] = (dh * u * s * (1.0 + g * (1.0 - s))).astype(low)
        part = dot(gate_g[at], gate_w[...]) + dot(up_g[at], up_w[...])
        parts[pl.ds(2 * d, 2)] = part.astype(low).reshape(2, rows, -1)

    reduce = Reduce(p, parts, second, scratch[9:])
    for i in range(line):
        reduce.send_across(i)

    quarter = units // 4
    half = units // 2

    def mine(which):
        start = lax.rem(which + 2, 3) * half
        return gate_up.at[pl.ds(pl.multiple_of(start, half), half)]

    def to_partner(which, j):
        return to_peer(
            "grp",
            partner,
            stage.at[j],
            theirs.at[which, pl.ds(pl.multiple_of(j * quarter, quarter), quarter)],
            stage_send.at[j],
            stage_recv.at[which, j],
        )

    def chip_copy():
        return to_peer(
            "grp",
            opposite,
            gate_up.at[pl.ds(2 * half, chip_in.shape[0])],
            chip_in,
            chip_send,
            chip_recv,
        )

    def save_pair(which):
        return pltpu.make_async_copy(mine(which), pair_hbm.at[which], out_sem.at[which])

    def core_sum(which):
        for j in range(2):
            to_partner(which, j).wait_recv()
        total_into(mine(which), mine(which), theirs.at[which])
        save_pair(which).start()

    @pl.loop(0, 3)
    def _(which):
        right = rights.at[jnp.minimum(which, 1)]

        def block(q):
            cols = pl.ds(pl.multiple_of(q * quarter, quarter), quarter)
            left = lefts[which, :, cols]
            return t_dot(left, right[...].reshape(left.shape[0], -1)).astype(low)

        @pl.loop(0, 2)
        def _(j):
            either(which > 0, lambda: to_partner(which - 1, j).wait_send())
            stage[j] = block(2 * (1 - core) + j)
            to_partner(which, j).start()

        @pl.when(which == 0)
        def _():
            for i in range(line - 1):
                reduce.b_hop(i)

        either(which > 1, lambda: core_sum(which - 1))

        at_end = p.low_end | p.high_end
        either(at_end, lambda: reduce.step(which, 0))

        @pl.loop(0, 2)
        def _(j):
            at = pl.ds(pl.multiple_of(j * quarter, quarter), quarter)
            mine(which)[at] = block(2 * core + j)

        @pl.when(at_end)
        def _():
            for c in range(1, CHUNKS):
                reduce.step(which, c)

        @pl.when(which == 0)
        def _():
            core_sum(0)
            chip_copy().start()

        @pl.when(jnp.logical_not(at_end))
        def _():
            for c in range(CHUNKS):
                reduce.step(which, c)

    core_sum(2)
    gather.drain()

    @pl.loop(0, line)
    def _(d):
        at = pl.ds(pl.multiple_of(d * pair, pair), pair)
        normed[pl.ds(2 * d, 2)] = dot(hidden[at], down_w[...]).astype(low).reshape(2, rows, -1)

    ffn_save = pltpu.make_async_copy(normed, ffn_hbm, out_sem.at[3])
    ffn_save.start()
    reduce.finish()
    for j in range(2):
        to_partner(2, j).wait_send()

    reduce.drain()
    chip_copy().wait()
    ffn_save.wait()
    for which in range(3):
        save_pair(which).wait()


def ffn(tokens, branch, gains, cot, gate_w, up_w, down_w, groups, ident):
    rows, width = tokens.shape
    count = cot.shape[0]
    line = count // 2
    units = gate_w.shape[0]
    low = tokens.dtype
    v = pltpu.VMEM
    tall = count * rows
    shape = jax.ShapeDtypeStruct
    big = (count, rows, width)
    half = (units // 2, width)
    return pl.pallas_call(
        functools.partial(ffn_kernel, line, groups),
        out_shape=(
            shape((rows, width), F32),
            shape(big, low),
            shape((3,) + half, low),
            shape((EARLY * PIECE, width), low),
        ),
        in_specs=[vm()] * 3 + [hbm()] * 4,
        out_specs=(vm(), hbm(), hbm(), hbm()),
        scratch_shapes=[v((rows, width), low)]
        + [v((2,) + big, low), v((2 * units, width), low), v((units, width), low)]
        + [v((3, tall, units), low), v(big, low), v((2, units // 4, width), low), v((3,) + half, low)]
        + gather_sems(count)
        + [DMA((4,)), DMA((4,)), DMA((2,)), DMA((3, 2)), DMA, DMA]
        + Reduce.scratch(line, rows, width, low),
        compiler_params=params(ident),
        name="ffn",
    )(tokens, branch, gains, cot, gate_w, up_w, down_w)


def attention_grad_kernel(
    line, groups, seqs,
    lengths, tokens, branch, cot, second, gains, cosine, sine,
    ffn_hbm, normed_hbm, attended_hbm, q_hbm, k_hbm, v_hbm, wq_hbm, wkv_hbm, wo_hbm, sums_hbm, early_hbm,
    mixed, input_grad, gain_out, total_hbm, wide_hbm, narrow_hbm,
    own, middle_grad, first, ffn_own, dbranch, normed, attended, q, k, v, wq, wkv, wo, da, dk_acc, dv_acc, dq_rows, dk_rows, dv_rows,
    halves, half_in, ffn_parts, sums, sums_in, stage, mine, theirs, mine_in, gain_held, gain_in, gain_sum, gain_all,
    *scratch,
):
    p = Place(line)
    count = 2 * line
    rank = lax.axis_index("grp")
    core = lax.rem(rank, 2)
    partner = rank + 1 - 2 * core
    opposite = lax.rem(rank + 2, groups)
    (
        load_sem, chip_send, chip_recv, half_send, half_recv, stage_send, stage_recv,
        back_send, back_recv, keep_sem, ga_send, ga_recv, gb_send, gb_recv,
    ) = scratch[3:17]
    n = Reduce.N_SCRATCH
    loads = [
        pltpu.make_async_copy(src, dst, load_sem.at[i])
        for i, (src, dst) in enumerate(
            (
                (wo_hbm, wo),
                (ffn_hbm, ffn_parts),
                (attended_hbm, attended),
                (q_hbm, q),
                (k_hbm, k),
                (v_hbm, v),
                (wq_hbm, wq),
                (wkv_hbm, wkv),
                (normed_hbm, normed),
                (early_hbm, sums_in.at[pl.ds(0, EARLY)]),
            )
        )
    ]
    p.arrive(groups)
    start_all(loads)

    def load_sum(i):
        return pltpu.make_async_copy(sums_hbm.at[i], sums.at[lax.rem(i, 2)], load_sem.at[10 + lax.rem(i, 2)])

    load_sum(0).start()
    load_sum(1).start()
    middle = tokens[...].astype(F32) + branch[...]
    inverse = inverse_rms(middle)
    grad = cot[...].astype(F32)
    grad = jnp.where(row_valid(p, lengths, grad.shape[0]), grad, jnp.zeros_like(grad))
    grad = grad + norm_grad(middle, inverse, gain_row(gains, 1), second[...])
    middle_grad[...] = grad
    own[...] = grad.astype(own.dtype)
    mid_total = jnp.sum(second[...] * middle * inverse, 0, keepdims=True)
    share = gain_held.shape[2]
    for b in range(count):
        gain_held[b] = jnp.zeros(gain_held.shape[1:], F32)
        gain_held[b, 1:2] = mid_total[:, b * share : (b + 1) * share]
    p.meet(groups)
    gather = Gather(p, own, dbranch, *scratch[:3])
    n_sums = sums_hbm.shape[0]
    part_rows = sums.shape[1]

    def chip_copy(i):
        return to_peer(
            "grp", opposite, sums_hbm.at[i], sums_in.at[i], chip_send.at[i], chip_recv.at[i]
        )

    gather.start()

    @pl.loop(EARLY, n_sums)
    def _(i):
        chip_copy(i).start()

    wait_all(loads)
    ffn_sum = Reduce(p, ffn_parts, ffn_own, scratch[17 : 17 + n])
    rows = own.shape[0]
    pair = 2 * rows
    slots = rows // seqs
    low = own.dtype
    scale = 1.0 / math.sqrt(HD)

    @pl.loop(0, line)
    def _(i):
        gather.hop(i + 1)

        @pl.when(i == line - 2)
        def _():
            for first_sends in range(DEPTH):
                ffn_sum.send_across(first_sends)

        d = p.near(i)
        gather.whole(d)
        grad = dot_t(dbranch[pl.ds(2 * d, 2)].reshape(pair, -1), wo[...]).astype(low)
        for block in range(2):
            for m in range(seqs):
                at = pl.ds(pl.multiple_of(d * 2 * slots + block * slots, slots), slots)
                da[m, at] = grad[block * rows + m * slots : block * rows + (m + 1) * slots]

    for i in range(line - 1):
        ffn_sum.b_hop(i)

    chunk = stage.shape[1]

    def to_partner(b):
        return to_peer(
            "grp",
            partner,
            stage.at[b // 2],
            theirs.at[pl.ds(b // 2 * chunk, chunk)],
            stage_send.at[b // 2],
            stage_recv.at[b // 2],
        )

    def gradient(b, left, right):
        value = t_dot(left, right[...].reshape(left.shape[0], -1)).astype(low)
        keep = core == b % 2

        @pl.when(keep)
        def _():
            mine[pl.ds(b // 2 * chunk, chunk)] = value

        @pl.when(jnp.logical_not(keep))
        def _():
            stage[b // 2] = value
            to_partner(b).start()

    total_slots = q.shape[1]
    tile = min(256, total_slots)

    def backward(m):
        dk_acc[...] = jnp.zeros_like(dk_acc)
        dv_acc[...] = jnp.zeros_like(dv_acc)

        def to_rows(target, value, start, size):
            for c in range(size // slots):
                b = start // slots + c
                target[pl.ds(pl.multiple_of(b * rows + m * slots, slots), slots)] = value[
                    c * slots : (c + 1) * slots
                ]

        for t in range(total_slots // tile):
            span = (t + 1) * tile
            at = pl.ds(t * tile, tile)
            query, grad = q[m, at], da[m, at]
            keys, values = k[m, pl.ds(0, span)], v[m, pl.ds(0, span)]
            probs = probabilities(query, keys, t * tile, lengths[m])
            dprobs = dot_t(grad, values)
            inner = jnp.sum(probs * dprobs, -1, keepdims=True)
            dscores = (probs * (dprobs - inner)).astype(low)
            dq = turn_back(dot(dscores, keys) * scale, cosine[at], sine[at])
            to_rows(dq_rows, dq.astype(low), t * tile, tile)
            dk_acc[pl.ds(0, span)] += t_dot(dscores, query)
            dv_acc[pl.ds(0, span)] += t_dot(probs.astype(low), grad)
        dk = turn_back(dk_acc[...] * scale, cosine[...], sine[...])
        to_rows(dk_rows, dk.astype(low), 0, total_slots)
        to_rows(dv_rows, dv_acc[...].astype(low), 0, total_slots)

    half = HD // 2

    def swap():
        return to_peer("shard", p.cross, halves.at[1 - p.y], half_in, half_send, half_recv)

    gradient(0, attended[:, :chunk], dbranch)
    gradient(1, attended[:, chunk:], dbranch)

    @pl.loop(0, seqs)
    def _(m):
        backward(m)
        ffn_sum.hop(m)
        ffn_sum.send_across(m + DEPTH)

    for h in range(2):
        halves[h, 0] = dk_rows[:, h * half : (h + 1) * half]
        halves[h, 1] = dv_rows[:, h * half : (h + 1) * half]
    swap().start()
    gather.drain()
    parts = dbranch
    gradient(2, dq_rows[:, :chunk], normed)
    gradient(3, dq_rows[:, chunk:], normed)

    spans = (pl.ds(0, 2 * chunk), pl.ds(2 * chunk, chunk))

    def attn_chip(part):
        return to_peer(
            "grp",
            opposite,
            mine.at[spans[part]],
            mine_in.at[spans[part]],
            chip_send.at[n_sums + part],
            chip_recv.at[n_sums + part],
        )

    def attn_pair(part, blocks):
        for b in blocks:
            to_partner(2 * b).wait_recv()
        at = mine.at[spans[part]]
        total_into(at, at, theirs.at[spans[part]])
        attn_chip(part).start()

    def back_attn(slot):
        if slot < 2:
            out = wide_hbm.at[slot, pl.ds(pl.multiple_of(core * chunk, chunk), chunk)]
        else:
            out = narrow_hbm.at[core]
        at = mine.at[pl.ds(slot * chunk, chunk)]
        n_slot = n_sums + slot
        sems = keep_sem.at[n_slot], back_send.at[n_slot], back_recv.at[n_slot]
        return pltpu.make_async_copy(at, out, sems[0]), to_peer("grp", partner, at, out, *sems[1:])

    def attn_total(part):
        attn_chip(part).wait()
        at = mine.at[spans[part]]
        total_into(at, at, mine_in.at[spans[part]])
        for slot in (0, 1) if part == 0 else (2,):
            start_all(back_attn(slot))


    @pl.loop(0, line)
    def _(d):
        at = pl.ds(pl.multiple_of(d * pair, pair), pair)
        part = dot(dq_rows[at], wq[...]) + dot(dk_rows[at], wkv[0]) + dot(dv_rows[at], wkv[1])
        parts[pl.ds(2 * d, 2)] = part.astype(low).reshape(2, rows, -1)

    for i in range(seqs, line - 1):
        ffn_sum.hop(i)
    def back(i):
        per_half = n_sums // 3
        start = core * per_half * part_rows + lax.rem(i, per_half) * part_rows
        at = pl.ds(pl.multiple_of(start, part_rows), part_rows)
        out = total_hbm.at[lax.div(i, per_half), at]
        return (
            pltpu.make_async_copy(sums_in.at[i], out, keep_sem.at[i]),
            to_peer("grp", partner, sums_in.at[i], out, back_send.at[i], back_recv.at[i]),
        )

    def sum_up(first_piece, end):
        @pl.loop(first_piece, end)
        def _(i):
            either(i >= EARLY, lambda: chip_copy(i).wait())
            load_sum(i).wait()
            total_into(sums_in.at[i], sums.at[lax.rem(i, 2)], sums_in.at[i])
            either(i + 2 < n_sums, lambda: load_sum(i + 2).start())
            start_all(back(i))

    def gain_copy(step, peer, origin):
        return to_peer(
            "shard", peer, gain_held.at[peer], gain_in.at[origin], ga_send.at[step], ga_recv.at[step]
        )

    def gain_group(step, peer, origin):
        return to_peer(
            "grp", peer, gain_sum, gain_all.at[origin], gb_send.at[step], gb_recv.at[step]
        )

    def gain_first():
        def body(i, total):
            at = pl.ds(pl.multiple_of(i * 16, 16), 16)
            for b in range(count):
                total = total + parts[b, at].astype(F32) * normed[b, at].astype(F32)
            return total

        total = lax.fori_loop(0, rows // 16, body, jnp.zeros((16, parts.shape[2]), F32))
        total = jnp.sum(total, 0, keepdims=True) / gain_row(gains, 0)
        for b in range(count):
            gain_held[b, 0:1] = total[:, b * share : (b + 1) * share]
        for step in range(1, count):
            gain_copy(step, lax.rem(p.me + step, count), p.me).start()

    def gain_second():
        for step in range(1, count):
            gain_copy(step, p.me, lax.rem(p.me + count - step, count)).wait_recv()
        gain_in[p.me] = gain_held[p.me]
        total = gain_in[0]
        for b in range(1, count):
            total = total + gain_in[b]
        gain_sum[...] = total
        gain_all[rank] = total
        for step in range(1, groups):
            gain_group(step, lax.rem(rank + step, groups), rank).start()

    sum_up(0, n_sums // 3)
    attn_pair(0, (0, 1))
    gain_first()
    ffn_sum.finish()
    reduce = Reduce(p, parts, first, scratch[17 + n :])
    for i in range(DEPTH):
        reduce.send_across(i)
    for i in range(line - 1):
        reduce.b_hop(i)

    def summed(which):
        return (halves[p.y, which].astype(F32) + half_in[which].astype(F32)).astype(low)

    valid = row_valid(p, lengths, rows)
    result = tokens[...].astype(F32) + branch[...] + ffn_own[...]
    mixed[...] = jnp.where(valid, result, jnp.zeros_like(result)).astype(low)

    swap().wait_recv()
    gradient(4, summed(0), normed)
    gradient(5, summed(1), normed)
    reduce.hop(0)
    reduce.send_across(DEPTH)
    attn_pair(1, (2,))
    sum_up(n_sums // 3, n_sums // 2)
    reduce.hop(1)
    reduce.send_across(DEPTH + 1)
    gain_second()
    sum_up(n_sums // 2, n_sums - 3)
    reduce.hop(2)
    sum_up(n_sums - 3, n_sums)
    attn_total(0)
    reduce.finish()
    attn_total(1)
    for step in range(1, groups):
        gain_group(step, rank, lax.rem(rank + groups - step, groups)).wait_recv()
    total = gain_all[0]
    for b in range(1, groups):
        total = total + gain_all[b]
    gain_out[...] = total
    source = tokens[...].astype(F32)
    inner = norm_grad(source, inverse_rms(source), gain_row(gains, 0), first[...])
    input_grad[...] = (middle_grad[...] + inner).astype(low)
    reduce.drain()
    ffn_sum.drain()
    swap().wait_send()
    for b in range(3):
        to_partner(2 * b).wait_send()
    for step in range(1, count):
        gain_copy(step, lax.rem(p.me + step, count), p.me).wait_send()
    for step in range(1, groups):
        gain_group(step, lax.rem(rank + step, groups), rank).wait_send()

    @pl.loop(0, n_sums)
    def _(i):
        wait_all(back(i))

    for slot in range(3):
        wait_all(back_attn(slot))


def attention_grad(
    lengths, tokens, branch, cot, second, gains, cosine, sine, ffn_parts, normed, attended, q, k, v, wq, wkv, wo, sums, early,
    groups, ident,
):
    rows, width = tokens.shape
    count = normed.shape[0]
    line = count // 2
    seqs, total_slots, hd = q.shape
    low = tokens.dtype
    vmem = pltpu.VMEM
    tall = count * rows
    half = hd // 2
    sums = sums.reshape(-1, PIECE, width)
    early = early.reshape(-1, PIECE, width)
    n_sums, part_rows, _ = sums.shape
    shape = jax.ShapeDtypeStruct
    big = vmem((count, rows, width), low)
    head = vmem((seqs, total_slots, hd), low)
    weight = vmem((hd, width), low)
    flat = vmem((tall, hd), low)
    acc = vmem((total_slots, hd), F32)
    third = vmem((3 * half, width), low)
    g = gains.shape
    block = vmem((rows, width), F32)
    return pl.pallas_call(
        functools.partial(attention_grad_kernel, line, groups, seqs),
        out_shape=(
            shape((rows, width), low),
            shape((rows, width), low),
            shape(g[1:], F32),
            shape((3, n_sums // 3 * 2 * part_rows, width), low),
            shape((2, 2 * half, width), low),
            shape((2, half, width), low),
        ),
        in_specs=[scalars()] + [vm()] * 7 + [hbm()] * 11,
        out_specs=(vm(), vm(), vm(), hbm(), hbm(), hbm()),
        scratch_shapes=[
            vmem((rows, width), low), block, block, block,
            big, big, flat, head, head, head, weight, vmem((2, hd, width), low), weight, head, acc, acc,
            flat, flat, flat,
            vmem((2, 2, tall, half), low), vmem((2, tall, half), low), big,
            vmem((2,) + sums.shape[1:], low), vmem(sums.shape, low), vmem((3, half, width), low), third, third, third,
            vmem(g, F32), vmem(g, F32), vmem(g[1:], F32), vmem((groups,) + g[1:], F32),
        ]
        + gather_sems(count)
        + [
            DMA((12,)), DMA((n_sums + 2,)), DMA((n_sums + 2,)), DMA, DMA, DMA((3,)), DMA((3,)),
            DMA((n_sums + 3,)), DMA((n_sums + 3,)), DMA((n_sums + 3,)),
            DMA((count,)), DMA((count,)), DMA((groups,)), DMA((groups,)),
        ]
        + Reduce.scratch(line, rows, width, low) * 2,
        compiler_params=params(ident),
        name="attention_grad",
    )(
        lengths, tokens, branch, cot, second, gains, cosine, sine, ffn_parts, normed, attended, q, k, v, wq, wkv, wo, sums, early
    )


epsilon = 1e-06
theta_base = 1000042.0
masked_value = -1e30


def turned(source):
    half_width = source.shape[-1] // 2
    return jnp.concatenate([-source[..., half_width:], source[..., :half_width]], -1)


def rotate(source, cosine_table, sine_table):
    return source * cosine_table + turned(source) * sine_table


def unrotate(source, cosine_table, sine_table):
    return source * cosine_table - turned(source) * sine_table


def norm_forward(source, norm_gain):
    inverse = lax.rsqrt(jnp.mean(source * source, -1, keepdims=True) + epsilon)
    return (source * inverse * norm_gain, inverse)


def norm_backward(source, inverse, norm_gain, grad_out):
    weighted = grad_out * norm_gain
    inner_sum = jnp.sum(weighted * source, -1, keepdims=True)
    grad_in = (
        inverse * weighted - source * inverse * inverse * inverse * inner_sum / source.shape[-1]
    )
    return (grad_in, jnp.sum(grad_out * source * inverse, 0))


def weight_terms(normed, query_grad, key_grad, value_grad, attended, branch_grad, shard_count):
    token_count, model_width = normed.shape
    query_share = query_grad.shape[1] // shard_count
    kv_share = key_grad.shape[1] // shard_count
    shard_rows = 2 * query_share + 2 * kv_share

    def weight_term(first_row, row_count):
        blocks = row_count // shard_rows

        def columns(matrix, share_cols):
            return matrix.reshape(token_count, blocks, share_cols)

        part_query = jnp.einsum(
            "tmr,td->mrd",
            columns(query_grad, query_share),
            normed,
            preferred_element_type=jnp.float32,
        )
        part_key = jnp.einsum(
            "tmr,td->mrd", columns(key_grad, kv_share), normed, preferred_element_type=jnp.float32
        )
        part_value = jnp.einsum(
            "tmr,td->mrd", columns(value_grad, kv_share), normed, preferred_element_type=jnp.float32
        )
        part_out = jnp.einsum(
            "tmr,td->mrd",
            columns(attended, query_share),
            branch_grad,
            preferred_element_type=jnp.float32,
        )
        return jnp.concatenate([part_query, part_key, part_value, part_out], 1).reshape(
            row_count, model_width
        )

    return (weight_term, shard_rows)


def local_rows(
    tokens,
    lengths,
    prenorm_gain,
    query_weight,
    key_weight,
    value_weight,
    out_weight,
    midnorm_gain,
    gate_weight,
    up_weight,
    down_weight,
    cotangent,
):
    shard_count = lax.axis_size("shard")
    shard_rank = lax.axis_index("shard")
    micro_count, seq_dev, model_width = tokens.shape
    slot_count = seq_dev * shard_count
    repeat_heads = NH // KVH
    query_width = NH * HD
    kv_width = KVH * HD
    score_scale = 1.0 / math.sqrt(HD)
    local_pos = shard_rank * seq_dev + jnp.arange(seq_dev, dtype=jnp.int32)
    key_pos = jnp.arange(slot_count, dtype=jnp.int32)
    inverse_freq = theta_base ** (-(jnp.arange(0, HD, 2).astype(jnp.float32) / HD))
    angles = local_pos.astype(jnp.float32)[:, None] * inverse_freq[None, :]
    cosine_table = jnp.concatenate([jnp.cos(angles), jnp.cos(angles)], -1)[:, None, :]
    sine_table = jnp.concatenate([jnp.sin(angles), jnp.sin(angles)], -1)[:, None, :]
    gate_total = jnp.zeros(gate_weight.shape, jnp.float32)
    up_total = jnp.zeros(up_weight.shape, jnp.float32)
    down_total = jnp.zeros(down_weight.shape, jnp.float32)
    prenorm_total = jnp.zeros((model_width,), jnp.float32)
    midnorm_total = jnp.zeros((model_width,), jnp.float32)
    attn_total = None
    mixed_rows = []
    input_rows = []
    for micro_index in range(micro_count):
        gathered = (
            lax.all_gather(query_weight, "shard", axis=0, tiled=True),
            lax.all_gather(key_weight, "shard", axis=0, tiled=True),
            lax.all_gather(value_weight, "shard", axis=0, tiled=True),
            lax.all_gather(prenorm_gain, "shard", axis=0, tiled=True),
            lax.all_gather(midnorm_gain, "shard", axis=0, tiled=True),
        )
        query_full, key_full, value_full, prenorm_full, midnorm_full = gathered
        prenorm_f = prenorm_full.astype(jnp.float32)
        midnorm_f = midnorm_full.astype(jnp.float32)
        source = tokens[micro_index].astype(jnp.float32)
        length_now = lengths[micro_index]
        valid_rows = local_pos < length_now
        scaled_first, inverse_first = norm_forward(source, prenorm_f)
        normed_first = scaled_first.astype(jnp.bfloat16)
        query_pre = jnp.einsum(
            "sd,qd->sq", normed_first, query_full, preferred_element_type=jnp.float32
        ).reshape(seq_dev, NH, HD)
        key_pre = jnp.einsum(
            "sd,qd->sq", normed_first, key_full, preferred_element_type=jnp.float32
        ).reshape(seq_dev, KVH, HD)
        value_pre = jnp.einsum(
            "sd,qd->sq", normed_first, value_full, preferred_element_type=jnp.float32
        )
        query_rot = rotate(query_pre, cosine_table, sine_table).astype(jnp.bfloat16)
        key_rot = rotate(key_pre, cosine_table, sine_table).astype(jnp.bfloat16)
        key_value = jnp.concatenate(
            [key_rot.reshape(seq_dev, kv_width), value_pre.astype(jnp.bfloat16)], 1
        )
        kv_all = lax.all_gather(key_value, "shard", axis=0, tiled=True)
        keys_all = kv_all[:, :kv_width].reshape(slot_count, KVH, HD)
        values_all = kv_all[:, kv_width:].reshape(slot_count, KVH, HD)
        query_group = query_rot.reshape(seq_dev, KVH, repeat_heads, HD)
        scores = (
            jnp.einsum("skrd,tkd->krst", query_group, keys_all, preferred_element_type=jnp.float32)
            * score_scale
        )
        allowed = (key_pos[None, :] <= local_pos[:, None]) & (key_pos[None, :] < length_now)
        scores = jnp.where(allowed, scores, masked_value)
        row_max = jnp.max(scores, -1, keepdims=True)
        exp_scores = jnp.exp(scores - row_max)
        attention_probs = exp_scores / jnp.sum(exp_scores, -1, keepdims=True)
        probs_low = attention_probs.astype(jnp.bfloat16)
        attended = (
            jnp.einsum("krst,tkd->skrd", probs_low, values_all, preferred_element_type=jnp.float32)
            .astype(jnp.bfloat16)
            .reshape(seq_dev, query_width)
        )
        branch = jnp.dot(
            attended,
            lax.all_gather(out_weight, "shard", axis=0, tiled=True),
            preferred_element_type=jnp.float32,
        )
        middle = source + branch
        scaled_second, inverse_second = norm_forward(middle, midnorm_f)
        normed_second = scaled_second.astype(jnp.bfloat16)
        normed_all = lax.all_gather(normed_second, "shard", axis=0, tiled=True)
        gate_pre = jnp.einsum(
            "sd,fd->sf", normed_all, gate_weight, preferred_element_type=jnp.float32
        )
        up_pre = jnp.einsum("sd,fd->sf", normed_all, up_weight, preferred_element_type=jnp.float32)
        sigmoid_gate = jax.nn.sigmoid(gate_pre)
        silu_gate = gate_pre * sigmoid_gate
        hidden = (silu_gate * up_pre).astype(jnp.bfloat16)
        ffn_part = lax.psum_scatter(
            jnp.dot(hidden, down_weight, preferred_element_type=jnp.float32).astype(jnp.bfloat16),
            "shard",
            scatter_dimension=0,
            tiled=True,
        ).astype(jnp.float32)
        mixed_rows.append(
            jnp.where(valid_rows[:, None], middle + ffn_part, 0.0).astype(jnp.bfloat16)
        )
        cot_low = jnp.where(
            valid_rows[:, None], cotangent[micro_index], jnp.zeros_like(cotangent[micro_index])
        )
        cot_all = lax.all_gather(cot_low, "shard", axis=0, tiled=True)
        hidden_grad = jnp.einsum(
            "sd,fd->sf", cot_all, down_weight, preferred_element_type=jnp.float32
        )
        down_total = down_total + jnp.einsum(
            "sf,sd->fd", hidden, cot_all, preferred_element_type=jnp.float32
        )
        gate_grad = (
            hidden_grad * up_pre * sigmoid_gate * (1.0 + gate_pre * (1.0 - sigmoid_gate))
        ).astype(jnp.bfloat16)
        up_grad = (hidden_grad * silu_gate).astype(jnp.bfloat16)
        gate_total = gate_total + jnp.einsum(
            "sf,sd->fd", gate_grad, normed_all, preferred_element_type=jnp.float32
        )
        up_total = up_total + jnp.einsum(
            "sf,sd->fd", up_grad, normed_all, preferred_element_type=jnp.float32
        )
        second_grad = lax.psum_scatter(
            jnp.dot(gate_grad, gate_weight, preferred_element_type=jnp.float32)
            + jnp.dot(up_grad, up_weight, preferred_element_type=jnp.float32),
            "shard",
            scatter_dimension=0,
            tiled=True,
        )
        middle_part, midnorm_part = norm_backward(middle, inverse_second, midnorm_f, second_grad)
        middle_grad = cot_low.astype(jnp.float32) + middle_part
        midnorm_total = midnorm_total + midnorm_part
        branch_grad = middle_grad.astype(jnp.bfloat16)
        attended_grad = jnp.einsum(
            "sd,qd->sq",
            branch_grad,
            lax.all_gather(out_weight, "shard", axis=0, tiled=True),
            preferred_element_type=jnp.float32,
        ).astype(jnp.bfloat16)
        attended_group = attended_grad.reshape(seq_dev, KVH, repeat_heads, HD)
        probs_grad = jnp.einsum(
            "skrd,tkd->krst", attended_group, values_all, preferred_element_type=jnp.float32
        )
        inner_sum = jnp.sum(attention_probs * probs_grad, -1, keepdims=True)
        scores_grad = (attention_probs * (probs_grad - inner_sum)).astype(jnp.bfloat16)
        query_rot_grad = (
            jnp.einsum(
                "krst,tkd->skrd", scores_grad, keys_all, preferred_element_type=jnp.float32
            ).reshape(seq_dev, NH, HD)
            * score_scale
        )
        query_grad = (
            unrotate(query_rot_grad, cosine_table, sine_table)
            .astype(jnp.bfloat16)
            .reshape(seq_dev, query_width)
        )
        row_count = lax.axis_size("shard") * seq_dev
        key_part = (
            jnp.einsum(
                "krst,skrd->tkd", scores_grad, query_group, preferred_element_type=jnp.float32
            )
            * score_scale
        )
        value_part = jnp.einsum(
            "krst,skrd->tkd", probs_low, attended_group, preferred_element_type=jnp.float32
        )
        kv_grad = lax.psum_scatter(
            jnp.concatenate(
                [key_part.reshape(row_count, kv_width), value_part.reshape(row_count, kv_width)], 1
            ).astype(jnp.bfloat16),
            "shard",
            scatter_dimension=0,
            tiled=True,
        ).astype(jnp.float32)
        key_grad = (
            unrotate(kv_grad[:, :kv_width].reshape(seq_dev, KVH, HD), cosine_table, sine_table)
            .astype(jnp.bfloat16)
            .reshape(seq_dev, kv_width)
        )
        value_grad = kv_grad[:, kv_width:].astype(jnp.bfloat16)
        first_grad = jnp.einsum(
            "sq,qd->sd", query_grad, query_full, preferred_element_type=jnp.float32
        )
        first_grad = first_grad + jnp.einsum(
            "sq,qd->sd", key_grad, key_full, preferred_element_type=jnp.float32
        )
        first_grad = first_grad + jnp.einsum(
            "sq,qd->sd", value_grad, value_full, preferred_element_type=jnp.float32
        )
        source_part, prenorm_part = norm_backward(source, inverse_first, prenorm_f, first_grad)
        input_rows.append((middle_grad + source_part).astype(jnp.bfloat16))
        prenorm_total = prenorm_total + prenorm_part
        saved = (normed_first, query_grad, key_grad, value_grad, attended, branch_grad)
        weight_term, shard_rows = weight_terms(*saved, shard_count)
        reduced = lax.psum_scatter(
            weight_term(jnp.int32(0), lax.axis_size("shard") * shard_rows).astype(jnp.bfloat16),
            "shard",
            scatter_dimension=0,
            tiled=True,
        ).astype(jnp.float32)
        attn_total = reduced if attn_total is None else attn_total + reduced
    gain_sums = lax.psum((prenorm_total, midnorm_total), ("grp", "shard"))
    gain_share = model_width // shard_count
    prenorm_gradient = lax.dynamic_slice_in_dim(
        gain_sums[0], shard_rank * gain_share, gain_share, 0
    )
    midnorm_gradient = lax.dynamic_slice_in_dim(
        gain_sums[1], shard_rank * gain_share, gain_share, 0
    )
    summed = (
        lax.psum(attn_total.astype(jnp.bfloat16), "grp").astype(jnp.float32),
        lax.psum(gate_total.astype(jnp.bfloat16), "grp").astype(jnp.float32),
        lax.psum(up_total.astype(jnp.bfloat16), "grp").astype(jnp.float32),
        lax.psum(down_total.astype(jnp.bfloat16), "grp").astype(jnp.float32),
    )
    attn_rows = summed[0]
    query_share = query_width // shard_count
    kv_share = kv_width // shard_count
    query_gradient = attn_rows[:query_share]
    key_gradient = attn_rows[query_share : query_share + kv_share]
    value_gradient = attn_rows[query_share + kv_share : query_share + 2 * kv_share]
    out_gradient = attn_rows[query_share + 2 * kv_share :]
    return (
        jnp.stack(mixed_rows),
        jnp.stack(input_rows),
        prenorm_gradient,
        query_gradient,
        key_gradient,
        value_gradient,
        out_gradient,
        midnorm_gradient,
        summed[1],
        summed[2],
        summed[3],
    )


def local_heads(
    tokens,
    lengths,
    prenorm_gain,
    query_weight,
    key_weight,
    value_weight,
    out_weight,
    midnorm_gain,
    gate_weight,
    up_weight,
    down_weight,
    cotangent,
):
    low = jnp.bfloat16
    count = lax.axis_size("shard")
    groups = lax.axis_size("grp")
    seqs, seq_dev, model_width = tokens.shape
    rows = seqs * seq_dev
    inverse_freq = jnp.asarray(theta_base ** (-np.arange(0, HD, 2) / HD), jnp.float32)
    tokens_low = tokens.reshape(rows, model_width)
    cot_low = cotangent.reshape(rows, model_width)
    branch, gains, normed_first, cot_all, queries, keys, values, attended, kv_head, cosine, sine = (
        attention(
            lengths,
            tokens_low,
            cot_low,
            prenorm_gain,
            midnorm_gain,
            inverse_freq[None, :],
            query_weight,
            key_weight,
            value_weight,
            out_weight,
            count,
            groups,
            1,
        )
    )
    second_grad, ffn_parts, pair_sums, early = ffn(
        tokens_low, branch, gains, cot_all, gate_weight, up_weight, down_weight, groups, 2
    )
    mixed, input_gradient, gain_own, totals, wide, narrow = attention_grad(
        lengths,
        tokens_low,
        branch,
        cot_low,
        second_grad,
        gains,
        cosine,
        sine,
        ffn_parts,
        normed_first,
        attended,
        queries,
        keys,
        values,
        query_weight,
        kv_head,
        out_weight,
        pair_sums,
        early,
        groups,
        3,
    )
    f32 = jnp.float32
    return (
        mixed.reshape(tokens.shape),
        input_gradient.reshape(tokens.shape),
        gain_own[0],
        wide[1].astype(f32),
        narrow[0].astype(f32),
        narrow[1].astype(f32),
        wide[0].astype(f32),
        gain_own[1],
        totals[1].astype(f32),
        totals[2].astype(f32),
        totals[0].astype(f32),
    )


def solution(mesh):
    planes = mesh.shape["shard"] == NH and mesh.shape["grp"] == 4
    local = local_heads if planes else local_rows
    in_specs = (
        P("grp", "shard", None),
        P("grp"),
        P("shard"),
        P("shard", None),
        P("shard", None),
        P("shard", None),
        P("shard", None),
        P("shard"),
        P("shard", None),
        P("shard", None),
        P("shard", None),
        P("grp", "shard", None),
    )
    out_specs = (
        P("grp", "shard", None),
        P("grp", "shard", None),
        P("shard"),
        P("shard", None),
        P("shard", None),
        P("shard", None),
        P("shard", None),
        P("shard"),
        P("shard", None),
        P("shard", None),
        P("shard", None),
    )
    return jax.shard_map(local, mesh=mesh, in_specs=in_specs, out_specs=out_specs, check_vma=False)
```

```python
import functools
import math

import jax
import jax.numpy as jnp
from jax import lax
from jax.experimental import pallas as pl
from jax.experimental.pallas import tpu as pltpu
from jax.sharding import PartitionSpec as P
import numpy as np

NH = 8
KVH = 4
HD = 256
MASKED = -1e30
EPSILON = 1e-06
DEPTH = 2
MESH = pl.DeviceIdType.MESH
F32 = jnp.float32
DMA = pltpu.SemaphoreType.DMA
REST = 16
PIECE = 128
EARLY = 3
CHUNKS = 2


def pieces(rows, rest=REST):
    size = -(-(rows - rest) // (16 * CHUNKS)) * 16
    cuts = [min(i * size, rows - rest) for i in range(CHUNKS + 1)] + [rows]
    return [pl.ds(a, b - a) for a, b in zip(cuts, cuts[1:])]


VMEM_LIMIT = 66_000_000


def either(condition, action):
    pl.when(condition)(action)


def total_into(dst, *srcs):
    step = 16

    @pl.loop(0, dst.shape[0] // step)
    def _(i):
        at = pl.ds(pl.multiple_of(i * step, step), step)
        value = srcs[0][at].astype(F32)
        for src in srcs[1:]:
            value = value + src[at].astype(F32)
        dst[at] = value.astype(dst.dtype)


class Place:
    def __init__(self, line):
        self.line = line
        self.me = lax.axis_index("shard")
        self.z = self.me // 2
        self.y = lax.rem(self.me, 2)
        self.cross = self.me + 1 - 2 * self.y
        self.low_end = self.z == 0
        self.high_end = self.z == line - 1
        near = []
        for z in range(line):
            order = [z]
            for k in range(1, line):
                order += [d for d in (z - k, z + k) if 0 <= d < line]
            near.append(order)
        self.tables = near

    def near(self, i):
        out = jnp.int32(0)
        for z in range(self.line):
            row = jnp.int32(self.tables[z][0])
            for k in range(1, self.line):
                row = jnp.where(i == k, self.tables[z][k], row)
            out = jnp.where(self.z == z, row, out)
        return out

    def far(self, i):
        return self.near(self.line - 1 - i)

    def greet(self, groups):
        self.arrive(groups)
        self.meet(groups)

    def meet(self, groups):
        pl.semaphore_wait(pltpu.get_barrier_semaphore(), 2 * self.line + groups - 2)

    def arrive(self, groups):
        barrier = pltpu.get_barrier_semaphore()
        count = 2 * self.line
        rank = lax.axis_index("grp")
        for step in range(1, count):
            pl.semaphore_signal(
                barrier,
                inc=1,
                device_id={"shard": lax.rem(self.me + step, count)},
                device_id_type=MESH,
            )
        for step in range(1, groups):
            pl.semaphore_signal(
                barrier,
                inc=1,
                device_id={"grp": lax.rem(rank + step, groups)},
                device_id_type=MESH,
            )


    def arrive_near(self, ranks):
        barrier = pltpu.get_barrier_semaphore()

        def signal(**peer):
            pl.semaphore_signal(barrier, inc=1, device_id=peer, device_id_type=MESH)

        signal(shard=self.cross)
        either(self.z > 0, lambda: signal(shard=self.me - 2))
        either(self.z < self.line - 1, lambda: signal(shard=self.me + 2))
        for rank in ranks:
            signal(grp=rank)

    def meet_near(self, ranks):
        ends = jnp.where(self.z > 0, 1, 0) + jnp.where(self.z < self.line - 1, 1, 0)
        pl.semaphore_wait(pltpu.get_barrier_semaphore(), 1 + len(ranks) + ends)


class Gather:
    UP, DOWN, CROSS = 0, 1, 2

    def __init__(self, place, own, out, local_sem, send_sem, recv_sem, rest=REST):
        self.p, self.own, self.out = place, own, out
        self.local_sem, self.send_sem, self.recv_sem = local_sem, send_sem, recv_sem
        self.pieces = pieces(own.shape[0], rest)
        self.last = len(self.pieces) - 1

    def copy(self, way, origin, part, own=False):
        p = self.p
        peer = (p.me + 2, p.me - 2, p.cross)[way]
        at = self.pieces[part]
        return pltpu.make_async_remote_copy(
            src_ref=self.own.at[at] if own else self.out.at[origin, at],
            dst_ref=self.out.at[origin, at],
            send_sem=self.send_sem.at[way, origin, part],
            recv_sem=self.recv_sem.at[origin, part],
            device_id={"shard": peer},
            device_id_type=MESH,
        )

    def arrived(self, origin, part):
        self.copy(self.CROSS, origin, part).wait_recv()

    def start(self):
        self.send_own()
        self.pass_rest()

    def send_own(self):
        p = self.p
        pltpu.make_async_copy(self.own, self.out.at[p.me], self.local_sem).start()
        for part in (self.last,) + tuple(range(self.last)):
            self.copy(self.CROSS, p.me, part, True).start()
        for part in range(self.last + 1):
            either(p.z < p.line - 1, lambda: self.copy(self.UP, p.me, part, True).start())
            either(p.z > 0, lambda: self.copy(self.DOWN, p.me, part, True).start())

    def pass_rest(self):
        p = self.p
        self.arrived(p.cross, self.last)
        either(p.z < p.line - 1, lambda: self.copy(self.UP, p.cross, self.last).start())
        either(p.z > 0, lambda: self.copy(self.DOWN, p.cross, self.last).start())
        pltpu.make_async_copy(self.own, self.out.at[p.me], self.local_sem).wait()

    def hop(self, k):
        p = self.p
        below, above = p.me - 2 * k, p.me + 2 * k
        has_below, has_above = p.z - k >= 0, p.z + k < p.line

        def first(origin, part, way, more):
            self.arrived(origin, part)
            self.copy(self.CROSS, origin, part).start()
            either(more, lambda: self.copy(way, origin, part).start())

        def last(origin, other, way, more):
            for block in (origin, other):
                self.arrived(block, self.last)
                either(more, lambda: self.copy(way, block, self.last).start())

        for part in range(self.last):
            either(has_below, lambda: first(below, part, self.UP, p.z < p.line - 1))
            either(has_above, lambda: first(above, part, self.DOWN, p.z > 0))
        either(has_below, lambda: last(below, p.cross - 2 * k, self.UP, p.z < p.line - 1))
        either(has_above, lambda: last(above, p.cross + 2 * k, self.DOWN, p.z > 0))

    def whole(self, position):
        for part in range(self.last):
            self.arrived(2 * position + 1 - self.p.y, part)

    def drain(self):
        p = self.p

        @pl.loop(0, p.line)
        def _(d):
            mine, other = 2 * d + p.y, 2 * d + 1 - p.y
            for part in range(self.last):
                self.copy(self.CROSS, mine, part).wait_send()

            @pl.when(d == p.z)
            def _():
                self.copy(self.CROSS, mine, self.last).wait_send()

            def line_sent(way):
                for part in range(self.last + 1):
                    self.copy(way, mine, part).wait_send()
                self.copy(way, other, self.last).wait_send()

            either((d <= p.z) & (p.z < p.line - 1), lambda: line_sent(self.UP))
            either((d >= p.z) & (p.z > 0), lambda: line_sent(self.DOWN))


class Reduce:
    BUP, BDN, BX = 0, 2, 4
    UP, DOWN, CROSS = 5, 5 + CHUNKS, 5 + 2 * CHUNKS
    WAYS = 5 + 3 * CHUNKS
    N_SCRATCH = 9

    @staticmethod
    def scratch(line, rows, width, dtype):
        v = pltpu.VMEM
        return (
            [v((line, rows - REST, width), dtype)] * 3
            + [v((line, 2, REST, width), dtype)] * 2
            + [v((REST, width), dtype)] * 2
            + [DMA((Reduce.WAYS, line)), DMA((Reduce.WAYS, line))]
        )

    def __init__(self, place, parts, out, scratch):
        self.p, self.parts, self.out = place, parts, out
        self.cross_in, self.up_in, self.down_in, self.bup_in, self.bdn_in = scratch[:5]
        self.bx_out, self.bx_in, self.send_sem, self.recv_sem = scratch[5:]
        self.pieces = pieces(parts.shape[1])
        self.b = self.pieces[-1]

    def desc(self, way, slot, src, dst, peer):
        return pltpu.make_async_remote_copy(
            src_ref=src,
            dst_ref=dst,
            send_sem=self.send_sem.at[way, slot],
            recv_sem=self.recv_sem.at[way, slot],
            device_id={"shard": peer},
            device_id_type=MESH,
        )

    def cross_copy(self, d, c):
        p, at = self.p, self.pieces[c]
        return self.desc(
            self.CROSS + c,
            d,
            self.parts.at[2 * d + 1 - p.y, at],
            self.cross_in.at[d, at],
            p.cross,
        )

    def line_copy(self, up, d, c):
        p, at = self.p, self.pieces[c]
        came = self.up_in if up else self.down_in
        return self.desc(
            (self.UP if up else self.DOWN) + c,
            d,
            self.cross_in.at[d, at],
            came.at[d, at],
            p.me + 2 if up else p.me - 2,
        )

    def b_copy(self, up, d, o, src=None):
        p = self.p
        held = self.bup_in if up else self.bdn_in
        return self.desc(
            (self.BUP if up else self.BDN) + o,
            d,
            held.at[d, o] if src is None else src,
            held.at[d, o],
            p.me + 2 if up else p.me - 2,
        )

    def bx_copy(self):
        return self.desc(self.BX, 0, self.bx_out, self.bx_in, self.p.cross)

    def column(self, o):
        return self.p.y if o == 0 else 1 - self.p.y

    def send_across(self, i):
        for c in range(CHUNKS):
            self.cross_copy(self.p.far(i), c).start()

    def b_hop(self, i):
        p = self.p
        d = p.far(i)

        def go(up):
            first = p.low_end if up else p.high_end
            held = self.bup_in if up else self.bdn_in
            for o in (1, 0):
                mine = self.parts.at[2 * d + self.column(o), self.b]
                either(first, lambda: self.b_copy(up, d, o, mine).start())

                @pl.when(jnp.logical_not(first))
                def _():
                    self.b_copy(up, d, o).wait_recv()
                    total_into(held.at[d, o], mine, held.at[d, o])
                    self.b_copy(up, d, o).start()

        either(d > p.z, lambda: go(True))
        either(d < p.z, lambda: go(False))

    def hop(self, i):
        for c in range(CHUNKS):
            self.step(i, c)

    def step(self, i, c):
        p = self.p
        d = p.far(i)
        self.cross_copy(d, c).wait_recv()
        at = self.pieces[c]
        mine = self.parts.at[2 * d + p.y, at]
        held = self.cross_in.at[d, at]

        def go(up):
            first = p.low_end if up else p.high_end
            came = self.up_in if up else self.down_in
            either(first, lambda: total_into(held, mine, held))

            @pl.when(jnp.logical_not(first))
            def _():
                self.line_copy(up, d, c).wait_recv()
                total_into(held, mine, held, came.at[d, at])

            self.line_copy(up, d, c).start()

        either(d > p.z, lambda: go(True))
        either(d < p.z, lambda: go(False))

    def close(self, dst, mine, ups, downs):
        p = self.p
        either(p.low_end, lambda: total_into(dst, *mine, downs))
        either(p.high_end, lambda: total_into(dst, *mine, ups))
        either(
            jnp.logical_not(p.low_end | p.high_end), lambda: total_into(dst, *mine, ups, downs)
        )

    def finish(self):
        p = self.p
        for o in (1, 0):
            either(jnp.logical_not(p.low_end), lambda: self.b_copy(True, p.z, o).wait_recv())
            either(jnp.logical_not(p.high_end), lambda: self.b_copy(False, p.z, o).wait_recv())
            if o:
                mine = self.parts.at[2 * p.z + self.column(o), self.b]
                self.close(self.bx_out, (mine,), self.bup_in.at[p.z, o], self.bdn_in.at[p.z, o])
                self.bx_copy().start()
        self.bx_copy().wait_recv()
        self.close(
            self.out.at[self.b],
            (self.parts.at[p.me, self.b], self.bx_in),
            self.bup_in.at[p.z, 0],
            self.bdn_in.at[p.z, 0],
        )
        for c in range(CHUNKS):
            self.cross_copy(p.z, c).wait_recv()
            either(jnp.logical_not(p.low_end), lambda: self.line_copy(True, p.z, c).wait_recv())
            either(jnp.logical_not(p.high_end), lambda: self.line_copy(False, p.z, c).wait_recv())
            at = self.pieces[c]
            self.close(
                self.out.at[at],
                (self.parts.at[p.me, at], self.cross_in.at[p.z, at]),
                self.up_in.at[p.z, at],
                self.down_in.at[p.z, at],
            )

    def drain(self):
        p = self.p
        self.bx_copy().wait_send()

        @pl.loop(0, p.line)
        def _(d):
            def line_sent(up):
                for c in range(CHUNKS):
                    self.line_copy(up, d, c).wait_send()
                self.b_copy(up, d, 0).wait_send()
                self.b_copy(up, d, 1).wait_send()

            for c in range(CHUNKS):
                self.cross_copy(d, c).wait_send()
            either(d > p.z, lambda: line_sent(True))
            either(d < p.z, lambda: line_sent(False))


def dot(a, b):
    return jnp.dot(a, b, preferred_element_type=F32)


def dot_t(a, b):
    return lax.dot_general(a, b, (((1,), (1,)), ((), ())), preferred_element_type=F32)


def t_dot(a, b):
    return lax.dot_general(a, b, (((0,), (0,)), ((), ())), preferred_element_type=F32)


def to_peer(axis, peer, src, dst, send_sem, recv_sem):
    return pltpu.make_async_remote_copy(
        src_ref=src,
        dst_ref=dst,
        send_sem=send_sem,
        recv_sem=recv_sem,
        device_id={axis: peer},
        device_id_type=MESH,
    )


def turn_by(v, cosine, sine):
    half = v.shape[-1] // 2
    a, b = v[:, :half], v[:, half:]
    return jnp.concatenate([a * cosine - b * sine, b * cosine + a * sine], -1)


def turn_back(v, cosine, sine):
    return turn_by(v, cosine, -sine)


def probabilities(query, keys, rows_from, limit):
    scores = dot_t(query, keys) * (1.0 / math.sqrt(HD))
    row = lax.broadcasted_iota(jnp.int32, scores.shape, 0) + rows_from
    col = lax.broadcasted_iota(jnp.int32, scores.shape, 1)
    scores = jnp.where((col <= row) & (col < limit), scores, MASKED)
    weight = jnp.exp(scores - jnp.max(scores, -1, keepdims=True))
    return weight / jnp.sum(weight, -1, keepdims=True)


def row_valid(place, lengths, rows):
    slots = rows // lengths.shape[0]
    row = lax.broadcasted_iota(jnp.int32, (rows, 1), 0)
    limit = jnp.full((rows, 1), lengths[0], jnp.int32)
    for n in range(1, lengths.shape[0]):
        limit = jnp.where(row >= n * slots, lengths[n], limit)
    return place.me * slots + lax.rem(row, slots) < limit


def gain_row(shares, which):
    return jnp.concatenate([shares[b, which : which + 1] for b in range(shares.shape[0])], 1)


def inverse_rms(x):
    return lax.rsqrt(jnp.mean(x * x, -1, keepdims=True) + EPSILON)


def norm_grad(x, inverse, gain, grad):
    weighted = grad * gain
    inner = jnp.sum(weighted * x, -1, keepdims=True)
    return inverse * weighted - x * inverse * inverse * inverse * inner / x.shape[-1]


def start_all(copies):
    for c in copies:
        c.start()


def wait_all(copies):
    for c in copies:
        c.wait()


def scalars():
    return pl.BlockSpec(memory_space=pltpu.SMEM)


def hbm():
    return pl.BlockSpec(memory_space=pl.ANY)


def vm():
    return pl.BlockSpec(memory_space=pltpu.VMEM)


def params(ident):
    return pltpu.CompilerParams(
        collective_id=ident, has_side_effects=True, vmem_limit_bytes=VMEM_LIMIT
    )


def gather_sems(count):
    return [DMA, DMA((3, count, CHUNKS + 1)), DMA((count, CHUNKS + 1))]


def attention_kernel(
    line, groups, seqs,
    lengths, own, cot_raw, pre_gain, mid_gain, freq, wq_hbm, wk_hbm, wv_hbm, wo_hbm,
    branch, small_out, normed_hbm, cot_hbm, q_hbm, k_hbm, v_hbm, attended_hbm, wkv_hbm, cos_hbm, sin_hbm,
    small, cot_own, rows_all, normed, cot_all, q, k, v, attended, wq, wkv, wo, cosine, sine, parts,
    *scratch,
):
    p = Place(line)
    count = 2 * line
    rank = lax.axis_index("grp")
    g1, g2 = scratch[:3], scratch[3:6]
    (load_sem, small_send, small_recv, wy_send, wg_send, w_recv, save_sem) = scratch[6:13]
    r_scratch = scratch[13:]
    half = wk_hbm.shape[0]
    piece = half // 2
    at_own = pl.ds(pl.multiple_of(p.y * half, half), half)
    loads = [
        pltpu.make_async_copy(src, dst, load_sem.at[i])
        for i, (src, dst) in enumerate(
            (
                (wk_hbm, wkv.at[0, at_own]),
                (wv_hbm, wkv.at[1, at_own]),
                (wq_hbm, wq),
                (wo_hbm, wo),
            )
        )
    ]
    p.arrive(groups)
    start_all(loads)

    small[...] = jnp.zeros_like(small)
    small[0:1] = pre_gain[...].astype(F32)[None, :]
    small[1:2] = mid_gain[...].astype(F32)[None, :]
    p.meet(groups)

    def small_copy(step, peer, origin):
        return to_peer(
            "shard", peer, small, small_out.at[origin], small_send.at[step], small_recv.at[step]
        )

    for step in range(1, count):
        small_copy(step, lax.rem(p.me + step, count), p.me).start()
    gather = Gather(p, own, rows_all, *g1, rest=2 * REST)
    gather.start()
    cots = Gather(p, cot_own, cot_all, *g2)
    small_out[p.me] = small[...]

    def rows_of(quarter, column):
        return wkv.at[
            quarter // 2,
            pl.ds(pl.multiple_of(column * half + lax.rem(quarter, 2) * piece, piece), piece),
        ]

    def across():
        ref = rows_of(rank, p.y)
        return to_peer("shard", p.cross, ref, ref, wy_send, w_recv.at[rank])

    def share(step):
        ref = rows_of(rank, 1 - p.y)
        return to_peer(
            "grp", lax.rem(rank + step, groups), ref, ref, wg_send.at[step], w_recv.at[rank]
        )

    wait_all(loads)
    across().start()
    pos = lax.broadcasted_iota(jnp.int32, cosine.shape, 0).astype(F32)
    angle = pos * freq[...]
    cosine[...] = jnp.cos(angle)
    sine[...] = jnp.sin(angle)
    cot = cot_raw[...]
    cot_own[...] = jnp.where(row_valid(p, lengths, cot.shape[0]), cot, jnp.zeros_like(cot))
    gather.hop(1)
    for step in range(1, count):
        small_copy(step, p.me, lax.rem(p.me + count - step, count)).wait_recv()
    gain = gain_row(small_out, 0)
    across().wait_recv()
    for step in range(1, groups):
        share(step).start()
    rows = own.shape[0]
    pair = 2 * rows
    slots = rows // seqs
    low = own.dtype
    for step in range(1, groups):
        quarter = lax.rem(rank + step, groups)
        ref = rows_of(quarter, 1 - p.y)
        to_peer("grp", rank, ref, ref, wg_send.at[step], w_recv.at[quarter]).wait_recv()

    @pl.loop(0, line)
    def _(i):
        d = p.near(i)
        gather.whole(d)
        x = rows_all[pl.ds(2 * d, 2)].reshape(pair, -1).astype(F32)
        n = (x * inverse_rms(x) * gain).astype(low)
        normed[pl.ds(2 * d, 2)] = n.reshape(2, rows, -1)
        at = pl.ds(pl.multiple_of(d * 2 * slots, 2 * slots), 2 * slots)
        c, s = cosine[at], sine[at]

        def by_rows(t):
            return jnp.concatenate([t[:slots]] * seqs + [t[slots:]] * seqs, 0)

        c, s = by_rows(c), by_rows(s)

        def put(target, value):
            for block in range(2):
                for m in range(seqs):
                    to = pl.ds(
                        pl.multiple_of(d * 2 * slots + block * slots, slots), slots
                    )
                    target[m, to] = value[block * rows + m * slots : block * rows + (m + 1) * slots]

        put(q, turn_by(dot_t(n, wq[...]), c, s).astype(low))
        put(k, turn_by(dot_t(n, wkv[0]), c, s).astype(low))
        put(v, dot_t(n, wkv[1]).astype(low))
        gather.hop(i + 2)
        either(i == line - 3, cots.send_own)

    saves = [
        pltpu.make_async_copy(src, dst, save_sem.at[i])
        for i, (src, dst) in enumerate(
            (
                (normed, normed_hbm),
                (q, q_hbm),
                (k, k_hbm),
                (v, v_hbm),
                (wkv, wkv_hbm),
                (cosine, cos_hbm),
                (sine, sin_hbm),
            )
        )
    ]
    start_all(saves)
    cots.pass_rest()
    total_slots = q.shape[1]
    tile = min(256, total_slots)

    @pl.loop(0, seqs)
    def _(n):
        for t in range(total_slots // tile):
            span = (t + 1) * tile
            at = pl.ds(t * tile, tile)
            probs = probabilities(q[n, at], k[n, pl.ds(0, span)], t * tile, lengths[n])
            out = dot(probs.astype(low), v[n, pl.ds(0, span)]).astype(low)
            for c in range(tile // slots):
                b = (t * tile) // slots + c
                attended[pl.ds(pl.multiple_of(b * rows + n * slots, slots), slots)] = out[
                    c * slots : (c + 1) * slots
                ]
        cots.hop(n + 1)

    for h in range(seqs + 1, line):
        cots.hop(h)

    @pl.loop(0, line)
    def _(d):
        at = pl.ds(pl.multiple_of(d * pair, pair), pair)
        parts[pl.ds(2 * d, 2)] = dot(attended[at], wo[...]).astype(low).reshape(2, rows, -1)

    reduce = Reduce(p, parts, branch, r_scratch)
    saves2 = [pltpu.make_async_copy(attended, attended_hbm, save_sem.at[7])]
    start_all(saves2)
    for d in range(line):
        cots.whole(d)
    for i in range(DEPTH):
        reduce.send_across(i)
    saves3 = [pltpu.make_async_copy(cot_all, cot_hbm, save_sem.at[8])]
    start_all(saves3)
    for i in range(line - 1):
        reduce.b_hop(i)
    for i in range(line - 1):
        reduce.hop(i)
        if i + DEPTH < line:
            reduce.send_across(i + DEPTH)
    reduce.finish()
    reduce.drain()
    gather.drain()
    cots.drain()
    wait_all(saves + saves2 + saves3)
    across().wait_send()
    for step in range(1, groups):
        share(step).wait_send()
    for step in range(1, count):
        small_copy(step, lax.rem(p.me + step, count), p.me).wait_send()


def attention(lengths, own, cot, pre_gain, mid_gain, freq, wq, wk, wv, wo, count, groups, ident):
    rows, width = own.shape
    seqs = lengths.shape[0]
    total_slots = count * rows // seqs
    small = (8, pre_gain.shape[0])
    line = count // 2
    low = own.dtype
    v = pltpu.VMEM
    shape = jax.ShapeDtypeStruct
    hd = wq.shape[0]
    big = (count, rows, width)
    head = (seqs, total_slots, hd)
    table = (total_slots, hd // 2)
    flat = (count * rows, hd)
    return pl.pallas_call(
        functools.partial(attention_kernel, line, groups, seqs),
        out_shape=(
            shape((rows, width), F32),
            shape((count,) + small, F32),
            shape(big, low),
            shape(big, low),
            shape(head, low),
            shape(head, low),
            shape(head, low),
            shape(flat, low),
            shape((2, hd, width), low),
            shape(table, F32),
            shape(table, F32),
        ),
        in_specs=[scalars()] + [vm()] * 5 + [hbm()] * 4,
        out_specs=(vm(), vm()) + (hbm(),) * 9,
        scratch_shapes=[
            v(small, F32), v((rows, width), low), v(big, low), v(big, low), v(big, low), v(head, low), v(head, low), v(head, low), v(flat, low),
            v((hd, width), low), v((2, hd, width), low), v((hd, width), low), v(table, F32), v(table, F32), v(big, low),
        ]
        + gather_sems(count) * 2
        + [DMA((4,)), DMA((count,)), DMA((count,)), DMA, DMA((groups,)), DMA((groups,)), DMA((9,))]
        + Reduce.scratch(line, rows, width, low),
        compiler_params=params(ident),
        name="attention",
    )(lengths, own, cot, pre_gain, mid_gain, freq, wq, wk, wv, wo)


def ffn_kernel(
    line, groups,
    tokens, branch, gains, cot_hbm, gate_hbm, up_hbm, down_hbm,
    second, ffn_hbm, pair_hbm, chip_in,
    own, rights, gate_up, down_w, lefts, parts, stage, theirs,
    *scratch,
):
    p = Place(line)
    rank = lax.axis_index("grp")
    core = lax.rem(rank, 2)
    partner = rank + 1 - 2 * core
    opposite = lax.rem(rank + 2, groups)
    (load_sem, out_sem, stage_send, stage_recv, chip_send, chip_recv) = scratch[3:9]
    units = down_w.shape[0]
    gate_w, up_w = gate_up.at[pl.ds(0, units)], gate_up.at[pl.ds(units, units)]
    cot, normed = rights.at[0], rights.at[1]
    hidden, gate_g, up_g = lefts.at[0], lefts.at[1], lefts.at[2]
    loads = [
        pltpu.make_async_copy(src, dst, load_sem.at[i])
        for i, (src, dst) in enumerate(
            ((cot_hbm, cot), (down_hbm, down_w), (gate_hbm, gate_w), (up_hbm, up_w))
        )
    ]
    p.arrive_near((partner, opposite))
    start_all(loads)
    middle = tokens[...].astype(F32) + branch[...]
    own[...] = (middle * inverse_rms(middle) * gain_row(gains, 1)).astype(own.dtype)
    p.meet_near((partner, opposite))
    gather = Gather(p, own, normed, *scratch[:3])
    gather.send_own()
    wait_all(loads[:2])
    rows = own.shape[0]
    pair = 2 * rows
    low = own.dtype

    @pl.loop(0, line)
    def _(d):
        at = pl.ds(pl.multiple_of(d * pair, pair), pair)
        gate_g[at] = dot_t(cot[pl.ds(2 * d, 2)].reshape(pair, -1), down_w[...]).astype(low)

    gather.pass_rest()
    wait_all(loads[2:])

    @pl.loop(0, line)
    def _(i):
        gather.hop(i + 1)
        d = p.near(i)
        gather.whole(d)
        x = normed[pl.ds(2 * d, 2)].reshape(pair, -1)
        g = dot_t(x, gate_w[...])
        u = dot_t(x, up_w[...])
        s = 1.0 / (1.0 + jnp.exp(-g))
        silu = g * s
        at = pl.ds(pl.multiple_of(d * pair, pair), pair)
        dh = gate_g[at].astype(F32)
        hidden[at] = (silu * u).astype(low)
        up_g[at] = (dh * silu).astype(low)
        gate_g[at] = (dh * u * s * (1.0 + g * (1.0 - s))).astype(low)
        part = dot(gate_g[at], gate_w[...]) + dot(up_g[at], up_w[...])
        parts[pl.ds(2 * d, 2)] = part.astype(low).reshape(2, rows, -1)

    reduce = Reduce(p, parts, second, scratch[9:])
    for i in range(line):
        reduce.send_across(i)

    quarter = units // 4
    half = units // 2

    def mine(which):
        start = lax.rem(which + 2, 3) * half
        return gate_up.at[pl.ds(pl.multiple_of(start, half), half)]

    def to_partner(which, j):
        return to_peer(
            "grp",
            partner,
            stage.at[j],
            theirs.at[which, pl.ds(pl.multiple_of(j * quarter, quarter), quarter)],
            stage_send.at[j],
            stage_recv.at[which, j],
        )

    def chip_copy():
        return to_peer(
            "grp",
            opposite,
            gate_up.at[pl.ds(2 * half, chip_in.shape[0])],
            chip_in,
            chip_send,
            chip_recv,
        )

    def save_pair(which):
        return pltpu.make_async_copy(mine(which), pair_hbm.at[which], out_sem.at[which])

    def core_sum(which):
        for j in range(2):
            to_partner(which, j).wait_recv()
        total_into(mine(which), mine(which), theirs.at[which])
        save_pair(which).start()

    @pl.loop(0, 3)
    def _(which):
        right = rights.at[jnp.minimum(which, 1)]

        def block(q):
            cols = pl.ds(pl.multiple_of(q * quarter, quarter), quarter)
            left = lefts[which, :, cols]
            return t_dot(left, right[...].reshape(left.shape[0], -1)).astype(low)

        @pl.loop(0, 2)
        def _(j):
            either(which > 0, lambda: to_partner(which - 1, j).wait_send())
            stage[j] = block(2 * (1 - core) + j)
            to_partner(which, j).start()

        @pl.when(which == 0)
        def _():
            for i in range(line - 1):
                reduce.b_hop(i)

        either(which > 1, lambda: core_sum(which - 1))

        at_end = p.low_end | p.high_end
        either(at_end, lambda: reduce.step(which, 0))

        @pl.loop(0, 2)
        def _(j):
            at = pl.ds(pl.multiple_of(j * quarter, quarter), quarter)
            mine(which)[at] = block(2 * core + j)

        @pl.when(at_end)
        def _():
            for c in range(1, CHUNKS):
                reduce.step(which, c)

        @pl.when(which == 0)
        def _():
            core_sum(0)
            chip_copy().start()

        @pl.when(jnp.logical_not(at_end))
        def _():
            for c in range(CHUNKS):
                reduce.step(which, c)

    core_sum(2)
    gather.drain()

    @pl.loop(0, line)
    def _(d):
        at = pl.ds(pl.multiple_of(d * pair, pair), pair)
        normed[pl.ds(2 * d, 2)] = dot(hidden[at], down_w[...]).astype(low).reshape(2, rows, -1)

    ffn_save = pltpu.make_async_copy(normed, ffn_hbm, out_sem.at[3])
    ffn_save.start()
    reduce.finish()
    for j in range(2):
        to_partner(2, j).wait_send()

    reduce.drain()
    chip_copy().wait()
    ffn_save.wait()
    for which in range(3):
        save_pair(which).wait()


def ffn(tokens, branch, gains, cot, gate_w, up_w, down_w, groups, ident):
    rows, width = tokens.shape
    count = cot.shape[0]
    line = count // 2
    units = gate_w.shape[0]
    low = tokens.dtype
    v = pltpu.VMEM
    tall = count * rows
    shape = jax.ShapeDtypeStruct
    big = (count, rows, width)
    half = (units // 2, width)
    return pl.pallas_call(
        functools.partial(ffn_kernel, line, groups),
        out_shape=(
            shape((rows, width), F32),
            shape(big, low),
            shape((3,) + half, low),
            shape((EARLY * PIECE, width), low),
        ),
        in_specs=[vm()] * 3 + [hbm()] * 4,
        out_specs=(vm(), hbm(), hbm(), hbm()),
        scratch_shapes=[v((rows, width), low)]
        + [v((2,) + big, low), v((2 * units, width), low), v((units, width), low)]
        + [v((3, tall, units), low), v(big, low), v((2, units // 4, width), low), v((3,) + half, low)]
        + gather_sems(count)
        + [DMA((4,)), DMA((4,)), DMA((2,)), DMA((3, 2)), DMA, DMA]
        + Reduce.scratch(line, rows, width, low),
        compiler_params=params(ident),
        name="ffn",
    )(tokens, branch, gains, cot, gate_w, up_w, down_w)


def attention_grad_kernel(
    line, groups, seqs,
    lengths, tokens, branch, cot, second, gains, cosine, sine,
    ffn_hbm, normed_hbm, attended_hbm, q_hbm, k_hbm, v_hbm, wq_hbm, wkv_hbm, wo_hbm, sums_hbm, early_hbm,
    mixed, input_grad, gain_out, total_hbm, wide_hbm, narrow_hbm,
    own, middle_grad, first, ffn_own, dbranch, normed, attended, q, k, v, wq, wkv, wo, da, dk_acc, dv_acc, dq_rows, dk_rows, dv_rows,
    halves, half_in, ffn_parts, sums, sums_in, stage, mine, theirs, mine_in, gain_held, gain_in, gain_sum, gain_all,
    *scratch,
):
    p = Place(line)
    count = 2 * line
    rank = lax.axis_index("grp")
    core = lax.rem(rank, 2)
    partner = rank + 1 - 2 * core
    opposite = lax.rem(rank + 2, groups)
    (
        load_sem, chip_send, chip_recv, half_send, half_recv, stage_send, stage_recv,
        back_send, back_recv, keep_sem, ga_send, ga_recv, gb_send, gb_recv,
    ) = scratch[3:17]
    n = Reduce.N_SCRATCH
    loads = [
        pltpu.make_async_copy(src, dst, load_sem.at[i])
        for i, (src, dst) in enumerate(
            (
                (wo_hbm, wo),
                (ffn_hbm, ffn_parts),
                (attended_hbm, attended),
                (q_hbm, q),
                (k_hbm, k),
                (v_hbm, v),
                (wq_hbm, wq),
                (wkv_hbm, wkv),
                (normed_hbm, normed),
                (early_hbm, sums_in.at[pl.ds(0, EARLY)]),
            )
        )
    ]
    p.arrive(groups)
    start_all(loads)

    def load_sum(i):
        return pltpu.make_async_copy(sums_hbm.at[i], sums.at[lax.rem(i, 2)], load_sem.at[10 + lax.rem(i, 2)])

    load_sum(0).start()
    load_sum(1).start()
    middle = tokens[...].astype(F32) + branch[...]
    inverse = inverse_rms(middle)
    grad = cot[...].astype(F32)
    grad = jnp.where(row_valid(p, lengths, grad.shape[0]), grad, jnp.zeros_like(grad))
    grad = grad + norm_grad(middle, inverse, gain_row(gains, 1), second[...])
    middle_grad[...] = grad
    own[...] = grad.astype(own.dtype)
    mid_total = jnp.sum(second[...] * middle * inverse, 0, keepdims=True)
    share = gain_held.shape[2]
    for b in range(count):
        gain_held[b] = jnp.zeros(gain_held.shape[1:], F32)
        gain_held[b, 1:2] = mid_total[:, b * share : (b + 1) * share]
    p.meet(groups)
    gather = Gather(p, own, dbranch, *scratch[:3])
    n_sums = sums_hbm.shape[0]
    part_rows = sums.shape[1]

    def chip_copy(i):
        return to_peer(
            "grp", opposite, sums_hbm.at[i], sums_in.at[i], chip_send.at[i], chip_recv.at[i]
        )

    gather.start()

    @pl.loop(EARLY, n_sums)
    def _(i):
        chip_copy(i).start()

    wait_all(loads)
    ffn_sum = Reduce(p, ffn_parts, ffn_own, scratch[17 : 17 + n])
    rows = own.shape[0]
    pair = 2 * rows
    slots = rows // seqs
    low = own.dtype
    scale = 1.0 / math.sqrt(HD)

    @pl.loop(0, line)
    def _(i):
        gather.hop(i + 1)

        @pl.when(i == line - 2)
        def _():
            for first_sends in range(DEPTH):
                ffn_sum.send_across(first_sends)

        d = p.near(i)
        gather.whole(d)
        grad = dot_t(dbranch[pl.ds(2 * d, 2)].reshape(pair, -1), wo[...]).astype(low)
        for block in range(2):
            for m in range(seqs):
                at = pl.ds(pl.multiple_of(d * 2 * slots + block * slots, slots), slots)
                da[m, at] = grad[block * rows + m * slots : block * rows + (m + 1) * slots]

    for i in range(line - 1):
        ffn_sum.b_hop(i)

    chunk = stage.shape[1]

    def to_partner(b):
        return to_peer(
            "grp",
            partner,
            stage.at[b // 2],
            theirs.at[pl.ds(b // 2 * chunk, chunk)],
            stage_send.at[b // 2],
            stage_recv.at[b // 2],
        )

    def gradient(b, left, right):
        value = t_dot(left, right[...].reshape(left.shape[0], -1)).astype(low)
        keep = core == b % 2

        @pl.when(keep)
        def _():
            mine[pl.ds(b // 2 * chunk, chunk)] = value

        @pl.when(jnp.logical_not(keep))
        def _():
            stage[b // 2] = value
            to_partner(b).start()

    total_slots = q.shape[1]
    tile = min(256, total_slots)

    def backward(m):
        dk_acc[...] = jnp.zeros_like(dk_acc)
        dv_acc[...] = jnp.zeros_like(dv_acc)

        def to_rows(target, value, start, size):
            for c in range(size // slots):
                b = start // slots + c
                target[pl.ds(pl.multiple_of(b * rows + m * slots, slots), slots)] = value[
                    c * slots : (c + 1) * slots
                ]

        for t in range(total_slots // tile):
            span = (t + 1) * tile
            at = pl.ds(t * tile, tile)
            query, grad = q[m, at], da[m, at]
            keys, values = k[m, pl.ds(0, span)], v[m, pl.ds(0, span)]
            probs = probabilities(query, keys, t * tile, lengths[m])
            dprobs = dot_t(grad, values)
            inner = jnp.sum(probs * dprobs, -1, keepdims=True)
            dscores = (probs * (dprobs - inner)).astype(low)
            dq = turn_back(dot(dscores, keys) * scale, cosine[at], sine[at])
            to_rows(dq_rows, dq.astype(low), t * tile, tile)
            dk_acc[pl.ds(0, span)] += t_dot(dscores, query)
            dv_acc[pl.ds(0, span)] += t_dot(probs.astype(low), grad)
        dk = turn_back(dk_acc[...] * scale, cosine[...], sine[...])
        to_rows(dk_rows, dk.astype(low), 0, total_slots)
        to_rows(dv_rows, dv_acc[...].astype(low), 0, total_slots)

    half = HD // 2

    def swap():
        return to_peer("shard", p.cross, halves.at[1 - p.y], half_in, half_send, half_recv)

    gradient(0, attended[:, :chunk], dbranch)
    gradient(1, attended[:, chunk:], dbranch)

    @pl.loop(0, seqs)
    def _(m):
        backward(m)
        ffn_sum.hop(m)
        ffn_sum.send_across(m + DEPTH)

    for h in range(2):
        halves[h, 0] = dk_rows[:, h * half : (h + 1) * half]
        halves[h, 1] = dv_rows[:, h * half : (h + 1) * half]
    swap().start()
    gather.drain()
    parts = dbranch
    gradient(2, dq_rows[:, :chunk], normed)
    gradient(3, dq_rows[:, chunk:], normed)

    spans = (pl.ds(0, 2 * chunk), pl.ds(2 * chunk, chunk))

    def attn_chip(part):
        return to_peer(
            "grp",
            opposite,
            mine.at[spans[part]],
            mine_in.at[spans[part]],
            chip_send.at[n_sums + part],
            chip_recv.at[n_sums + part],
        )

    def attn_pair(part, blocks):
        for b in blocks:
            to_partner(2 * b).wait_recv()
        at = mine.at[spans[part]]
        total_into(at, at, theirs.at[spans[part]])
        attn_chip(part).start()

    def back_attn(slot):
        if slot < 2:
            out = wide_hbm.at[slot, pl.ds(pl.multiple_of(core * chunk, chunk), chunk)]
        else:
            out = narrow_hbm.at[core]
        at = mine.at[pl.ds(slot * chunk, chunk)]
        n_slot = n_sums + slot
        sems = keep_sem.at[n_slot], back_send.at[n_slot], back_recv.at[n_slot]
        return pltpu.make_async_copy(at, out, sems[0]), to_peer("grp", partner, at, out, *sems[1:])

    def attn_total(part):
        attn_chip(part).wait()
        at = mine.at[spans[part]]
        total_into(at, at, mine_in.at[spans[part]])
        for slot in (0, 1) if part == 0 else (2,):
            start_all(back_attn(slot))


    @pl.loop(0, line)
    def _(d):
        at = pl.ds(pl.multiple_of(d * pair, pair), pair)
        part = dot(dq_rows[at], wq[...]) + dot(dk_rows[at], wkv[0]) + dot(dv_rows[at], wkv[1])
        parts[pl.ds(2 * d, 2)] = part.astype(low).reshape(2, rows, -1)

    for i in range(seqs, line - 1):
        ffn_sum.hop(i)
    def back(i):
        per_half = n_sums // 3
        start = core * per_half * part_rows + lax.rem(i, per_half) * part_rows
        at = pl.ds(pl.multiple_of(start, part_rows), part_rows)
        out = total_hbm.at[lax.div(i, per_half), at]
        return (
            pltpu.make_async_copy(sums_in.at[i], out, keep_sem.at[i]),
            to_peer("grp", partner, sums_in.at[i], out, back_send.at[i], back_recv.at[i]),
        )

    def sum_up(first_piece, end):
        @pl.loop(first_piece, end)
        def _(i):
            either(i >= EARLY, lambda: chip_copy(i).wait())
            load_sum(i).wait()
            total_into(sums_in.at[i], sums.at[lax.rem(i, 2)], sums_in.at[i])
            either(i + 2 < n_sums, lambda: load_sum(i + 2).start())
            start_all(back(i))

    def gain_copy(step, peer, origin):
        return to_peer(
            "shard", peer, gain_held.at[peer], gain_in.at[origin], ga_send.at[step], ga_recv.at[step]
        )

    def gain_group(step, peer, origin):
        return to_peer(
            "grp", peer, gain_sum, gain_all.at[origin], gb_send.at[step], gb_recv.at[step]
        )

    def gain_first():
        def body(i, total):
            at = pl.ds(pl.multiple_of(i * 16, 16), 16)
            for b in range(count):
                total = total + parts[b, at].astype(F32) * normed[b, at].astype(F32)
            return total

        total = lax.fori_loop(0, rows // 16, body, jnp.zeros((16, parts.shape[2]), F32))
        total = jnp.sum(total, 0, keepdims=True) / gain_row(gains, 0)
        for b in range(count):
            gain_held[b, 0:1] = total[:, b * share : (b + 1) * share]
        for step in range(1, count):
            gain_copy(step, lax.rem(p.me + step, count), p.me).start()

    def gain_second():
        for step in range(1, count):
            gain_copy(step, p.me, lax.rem(p.me + count - step, count)).wait_recv()
        gain_in[p.me] = gain_held[p.me]
        total = gain_in[0]
        for b in range(1, count):
            total = total + gain_in[b]
        gain_sum[...] = total
        gain_all[rank] = total
        for step in range(1, groups):
            gain_group(step, lax.rem(rank + step, groups), rank).start()

    gain_first()
    sum_up(0, n_sums // 3)
    attn_pair(0, (0, 1))
    ffn_sum.finish()
    reduce = Reduce(p, parts, first, scratch[17 + n :])
    for i in range(DEPTH):
        reduce.send_across(i)
    for i in range(line - 1):
        reduce.b_hop(i)

    def summed(which):
        return (halves[p.y, which].astype(F32) + half_in[which].astype(F32)).astype(low)

    valid = row_valid(p, lengths, rows)
    result = tokens[...].astype(F32) + branch[...] + ffn_own[...]
    mixed[...] = jnp.where(valid, result, jnp.zeros_like(result)).astype(low)

    swap().wait_recv()
    gradient(4, summed(0), normed)
    gradient(5, summed(1), normed)
    reduce.hop(0)
    reduce.send_across(DEPTH)
    sum_up(n_sums // 3, n_sums // 2)
    attn_pair(1, (2,))
    reduce.hop(1)
    reduce.send_across(DEPTH + 1)
    gain_second()
    sum_up(n_sums // 2, n_sums - 3)
    reduce.hop(2)
    sum_up(n_sums - 3, n_sums)
    attn_total(0)
    reduce.finish()
    attn_total(1)
    for step in range(1, groups):
        gain_group(step, rank, lax.rem(rank + groups - step, groups)).wait_recv()
    total = gain_all[0]
    for b in range(1, groups):
        total = total + gain_all[b]
    gain_out[...] = total
    source = tokens[...].astype(F32)
    inner = norm_grad(source, inverse_rms(source), gain_row(gains, 0), first[...])
    input_grad[...] = (middle_grad[...] + inner).astype(low)
    reduce.drain()
    ffn_sum.drain()
    swap().wait_send()
    for b in range(3):
        to_partner(2 * b).wait_send()
    for step in range(1, count):
        gain_copy(step, lax.rem(p.me + step, count), p.me).wait_send()
    for step in range(1, groups):
        gain_group(step, lax.rem(rank + step, groups), rank).wait_send()

    @pl.loop(0, n_sums)
    def _(i):
        wait_all(back(i))

    for slot in range(3):
        wait_all(back_attn(slot))


def attention_grad(
    lengths, tokens, branch, cot, second, gains, cosine, sine, ffn_parts, normed, attended, q, k, v, wq, wkv, wo, sums, early,
    groups, ident,
):
    rows, width = tokens.shape
    count = normed.shape[0]
    line = count // 2
    seqs, total_slots, hd = q.shape
    low = tokens.dtype
    vmem = pltpu.VMEM
    tall = count * rows
    half = hd // 2
    sums = sums.reshape(-1, PIECE, width)
    early = early.reshape(-1, PIECE, width)
    n_sums, part_rows, _ = sums.shape
    shape = jax.ShapeDtypeStruct
    big = vmem((count, rows, width), low)
    head = vmem((seqs, total_slots, hd), low)
    weight = vmem((hd, width), low)
    flat = vmem((tall, hd), low)
    acc = vmem((total_slots, hd), F32)
    third = vmem((3 * half, width), low)
    g = gains.shape
    block = vmem((rows, width), F32)
    return pl.pallas_call(
        functools.partial(attention_grad_kernel, line, groups, seqs),
        out_shape=(
            shape((rows, width), low),
            shape((rows, width), low),
            shape(g[1:], F32),
            shape((3, n_sums // 3 * 2 * part_rows, width), low),
            shape((2, 2 * half, width), low),
            shape((2, half, width), low),
        ),
        in_specs=[scalars()] + [vm()] * 7 + [hbm()] * 11,
        out_specs=(vm(), vm(), vm(), hbm(), hbm(), hbm()),
        scratch_shapes=[
            vmem((rows, width), low), block, block, block,
            big, big, flat, head, head, head, weight, vmem((2, hd, width), low), weight, head, acc, acc,
            flat, flat, flat,
            vmem((2, 2, tall, half), low), vmem((2, tall, half), low), big,
            vmem((2,) + sums.shape[1:], low), vmem(sums.shape, low), vmem((3, half, width), low), third, third, third,
            vmem(g, F32), vmem(g, F32), vmem(g[1:], F32), vmem((groups,) + g[1:], F32),
        ]
        + gather_sems(count)
        + [
            DMA((12,)), DMA((n_sums + 2,)), DMA((n_sums + 2,)), DMA, DMA, DMA((3,)), DMA((3,)),
            DMA((n_sums + 3,)), DMA((n_sums + 3,)), DMA((n_sums + 3,)),
            DMA((count,)), DMA((count,)), DMA((groups,)), DMA((groups,)),
        ]
        + Reduce.scratch(line, rows, width, low) * 2,
        compiler_params=params(ident),
        name="attention_grad",
    )(
        lengths, tokens, branch, cot, second, gains, cosine, sine, ffn_parts, normed, attended, q, k, v, wq, wkv, wo, sums, early
    )


epsilon = 1e-06
theta_base = 1000042.0
masked_value = -1e30


def turned(source):
    half_width = source.shape[-1] // 2
    return jnp.concatenate([-source[..., half_width:], source[..., :half_width]], -1)


def rotate(source, cosine_table, sine_table):
    return source * cosine_table + turned(source) * sine_table


def unrotate(source, cosine_table, sine_table):
    return source * cosine_table - turned(source) * sine_table


def norm_forward(source, norm_gain):
    inverse = lax.rsqrt(jnp.mean(source * source, -1, keepdims=True) + epsilon)
    return (source * inverse * norm_gain, inverse)


def norm_backward(source, inverse, norm_gain, grad_out):
    weighted = grad_out * norm_gain
    inner_sum = jnp.sum(weighted * source, -1, keepdims=True)
    grad_in = (
        inverse * weighted - source * inverse * inverse * inverse * inner_sum / source.shape[-1]
    )
    return (grad_in, jnp.sum(grad_out * source * inverse, 0))


def weight_terms(normed, query_grad, key_grad, value_grad, attended, branch_grad, shard_count):
    token_count, model_width = normed.shape
    query_share = query_grad.shape[1] // shard_count
    kv_share = key_grad.shape[1] // shard_count
    shard_rows = 2 * query_share + 2 * kv_share

    def weight_term(first_row, row_count):
        blocks = row_count // shard_rows

        def columns(matrix, share_cols):
            return matrix.reshape(token_count, blocks, share_cols)

        part_query = jnp.einsum(
            "tmr,td->mrd",
            columns(query_grad, query_share),
            normed,
            preferred_element_type=jnp.float32,
        )
        part_key = jnp.einsum(
            "tmr,td->mrd", columns(key_grad, kv_share), normed, preferred_element_type=jnp.float32
        )
        part_value = jnp.einsum(
            "tmr,td->mrd", columns(value_grad, kv_share), normed, preferred_element_type=jnp.float32
        )
        part_out = jnp.einsum(
            "tmr,td->mrd",
            columns(attended, query_share),
            branch_grad,
            preferred_element_type=jnp.float32,
        )
        return jnp.concatenate([part_query, part_key, part_value, part_out], 1).reshape(
            row_count, model_width
        )

    return (weight_term, shard_rows)


def local_rows(
    tokens,
    lengths,
    prenorm_gain,
    query_weight,
    key_weight,
    value_weight,
    out_weight,
    midnorm_gain,
    gate_weight,
    up_weight,
    down_weight,
    cotangent,
):
    shard_count = lax.axis_size("shard")
    shard_rank = lax.axis_index("shard")
    micro_count, seq_dev, model_width = tokens.shape
    slot_count = seq_dev * shard_count
    repeat_heads = NH // KVH
    query_width = NH * HD
    kv_width = KVH * HD
    score_scale = 1.0 / math.sqrt(HD)
    local_pos = shard_rank * seq_dev + jnp.arange(seq_dev, dtype=jnp.int32)
    key_pos = jnp.arange(slot_count, dtype=jnp.int32)
    inverse_freq = theta_base ** (-(jnp.arange(0, HD, 2).astype(jnp.float32) / HD))
    angles = local_pos.astype(jnp.float32)[:, None] * inverse_freq[None, :]
    cosine_table = jnp.concatenate([jnp.cos(angles), jnp.cos(angles)], -1)[:, None, :]
    sine_table = jnp.concatenate([jnp.sin(angles), jnp.sin(angles)], -1)[:, None, :]
    gate_total = jnp.zeros(gate_weight.shape, jnp.float32)
    up_total = jnp.zeros(up_weight.shape, jnp.float32)
    down_total = jnp.zeros(down_weight.shape, jnp.float32)
    prenorm_total = jnp.zeros((model_width,), jnp.float32)
    midnorm_total = jnp.zeros((model_width,), jnp.float32)
    attn_total = None
    mixed_rows = []
    input_rows = []
    for micro_index in range(micro_count):
        gathered = (
            lax.all_gather(query_weight, "shard", axis=0, tiled=True),
            lax.all_gather(key_weight, "shard", axis=0, tiled=True),
            lax.all_gather(value_weight, "shard", axis=0, tiled=True),
            lax.all_gather(prenorm_gain, "shard", axis=0, tiled=True),
            lax.all_gather(midnorm_gain, "shard", axis=0, tiled=True),
        )
        query_full, key_full, value_full, prenorm_full, midnorm_full = gathered
        prenorm_f = prenorm_full.astype(jnp.float32)
        midnorm_f = midnorm_full.astype(jnp.float32)
        source = tokens[micro_index].astype(jnp.float32)
        length_now = lengths[micro_index]
        valid_rows = local_pos < length_now
        scaled_first, inverse_first = norm_forward(source, prenorm_f)
        normed_first = scaled_first.astype(jnp.bfloat16)
        query_pre = jnp.einsum(
            "sd,qd->sq", normed_first, query_full, preferred_element_type=jnp.float32
        ).reshape(seq_dev, NH, HD)
        key_pre = jnp.einsum(
            "sd,qd->sq", normed_first, key_full, preferred_element_type=jnp.float32
        ).reshape(seq_dev, KVH, HD)
        value_pre = jnp.einsum(
            "sd,qd->sq", normed_first, value_full, preferred_element_type=jnp.float32
        )
        query_rot = rotate(query_pre, cosine_table, sine_table).astype(jnp.bfloat16)
        key_rot = rotate(key_pre, cosine_table, sine_table).astype(jnp.bfloat16)
        key_value = jnp.concatenate(
            [key_rot.reshape(seq_dev, kv_width), value_pre.astype(jnp.bfloat16)], 1
        )
        kv_all = lax.all_gather(key_value, "shard", axis=0, tiled=True)
        keys_all = kv_all[:, :kv_width].reshape(slot_count, KVH, HD)
        values_all = kv_all[:, kv_width:].reshape(slot_count, KVH, HD)
        query_group = query_rot.reshape(seq_dev, KVH, repeat_heads, HD)
        scores = (
            jnp.einsum("skrd,tkd->krst", query_group, keys_all, preferred_element_type=jnp.float32)
            * score_scale
        )
        allowed = (key_pos[None, :] <= local_pos[:, None]) & (key_pos[None, :] < length_now)
        scores = jnp.where(allowed, scores, masked_value)
        row_max = jnp.max(scores, -1, keepdims=True)
        exp_scores = jnp.exp(scores - row_max)
        attention_probs = exp_scores / jnp.sum(exp_scores, -1, keepdims=True)
        probs_low = attention_probs.astype(jnp.bfloat16)
        attended = (
            jnp.einsum("krst,tkd->skrd", probs_low, values_all, preferred_element_type=jnp.float32)
            .astype(jnp.bfloat16)
            .reshape(seq_dev, query_width)
        )
        branch = jnp.dot(
            attended,
            lax.all_gather(out_weight, "shard", axis=0, tiled=True),
            preferred_element_type=jnp.float32,
        )
        middle = source + branch
        scaled_second, inverse_second = norm_forward(middle, midnorm_f)
        normed_second = scaled_second.astype(jnp.bfloat16)
        normed_all = lax.all_gather(normed_second, "shard", axis=0, tiled=True)
        gate_pre = jnp.einsum(
            "sd,fd->sf", normed_all, gate_weight, preferred_element_type=jnp.float32
        )
        up_pre = jnp.einsum("sd,fd->sf", normed_all, up_weight, preferred_element_type=jnp.float32)
        sigmoid_gate = jax.nn.sigmoid(gate_pre)
        silu_gate = gate_pre * sigmoid_gate
        hidden = (silu_gate * up_pre).astype(jnp.bfloat16)
        ffn_part = lax.psum_scatter(
            jnp.dot(hidden, down_weight, preferred_element_type=jnp.float32).astype(jnp.bfloat16),
            "shard",
            scatter_dimension=0,
            tiled=True,
        ).astype(jnp.float32)
        mixed_rows.append(
            jnp.where(valid_rows[:, None], middle + ffn_part, 0.0).astype(jnp.bfloat16)
        )
        cot_low = jnp.where(
            valid_rows[:, None], cotangent[micro_index], jnp.zeros_like(cotangent[micro_index])
        )
        cot_all = lax.all_gather(cot_low, "shard", axis=0, tiled=True)
        hidden_grad = jnp.einsum(
            "sd,fd->sf", cot_all, down_weight, preferred_element_type=jnp.float32
        )
        down_total = down_total + jnp.einsum(
            "sf,sd->fd", hidden, cot_all, preferred_element_type=jnp.float32
        )
        gate_grad = (
            hidden_grad * up_pre * sigmoid_gate * (1.0 + gate_pre * (1.0 - sigmoid_gate))
        ).astype(jnp.bfloat16)
        up_grad = (hidden_grad * silu_gate).astype(jnp.bfloat16)
        gate_total = gate_total + jnp.einsum(
            "sf,sd->fd", gate_grad, normed_all, preferred_element_type=jnp.float32
        )
        up_total = up_total + jnp.einsum(
            "sf,sd->fd", up_grad, normed_all, preferred_element_type=jnp.float32
        )
        second_grad = lax.psum_scatter(
            jnp.dot(gate_grad, gate_weight, preferred_element_type=jnp.float32)
            + jnp.dot(up_grad, up_weight, preferred_element_type=jnp.float32),
            "shard",
            scatter_dimension=0,
            tiled=True,
        )
        middle_part, midnorm_part = norm_backward(middle, inverse_second, midnorm_f, second_grad)
        middle_grad = cot_low.astype(jnp.float32) + middle_part
        midnorm_total = midnorm_total + midnorm_part
        branch_grad = middle_grad.astype(jnp.bfloat16)
        attended_grad = jnp.einsum(
            "sd,qd->sq",
            branch_grad,
            lax.all_gather(out_weight, "shard", axis=0, tiled=True),
            preferred_element_type=jnp.float32,
        ).astype(jnp.bfloat16)
        attended_group = attended_grad.reshape(seq_dev, KVH, repeat_heads, HD)
        probs_grad = jnp.einsum(
            "skrd,tkd->krst", attended_group, values_all, preferred_element_type=jnp.float32
        )
        inner_sum = jnp.sum(attention_probs * probs_grad, -1, keepdims=True)
        scores_grad = (attention_probs * (probs_grad - inner_sum)).astype(jnp.bfloat16)
        query_rot_grad = (
            jnp.einsum(
                "krst,tkd->skrd", scores_grad, keys_all, preferred_element_type=jnp.float32
            ).reshape(seq_dev, NH, HD)
            * score_scale
        )
        query_grad = (
            unrotate(query_rot_grad, cosine_table, sine_table)
            .astype(jnp.bfloat16)
            .reshape(seq_dev, query_width)
        )
        row_count = lax.axis_size("shard") * seq_dev
        key_part = (
            jnp.einsum(
                "krst,skrd->tkd", scores_grad, query_group, preferred_element_type=jnp.float32
            )
            * score_scale
        )
        value_part = jnp.einsum(
            "krst,skrd->tkd", probs_low, attended_group, preferred_element_type=jnp.float32
        )
        kv_grad = lax.psum_scatter(
            jnp.concatenate(
                [key_part.reshape(row_count, kv_width), value_part.reshape(row_count, kv_width)], 1
            ).astype(jnp.bfloat16),
            "shard",
            scatter_dimension=0,
            tiled=True,
        ).astype(jnp.float32)
        key_grad = (
            unrotate(kv_grad[:, :kv_width].reshape(seq_dev, KVH, HD), cosine_table, sine_table)
            .astype(jnp.bfloat16)
            .reshape(seq_dev, kv_width)
        )
        value_grad = kv_grad[:, kv_width:].astype(jnp.bfloat16)
        first_grad = jnp.einsum(
            "sq,qd->sd", query_grad, query_full, preferred_element_type=jnp.float32
        )
        first_grad = first_grad + jnp.einsum(
            "sq,qd->sd", key_grad, key_full, preferred_element_type=jnp.float32
        )
        first_grad = first_grad + jnp.einsum(
            "sq,qd->sd", value_grad, value_full, preferred_element_type=jnp.float32
        )
        source_part, prenorm_part = norm_backward(source, inverse_first, prenorm_f, first_grad)
        input_rows.append((middle_grad + source_part).astype(jnp.bfloat16))
        prenorm_total = prenorm_total + prenorm_part
        saved = (normed_first, query_grad, key_grad, value_grad, attended, branch_grad)
        weight_term, shard_rows = weight_terms(*saved, shard_count)
        reduced = lax.psum_scatter(
            weight_term(jnp.int32(0), lax.axis_size("shard") * shard_rows).astype(jnp.bfloat16),
            "shard",
            scatter_dimension=0,
            tiled=True,
        ).astype(jnp.float32)
        attn_total = reduced if attn_total is None else attn_total + reduced
    gain_sums = lax.psum((prenorm_total, midnorm_total), ("grp", "shard"))
    gain_share = model_width // shard_count
    prenorm_gradient = lax.dynamic_slice_in_dim(
        gain_sums[0], shard_rank * gain_share, gain_share, 0
    )
    midnorm_gradient = lax.dynamic_slice_in_dim(
        gain_sums[1], shard_rank * gain_share, gain_share, 0
    )
    summed = (
        lax.psum(attn_total.astype(jnp.bfloat16), "grp").astype(jnp.float32),
        lax.psum(gate_total.astype(jnp.bfloat16), "grp").astype(jnp.float32),
        lax.psum(up_total.astype(jnp.bfloat16), "grp").astype(jnp.float32),
        lax.psum(down_total.astype(jnp.bfloat16), "grp").astype(jnp.float32),
    )
    attn_rows = summed[0]
    query_share = query_width // shard_count
    kv_share = kv_width // shard_count
    query_gradient = attn_rows[:query_share]
    key_gradient = attn_rows[query_share : query_share + kv_share]
    value_gradient = attn_rows[query_share + kv_share : query_share + 2 * kv_share]
    out_gradient = attn_rows[query_share + 2 * kv_share :]
    return (
        jnp.stack(mixed_rows),
        jnp.stack(input_rows),
        prenorm_gradient,
        query_gradient,
        key_gradient,
        value_gradient,
        out_gradient,
        midnorm_gradient,
        summed[1],
        summed[2],
        summed[3],
    )


def local_heads(
    tokens,
    lengths,
    prenorm_gain,
    query_weight,
    key_weight,
    value_weight,
    out_weight,
    midnorm_gain,
    gate_weight,
    up_weight,
    down_weight,
    cotangent,
):
    low = jnp.bfloat16
    count = lax.axis_size("shard")
    groups = lax.axis_size("grp")
    seqs, seq_dev, model_width = tokens.shape
    rows = seqs * seq_dev
    inverse_freq = jnp.asarray(theta_base ** (-np.arange(0, HD, 2) / HD), jnp.float32)
    tokens_low = tokens.reshape(rows, model_width)
    cot_low = cotangent.reshape(rows, model_width)
    branch, gains, normed_first, cot_all, queries, keys, values, attended, kv_head, cosine, sine = (
        attention(
            lengths,
            tokens_low,
            cot_low,
            prenorm_gain,
            midnorm_gain,
            inverse_freq[None, :],
            query_weight,
            key_weight,
            value_weight,
            out_weight,
            count,
            groups,
            1,
        )
    )
    second_grad, ffn_parts, pair_sums, early = ffn(
        tokens_low, branch, gains, cot_all, gate_weight, up_weight, down_weight, groups, 2
    )
    mixed, input_gradient, gain_own, totals, wide, narrow = attention_grad(
        lengths,
        tokens_low,
        branch,
        cot_low,
        second_grad,
        gains,
        cosine,
        sine,
        ffn_parts,
        normed_first,
        attended,
        queries,
        keys,
        values,
        query_weight,
        kv_head,
        out_weight,
        pair_sums,
        early,
        groups,
        3,
    )
    f32 = jnp.float32
    return (
        mixed.reshape(tokens.shape),
        input_gradient.reshape(tokens.shape),
        gain_own[0],
        wide[1].astype(f32),
        narrow[0].astype(f32),
        narrow[1].astype(f32),
        wide[0].astype(f32),
        gain_own[1],
        totals[1].astype(f32),
        totals[2].astype(f32),
        totals[0].astype(f32),
    )


def solution(mesh):
    planes = mesh.shape["shard"] == NH and mesh.shape["grp"] == 4
    local = local_heads if planes else local_rows
    in_specs = (
        P("grp", "shard", None),
        P("grp"),
        P("shard"),
        P("shard", None),
        P("shard", None),
        P("shard", None),
        P("shard", None),
        P("shard"),
        P("shard", None),
        P("shard", None),
        P("shard", None),
        P("grp", "shard", None),
    )
    out_specs = (
        P("grp", "shard", None),
        P("grp", "shard", None),
        P("shard"),
        P("shard", None),
        P("shard", None),
        P("shard", None),
        P("shard", None),
        P("shard"),
        P("shard", None),
        P("shard", None),
        P("shard", None),
    )
    return jax.shard_map(local, mesh=mesh, in_specs=in_specs, out_specs=out_specs, check_vma=False)
```
